32 devices in a mesh: dp: 8 (over y, x, core), seq: 4 (over z).
Axes of the slice: x: 2, y: 2, z: 4, core: 2. Of those that a mesh axis runs over, the one named last changes fastest.
Arguments:
- tokens: bfloat16 [24, 2048, 768], P('dp', 'seq'), may hold values from -6 to 6
- w_qkv: bfloat16 [768, 2304], replicated, may hold values from -0.3125 to 0.3125
- w_out: bfloat16 [768, 768], replicated, may hold values from -0.875 to 0.875
- w_up: bfloat16 [768, 3072], replicated, may hold values from -0.21875 to 0.21875
- w_down: bfloat16 [3072, 768], replicated, may hold values from -0.109375 to 0.109375
- conv_filter: bfloat16 [33, 768], replicated, may hold values from -0.51953125 to 0.51953125
- gain_att: float32 [768], replicated, may hold values from 0.5 to 1.5
- gain_ffn: float32 [768], replicated, may hold values from 0.5 to 1.5
- grad_out: bfloat16 [24, 2048, 768], P('dp', 'seq'), may hold values from -6 to 6
Outputs:
- layer_out: bfloat16 [24, 2048, 768], P('dp', 'seq')
- grad_tokens: bfloat16 [24, 2048, 768], P('dp', 'seq')
- grad_w_qkv: float32 [768, 2304], P('dp', 'seq')
- grad_w_out: float32 [768, 768], P('dp', 'seq')
- grad_w_up: float32 [768, 3072], P('dp', 'seq')
- grad_w_down: float32 [3072, 768], P('dp', 'seq')
- grad_filter: float32 [33, 768], replicated
- grad_gain_att: float32 [768], replicated
- grad_gain_ffn: float32 [768], replicated
The draws below stay inside these ranges and needn't reach their ends.
All inputs are finite; a program needn't handle non-finite values.
Results may differ from the reference program's by a relative error of at most 0.035.
Values may be sent and summed in bfloat16 or wider, within the bound.
A program may use at most 320 MiB of HBM per device.

```python
import jax
import jax.numpy as jnp
from jax import lax

D = 768
H = 12
E = 64
FF = 3072
M = 64
KW = 33
NEWTON = 6
LENGTH = 2048
BATCH = 24


def draw_tokens(key, part):
    first_key, second_key = jax.random.split(jax.random.fold_in(key, 11))
    seg_len = LENGTH // M
    common = jax.random.normal(first_key, (BATCH, M, 1, D), jnp.float32)
    noise = jax.random.normal(second_key, (BATCH, M, seg_len, D), jnp.float32)
    mixed_rows = 0.8 * common + 0.6 * noise
    return jnp.clip(mixed_rows, -6.0, 6.0).reshape(BATCH, LENGTH, D).astype(jnp.bfloat16)


def levels(key, dims, cuts, smallest, top_value):
    factor_of, own = 1.0, jax.random.fold_in(key, 6)
    for axis_at, blocks in cuts:
        draws = jnp.exp(jax.random.uniform(jax.random.fold_in(own, axis_at), (blocks,), jnp.float32, smallest / len(cuts), top_value / len(cuts)))
        factor_of = factor_of * jnp.repeat(draws, dims[axis_at] // blocks).reshape([-1 if axis == axis_at else 1 for axis in range(len(dims))])
    return factor_of


def bell_draw(stream_key, shape, scale, bound, pieces=(), held_as=jnp.bfloat16):
    result = scale * jax.random.normal(stream_key, shape, jnp.float32)
    if pieces:
        result = result * levels(stream_key, shape, pieces, -0.22, 0.18)
    return jnp.clip(result, -bound, bound).astype(held_as)


def setup_inputs(seed: int = 0) -> dict:
    key_list = jax.random.split(jax.random.key(seed), 10)
    return {
        "tokens": draw_tokens(jax.random.fold_in(key_list[9], 71), 0),
        "w_qkv": bell_draw(key_list[1], (D, 3 * D), (D // 2) ** -0.5, 0.3125),
        "w_out": bell_draw(key_list[2], (D, D), (D // 16) ** -0.5, 0.875),
        "w_up": bell_draw(key_list[3], (D, FF), D ** -0.5, 0.21875),
        "w_down": bell_draw(key_list[4], (FF, D), FF ** -0.5, 0.109375),
        "conv_filter": bell_draw(key_list[5], (KW, D), (0.5 * KW ** -0.5), 0.51953125),
        "gain_att": jnp.clip(1.0 + 0.1 * jax.random.normal(key_list[6], (D,), jnp.float32), 0.5, 1.5),
        "gain_ffn": jnp.clip(1.0 + 0.1 * jax.random.normal(key_list[7], (D,), jnp.float32), 0.5, 1.5),
        "grad_out": bell_draw(key_list[8], (BATCH, LENGTH, D), 1.0, 6.0, ((0, 8), (1, 4))),
    }


highest = lax.Precision.HIGHEST
epsilon = 1e-05
root_half = 0.7071067811865476

@jax.custom_vjp
def low(v):
    return lax.optimization_barrier(v.astype(jnp.bfloat16)).astype(jnp.float32)

@jax.custom_vjp
def low_back(v):
    return v

def low_keep(v):
    return (low(v), None)

def low_pass(kept, grad):
    return (grad,)

def back_keep(v):
    return (v, None)

def back_low(kept, grad):
    return (low(grad),)
low.defvjp(low_keep, low_pass)
low_back.defvjp(back_keep, back_low)

def softmax_along(scores, axis):
    shifted = jnp.exp(scores - lax.optimization_barrier(jnp.max(scores, axis=axis, keepdims=True)))
    return shifted / lax.optimization_barrier(jnp.sum(shifted, axis=axis, keepdims=True))

def layer_norm(residual):
    centre = residual - lax.optimization_barrier(jnp.mean(residual, axis=-1, keepdims=True))
    return centre * lax.rsqrt(lax.optimization_barrier(jnp.mean(centre * centre, axis=-1, keepdims=True)) + epsilon)

def batch_product(left, right):
    return jnp.einsum('...ij,...jk->...ik', left, right, precision=highest)

def newton_inverse(kernel):
    column = lax.optimization_barrier(jnp.sum(kernel, axis=-2))
    col_scale = 1.0 / lax.optimization_barrier(jnp.max(column, axis=-1))
    approx = jnp.swapaxes(kernel, -1, -2) * col_scale[..., None, None]
    identity = jnp.eye(kernel.shape[-1], dtype=jnp.float32)
    for newton_step in range(NEWTON):
        product = batch_product(kernel, approx)
        inner_term = 7.0 * identity - product
        inner_term = 15.0 * identity - batch_product(product, inner_term)
        inner_term = 13.0 * identity - batch_product(product, inner_term)
        approx = 0.25 * batch_product(approx, inner_term)
    return approx

def landmark_mix(q_land, k_land, summary):
    middle = softmax_along(jnp.einsum('...mhe,...nhe->...hmn', q_land, k_land, precision=highest), -1)
    return batch_product(newton_inverse(middle), summary)

def one_sequence(params, seq_tokens):
    w_qkv, w_out, w_up, w_down, conv_filter, gain_att, gain_ffn = params
    seq_len, features = seq_tokens.shape
    seg_len = seq_len // M
    rim_width = KW // 2
    projected = jnp.dot(seq_tokens, w_qkv, precision=highest, preferred_element_type=jnp.float32)
    queries = low(low_back(0.125 * projected[:, :features]))
    key_rows = low(low_back(projected[:, features:2 * features]))
    value_rows = low(low_back(projected[:, 2 * features:]))
    q_land = low(lax.optimization_barrier(jnp.mean(queries.reshape(M, seg_len, features), axis=1))).reshape(M, H, E)
    k_land = low(lax.optimization_barrier(jnp.mean(key_rows.reshape(M, seg_len, features), axis=1))).reshape(M, H, E)
    q_heads = queries.reshape(seq_len, H, E)
    k_heads = key_rows.reshape(seq_len, H, E)
    v_heads = value_rows.reshape(seq_len, H, E)
    first_scores = low_back(jnp.einsum('the,mhe->hmt', q_heads, k_land, precision=highest))
    first_low = low(softmax_along(first_scores, 1))
    third_scores = low_back(jnp.einsum('mhe,the->hmt', q_land, k_heads, precision=highest))
    row_weights = jnp.exp(third_scores - lax.optimization_barrier(jnp.max(third_scores, axis=2, keepdims=True)))
    row_total = lax.optimization_barrier(jnp.sum(row_weights, axis=2))
    numerator = low_back(jnp.einsum('hmt,the->hme', low(row_weights), v_heads, precision=highest))
    summary = low_back(numerator / row_total[:, :, None])
    mixed_land = low(landmark_mix(q_land, k_land, summary))
    attended = jnp.einsum('hmt,hme->the', first_low, mixed_land, precision=highest).reshape(seq_len, features)
    padded = jnp.pad(value_rows, ((rim_width, rim_width), (0, 0)))
    conv_out = jnp.zeros((seq_len, features), jnp.float32)
    for tap_index in range(KW):
        conv_out = conv_out + conv_filter[tap_index] * padded[tap_index:tap_index + seq_len]
    mixed_all = low(low_back(attended + conv_out))
    residual = seq_tokens + low_back(jnp.dot(mixed_all, w_out, precision=highest, preferred_element_type=jnp.float32))
    hidden = layer_norm(residual) * gain_att
    up_proj = low_back(jnp.dot(low(hidden), w_up, precision=highest, preferred_element_type=jnp.float32))
    activated = low(0.5 * up_proj * (1.0 + lax.erf(up_proj * root_half)))
    residual_two = hidden + low_back(jnp.dot(activated, w_down, precision=highest, preferred_element_type=jnp.float32))
    return layer_norm(residual_two) * gain_ffn

def reference(tokens, w_qkv, w_out, w_up, w_down, conv_filter, gain_att, gain_ffn, grad_out):
    params = (w_qkv.astype(jnp.float32), w_out.astype(jnp.float32), w_up.astype(jnp.float32), w_down.astype(jnp.float32), conv_filter.astype(jnp.float32), gain_att.astype(jnp.float32), gain_ffn.astype(jnp.float32))
    inputs = tokens.astype(jnp.float32)

    def forward(weights, rows_all):

        def per_sequence(seq_tokens):
            return one_sequence(weights, seq_tokens)
        return lax.map(jax.checkpoint(per_sequence), rows_all)
    outputs, pullback = jax.vjp(forward, params, inputs)
    weight_grads, input_grads = pullback(grad_out.astype(jnp.float32))
    return (outputs.astype(jnp.bfloat16), input_grads.astype(jnp.bfloat16), weight_grads[0], weight_grads[1], weight_grads[2], weight_grads[3], weight_grads[4], weight_grads[5], weight_grads[6])
```

```python
import functools

import jax
import jax.numpy as jnp
from jax import lax
from jax.experimental import pallas as pl
from jax.experimental.pallas import tpu as pltpu
from jax.sharding import PartitionSpec as P

H = 12
E = 64
M = 64
KW = 33
RIM = KW // 2
NEWTON = 6

f32 = jnp.float32
bf16 = jnp.bfloat16
epsilon = 1e-05
root_half = 0.7071067811865476
inv_root_two_pi = 0.3989422804014327
MB = 1 << 20

ERFC_P = 0.39
ERFC_C = (
    0.23532530842493793,
    0.09138785409700201,
    0.6495607954603394,
    -0.6354020079402325,
    0.8866654334206034,
    -0.22753738516480188,
)


def dot(a, b):
    return lax.dot_general(a, b, (((1,), (0,)), ((), ())), preferred_element_type=f32)


def dot_nt(a, b):
    return lax.dot_general(a, b, (((1,), (1,)), ((), ())), preferred_element_type=f32)


def dot_tn(a, b):
    return lax.dot_general(a, b, (((0,), (0,)), ((), ())), preferred_element_type=f32)


def lane_group(shape):
    return lax.broadcasted_iota(jnp.int32, shape, len(shape) - 1) // E


def group_masks(shape, count, dtype):
    groups = lane_group(shape)
    return [(groups == h).astype(f32).astype(dtype) for h in range(count)]


def block_diag(x, masks):
    return jnp.concatenate([x * m for m in masks], axis=0)


def diag_blocks(n, masks):
    return sum(n[E * h : E * h + E] * m for h, m in enumerate(masks))


def params(limit=None, **kw):
    return pltpu.CompilerParams(vmem_limit_bytes=limit, **kw)


def project_kernel(tok_ref, w_ref, q_ref, k_ref, v_ref, ql_ref, kl_ref):
    rows, features = tok_ref.shape[1:]
    marks = ql_ref.shape[1]
    seg = rows // marks
    x = tok_ref[0]
    row = lax.broadcasted_iota(jnp.int32, (marks, rows), 0)
    col = lax.broadcasted_iota(jnp.int32, (marks, rows), 1)
    mean = jnp.where(col // seg == row, 1.0 / seg, 0.0).astype(bf16)
    for part, out in enumerate((q_ref, k_ref, v_ref)):
        for c in range(0, features, 256):
            p = dot(x, w_ref[:, part * features + c : part * features + c + 256])
            if part == 0:
                p = 0.125 * p
            low = p.astype(bf16)
            out[0, :, c : c + 256] = low
            if part < 2:
                (ql_ref, kl_ref)[part][0, :, c : c + 256] = dot(mean, low).astype(bf16)


def project(tokens, w_qkv, marks):
    seqs, rows, features = tokens.shape
    full = pl.BlockSpec((1, rows, features), lambda s: (s, 0, 0))
    land = pl.BlockSpec((1, marks, features), lambda s: (s, 0, 0))
    return pl.pallas_call(
        project_kernel,
        grid=(seqs,),
        in_specs=[full, pl.BlockSpec(w_qkv.shape, lambda s: (0, 0))],
        out_specs=[full] * 3 + [land] * 2,
        out_shape=[jax.ShapeDtypeStruct(tokens.shape, bf16)] * 3
        + [jax.ShapeDtypeStruct((seqs, marks, features), bf16)] * 2,
        compiler_params=params(48 * MB),
        name="project",
    )(tokens, w_qkv)


def scores_kernel(q_ref, k_ref, v_ref, ql_ref, kl_ref, w_ref, p_ref, num_ref, stat_ref):
    rows, features = q_ref.shape[1:]
    masks = group_masks((M, 4 * E), 4, bf16)
    masks_wide = group_masks((M, 4 * E), 4, f32)
    ones = jnp.where(
        lane_group((4 * E, 4 * E)) == lax.broadcasted_iota(jnp.int32, (4 * E, 4 * E), 0) // E, 1.0, 0.0
    ).astype(bf16)
    stat_ref[...] = jnp.zeros_like(stat_ref)
    chunk = min(128, rows)
    upper = lax.broadcasted_iota(jnp.int32, (chunk, 2 * E), 1) >= E
    for g in range(features // 256):
        sl = slice(256 * g, 256 * g + 256)
        s3 = dot_nt(k_ref[0, :, sl], block_diag(ql_ref[0, :, sl], masks))
        peak = jnp.max(s3, axis=0, keepdims=True)
        e3 = jnp.exp(s3 - peak)
        total = jnp.sum(e3, axis=0, keepdims=True)
        low = e3.astype(bf16)
        w_ref[0, :, sl] = low
        num = diag_blocks(dot_tn(low, v_ref[0, :, sl]), masks_wide).astype(bf16)
        for i in range(2):
            lanes = slice(128 * i, 128 * i + 128)
            num_ref[2 * g + i] = num[:, lanes]
            stat_ref[2 * g + i, 0:1, :] = peak[:, lanes]
            stat_ref[2 * g + i, 1:2, :] = total[:, lanes]
        kd = block_diag(kl_ref[0, :, sl], masks)
        for r in range(0, rows, chunk):
            s1 = dot_nt(q_ref[0, r : r + chunk, sl], kd)
            parts = []
            for i in range(2):
                x = s1[:, 128 * i : 128 * i + 128]
                top_a = jnp.max(jnp.where(upper, -jnp.inf, x), axis=1, keepdims=True)
                top_b = jnp.max(jnp.where(upper, x, -jnp.inf), axis=1, keepdims=True)
                parts.append(jnp.exp(x - jnp.where(upper, top_b, top_a)))
            e1 = jnp.concatenate(parts, axis=1)
            p_ref[0, r : r + chunk, sl] = (e1 / dot(e1.astype(bf16), ones)).astype(bf16)


def scores(q, k, v, q_land, k_land):
    seqs, rows, features = q.shape
    pairs = features // 128
    full = pl.BlockSpec((1, rows, features), lambda s: (s, 0, 0))
    land = pl.BlockSpec((1, M, features), lambda s: (s, 0, 0))
    return pl.pallas_call(
        scores_kernel,
        grid=(seqs,),
        in_specs=[full] * 3 + [land] * 2,
        out_specs=[full] * 2
        + [
            pl.BlockSpec((pairs, M, 128), lambda s: (s, 0, 0)),
            pl.BlockSpec((pairs, 8, 128), lambda s: (s, 0, 0)),
        ],
        out_shape=[jax.ShapeDtypeStruct(q.shape, bf16)] * 2
        + [
            jax.ShapeDtypeStruct((seqs * pairs, M, 128), bf16),
            jax.ShapeDtypeStruct((seqs * pairs, 8, 128), f32),
        ],
        compiler_params=params(48 * MB),
        name="scores",
    )(q, k, v, q_land, k_land)


def fill_pad(pad, x_ref, l_ref, r_ref):
    rows = x_ref.shape[1]
    pad[0:RIM, :] = l_ref[0].astype(f32)
    pad[RIM : RIM + rows, :] = x_ref[0].astype(f32)
    pad[RIM + rows : RIM + rows + RIM, :] = r_ref[0].astype(f32)


def conv_kernel(v_ref, l_ref, r_ref, f_ref, o_ref, pad):
    rows = v_ref.shape[1]
    fill_pad(pad, v_ref, l_ref, r_ref)
    for c in range(0, rows, 64):
        acc = jnp.zeros((64, 128), f32)
        for j in range(KW):
            acc = acc + f_ref[j : j + 1, :] * pad[c + j : c + j + 64, :]
        o_ref[0, c : c + 64, :] = acc.astype(bf16)


def conv(v, left, right, taps):
    seqs, rows, features = v.shape
    sp = lambda n: pl.BlockSpec((1, n, 128), lambda s, g: (s, 0, g))
    return pl.pallas_call(
        conv_kernel,
        grid=(seqs, features // 128),
        in_specs=[sp(rows), sp(RIM), sp(RIM), pl.BlockSpec((KW, 128), lambda s, g: (0, g))],
        out_specs=sp(rows),
        out_shape=jax.ShapeDtypeStruct(v.shape, bf16),
        scratch_shapes=[pltpu.VMEM((rows + 2 * RIM, 128), f32)],
        name="conv",
    )(v, left, right, taps)


def conv_back_kernel(g_ref, l_ref, r_ref, v_ref, f_ref, o_ref, gf_ref, pad, facc):
    rows = v_ref.shape[1]
    fill_pad(pad, g_ref, l_ref, r_ref)

    @pl.when(pl.program_id(1) == 0)
    def _():
        facc[...] = jnp.zeros_like(facc)

    for c in range(0, rows, 64):
        acc = jnp.zeros((64, 128), f32)
        vals = v_ref[0, c : c + 64, :].astype(f32)
        for j in range(KW):
            moved = pad[c + 2 * RIM - j : c + 2 * RIM - j + 64, :]
            acc = acc + f_ref[j : j + 1, :] * moved
            facc[8 * j : 8 * j + 8, :] += (vals * moved).reshape(8, 8, 128).sum(0)
        o_ref[0, c : c + 64, :] = acc.astype(bf16)

    @pl.when(pl.program_id(1) == pl.num_programs(1) - 1)
    def _():
        gf_ref[...] = facc[...].reshape(KW, 8, 128).sum(1)


def conv_back(g, left, right, v, taps):
    seqs, rows, features = v.shape
    sp = lambda n: pl.BlockSpec((1, n, 128), lambda g, s: (s, 0, g))
    fs = pl.BlockSpec((KW, 128), lambda g, s: (0, g))
    return pl.pallas_call(
        conv_back_kernel,
        grid=(features // 128, seqs),
        in_specs=[sp(rows), sp(RIM), sp(RIM), sp(rows), fs],
        out_specs=[sp(rows), fs],
        out_shape=[jax.ShapeDtypeStruct(v.shape, bf16), jax.ShapeDtypeStruct((KW, features), f32)],
        scratch_shapes=[pltpu.VMEM((rows + 2 * RIM, 128), f32), pltpu.VMEM((KW * 8, 128), f32)],
        name="conv_back",
    )(g, left, right, v, taps)


def split(x):
    hi = x.astype(bf16)
    return hi, (x - hi.astype(f32)).astype(bf16)


def stack_parts(xs, axis):
    return jnp.concatenate([part for x in xs for part in split(x)], axis=axis)


def pair_sums(out, count):
    top = lambda i, j: out[128 * i + 64 * j : 128 * i + 64 * j + 64]
    return [
        top(i, 0)[:, :128] + (top(i, 0)[:, 128:] + top(i, 1)[:, :128]) for i in range(count)
    ]


def pair_nn(lefts, right, masks):
    hi, lo = split(right)
    packed = jnp.concatenate([block_diag(hi, masks), block_diag(lo, masks)], axis=1)
    return pair_sums(dot(stack_parts(lefts, 0), packed), len(lefts))


def pair_nt(lefts, right, masks):
    hi, lo = split(right)
    packed = jnp.concatenate([block_diag(hi, masks), block_diag(lo, masks)], axis=0)
    return pair_sums(dot_nt(stack_parts(lefts, 0), packed), len(lefts))


def pair_tn(left, rights, masks_wide):
    out = dot_tn(stack_parts([left], 1), stack_parts(rights, 1))
    results = []
    for i in range(len(rights)):
        full = out[:128, 256 * i : 256 * i + 128] + (
            out[:128, 256 * i + 128 : 256 * i + 256] + out[128:, 256 * i : 256 * i + 128]
        )
        results.append(diag_blocks(full, masks_wide))
    return results


def half_reduce(x, upper, op, fill):
    a = op(jnp.where(upper, fill, x), axis=1, keepdims=True)
    b = op(jnp.where(upper, x, fill), axis=1, keepdims=True)
    return jnp.where(upper, b, a)


def to_column(row, same, upper):
    return half_reduce(jnp.where(same, row, 0.0), upper, jnp.sum, 0.0)


def to_row(col, same):
    return jnp.sum(jnp.where(same, col, 0.0), axis=0, keepdims=True)


def pair_consts():
    lane = lax.broadcasted_iota(jnp.int32, (M, 128), 1)
    row = lax.broadcasted_iota(jnp.int32, (M, 128), 0)
    return lane >= E, row == lane % E, group_masks((M, 128), 2, bf16), group_masks((M, 128), 2, f32)


def inverse_kernel(
    num_ref, stat_ref, ql_ref, kl_ref, mixed_ref, sum_ref, mid_ref, z_ref, p_ref, a_ref, w_ref,
    scale_ref, tot_ref, alpha_ref,
):
    ranks, own = num_ref.shape[:2]
    upper, same, masks, masks_wide = pair_consts()
    for i in range(own):
        peak = stat_ref[0, i, 0:1, :]
        for r in range(1, ranks):
            peak = jnp.maximum(peak, stat_ref[r, i, 0:1, :])
        total = jnp.zeros((1, 128), f32)
        numer = jnp.zeros((M, 128), f32)
        for r in range(ranks):
            alpha = jnp.exp(stat_ref[r, i, 0:1, :] - peak)
            total = total + alpha * stat_ref[r, i, 1:2, :]
            column = to_column(alpha, same, upper)
            alpha_ref[r, i] = column
            numer = numer + column * num_ref[r, i].astype(f32)
        total = to_column(total, same, upper)
        tot_ref[i] = total
        sum_ref[i] = numer / total
        ql, kl = ql_ref[i], kl_ref[i]
        s2 = dot_nt(ql, block_diag(kl, masks))
        e2 = jnp.exp(s2 - half_reduce(s2, upper, jnp.max, -jnp.inf))
        middle = e2 / half_reduce(e2, upper, jnp.sum, 0.0)
        mid_ref[i] = middle
        st = dot_nt(kl, block_diag(ql, masks))
        et = jnp.exp(st - jnp.max(st, axis=0, keepdims=True))
        flipped = et / jnp.sum(et, axis=0, keepdims=True)
        column = jnp.sum(middle, axis=0, keepdims=True)
        scale = 1.0 / half_reduce(column, upper[0:1], jnp.max, -jnp.inf)
        scale_ref[i] = jnp.broadcast_to(scale, (8, 128))
        z_ref[0, i] = flipped * scale

    def step(it, carry):
        zs = [z_ref[it, i] for i in range(own)]
        ps = [pair_nn([mid_ref[i]], zs[i], masks)[0] for i in range(own)]
        second = [pair_nn([ps[i], zs[i]], ps[i], masks) for i in range(own)]
        for i in range(own):
            p2, a = second[i]
            w = 7.0 * ps[i] - p2
            p_ref[it, i] = ps[i]
            a_ref[it, i] = a
            w_ref[it, i] = w
            z_ref[it + 1, i] = 0.25 * (13.0 * zs[i] - 15.0 * a + pair_nn([a], w, masks)[0])
        return carry

    lax.fori_loop(0, NEWTON, step, 0)
    for i in range(own):
        mixed_ref[i] = pair_nn([z_ref[NEWTON, i]], sum_ref[i], masks)[0].astype(bf16)


def inverse(num, stat, ql, kl):
    ranks, own = num.shape[:2]
    mat = jax.ShapeDtypeStruct((own, M, 128), f32)
    steps = lambda n: jax.ShapeDtypeStruct((n, own, M, 128), f32)
    return pl.pallas_call(
        inverse_kernel,
        out_shape=[
            jax.ShapeDtypeStruct((own, M, 128), bf16), mat, mat, steps(NEWTON + 1), steps(NEWTON),
            steps(NEWTON), steps(NEWTON), jax.ShapeDtypeStruct((own, 8, 128), f32), mat, steps(ranks),
        ],
        compiler_params=params(48 * MB),
        name="inverse",
    )(num, stat, ql, kl)


def inverse_back_kernel(
    land_ref, ql_ref, kl_ref, sum_ref, mid_ref, z_ref, p_ref, a_ref, w_ref, scale_ref, tot_ref,
    alpha_ref, gn_ref, gt_ref, mq_ref, mk_ref, g_ref, dk_ref,
):
    ranks, own = land_ref.shape[:2]
    upper, same, masks, masks_wide = pair_consts()
    for i in range(own):
        land = land_ref[0, i].astype(f32)
        for r in range(1, ranks):
            land = land + land_ref[r, i].astype(f32)
        summary, total = sum_ref[i], tot_ref[i]
        gs = pair_tn(z_ref[NEWTON, i], [land], masks_wide)[0].astype(bf16).astype(f32)
        gn = (gs / total).astype(bf16).astype(f32)
        gt = -half_reduce(gs * summary, upper, jnp.sum, 0.0) / total
        for r in range(ranks):
            gn_ref[r, i] = (alpha_ref[r, i] * gn).astype(bf16)
            gt_ref[r, i] = jnp.broadcast_to(to_row(alpha_ref[r, i] * gt, same), (8, 128))
        g_ref[i] = pair_nt([land], summary, masks)[0]
        dk_ref[i] = jnp.zeros((M, 128), f32)

    def step(back, carry):
        it = NEWTON - 1 - back
        gs = [g_ref[i] for i in range(own)]
        das, dws = [], []
        for i in range(own):
            das.append(0.25 * (pair_nt([gs[i]], w_ref[it, i], masks)[0] - 15.0 * gs[i]))
            dws.append(0.25 * pair_tn(a_ref[it, i], [gs[i]], masks_wide)[0])
        dps, parts = [], []
        for i in range(own):
            right = pair_nt([dws[i], das[i]], p_ref[it, i], masks)
            left = pair_tn(p_ref[it, i], [dws[i]], masks_wide)[0]
            dps.append(7.0 * dws[i] - right[0] - left + pair_tn(z_ref[it, i], [das[i]], masks_wide)[0])
            parts.append(3.25 * gs[i] + right[1])
        for i in range(own):
            g_ref[i] = parts[i] + pair_tn(mid_ref[i], [dps[i]], masks_wide)[0]
            dk_ref[i] += pair_nt([dps[i]], z_ref[it, i], masks)[0]
        return carry

    lax.fori_loop(0, NEWTON, step, 0)
    eye = jnp.where(same, 1.0, 0.0).astype(bf16)
    for i in range(own):
        g, middle, scale = g_ref[i], mid_ref[i], scale_ref[i, 0:1, :]
        turned = dot_tn(stack_parts([g], 1), eye)
        turned = diag_blocks(turned[:128] + turned[128:], masks_wide)
        column = jnp.sum(middle, axis=0, keepdims=True)
        top = half_reduce(column, upper[0:1], jnp.max, -jnp.inf)
        hit = jnp.where(column == top, 1.0, 0.0)
        share = hit / half_reduce(hit, upper[0:1], jnp.sum, 0.0)
        d_scale = half_reduce(jnp.sum(turned * middle, axis=0, keepdims=True), upper[0:1], jnp.sum, 0.0)
        dk = dk_ref[i] + turned * scale - share * (d_scale * scale * scale)
        ds = middle * (dk - half_reduce(middle * dk, upper, jnp.sum, 0.0))
        hi, lo = split(ds)
        both = dot(jnp.concatenate([hi, lo], axis=0), block_diag(kl_ref[i], masks))
        mq_ref[i] = both[:M] + both[M:]
        turned = dot_tn(jnp.concatenate([hi, lo], axis=1), ql_ref[i])
        mk_ref[i] = diag_blocks(turned[:128] + turned[128:], masks_wide)


def inverse_back(land, ql, kl, saved):
    ranks, own = land.shape[:2]
    mat = jax.ShapeDtypeStruct((own, M, 128), f32)
    return pl.pallas_call(
        inverse_back_kernel,
        out_shape=[
            jax.ShapeDtypeStruct((ranks, own, M, 128), bf16),
            jax.ShapeDtypeStruct((ranks, own, 8, 128), f32), mat, mat,
        ],
        scratch_shapes=[pltpu.VMEM((own, M, 128), f32)] * 2,
        compiler_params=params(48 * MB),
        name="inverse_back",
    )(land, ql, kl, *saved)


def mean_of(x):
    return jnp.mean(x, axis=-1, keepdims=True)


def gelu_and_slope(u):
    x = jnp.abs(u) * root_half
    t = 1.0 / (1.0 + ERFC_P * x)
    poly = jnp.full_like(t, ERFC_C[-1])
    for c in ERFC_C[-2::-1]:
        poly = poly * t + c
    bell = jnp.exp(-0.5 * u * u)
    half = (0.5 * t) * poly * bell
    cdf = jnp.where(u < 0.0, half, 1.0 - half)
    return u * cdf, cdf + u * bell * inv_root_two_pi


def row_kernel(
    tok_ref, p_ref, conv_ref, mix_ref, top_ref, w_out_ref, w_up_ref, w_down_ref, ga_ref, gf_ref,
    out_ref, proj_ref, gm_ref, wg_ref, gains_ref,
    act, gul, slope, hid_t, gdl_t, mix_t, gpr, resid,
):
    step = pl.program_id(0)
    size, features = tok_ref.shape
    blocks = act.shape[0] // size
    ff = act.shape[1]
    wide = features

    @pl.when(step == 0)
    def _():
        gains_ref[...] = jnp.zeros_like(gains_ref)

    @pl.when(step < blocks)
    def _():
        start = pl.multiple_of(step * size, size)
        rows = pl.ds(start, size)
        masks = group_masks((M, 4 * E), 4, bf16)
        for g in range(features // 256):
            sl = slice(256 * g, 256 * g + 256)
            att = dot(p_ref[:, sl], block_diag(mix_ref[0, :, sl], masks))
            low = (att + conv_ref[:, sl].astype(f32)).astype(bf16)
            resid[:, sl] = low
        mixed = resid[...]
        mix_t[:, rows] = mixed.T
        residual = tok_ref[...].astype(f32) + dot(mixed, w_out_ref[...])
        centre = residual - mean_of(residual)
        s_att = lax.rsqrt(mean_of(centre * centre) + epsilon)
        normed = centre * s_att
        gain_att = ga_ref[...]
        hidden = normed * gain_att
        hid_low = hidden.astype(bf16)
        hid_t[:, rows] = hid_low.T
        down = jnp.zeros((size, features), f32)
        for j in range(0, ff, wide):
            up = dot(hid_low, w_up_ref[:, j : j + wide])
            a, sl = gelu_and_slope(up)
            low = a.astype(bf16)
            act[rows, j : j + wide] = low
            slope[:, j : j + wide] = sl.astype(bf16)
            down = down + dot(low, w_down_ref[j : j + wide, :])
        residual_two = hidden + down
        centre_two = residual_two - mean_of(residual_two)
        s_ffn = lax.rsqrt(mean_of(centre_two * centre_two) + epsilon)
        normed_two = centre_two * s_ffn
        gain_ffn = gf_ref[...]
        out_ref[...] = (normed_two * gain_ffn).astype(bf16)
        top = top_ref[...].astype(f32)
        gains_ref[8:16, :] += (top * normed_two).reshape(size // 8, 8, features).sum(0)
        g = top * gain_ffn
        grad_two = s_ffn * (g - mean_of(g) - normed_two * mean_of(g * normed_two))
        gdl = grad_two.astype(bf16)
        gdl_t[:, rows] = gdl.T
        back = jnp.zeros((size, features), f32)
        for j in range(0, ff, wide):
            gu = dot_nt(gdl, w_down_ref[j : j + wide, :]) * slope[:, j : j + wide].astype(f32)
            low = gu.astype(bf16)
            gul[rows, j : j + wide] = low
            back = back + dot_nt(low, w_up_ref[:, j : j + wide])
        grad_hidden = grad_two + back
        gains_ref[0:8, :] += (grad_hidden * normed).reshape(size // 8, 8, features).sum(0)
        g = grad_hidden * gain_att
        proj = (s_att * (g - mean_of(g) - normed * mean_of(g * normed))).astype(bf16)
        proj_ref[...] = proj
        gpr[rows, :] = proj
        gm_ref[...] = dot_nt(proj, w_out_ref[...]).astype(bf16)

    chunks = ff // wide
    for first, left, right in ((0, hid_t, gul), (chunks, gdl_t, act), (2 * chunks, mix_t, gpr)):
        count = chunks if first < 2 * chunks else 1

        @pl.when((step >= blocks + first) & (step < blocks + first + count))
        def _(first=first, left=left, right=right):
            base = (step - blocks - first) * wide
            for c in range(0, wide, 256):
                cols = pl.ds(pl.multiple_of(base + c, 256), 256)
                wg_ref[0, :, c : c + 256] = dot(left[...], right[:, cols]).astype(bf16)


def row_pass(tokens, probs, conv_out, mixed, grad_out, w_out, w_up, w_down, gain_att, gain_ffn):
    seqs, rows, features = tokens.shape
    ff = w_up.shape[1]
    size = min(256, rows)
    total = seqs * rows
    blocks = total // size
    grads = 2 * (ff // features) + 1
    here = lambda i: jnp.minimum(i, blocks - 1)
    block = pl.BlockSpec((size, features), lambda i: (here(i), 0))
    whole = lambda a: pl.BlockSpec(a.shape, lambda i: (0,) * a.ndim, pipeline_mode=pl.Buffered(1))
    flat = lambda a: a.reshape(total, features)
    gains = [gain_att.reshape(1, features), gain_ffn.reshape(1, features)]
    row_out = jax.ShapeDtypeStruct((total, features), bf16)
    tall = pltpu.VMEM((features, total), bf16)
    return pl.pallas_call(
        row_kernel,
        grid=(blocks + grads,),
        in_specs=[
            block, block, block,
            pl.BlockSpec((1, M, features), lambda i: (here(i) * size // rows, 0, 0)),
            block, whole(w_out), whole(w_up), whole(w_down), whole(gains[0]), whole(gains[1]),
        ],
        out_specs=[block] * 3
        + [
            pl.BlockSpec((1, features, features), lambda i: (jnp.maximum(i - blocks, 0), 0, 0)),
            pl.BlockSpec((16, features), lambda i: (0, 0)),
        ],
        out_shape=[row_out] * 3
        + [
            jax.ShapeDtypeStruct((grads, features, features), bf16),
            jax.ShapeDtypeStruct((16, features), f32),
        ],
        scratch_shapes=[
            pltpu.VMEM((total, ff), bf16), pltpu.VMEM((total, ff), bf16), pltpu.VMEM((size, ff), bf16),
            tall, tall, tall, pltpu.VMEM((total, features), bf16), pltpu.VMEM((size, features), bf16),
        ],
        compiler_params=params(60 * MB),
        name="row_pass",
    )(flat(tokens), flat(probs), flat(conv_out), mixed, flat(grad_out), w_out, w_up, w_down, *gains)


def first_back_kernel(gm_ref, p_ref, q_ref, mix_ref, kl_ref, land_ref, gq_ref, klp_ref):
    features = gm_ref.shape[2]
    masks = group_masks((M, 4 * E), 4, bf16)
    masks_wide = group_masks((M, 4 * E), 4, f32)
    ones = jnp.where(
        lane_group((4 * E, 4 * E)) == lax.broadcasted_iota(jnp.int32, (4 * E, 4 * E), 0) // E, 1.0, 0.0
    ).astype(bf16)
    for g in range(features // 256):
        sl = slice(256 * g, 256 * g + 256)
        gm, p = gm_ref[0, :, sl], p_ref[0, :, sl]
        land = diag_blocks(dot_tn(p, gm), masks_wide).astype(bf16)
        for i in range(2):
            land_ref[2 * g + i] = land[:, 128 * i : 128 * i + 128]
        d = dot_nt(gm, block_diag(mix_ref[0, :, sl], masks))
        pw = p.astype(f32)
        gs = (pw * (d - dot((pw * d).astype(bf16), ones))).astype(bf16)
        gq_ref[0, :, sl] = dot(gs, block_diag(kl_ref[0, :, sl], masks)).astype(bf16)
        klp_ref[0, :, sl] = diag_blocks(dot_tn(gs, q_ref[0, :, sl]), masks_wide)


def first_back(gm, probs, q, mixed, k_land):
    seqs, rows, features = q.shape
    pairs = features // 128
    full = pl.BlockSpec((1, rows, features), lambda s: (s, 0, 0))
    land = pl.BlockSpec((1, M, features), lambda s: (s, 0, 0))
    return pl.pallas_call(
        first_back_kernel,
        grid=(seqs,),
        in_specs=[full] * 3 + [land] * 2,
        out_specs=[pl.BlockSpec((pairs, M, 128), lambda s: (s, 0, 0)), full, land],
        out_shape=[
            jax.ShapeDtypeStruct((seqs * pairs, M, 128), bf16),
            jax.ShapeDtypeStruct(q.shape, bf16),
            jax.ShapeDtypeStruct((seqs, M, features), f32),
        ],
        compiler_params=params(48 * MB),
        name="first_back",
    )(gm, probs, q, mixed, k_land)


def third_back_kernel(w_ref, v_ref, k_ref, gc_ref, gn_ref, gt_ref, ql_ref, gv_ref, gk_ref, qlp_ref):
    features = w_ref.shape[2]
    masks = group_masks((M, 4 * E), 4, bf16)
    masks_wide = group_masks((M, 4 * E), 4, f32)
    for g in range(features // 256):
        sl = slice(256 * g, 256 * g + 256)
        w = w_ref[0, :, sl]
        gn = jnp.concatenate([gn_ref[2 * g], gn_ref[2 * g + 1]], axis=1)
        gt = jnp.concatenate([gt_ref[2 * g, 0:1, :], gt_ref[2 * g + 1, 0:1, :]], axis=1)
        gd = block_diag(gn, masks)
        gs = (w.astype(f32) * (dot_nt(v_ref[0, :, sl], gd) + gt)).astype(bf16)
        gv_ref[0, :, sl] = (dot(w, gd) + gc_ref[0, :, sl].astype(f32)).astype(bf16)
        gk_ref[0, :, sl] = dot(gs, block_diag(ql_ref[0, :, sl], masks)).astype(bf16)
        qlp_ref[0, :, sl] = diag_blocks(dot_tn(gs, k_ref[0, :, sl]), masks_wide)


def third_back(w, v, k, grad_conv, gn, gt, q_land):
    seqs, rows, features = v.shape
    pairs = features // 128
    full = pl.BlockSpec((1, rows, features), lambda s: (s, 0, 0))
    land = pl.BlockSpec((1, M, features), lambda s: (s, 0, 0))
    return pl.pallas_call(
        third_back_kernel,
        grid=(seqs,),
        in_specs=[full] * 4
        + [
            pl.BlockSpec((pairs, M, 128), lambda s: (s, 0, 0)),
            pl.BlockSpec((pairs, 8, 128), lambda s: (s, 0, 0)),
            land,
        ],
        out_specs=[full, full, land],
        out_shape=[jax.ShapeDtypeStruct(v.shape, bf16)] * 2
        + [jax.ShapeDtypeStruct((seqs, M, features), f32)],
        compiler_params=params(48 * MB),
        name="third_back",
    )(w, v, k, grad_conv, gn, gt, q_land)


def last_kernel(tok_ref, gq_ref, gk_ref, gv_ref, qo_ref, ko_ref, proj_ref, w_ref, gt_ref, wg_ref, d, tok_t):
    step = pl.program_id(0)
    seqs = tok_t.shape[1] // tok_ref.shape[1]
    rows, features = tok_ref.shape[1:]
    marks = qo_ref.shape[1]
    seg = rows // marks

    @pl.when(step < seqs)
    def _():
        here = pl.ds(pl.multiple_of(step * rows, rows), rows)
        for part, (core, own) in enumerate(((gq_ref, qo_ref), (gk_ref, ko_ref))):
            for m in range(marks):
                at = pl.ds(pl.multiple_of(step * rows + m * seg, seg), seg)
                x = core[0, m * seg : m * seg + seg, :].astype(f32) + own[0, m : m + 1, :] * (1.0 / seg)
                x = x.astype(bf16)
                if part == 0:
                    x = x * jnp.asarray(0.125, bf16)
                d[at, part * features : part * features + features] = x
        d[here, 2 * features :] = gv_ref[0]
        tok_t[:, here] = tok_ref[0].T
        for c in range(0, rows, 128):
            at = pl.ds(pl.multiple_of(step * rows + c, 128), 128)
            gt_ref[0, c : c + 128, :] = (
                proj_ref[0, c : c + 128, :].astype(f32) + dot_nt(d[at, :], w_ref[...])
            ).astype(bf16)

    @pl.when(step >= seqs)
    def _():
        base = (step - seqs) * features
        for c in range(0, features, 256):
            cols = pl.ds(pl.multiple_of(base + c, 256), 256)
            wg_ref[0, :, c : c + 256] = dot(tok_t[...], d[:, cols]).astype(bf16)


def last_pass(tokens, gq, gk, gv, q_own, k_own, proj, w_qkv):
    seqs, rows, features = tokens.shape
    marks = q_own.shape[1]
    here = lambda i: jnp.minimum(i, seqs - 1)
    full = pl.BlockSpec((1, rows, features), lambda i: (here(i), 0, 0))
    land = pl.BlockSpec((1, marks, features), lambda i: (here(i), 0, 0))
    return pl.pallas_call(
        last_kernel,
        grid=(seqs + 3,),
        in_specs=[full] * 4 + [land] * 2
        + [full, pl.BlockSpec(w_qkv.shape, lambda i: (0, 0), pipeline_mode=pl.Buffered(1))],
        out_specs=[full, pl.BlockSpec((1, features, features), lambda i: (jnp.maximum(i - seqs, 0), 0, 0))],
        out_shape=[
            jax.ShapeDtypeStruct(tokens.shape, bf16),
            jax.ShapeDtypeStruct((3, features, features), bf16),
        ],
        scratch_shapes=[
            pltpu.VMEM((seqs * rows, 3 * features), bf16), pltpu.VMEM((features, seqs * rows), bf16),
        ],
        compiler_params=params(56 * MB),
        name="last_pass",
    )(tokens, gq, gk, gv, q_own, k_own, proj, w_qkv)


def halo(cells, width):
    count = lax.axis_size("seq")
    head, tail = cells[:, :width], cells[:, cells.shape[1] - width :]
    left = lax.ppermute(tail, "seq", [(i, i + 1) for i in range(count - 1)])
    right = lax.ppermute(head, "seq", [(i + 1, i) for i in range(count - 1)])
    return left, right


def scatter_sum(grad):
    share = lax.psum_scatter(grad, "dp", scatter_dimension=0, tiled=True)
    return lax.psum_scatter(share, "seq", scatter_dimension=1, tiled=True).astype(f32)


def per_device(tokens, w_qkv, w_out, w_up, w_down, conv_filter, gain_att, gain_ffn, grad_out):
    seqs, rows, features = tokens.shape
    ranks = lax.axis_size("seq")
    rank = lax.axis_index("seq")
    marks = M // ranks
    ff = w_up.shape[1]
    pairs = seqs * (features // 128)
    own = -(-pairs // ranks)

    def to_pairs(x):
        x = x.reshape(seqs, M, features // 128, 128).transpose(0, 2, 1, 3)
        return x.reshape(pairs, M, 128)

    def from_pairs(x):
        x = x[:pairs].reshape(seqs, features // 128, M, 128).transpose(0, 2, 1, 3)
        return x.reshape(seqs, M, features)

    def pad_pairs(x):
        return jnp.pad(x, ((0, ranks * own - pairs),) + ((0, 0),) * (x.ndim - 1))

    def exchange(x):
        out = lax.all_to_all(pad_pairs(x), "seq", 0, 0, tiled=True)
        return out.reshape((ranks, own) + x.shape[1:])

    def mine(x):
        return lax.dynamic_slice_in_dim(pad_pairs(x), rank * own, own, 0)

    q, k, v, q_part, k_part = project(tokens, w_qkv, marks)
    land = lax.all_gather(jnp.stack([q_part, k_part]), "seq", axis=2, tiled=True)
    q_land, k_land = land[0], land[1]
    v_left, v_right = halo(v, RIM)
    taps = conv_filter.astype(f32)
    weights, probs, num, stat = scores(q, k, v, q_land, k_land)
    num_parts, stat_parts = exchange(num), exchange(stat)
    conv_out = conv(v, v_left, v_right, taps)
    ql_own, kl_own = mine(to_pairs(q_land)), mine(to_pairs(k_land))
    mixed_own, *saved = inverse(num_parts, stat_parts, ql_own, kl_own)
    mixed = from_pairs(lax.all_gather(mixed_own, "seq", axis=0, tiled=True))
    layer_out, proj, gm, wg, gains = row_pass(
        tokens, probs, conv_out, mixed, grad_out, w_out, w_up, w_down, gain_att, gain_ffn
    )
    shape3 = (seqs, rows, features)
    gm = gm.reshape(shape3)
    chunks = ff // features
    up_share = scatter_sum(wg[:chunks].transpose(1, 0, 2).reshape(features, ff))
    down_share = scatter_sum(wg[chunks : 2 * chunks].transpose(0, 2, 1).reshape(ff, features))
    out_share = scatter_sum(wg[2 * chunks])
    land_part, gq, k_land_part = first_back(gm, probs, q, mixed, k_land)
    g_left, g_right = halo(gm, RIM)
    land_parts = exchange(land_part)
    grad_conv, taps_grad = conv_back(gm, g_left, g_right, v, taps)
    gn_own, gt_own, mid_q, mid_k = inverse_back(land_parts, ql_own, kl_own, saved)

    def give_back(x):
        x = x.reshape((ranks * own,) + x.shape[2:])
        return lax.all_to_all(x, "seq", 0, 0, tiled=True)[:pairs]

    grad_values, gk, q_land_part = third_back(
        weights, v, k, grad_conv, give_back(gn_own), give_back(gt_own), q_land
    )

    def place(x):
        full = jnp.zeros((ranks * own, M, 128), f32)
        return from_pairs(lax.dynamic_update_slice_in_dim(full, x, rank * own, 0))

    both = jnp.stack([q_land_part + place(mid_q), k_land_part + place(mid_k)]).astype(bf16)
    both = both.reshape(2, seqs, ranks, marks, features).transpose(2, 0, 1, 3, 4)
    both = lax.all_to_all(both, "seq", 0, 0, tiled=True).astype(f32).sum(0)
    grad_tokens, qkv_grad = last_pass(tokens, gq, gk, grad_values, both[0], both[1], proj.reshape(shape3), w_qkv)
    qkv_share = scatter_sum(qkv_grad.transpose(1, 0, 2).reshape(features, 3 * features))
    gains = gains.reshape(2, 8, features).sum(1)
    small = lax.psum(jnp.concatenate([taps_grad, gains]), ("dp", "seq"))
    return (
        layer_out.reshape(shape3),
        grad_tokens,
        qkv_share,
        out_share,
        up_share,
        down_share,
        small[:KW],
        small[KW],
        small[KW + 1],
    )


def solution(mesh):
    placed = (P("dp", "seq", None), P(), P(), P(), P(), P(), P(), P(), P("dp", "seq", None))
    return jax.shard_map(
        per_device,
        mesh=mesh,
        in_specs=placed,
        out_specs=(
            P("dp", "seq", None),
            P("dp", "seq", None),
            P("dp", "seq"),
            P("dp", "seq"),
            P("dp", "seq"),
            P("dp", "seq"),
            P(),
            P(),
            P(),
        ),
        check_vma=False,
    )
```

```python
import functools

import jax
import jax.numpy as jnp
from jax import lax
from jax.experimental import pallas as pl
from jax.experimental.pallas import tpu as pltpu
from jax.sharding import PartitionSpec as P

H = 12
E = 64
M = 64
KW = 33
RIM = KW // 2
NEWTON = 6

f32 = jnp.float32
bf16 = jnp.bfloat16
epsilon = 1e-05
root_half = 0.7071067811865476
inv_root_two_pi = 0.3989422804014327
MB = 1 << 20

ERFC_P = 0.39
ERFC_C = (
    0.23532530842493793,
    0.09138785409700201,
    0.6495607954603394,
    -0.6354020079402325,
    0.8866654334206034,
    -0.22753738516480188,
)


def dot(a, b):
    return lax.dot_general(a, b, (((1,), (0,)), ((), ())), preferred_element_type=f32)


def dot_nt(a, b):
    return lax.dot_general(a, b, (((1,), (1,)), ((), ())), preferred_element_type=f32)


def dot_tn(a, b):
    return lax.dot_general(a, b, (((0,), (0,)), ((), ())), preferred_element_type=f32)


def lane_group(shape):
    return lax.broadcasted_iota(jnp.int32, shape, len(shape) - 1) // E


def group_masks(shape, count, dtype):
    groups = lane_group(shape)
    return [(groups == h).astype(f32).astype(dtype) for h in range(count)]


def block_diag(x, masks):
    return jnp.concatenate([x * m for m in masks], axis=0)


def diag_blocks(n, masks):
    return sum(n[E * h : E * h + E] * m for h, m in enumerate(masks))


def params(limit=None, **kw):
    return pltpu.CompilerParams(vmem_limit_bytes=limit, **kw)


MESH = pl.DeviceIdType.MESH
ANY = pl.BlockSpec(memory_space=pl.ANY)


def seq_place():
    return lax.axis_index("seq"), lax.axis_size("seq")


def seq_peers():
    me, count = seq_place()
    return [(o, lax.rem(me + o, count)) for o in range(1, count)]


def greet(extra=()):
    barrier = pltpu.get_barrier_semaphore()
    targets = [{"seq": peer} for _, peer in seq_peers()] + list(extra)
    for target in targets:
        pl.semaphore_signal(barrier, inc=1, device_id=target, device_id_type=MESH)
    pl.semaphore_wait(barrier, len(targets))


def remote(src, dst, send, recv, target):
    return pltpu.make_async_remote_copy(
        src_ref=src, dst_ref=dst, send_sem=send, recv_sem=recv, device_id=target, device_id_type=MESH
    )


def swap_copies(src, dst, own, sems):
    me, count = seq_place()
    copies = [
        remote(src.at[pl.ds(peer * own, own)], dst.at[me], sems.at[0, o], sems.at[1, o], {"seq": peer})
        for o, peer in seq_peers()
    ]
    return copies, pltpu.make_async_copy(src.at[pl.ds(me * own, own)], dst.at[me], sems.at[0, 0])


def spread_copies(src, dst, own, sems):
    me, count = seq_place()
    at = dst.at[pl.ds(me * own, own)]
    copies = [
        remote(src, at, sems.at[0, o], sems.at[1, o], {"seq": peer}) for o, peer in seq_peers()
    ]
    return copies, pltpu.make_async_copy(src, at, sems.at[0, 0])


def begin(pair):
    for copy in pair[0]:
        copy.start()
    pair[1].start()


def finish(pair):
    for copy in pair[0]:
        copy.wait()
    pair[1].wait()


def rank_sems():
    return pltpu.SemaphoreType.DMA((2, lax.axis_size("seq")))


def project_kernel(
    tok_ref, w_ref, q_ref, k_ref, v_ref, land_out, rim_out, land, rim, send, recv, local, rim_send, rim_recv,
    rim_local,
):
    step = pl.program_id(0)
    seqs = pl.num_programs(0)
    me, count = seq_place()
    rows, features = tok_ref.shape[1:]
    marks = land.shape[2]
    seg = rows // marks

    @pl.when(step == 0)
    def _():
        greet()

    x = tok_ref[0]
    row = lax.broadcasted_iota(jnp.int32, (marks, rows), 0)
    col = lax.broadcasted_iota(jnp.int32, (marks, rows), 1)
    mean = jnp.where(col // seg == row, 1.0 / seg, 0.0).astype(bf16)
    for part, out in enumerate((q_ref, k_ref, v_ref)):
        for c in range(0, features, 256):
            p = dot(x, w_ref[:, part * features + c : part * features + c + 256])
            if part == 0:
                p = 0.125 * p
            low = p.astype(bf16)
            out[0, :, c : c + 256] = low
            if part < 2:
                land[step, part, :, c : c + 256] = dot(mean, low).astype(bf16)
            else:
                rim[step, 0, :, c : c + 256] = low[rows - RIM :]
                rim[step, 1, :, c : c + 256] = low[:RIM]

    def copies(s):
        spot = land_out.at[s, :, pl.ds(me * marks, marks)]
        sends = [
            remote(land.at[s], spot, send.at[s, o], recv.at[s, o], {"seq": peer}) for o, peer in seq_peers()
        ]
        return sends, pltpu.make_async_copy(land.at[s], spot, local.at[s])

    def rim_copy(s, side):
        there = lax.rem(me + (1 if side == 0 else count - 1), count)
        return remote(
            rim.at[s, side], rim_out.at[s, side], rim_send.at[s, side], rim_recv.at[s, side], {"seq": there}
        )

    begin(copies(step))
    for side in range(2):
        rim_copy(step, side).start()

    @pl.when(step == seqs - 1)
    def _():
        def drain(s, carry):
            finish(copies(s))
            for side in range(2):
                rim_copy(s, side).wait()
            return carry

        lax.fori_loop(0, seqs, drain, 0)


def project(tokens, w_qkv, marks):
    seqs, rows, features = tokens.shape
    ranks = lax.axis_size("seq")
    full = pl.BlockSpec((1, rows, features), lambda s: (s, 0, 0))
    dma = pltpu.SemaphoreType.DMA
    return pl.pallas_call(
        project_kernel,
        grid=(seqs,),
        in_specs=[full, pl.BlockSpec(w_qkv.shape, lambda s: (0, 0), pipeline_mode=pl.Buffered(1))],
        out_specs=[full] * 3 + [ANY] * 2,
        out_shape=[jax.ShapeDtypeStruct(tokens.shape, bf16)] * 3
        + [
            jax.ShapeDtypeStruct((seqs, 2, M, features), bf16),
            jax.ShapeDtypeStruct((seqs, 2, RIM, features), bf16),
        ],
        scratch_shapes=[
            pltpu.VMEM((seqs, 2, marks, features), bf16), pltpu.VMEM((seqs, 2, RIM, features), bf16),
            dma((seqs, ranks)), dma((seqs, ranks)), dma((seqs,)), dma((seqs, 2)), dma((seqs, 2)), dma((seqs,)),
        ],
        compiler_params=params(48 * MB, collective_id=0, has_side_effects=True),
        name="project",
    )(tokens, w_qkv)


def fill_pad(pad, x_ref, rim_ref):
    rows = x_ref.shape[1]
    me, count = seq_place()
    pad[0:RIM, :] = jnp.where(me > 0, rim_ref[0, 0].astype(f32), 0.0)
    pad[RIM : RIM + rows, :] = x_ref[0].astype(f32)
    pad[RIM + rows : RIM + rows + RIM, :] = jnp.where(me < count - 1, rim_ref[0, 1].astype(f32), 0.0)


def conv_tile(v_ref, rim_ref, f_ref, o_ref, pad):
    rows = v_ref.shape[1]
    fill_pad(pad, v_ref, rim_ref)
    for c in range(0, rows, 64):
        acc = jnp.zeros((64, 128), f32)
        for j in range(KW):
            acc = acc + f_ref[j : j + 1, :] * pad[c + j : c + j + 64, :]
        o_ref[0, c : c + 64, :] = acc.astype(bf16)


def conv_specs(rows, first_step, first_group, groups):
    at = lambda i: jnp.maximum(i - first_step, 0)
    seq = lambda i: at(i) // groups
    group = lambda i: at(i) % groups
    return (
        pl.BlockSpec((1, rows, 128), lambda i: (seq(i), 0, first_group + group(i))),
        pl.BlockSpec((1, 2, RIM, 128), lambda i: (seq(i), 0, 0, first_group + group(i))),
        pl.BlockSpec((KW, 128), lambda i: (0, first_group + group(i))),
        pl.BlockSpec((1, rows, 128), lambda i: (seq(i), 0, group(i))),
    )


def conv_back_kernel(g_ref, rim_ref, v_ref, f_ref, o_ref, gf_ref, pad, facc):
    rows = v_ref.shape[1]
    fill_pad(pad, g_ref, rim_ref)

    @pl.when(pl.program_id(1) == 0)
    def _():
        facc[...] = jnp.zeros_like(facc)

    for c in range(0, rows, 64):
        acc = jnp.zeros((64, 128), f32)
        vals = v_ref[0, c : c + 64, :].astype(f32)
        for j in range(KW):
            moved = pad[c + 2 * RIM - j : c + 2 * RIM - j + 64, :]
            acc = acc + f_ref[j : j + 1, :] * moved
            facc[8 * j : 8 * j + 8, :] += (vals * moved).reshape(8, 8, 128).sum(0)
        o_ref[0, c : c + 64, :] = acc.astype(bf16)

    @pl.when(pl.program_id(1) == pl.num_programs(1) - 1)
    def _():
        gf_ref[...] = facc[...].reshape(KW, 8, 128).sum(1)


def conv_back(g, rim, v, taps):
    seqs, rows, features = v.shape
    sp = lambda n: pl.BlockSpec((1, n, 128), lambda g, s: (s, 0, g))
    fs = pl.BlockSpec((KW, 128), lambda g, s: (0, g))
    return pl.pallas_call(
        conv_back_kernel,
        grid=(features // 128, seqs),
        in_specs=[sp(rows), pl.BlockSpec((1, 2, RIM, 128), lambda g, s: (s, 0, 0, g)), sp(rows), fs],
        out_specs=[sp(rows), fs],
        out_shape=[jax.ShapeDtypeStruct(v.shape, bf16), jax.ShapeDtypeStruct((KW, features), f32)],
        scratch_shapes=[pltpu.VMEM((rows + 2 * RIM, 128), f32), pltpu.VMEM((KW * 8, 128), f32)],
        name="conv_back",
    )(g, rim, v, taps)


def score_step(step, q_ref, k_ref, v_ref, land_ref, w_ref, p_ref, num_ref, stat_ref):
    rows, features = q_ref.shape[1:]
    pairs = features // 128
    masks = group_masks((M, 4 * E), 4, bf16)
    masks_wide = group_masks((M, 4 * E), 4, f32)
    ones = jnp.where(
        lane_group((4 * E, 4 * E)) == lax.broadcasted_iota(jnp.int32, (4 * E, 4 * E), 0) // E, 1.0, 0.0
    ).astype(bf16)
    chunk = min(128, rows)
    upper = lax.broadcasted_iota(jnp.int32, (chunk, 2 * E), 1) >= E
    for g in range(features // 256):
        sl = slice(256 * g, 256 * g + 256)
        s3 = dot_nt(k_ref[0, :, sl], block_diag(land_ref[0, 0, :, sl], masks))
        peak = jnp.max(s3, axis=0, keepdims=True)
        e3 = jnp.exp(s3 - peak)
        total = jnp.sum(e3, axis=0, keepdims=True)
        low = e3.astype(bf16)
        w_ref[0, :, sl] = low
        num = diag_blocks(dot_tn(low, v_ref[0, :, sl]), masks_wide).astype(bf16)
        for i in range(2):
            lanes = slice(128 * i, 128 * i + 128)
            num_ref[step * pairs + 2 * g + i] = num[:, lanes]
            stat_ref[step * pairs + 2 * g + i] = jnp.concatenate(
                [peak[:, lanes], total[:, lanes], jnp.zeros((6, 128), f32)], axis=0
            )
        kd = block_diag(land_ref[0, 1, :, sl], masks)
        for r in range(0, rows, chunk):
            s1 = dot_nt(q_ref[0, r : r + chunk, sl], kd)
            parts = []
            for i in range(2):
                x = s1[:, 128 * i : 128 * i + 128]
                top_a = jnp.max(jnp.where(upper, -jnp.inf, x), axis=1, keepdims=True)
                top_b = jnp.max(jnp.where(upper, x, -jnp.inf), axis=1, keepdims=True)
                parts.append(jnp.exp(x - jnp.where(upper, top_b, top_a)))
            e1 = jnp.concatenate(parts, axis=1)
            p_ref[0, r : r + chunk, sl] = (e1 / dot(e1.astype(bf16), ones)).astype(bf16)


def scores_kernel(
    seqs, q_ref, k_ref, v_ref, land_ref, cv_ref, rim_ref, f_ref, w_ref, p_ref, co_ref, num_out, stat_out,
    num, stat, pad, num_sems, stat_sems,
):
    step = pl.program_id(0)
    steps = pl.num_programs(0)
    own = num_out.shape[1]
    pairs = q_ref.shape[2] // 128

    @pl.when(step == 0)
    def _():
        greet()
        if num.shape[0] > seqs * pairs:
            num[seqs * pairs :] = jnp.zeros_like(num[seqs * pairs :])
            stat[seqs * pairs :] = jnp.zeros_like(stat[seqs * pairs :])

    @pl.when(step < seqs)
    def _():
        score_step(step, q_ref, k_ref, v_ref, land_ref, w_ref, p_ref, num, stat)

    @pl.when(step == seqs - 1)
    def _():
        begin(swap_copies(num, num_out, own, num_sems))
        begin(swap_copies(stat, stat_out, own, stat_sems))

    @pl.when(step >= seqs)
    def _():
        conv_tile(cv_ref, rim_ref, f_ref, co_ref, pad)

    @pl.when(step == steps - 1)
    def _():
        finish(swap_copies(num, num_out, own, num_sems))
        finish(swap_copies(stat, stat_out, own, stat_sems))


def scores(q, k, v, land, rim, taps, own, groups):
    seqs, rows, features = q.shape
    ranks = lax.axis_size("seq")
    here = lambda i: jnp.minimum(i, seqs - 1)
    full = pl.BlockSpec((1, rows, features), lambda i: (here(i), 0, 0))
    cv, rims, ft, co = conv_specs(rows, seqs, 0, groups)
    return pl.pallas_call(
        functools.partial(scores_kernel, seqs),
        grid=(seqs + seqs * groups,),
        in_specs=[full] * 3
        + [pl.BlockSpec((1, 2, M, features), lambda i: (here(i), 0, 0, 0)), cv, rims, ft],
        out_specs=[full] * 2 + [co, ANY, ANY],
        out_shape=[jax.ShapeDtypeStruct(q.shape, bf16)] * 2
        + [
            jax.ShapeDtypeStruct((seqs, rows, 128 * groups), bf16),
            jax.ShapeDtypeStruct((ranks, own, M, 128), bf16),
            jax.ShapeDtypeStruct((ranks, own, 8, 128), f32),
        ],
        scratch_shapes=[
            pltpu.VMEM((ranks * own, M, 128), bf16), pltpu.VMEM((ranks * own, 8, 128), f32),
            pltpu.VMEM((rows + 2 * RIM, 128), f32), rank_sems(), rank_sems(),
        ],
        compiler_params=params(48 * MB, collective_id=1, has_side_effects=True),
        name="scores",
    )(q, k, v, land, v, rim, taps)


def split(x):
    hi = x.astype(bf16)
    return hi, (x - hi.astype(f32)).astype(bf16)


def stack_parts(xs, axis):
    return jnp.concatenate([part for x in xs for part in split(x)], axis=axis)


def pair_sums(out, count):
    top = lambda i, j: out[128 * i + 64 * j : 128 * i + 64 * j + 64]
    return [
        top(i, 0)[:, :128] + (top(i, 0)[:, 128:] + top(i, 1)[:, :128]) for i in range(count)
    ]


def pair_nn(lefts, right, masks):
    hi, lo = split(right)
    packed = jnp.concatenate([block_diag(hi, masks), block_diag(lo, masks)], axis=1)
    return pair_sums(dot(stack_parts(lefts, 0), packed), len(lefts))


def pair_nt(lefts, right, masks):
    hi, lo = split(right)
    packed = jnp.concatenate([block_diag(hi, masks), block_diag(lo, masks)], axis=0)
    return pair_sums(dot_nt(stack_parts(lefts, 0), packed), len(lefts))


def pair_tn(left, rights, masks_wide):
    out = dot_tn(stack_parts([left], 1), stack_parts(rights, 1))
    results = []
    for i in range(len(rights)):
        full = out[:128, 256 * i : 256 * i + 128] + (
            out[:128, 256 * i + 128 : 256 * i + 256] + out[128:, 256 * i : 256 * i + 128]
        )
        results.append(diag_blocks(full, masks_wide))
    return results


def half_reduce(x, upper, op, fill):
    a = op(jnp.where(upper, fill, x), axis=1, keepdims=True)
    b = op(jnp.where(upper, x, fill), axis=1, keepdims=True)
    return jnp.where(upper, b, a)


def to_column(row, same, upper):
    return half_reduce(jnp.where(same, row, 0.0), upper, jnp.sum, 0.0)


def to_row(col, same):
    return jnp.sum(jnp.where(same, col, 0.0), axis=0, keepdims=True)


def pair_consts():
    lane = lax.broadcasted_iota(jnp.int32, (M, 128), 1)
    row = lax.broadcasted_iota(jnp.int32, (M, 128), 0)
    return lane >= E, row == lane % E, group_masks((M, 128), 2, bf16), group_masks((M, 128), 2, f32)


def own_pair(land_ref, i, own):
    me, _ = seq_place()
    per = land_ref.shape[2] // 128
    p = jnp.minimum(me * own + i, land_ref.shape[0] * per - 1)
    return land_ref[p // per, :, pl.ds(pl.multiple_of((p % per) * 128, 128), 128)]


def inverse_step(
    num_ref, stat_ref, land_ref, mixed_ref, sum_ref, mid_ref, z_ref, p_ref, a_ref, w_ref,
    scale_ref, tot_ref, alpha_ref,
):
    ranks, own = num_ref.shape[:2]
    upper, same, masks, masks_wide = pair_consts()
    for i in range(own):
        peak = stat_ref[0, i, 0:1, :]
        for r in range(1, ranks):
            peak = jnp.maximum(peak, stat_ref[r, i, 0:1, :])
        total = jnp.zeros((1, 128), f32)
        numer = jnp.zeros((M, 128), f32)
        for r in range(ranks):
            alpha = jnp.exp(stat_ref[r, i, 0:1, :] - peak)
            total = total + alpha * stat_ref[r, i, 1:2, :]
            column = to_column(alpha, same, upper)
            alpha_ref[r, i] = column
            numer = numer + column * num_ref[r, i].astype(f32)
        total = to_column(total, same, upper)
        tot_ref[i] = total
        sum_ref[i] = numer / total
        ql, kl = own_pair(land_ref.at[:, 0], i, own), own_pair(land_ref.at[:, 1], i, own)
        s2 = dot_nt(ql, block_diag(kl, masks))
        e2 = jnp.exp(s2 - half_reduce(s2, upper, jnp.max, -jnp.inf))
        middle = e2 / half_reduce(e2, upper, jnp.sum, 0.0)
        mid_ref[i] = middle
        st = dot_nt(kl, block_diag(ql, masks))
        et = jnp.exp(st - jnp.max(st, axis=0, keepdims=True))
        flipped = et / jnp.sum(et, axis=0, keepdims=True)
        column = jnp.sum(middle, axis=0, keepdims=True)
        scale = 1.0 / half_reduce(column, upper[0:1], jnp.max, -jnp.inf)
        scale_ref[i] = jnp.broadcast_to(scale, (8, 128))
        z_ref[0, i] = flipped * scale

    def step(it, carry):
        zs = [z_ref[it, i] for i in range(own)]
        ps = [pair_nn([mid_ref[i]], zs[i], masks)[0] for i in range(own)]
        second = [pair_nn([ps[i], zs[i]], ps[i], masks) for i in range(own)]
        for i in range(own):
            p2, a = second[i]
            w = 7.0 * ps[i] - p2
            p_ref[it, i] = ps[i]
            a_ref[it, i] = a
            w_ref[it, i] = w
            z_ref[it + 1, i] = 0.25 * (13.0 * zs[i] - 15.0 * a + pair_nn([a], w, masks)[0])
        return carry

    lax.fori_loop(0, NEWTON, step, 0)
    for i in range(own):
        mixed_ref[i] = pair_nn([z_ref[NEWTON, i]], sum_ref[i], masks)[0].astype(bf16)


def inverse_kernel(
    num_ref, stat_ref, land_ref, cv_ref, rim_ref, f_ref, mixed_out, co_ref, sum_ref, mid_ref, z_ref, p_ref,
    a_ref, w_ref, scale_ref, tot_ref, alpha_ref, mixed, pad, sems,
):
    step = pl.program_id(0)
    own = num_ref.shape[1]

    @pl.when(step == 0)
    def _():
        greet()
        inverse_step(
            num_ref, stat_ref, land_ref, mixed, sum_ref, mid_ref, z_ref, p_ref, a_ref, w_ref, scale_ref,
            tot_ref, alpha_ref,
        )
        begin(spread_copies(mixed, mixed_out, own, sems))

    @pl.when(step > 0)
    def _():
        conv_tile(cv_ref, rim_ref, f_ref, co_ref, pad)

    @pl.when(step == pl.num_programs(0) - 1)
    def _():
        finish(spread_copies(mixed, mixed_out, own, sems))


def inverse(num, stat, land, v, rim, taps, first_group):
    ranks, own = num.shape[:2]
    seqs, rows, features = v.shape
    groups = features // 128 - first_group
    mat = jax.ShapeDtypeStruct((own, M, 128), f32)
    steps = lambda n: jax.ShapeDtypeStruct((n, own, M, 128), f32)
    whole = lambda a: pl.BlockSpec(a.shape, lambda i: (0,) * len(a.shape), pipeline_mode=pl.Buffered(1))
    saved = [
        mat, mat, steps(NEWTON + 1), steps(NEWTON), steps(NEWTON), steps(NEWTON),
        jax.ShapeDtypeStruct((own, 8, 128), f32), mat, steps(ranks),
    ]
    cv, rims, ft, co = conv_specs(rows, 1, first_group, groups)
    return pl.pallas_call(
        inverse_kernel,
        grid=(1 + seqs * groups,),
        in_specs=[whole(num), whole(stat), whole(land), cv, rims, ft],
        out_specs=[ANY, co] + [whole(a) for a in saved],
        out_shape=[
            jax.ShapeDtypeStruct((ranks * own, M, 128), bf16),
            jax.ShapeDtypeStruct((seqs, rows, 128 * groups), bf16),
        ]
        + saved,
        scratch_shapes=[
            pltpu.VMEM((own, M, 128), bf16), pltpu.VMEM((rows + 2 * RIM, 128), f32), rank_sems(),
        ],
        compiler_params=params(48 * MB, collective_id=2, has_side_effects=True),
        name="inverse",
    )(num, stat, land, v, rim, taps)


def inverse_back_kernel(
    land_ref, marks_ref, sum_ref, mid_ref, z_ref, p_ref, a_ref, w_ref, scale_ref, tot_ref,
    alpha_ref, gn_ref, gt_ref, mq_ref, mk_ref, g_ref, dk_ref,
):
    ranks, own = land_ref.shape[:2]
    upper, same, masks, masks_wide = pair_consts()
    for i in range(own):
        land = land_ref[0, i].astype(f32)
        for r in range(1, ranks):
            land = land + land_ref[r, i].astype(f32)
        summary, total = sum_ref[i], tot_ref[i]
        gs = pair_tn(z_ref[NEWTON, i], [land], masks_wide)[0].astype(bf16).astype(f32)
        gn = (gs / total).astype(bf16).astype(f32)
        gt = -half_reduce(gs * summary, upper, jnp.sum, 0.0) / total
        for r in range(ranks):
            gn_ref[r, i] = (alpha_ref[r, i] * gn).astype(bf16)
            gt_ref[r, i] = jnp.broadcast_to(to_row(alpha_ref[r, i] * gt, same), (8, 128))
        g_ref[i] = pair_nt([land], summary, masks)[0]
        dk_ref[i] = jnp.zeros((M, 128), f32)

    def step(back, carry):
        it = NEWTON - 1 - back
        gs = [g_ref[i] for i in range(own)]
        das, dws = [], []
        for i in range(own):
            das.append(0.25 * (pair_nt([gs[i]], w_ref[it, i], masks)[0] - 15.0 * gs[i]))
            dws.append(0.25 * pair_tn(a_ref[it, i], [gs[i]], masks_wide)[0])
        dps, parts = [], []
        for i in range(own):
            right = pair_nt([dws[i], das[i]], p_ref[it, i], masks)
            left = pair_tn(p_ref[it, i], [dws[i]], masks_wide)[0]
            dps.append(7.0 * dws[i] - right[0] - left + pair_tn(z_ref[it, i], [das[i]], masks_wide)[0])
            parts.append(3.25 * gs[i] + right[1])
        for i in range(own):
            g_ref[i] = parts[i] + pair_tn(mid_ref[i], [dps[i]], masks_wide)[0]
            dk_ref[i] += pair_nt([dps[i]], z_ref[it, i], masks)[0]
        return carry

    lax.fori_loop(0, NEWTON, step, 0)
    eye = jnp.where(same, 1.0, 0.0).astype(bf16)
    for i in range(own):
        g, middle, scale = g_ref[i], mid_ref[i], scale_ref[i, 0:1, :]
        turned = dot_tn(stack_parts([g], 1), eye)
        turned = diag_blocks(turned[:128] + turned[128:], masks_wide)
        column = jnp.sum(middle, axis=0, keepdims=True)
        top = half_reduce(column, upper[0:1], jnp.max, -jnp.inf)
        hit = jnp.where(column == top, 1.0, 0.0)
        share = hit / half_reduce(hit, upper[0:1], jnp.sum, 0.0)
        d_scale = half_reduce(jnp.sum(turned * middle, axis=0, keepdims=True), upper[0:1], jnp.sum, 0.0)
        dk = dk_ref[i] + turned * scale - share * (d_scale * scale * scale)
        ds = middle * (dk - half_reduce(middle * dk, upper, jnp.sum, 0.0))
        hi, lo = split(ds)
        both = dot(jnp.concatenate([hi, lo], axis=0), block_diag(own_pair(marks_ref.at[:, 1], i, own), masks))
        mq_ref[i] = both[:M] + both[M:]
        turned = dot_tn(jnp.concatenate([hi, lo], axis=1), own_pair(marks_ref.at[:, 0], i, own))
        mk_ref[i] = diag_blocks(turned[:128] + turned[128:], masks_wide)


def inverse_back(land, marks, saved):
    ranks, own = land.shape[:2]
    mat = jax.ShapeDtypeStruct((own, M, 128), f32)
    return pl.pallas_call(
        inverse_back_kernel,
        out_shape=[
            jax.ShapeDtypeStruct((ranks, own, M, 128), bf16),
            jax.ShapeDtypeStruct((ranks, own, 8, 128), f32), mat, mat,
        ],
        scratch_shapes=[pltpu.VMEM((own, M, 128), f32)] * 2,
        compiler_params=params(48 * MB),
        name="inverse_back",
    )(land, marks, *saved)


def mean_of(x):
    return jnp.mean(x, axis=-1, keepdims=True)


def gelu_and_slope(u):
    x = jnp.abs(u) * root_half
    t = 1.0 / (1.0 + ERFC_P * x)
    poly = jnp.full_like(t, ERFC_C[-1])
    for c in ERFC_C[-2::-1]:
        poly = poly * t + c
    bell = jnp.exp(-0.5 * u * u)
    half = (0.5 * t) * poly * bell
    cdf = jnp.where(u < 0.0, half, 1.0 - half)
    return u * cdf, cdf + u * bell * inv_root_two_pi


def row_kernel(
    tok_ref, p_ref, conv_a_ref, conv_b_ref, mix_ref, top_ref, w_out_ref, w_up_ref, w_down_ref, ga_ref, gf_ref,
    out_ref, proj_ref, gm_ref, wg_ref, gains_ref,
    act, gul, slope, hid_t, gdl_t, mix_t, gpr, resid,
):
    step = pl.program_id(0)
    size, features = tok_ref.shape
    blocks = act.shape[0] // size
    ff = act.shape[1]
    wide = features

    @pl.when(step == 0)
    def _():
        gains_ref[...] = jnp.zeros_like(gains_ref)

    @pl.when(step < blocks)
    def _():
        start = pl.multiple_of(step * size, size)
        rows = pl.ds(start, size)
        masks = group_masks((M, 4 * E), 4, bf16)
        for g in range(features // 256):
            sl = slice(256 * g, 256 * g + 256)
            att = dot(p_ref[:, sl], block_diag(mix_ref[0, :, sl], masks))
            resid[:, sl] = att
        half = conv_a_ref.shape[1]
        resid[:, :half] += conv_a_ref[...].astype(f32)
        resid[:, half:] += conv_b_ref[...].astype(f32)
        mixed = resid[...].astype(bf16)
        mix_t[:, rows] = mixed.T
        residual = tok_ref[...].astype(f32) + dot(mixed, w_out_ref[...])
        centre = residual - mean_of(residual)
        s_att = lax.rsqrt(mean_of(centre * centre) + epsilon)
        normed = centre * s_att
        gain_att = ga_ref[...]
        hidden = normed * gain_att
        hid_low = hidden.astype(bf16)
        hid_t[:, rows] = hid_low.T
        down = jnp.zeros((size, features), f32)
        for j in range(0, ff, wide):
            up = dot(hid_low, w_up_ref[:, j : j + wide])
            a, sl = gelu_and_slope(up)
            low = a.astype(bf16)
            act[rows, j : j + wide] = low
            slope[:, j : j + wide] = sl.astype(bf16)
            down = down + dot(low, w_down_ref[j : j + wide, :])
        residual_two = hidden + down
        centre_two = residual_two - mean_of(residual_two)
        s_ffn = lax.rsqrt(mean_of(centre_two * centre_two) + epsilon)
        normed_two = centre_two * s_ffn
        gain_ffn = gf_ref[...]
        out_ref[...] = (normed_two * gain_ffn).astype(bf16)
        top = top_ref[...].astype(f32)
        gains_ref[8:16, :] += (top * normed_two).reshape(size // 8, 8, features).sum(0)
        g = top * gain_ffn
        grad_two = s_ffn * (g - mean_of(g) - normed_two * mean_of(g * normed_two))
        gdl = grad_two.astype(bf16)
        gdl_t[:, rows] = gdl.T
        back = jnp.zeros((size, features), f32)
        for j in range(0, ff, wide):
            gu = dot_nt(gdl, w_down_ref[j : j + wide, :]) * slope[:, j : j + wide].astype(f32)
            low = gu.astype(bf16)
            gul[rows, j : j + wide] = low
            back = back + dot_nt(low, w_up_ref[:, j : j + wide])
        grad_hidden = grad_two + back
        gains_ref[0:8, :] += (grad_hidden * normed).reshape(size // 8, 8, features).sum(0)
        g = grad_hidden * gain_att
        proj = (s_att * (g - mean_of(g) - normed * mean_of(g * normed))).astype(bf16)
        proj_ref[...] = proj
        gpr[rows, :] = proj
        gm_ref[...] = dot_nt(proj, w_out_ref[...]).astype(bf16)

    chunks = ff // wide
    for first, left, right in ((0, hid_t, gul), (chunks, gdl_t, act), (2 * chunks, mix_t, gpr)):
        count = chunks if first < 2 * chunks else 1

        @pl.when((step >= blocks + first) & (step < blocks + first + count))
        def _(first=first, left=left, right=right):
            base = (step - blocks - first) * wide
            for c in range(0, wide, 256):
                cols = pl.ds(pl.multiple_of(base + c, 256), 256)
                wg_ref[0, :, c : c + 256] = dot(left[...], right[:, cols]).astype(bf16)


def row_pass(tokens, probs, conv_a, conv_b, mixed, grad_out, w_out, w_up, w_down, gain_att, gain_ffn):
    seqs, rows, features = tokens.shape
    ff = w_up.shape[1]
    size = min(256, rows)
    total = seqs * rows
    blocks = total // size
    grads = 2 * (ff // features) + 1
    here = lambda i: jnp.minimum(i, blocks - 1)
    block = pl.BlockSpec((size, features), lambda i: (here(i), 0))
    whole = lambda a: pl.BlockSpec(a.shape, lambda i: (0,) * a.ndim, pipeline_mode=pl.Buffered(1))
    flat = lambda a: a.reshape(total, a.shape[2])
    part = lambda a: pl.BlockSpec((size, a.shape[2]), lambda i: (here(i), 0))
    gains = [gain_att.reshape(1, features), gain_ffn.reshape(1, features)]
    row_out = jax.ShapeDtypeStruct((total, features), bf16)
    tall = pltpu.VMEM((features, total), bf16)
    return pl.pallas_call(
        row_kernel,
        grid=(blocks + grads,),
        in_specs=[
            block, block, part(conv_a), part(conv_b),
            pl.BlockSpec((1, M, features), lambda i: (here(i) * size // rows, 0, 0)),
            block, whole(w_out), whole(w_up), whole(w_down), whole(gains[0]), whole(gains[1]),
        ],
        out_specs=[block] * 3
        + [
            pl.BlockSpec((1, features, features), lambda i: (jnp.maximum(i - blocks, 0), 0, 0)),
            pl.BlockSpec((16, features), lambda i: (0, 0)),
        ],
        out_shape=[row_out] * 3
        + [
            jax.ShapeDtypeStruct((grads, features, features), bf16),
            jax.ShapeDtypeStruct((16, features), f32),
        ],
        scratch_shapes=[
            pltpu.VMEM((total, ff), bf16), pltpu.VMEM((total, ff), bf16), pltpu.VMEM((size, ff), bf16),
            tall, tall, tall, pltpu.VMEM((total, features), bf16), pltpu.VMEM((size, features), f32),
        ],
        compiler_params=params(60 * MB),
        name="row_pass",
    )(flat(tokens), flat(probs), flat(conv_a), flat(conv_b), mixed, flat(grad_out), w_out, w_up, w_down, *gains)


def first_back_kernel(gm_ref, p_ref, q_ref, mix_ref, kl_ref, land_ref, gq_ref, klp_ref):
    features = gm_ref.shape[2]
    masks = group_masks((M, 4 * E), 4, bf16)
    masks_wide = group_masks((M, 4 * E), 4, f32)
    ones = jnp.where(
        lane_group((4 * E, 4 * E)) == lax.broadcasted_iota(jnp.int32, (4 * E, 4 * E), 0) // E, 1.0, 0.0
    ).astype(bf16)
    for g in range(features // 256):
        sl = slice(256 * g, 256 * g + 256)
        gm, p = gm_ref[0, :, sl], p_ref[0, :, sl]
        land = diag_blocks(dot_tn(p, gm), masks_wide).astype(bf16)
        for i in range(2):
            land_ref[2 * g + i] = land[:, 128 * i : 128 * i + 128]
        d = dot_nt(gm, block_diag(mix_ref[0, :, sl], masks))
        pw = p.astype(f32)
        gs = (pw * (d - dot((pw * d).astype(bf16), ones))).astype(bf16)
        gq_ref[0, :, sl] = dot(gs, block_diag(kl_ref[0, :, sl], masks)).astype(bf16)
        klp_ref[0, :, sl] = diag_blocks(dot_tn(gs, q_ref[0, :, sl]), masks_wide)


def first_back(gm, probs, q, mixed, k_land):
    seqs, rows, features = q.shape
    pairs = features // 128
    full = pl.BlockSpec((1, rows, features), lambda s: (s, 0, 0))
    land = pl.BlockSpec((1, M, features), lambda s: (s, 0, 0))
    return pl.pallas_call(
        first_back_kernel,
        grid=(seqs,),
        in_specs=[full] * 3 + [land] * 2,
        out_specs=[pl.BlockSpec((pairs, M, 128), lambda s: (s, 0, 0)), full, land],
        out_shape=[
            jax.ShapeDtypeStruct((seqs * pairs, M, 128), bf16),
            jax.ShapeDtypeStruct(q.shape, bf16),
            jax.ShapeDtypeStruct((seqs, M, features), f32),
        ],
        compiler_params=params(48 * MB),
        name="first_back",
    )(gm, probs, q, mixed, k_land)


def third_back_kernel(w_ref, v_ref, k_ref, gc_ref, gn_ref, gt_ref, ql_ref, gv_ref, gk_ref, qlp_ref):
    features = w_ref.shape[2]
    masks = group_masks((M, 4 * E), 4, bf16)
    masks_wide = group_masks((M, 4 * E), 4, f32)
    for g in range(features // 256):
        sl = slice(256 * g, 256 * g + 256)
        w = w_ref[0, :, sl]
        gn = jnp.concatenate([gn_ref[2 * g], gn_ref[2 * g + 1]], axis=1)
        gt = jnp.concatenate([gt_ref[2 * g, 0:1, :], gt_ref[2 * g + 1, 0:1, :]], axis=1)
        gd = block_diag(gn, masks)
        gs = (w.astype(f32) * (dot_nt(v_ref[0, :, sl], gd) + gt)).astype(bf16)
        gv_ref[0, :, sl] = (dot(w, gd) + gc_ref[0, :, sl].astype(f32)).astype(bf16)
        gk_ref[0, :, sl] = dot(gs, block_diag(ql_ref[0, :, sl], masks)).astype(bf16)
        qlp_ref[0, :, sl] = diag_blocks(dot_tn(gs, k_ref[0, :, sl]), masks_wide)


def third_back(w, v, k, grad_conv, gn, gt, q_land):
    seqs, rows, features = v.shape
    pairs = features // 128
    full = pl.BlockSpec((1, rows, features), lambda s: (s, 0, 0))
    land = pl.BlockSpec((1, M, features), lambda s: (s, 0, 0))
    return pl.pallas_call(
        third_back_kernel,
        grid=(seqs,),
        in_specs=[full] * 4
        + [
            pl.BlockSpec((pairs, M, 128), lambda s: (s, 0, 0)),
            pl.BlockSpec((pairs, 8, 128), lambda s: (s, 0, 0)),
            land,
        ],
        out_specs=[full, full, land],
        out_shape=[jax.ShapeDtypeStruct(v.shape, bf16)] * 2
        + [jax.ShapeDtypeStruct((seqs, M, features), f32)],
        compiler_params=params(48 * MB),
        name="third_back",
    )(w, v, k, grad_conv, gn, gt, q_land)


def last_kernel(tok_ref, gq_ref, gk_ref, gv_ref, qo_ref, ko_ref, proj_ref, w_ref, gt_ref, wg_ref, d, tok_t):
    step = pl.program_id(0)
    seqs = tok_t.shape[1] // tok_ref.shape[1]
    rows, features = tok_ref.shape[1:]
    marks = qo_ref.shape[1]
    seg = rows // marks

    @pl.when(step < seqs)
    def _():
        here = pl.ds(pl.multiple_of(step * rows, rows), rows)
        for part, (core, own) in enumerate(((gq_ref, qo_ref), (gk_ref, ko_ref))):
            for m in range(marks):
                at = pl.ds(pl.multiple_of(step * rows + m * seg, seg), seg)
                x = core[0, m * seg : m * seg + seg, :].astype(f32) + own[0, m : m + 1, :] * (1.0 / seg)
                x = x.astype(bf16)
                if part == 0:
                    x = x * jnp.asarray(0.125, bf16)
                d[at, part * features : part * features + features] = x
        d[here, 2 * features :] = gv_ref[0]
        tok_t[:, here] = tok_ref[0].T
        for c in range(0, rows, 128):
            at = pl.ds(pl.multiple_of(step * rows + c, 128), 128)
            gt_ref[0, c : c + 128, :] = (
                proj_ref[0, c : c + 128, :].astype(f32) + dot_nt(d[at, :], w_ref[...])
            ).astype(bf16)

    @pl.when(step >= seqs)
    def _():
        base = (step - seqs) * features
        for c in range(0, features, 256):
            cols = pl.ds(pl.multiple_of(base + c, 256), 256)
            wg_ref[0, :, c : c + 256] = dot(tok_t[...], d[:, cols]).astype(bf16)


def last_pass(tokens, gq, gk, gv, q_own, k_own, proj, w_qkv):
    seqs, rows, features = tokens.shape
    marks = q_own.shape[1]
    here = lambda i: jnp.minimum(i, seqs - 1)
    full = pl.BlockSpec((1, rows, features), lambda i: (here(i), 0, 0))
    land = pl.BlockSpec((1, marks, features), lambda i: (here(i), 0, 0))
    return pl.pallas_call(
        last_kernel,
        grid=(seqs + 3,),
        in_specs=[full] * 4 + [land] * 2
        + [full, pl.BlockSpec(w_qkv.shape, lambda i: (0, 0), pipeline_mode=pl.Buffered(1))],
        out_specs=[full, pl.BlockSpec((1, features, features), lambda i: (jnp.maximum(i - seqs, 0), 0, 0))],
        out_shape=[
            jax.ShapeDtypeStruct(tokens.shape, bf16),
            jax.ShapeDtypeStruct((3, features, features), bf16),
        ],
        scratch_shapes=[
            pltpu.VMEM((seqs * rows, 3 * features), bf16), pltpu.VMEM((features, seqs * rows), bf16),
        ],
        compiler_params=params(56 * MB),
        name="last_pass",
    )(tokens, gq, gk, gv, q_own, k_own, proj, w_qkv)


def halo(cells, width):
    count = lax.axis_size("seq")
    head, tail = cells[:, :width], cells[:, cells.shape[1] - width :]
    left = lax.ppermute(tail, "seq", [(i, i + 1) for i in range(count - 1)])
    right = lax.ppermute(head, "seq", [(i + 1, i) for i in range(count - 1)])
    return jnp.stack([left, right], axis=1)


def scatter_sum(grad):
    share = lax.psum_scatter(grad, "dp", scatter_dimension=0, tiled=True)
    return lax.psum_scatter(share, "seq", scatter_dimension=1, tiled=True).astype(f32)


def per_device(tokens, w_qkv, w_out, w_up, w_down, conv_filter, gain_att, gain_ffn, grad_out):
    seqs, rows, features = tokens.shape
    ranks = lax.axis_size("seq")
    rank = lax.axis_index("seq")
    marks = M // ranks
    ff = w_up.shape[1]
    pairs = seqs * (features // 128)
    own = -(-pairs // ranks)

    def from_pairs(x):
        x = x[:pairs].reshape(seqs, features // 128, M, 128).transpose(0, 2, 1, 3)
        return x.reshape(seqs, M, features)

    def pad_pairs(x):
        return jnp.pad(x, ((0, ranks * own - pairs),) + ((0, 0),) * (x.ndim - 1))

    def exchange(x):
        out = lax.all_to_all(pad_pairs(x), "seq", 0, 0, tiled=True)
        return out.reshape((ranks, own) + x.shape[1:])

    taps = conv_filter.astype(f32)
    q, k, v, land, v_rim = project(tokens, w_qkv, marks)
    q_land, k_land = land[:, 0], land[:, 1]
    first_group = features // 256
    weights, probs, conv_a, num_parts, stat_parts = scores(q, k, v, land, v_rim, taps, own, first_group)
    mixed_pairs, conv_b, *saved = inverse(num_parts, stat_parts, land, v, v_rim, taps, first_group)
    mixed = from_pairs(mixed_pairs)
    layer_out, proj, gm, wg, gains = row_pass(
        tokens, probs, conv_a, conv_b, mixed, grad_out, w_out, w_up, w_down, gain_att, gain_ffn
    )
    shape3 = (seqs, rows, features)
    gm = gm.reshape(shape3)
    chunks = ff // features
    up_share = scatter_sum(wg[:chunks].transpose(1, 0, 2).reshape(features, ff))
    down_share = scatter_sum(wg[chunks : 2 * chunks].transpose(0, 2, 1).reshape(ff, features))
    out_share = scatter_sum(wg[2 * chunks])
    land_part, gq, k_land_part = first_back(gm, probs, q, mixed, k_land)
    g_rim = halo(gm, RIM)
    land_parts = exchange(land_part)
    grad_conv, taps_grad = conv_back(gm, g_rim, v, taps)
    gn_own, gt_own, mid_q, mid_k = inverse_back(land_parts, land, saved)

    def give_back(x):
        x = x.reshape((ranks * own,) + x.shape[2:])
        return lax.all_to_all(x, "seq", 0, 0, tiled=True)[:pairs]

    grad_values, gk, q_land_part = third_back(
        weights, v, k, grad_conv, give_back(gn_own), give_back(gt_own), q_land
    )

    def place(x):
        full = jnp.zeros((ranks * own, M, 128), f32)
        return from_pairs(lax.dynamic_update_slice_in_dim(full, x, rank * own, 0))

    both = jnp.stack([q_land_part + place(mid_q), k_land_part + place(mid_k)]).astype(bf16)
    both = both.reshape(2, seqs, ranks, marks, features).transpose(2, 0, 1, 3, 4)
    both = lax.all_to_all(both, "seq", 0, 0, tiled=True).astype(f32).sum(0)
    grad_tokens, qkv_grad = last_pass(tokens, gq, gk, grad_values, both[0], both[1], proj.reshape(shape3), w_qkv)
    qkv_share = scatter_sum(qkv_grad.transpose(1, 0, 2).reshape(features, 3 * features))
    gains = gains.reshape(2, 8, features).sum(1)
    small = lax.psum(jnp.concatenate([taps_grad, gains]), ("dp", "seq"))
    return (
        layer_out.reshape(shape3),
        grad_tokens,
        qkv_share,
        out_share,
        up_share,
        down_share,
        small[:KW],
        small[KW],
        small[KW + 1],
    )


def solution(mesh):
    placed = (P("dp", "seq", None), P(), P(), P(), P(), P(), P(), P(), P("dp", "seq", None))
    return jax.shard_map(
        per_device,
        mesh=mesh,
        in_specs=placed,
        out_specs=(
            P("dp", "seq", None),
            P("dp", "seq", None),
            P("dp", "seq"),
            P("dp", "seq"),
            P("dp", "seq"),
            P("dp", "seq"),
            P(),
            P(),
            P(),
        ),
        check_vma=False,
    )
```

```python
import functools

import jax
import jax.numpy as jnp
from jax import lax
from jax.experimental import pallas as pl
from jax.experimental.pallas import tpu as pltpu
from jax.sharding import PartitionSpec as P

H = 12
E = 64
M = 64
KW = 33
RIM = KW // 2
NEWTON = 6

f32 = jnp.float32
bf16 = jnp.bfloat16
epsilon = 1e-05
root_half = 0.7071067811865476
inv_root_two_pi = 0.3989422804014327
MB = 1 << 20

ERFC_P = 0.39
ERFC_C = (
    0.23532530842493793,
    0.09138785409700201,
    0.6495607954603394,
    -0.6354020079402325,
    0.8866654334206034,
    -0.22753738516480188,
)


def dot(a, b):
    return lax.dot_general(a, b, (((1,), (0,)), ((), ())), preferred_element_type=f32)


def dot_nt(a, b):
    return lax.dot_general(a, b, (((1,), (1,)), ((), ())), preferred_element_type=f32)


def dot_tn(a, b):
    return lax.dot_general(a, b, (((0,), (0,)), ((), ())), preferred_element_type=f32)


def lane_group(shape):
    return lax.broadcasted_iota(jnp.int32, shape, len(shape) - 1) // E


def group_masks(shape, count, dtype):
    groups = lane_group(shape)
    return [(groups == h).astype(f32).astype(dtype) for h in range(count)]


def block_diag(x, masks):
    return jnp.concatenate([x * m for m in masks], axis=0)


def diag_blocks(n, masks):
    return sum(n[E * h : E * h + E] * m for h, m in enumerate(masks))


def params(limit=None, **kw):
    return pltpu.CompilerParams(vmem_limit_bytes=limit, **kw)


MESH = pl.DeviceIdType.MESH
ANY = pl.BlockSpec(memory_space=pl.ANY)


def seq_place():
    return lax.axis_index("seq"), lax.axis_size("seq")


def seq_peers():
    me, count = seq_place()
    return [(o, lax.rem(me + o, count)) for o in range(1, count)]


def greet(extra=()):
    barrier = pltpu.get_barrier_semaphore()
    targets = [{"seq": peer} for _, peer in seq_peers()] + list(extra)
    for target in targets:
        pl.semaphore_signal(barrier, inc=1, device_id=target, device_id_type=MESH)
    pl.semaphore_wait(barrier, len(targets))


def remote(src, dst, send, recv, target):
    return pltpu.make_async_remote_copy(
        src_ref=src, dst_ref=dst, send_sem=send, recv_sem=recv, device_id=target, device_id_type=MESH
    )


def swap_copies(src, dst, own, sems):
    me, count = seq_place()
    copies = [
        remote(src.at[pl.ds(peer * own, own)], dst.at[me], sems.at[0, o], sems.at[1, o], {"seq": peer})
        for o, peer in seq_peers()
    ]
    return copies, pltpu.make_async_copy(src.at[pl.ds(me * own, own)], dst.at[me], sems.at[0, 0])


def spread_copies(src, dst, own, sems):
    me, count = seq_place()
    at = dst.at[pl.ds(me * own, own)]
    copies = [
        remote(src, at, sems.at[0, o], sems.at[1, o], {"seq": peer}) for o, peer in seq_peers()
    ]
    return copies, pltpu.make_async_copy(src, at, sems.at[0, 0])


def begin(pair):
    for copy in pair[0]:
        copy.start()
    pair[1].start()


def finish(pair):
    for copy in pair[0]:
        copy.wait()
    pair[1].wait()


def swap_rows(src, dst, sems):
    me, _ = seq_place()
    copies = [
        remote(src.at[peer], dst.at[me], sems.at[0, o], sems.at[1, o], {"seq": peer}) for o, peer in seq_peers()
    ]
    return copies, pltpu.make_async_copy(src.at[me], dst.at[me], sems.at[0, 0])


def cube():
    d = lax.axis_index("dp")
    core, x, y = d % 2, (d // 2) % 2, d // 4
    return core, x, y, {"dp": d + 1 - 2 * core}, {"dp": d + 2 - 4 * x}, {"dp": d + 4 - 8 * y}


def add_low(a, b):
    return (a.astype(f32) + b.astype(f32)).astype(bf16)


def rank_sems():
    return pltpu.SemaphoreType.DMA((2, lax.axis_size("seq")))


def project_kernel(
    tok_ref, w_ref, q_ref, k_ref, v_ref, land_out, rim_out, land, rim, send, recv, local, rim_send, rim_recv,
    rim_local,
):
    step = pl.program_id(0)
    seqs = pl.num_programs(0)
    me, count = seq_place()
    rows, features = tok_ref.shape[1:]
    marks = land.shape[2]
    seg = rows // marks

    @pl.when(step == 0)
    def _():
        greet()

    x = tok_ref[0]
    row = lax.broadcasted_iota(jnp.int32, (marks, rows), 0)
    col = lax.broadcasted_iota(jnp.int32, (marks, rows), 1)
    mean = jnp.where(col // seg == row, 1.0 / seg, 0.0).astype(bf16)
    for part, out in enumerate((q_ref, k_ref, v_ref)):
        for c in range(0, features, 256):
            p = dot(x, w_ref[:, part * features + c : part * features + c + 256])
            if part == 0:
                p = 0.125 * p
            low = p.astype(bf16)
            out[0, :, c : c + 256] = low
            if part < 2:
                land[step, part, :, c : c + 256] = dot(mean, low).astype(bf16)
            else:
                rim[step, 0, :, c : c + 256] = low[rows - RIM :]
                rim[step, 1, :, c : c + 256] = low[:RIM]

    def copies(s):
        spot = land_out.at[s, :, pl.ds(me * marks, marks)]
        sends = [
            remote(land.at[s], spot, send.at[s, o], recv.at[s, o], {"seq": peer}) for o, peer in seq_peers()
        ]
        return sends, pltpu.make_async_copy(land.at[s], spot, local.at[s])

    def rim_copy(s, side):
        there = lax.rem(me + (1 if side == 0 else count - 1), count)
        return remote(
            rim.at[s, side], rim_out.at[s, side], rim_send.at[s, side], rim_recv.at[s, side], {"seq": there}
        )

    begin(copies(step))
    for side in range(2):
        rim_copy(step, side).start()

    @pl.when(step == seqs - 1)
    def _():
        def drain(s, carry):
            finish(copies(s))
            for side in range(2):
                rim_copy(s, side).wait()
            return carry

        lax.fori_loop(0, seqs, drain, 0)


def project(tokens, w_qkv, marks):
    seqs, rows, features = tokens.shape
    ranks = lax.axis_size("seq")
    full = pl.BlockSpec((1, rows, features), lambda s: (s, 0, 0))
    dma = pltpu.SemaphoreType.DMA
    return pl.pallas_call(
        project_kernel,
        grid=(seqs,),
        in_specs=[full, pl.BlockSpec(w_qkv.shape, lambda s: (0, 0), pipeline_mode=pl.Buffered(1))],
        out_specs=[full] * 3 + [ANY] * 2,
        out_shape=[jax.ShapeDtypeStruct(tokens.shape, bf16)] * 3
        + [
            jax.ShapeDtypeStruct((seqs, 2, M, features), bf16),
            jax.ShapeDtypeStruct((seqs, 2, RIM, features), bf16),
        ],
        scratch_shapes=[
            pltpu.VMEM((seqs, 2, marks, features), bf16), pltpu.VMEM((seqs, 2, RIM, features), bf16),
            dma((seqs, ranks)), dma((seqs, ranks)), dma((seqs,)), dma((seqs, 2)), dma((seqs, 2)), dma((seqs,)),
        ],
        compiler_params=params(48 * MB, collective_id=0, has_side_effects=True),
        name="project",
    )(tokens, w_qkv)


def fill_pad(pad, x_ref, rim_ref):
    rows = x_ref.shape[1]
    me, count = seq_place()
    pad[0:RIM, :] = jnp.where(me > 0, rim_ref[0, 0].astype(f32), 0.0)
    pad[RIM : RIM + rows, :] = x_ref[0].astype(f32)
    pad[RIM + rows : RIM + rows + RIM, :] = jnp.where(me < count - 1, rim_ref[0, 1].astype(f32), 0.0)


def conv_tile(v_ref, rim_ref, f_ref, o_ref, pad):
    rows = v_ref.shape[1]
    fill_pad(pad, v_ref, rim_ref)
    for c in range(0, rows, 64):
        acc = jnp.zeros((64, 128), f32)
        for j in range(KW):
            acc = acc + f_ref[j : j + 1, :] * pad[c + j : c + j + 64, :]
        o_ref[0, c : c + 64, :] = acc.astype(bf16)


def conv_specs(rows, first_step, first_group, groups):
    at = lambda i: jnp.maximum(i - first_step, 0)
    seq = lambda i: at(i) // groups
    group = lambda i: at(i) % groups
    return (
        pl.BlockSpec((1, rows, 128), lambda i: (seq(i), 0, first_group + group(i))),
        pl.BlockSpec((1, 2, RIM, 128), lambda i: (seq(i), 0, 0, first_group + group(i))),
        pl.BlockSpec((KW, 128), lambda i: (0, first_group + group(i))),
        pl.BlockSpec((1, rows, 128), lambda i: (seq(i), 0, group(i))),
    )


def conv_back_tile(seq, seqs, g_ref, rim_ref, v_ref, f_ref, o_ref, gf_ref, pad, facc):
    rows = v_ref.shape[1]
    fill_pad(pad, g_ref, rim_ref)

    @pl.when(seq == 0)
    def _():
        facc[...] = jnp.zeros_like(facc)

    for c in range(0, rows, 64):
        acc = jnp.zeros((64, 128), f32)
        vals = v_ref[0, c : c + 64, :].astype(f32)
        for j in range(KW):
            moved = pad[c + 2 * RIM - j : c + 2 * RIM - j + 64, :]
            acc = acc + f_ref[j : j + 1, :] * moved
            facc[8 * j : 8 * j + 8, :] += (vals * moved).reshape(8, 8, 128).sum(0)
        o_ref[0, c : c + 64, :] = acc.astype(bf16)

    @pl.when(seq == seqs - 1)
    def _():
        gf_ref[...] = facc[...].reshape(KW, 8, 128).sum(1)


def conv_back_kernel(g_ref, rim_ref, v_ref, f_ref, o_ref, gf_ref, pad, facc):
    conv_back_tile(
        pl.program_id(1), pl.num_programs(1), g_ref, rim_ref, v_ref, f_ref, o_ref, gf_ref, pad, facc
    )


def conv_back_specs(rows, seqs, first_step, first_group):
    at = lambda i: jnp.maximum(i - first_step, 0)
    seq = lambda i: at(i) % seqs
    group = lambda i: at(i) // seqs
    return (
        pl.BlockSpec((1, rows, 128), lambda i: (seq(i), 0, first_group + group(i))),
        pl.BlockSpec((1, 2, RIM, 128), lambda i: (seq(i), 0, 0, first_group + group(i))),
        pl.BlockSpec((KW, 128), lambda i: (0, first_group + group(i))),
        pl.BlockSpec((1, rows, 128), lambda i: (seq(i), 0, group(i))),
        pl.BlockSpec((KW, 128), lambda i: (0, group(i))),
    )


def conv_back(g, rim, v, taps):
    seqs, rows, features = v.shape
    sp = lambda n: pl.BlockSpec((1, n, 128), lambda g, s: (s, 0, g))
    fs = pl.BlockSpec((KW, 128), lambda g, s: (0, g))
    return pl.pallas_call(
        conv_back_kernel,
        grid=(features // 128, seqs),
        in_specs=[sp(rows), pl.BlockSpec((1, 2, RIM, 128), lambda g, s: (s, 0, 0, g)), sp(rows), fs],
        out_specs=[sp(rows), fs],
        out_shape=[jax.ShapeDtypeStruct(v.shape, bf16), jax.ShapeDtypeStruct((KW, features), f32)],
        scratch_shapes=[pltpu.VMEM((rows + 2 * RIM, 128), f32), pltpu.VMEM((KW * 8, 128), f32)],
        name="conv_back",
    )(g, rim, v, taps)


def score_step(step, q_ref, k_ref, v_ref, land_ref, w_ref, p_ref, num_ref, stat_ref):
    rows, features = q_ref.shape[1:]
    pairs = features // 128
    masks = group_masks((M, 4 * E), 4, bf16)
    masks_wide = group_masks((M, 4 * E), 4, f32)
    ones = jnp.where(
        lane_group((4 * E, 4 * E)) == lax.broadcasted_iota(jnp.int32, (4 * E, 4 * E), 0) // E, 1.0, 0.0
    ).astype(bf16)
    chunk = min(128, rows)
    upper = lax.broadcasted_iota(jnp.int32, (chunk, 2 * E), 1) >= E
    for g in range(features // 256):
        sl = slice(256 * g, 256 * g + 256)
        s3 = dot_nt(k_ref[0, :, sl], block_diag(land_ref[0, 0, :, sl], masks))
        peak = jnp.max(s3, axis=0, keepdims=True)
        e3 = jnp.exp(s3 - peak)
        total = jnp.sum(e3, axis=0, keepdims=True)
        low = e3.astype(bf16)
        w_ref[0, :, sl] = low
        num = diag_blocks(dot_tn(low, v_ref[0, :, sl]), masks_wide).astype(bf16)
        for i in range(2):
            lanes = slice(128 * i, 128 * i + 128)
            num_ref[step * pairs + 2 * g + i] = num[:, lanes]
            stat_ref[step * pairs + 2 * g + i] = jnp.concatenate(
                [peak[:, lanes], total[:, lanes], jnp.zeros((6, 128), f32)], axis=0
            )
        kd = block_diag(land_ref[0, 1, :, sl], masks)
        for r in range(0, rows, chunk):
            s1 = dot_nt(q_ref[0, r : r + chunk, sl], kd)
            parts = []
            for i in range(2):
                x = s1[:, 128 * i : 128 * i + 128]
                top_a = jnp.max(jnp.where(upper, -jnp.inf, x), axis=1, keepdims=True)
                top_b = jnp.max(jnp.where(upper, x, -jnp.inf), axis=1, keepdims=True)
                parts.append(jnp.exp(x - jnp.where(upper, top_b, top_a)))
            e1 = jnp.concatenate(parts, axis=1)
            p_ref[0, r : r + chunk, sl] = (e1 / dot(e1.astype(bf16), ones)).astype(bf16)


def scores_kernel(
    seqs, q_ref, k_ref, v_ref, land_ref, cv_ref, rim_ref, f_ref, w_ref, p_ref, co_ref, num_out, stat_out,
    num, stat, pad, num_sems, stat_sems,
):
    step = pl.program_id(0)
    steps = pl.num_programs(0)
    own = num_out.shape[1]
    pairs = q_ref.shape[2] // 128

    @pl.when(step == 0)
    def _():
        greet()
        if num.shape[0] > seqs * pairs:
            num[seqs * pairs :] = jnp.zeros_like(num[seqs * pairs :])
            stat[seqs * pairs :] = jnp.zeros_like(stat[seqs * pairs :])

    @pl.when(step < seqs)
    def _():
        score_step(step, q_ref, k_ref, v_ref, land_ref, w_ref, p_ref, num, stat)

    @pl.when(step == seqs - 1)
    def _():
        begin(swap_copies(num, num_out, own, num_sems))
        begin(swap_copies(stat, stat_out, own, stat_sems))

    @pl.when(step >= seqs)
    def _():
        conv_tile(cv_ref, rim_ref, f_ref, co_ref, pad)

    @pl.when(step == steps - 1)
    def _():
        finish(swap_copies(num, num_out, own, num_sems))
        finish(swap_copies(stat, stat_out, own, stat_sems))


def scores(q, k, v, land, rim, taps, own, groups):
    seqs, rows, features = q.shape
    ranks = lax.axis_size("seq")
    here = lambda i: jnp.minimum(i, seqs - 1)
    full = pl.BlockSpec((1, rows, features), lambda i: (here(i), 0, 0))
    cv, rims, ft, co = conv_specs(rows, seqs, 0, groups)
    return pl.pallas_call(
        functools.partial(scores_kernel, seqs),
        grid=(seqs + seqs * groups,),
        in_specs=[full] * 3
        + [pl.BlockSpec((1, 2, M, features), lambda i: (here(i), 0, 0, 0)), cv, rims, ft],
        out_specs=[full] * 2 + [co, ANY, ANY],
        out_shape=[jax.ShapeDtypeStruct(q.shape, bf16)] * 2
        + [
            jax.ShapeDtypeStruct((seqs, rows, 128 * groups), bf16),
            jax.ShapeDtypeStruct((ranks, own, M, 128), bf16),
            jax.ShapeDtypeStruct((ranks, own, 8, 128), f32),
        ],
        scratch_shapes=[
            pltpu.VMEM((ranks * own, M, 128), bf16), pltpu.VMEM((ranks * own, 8, 128), f32),
            pltpu.VMEM((rows + 2 * RIM, 128), f32), rank_sems(), rank_sems(),
        ],
        compiler_params=params(48 * MB, collective_id=1, has_side_effects=True),
        name="scores",
    )(q, k, v, land, v, rim, taps)


def split(x):
    hi = x.astype(bf16)
    return hi, (x - hi.astype(f32)).astype(bf16)


def stack_parts(xs, axis):
    return jnp.concatenate([part for x in xs for part in split(x)], axis=axis)


def pair_sums(out, count):
    top = lambda i, j: out[128 * i + 64 * j : 128 * i + 64 * j + 64]
    return [
        top(i, 0)[:, :128] + (top(i, 0)[:, 128:] + top(i, 1)[:, :128]) for i in range(count)
    ]


def pair_nn(lefts, right, masks):
    hi, lo = split(right)
    packed = jnp.concatenate([block_diag(hi, masks), block_diag(lo, masks)], axis=1)
    return pair_sums(dot(stack_parts(lefts, 0), packed), len(lefts))


def pair_nt(lefts, right, masks):
    hi, lo = split(right)
    packed = jnp.concatenate([block_diag(hi, masks), block_diag(lo, masks)], axis=0)
    return pair_sums(dot_nt(stack_parts(lefts, 0), packed), len(lefts))


def pair_tn(left, rights, masks_wide):
    out = dot_tn(stack_parts([left], 1), stack_parts(rights, 1))
    results = []
    for i in range(len(rights)):
        full = out[:128, 256 * i : 256 * i + 128] + (
            out[:128, 256 * i + 128 : 256 * i + 256] + out[128:, 256 * i : 256 * i + 128]
        )
        results.append(diag_blocks(full, masks_wide))
    return results


def half_reduce(x, upper, op, fill):
    a = op(jnp.where(upper, fill, x), axis=1, keepdims=True)
    b = op(jnp.where(upper, x, fill), axis=1, keepdims=True)
    return jnp.where(upper, b, a)


def to_column(row, same, upper):
    return half_reduce(jnp.where(same, row, 0.0), upper, jnp.sum, 0.0)


def to_row(col, same):
    return jnp.sum(jnp.where(same, col, 0.0), axis=0, keepdims=True)


def pair_consts():
    lane = lax.broadcasted_iota(jnp.int32, (M, 128), 1)
    row = lax.broadcasted_iota(jnp.int32, (M, 128), 0)
    return lane >= E, row == lane % E, group_masks((M, 128), 2, bf16), group_masks((M, 128), 2, f32)


def own_pair(land_ref, i, own):
    me, _ = seq_place()
    per = land_ref.shape[2] // 128
    p = jnp.minimum(me * own + i, land_ref.shape[0] * per - 1)
    return land_ref[p // per, :, pl.ds(pl.multiple_of((p % per) * 128, 128), 128)]


def inverse_step(
    num_ref, stat_ref, land_ref, mixed_ref, sum_ref, mid_ref, z_ref, p_ref, a_ref, w_ref,
    scale_ref, tot_ref, alpha_ref,
):
    ranks, own = num_ref.shape[:2]
    upper, same, masks, masks_wide = pair_consts()
    for i in range(own):
        peak = stat_ref[0, i, 0:1, :]
        for r in range(1, ranks):
            peak = jnp.maximum(peak, stat_ref[r, i, 0:1, :])
        total = jnp.zeros((1, 128), f32)
        numer = jnp.zeros((M, 128), f32)
        for r in range(ranks):
            alpha = jnp.exp(stat_ref[r, i, 0:1, :] - peak)
            total = total + alpha * stat_ref[r, i, 1:2, :]
            column = to_column(alpha, same, upper)
            alpha_ref[r, i] = column
            numer = numer + column * num_ref[r, i].astype(f32)
        total = to_column(total, same, upper)
        tot_ref[i] = total
        sum_ref[i] = numer / total
        ql, kl = own_pair(land_ref.at[:, 0], i, own), own_pair(land_ref.at[:, 1], i, own)
        s2 = dot_nt(ql, block_diag(kl, masks))
        e2 = jnp.exp(s2 - half_reduce(s2, upper, jnp.max, -jnp.inf))
        middle = e2 / half_reduce(e2, upper, jnp.sum, 0.0)
        mid_ref[i] = middle
        st = dot_nt(kl, block_diag(ql, masks))
        et = jnp.exp(st - jnp.max(st, axis=0, keepdims=True))
        flipped = et / jnp.sum(et, axis=0, keepdims=True)
        column = jnp.sum(middle, axis=0, keepdims=True)
        scale = 1.0 / half_reduce(column, upper[0:1], jnp.max, -jnp.inf)
        scale_ref[i] = jnp.broadcast_to(scale, (8, 128))
        z_ref[0, i] = flipped * scale

    def step(it, carry):
        zs = [z_ref[it, i] for i in range(own)]
        ps = [pair_nn([mid_ref[i]], zs[i], masks)[0] for i in range(own)]
        second = [pair_nn([ps[i], zs[i]], ps[i], masks) for i in range(own)]
        for i in range(own):
            p2, a = second[i]
            w = 7.0 * ps[i] - p2
            p_ref[it, i] = ps[i]
            a_ref[it, i] = a
            w_ref[it, i] = w
            z_ref[it + 1, i] = 0.25 * (13.0 * zs[i] - 15.0 * a + pair_nn([a], w, masks)[0])
        return carry

    lax.fori_loop(0, NEWTON, step, 0)
    for i in range(own):
        mixed_ref[i] = pair_nn([z_ref[NEWTON, i]], sum_ref[i], masks)[0].astype(bf16)


def inverse_kernel(
    num_ref, stat_ref, land_ref, cv_ref, rim_ref, f_ref, mixed_out, co_ref, sum_ref, mid_ref, z_ref, p_ref,
    a_ref, w_ref, scale_ref, tot_ref, alpha_ref, mixed, pad, sems,
):
    step = pl.program_id(0)
    own = num_ref.shape[1]

    @pl.when(step == 0)
    def _():
        greet()
        inverse_step(
            num_ref, stat_ref, land_ref, mixed, sum_ref, mid_ref, z_ref, p_ref, a_ref, w_ref, scale_ref,
            tot_ref, alpha_ref,
        )
        begin(spread_copies(mixed, mixed_out, own, sems))

    @pl.when(step > 0)
    def _():
        conv_tile(cv_ref, rim_ref, f_ref, co_ref, pad)

    @pl.when(step == pl.num_programs(0) - 1)
    def _():
        finish(spread_copies(mixed, mixed_out, own, sems))


def inverse(num, stat, land, v, rim, taps, first_group):
    ranks, own = num.shape[:2]
    seqs, rows, features = v.shape
    groups = features // 128 - first_group
    mat = jax.ShapeDtypeStruct((own, M, 128), f32)
    steps = lambda n: jax.ShapeDtypeStruct((n, own, M, 128), f32)
    whole = lambda a: pl.BlockSpec(a.shape, lambda i: (0,) * len(a.shape), pipeline_mode=pl.Buffered(1))
    saved = [
        mat, mat, steps(NEWTON + 1), steps(NEWTON), steps(NEWTON), steps(NEWTON),
        jax.ShapeDtypeStruct((own, 8, 128), f32), mat, steps(ranks),
    ]
    cv, rims, ft, co = conv_specs(rows, 1, first_group, groups)
    return pl.pallas_call(
        inverse_kernel,
        grid=(1 + seqs * groups,),
        in_specs=[whole(num), whole(stat), whole(land), cv, rims, ft],
        out_specs=[ANY, co] + [whole(a) for a in saved],
        out_shape=[
            jax.ShapeDtypeStruct((ranks * own, M, 128), bf16),
            jax.ShapeDtypeStruct((seqs, rows, 128 * groups), bf16),
        ]
        + saved,
        scratch_shapes=[
            pltpu.VMEM((own, M, 128), bf16), pltpu.VMEM((rows + 2 * RIM, 128), f32), rank_sems(),
        ],
        compiler_params=params(48 * MB, collective_id=2, has_side_effects=True),
        name="inverse",
    )(num, stat, land, v, rim, taps)


def inverse_back_step(
    land_ref, marks_ref, sum_ref, mid_ref, z_ref, p_ref, a_ref, w_ref, scale_ref, tot_ref,
    alpha_ref, gn_ref, gt_ref, mq_ref, mk_ref, g_ref, dk_ref,
):
    ranks, own = land_ref.shape[:2]
    upper, same, masks, masks_wide = pair_consts()
    for i in range(own):
        land = land_ref[0, i].astype(f32)
        for r in range(1, ranks):
            land = land + land_ref[r, i].astype(f32)
        summary, total = sum_ref[i], tot_ref[i]
        gs = pair_tn(z_ref[NEWTON, i], [land], masks_wide)[0].astype(bf16).astype(f32)
        gn = (gs / total).astype(bf16).astype(f32)
        gt = -half_reduce(gs * summary, upper, jnp.sum, 0.0) / total
        for r in range(ranks):
            gn_ref[r, i] = (alpha_ref[r, i] * gn).astype(bf16)
            gt_ref[r, i] = jnp.broadcast_to(to_row(alpha_ref[r, i] * gt, same), (8, 128))
        g_ref[i] = pair_nt([land], summary, masks)[0]
        dk_ref[i] = jnp.zeros((M, 128), f32)

    def step(back, carry):
        it = NEWTON - 1 - back
        gs = [g_ref[i] for i in range(own)]
        das, dws = [], []
        for i in range(own):
            das.append(0.25 * (pair_nt([gs[i]], w_ref[it, i], masks)[0] - 15.0 * gs[i]))
            dws.append(0.25 * pair_tn(a_ref[it, i], [gs[i]], masks_wide)[0])
        dps, parts = [], []
        for i in range(own):
            right = pair_nt([dws[i], das[i]], p_ref[it, i], masks)
            left = pair_tn(p_ref[it, i], [dws[i]], masks_wide)[0]
            dps.append(7.0 * dws[i] - right[0] - left + pair_tn(z_ref[it, i], [das[i]], masks_wide)[0])
            parts.append(3.25 * gs[i] + right[1])
        for i in range(own):
            g_ref[i] = parts[i] + pair_tn(mid_ref[i], [dps[i]], masks_wide)[0]
            dk_ref[i] += pair_nt([dps[i]], z_ref[it, i], masks)[0]
        return carry

    lax.fori_loop(0, NEWTON, step, 0)
    eye = jnp.where(same, 1.0, 0.0).astype(bf16)
    for i in range(own):
        g, middle, scale = g_ref[i], mid_ref[i], scale_ref[i, 0:1, :]
        turned = dot_tn(stack_parts([g], 1), eye)
        turned = diag_blocks(turned[:128] + turned[128:], masks_wide)
        column = jnp.sum(middle, axis=0, keepdims=True)
        top = half_reduce(column, upper[0:1], jnp.max, -jnp.inf)
        hit = jnp.where(column == top, 1.0, 0.0)
        share = hit / half_reduce(hit, upper[0:1], jnp.sum, 0.0)
        d_scale = half_reduce(jnp.sum(turned * middle, axis=0, keepdims=True), upper[0:1], jnp.sum, 0.0)
        dk = dk_ref[i] + turned * scale - share * (d_scale * scale * scale)
        ds = middle * (dk - half_reduce(middle * dk, upper, jnp.sum, 0.0))
        hi, lo = split(ds)
        both = dot(jnp.concatenate([hi, lo], axis=0), block_diag(own_pair(marks_ref.at[:, 1], i, own), masks))
        mq_ref[i] = both[:M] + both[M:]
        turned = dot_tn(jnp.concatenate([hi, lo], axis=1), own_pair(marks_ref.at[:, 0], i, own))
        mk_ref[i] = diag_blocks(turned[:128] + turned[128:], masks_wide)


def inverse_back(land, marks, saved):
    ranks, own = land.shape[:2]
    mat = jax.ShapeDtypeStruct((own, M, 128), f32)
    return pl.pallas_call(
        inverse_back_step,
        out_shape=[
            jax.ShapeDtypeStruct((ranks, own, M, 128), bf16),
            jax.ShapeDtypeStruct((ranks, own, 8, 128), f32), mat, mat,
        ],
        scratch_shapes=[pltpu.VMEM((own, M, 128), f32)] * 2,
        compiler_params=params(48 * MB),
        name="inverse_back",
    )(land, marks, *saved)


def mean_of(x):
    return jnp.mean(x, axis=-1, keepdims=True)


def gelu_and_slope(u):
    x = jnp.abs(u) * root_half
    t = 1.0 / (1.0 + ERFC_P * x)
    poly = jnp.full_like(t, ERFC_C[-1])
    for c in ERFC_C[-2::-1]:
        poly = poly * t + c
    bell = jnp.exp(-0.5 * u * u)
    half = (0.5 * t) * poly * bell
    cdf = jnp.where(u < 0.0, half, 1.0 - half)
    return u * cdf, cdf + u * bell * inv_root_two_pi


def row_block(
    step, tok_ref, p_ref, conv_a_ref, conv_b_ref, mix_ref, top_ref, w_out_ref, w_up_ref, w_down_ref, ga_ref,
    gf_ref, out_ref, proj_ref, gm_ref, gains_ref, act, gul, slope, hid_t, gdl_t, mix_t, gpr, resid,
):
    size, features = tok_ref.shape
    ff = act.shape[1]
    wide = features
    start = pl.multiple_of(step * size, size)
    rows = pl.ds(start, size)
    masks = group_masks((M, 4 * E), 4, bf16)
    for g in range(features // 256):
        sl = slice(256 * g, 256 * g + 256)
        att = dot(p_ref[:, sl], block_diag(mix_ref[0, :, sl], masks))
        resid[:, sl] = att
    half = conv_a_ref.shape[1]
    resid[:, :half] += conv_a_ref[...].astype(f32)
    resid[:, half:] += conv_b_ref[...].astype(f32)
    mixed = resid[...].astype(bf16)
    mix_t[:, rows] = mixed.T
    residual = tok_ref[...].astype(f32) + dot(mixed, w_out_ref[...])
    centre = residual - mean_of(residual)
    s_att = lax.rsqrt(mean_of(centre * centre) + epsilon)
    normed = centre * s_att
    gain_att = ga_ref[...]
    hidden = normed * gain_att
    hid_low = hidden.astype(bf16)
    hid_t[:, rows] = hid_low.T
    down = jnp.zeros((size, features), f32)
    for j in range(0, ff, wide):
        up = dot(hid_low, w_up_ref[:, j : j + wide])
        a, sl = gelu_and_slope(up)
        low = a.astype(bf16)
        act[rows, j : j + wide] = low
        slope[:, j : j + wide] = sl.astype(bf16)
        down = down + dot(low, w_down_ref[j : j + wide, :])
    residual_two = hidden + down
    centre_two = residual_two - mean_of(residual_two)
    s_ffn = lax.rsqrt(mean_of(centre_two * centre_two) + epsilon)
    normed_two = centre_two * s_ffn
    gain_ffn = gf_ref[...]
    out_ref[...] = (normed_two * gain_ffn).astype(bf16)
    top = top_ref[...].astype(f32)
    gains_ref[8:16, :] += (top * normed_two).reshape(size // 8, 8, features).sum(0)
    g = top * gain_ffn
    grad_two = s_ffn * (g - mean_of(g) - normed_two * mean_of(g * normed_two))
    gdl = grad_two.astype(bf16)
    gdl_t[:, rows] = gdl.T
    back = jnp.zeros((size, features), f32)
    for j in range(0, ff, wide):
        gu = dot_nt(gdl, w_down_ref[j : j + wide, :]) * slope[:, j : j + wide].astype(f32)
        low = gu.astype(bf16)
        gul[rows, j : j + wide] = low
        back = back + dot_nt(low, w_up_ref[:, j : j + wide])
    grad_hidden = grad_two + back
    gains_ref[0:8, :] += (grad_hidden * normed).reshape(size // 8, 8, features).sum(0)
    g = grad_hidden * gain_att
    proj = (s_att * (g - mean_of(g) - normed * mean_of(g * normed))).astype(bf16)
    proj_ref[...] = proj
    gpr[rows, :] = proj
    gm_ref[...] = dot_nt(proj, w_out_ref[...]).astype(bf16)


def row_kernel(
    tok_ref, p_ref, conv_a_ref, conv_b_ref, mix_ref, top_ref, w_out_ref, w_up_ref, w_down_ref, ga_ref, gf_ref,
    out_ref, proj_ref, gm_ref, wg_ref, gains_ref,
    act, gul, slope, hid_t, gdl_t, mix_t, gpr, resid,
):
    step = pl.program_id(0)
    size, features = tok_ref.shape
    blocks = act.shape[0] // size
    ff = act.shape[1]
    wide = features

    @pl.when(step == 0)
    def _():
        gains_ref[...] = jnp.zeros_like(gains_ref)

    @pl.when(step < blocks)
    def _():
        row_block(
            step, tok_ref, p_ref, conv_a_ref, conv_b_ref, mix_ref, top_ref, w_out_ref, w_up_ref, w_down_ref,
            ga_ref, gf_ref, out_ref, proj_ref, gm_ref, gains_ref, act, gul, slope, hid_t, gdl_t, mix_t, gpr,
            resid,
        )

    chunks = ff // wide
    for first, left, right in ((0, hid_t, gul), (chunks, gdl_t, act), (2 * chunks, mix_t, gpr)):
        count = chunks if first < 2 * chunks else 1

        @pl.when((step >= blocks + first) & (step < blocks + first + count))
        def _(first=first, left=left, right=right):
            base = (step - blocks - first) * wide
            for c in range(0, wide, 256):
                cols = pl.ds(pl.multiple_of(base + c, 256), 256)
                wg_ref[0, :, c : c + 256] = dot(left[...], right[:, cols]).astype(bf16)


def row_pass(tokens, probs, conv_a, conv_b, mixed, grad_out, w_out, w_up, w_down, gain_att, gain_ffn):
    seqs, rows, features = tokens.shape
    ff = w_up.shape[1]
    size = min(256, rows)
    total = seqs * rows
    blocks = total // size
    grads = 2 * (ff // features) + 1
    here = lambda i: jnp.minimum(i, blocks - 1)
    block = pl.BlockSpec((size, features), lambda i: (here(i), 0))
    whole = lambda a: pl.BlockSpec(a.shape, lambda i: (0,) * a.ndim, pipeline_mode=pl.Buffered(1))
    flat = lambda a: a.reshape(total, a.shape[2])
    part = lambda a: pl.BlockSpec((size, a.shape[2]), lambda i: (here(i), 0))
    gains = [gain_att.reshape(1, features), gain_ffn.reshape(1, features)]
    row_out = jax.ShapeDtypeStruct((total, features), bf16)
    tall = pltpu.VMEM((features, total), bf16)
    return pl.pallas_call(
        row_kernel,
        grid=(blocks + grads,),
        in_specs=[
            block, block, part(conv_a), part(conv_b),
            pl.BlockSpec((1, M, features), lambda i: (here(i) * size // rows, 0, 0)),
            block, whole(w_out), whole(w_up), whole(w_down), whole(gains[0]), whole(gains[1]),
        ],
        out_specs=[block] * 3
        + [
            pl.BlockSpec((1, features, features), lambda i: (jnp.maximum(i - blocks, 0), 0, 0)),
            pl.BlockSpec((16, features), lambda i: (0, 0)),
        ],
        out_shape=[row_out] * 3
        + [
            jax.ShapeDtypeStruct((grads, features, features), bf16),
            jax.ShapeDtypeStruct((16, features), f32),
        ],
        scratch_shapes=[
            pltpu.VMEM((total, ff), bf16), pltpu.VMEM((total, ff), bf16), pltpu.VMEM((size, ff), bf16),
            tall, tall, tall, pltpu.VMEM((total, features), bf16), pltpu.VMEM((size, features), f32),
        ],
        compiler_params=params(60 * MB),
        name="row_pass",
    )(flat(tokens), flat(probs), flat(conv_a), flat(conv_b), mixed, flat(grad_out), w_out, w_up, w_down, *gains)


def row_share_kernel(
    tok_ref, p_ref, conv_a_ref, conv_b_ref, mix_ref, top_ref, w_out_ref, w_up_ref, w_down_ref, ga_ref, gf_ref,
    out_ref, proj_ref, gm_ref, gains_ref, g_out, rim_out,
    act, gul, slope, hid_t, gdl_t, mix_t, gpr, resid, rim, parts, got, sums,
    send, recv, out_sem, last_sem, rim_send, rim_recv,
):
    step = pl.program_id(0)
    size, features = tok_ref.shape
    blocks = act.shape[0] // size
    seqs = rim.shape[0]
    per = blocks // seqs
    ff = act.shape[1]
    wide = features
    chunks = ff // wide
    count_all = 2 * chunks + 1
    me, count = seq_place()
    core, _, _, sibling, _, _ = cube()
    half = wide // 2

    @pl.when(step == 0)
    def _():
        gains_ref[...] = jnp.zeros_like(gains_ref)
        greet([sibling])

    def rim_copy(s, side):
        there = lax.rem(me + (1 if side == 0 else count - 1), count)
        return remote(
            rim.at[s, side], rim_out.at[s, side], rim_send.at[s, side], rim_recv.at[s, side], {"seq": there}
        )

    @pl.when(step < blocks)
    def _():
        row_block(
            step, tok_ref, p_ref, conv_a_ref, conv_b_ref, mix_ref, top_ref, w_out_ref, w_up_ref, w_down_ref,
            ga_ref, gf_ref, out_ref, proj_ref, gm_ref, gains_ref, act, gul, slope, hid_t, gdl_t, mix_t, gpr,
            resid,
        )
        s = step // per

        @pl.when(step % per == 0)
        def _():
            rim[s, 1] = gm_ref[:RIM, :]
            rim_copy(s, 1).start()

        @pl.when(step % per == per - 1)
        def _():
            rim[s, 0] = gm_ref[size - RIM :, :]
            rim_copy(s, 0).start()

    j = step - blocks
    slot = lax.rem(jnp.maximum(j, 0), 2)

    def share(at):
        return remote(parts.at[at % 2, 1 - core], got.at[at], send.at[at], recv.at[at], sibling)

    @pl.when(j >= 2)
    def _():
        share(j - 2).wait_send()

    @pl.when((j >= 0) & (j < chunks))
    def _():
        for c in range(0, wide, 256):
            cols = pl.ds(pl.multiple_of(j * wide + c, 256), 256)
            low = dot(hid_t[...], gul[:, cols]).astype(bf16)
            for l in range(0, 256, 128):
                side, lane = (c + l) // half, (c + l) % half
                for d in range(8):
                    parts[slot, d % 2, d // 2, 96 * side : 96 * side + 96, lane : lane + 128] = low[
                        96 * d : 96 * d + 96, l : l + 128
                    ]

    @pl.when((j >= chunks) & (j < 2 * chunks))
    def _():
        for c in range(0, wide, 256):
            cols = pl.ds(pl.multiple_of((j - chunks) * wide + c, 256), 256)
            low = dot(gdl_t[...], act[:, cols]).astype(bf16)
            for l in range(0, 256, 128):
                side, lane = (c + l) // half, (c + l) % half
                for z in range(4):
                    parts[slot, side, z, :, lane : lane + 128] = low[192 * z : 192 * z + 192, l : l + 128]

    @pl.when(j == 2 * chunks)
    def _():
        for c in range(2):
            low = dot(mix_t[...], gpr[:, half * c : half * c + half]).astype(bf16)
            for zz in range(2):
                z = 2 * c + zz
                for d in range(8):
                    block = low[96 * d : 96 * d + 96, 192 * zz : 192 * zz + 192]
                    parts[slot, d % 2, d // 2, 48 * z : 48 * z + 48, :] = jnp.concatenate(
                        [block[:48], block[48:]], axis=1
                    )

    @pl.when((j >= 0) & (j < count_all))
    def _():
        share(j).start()

    done = j - 1

    def up_copy(at):
        return pltpu.make_async_copy(sums.at[at % 2], g_out.at[at, :, 0:192, :], out_sem.at[at % 2])

    def down_copy(at):
        return pltpu.make_async_copy(
            sums.at[at % 2], g_out.at[:, at - chunks, 192:384, :], out_sem.at[at % 2]
        )

    def out_copy(z):
        return pltpu.make_async_copy(
            sums.at[0, :, 48 * z : 48 * z + 48, :], g_out.at[z, :, 384:432, :], last_sem.at[z]
        )

    def drain(at):
        @pl.when((at >= 0) & (at < chunks))
        def _():
            up_copy(at).wait()

        @pl.when((at >= chunks) & (at < 2 * chunks))
        def _():
            down_copy(at).wait()

    drain(done - 2)

    @pl.when(done >= 0)
    def _():
        share(done).wait_recv()
        sums[done % 2] = add_low(parts[done % 2, core], got[done])

    @pl.when((done >= 0) & (done < chunks))
    def _():
        up_copy(done).start()

    @pl.when((done >= chunks) & (done < 2 * chunks))
    def _():
        down_copy(done).start()

    @pl.when(done == 2 * chunks)
    def _():
        for z in range(4):
            out_copy(z).start()
        share(done).wait_send()
        drain(done - 1)
        for z in range(4):
            out_copy(z).wait()

        def rims(s, carry):
            for side in range(2):
                rim_copy(s, side).wait()
            return carry

        lax.fori_loop(0, seqs, rims, 0)


def row_share(tokens, probs, conv_a, conv_b, mixed, grad_out, w_out, w_up, w_down, gain_att, gain_ffn):
    seqs, rows, features = tokens.shape
    ff = w_up.shape[1]
    size = min(256, rows)
    total = seqs * rows
    blocks = total // size
    grads = 2 * (ff // features) + 1
    here = lambda i: jnp.minimum(i, blocks - 1)
    block = pl.BlockSpec((size, features), lambda i: (here(i), 0))
    whole = lambda a: pl.BlockSpec(a.shape, lambda i: (0,) * a.ndim, pipeline_mode=pl.Buffered(1))
    flat = lambda a: a.reshape(total, a.shape[2])
    part = lambda a: pl.BlockSpec((size, a.shape[2]), lambda i: (here(i), 0))
    gains = [gain_att.reshape(1, features), gain_ffn.reshape(1, features)]
    row_out = jax.ShapeDtypeStruct((total, features), bf16)
    tall = pltpu.VMEM((features, total), bf16)
    dma = pltpu.SemaphoreType.DMA
    return pl.pallas_call(
        row_share_kernel,
        grid=(blocks + grads + 1,),
        in_specs=[
            block, block, part(conv_a), part(conv_b),
            pl.BlockSpec((1, M, features), lambda i: (here(i) * size // rows, 0, 0)),
            block, whole(w_out), whole(w_up), whole(w_down), whole(gains[0]), whole(gains[1]),
        ],
        out_specs=[block] * 3 + [pl.BlockSpec((16, features), lambda i: (0, 0)), ANY, ANY],
        out_shape=[row_out] * 3
        + [
            jax.ShapeDtypeStruct((16, features), f32),
            jax.ShapeDtypeStruct((4, 4, 432, 384), bf16),
            jax.ShapeDtypeStruct((seqs, 2, RIM, features), bf16),
        ],
        scratch_shapes=[
            pltpu.VMEM((total, ff), bf16), pltpu.VMEM((total, ff), bf16), pltpu.VMEM((size, ff), bf16),
            tall, tall, tall, pltpu.VMEM((total, features), bf16), pltpu.VMEM((size, features), f32),
            pltpu.VMEM((seqs, 2, RIM, features), bf16),
            pltpu.VMEM((2, 2, 4, 192, 384), bf16), pltpu.VMEM((grads, 4, 192, 384), bf16),
            pltpu.VMEM((2, 4, 192, 384), bf16),
            dma((grads,)), dma((grads,)), dma((2,)), dma((4,)), dma((seqs, 2)), dma((seqs, 2)),
        ],
        compiler_params=params(62 * MB, collective_id=3, has_side_effects=True),
        name="row_share",
    )(flat(tokens), flat(probs), flat(conv_a), flat(conv_b), mixed, flat(grad_out), w_out, w_up, w_down, *gains)


def first_back_step(gm_ref, p_ref, q_ref, mix_ref, kl_of, put_land, gq_ref, put_klp):
    features = gm_ref.shape[2]
    masks = group_masks((M, 4 * E), 4, bf16)
    masks_wide = group_masks((M, 4 * E), 4, f32)
    ones = jnp.where(
        lane_group((4 * E, 4 * E)) == lax.broadcasted_iota(jnp.int32, (4 * E, 4 * E), 0) // E, 1.0, 0.0
    ).astype(bf16)
    for g in range(features // 256):
        sl = slice(256 * g, 256 * g + 256)
        gm, p = gm_ref[0, :, sl], p_ref[0, :, sl]
        put_land(g, diag_blocks(dot_tn(p, gm), masks_wide).astype(bf16))
        d = dot_nt(gm, block_diag(mix_ref[0, :, sl], masks))
        pw = p.astype(f32)
        gs = (pw * (d - dot((pw * d).astype(bf16), ones))).astype(bf16)
        gq_ref[0, :, sl] = dot(gs, block_diag(kl_of(sl), masks)).astype(bf16)
        put_klp(g, diag_blocks(dot_tn(gs, q_ref[0, :, sl]), masks_wide))


def first_back_kernel(gm_ref, p_ref, q_ref, mix_ref, kl_ref, land_ref, gq_ref, klp_ref):
    def put_land(g, x):
        for i in range(2):
            land_ref[2 * g + i] = x[:, 128 * i : 128 * i + 128]

    def put_klp(g, x):
        klp_ref[0, :, 256 * g : 256 * g + 256] = x

    first_back_step(gm_ref, p_ref, q_ref, mix_ref, lambda sl: kl_ref[0, :, sl], put_land, gq_ref, put_klp)


def first_back(gm, probs, q, mixed, k_land):
    seqs, rows, features = q.shape
    pairs = features // 128
    full = pl.BlockSpec((1, rows, features), lambda s: (s, 0, 0))
    land = pl.BlockSpec((1, M, features), lambda s: (s, 0, 0))
    return pl.pallas_call(
        first_back_kernel,
        grid=(seqs,),
        in_specs=[full] * 3 + [land] * 2,
        out_specs=[pl.BlockSpec((pairs, M, 128), lambda s: (s, 0, 0)), full, land],
        out_shape=[
            jax.ShapeDtypeStruct((seqs * pairs, M, 128), bf16),
            jax.ShapeDtypeStruct(q.shape, bf16),
            jax.ShapeDtypeStruct((seqs, M, features), f32),
        ],
        compiler_params=params(48 * MB),
        name="first_back",
    )(gm, probs, q, mixed, k_land)


def third_back_kernel(w_ref, v_ref, k_ref, gc_ref, gn_ref, gt_ref, ql_ref, gv_ref, gk_ref, qlp_ref):
    features = w_ref.shape[2]
    masks = group_masks((M, 4 * E), 4, bf16)
    masks_wide = group_masks((M, 4 * E), 4, f32)
    for g in range(features // 256):
        sl = slice(256 * g, 256 * g + 256)
        w = w_ref[0, :, sl]
        gn = jnp.concatenate([gn_ref[2 * g], gn_ref[2 * g + 1]], axis=1)
        gt = jnp.concatenate([gt_ref[2 * g, 0:1, :], gt_ref[2 * g + 1, 0:1, :]], axis=1)
        gd = block_diag(gn, masks)
        gs = (w.astype(f32) * (dot_nt(v_ref[0, :, sl], gd) + gt)).astype(bf16)
        gv_ref[0, :, sl] = (dot(w, gd) + gc_ref[0, :, sl].astype(f32)).astype(bf16)
        gk_ref[0, :, sl] = dot(gs, block_diag(ql_ref[0, :, sl], masks)).astype(bf16)
        qlp_ref[0, :, sl] = diag_blocks(dot_tn(gs, k_ref[0, :, sl]), masks_wide)


def third_back(w, v, k, grad_conv, gn, gt, q_land):
    seqs, rows, features = v.shape
    pairs = features // 128
    full = pl.BlockSpec((1, rows, features), lambda s: (s, 0, 0))
    land = pl.BlockSpec((1, M, features), lambda s: (s, 0, 0))
    return pl.pallas_call(
        third_back_kernel,
        grid=(seqs,),
        in_specs=[full] * 4
        + [
            pl.BlockSpec((pairs, M, 128), lambda s: (s, 0, 0)),
            pl.BlockSpec((pairs, 8, 128), lambda s: (s, 0, 0)),
            land,
        ],
        out_specs=[full, full, land],
        out_shape=[jax.ShapeDtypeStruct(v.shape, bf16)] * 2
        + [jax.ShapeDtypeStruct((seqs, M, features), f32)],
        compiler_params=params(48 * MB),
        name="third_back",
    )(w, v, k, grad_conv, gn, gt, q_land)


def last_kernel(tok_ref, gq_ref, gk_ref, gv_ref, qo_ref, ko_ref, proj_ref, w_ref, gt_ref, wg_ref, d, tok_t):
    step = pl.program_id(0)
    seqs = tok_t.shape[1] // tok_ref.shape[1]
    rows, features = tok_ref.shape[1:]
    marks = qo_ref.shape[1]
    seg = rows // marks

    @pl.when(step < seqs)
    def _():
        here = pl.ds(pl.multiple_of(step * rows, rows), rows)
        for part, (core, own) in enumerate(((gq_ref, qo_ref), (gk_ref, ko_ref))):
            for m in range(marks):
                at = pl.ds(pl.multiple_of(step * rows + m * seg, seg), seg)
                x = core[0, m * seg : m * seg + seg, :].astype(f32) + own[0, m : m + 1, :] * (1.0 / seg)
                x = x.astype(bf16)
                if part == 0:
                    x = x * jnp.asarray(0.125, bf16)
                d[at, part * features : part * features + features] = x
        d[here, 2 * features :] = gv_ref[0]
        tok_t[:, here] = tok_ref[0].T
        for c in range(0, rows, 128):
            at = pl.ds(pl.multiple_of(step * rows + c, 128), 128)
            gt_ref[0, c : c + 128, :] = (
                proj_ref[0, c : c + 128, :].astype(f32) + dot_nt(d[at, :], w_ref[...])
            ).astype(bf16)

    @pl.when(step >= seqs)
    def _():
        base = (step - seqs) * features
        for c in range(0, features, 256):
            cols = pl.ds(pl.multiple_of(base + c, 256), 256)
            wg_ref[0, :, c : c + 256] = dot(tok_t[...], d[:, cols]).astype(bf16)


def last_pass(tokens, gq, gk, gv, q_own, k_own, proj, w_qkv):
    seqs, rows, features = tokens.shape
    marks = q_own.shape[1]
    here = lambda i: jnp.minimum(i, seqs - 1)
    full = pl.BlockSpec((1, rows, features), lambda i: (here(i), 0, 0))
    land = pl.BlockSpec((1, marks, features), lambda i: (here(i), 0, 0))
    return pl.pallas_call(
        last_kernel,
        grid=(seqs + 3,),
        in_specs=[full] * 4 + [land] * 2
        + [full, pl.BlockSpec(w_qkv.shape, lambda i: (0, 0), pipeline_mode=pl.Buffered(1))],
        out_specs=[full, pl.BlockSpec((1, features, features), lambda i: (jnp.maximum(i - seqs, 0), 0, 0))],
        out_shape=[
            jax.ShapeDtypeStruct(tokens.shape, bf16),
            jax.ShapeDtypeStruct((3, features, features), bf16),
        ],
        scratch_shapes=[
            pltpu.VMEM((seqs * rows, 3 * features), bf16), pltpu.VMEM((features, seqs * rows), bf16),
        ],
        compiler_params=params(56 * MB),
        name="last_pass",
    )(tokens, gq, gk, gv, q_own, k_own, proj, w_qkv)


def add_pairs(dst, own, start, pairs):
    for i in range(own.shape[0]):
        @pl.when(start + i < pairs)
        def _(i=i):
            dst[start + i] += own[i]


def first_conv_kernel(
    gm_ref, p_ref, q_ref, mix_ref, marks_ref, cg_ref, rim_ref, cv_ref, f_ref, g_in,
    gq_ref, klp_ref, co_ref, gf_ref, land_out, got,
    land, pad, facc, land_sems, sems,
):
    step = pl.program_id(0)
    steps = pl.num_programs(0)
    own = land_out.shape[1]
    pairs = q_ref.shape[2] // 128
    seqs = klp_ref.shape[0] // pairs
    core, x, y, _, along_x, along_y = cube()
    halves = [
        remote(g_in.at[0:2, :, 1 - x], got.at[0], sems.at[0, 0], sems.at[1, 0], along_x),
        remote(g_in.at[2:4, 1 - y], got.at[1], sems.at[0, 1], sems.at[1, 1], along_y),
    ]

    @pl.when(step == 0)
    def _():
        greet([along_x, along_y])
        for copy in halves:
            copy.start()
        if land.shape[0] > seqs * pairs:
            land[seqs * pairs :] = jnp.zeros_like(land[seqs * pairs :])

    @pl.when(step < seqs)
    def _():
        def put_land(g, v):
            for i in range(2):
                land[step * pairs + 2 * g + i] = v[:, 128 * i : 128 * i + 128]

        def put_klp(g, v):
            for i in range(2):
                klp_ref[step * pairs + 2 * g + i] = v[:, 128 * i : 128 * i + 128]

        first_back_step(
            gm_ref, p_ref, q_ref, mix_ref, lambda sl: marks_ref[0, 1, :, sl], put_land, gq_ref, put_klp
        )

    @pl.when(step == seqs - 1)
    def _():
        begin(swap_copies(land, land_out, own, land_sems))

    @pl.when(step >= seqs)
    def _():
        seq = (step - seqs) % seqs
        conv_back_tile(seq, seqs, cg_ref, rim_ref, cv_ref, f_ref, co_ref, gf_ref, pad, facc)

    @pl.when(step == steps - 1)
    def _():
        finish(swap_copies(land, land_out, own, land_sems))
        for copy in halves:
            copy.wait()


def first_conv(gm, probs, q, mixed, land, rim, v, taps, grads, own, groups):
    seqs, rows, features = q.shape
    ranks = lax.axis_size("seq")
    pairs = features // 128
    here = lambda i: jnp.minimum(i, seqs - 1)
    full = pl.BlockSpec((1, rows, features), lambda i: (here(i), 0, 0))
    cv, rims, ft, co, go = conv_back_specs(rows, seqs, seqs, 0)
    return pl.pallas_call(
        first_conv_kernel,
        grid=(seqs + seqs * groups,),
        in_specs=[full] * 3
        + [
            pl.BlockSpec((1, M, features), lambda i: (here(i), 0, 0)),
            pl.BlockSpec((1, 2, M, features), lambda i: (here(i), 0, 0, 0)),
            cv, rims, cv, ft, ANY,
        ],
        out_specs=[full, pl.BlockSpec((seqs * pairs, M, 128), lambda i: (0, 0, 0)), co, go, ANY, ANY],
        out_shape=[
            jax.ShapeDtypeStruct(q.shape, bf16),
            jax.ShapeDtypeStruct((seqs * pairs, M, 128), f32),
            jax.ShapeDtypeStruct((seqs, rows, 128 * groups), bf16),
            jax.ShapeDtypeStruct((KW, 128 * groups), f32),
            jax.ShapeDtypeStruct((ranks, own, M, 128), bf16),
            jax.ShapeDtypeStruct((2, 2, 2) + grads.shape[3:], bf16),
        ],
        scratch_shapes=[
            pltpu.VMEM((ranks * own, M, 128), bf16), pltpu.VMEM((rows + 2 * RIM, 128), f32),
            pltpu.VMEM((KW * 8, 128), f32), rank_sems(), pltpu.SemaphoreType.DMA((2, 2)),
        ],
        compiler_params=params(48 * MB, collective_id=4, has_side_effects=True),
        name="first_conv",
    )(gm, probs, q, mixed, land, gm, rim, v, taps, grads)


def inverse_conv_kernel(
    land_ref, marks_ref, sum_ref, mid_ref, z_ref, p_ref, a_ref, w_ref, scale_ref, tot_ref, alpha_ref, klp_ref,
    cg_ref, rim_ref, cv_ref, f_ref, s_in,
    mq_ref, co_ref, gf_ref, gn_out, gt_out, kl_out, got,
    gn, gt, mk, g_acc, dk_acc, kl, pad, facc, gn_sems, gt_sems, kl_sems, sems,
):
    step = pl.program_id(0)
    ranks, own = land_ref.shape[:2]
    me, _ = seq_place()
    marks = kl_out.shape[2]
    seqs = marks_ref.shape[0]
    core, x, y, _, along_x, along_y = cube()
    halves = [
        remote(s_in.at[0, :, 1 - y], got.at[0], sems.at[0, 0], sems.at[1, 0], along_y),
        remote(s_in.at[1, :, 1 - x], got.at[1], sems.at[0, 1], sems.at[1, 1], along_x),
    ]

    def mark_copies():
        sends = [
            remote(
                kl.at[:, pl.ds(peer * marks, marks)], kl_out.at[me], kl_sems.at[0, o], kl_sems.at[1, o],
                {"seq": peer},
            )
            for o, peer in seq_peers()
        ]
        return sends, pltpu.make_async_copy(
            kl.at[:, pl.ds(me * marks, marks)], kl_out.at[me], kl_sems.at[0, 0]
        )

    exchanges = [
        swap_rows(gn, gn_out, gn_sems), swap_rows(gt, gt_out, gt_sems), mark_copies(),
    ]

    @pl.when(step == 0)
    def _():
        greet([along_x, along_y])
        for copy in halves:
            copy.start()
        inverse_back_step(
            land_ref, marks_ref, sum_ref, mid_ref, z_ref, p_ref, a_ref, w_ref, scale_ref, tot_ref, alpha_ref,
            gn, gt, mq_ref, mk, g_acc, dk_acc,
        )
        add_pairs(klp_ref, mk, me * own, klp_ref.shape[0])
        kl[...] = klp_ref[...].astype(bf16)
        for pair in exchanges:
            begin(pair)

    @pl.when(step > 0)
    def _():
        conv_back_tile((step - 1) % seqs, seqs, cg_ref, rim_ref, cv_ref, f_ref, co_ref, gf_ref, pad, facc)

    @pl.when(step == pl.num_programs(0) - 1)
    def _():
        for pair in exchanges:
            finish(pair)
        for copy in halves:
            copy.wait()


def inverse_conv(land_parts, land, saved, klp, gm, rim, v, taps, sums, first_group):
    ranks, own = land_parts.shape[:2]
    seqs, rows, features = v.shape
    pairs = features // 128 * seqs
    groups = features // 128 - first_group
    marks = M // ranks
    mat = jax.ShapeDtypeStruct((own, M, 128), f32)
    whole = lambda a: pl.BlockSpec(a.shape, lambda i: (0,) * len(a.shape), pipeline_mode=pl.Buffered(1))
    cv, rims, ft, co, go = conv_back_specs(rows, seqs, 1, first_group)
    return pl.pallas_call(
        inverse_conv_kernel,
        grid=(1 + seqs * groups,),
        in_specs=[whole(land_parts), whole(land)] + [whole(a) for a in saved] + [whole(klp), cv, rims, cv, ft, ANY],
        out_specs=[whole(mat), co, go] + [ANY] * 4,
        out_shape=[
            mat,
            jax.ShapeDtypeStruct((seqs, rows, 128 * groups), bf16),
            jax.ShapeDtypeStruct((KW, 128 * groups), f32),
            jax.ShapeDtypeStruct((ranks, own, M, 128), bf16),
            jax.ShapeDtypeStruct((ranks, own, 8, 128), f32),
            jax.ShapeDtypeStruct((ranks, pairs, marks, 128), bf16),
            jax.ShapeDtypeStruct((2, 2) + sums.shape[3:], bf16),
        ],
        scratch_shapes=[
            pltpu.VMEM((ranks, own, M, 128), bf16), pltpu.VMEM((ranks, own, 8, 128), f32),
            pltpu.VMEM((own, M, 128), f32), pltpu.VMEM((own, M, 128), f32), pltpu.VMEM((own, M, 128), f32),
            pltpu.VMEM((pairs, M, 128), bf16), pltpu.VMEM((rows + 2 * RIM, 128), f32),
            pltpu.VMEM((KW * 8, 128), f32), rank_sems(), rank_sems(), rank_sems(),
            pltpu.SemaphoreType.DMA((2, 2)),
        ],
        compiler_params=params(48 * MB, collective_id=5, has_side_effects=True),
        name="inverse_conv",
    )(land_parts, land, *saved, klp, gm, rim, v, taps, sums)


def third_step(w_ref, v_ref, k_ref, conv_of, gn_of, gt_of, ql_of, put_v, put_k, put_qlp):
    features = w_ref.shape[2]
    masks = group_masks((M, 4 * E), 4, bf16)
    masks_wide = group_masks((M, 4 * E), 4, f32)
    for g in range(features // 256):
        sl = slice(256 * g, 256 * g + 256)
        w = w_ref[0, :, sl]
        gd = block_diag(jnp.concatenate([gn_of(2 * g), gn_of(2 * g + 1)], axis=1), masks)
        gt = jnp.concatenate([gt_of(2 * g), gt_of(2 * g + 1)], axis=1)
        gs = (w.astype(f32) * (dot_nt(v_ref[0, :, sl], gd) + gt)).astype(bf16)
        put_v(g, (dot(w, gd) + conv_of(g)).astype(bf16))
        put_k(g, dot(gs, block_diag(ql_of(sl), masks)))
        put_qlp(g, diag_blocks(dot_tn(gs, k_ref[0, :, sl]), masks_wide))


def final_kernel(
    w_ref, v_ref, k_ref, tok_ref, ca_ref, cb_ref, gn_ref, gt_ref, marks_ref, gq_ref, kl_ref, mq_ref, proj_ref,
    wq_ref, small_ref, v_in,
    gtok_ref, share_ref, tot_ref, w_out,
    d, tok_t, qlp, qlow, qgot, part, got_a, sum_a, got_b, sum_b, got_c, sum_c, got_z,
    sm_got, sm_sum, q_sems, z_sems, a_send, a_recv, b_sems, c_sems, zq_sems, s_send, s_recv, s_sems,
):
    step = pl.program_id(0)
    seqs, _, rows, features = 3, 0, tok_ref.shape[1], tok_ref.shape[2]
    seqs = gq_ref.shape[0]
    pairs = features // 128
    ranks, marks = kl_ref.shape[0], kl_ref.shape[2]
    own = mq_ref.shape[0]
    seg = rows // marks
    me, _ = seq_place()
    core, x, y, sibling, along_x, along_y = cube()

    def z_copies():
        sends = [
            remote(v_in.at[peer], w_out.at[me], z_sems.at[0, o], z_sems.at[1, o], {"seq": peer})
            for o, peer in seq_peers()
        ]
        return sends, pltpu.make_async_copy(v_in.at[me], w_out.at[me], z_sems.at[0, 0])

    def q_copies():
        sends = [
            remote(
                qlow.at[:, pl.ds(peer * marks, marks)], qgot.at[me], q_sems.at[0, o], q_sems.at[1, o],
                {"seq": peer},
            )
            for o, peer in seq_peers()
        ]
        return sends, pltpu.make_async_copy(
            qlow.at[:, pl.ds(me * marks, marks)], qgot.at[me], q_sems.at[0, 0]
        )

    def a_copy(p):
        return remote(
            part.at[1 - core, pl.ds(4 * p, 4)], got_a.at[pl.ds(4 * p, 4)], a_send.at[p], a_recv.at[p], sibling
        )

    b_copies = [
        remote(sum_a.at[0:6, :, 1 - x], got_b.at[0], b_sems.at[0, 0], b_sems.at[1, 0], along_x),
        remote(sum_a.at[6:12, 1 - y], got_b.at[1], b_sems.at[0, 1], b_sems.at[1, 1], along_y),
    ]
    c_copies = [
        remote(sum_b.at[0, :, 1 - y], got_c.at[0], c_sems.at[0, 0], c_sems.at[1, 0], along_y),
        remote(sum_b.at[1, :, 1 - x], got_c.at[1], c_sems.at[0, 1], c_sems.at[1, 1], along_x),
    ]
    zq_copies = [
        remote(sum_c.at[pl.ds(3 * peer, 3)], got_z.at[me], zq_sems.at[0, o], zq_sems.at[1, o], {"seq": peer})
        for o, peer in seq_peers()
    ]

    small_copies = [
        remote(sm_sum.at[i], sm_got.at[i], s_send.at[i], s_recv.at[i], target)
        for i, target in enumerate((sibling, along_x, along_y))
    ]

    def small_spread():
        return [
            remote(sm_sum.at[3], sm_got.at[3 + me], s_sems.at[0, o], s_sems.at[1, o], {"seq": peer})
            for o, peer in seq_peers()
        ]

    @pl.when(step == 0)
    def _():
        greet([sibling, along_x, along_y])
        begin(z_copies())
        sm_sum[0] = small_ref[...]
        small_copies[0].start()

    for i in range(1, 4):
        @pl.when(step == i)
        def _(i=i):
            small_copies[i - 1].wait()
            sm_sum[i] = sm_sum[i - 1] + sm_got[i - 1]
            if i < 3:
                small_copies[i].start()
            else:
                for copy in small_spread():
                    copy.start()

    def land_rows(of):
        total = of(0).astype(f32)
        for r in range(1, ranks):
            total = total + of(r).astype(f32)
        return total * (1.0 / seg)

    @pl.when(step < seqs)
    def _():
        start = step * rows

        def conv_of(g):
            half = ca_ref.shape[2]
            at = 256 * g
            pieces = []
            for l in (at, at + 128):
                ref, lane = (ca_ref, l) if l < half else (cb_ref, l - half)
                pieces.append(ref[0, :, lane : lane + 128].astype(f32))
            return jnp.concatenate(pieces, axis=1)

        def put_v(g, val):
            d[pl.ds(pl.multiple_of(start, rows), rows), 2 * features + 256 * g : 2 * features + 256 * g + 256] = val

        def put_k(g, val):
            for i in range(2):
                p = step * pairs + 2 * g + i
                spread = land_rows(lambda r: kl_ref[r, p])
                lane = features + 256 * g + 128 * i
                for m in range(marks):
                    at = pl.ds(pl.multiple_of(start + m * seg, seg), seg)
                    d[at, lane : lane + 128] = (
                        val[m * seg : m * seg + seg, 128 * i : 128 * i + 128] + spread[m : m + 1]
                    ).astype(bf16)

        def put_qlp(g, val):
            for i in range(2):
                qlp[step * pairs + 2 * g + i] = val[:, 128 * i : 128 * i + 128]

        third_step(
            w_ref, v_ref, k_ref, conv_of, lambda i: gn_ref[step * pairs + i],
            lambda i: gt_ref[step * pairs + i, 0:1, :], lambda sl: marks_ref[0, 0, :, sl], put_v, put_k, put_qlp,
        )
        tok_t[:, pl.ds(pl.multiple_of(start, rows), rows)] = tok_ref[0].T

    @pl.when(step == seqs - 1)
    def _():
        add_pairs(qlp, mq_ref, me * own, seqs * pairs)
        qlow[...] = qlp[...].astype(bf16)
        begin(q_copies())

    @pl.when(step == seqs + 2)
    def _():
        finish(q_copies())

        def fill(s, carry):
            for g in range(pairs):
                spread = land_rows(lambda r: qgot[r, s * pairs + g])
                for m in range(marks):
                    at = pl.ds(pl.multiple_of(s * rows + m * seg, seg), seg)
                    val = gq_ref[s, m * seg : m * seg + seg, 128 * g : 128 * g + 128].astype(f32)
                    low = (val + spread[m : m + 1]).astype(bf16) * jnp.asarray(0.125, bf16)
                    d[at, 128 * g : 128 * g + 128] = low
            return carry

        lax.fori_loop(0, seqs, fill, 0)

    @pl.when((step >= seqs) & (step < seqs + 3))
    def _():
        p = seqs + 2 - step
        for c in range(2):
            cols = pl.ds(pl.multiple_of(p * features + 384 * c, 128), 384)
            low = dot(tok_t[...], d[:, cols]).astype(bf16)
            for i in range(2):
                for dd in range(8):
                    block = low[96 * dd : 96 * dd + 96, 192 * i : 192 * i + 192]
                    part[dd % 2, 4 * p + 2 * c + i, dd // 2] = jnp.concatenate([block[:48], block[48:]], axis=1)
        a_copy(p).start()

    @pl.when(step == seqs + 3)
    def _():
        for p in range(3):
            a_copy(p).wait()
        for yx in range(4):
            sum_a[:, yx // 2, yx % 2] = add_low(part[core, :, yx], got_a[:, yx])
        for copy in b_copies:
            copy.start()

    @pl.when(step == seqs + 4)
    def _():
        for copy in b_copies:
            copy.wait()
        sum_b[0] = add_low(sum_a[0:6, :, x], got_b[0])
        sum_b[1] = add_low(sum_a[6:12, y], got_b[1])
        for copy in c_copies:
            copy.start()

    @pl.when(step == seqs + 5)
    def _():
        for copy in c_copies:
            copy.wait()
        sum_c[0:6] = add_low(sum_b[0, :, y], got_c[0])
        sum_c[6:12] = add_low(sum_b[1, :, x], got_c[1])
        for copy in zq_copies:
            copy.start()

    @pl.when((step >= seqs + 3) & (step < 2 * seqs + 3))
    def _():
        start = (step - seqs - 3) * rows
        for c in range(0, rows, 128):
            at = pl.ds(pl.multiple_of(start + c, 128), 128)
            gtok_ref[0, c : c + 128, :] = (
                proj_ref[0, c : c + 128, :].astype(f32) + dot_nt(d[at, :], wq_ref[...])
            ).astype(bf16)

    @pl.when(step == 2 * seqs + 3)
    def _():
        for copy in zq_copies:
            copy.wait()
        got_z[me] = sum_c[pl.ds(3 * me, 3)]
        share_ref[...] = sum(got_z[r].astype(f32) for r in range(ranks))
        for copy in small_spread():
            copy.wait()
        sm_got[3 + me] = sm_sum[3]
        tot_ref[...] = (sm_got[3] + sm_got[4]) + (sm_got[5] + sm_got[6])
        finish(z_copies())


def final_pass(
    weights, v, k, tokens, conv_a, conv_b, gn, gt, land, gq, kl_parts, mid_q, proj, w_qkv, small, ff_sums
):
    seqs, rows, features = tokens.shape
    ranks = lax.axis_size("seq")
    pairs = features // 128 * seqs
    marks = M // ranks
    here = lambda i: jnp.minimum(i, seqs - 1)
    late = lambda i: jnp.clip(i - seqs - 3, 0, seqs - 1)
    full = lambda a: pl.BlockSpec((1, rows, a.shape[2]), lambda i: (here(i), 0, 0))
    later = pl.BlockSpec((1, rows, features), lambda i: (late(i), 0, 0))
    whole = lambda a: pl.BlockSpec(a.shape, lambda i: (0,) * len(a.shape), pipeline_mode=pl.Buffered(1))
    vm = lambda *shape: pltpu.VMEM(shape, bf16)
    dma = pltpu.SemaphoreType.DMA
    return pl.pallas_call(
        final_kernel,
        grid=(2 * seqs + 4,),
        in_specs=[full(weights), full(v), full(k), full(tokens), full(conv_a), full(conv_b), whole(gn), whole(gt)]
        + [pl.BlockSpec((1, 2, M, features), lambda i: (here(i), 0, 0, 0)), whole(gq), whole(kl_parts), whole(mid_q)]
        + [later, whole(w_qkv), whole(small), ANY],
        out_specs=[later, whole(jax.ShapeDtypeStruct((3, 48, 384), f32)), whole(small), ANY],
        out_shape=[
            jax.ShapeDtypeStruct(tokens.shape, bf16),
            jax.ShapeDtypeStruct((3, 48, 384), f32),
            jax.ShapeDtypeStruct(small.shape, f32),
            jax.ShapeDtypeStruct(ff_sums.shape, bf16),
        ],
        scratch_shapes=[
            vm(seqs * rows, 3 * features), vm(features, seqs * rows), pltpu.VMEM((pairs, M, 128), f32),
            vm(pairs, M, 128), vm(ranks, pairs, marks, 128), vm(2, 12, 4, 48, 384), vm(12, 4, 48, 384),
            vm(12, 2, 2, 48, 384), vm(2, 6, 2, 48, 384), vm(2, 6, 2, 48, 384), vm(2, 6, 48, 384), vm(12, 48, 384),
            vm(ranks, 3, 48, 384), pltpu.VMEM((3 + ranks,) + small.shape, f32),
            pltpu.VMEM((4,) + small.shape, f32), rank_sems(), rank_sems(), dma((3,)), dma((3,)), dma((2, 2)),
            dma((2, 2)), rank_sems(), dma((3,)), dma((3,)), rank_sems(),
        ],
        compiler_params=params(58 * MB, collective_id=6, has_side_effects=True),
        name="final_pass",
    )(weights, v, k, tokens, conv_a, conv_b, gn, gt, land, gq, kl_parts, mid_q, proj, w_qkv, small, ff_sums)


def halo(cells, width):
    count = lax.axis_size("seq")
    head, tail = cells[:, :width], cells[:, cells.shape[1] - width :]
    left = lax.ppermute(tail, "seq", [(i, i + 1) for i in range(count - 1)])
    right = lax.ppermute(head, "seq", [(i + 1, i) for i in range(count - 1)])
    return jnp.stack([left, right], axis=1)


def scatter_sum(grad):
    share = lax.psum_scatter(grad, "dp", scatter_dimension=0, tiled=True)
    return lax.psum_scatter(share, "seq", scatter_dimension=1, tiled=True).astype(f32)


def per_device_general(tokens, w_qkv, w_out, w_up, w_down, conv_filter, gain_att, gain_ffn, grad_out):
    seqs, rows, features = tokens.shape
    ranks = lax.axis_size("seq")
    rank = lax.axis_index("seq")
    marks = M // ranks
    ff = w_up.shape[1]
    pairs = seqs * (features // 128)
    own = -(-pairs // ranks)

    def from_pairs(x):
        x = x[:pairs].reshape(seqs, features // 128, M, 128).transpose(0, 2, 1, 3)
        return x.reshape(seqs, M, features)

    def pad_pairs(x):
        return jnp.pad(x, ((0, ranks * own - pairs),) + ((0, 0),) * (x.ndim - 1))

    def exchange(x):
        out = lax.all_to_all(pad_pairs(x), "seq", 0, 0, tiled=True)
        return out.reshape((ranks, own) + x.shape[1:])

    taps = conv_filter.astype(f32)
    q, k, v, land, v_rim = project(tokens, w_qkv, marks)
    q_land, k_land = land[:, 0], land[:, 1]
    first_group = features // 256
    weights, probs, conv_a, num_parts, stat_parts = scores(q, k, v, land, v_rim, taps, own, first_group)
    mixed_pairs, conv_b, *saved = inverse(num_parts, stat_parts, land, v, v_rim, taps, first_group)
    mixed = from_pairs(mixed_pairs)
    layer_out, proj, gm, wg, gains = row_pass(
        tokens, probs, conv_a, conv_b, mixed, grad_out, w_out, w_up, w_down, gain_att, gain_ffn
    )
    shape3 = (seqs, rows, features)
    gm = gm.reshape(shape3)
    chunks = ff // features
    up_share = scatter_sum(wg[:chunks].transpose(1, 0, 2).reshape(features, ff))
    down_share = scatter_sum(wg[chunks : 2 * chunks].transpose(0, 2, 1).reshape(ff, features))
    out_share = scatter_sum(wg[2 * chunks])
    land_part, gq, k_land_part = first_back(gm, probs, q, mixed, k_land)
    g_rim = halo(gm, RIM)
    land_parts = exchange(land_part)
    grad_conv, taps_grad = conv_back(gm, g_rim, v, taps)
    gn_own, gt_own, mid_q, mid_k = inverse_back(land_parts, land, saved)

    def give_back(x):
        x = x.reshape((ranks * own,) + x.shape[2:])
        return lax.all_to_all(x, "seq", 0, 0, tiled=True)[:pairs]

    grad_values, gk, q_land_part = third_back(
        weights, v, k, grad_conv, give_back(gn_own), give_back(gt_own), q_land
    )

    def place(x):
        full = jnp.zeros((ranks * own, M, 128), f32)
        return from_pairs(lax.dynamic_update_slice_in_dim(full, x, rank * own, 0))

    both = jnp.stack([q_land_part + place(mid_q), k_land_part + place(mid_k)]).astype(bf16)
    both = both.reshape(2, seqs, ranks, marks, features).transpose(2, 0, 1, 3, 4)
    both = lax.all_to_all(both, "seq", 0, 0, tiled=True).astype(f32).sum(0)
    grad_tokens, qkv_grad = last_pass(tokens, gq, gk, grad_values, both[0], both[1], proj.reshape(shape3), w_qkv)
    qkv_share = scatter_sum(qkv_grad.transpose(1, 0, 2).reshape(features, 3 * features))
    gains = gains.reshape(2, 8, features).sum(1)
    small = lax.psum(jnp.concatenate([taps_grad, gains]), ("dp", "seq"))
    return (
        layer_out.reshape(shape3),
        grad_tokens,
        qkv_share,
        out_share,
        up_share,
        down_share,
        small[:KW],
        small[KW],
        small[KW + 1],
    )


def pick(x, index, axis):
    return lax.dynamic_index_in_dim(x, index, axis, keepdims=False)


def per_device(tokens, w_qkv, w_out, w_up, w_down, conv_filter, gain_att, gain_ffn, grad_out):
    seqs, rows, features = tokens.shape
    ranks = lax.axis_size("seq")
    marks = M // ranks
    pairs = seqs * (features // 128)
    own = -(-pairs // ranks)
    taps = conv_filter.astype(f32)
    half = features // 256
    core, x, y, _, _, _ = cube()

    q, k, v, land, v_rim = project(tokens, w_qkv, marks)
    weights, probs, conv_a, num_parts, stat_parts = scores(q, k, v, land, v_rim, taps, own, half)
    mixed_pairs, conv_b, *saved = inverse(num_parts, stat_parts, land, v, v_rim, taps, half)
    mixed = mixed_pairs[:pairs].reshape(seqs, features // 128, M, 128).transpose(0, 2, 1, 3)
    mixed = mixed.reshape(seqs, M, features)
    layer_out, proj, gm, gains, grads, g_rim = row_share(
        tokens, probs, conv_a, conv_b, mixed, grad_out, w_out, w_up, w_down, gain_att, gain_ffn
    )
    shape3 = (seqs, rows, features)
    gm = gm.reshape(shape3)
    grads = grads.reshape(4, 2, 2, 432, 384)
    gq, klp, gconv_a, taps_a, land_parts, got = first_conv(
        gm, probs, q, mixed, land, g_rim, v, taps, grads, own, half
    )
    sums = jnp.stack([add_low(pick(grads[0:2], x, 2), got[0]), add_low(pick(grads[2:4], y, 1), got[1])])
    mid_q, gconv_b, taps_b, gn, gt, kl_parts, got = inverse_conv(
        land_parts, land, saved, klp, gm, g_rim, v, taps, sums, half
    )
    sums = jnp.concatenate([add_low(pick(sums[0], y, 1), got[0]), add_low(pick(sums[1], x, 1), got[1])])
    gains = gains.reshape(2, 8, features).sum(1)
    small = jnp.concatenate(
        [jnp.concatenate([taps_a, taps_b], axis=1), gains, jnp.zeros((5, features), f32)]
    )
    grad_tokens, qkv, small, ff = final_pass(
        weights, v, k, tokens, gconv_a, gconv_b, gn.reshape(ranks * own, M, 128),
        gt.reshape(ranks * own, 8, 128), land, gq, kl_parts, mid_q, proj.reshape(shape3), w_qkv, small, sums,
    )
    ff = ff.astype(f32).sum(0)
    halves = lambda a: a.reshape(-1, 48, 2, 192).transpose(2, 1, 0, 3).reshape(96, -1)
    up = ff[:192].reshape(2, 96, 384).transpose(1, 0, 2).reshape(96, 768)
    return (
        layer_out.reshape(shape3),
        grad_tokens,
        halves(qkv),
        halves(ff[384:432]),
        up,
        ff[192:384].T,
        small[:KW],
        small[KW],
        small[KW + 1],
    )


def solution(mesh):
    placed = (P("dp", "seq", None), P(), P(), P(), P(), P(), P(), P(), P("dp", "seq", None))
    eight_by_four = mesh.shape["dp"] == 8 and mesh.shape["seq"] == 4
    return jax.shard_map(
        per_device if eight_by_four else per_device_general,
        mesh=mesh,
        in_specs=placed,
        out_specs=(
            P("dp", "seq", None),
            P("dp", "seq", None),
            P("dp", "seq"),
            P("dp", "seq"),
            P("dp", "seq"),
            P("dp", "seq"),
            P(),
            P(),
            P(),
        ),
        check_vma=False,
    )
```

```python
import functools

import jax
import jax.numpy as jnp
from jax import lax
from jax.experimental import pallas as pl
from jax.experimental.pallas import tpu as pltpu
from jax.sharding import PartitionSpec as P

H = 12
E = 64
M = 64
KW = 33
RIM = KW // 2
NEWTON = 6

f32 = jnp.float32
bf16 = jnp.bfloat16
epsilon = 1e-05
root_half = 0.7071067811865476
inv_root_two_pi = 0.3989422804014327
MB = 1 << 20

ERFC_P = 0.39
ERFC_C = (
    0.23532530842493793,
    0.09138785409700201,
    0.6495607954603394,
    -0.6354020079402325,
    0.8866654334206034,
    -0.22753738516480188,
)


def dot(a, b):
    return lax.dot_general(a, b, (((1,), (0,)), ((), ())), preferred_element_type=f32)


def dot_nt(a, b):
    return lax.dot_general(a, b, (((1,), (1,)), ((), ())), preferred_element_type=f32)


def dot_tn(a, b):
    return lax.dot_general(a, b, (((0,), (0,)), ((), ())), preferred_element_type=f32)


def lane_group(shape):
    return lax.broadcasted_iota(jnp.int32, shape, len(shape) - 1) // E


def group_masks(shape, count, dtype):
    groups = lane_group(shape)
    return [(groups == h).astype(f32).astype(dtype) for h in range(count)]


def block_diag(x, masks):
    return jnp.concatenate([x * m for m in masks], axis=0)


def diag_blocks(n, masks):
    return sum(n[E * h : E * h + E] * m for h, m in enumerate(masks))


def quad(ref, g):
    return jnp.concatenate([ref[2 * g], ref[2 * g + 1]], axis=1)


def params(limit=None, **kw):
    return pltpu.CompilerParams(vmem_limit_bytes=limit, **kw)


MESH = pl.DeviceIdType.MESH
ANY = pl.BlockSpec(memory_space=pl.ANY)


def seq_place():
    return lax.axis_index("seq"), lax.axis_size("seq")


def seq_peers():
    me, count = seq_place()
    return [(o, lax.rem(me + o, count)) for o in range(1, count)]


def greet(extra=()):
    barrier = pltpu.get_barrier_semaphore()
    targets = [{"seq": peer} for _, peer in seq_peers()] + list(extra)
    for target in targets:
        pl.semaphore_signal(barrier, inc=1, device_id=target, device_id_type=MESH)
    pl.semaphore_wait(barrier, len(targets))


def remote(src, dst, send, recv, target):
    return pltpu.make_async_remote_copy(
        src_ref=src, dst_ref=dst, send_sem=send, recv_sem=recv, device_id=target, device_id_type=MESH
    )


def swap_copies(src, dst, own, sems):
    me, count = seq_place()
    copies = [
        remote(src.at[pl.ds(peer * own, own)], dst.at[me], sems.at[0, o], sems.at[1, o], {"seq": peer})
        for o, peer in seq_peers()
    ]
    return copies, pltpu.make_async_copy(src.at[pl.ds(me * own, own)], dst.at[me], sems.at[0, 0])


def spread_copies(src, dst, own, sems):
    me, count = seq_place()
    at = dst.at[pl.ds(me * own, own)]
    copies = [
        remote(src, at, sems.at[0, o], sems.at[1, o], {"seq": peer}) for o, peer in seq_peers()
    ]
    return copies, pltpu.make_async_copy(src, at, sems.at[0, 0])


def begin(pair):
    for copy in pair[0]:
        copy.start()
    pair[1].start()


def finish(pair):
    for copy in pair[0]:
        copy.wait()
    pair[1].wait()


def swap_rows(src, dst, sems):
    me, _ = seq_place()
    copies = [
        remote(src.at[peer], dst.at[me], sems.at[0, o], sems.at[1, o], {"seq": peer}) for o, peer in seq_peers()
    ]
    return copies, pltpu.make_async_copy(src.at[me], dst.at[me], sems.at[0, 0])


def cube():
    d = lax.axis_index("dp")
    core, x, y = d % 2, (d // 2) % 2, d // 4
    return core, x, y, {"dp": d + 1 - 2 * core}, {"dp": d + 2 - 4 * x}, {"dp": d + 4 - 8 * y}


def add_low(a, b):
    return (a.astype(f32) + b.astype(f32)).astype(bf16)


def rank_sems():
    return pltpu.SemaphoreType.DMA((2, lax.axis_size("seq")))


def project_kernel(
    tok_ref, w_ref, q_ref, k_ref, v_ref, land_out, rim_out, land, rim, send, recv, local, rim_send, rim_recv,
    rim_local,
):
    step = pl.program_id(0)
    seqs = pl.num_programs(0)
    me, count = seq_place()
    rows, features = tok_ref.shape[1:]
    marks = land.shape[2]
    seg = rows // marks

    @pl.when(step == 0)
    def _():
        greet()

    x = tok_ref[0]
    for part, out in enumerate((q_ref, k_ref, v_ref)):
        for c in range(0, features, 256):
            p = dot(x, w_ref[:, part * features + c : part * features + c + 256])
            if part == 0:
                p = 0.125 * p
            low = p.astype(bf16)
            out[0, :, c : c + 256] = low
            if part < 2:
                total = low.astype(f32).reshape(marks, seg, 256).sum(1)
                land[step, part, :, c : c + 256] = (total * (1.0 / seg)).astype(bf16)
            else:
                rim[step, 0, :, c : c + 256] = low[rows - RIM :]
                rim[step, 1, :, c : c + 256] = low[:RIM]

    def copies(s):
        spot = land_out.at[s, :, pl.ds(me * marks, marks)]
        sends = [
            remote(land.at[s], spot, send.at[s, o], recv.at[s, o], {"seq": peer}) for o, peer in seq_peers()
        ]
        return sends, pltpu.make_async_copy(land.at[s], spot, local.at[s])

    def rim_copy(s, side):
        there = lax.rem(me + (1 if side == 0 else count - 1), count)
        return remote(
            rim.at[s, side], rim_out.at[s, side], rim_send.at[s, side], rim_recv.at[s, side], {"seq": there}
        )

    begin(copies(step))
    for side in range(2):
        rim_copy(step, side).start()

    @pl.when(step == seqs - 1)
    def _():
        def drain(s, carry):
            finish(copies(s))
            for side in range(2):
                rim_copy(s, side).wait()
            return carry

        lax.fori_loop(0, seqs, drain, 0)


def project(tokens, w_qkv, marks):
    seqs, rows, features = tokens.shape
    ranks = lax.axis_size("seq")
    full = pl.BlockSpec((1, rows, features), lambda s: (s, 0, 0))
    dma = pltpu.SemaphoreType.DMA
    return pl.pallas_call(
        project_kernel,
        grid=(seqs,),
        in_specs=[full, pl.BlockSpec(w_qkv.shape, lambda s: (0, 0), pipeline_mode=pl.Buffered(1))],
        out_specs=[full] * 3 + [ANY] * 2,
        out_shape=[jax.ShapeDtypeStruct(tokens.shape, bf16)] * 3
        + [
            jax.ShapeDtypeStruct((seqs, 2, M, features), bf16),
            jax.ShapeDtypeStruct((seqs, 2, RIM, features), bf16),
        ],
        scratch_shapes=[
            pltpu.VMEM((seqs, 2, marks, features), bf16), pltpu.VMEM((seqs, 2, RIM, features), bf16),
            dma((seqs, ranks)), dma((seqs, ranks)), dma((seqs,)), dma((seqs, 2)), dma((seqs, 2)), dma((seqs,)),
        ],
        compiler_params=params(62 * MB, collective_id=0, has_side_effects=True),
        name="project",
    )(tokens, w_qkv)


def fill_pad(pad, x_ref, rim_ref):
    rows = x_ref.shape[1]
    me, count = seq_place()
    pad[0:RIM, :] = jnp.where(me > 0, rim_ref[0, 0].astype(f32), 0.0)
    pad[RIM : RIM + rows, :] = x_ref[0].astype(f32)
    pad[RIM + rows : RIM + rows + RIM, :] = jnp.where(me < count - 1, rim_ref[0, 1].astype(f32), 0.0)


def conv_tile(v_ref, rim_ref, f_ref, o_ref, pad):
    rows = v_ref.shape[1]
    fill_pad(pad, v_ref, rim_ref)
    for c in range(0, rows, 64):
        acc = jnp.zeros((64, 128), f32)
        for j in range(KW):
            acc = acc + f_ref[j : j + 1, :] * pad[c + j : c + j + 64, :]
        o_ref[0, c : c + 64, :] = acc.astype(bf16)


def conv_specs(rows, first_step, first_group, groups):
    at = lambda i: jnp.maximum(i - first_step, 0)
    seq = lambda i: at(i) // groups
    group = lambda i: at(i) % groups
    return (
        pl.BlockSpec((1, rows, 128), lambda i: (seq(i), 0, first_group + group(i))),
        pl.BlockSpec((1, 2, RIM, 128), lambda i: (seq(i), 0, 0, first_group + group(i))),
        pl.BlockSpec((KW, 128), lambda i: (0, first_group + group(i))),
        pl.BlockSpec((1, rows, 128), lambda i: (seq(i), 0, group(i))),
    )


def conv_back_tile(seq, seqs, g_ref, rim_ref, v_ref, f_ref, o_ref, gf_ref, pad, facc):
    rows = v_ref.shape[1]
    fill_pad(pad, g_ref, rim_ref)

    @pl.when(seq == 0)
    def _():
        facc[...] = jnp.zeros_like(facc)

    for c in range(0, rows, 64):
        acc = jnp.zeros((64, 128), f32)
        vals = v_ref[0, c : c + 64, :].astype(f32)
        for j in range(KW):
            moved = pad[c + 2 * RIM - j : c + 2 * RIM - j + 64, :]
            acc = acc + f_ref[j : j + 1, :] * moved
            facc[8 * j : 8 * j + 8, :] += (vals * moved).reshape(8, 8, 128).sum(0)
        o_ref[0, c : c + 64, :] = acc.astype(bf16)

    @pl.when(seq == seqs - 1)
    def _():
        gf_ref[...] = facc[...].reshape(KW, 8, 128).sum(1)


def conv_back_kernel(g_ref, rim_ref, v_ref, f_ref, o_ref, gf_ref, pad, facc):
    conv_back_tile(
        pl.program_id(1), pl.num_programs(1), g_ref, rim_ref, v_ref, f_ref, o_ref, gf_ref, pad, facc
    )


def conv_back_specs(rows, seqs, first_step, first_group):
    at = lambda i: jnp.maximum(i - first_step, 0)
    seq = lambda i: at(i) % seqs
    group = lambda i: at(i) // seqs
    return (
        pl.BlockSpec((1, rows, 128), lambda i: (seq(i), 0, first_group + group(i))),
        pl.BlockSpec((1, 2, RIM, 128), lambda i: (seq(i), 0, 0, first_group + group(i))),
        pl.BlockSpec((KW, 128), lambda i: (0, first_group + group(i))),
        pl.BlockSpec((1, rows, 128), lambda i: (seq(i), 0, group(i))),
        pl.BlockSpec((KW, 128), lambda i: (0, group(i))),
    )


def conv_back(g, rim, v, taps):
    seqs, rows, features = v.shape
    sp = lambda n: pl.BlockSpec((1, n, 128), lambda g, s: (s, 0, g))
    fs = pl.BlockSpec((KW, 128), lambda g, s: (0, g))
    return pl.pallas_call(
        conv_back_kernel,
        grid=(features // 128, seqs),
        in_specs=[sp(rows), pl.BlockSpec((1, 2, RIM, 128), lambda g, s: (s, 0, 0, g)), sp(rows), fs],
        out_specs=[sp(rows), fs],
        out_shape=[jax.ShapeDtypeStruct(v.shape, bf16), jax.ShapeDtypeStruct((KW, features), f32)],
        scratch_shapes=[pltpu.VMEM((rows + 2 * RIM, 128), f32), pltpu.VMEM((KW * 8, 128), f32)],
        name="conv_back",
    )(g, rim, v, taps)


def score_step(step, q_ref, k_ref, v_ref, land_ref, w_ref, p_ref, num_ref, stat_ref):
    rows, features = q_ref.shape[1:]
    pairs = features // 128
    masks = group_masks((M, 4 * E), 4, bf16)
    masks_wide = group_masks((M, 4 * E), 4, f32)
    ones = jnp.where(
        lane_group((4 * E, 4 * E)) == lax.broadcasted_iota(jnp.int32, (4 * E, 4 * E), 0) // E, 1.0, 0.0
    ).astype(bf16)
    chunk = min(128, rows)
    upper = lax.broadcasted_iota(jnp.int32, (chunk, 2 * E), 1) >= E
    for g in range(features // 256):
        sl = slice(256 * g, 256 * g + 256)
        s3 = dot_nt(k_ref[0, :, sl], block_diag(land_ref[0, 0, :, sl], masks))
        peak = jnp.max(s3, axis=0, keepdims=True)
        e3 = jnp.exp(s3 - peak)
        total = jnp.sum(e3, axis=0, keepdims=True)
        low = e3.astype(bf16)
        w_ref[0, :, sl] = low
        num = diag_blocks(dot_tn(low, v_ref[0, :, sl]), masks_wide).astype(bf16)
        for i in range(2):
            lanes = slice(128 * i, 128 * i + 128)
            num_ref[step * pairs + 2 * g + i] = num[:, lanes]
            stat_ref[step * pairs + 2 * g + i] = jnp.concatenate(
                [peak[:, lanes], total[:, lanes], jnp.zeros((6, 128), f32)], axis=0
            )
        kd = block_diag(land_ref[0, 1, :, sl], masks)
        for r in range(0, rows, chunk):
            s1 = dot_nt(q_ref[0, r : r + chunk, sl], kd)
            parts = []
            for i in range(2):
                x = s1[:, 128 * i : 128 * i + 128]
                top_a = jnp.max(jnp.where(upper, -jnp.inf, x), axis=1, keepdims=True)
                top_b = jnp.max(jnp.where(upper, x, -jnp.inf), axis=1, keepdims=True)
                parts.append(jnp.exp(x - jnp.where(upper, top_b, top_a)))
            e1 = jnp.concatenate(parts, axis=1)
            p_ref[0, r : r + chunk, sl] = (e1 / dot(e1.astype(bf16), ones)).astype(bf16)


def scores_kernel(
    seqs, q_ref, k_ref, v_ref, land_ref, cv_ref, rim_ref, f_ref, w_ref, p_ref, co_ref, num_out, stat_out,
    num, stat, pad, num_sems, stat_sems,
):
    step = pl.program_id(0)
    steps = pl.num_programs(0)
    own = num_out.shape[1]
    pairs = q_ref.shape[2] // 128

    @pl.when(step == 0)
    def _():
        greet()
        if num.shape[0] > seqs * pairs:
            num[seqs * pairs :] = jnp.zeros_like(num[seqs * pairs :])
            stat[seqs * pairs :] = jnp.zeros_like(stat[seqs * pairs :])

    @pl.when(step < seqs)
    def _():
        score_step(step, q_ref, k_ref, v_ref, land_ref, w_ref, p_ref, num, stat)

    @pl.when(step == seqs - 1)
    def _():
        begin(swap_copies(num, num_out, own, num_sems))
        begin(swap_copies(stat, stat_out, own, stat_sems))

    @pl.when(step >= seqs)
    def _():
        conv_tile(cv_ref, rim_ref, f_ref, co_ref, pad)

    @pl.when(step == steps - 1)
    def _():
        finish(swap_copies(num, num_out, own, num_sems))
        finish(swap_copies(stat, stat_out, own, stat_sems))


def scores(q, k, v, land, rim, taps, own, groups):
    seqs, rows, features = q.shape
    ranks = lax.axis_size("seq")
    here = lambda i: jnp.minimum(i, seqs - 1)
    full = pl.BlockSpec((1, rows, features), lambda i: (here(i), 0, 0))
    cv, rims, ft, co = conv_specs(rows, seqs, 0, groups)
    return pl.pallas_call(
        functools.partial(scores_kernel, seqs),
        grid=(seqs + seqs * groups,),
        in_specs=[full] * 3
        + [pl.BlockSpec((1, 2, M, features), lambda i: (here(i), 0, 0, 0)), cv, rims, ft],
        out_specs=[full] * 2 + [co, ANY, ANY],
        out_shape=[jax.ShapeDtypeStruct(q.shape, bf16)] * 2
        + [
            jax.ShapeDtypeStruct((seqs, rows, 128 * groups), bf16),
            jax.ShapeDtypeStruct((ranks, own, M, 128), bf16),
            jax.ShapeDtypeStruct((ranks, own, 8, 128), f32),
        ],
        scratch_shapes=[
            pltpu.VMEM((ranks * own, M, 128), bf16), pltpu.VMEM((ranks * own, 8, 128), f32),
            pltpu.VMEM((rows + 2 * RIM, 128), f32), rank_sems(), rank_sems(),
        ],
        compiler_params=params(62 * MB, collective_id=1, has_side_effects=True),
        name="scores",
    )(q, k, v, land, v, rim, taps)


def split(x):
    hi = x.astype(bf16)
    return hi, (x - hi.astype(f32)).astype(bf16)


def stack_parts(xs, axis):
    return jnp.concatenate([part for x in xs for part in split(x)], axis=axis)


def pair_sums(out, count):
    top = lambda i, j: out[128 * i + 64 * j : 128 * i + 64 * j + 64]
    return [
        top(i, 0)[:, :128] + (top(i, 0)[:, 128:] + top(i, 1)[:, :128]) for i in range(count)
    ]


def pair_nn(lefts, right, masks):
    hi, lo = split(right)
    packed = jnp.concatenate([block_diag(hi, masks), block_diag(lo, masks)], axis=1)
    return pair_sums(dot(stack_parts(lefts, 0), packed), len(lefts))


def pair_nt(lefts, right, masks):
    hi, lo = split(right)
    packed = jnp.concatenate([block_diag(hi, masks), block_diag(lo, masks)], axis=0)
    return pair_sums(dot_nt(stack_parts(lefts, 0), packed), len(lefts))


def pair_tn(left, rights, masks_wide):
    out = dot_tn(stack_parts([left], 1), stack_parts(rights, 1))
    results = []
    for i in range(len(rights)):
        full = out[:128, 256 * i : 256 * i + 128] + (
            out[:128, 256 * i + 128 : 256 * i + 256] + out[128:, 256 * i : 256 * i + 128]
        )
        results.append(diag_blocks(full, masks_wide))
    return results


def half_reduce(x, upper, op, fill):
    a = op(jnp.where(upper, fill, x), axis=1, keepdims=True)
    b = op(jnp.where(upper, x, fill), axis=1, keepdims=True)
    return jnp.where(upper, b, a)


def to_column(row, same, upper):
    return half_reduce(jnp.where(same, row, 0.0), upper, jnp.sum, 0.0)


def to_row(col, same):
    return jnp.sum(jnp.where(same, col, 0.0), axis=0, keepdims=True)


def pair_consts():
    lane = lax.broadcasted_iota(jnp.int32, (M, 128), 1)
    row = lax.broadcasted_iota(jnp.int32, (M, 128), 0)
    return lane >= E, row == lane % E, group_masks((M, 128), 2, bf16), group_masks((M, 128), 2, f32)


def own_pair(land_ref, i, own):
    me, _ = seq_place()
    per = land_ref.shape[2] // 128
    p = jnp.minimum(me * own + i, land_ref.shape[0] * per - 1)
    return land_ref[p // per, :, pl.ds(pl.multiple_of((p % per) * 128, 128), 128)]


def inverse_step(
    num_ref, stat_ref, land_ref, mixed_ref, sum_ref, mid_ref, z_ref, p_ref, a_ref, w_ref,
    scale_ref, tot_ref, alpha_ref,
):
    ranks, own = num_ref.shape[:2]
    upper, same, masks, masks_wide = pair_consts()
    for i in range(own):
        peak = stat_ref[0, i, 0:1, :]
        for r in range(1, ranks):
            peak = jnp.maximum(peak, stat_ref[r, i, 0:1, :])
        total = jnp.zeros((1, 128), f32)
        numer = jnp.zeros((M, 128), f32)
        for r in range(ranks):
            alpha = jnp.exp(stat_ref[r, i, 0:1, :] - peak)
            total = total + alpha * stat_ref[r, i, 1:2, :]
            column = to_column(alpha, same, upper)
            alpha_ref[r, i] = column
            numer = numer + column * num_ref[r, i].astype(f32)
        total = to_column(total, same, upper)
        tot_ref[i] = total
        sum_ref[i] = numer / total
        ql, kl = own_pair(land_ref.at[:, 0], i, own), own_pair(land_ref.at[:, 1], i, own)
        s2 = dot_nt(ql, block_diag(kl, masks))
        e2 = jnp.exp(s2 - half_reduce(s2, upper, jnp.max, -jnp.inf))
        middle = e2 / half_reduce(e2, upper, jnp.sum, 0.0)
        mid_ref[i] = middle
        st = dot_nt(kl, block_diag(ql, masks))
        et = jnp.exp(st - jnp.max(st, axis=0, keepdims=True))
        flipped = et / jnp.sum(et, axis=0, keepdims=True)
        column = jnp.sum(middle, axis=0, keepdims=True)
        scale = 1.0 / half_reduce(column, upper[0:1], jnp.max, -jnp.inf)
        scale_ref[i] = jnp.broadcast_to(scale, (8, 128))
        z_ref[0, i] = flipped * scale

    def step(it, carry):
        zs = [z_ref[it, i] for i in range(own)]
        ps = [pair_nn([mid_ref[i]], zs[i], masks)[0] for i in range(own)]
        second = [pair_nn([ps[i], zs[i]], ps[i], masks) for i in range(own)]
        for i in range(own):
            p2, a = second[i]
            w = 7.0 * ps[i] - p2
            p_ref[it, i] = ps[i]
            a_ref[it, i] = a
            w_ref[it, i] = w
            z_ref[it + 1, i] = 0.25 * (13.0 * zs[i] - 15.0 * a + pair_nn([a], w, masks)[0])
        return carry

    lax.fori_loop(0, NEWTON, step, 0)
    for i in range(own):
        mixed_ref[i] = pair_nn([z_ref[NEWTON, i]], sum_ref[i], masks)[0].astype(bf16)


def inverse_kernel(
    num_ref, stat_ref, land_ref, cv_ref, rim_ref, f_ref, mixed_out, co_ref, sum_ref, mid_ref, z_ref, p_ref,
    a_ref, w_ref, scale_ref, tot_ref, alpha_ref, mixed, pad, sems,
):
    step = pl.program_id(0)
    own = num_ref.shape[1]

    @pl.when(step == 0)
    def _():
        greet()
        inverse_step(
            num_ref, stat_ref, land_ref, mixed, sum_ref, mid_ref, z_ref, p_ref, a_ref, w_ref, scale_ref,
            tot_ref, alpha_ref,
        )
        begin(spread_copies(mixed, mixed_out, own, sems))

    @pl.when(step > 0)
    def _():
        conv_tile(cv_ref, rim_ref, f_ref, co_ref, pad)

    @pl.when(step == pl.num_programs(0) - 1)
    def _():
        finish(spread_copies(mixed, mixed_out, own, sems))


def inverse(num, stat, land, v, rim, taps, first_group):
    ranks, own = num.shape[:2]
    seqs, rows, features = v.shape
    groups = features // 128 - first_group
    mat = jax.ShapeDtypeStruct((own, M, 128), f32)
    steps = lambda n: jax.ShapeDtypeStruct((n, own, M, 128), f32)
    whole = lambda a: pl.BlockSpec(a.shape, lambda i: (0,) * len(a.shape), pipeline_mode=pl.Buffered(1))
    saved = [
        mat, mat, steps(NEWTON + 1), steps(NEWTON), steps(NEWTON), steps(NEWTON),
        jax.ShapeDtypeStruct((own, 8, 128), f32), mat, steps(ranks),
    ]
    cv, rims, ft, co = conv_specs(rows, 1, first_group, groups)
    return pl.pallas_call(
        inverse_kernel,
        grid=(1 + seqs * groups,),
        in_specs=[whole(num), whole(stat), whole(land), cv, rims, ft],
        out_specs=[ANY, co] + [whole(a) for a in saved],
        out_shape=[
            jax.ShapeDtypeStruct((ranks * own, M, 128), bf16),
            jax.ShapeDtypeStruct((seqs, rows, 128 * groups), bf16),
        ]
        + saved,
        scratch_shapes=[
            pltpu.VMEM((own, M, 128), bf16), pltpu.VMEM((rows + 2 * RIM, 128), f32), rank_sems(),
        ],
        compiler_params=params(62 * MB, collective_id=2, has_side_effects=True),
        name="inverse",
    )(num, stat, land, v, rim, taps)


def inverse_back_step(
    land_ref, marks_ref, sum_ref, mid_ref, z_ref, p_ref, a_ref, w_ref, scale_ref, tot_ref,
    alpha_ref, gn_ref, gt_ref, mq_ref, mk_ref, g_ref, dk_ref,
):
    ranks, own = land_ref.shape[:2]
    upper, same, masks, masks_wide = pair_consts()
    for i in range(own):
        land = land_ref[0, i].astype(f32)
        for r in range(1, ranks):
            land = land + land_ref[r, i].astype(f32)
        summary, total = sum_ref[i], tot_ref[i]
        gs = pair_tn(z_ref[NEWTON, i], [land], masks_wide)[0].astype(bf16).astype(f32)
        gn = (gs / total).astype(bf16).astype(f32)
        gt = -half_reduce(gs * summary, upper, jnp.sum, 0.0) / total
        for r in range(ranks):
            gn_ref[r, i] = (alpha_ref[r, i] * gn).astype(bf16)
            gt_ref[r, i] = jnp.broadcast_to(to_row(alpha_ref[r, i] * gt, same), (8, 128))
        g_ref[i] = pair_nt([land], summary, masks)[0]
        dk_ref[i] = jnp.zeros((M, 128), f32)

    def step(back, carry):
        it = NEWTON - 1 - back
        gs = [g_ref[i] for i in range(own)]
        das, dws = [], []
        for i in range(own):
            das.append(0.25 * (pair_nt([gs[i]], w_ref[it, i], masks)[0] - 15.0 * gs[i]))
            dws.append(0.25 * pair_tn(a_ref[it, i], [gs[i]], masks_wide)[0])
        dps, parts = [], []
        for i in range(own):
            right = pair_nt([dws[i], das[i]], p_ref[it, i], masks)
            left = pair_tn(p_ref[it, i], [dws[i]], masks_wide)[0]
            dps.append(7.0 * dws[i] - right[0] - left + pair_tn(z_ref[it, i], [das[i]], masks_wide)[0])
            parts.append(3.25 * gs[i] + right[1])
        for i in range(own):
            g_ref[i] = parts[i] + pair_tn(mid_ref[i], [dps[i]], masks_wide)[0]
            dk_ref[i] += pair_nt([dps[i]], z_ref[it, i], masks)[0]
        return carry

    lax.fori_loop(0, NEWTON, step, 0)
    eye = jnp.where(same, 1.0, 0.0).astype(bf16)
    for i in range(own):
        g, middle, scale = g_ref[i], mid_ref[i], scale_ref[i, 0:1, :]
        turned = dot_tn(stack_parts([g], 1), eye)
        turned = diag_blocks(turned[:128] + turned[128:], masks_wide)
        column = jnp.sum(middle, axis=0, keepdims=True)
        top = half_reduce(column, upper[0:1], jnp.max, -jnp.inf)
        hit = jnp.where(column == top, 1.0, 0.0)
        share = hit / half_reduce(hit, upper[0:1], jnp.sum, 0.0)
        d_scale = half_reduce(jnp.sum(turned * middle, axis=0, keepdims=True), upper[0:1], jnp.sum, 0.0)
        dk = dk_ref[i] + turned * scale - share * (d_scale * scale * scale)
        ds = middle * (dk - half_reduce(middle * dk, upper, jnp.sum, 0.0))
        hi, lo = split(ds)
        both = dot(jnp.concatenate([hi, lo], axis=0), block_diag(own_pair(marks_ref.at[:, 1], i, own), masks))
        mq_ref[i] = both[:M] + both[M:]
        turned = dot_tn(jnp.concatenate([hi, lo], axis=1), own_pair(marks_ref.at[:, 0], i, own))
        mk_ref[i] = diag_blocks(turned[:128] + turned[128:], masks_wide)


def inverse_back(land, marks, saved):
    ranks, own = land.shape[:2]
    mat = jax.ShapeDtypeStruct((own, M, 128), f32)
    return pl.pallas_call(
        inverse_back_step,
        out_shape=[
            jax.ShapeDtypeStruct((ranks, own, M, 128), bf16),
            jax.ShapeDtypeStruct((ranks, own, 8, 128), f32), mat, mat,
        ],
        scratch_shapes=[pltpu.VMEM((own, M, 128), f32)] * 2,
        compiler_params=params(62 * MB),
        name="inverse_back",
    )(land, marks, *saved)


def mean_of(x):
    return jnp.mean(x, axis=-1, keepdims=True)


def gelu_and_slope(u):
    x = jnp.abs(u) * root_half
    t = 1.0 / (1.0 + ERFC_P * x)
    poly = jnp.full_like(t, ERFC_C[-1])
    for c in ERFC_C[-2::-1]:
        poly = poly * t + c
    bell = jnp.exp(-0.5 * u * u)
    half = (0.5 * t) * poly * bell
    cdf = jnp.where(u < 0.0, half, 1.0 - half)
    return u * cdf, cdf + u * bell * inv_root_two_pi


def row_block(
    step, tok_ref, p_ref, conv_a_ref, conv_b_ref, mix_ref, top_ref, w_out_ref, w_up_ref, w_down_ref, ga_ref,
    gf_ref, out_ref, proj_ref, gm_ref, gains_ref, act, gul, slope, hid_t, gdl_t, mix_t, gpr, resid, whole,
):
    size, features = tok_ref.shape
    ff = act.shape[1]
    wide = features
    start = pl.multiple_of(step * size, size)
    rows = pl.ds(start, size)
    near = rows if whole else pl.ds(0, size)
    masks = group_masks((M, 4 * E), 4, bf16)
    for g in range(features // 256):
        sl = slice(256 * g, 256 * g + 256)
        att = dot(p_ref[:, sl], block_diag(quad(mix_ref, g), masks))
        resid[:, sl] = att
    half = conv_a_ref.shape[1]
    resid[:, :half] += conv_a_ref[...].astype(f32)
    resid[:, half:] += conv_b_ref[...].astype(f32)
    mixed = resid[...].astype(bf16)
    mix_t[:, near] = mixed.T
    residual = tok_ref[...].astype(f32) + dot(mixed, w_out_ref[...])
    centre = residual - mean_of(residual)
    s_att = lax.rsqrt(mean_of(centre * centre) + epsilon)
    normed = centre * s_att
    gain_att = ga_ref[...]
    hidden = normed * gain_att
    hid_low = hidden.astype(bf16)
    hid_t[:, rows] = hid_low.T
    down = jnp.zeros((size, features), f32)
    for j in range(0, ff, wide):
        up = dot(hid_low, w_up_ref[:, j : j + wide])
        a, sl = gelu_and_slope(up)
        low = a.astype(bf16)
        act[near, j : j + wide] = low
        slope[:, j : j + wide] = sl.astype(bf16)
        down = down + dot(low, w_down_ref[j : j + wide, :])
    residual_two = hidden + down
    centre_two = residual_two - mean_of(residual_two)
    s_ffn = lax.rsqrt(mean_of(centre_two * centre_two) + epsilon)
    normed_two = centre_two * s_ffn
    gain_ffn = gf_ref[...]
    out_ref[...] = (normed_two * gain_ffn).astype(bf16)
    top = top_ref[...].astype(f32)
    gains_ref[8:16, :] += (top * normed_two).reshape(size // 8, 8, features).sum(0)
    g = top * gain_ffn
    grad_two = s_ffn * (g - mean_of(g) - normed_two * mean_of(g * normed_two))
    gdl = grad_two.astype(bf16)
    gdl_t[:, near] = gdl.T
    back = jnp.zeros((size, features), f32)
    for j in range(0, ff, wide):
        gu = dot_nt(gdl, w_down_ref[j : j + wide, :]) * slope[:, j : j + wide].astype(f32)
        low = gu.astype(bf16)
        gul[rows, j : j + wide] = low
        back = back + dot_nt(low, w_up_ref[:, j : j + wide])
    grad_hidden = grad_two + back
    gains_ref[0:8, :] += (grad_hidden * normed).reshape(size // 8, 8, features).sum(0)
    g = grad_hidden * gain_att
    proj = (s_att * (g - mean_of(g) - normed * mean_of(g * normed))).astype(bf16)
    proj_ref[...] = proj
    if whole:
        gpr[rows, :] = proj
    gm_ref[...] = dot_nt(proj, w_out_ref[...]).astype(bf16)


def row_kernel(
    tok_ref, p_ref, conv_a_ref, conv_b_ref, mix_ref, top_ref, w_out_ref, w_up_ref, w_down_ref, ga_ref, gf_ref,
    out_ref, proj_ref, gm_ref, wg_ref, gains_ref,
    act, gul, slope, hid_t, gdl_t, mix_t, gpr, resid,
):
    step = pl.program_id(0)
    size, features = tok_ref.shape
    blocks = act.shape[0] // size
    ff = act.shape[1]
    wide = features

    @pl.when(step == 0)
    def _():
        gains_ref[...] = jnp.zeros_like(gains_ref)

    @pl.when(step < blocks)
    def _():
        row_block(
            step, tok_ref, p_ref, conv_a_ref, conv_b_ref, mix_ref, top_ref, w_out_ref, w_up_ref, w_down_ref,
            ga_ref, gf_ref, out_ref, proj_ref, gm_ref, gains_ref, act, gul, slope, hid_t, gdl_t, mix_t, gpr,
            resid, True,
        )

    chunks = ff // wide
    for first, left, right in ((0, hid_t, gul), (chunks, gdl_t, act), (2 * chunks, mix_t, gpr)):
        count = chunks if first < 2 * chunks else 1

        @pl.when((step >= blocks + first) & (step < blocks + first + count))
        def _(first=first, left=left, right=right):
            base = (step - blocks - first) * wide
            for c in range(0, wide, 256):
                cols = pl.ds(pl.multiple_of(base + c, 256), 256)
                wg_ref[0, :, c : c + 256] = dot(left[...], right[:, cols]).astype(bf16)


def row_pass(tokens, probs, conv_a, conv_b, mixed, grad_out, w_out, w_up, w_down, gain_att, gain_ffn):
    seqs, rows, features = tokens.shape
    ff = w_up.shape[1]
    size = min(256, rows)
    total = seqs * rows
    blocks = total // size
    grads = 2 * (ff // features) + 1
    here = lambda i: jnp.minimum(i, blocks - 1)
    block = pl.BlockSpec((size, features), lambda i: (here(i), 0))
    whole = lambda a: pl.BlockSpec(a.shape, lambda i: (0,) * a.ndim, pipeline_mode=pl.Buffered(1))
    flat = lambda a: a.reshape(total, a.shape[2])
    part = lambda a: pl.BlockSpec((size, a.shape[2]), lambda i: (here(i), 0))
    gains = [gain_att.reshape(1, features), gain_ffn.reshape(1, features)]
    row_out = jax.ShapeDtypeStruct((total, features), bf16)
    tall = pltpu.VMEM((features, total), bf16)
    return pl.pallas_call(
        row_kernel,
        grid=(blocks + grads,),
        in_specs=[
            block, block, part(conv_a), part(conv_b),
            pl.BlockSpec((features // 128, M, 128), lambda i: (here(i) * size // rows, 0, 0)),
            block, whole(w_out), whole(w_up), whole(w_down), whole(gains[0]), whole(gains[1]),
        ],
        out_specs=[block] * 3
        + [
            pl.BlockSpec((1, features, features), lambda i: (jnp.maximum(i - blocks, 0), 0, 0)),
            pl.BlockSpec((16, features), lambda i: (0, 0)),
        ],
        out_shape=[row_out] * 3
        + [
            jax.ShapeDtypeStruct((grads, features, features), bf16),
            jax.ShapeDtypeStruct((16, features), f32),
        ],
        scratch_shapes=[
            pltpu.VMEM((total, ff), bf16), pltpu.VMEM((total, ff), bf16), pltpu.VMEM((size, ff), bf16),
            tall, tall, tall, pltpu.VMEM((total, features), bf16), pltpu.VMEM((size, features), f32),
        ],
        compiler_params=params(62 * MB),
        name="row_pass",
    )(flat(tokens), flat(probs), flat(conv_a), flat(conv_b), mixed, flat(grad_out), w_out, w_up, w_down, *gains)


def row_share_kernel(
    tok_ref, p_ref, conv_a_ref, conv_b_ref, mix_ref, top_ref, w_out_ref, w_up_ref, w_down_ref, ga_ref, gf_ref,
    out_ref, proj_ref, gm_ref, gains_ref, act_ref, gdl_t_ref, mix_t_ref, g_out, rim_out,
    gul, slope, hid_t, resid, rim, parts, got, sums, send, recv, out_sem, rim_send, rim_recv,
):
    step = pl.program_id(0)
    size, features = tok_ref.shape
    blocks = gul.shape[0] // size
    seqs = rim.shape[0]
    per = blocks // seqs
    chunks = gul.shape[1] // features
    me, count = seq_place()
    core, _, _, sibling, _, _ = cube()
    half = features // 2

    @pl.when(step == 0)
    def _():
        gains_ref[...] = jnp.zeros_like(gains_ref)
        greet([sibling])

    def rim_copy(s, side):
        there = lax.rem(me + (1 if side == 0 else count - 1), count)
        return remote(
            rim.at[s, side], rim_out.at[s, side], rim_send.at[s, side], rim_recv.at[s, side], {"seq": there}
        )

    @pl.when(step < blocks)
    def _():
        row_block(
            step, tok_ref, p_ref, conv_a_ref, conv_b_ref, mix_ref, top_ref, w_out_ref, w_up_ref, w_down_ref,
            ga_ref, gf_ref, out_ref, proj_ref, gm_ref, gains_ref, act_ref, gul, slope, hid_t, gdl_t_ref,
            mix_t_ref, None, resid, False,
        )
        s = step // per

        @pl.when(step % per == 0)
        def _():
            rim[s, 1] = gm_ref[:RIM, :]
            rim_copy(s, 1).start()

        @pl.when(step % per == per - 1)
        def _():
            rim[s, 0] = gm_ref[size - RIM :, :]
            rim_copy(s, 0).start()

    j = step - blocks
    slot = lax.rem(jnp.maximum(j, 0), 2)

    def share(at):
        return remote(parts.at[at % 2, 1 - core], got.at[at], send.at[at], recv.at[at], sibling)

    def out_copy(at):
        return pltpu.make_async_copy(sums.at[at % 2], g_out.at[at], out_sem.at[at % 2])

    @pl.when((j >= 2) & (j < chunks))
    def _():
        share(j - 2).wait_send()

    @pl.when((j >= 0) & (j < chunks))
    def _():
        for c in range(0, features, 256):
            cols = pl.ds(pl.multiple_of(j * features + c, 256), 256)
            low = dot(hid_t[...], gul[:, cols]).astype(bf16)
            for l in range(0, 256, 128):
                side, lane = (c + l) // half, (c + l) % half
                for d in range(8):
                    parts[slot, d % 2, d // 2, 96 * side : 96 * side + 96, lane : lane + 128] = low[
                        96 * d : 96 * d + 96, l : l + 128
                    ]
        share(j).start()

    done = j - 1

    @pl.when(done >= 2)
    def _():
        out_copy(done - 2).wait()

    @pl.when(done >= 0)
    def _():
        share(done).wait_recv()
        sums[done % 2] = add_low(parts[done % 2, core], got[done])
        out_copy(done).start()

    @pl.when(done == chunks - 1)
    def _():
        share(done - 1).wait_send()
        share(done).wait_send()
        out_copy(done - 1).wait()
        out_copy(done).wait()

        def rims(s, carry):
            for side in range(2):
                rim_copy(s, side).wait()
            return carry

        lax.fori_loop(0, seqs, rims, 0)


def row_share(tokens, probs, conv_a, conv_b, mixed, grad_out, w_out, w_up, w_down, gain_att, gain_ffn):
    seqs, rows, features = tokens.shape
    ff = w_up.shape[1]
    size = min(256, rows)
    total = seqs * rows
    blocks = total // size
    chunks = ff // features
    here = lambda i: jnp.minimum(i, blocks - 1)
    block = pl.BlockSpec((size, features), lambda i: (here(i), 0))
    turned = pl.BlockSpec((features, size), lambda i: (0, here(i)))
    whole = lambda a: pl.BlockSpec(a.shape, lambda i: (0,) * a.ndim, pipeline_mode=pl.Buffered(1))
    flat = lambda a: a.reshape(total, a.shape[2])
    part = lambda a: pl.BlockSpec((size, a.shape[2]), lambda i: (here(i), 0))
    gains = [gain_att.reshape(1, features), gain_ffn.reshape(1, features)]
    row_out = jax.ShapeDtypeStruct((total, features), bf16)
    turned_out = jax.ShapeDtypeStruct((features, total), bf16)
    dma = pltpu.SemaphoreType.DMA
    return pl.pallas_call(
        row_share_kernel,
        grid=(blocks + chunks + 1,),
        in_specs=[
            block, block, part(conv_a), part(conv_b),
            pl.BlockSpec((features // 128, M, 128), lambda i: (here(i) * size // rows, 0, 0)),
            block, whole(w_out), whole(w_up), whole(w_down), whole(gains[0]), whole(gains[1]),
        ],
        out_specs=[block] * 3
        + [
            pl.BlockSpec((16, features), lambda i: (0, 0)), pl.BlockSpec((size, ff), lambda i: (here(i), 0)),
            turned, turned, ANY, ANY,
        ],
        out_shape=[row_out] * 3
        + [
            jax.ShapeDtypeStruct((16, features), f32), jax.ShapeDtypeStruct((total, ff), bf16),
            turned_out, turned_out, jax.ShapeDtypeStruct((chunks, 4, 192, 384), bf16),
            jax.ShapeDtypeStruct((seqs, 2, RIM, features), bf16),
        ],
        scratch_shapes=[
            pltpu.VMEM((total, ff), bf16), pltpu.VMEM((size, ff), bf16), pltpu.VMEM((features, total), bf16),
            pltpu.VMEM((size, features), f32), pltpu.VMEM((seqs, 2, RIM, features), bf16),
            pltpu.VMEM((2, 2, 4, 192, 384), bf16), pltpu.VMEM((chunks, 4, 192, 384), bf16),
            pltpu.VMEM((2, 4, 192, 384), bf16),
            dma((chunks,)), dma((chunks,)), dma((2,)), dma((seqs, 2)), dma((seqs, 2)),
        ],
        compiler_params=params(62 * MB, collective_id=3, has_side_effects=True),
        name="row_share",
    )(flat(tokens), flat(probs), flat(conv_a), flat(conv_b), mixed, flat(grad_out), w_out, w_up, w_down, *gains)


def first_back_step(gm_ref, p_ref, q_ref, mix_ref, kl_of, put_land, gq_ref, put_klp):
    features = gm_ref.shape[2]
    masks = group_masks((M, 4 * E), 4, bf16)
    masks_wide = group_masks((M, 4 * E), 4, f32)
    ones = jnp.where(
        lane_group((4 * E, 4 * E)) == lax.broadcasted_iota(jnp.int32, (4 * E, 4 * E), 0) // E, 1.0, 0.0
    ).astype(bf16)
    for g in range(features // 256):
        sl = slice(256 * g, 256 * g + 256)
        gm, p = gm_ref[0, :, sl], p_ref[0, :, sl]
        put_land(g, diag_blocks(dot_tn(p, gm), masks_wide).astype(bf16))
        d = dot_nt(gm, block_diag(quad(mix_ref, g), masks))
        pw = p.astype(f32)
        gs = (pw * (d - dot((pw * d).astype(bf16), ones))).astype(bf16)
        gq_ref[0, :, sl] = dot(gs, block_diag(kl_of(sl), masks)).astype(bf16)
        put_klp(g, diag_blocks(dot_tn(gs, q_ref[0, :, sl]), masks_wide))


def first_back_kernel(gm_ref, p_ref, q_ref, mix_ref, kl_ref, land_ref, gq_ref, klp_ref):
    def put_land(g, x):
        for i in range(2):
            land_ref[2 * g + i] = x[:, 128 * i : 128 * i + 128]

    def put_klp(g, x):
        klp_ref[0, :, 256 * g : 256 * g + 256] = x

    first_back_step(gm_ref, p_ref, q_ref, mix_ref, lambda sl: kl_ref[0, :, sl], put_land, gq_ref, put_klp)


def first_back(gm, probs, q, mixed, k_land):
    seqs, rows, features = q.shape
    pairs = features // 128
    full = pl.BlockSpec((1, rows, features), lambda s: (s, 0, 0))
    land = pl.BlockSpec((1, M, features), lambda s: (s, 0, 0))
    return pl.pallas_call(
        first_back_kernel,
        grid=(seqs,),
        in_specs=[full] * 3 + [pl.BlockSpec((pairs, M, 128), lambda s: (s, 0, 0)), land],
        out_specs=[pl.BlockSpec((pairs, M, 128), lambda s: (s, 0, 0)), full, land],
        out_shape=[
            jax.ShapeDtypeStruct((seqs * pairs, M, 128), bf16),
            jax.ShapeDtypeStruct(q.shape, bf16),
            jax.ShapeDtypeStruct((seqs, M, features), f32),
        ],
        compiler_params=params(62 * MB),
        name="first_back",
    )(gm, probs, q, mixed, k_land)


def third_back_kernel(w_ref, v_ref, k_ref, gc_ref, gn_ref, gt_ref, ql_ref, gv_ref, gk_ref, qlp_ref):
    features = w_ref.shape[2]
    masks = group_masks((M, 4 * E), 4, bf16)
    masks_wide = group_masks((M, 4 * E), 4, f32)
    for g in range(features // 256):
        sl = slice(256 * g, 256 * g + 256)
        w = w_ref[0, :, sl]
        gn = jnp.concatenate([gn_ref[2 * g], gn_ref[2 * g + 1]], axis=1)
        gt = jnp.concatenate([gt_ref[2 * g, 0:1, :], gt_ref[2 * g + 1, 0:1, :]], axis=1)
        gd = block_diag(gn, masks)
        gs = (w.astype(f32) * (dot_nt(v_ref[0, :, sl], gd) + gt)).astype(bf16)
        gv_ref[0, :, sl] = (dot(w, gd) + gc_ref[0, :, sl].astype(f32)).astype(bf16)
        gk_ref[0, :, sl] = dot(gs, block_diag(ql_ref[0, :, sl], masks)).astype(bf16)
        qlp_ref[0, :, sl] = diag_blocks(dot_tn(gs, k_ref[0, :, sl]), masks_wide)


def third_back(w, v, k, grad_conv, gn, gt, q_land):
    seqs, rows, features = v.shape
    pairs = features // 128
    full = pl.BlockSpec((1, rows, features), lambda s: (s, 0, 0))
    land = pl.BlockSpec((1, M, features), lambda s: (s, 0, 0))
    return pl.pallas_call(
        third_back_kernel,
        grid=(seqs,),
        in_specs=[full] * 4
        + [
            pl.BlockSpec((pairs, M, 128), lambda s: (s, 0, 0)),
            pl.BlockSpec((pairs, 8, 128), lambda s: (s, 0, 0)),
            land,
        ],
        out_specs=[full, full, land],
        out_shape=[jax.ShapeDtypeStruct(v.shape, bf16)] * 2
        + [jax.ShapeDtypeStruct((seqs, M, features), f32)],
        compiler_params=params(62 * MB),
        name="third_back",
    )(w, v, k, grad_conv, gn, gt, q_land)


def last_kernel(tok_ref, gq_ref, gk_ref, gv_ref, qo_ref, ko_ref, proj_ref, w_ref, gt_ref, wg_ref, d, tok_t):
    step = pl.program_id(0)
    seqs = tok_t.shape[1] // tok_ref.shape[1]
    rows, features = tok_ref.shape[1:]
    marks = qo_ref.shape[1]
    seg = rows // marks

    @pl.when(step < seqs)
    def _():
        here = pl.ds(pl.multiple_of(step * rows, rows), rows)
        for part, (core, own) in enumerate(((gq_ref, qo_ref), (gk_ref, ko_ref))):
            for m in range(marks):
                at = pl.ds(pl.multiple_of(step * rows + m * seg, seg), seg)
                x = core[0, m * seg : m * seg + seg, :].astype(f32) + own[0, m : m + 1, :] * (1.0 / seg)
                x = x.astype(bf16)
                if part == 0:
                    x = x * jnp.asarray(0.125, bf16)
                d[at, part * features : part * features + features] = x
        d[here, 2 * features :] = gv_ref[0]
        tok_t[:, here] = tok_ref[0].T
        for c in range(0, rows, 128):
            at = pl.ds(pl.multiple_of(step * rows + c, 128), 128)
            gt_ref[0, c : c + 128, :] = (
                proj_ref[0, c : c + 128, :].astype(f32) + dot_nt(d[at, :], w_ref[...])
            ).astype(bf16)

    @pl.when(step >= seqs)
    def _():
        base = (step - seqs) * features
        for c in range(0, features, 256):
            cols = pl.ds(pl.multiple_of(base + c, 256), 256)
            wg_ref[0, :, c : c + 256] = dot(tok_t[...], d[:, cols]).astype(bf16)


def last_pass(tokens, gq, gk, gv, q_own, k_own, proj, w_qkv):
    seqs, rows, features = tokens.shape
    marks = q_own.shape[1]
    here = lambda i: jnp.minimum(i, seqs - 1)
    full = pl.BlockSpec((1, rows, features), lambda i: (here(i), 0, 0))
    land = pl.BlockSpec((1, marks, features), lambda i: (here(i), 0, 0))
    return pl.pallas_call(
        last_kernel,
        grid=(seqs + 3,),
        in_specs=[full] * 4 + [land] * 2
        + [full, pl.BlockSpec(w_qkv.shape, lambda i: (0, 0), pipeline_mode=pl.Buffered(1))],
        out_specs=[full, pl.BlockSpec((1, features, features), lambda i: (jnp.maximum(i - seqs, 0), 0, 0))],
        out_shape=[
            jax.ShapeDtypeStruct(tokens.shape, bf16),
            jax.ShapeDtypeStruct((3, features, features), bf16),
        ],
        scratch_shapes=[
            pltpu.VMEM((seqs * rows, 3 * features), bf16), pltpu.VMEM((features, seqs * rows), bf16),
        ],
        compiler_params=params(62 * MB),
        name="last_pass",
    )(tokens, gq, gk, gv, q_own, k_own, proj, w_qkv)


def add_pairs(dst, own, start, pairs):
    for i in range(own.shape[0]):
        @pl.when(start + i < pairs)
        def _(i=i):
            dst[start + i] += own[i]


def cross_copies(src, got, sems):
    _, x, y, _, along_x, along_y = cube()
    return [
        remote(src.at[0:2, :, 1 - x], got.at[0], sems.at[0, 0], sems.at[1, 0], along_x),
        remote(src.at[2:4, 1 - y], got.at[1], sems.at[0, 1], sems.at[1, 1], along_y),
    ]


def kept_copies(src, kept, sems):
    _, x, y, _, _, _ = cube()
    return [
        pltpu.make_async_copy(src.at[0:2, :, x], kept.at[0], sems.at[0]),
        pltpu.make_async_copy(src.at[2:4, y], kept.at[1], sems.at[1]),
    ]


def turn_copies(kept, got, sems):
    _, x, y, _, along_x, along_y = cube()
    return [
        remote(kept.at[0, :, 1 - y], got.at[0], sems.at[0, 0], sems.at[1, 0], along_y),
        remote(kept.at[1, :, 1 - x], got.at[1], sems.at[0, 1], sems.at[1, 1], along_x),
    ]


def cross_add(kept, got):
    for half in range(2):
        for rank in range(2):
            kept[half, rank] = add_low(kept[half, rank], got[half, rank])


def turn_add(out, kept, got):
    _, x, y, _, _, _ = cube()
    for half, place in ((0, y), (1, x)):
        for rank in range(2):
            out[2 * half + rank] = add_low(kept[half, rank, place], got[half, rank])


def stage_scratch(rows):
    dma = pltpu.SemaphoreType.DMA
    return [
        pltpu.VMEM((2, 2, 2, rows, 384), bf16), pltpu.VMEM((2, 2, 2, rows, 384), bf16),
        pltpu.VMEM((2, 2, rows, 384), bf16), dma((2,)), dma((2, 2)), dma((2, 2)),
    ]


def down_first_kernel(
    act_ref, gdl_t_ref, mix_t_ref, proj_ref, gm_ref, p_ref, q_ref, mix_ref, marks_ref, cg_ref, rim_ref, cv_ref,
    f_ref, up_in,
    gq_ref, klp_ref, co_ref, gf_ref, up_ref, g_out, land_out,
    parts, got, sums, land, pad, facc, kept, crossed, turned, kept_sems, cross_sems, turn_sems,
    send, recv, out_sem, last_sem, land_sems,
):
    step = pl.program_id(0)
    steps = pl.num_programs(0)
    features = q_ref.shape[2]
    pairs = features // 128
    seqs = klp_ref.shape[0] // pairs
    own = land_out.shape[1]
    core, _, _, sibling, along_x, along_y = cube()
    half = features // 2
    chunks = 4
    first = chunks + 1
    conv = first + seqs
    cross = cross_copies(up_in, crossed, cross_sems)
    keep = kept_copies(up_in, kept, kept_sems)
    turn = turn_copies(kept, turned, turn_sems)

    @pl.when(step == 0)
    def _():
        greet([sibling, along_x, along_y])
        for copy in cross + keep:
            copy.start()
        if land.shape[0] > seqs * pairs:
            land[seqs * pairs :] = jnp.zeros_like(land[seqs * pairs :])

    slot = lax.rem(step, 2)

    def share(at):
        return remote(parts.at[at % 2, 1 - core], got.at[at], send.at[at], recv.at[at], sibling)

    def down_copy(at):
        return pltpu.make_async_copy(sums.at[at % 2], g_out.at[:, at, 0:192, :], out_sem.at[at % 2])

    def out_copy(z):
        return pltpu.make_async_copy(
            sums.at[0, :, 48 * z : 48 * z + 48, :], g_out.at[z, :, 192:240, :], last_sem.at[z]
        )

    @pl.when((step >= 2) & (step <= chunks))
    def _():
        share(step - 2).wait_send()

    @pl.when(step < chunks)
    def _():
        for c in range(0, features, 256):
            low = dot(gdl_t_ref[...], act_ref[:, c : c + 256]).astype(bf16)
            for l in range(0, 256, 128):
                side, lane = (c + l) // half, (c + l) % half
                for z in range(4):
                    parts[slot, side, z, :, lane : lane + 128] = low[192 * z : 192 * z + 192, l : l + 128]
        share(step).start()

    @pl.when(step == chunks)
    def _():
        for c in range(2):
            low = dot(mix_t_ref[...], proj_ref[:, half * c : half * c + half]).astype(bf16)
            for zz in range(2):
                z = 2 * c + zz
                for d in range(8):
                    block = low[96 * d : 96 * d + 96, 192 * zz : 192 * zz + 192]
                    parts[slot, d % 2, d // 2, 48 * z : 48 * z + 48, :] = jnp.concatenate(
                        [block[:48], block[48:]], axis=1
                    )
        share(step).start()

    done = step - 1

    @pl.when((done >= 2) & (done <= chunks))
    def _():
        down_copy(done - 2).wait()

    @pl.when((done >= 0) & (done <= chunks))
    def _():
        share(done).wait_recv()
        sums[done % 2] = add_low(parts[done % 2, core], got[done])

    @pl.when((done >= 0) & (done < chunks))
    def _():
        down_copy(done).start()

    @pl.when(done == chunks)
    def _():
        for z in range(4):
            out_copy(z).start()

    @pl.when((step >= first) & (step < conv))
    def _():
        seq = step - first

        def put_land(g, v):
            for i in range(2):
                land[seq * pairs + 2 * g + i] = v[:, 128 * i : 128 * i + 128]

        def put_klp(g, v):
            for i in range(2):
                klp_ref[seq * pairs + 2 * g + i] = v[:, 128 * i : 128 * i + 128]

        first_back_step(
            gm_ref, p_ref, q_ref, mix_ref, lambda sl: marks_ref[0, 1, :, sl], put_land, gq_ref, put_klp
        )

    @pl.when(step == conv - 1)
    def _():
        begin(swap_copies(land, land_out, own, land_sems))

    @pl.when(step == conv)
    def _():
        for copy in cross + keep:
            copy.wait()
        cross_add(kept, crossed)
        for copy in turn:
            copy.start()

    @pl.when(step >= conv)
    def _():
        seq = (step - conv) % seqs
        conv_back_tile(seq, seqs, cg_ref, rim_ref, cv_ref, f_ref, co_ref, gf_ref, pad, facc)

    @pl.when(step == steps - 1)
    def _():
        for copy in turn:
            copy.wait()
        turn_add(up_ref, kept, turned)
        share(chunks - 1).wait_send()
        share(chunks).wait_send()
        down_copy(chunks - 1).wait()
        for z in range(4):
            out_copy(z).wait()
        finish(swap_copies(land, land_out, own, land_sems))


def down_first(act, gdl_t, mix_t, proj, gm, probs, q, mixed, land, rim, v, taps, ups, own, groups):
    seqs, rows, features = q.shape
    total, ff = act.shape
    ranks = lax.axis_size("seq")
    pairs = features // 128
    chunks = ff // features
    first = chunks + 1
    here = lambda i: jnp.clip(i - first, 0, seqs - 1)
    full = pl.BlockSpec((1, rows, features), lambda i: (here(i), 0, 0))
    whole = lambda a: pl.BlockSpec(a.shape, lambda i: (0,) * len(a.shape), pipeline_mode=pl.Buffered(1))
    cv, rims, ft, co, go = conv_back_specs(rows, seqs, first + seqs, 0)
    up_sum = jax.ShapeDtypeStruct((4, 192, 384), bf16)
    dma = pltpu.SemaphoreType.DMA
    return pl.pallas_call(
        down_first_kernel,
        grid=(first + seqs + seqs * groups,),
        in_specs=[
            pl.BlockSpec((total, features), lambda i: (0, jnp.minimum(i, chunks - 1))),
            whole(gdl_t), whole(mix_t), whole(proj), full, full, full,
            pl.BlockSpec((pairs, M, 128), lambda i: (here(i), 0, 0)),
            pl.BlockSpec((1, 2, M, features), lambda i: (here(i), 0, 0, 0)),
            cv, rims, cv, ft, ANY,
        ],
        out_specs=[full, pl.BlockSpec((seqs * pairs, M, 128), lambda i: (0, 0, 0)), co, go, whole(up_sum), ANY, ANY],
        out_shape=[
            jax.ShapeDtypeStruct(q.shape, bf16),
            jax.ShapeDtypeStruct((seqs * pairs, M, 128), f32),
            jax.ShapeDtypeStruct((seqs, rows, 128 * groups), bf16),
            jax.ShapeDtypeStruct((KW, 128 * groups), f32),
            up_sum,
            jax.ShapeDtypeStruct((4, 4, 240, 384), bf16),
            jax.ShapeDtypeStruct((ranks, own, M, 128), bf16),
        ],
        scratch_shapes=[
            pltpu.VMEM((2, 2, 4, 192, 384), bf16), pltpu.VMEM((chunks + 1, 4, 192, 384), bf16),
            pltpu.VMEM((2, 4, 192, 384), bf16), pltpu.VMEM((ranks * own, M, 128), bf16),
            pltpu.VMEM((rows + 2 * RIM, 128), f32), pltpu.VMEM((KW * 8, 128), f32),
        ]
        + stage_scratch(192)
        + [dma((chunks + 1,)), dma((chunks + 1,)), dma((2,)), dma((4,)), rank_sems()],
        compiler_params=params(62 * MB, collective_id=4, has_side_effects=True),
        name="down_first",
    )(act, gdl_t, mix_t, proj, gm, probs, q, mixed, land, gm, rim, v, taps, ups)


def inverse_conv_kernel(
    late, land_ref, marks_ref, sum_ref, mid_ref, z_ref, p_ref, a_ref, w_ref, scale_ref, tot_ref, alpha_ref, klp_ref,
    cg_ref, rim_ref, cv_ref, f_ref, down_in, up_in,
    mq_ref, co_ref, gf_ref, down_ref, gn_out, gt_out, kl_out, up_out,
    gn, gt, gt_low, mk, g_acc, dk_acc, kl, pad, facc, kept, crossed, turned, kept_sems, cross_sems, turn_sems,
    gn_sems, gt_sems, kl_sems, up_sems,
):
    step = pl.program_id(0)
    ranks, own = land_ref.shape[:2]
    me, _ = seq_place()
    marks = kl_out.shape[2]
    seqs = marks_ref.shape[0]
    _, _, _, _, along_x, along_y = cube()
    cross = cross_copies(down_in, crossed, cross_sems)
    keep = kept_copies(down_in, kept, kept_sems)
    turn = turn_copies(kept, turned, turn_sems)

    def mark_copies():
        sends = [
            remote(
                kl.at[:, pl.ds(peer * marks, marks)], kl_out.at[me], kl_sems.at[0, o], kl_sems.at[1, o],
                {"seq": peer},
            )
            for o, peer in seq_peers()
        ]
        return sends, pltpu.make_async_copy(
            kl.at[:, pl.ds(me * marks, marks)], kl_out.at[me], kl_sems.at[0, 0]
        )

    exchanges = [swap_rows(gn, gn_out, gn_sems), swap_rows(gt_low, gt_out, gt_sems), mark_copies()]
    ups = swap_rows(up_in, up_out, up_sems)

    @pl.when(step == 0)
    def _():
        greet([along_x, along_y])
        for copy in cross + keep:
            copy.start()
        begin(ups)
        inverse_back_step(
            land_ref, marks_ref, sum_ref, mid_ref, z_ref, p_ref, a_ref, w_ref, scale_ref, tot_ref, alpha_ref,
            gn, gt, mq_ref, mk, g_acc, dk_acc,
        )
        for r in range(ranks):
            gt_low[r] = jnp.concatenate(
                [gt[r, i, 0:1, :] for i in range(own)] + [jnp.zeros((8 - own, 128), f32)], axis=0
            )
        add_pairs(klp_ref, mk, me * own, klp_ref.shape[0])
        kl[...] = klp_ref[...].astype(bf16)
        for pair in exchanges:
            begin(pair)

    @pl.when(step == late)
    def _():
        for copy in cross + keep:
            copy.wait()
        cross_add(kept, crossed)
        for copy in turn:
            copy.start()

    @pl.when(step > 0)
    def _():
        conv_back_tile((step - 1) % seqs, seqs, cg_ref, rim_ref, cv_ref, f_ref, co_ref, gf_ref, pad, facc)

    @pl.when(step == pl.num_programs(0) - 1)
    def _():
        for copy in turn:
            copy.wait()
        turn_add(down_ref, kept, turned)
        for pair in exchanges:
            finish(pair)
        finish(ups)


def inverse_conv(land_parts, land, saved, klp, gm, rim, v, taps, downs, ups, first_group):
    ranks, own = land_parts.shape[:2]
    seqs, rows, features = v.shape
    pairs = features // 128 * seqs
    groups = features // 128 - first_group
    marks = M // ranks
    mat = jax.ShapeDtypeStruct((own, M, 128), f32)
    down_sum = jax.ShapeDtypeStruct((4, 240, 384), bf16)
    whole = lambda a: pl.BlockSpec(a.shape, lambda i: (0,) * len(a.shape), pipeline_mode=pl.Buffered(1))
    cv, rims, ft, co, go = conv_back_specs(rows, seqs, 1, first_group)
    return pl.pallas_call(
        functools.partial(inverse_conv_kernel, 7),
        grid=(1 + seqs * groups,),
        in_specs=[whole(land_parts), whole(land)]
        + [whole(a) for a in saved]
        + [whole(klp), cv, rims, cv, ft, ANY, ANY],
        out_specs=[whole(mat), co, go, whole(down_sum)] + [ANY] * 4,
        out_shape=[
            mat,
            jax.ShapeDtypeStruct((seqs, rows, 128 * groups), bf16),
            jax.ShapeDtypeStruct((KW, 128 * groups), f32),
            down_sum,
            jax.ShapeDtypeStruct((ranks, own, M, 128), bf16),
            jax.ShapeDtypeStruct((ranks, 8, 128), f32),
            jax.ShapeDtypeStruct((ranks, pairs, marks, 128), bf16),
            jax.ShapeDtypeStruct(ups.shape, bf16),
        ],
        scratch_shapes=[
            pltpu.VMEM((ranks, own, M, 128), bf16), pltpu.VMEM((ranks, own, 8, 128), f32),
            pltpu.VMEM((ranks, 8, 128), f32),
            pltpu.VMEM((own, M, 128), f32), pltpu.VMEM((own, M, 128), f32), pltpu.VMEM((own, M, 128), f32),
            pltpu.VMEM((pairs, M, 128), bf16), pltpu.VMEM((rows + 2 * RIM, 128), f32),
            pltpu.VMEM((KW * 8, 128), f32),
        ]
        + stage_scratch(240)
        + [rank_sems(), rank_sems(), rank_sems(), rank_sems()],
        compiler_params=params(62 * MB, collective_id=5, has_side_effects=True),
        name="inverse_conv",
    )(land_parts, land, *saved, klp, gm, rim, v, taps, downs, ups)


def third_step(w_ref, v_ref, k_ref, conv_of, gn_of, gt_of, ql_of, put_v, put_k, put_qlp):
    features = w_ref.shape[2]
    masks = group_masks((M, 4 * E), 4, bf16)
    masks_wide = group_masks((M, 4 * E), 4, f32)
    for g in range(features // 256):
        sl = slice(256 * g, 256 * g + 256)
        w = w_ref[0, :, sl]
        gd = block_diag(jnp.concatenate([gn_of(2 * g), gn_of(2 * g + 1)], axis=1), masks)
        gt = jnp.concatenate([gt_of(2 * g), gt_of(2 * g + 1)], axis=1)
        gs = (w.astype(f32) * (dot_nt(v_ref[0, :, sl], gd) + gt)).astype(bf16)
        put_v(g, (dot(w, gd) + conv_of(g)).astype(bf16))
        put_k(g, dot(gs, block_diag(ql_of(sl), masks)))
        put_qlp(g, diag_blocks(dot_tn(gs, k_ref[0, :, sl]), masks_wide))


def final_kernel(
    w_ref, v_ref, k_ref, tok_ref, ca_ref, cb_ref, gn_ref, gt_ref, marks_ref, gq_ref, kl_ref, mq_ref, proj_ref,
    wq_ref, small_ref, up_ref, down_in,
    gtok_ref, up_out, down_out, out_out, qkv_out, tot_ref,
    d, tok_t, qlp, qlow, qgot, part, got_a, sum_a, got_b, sum_b, got_c, sum_c, got_z, down,
    sm_got, sm_sum, q_sems, z_sems, late_sems, a_send, a_recv, b_sems, c_sems, zq_send, zq_recv, s_send, s_recv,
    s_sems,
):
    step = pl.program_id(0)
    rows, features = tok_ref.shape[1:]
    seqs = gq_ref.shape[0]
    pairs = features // 128
    ranks, marks = kl_ref.shape[0], kl_ref.shape[2]
    own = mq_ref.shape[0]
    seg = rows // marks
    last = pl.num_programs(0) - 1
    me, _ = seq_place()
    core, x, y, sibling, along_x, along_y = cube()

    def z_copies(rows_of, sems):
        sends = [
            remote(down_in.at[peer, rows_of], down.at[me, rows_of], sems.at[0, o], sems.at[1, o], {"seq": peer})
            for o, peer in seq_peers()
        ]
        return sends, pltpu.make_async_copy(down_in.at[me, rows_of], down.at[me, rows_of], sems.at[0, 0])

    early = z_copies(pl.ds(0, 96), z_sems)
    late = z_copies(pl.ds(96, 144), late_sems)

    def q_copies():
        sends = [
            remote(
                qlow.at[:, pl.ds(peer * marks, marks)], qgot.at[me], q_sems.at[0, o], q_sems.at[1, o],
                {"seq": peer},
            )
            for o, peer in seq_peers()
        ]
        return sends, pltpu.make_async_copy(
            qlow.at[:, pl.ds(me * marks, marks)], qgot.at[me], q_sems.at[0, 0]
        )

    def a_copy(p):
        return remote(
            part.at[1 - core, pl.ds(4 * p, 4)], got_a.at[pl.ds(4 * p, 4)], a_send.at[p], a_recv.at[p], sibling
        )

    def b_copies(p):
        return [
            remote(
                sum_a.at[4 * p : 4 * p + 2, :, 1 - x], got_b.at[p, 0], b_sems.at[0, p, 0], b_sems.at[1, p, 0],
                along_x,
            ),
            remote(
                sum_a.at[4 * p + 2 : 4 * p + 4, 1 - y], got_b.at[p, 1], b_sems.at[0, p, 1], b_sems.at[1, p, 1],
                along_y,
            ),
        ]

    def c_copies(p):
        return [
            remote(
                sum_b.at[p, 0, :, 1 - y], got_c.at[p, 0], c_sems.at[0, p, 0], c_sems.at[1, p, 0], along_y
            ),
            remote(
                sum_b.at[p, 1, :, 1 - x], got_c.at[p, 1], c_sems.at[0, p, 1], c_sems.at[1, p, 1], along_x
            ),
        ]

    def zq_copy(group):
        rank, place = group // 3, group % 3
        offset = lax.rem(rank - me + ranks, ranks)
        return rank, remote(
            sum_c.at[group], got_z.at[me, place], zq_send.at[group], zq_recv.at[place, offset], {"seq": rank}
        )

    def stage_b(p):
        a_copy(p).wait()
        for yx in range(4):
            sum_a[4 * p : 4 * p + 4, yx // 2, yx % 2] = add_low(
                part[core, 4 * p : 4 * p + 4, yx], got_a[4 * p : 4 * p + 4, yx]
            )
        for copy in b_copies(p):
            copy.start()

    def stage_c(p):
        for copy in b_copies(p):
            copy.wait()
        sum_b[p, 0] = add_low(sum_a[4 * p : 4 * p + 2, :, x], got_b[p, 0])
        sum_b[p, 1] = add_low(sum_a[4 * p + 2 : 4 * p + 4, y], got_b[p, 1])
        for copy in c_copies(p):
            copy.start()

    def stage_z(p):
        for copy in c_copies(p):
            copy.wait()
        sum_c[4 * p : 4 * p + 2] = add_low(sum_b[p, 0, :, y], got_c[p, 0])
        sum_c[4 * p + 2 : 4 * p + 4] = add_low(sum_b[p, 1, :, x], got_c[p, 1])
        for group in range(4 * p, 4 * p + 4):
            rank, copy = zq_copy(group)

            @pl.when(rank != me)
            def _(copy=copy):
                copy.start()

    small_copies = [
        remote(sm_sum.at[i], sm_got.at[i], s_send.at[i], s_recv.at[i], target)
        for i, target in enumerate((sibling, along_x, along_y))
    ]

    def small_spread():
        return [
            remote(sm_sum.at[3], sm_got.at[3 + me], s_sems.at[0, o], s_sems.at[1, o], {"seq": peer})
            for o, peer in seq_peers()
        ]

    @pl.when(step == 0)
    def _():
        greet([sibling, along_x, along_y])
        begin(early)
        sm_sum[0] = small_ref[...]
        small_copies[0].start()
        up = up_ref[0].astype(f32)
        for r in range(1, ranks):
            up = up + up_ref[r].astype(f32)
        up_out[:, :384] = up[:96]
        up_out[:, 384:] = up[96:]

    for i in range(1, 4):
        @pl.when(step == i)
        def _(i=i):
            small_copies[i - 1].wait()
            sm_sum[i] = sm_sum[i - 1] + sm_got[i - 1]
            if i < 3:
                small_copies[i].start()
            else:
                for copy in small_spread():
                    copy.start()

    def land_rows(of):
        total = of(0).astype(f32)
        for r in range(1, ranks):
            total = total + of(r).astype(f32)
        return total * (1.0 / seg)

    @pl.when(step < seqs)
    def _():
        start = step * rows

        def conv_of(g):
            half = ca_ref.shape[2]
            at = 256 * g
            pieces = []
            for l in (at, at + 128):
                ref, lane = (ca_ref, l) if l < half else (cb_ref, l - half)
                pieces.append(ref[0, :, lane : lane + 128].astype(f32))
            return jnp.concatenate(pieces, axis=1)

        def gt_of(i):
            p = step * pairs + i
            return gt_ref[p // own, pl.ds(p % own, 1), :]

        def gn_of(i):
            p = step * pairs + i
            return gn_ref[p // own, p % own]

        def put_v(g, val):
            d[pl.ds(pl.multiple_of(start, rows), rows), 2 * features + 256 * g : 2 * features + 256 * g + 256] = val

        def put_k(g, val):
            for i in range(2):
                p = step * pairs + 2 * g + i
                spread = land_rows(lambda r: kl_ref[r, p])
                lane = features + 256 * g + 128 * i
                for m in range(marks):
                    at = pl.ds(pl.multiple_of(start + m * seg, seg), seg)
                    d[at, lane : lane + 128] = (
                        val[m * seg : m * seg + seg, 128 * i : 128 * i + 128] + spread[m : m + 1]
                    ).astype(bf16)

        def put_qlp(g, val):
            for i in range(2):
                qlp[step * pairs + 2 * g + i] = val[:, 128 * i : 128 * i + 128]

        third_step(
            w_ref, v_ref, k_ref, conv_of, gn_of, gt_of, lambda sl: marks_ref[0, 0, :, sl], put_v, put_k, put_qlp
        )
        tok_t[:, pl.ds(pl.multiple_of(start, rows), rows)] = tok_ref[0].T

    @pl.when(step == seqs - 1)
    def _():
        add_pairs(qlp, mq_ref, me * own, seqs * pairs)
        qlow[...] = qlp[...].astype(bf16)
        begin(q_copies())

    @pl.when(step == seqs + 2)
    def _():
        stage_b(2)
        finish(q_copies())
        begin(late)

        def fill(s, carry):
            for g in range(pairs):
                spread = land_rows(lambda r: qgot[r, s * pairs + g])
                for m in range(marks):
                    at = pl.ds(pl.multiple_of(s * rows + m * seg, seg), seg)
                    val = gq_ref[s, m * seg : m * seg + seg, 128 * g : 128 * g + 128].astype(f32)
                    low = (val + spread[m : m + 1]).astype(bf16) * jnp.asarray(0.125, bf16)
                    d[at, 128 * g : 128 * g + 128] = low
            return carry

        lax.fori_loop(0, seqs, fill, 0)

    for at, stages in (
        (seqs + 3, [(stage_b, 1)]),
        (seqs + 4, [(stage_b, 0)]),
        (seqs + 5, [(stage_c, 2)]),
        (seqs + 7, [(stage_z, 2)]),
        (seqs + 8, [(stage_c, 1)]),
    ):
        @pl.when(step == at)
        def _(stages=stages):
            for stage, p in stages:
                stage(p)

    @pl.when((step >= seqs) & (step < seqs + 3))
    def _():
        p = seqs + 2 - step
        for c in range(2):
            cols = pl.ds(pl.multiple_of(p * features + 384 * c, 128), 384)
            low = dot(tok_t[...], d[:, cols]).astype(bf16)
            for i in range(2):
                for dd in range(8):
                    block = low[96 * dd : 96 * dd + 96, 192 * i : 192 * i + 192]
                    part[dd % 2, 4 * p + 2 * c + i, dd // 2] = jnp.concatenate([block[:48], block[48:]], axis=1)
        a_copy(p).start()

    @pl.when((step >= seqs + 3) & (step < last))
    def _():
        size = gtok_ref.shape[0]
        start = (step - seqs - 3) * size
        for c in range(0, size, 128):
            at = pl.ds(pl.multiple_of(start + c, 128), 128)
            gtok_ref[c : c + 128, :] = (
                proj_ref[c : c + 128, :].astype(f32) + dot_nt(d[at, :], wq_ref[...])
            ).astype(bf16)

    def unfold(block):
        return jnp.concatenate([block[:, :192], block[:, 192:]], axis=0)

    @pl.when(step == last)
    def _():
        stage_z(1)
        stage_c(0)
        for copy in small_spread():
            copy.wait()
        sm_got[3 + me] = sm_sum[3]
        tot_ref[...] = (sm_got[3] + sm_got[4]) + (sm_got[5] + sm_got[6])
        finish(early)
        finish(late)
        total = down[0].astype(f32)
        for r in range(1, ranks):
            total = total + down[r].astype(f32)
        down_out[...] = total[:192].T
        out_out[...] = unfold(total[192:240])
        stage_z(0)
        for group in range(12):
            rank, copy = zq_copy(group)

            @pl.when(rank != me)
            def _(copy=copy):
                copy.wait_send()

        for o in range(1, ranks):
            source = lax.rem(me - o + ranks, ranks)
            for place in range(3):
                remote(
                    sum_c.at[0], got_z.at[source, place], zq_send.at[0], zq_recv.at[place, o], {"seq": source}
                ).wait_recv()
        for place in range(3):
            got_z[me, place] = sum_c[3 * me + place]
        shares = []
        for place in range(3):
            total = got_z[0, place].astype(f32)
            for r in range(1, ranks):
                total = total + got_z[r, place].astype(f32)
            shares.append(unfold(total))
        qkv_out[...] = jnp.concatenate(shares, axis=1)


def final_pass(
    weights, v, k, tokens, conv_a, conv_b, gn, gt, land, gq, kl_parts, mid_q, proj, w_qkv, small, ups, downs
):
    seqs, rows, features = tokens.shape
    ranks = lax.axis_size("seq")
    pairs = features // 128 * seqs
    marks = M // ranks
    total = seqs * rows
    size = 256
    blocks = total // size
    here = lambda i: jnp.minimum(i, seqs - 1)
    late = lambda i: jnp.clip(i - seqs - 3, 0, blocks - 1)
    full = lambda a: pl.BlockSpec((1, rows, a.shape[2]), lambda i: (here(i), 0, 0))
    later = pl.BlockSpec((size, features), lambda i: (late(i), 0))
    whole = lambda a: pl.BlockSpec(a.shape, lambda i: (0,) * len(a.shape), pipeline_mode=pl.Buffered(1))
    vm = lambda *shape: pltpu.VMEM(shape, bf16)
    dma = pltpu.SemaphoreType.DMA
    shares = [jax.ShapeDtypeStruct(s, f32) for s in ((96, 768), (384, 192), (96, 192), (96, 576))]
    return pl.pallas_call(
        final_kernel,
        grid=(seqs + 3 + blocks + 1,),
        in_specs=[full(weights), full(v), full(k), full(tokens), full(conv_a), full(conv_b), whole(gn), whole(gt)]
        + [pl.BlockSpec((1, 2, M, features), lambda i: (here(i), 0, 0, 0)), whole(gq), whole(kl_parts), whole(mid_q)]
        + [later, whole(w_qkv), whole(small), whole(ups), ANY],
        out_specs=[later] + [whole(a) for a in shares] + [whole(small)],
        out_shape=[jax.ShapeDtypeStruct((total, features), bf16)]
        + shares
        + [jax.ShapeDtypeStruct(small.shape, f32)],
        scratch_shapes=[
            vm(total, 3 * features), vm(features, total), pltpu.VMEM((pairs, M, 128), f32),
            vm(pairs, M, 128), vm(ranks, pairs, marks, 128), vm(2, 12, 4, 48, 384), vm(12, 4, 48, 384),
            vm(12, 2, 2, 48, 384), vm(3, 2, 2, 2, 48, 384), vm(3, 2, 2, 2, 48, 384), vm(3, 2, 2, 48, 384),
            vm(12, 48, 384), vm(ranks, 3, 48, 384), vm(ranks, 240, 384),
            pltpu.VMEM((3 + ranks,) + small.shape, f32), pltpu.VMEM((4,) + small.shape, f32),
            rank_sems(), rank_sems(), rank_sems(), dma((3,)), dma((3,)), dma((2, 3, 2)), dma((2, 3, 2)),
            dma((12,)), dma((3, ranks)), dma((3,)), dma((3,)), rank_sems(),
        ],
        compiler_params=params(62 * MB, collective_id=6, has_side_effects=True),
        name="final_pass",
    )(
        weights, v, k, tokens, conv_a, conv_b, gn, gt, land, gq, kl_parts, mid_q, proj, w_qkv, small, ups, downs
    )


def halo(cells, width):
    count = lax.axis_size("seq")
    head, tail = cells[:, :width], cells[:, cells.shape[1] - width :]
    left = lax.ppermute(tail, "seq", [(i, i + 1) for i in range(count - 1)])
    right = lax.ppermute(head, "seq", [(i + 1, i) for i in range(count - 1)])
    return jnp.stack([left, right], axis=1)


def scatter_sum(grad):
    share = lax.psum_scatter(grad, "dp", scatter_dimension=0, tiled=True)
    return lax.psum_scatter(share, "seq", scatter_dimension=1, tiled=True).astype(f32)


def per_device_general(tokens, w_qkv, w_out, w_up, w_down, conv_filter, gain_att, gain_ffn, grad_out):
    seqs, rows, features = tokens.shape
    ranks = lax.axis_size("seq")
    rank = lax.axis_index("seq")
    marks = M // ranks
    ff = w_up.shape[1]
    pairs = seqs * (features // 128)
    own = -(-pairs // ranks)

    def from_pairs(x):
        x = x[:pairs].reshape(seqs, features // 128, M, 128).transpose(0, 2, 1, 3)
        return x.reshape(seqs, M, features)

    def pad_pairs(x):
        return jnp.pad(x, ((0, ranks * own - pairs),) + ((0, 0),) * (x.ndim - 1))

    def exchange(x):
        out = lax.all_to_all(pad_pairs(x), "seq", 0, 0, tiled=True)
        return out.reshape((ranks, own) + x.shape[1:])

    taps = conv_filter.astype(f32)
    q, k, v, land, v_rim = project(tokens, w_qkv, marks)
    q_land, k_land = land[:, 0], land[:, 1]
    first_group = features // 256
    weights, probs, conv_a, num_parts, stat_parts = scores(q, k, v, land, v_rim, taps, own, first_group)
    mixed_pairs, conv_b, *saved = inverse(num_parts, stat_parts, land, v, v_rim, taps, first_group)
    mixed = mixed_pairs
    layer_out, proj, gm, wg, gains = row_pass(
        tokens, probs, conv_a, conv_b, mixed, grad_out, w_out, w_up, w_down, gain_att, gain_ffn
    )
    shape3 = (seqs, rows, features)
    gm = gm.reshape(shape3)
    chunks = ff // features
    up_share = scatter_sum(wg[:chunks].transpose(1, 0, 2).reshape(features, ff))
    down_share = scatter_sum(wg[chunks : 2 * chunks].transpose(0, 2, 1).reshape(ff, features))
    out_share = scatter_sum(wg[2 * chunks])
    land_part, gq, k_land_part = first_back(gm, probs, q, mixed, k_land)
    g_rim = halo(gm, RIM)
    land_parts = exchange(land_part)
    grad_conv, taps_grad = conv_back(gm, g_rim, v, taps)
    gn_own, gt_own, mid_q, mid_k = inverse_back(land_parts, land, saved)

    def give_back(x):
        x = x.reshape((ranks * own,) + x.shape[2:])
        return lax.all_to_all(x, "seq", 0, 0, tiled=True)[:pairs]

    grad_values, gk, q_land_part = third_back(
        weights, v, k, grad_conv, give_back(gn_own), give_back(gt_own), q_land
    )

    def place(x):
        full = jnp.zeros((ranks * own, M, 128), f32)
        return from_pairs(lax.dynamic_update_slice_in_dim(full, x, rank * own, 0))

    both = jnp.stack([q_land_part + place(mid_q), k_land_part + place(mid_k)]).astype(bf16)
    both = both.reshape(2, seqs, ranks, marks, features).transpose(2, 0, 1, 3, 4)
    both = lax.all_to_all(both, "seq", 0, 0, tiled=True).astype(f32).sum(0)
    grad_tokens, qkv_grad = last_pass(tokens, gq, gk, grad_values, both[0], both[1], proj.reshape(shape3), w_qkv)
    qkv_share = scatter_sum(qkv_grad.transpose(1, 0, 2).reshape(features, 3 * features))
    gains = gains.reshape(2, 8, features).sum(1)
    small = lax.psum(jnp.concatenate([taps_grad, gains]), ("dp", "seq"))
    return (
        layer_out.reshape(shape3),
        grad_tokens,
        qkv_share,
        out_share,
        up_share,
        down_share,
        small[:KW],
        small[KW],
        small[KW + 1],
    )


def per_device(tokens, w_qkv, w_out, w_up, w_down, conv_filter, gain_att, gain_ffn, grad_out):
    seqs, rows, features = tokens.shape
    ranks = lax.axis_size("seq")
    marks = M // ranks
    pairs = seqs * (features // 128)
    own = -(-pairs // ranks)
    taps = conv_filter.astype(f32)
    half = features // 256
    shape3 = (seqs, rows, features)

    q, k, v, land, v_rim = project(tokens, w_qkv, marks)
    weights, probs, conv_a, num_parts, stat_parts = scores(q, k, v, land, v_rim, taps, own, half)
    mixed, conv_b, *saved = inverse(num_parts, stat_parts, land, v, v_rim, taps, half)
    layer_out, proj, gm, gains, act, gdl_t, mix_t, ups, g_rim = row_share(
        tokens, probs, conv_a, conv_b, mixed, grad_out, w_out, w_up, w_down, gain_att, gain_ffn
    )
    gm = gm.reshape(shape3)
    early = 2
    gq, klp, gconv_a, taps_a, ups, downs, land_parts = down_first(
        act, gdl_t, mix_t, proj, gm, probs, q, mixed, land, g_rim, v, taps, ups.reshape(4, 2, 2, 192, 384), own,
        early,
    )
    mid_q, gconv_b, taps_b, downs, gn, gt, kl_parts, ups = inverse_conv(
        land_parts, land, saved, klp, gm, g_rim, v, taps, downs.reshape(4, 2, 2, 240, 384), ups, early
    )
    gains = gains.reshape(2, 8, features).sum(1)
    small = jnp.concatenate(
        [jnp.concatenate([taps_a, taps_b], axis=1), gains, jnp.zeros((5, features), f32)]
    )
    grad_tokens, up, down, out, qkv, small = final_pass(
        weights, v, k, tokens, gconv_a, gconv_b, gn, gt, land, gq, kl_parts, mid_q, proj, w_qkv, small, ups, downs
    )
    return (
        layer_out.reshape(shape3),
        grad_tokens.reshape(shape3),
        qkv,
        out,
        up,
        down,
        small[:KW],
        small[KW],
        small[KW + 1],
    )


def solution(mesh):
    placed = (P("dp", "seq", None), P(), P(), P(), P(), P(), P(), P(), P("dp", "seq", None))
    eight_by_four = mesh.shape["dp"] == 8 and mesh.shape["seq"] == 4
    return jax.shard_map(
        per_device if eight_by_four else per_device_general,
        mesh=mesh,
        in_specs=placed,
        out_specs=(
            P("dp", "seq", None),
            P("dp", "seq", None),
            P("dp", "seq"),
            P("dp", "seq"),
            P("dp", "seq"),
            P("dp", "seq"),
            P(),
            P(),
            P(),
        ),
        check_vma=False,
    )
```

```python
import functools

import jax
import jax.numpy as jnp
from jax import lax
from jax.experimental import pallas as pl
from jax.experimental.pallas import tpu as pltpu
from jax.sharding import PartitionSpec as P

H = 12
E = 64
M = 64
KW = 33
RIM = KW // 2
NEWTON = 6

f32 = jnp.float32
bf16 = jnp.bfloat16
epsilon = 1e-05
root_half = 0.7071067811865476
inv_root_two_pi = 0.3989422804014327
MB = 1 << 20

ERFC_P = 0.6
ERFC_C = (0.37028039425845705, 0.14043533559747823, 0.7278464793107866, -0.23856251479455173)
log2_e = 1.4426950408889634


def dot(a, b):
    return lax.dot_general(a, b, (((1,), (0,)), ((), ())), preferred_element_type=f32)


def dot_nt(a, b):
    return lax.dot_general(a, b, (((1,), (1,)), ((), ())), preferred_element_type=f32)


def dot_tn(a, b):
    return lax.dot_general(a, b, (((0,), (0,)), ((), ())), preferred_element_type=f32)


def lane_group(shape):
    return lax.broadcasted_iota(jnp.int32, shape, len(shape) - 1) // E


def group_masks(shape, count, dtype):
    groups = lane_group(shape)
    return [(groups == h).astype(f32).astype(dtype) for h in range(count)]


def block_diag(x, masks):
    return jnp.concatenate([x * m for m in masks], axis=0)


def diag_blocks(n, masks):
    return sum(n[E * h : E * h + E] * m for h, m in enumerate(masks))


def quad(ref, g):
    return jnp.concatenate([ref[2 * g], ref[2 * g + 1]], axis=1)


def params(limit=None, **kw):
    return pltpu.CompilerParams(vmem_limit_bytes=limit, **kw)


MESH = pl.DeviceIdType.MESH
ANY = pl.BlockSpec(memory_space=pl.ANY)


def seq_place():
    return lax.axis_index("seq"), lax.axis_size("seq")


def seq_peers():
    me, count = seq_place()
    return [(o, lax.rem(me + o, count)) for o in range(1, count)]


def greet(extra=()):
    barrier = pltpu.get_barrier_semaphore()
    targets = [{"seq": peer} for _, peer in seq_peers()] + list(extra)
    for target in targets:
        pl.semaphore_signal(barrier, inc=1, device_id=target, device_id_type=MESH)
    pl.semaphore_wait(barrier, len(targets))


def remote(src, dst, send, recv, target):
    return pltpu.make_async_remote_copy(
        src_ref=src, dst_ref=dst, send_sem=send, recv_sem=recv, device_id=target, device_id_type=MESH
    )


def swap_copies(src, dst, own, sems):
    me, count = seq_place()
    copies = [
        remote(src.at[pl.ds(peer * own, own)], dst.at[me], sems.at[0, o], sems.at[1, o], {"seq": peer})
        for o, peer in seq_peers()
    ]
    return copies, pltpu.make_async_copy(src.at[pl.ds(me * own, own)], dst.at[me], sems.at[0, 0])


def spread_copies(src, dst, own, sems):
    me, count = seq_place()
    at = dst.at[pl.ds(me * own, own)]
    copies = [
        remote(src, at, sems.at[0, o], sems.at[1, o], {"seq": peer}) for o, peer in seq_peers()
    ]
    return copies, pltpu.make_async_copy(src, at, sems.at[0, 0])


def begin(pair):
    for copy in pair[0]:
        copy.start()
    pair[1].start()


def finish(pair):
    for copy in pair[0]:
        copy.wait()
    pair[1].wait()


def swap_rows(src, dst, sems):
    me, _ = seq_place()
    copies = [
        remote(src.at[peer], dst.at[me], sems.at[0, o], sems.at[1, o], {"seq": peer}) for o, peer in seq_peers()
    ]
    return copies, pltpu.make_async_copy(src.at[me], dst.at[me], sems.at[0, 0])


def cube():
    d = lax.axis_index("dp")
    core, x, y = d % 2, (d // 2) % 2, d // 4
    return core, x, y, {"dp": d + 1 - 2 * core}, {"dp": d + 2 - 4 * x}, {"dp": d + 4 - 8 * y}


def add_low(a, b):
    return (a.astype(f32) + b.astype(f32)).astype(bf16)


def rank_sems():
    return pltpu.SemaphoreType.DMA((2, lax.axis_size("seq")))


def project_kernel(
    tok_ref, w_ref, q_ref, k_ref, v_ref, kl_ref, land_out, rim_out, land, rim, send, recv, local, rim_send, rim_recv,
    rim_local,
):
    step = pl.program_id(0)
    seqs = pl.num_programs(0)
    me, count = seq_place()
    rows, features = tok_ref.shape[1:]
    marks = land.shape[1]
    seg = rows // marks

    @pl.when(step == 0)
    def _():
        greet()

    x = tok_ref[0]
    for part, out in enumerate((q_ref, k_ref, v_ref)):
        for c in range(0, features, 256):
            p = dot(x, w_ref[:, part * features + c : part * features + c + 256])
            if part == 0:
                p = 0.125 * p
            low = p.astype(bf16)
            out[0, :, c : c + 256] = low
            if part < 2:
                total = low.astype(f32).reshape(marks, seg, 256).sum(1)
                mean = (total * (1.0 / seg)).astype(bf16)
                if part == 0:
                    land[step, :, c : c + 256] = mean
                else:
                    kl_ref[0, :, c : c + 256] = mean
            else:
                rim[step, 0, :, c : c + 256] = low[rows - RIM :]
                rim[step, 1, :, c : c + 256] = low[:RIM]

    def copies(s):
        spot = land_out.at[s, pl.ds(me * marks, marks)]
        sends = [
            remote(land.at[s], spot, send.at[s, o], recv.at[s, o], {"seq": peer}) for o, peer in seq_peers()
        ]
        return sends, pltpu.make_async_copy(land.at[s], spot, local.at[s])

    def rim_copy(s, side):
        there = lax.rem(me + (1 if side == 0 else count - 1), count)
        return remote(
            rim.at[s, side], rim_out.at[s, side], rim_send.at[s, side], rim_recv.at[s, side], {"seq": there}
        )

    begin(copies(step))
    for side in range(2):
        rim_copy(step, side).start()

    @pl.when(step == seqs - 1)
    def _():
        def drain(s, carry):
            finish(copies(s))
            for side in range(2):
                rim_copy(s, side).wait()
            return carry

        lax.fori_loop(0, seqs, drain, 0)


def project(tokens, w_qkv, marks):
    seqs, rows, features = tokens.shape
    ranks = lax.axis_size("seq")
    full = pl.BlockSpec((1, rows, features), lambda s: (s, 0, 0))
    dma = pltpu.SemaphoreType.DMA
    return pl.pallas_call(
        project_kernel,
        grid=(seqs,),
        in_specs=[full, pl.BlockSpec(w_qkv.shape, lambda s: (0, 0), pipeline_mode=pl.Buffered(1))],
        out_specs=[full] * 3 + [pl.BlockSpec((1, marks, features), lambda s: (s, 0, 0))] + [ANY] * 2,
        out_shape=[jax.ShapeDtypeStruct(tokens.shape, bf16)] * 3
        + [
            jax.ShapeDtypeStruct((seqs, marks, features), bf16),
            jax.ShapeDtypeStruct((seqs, M, features), bf16),
            jax.ShapeDtypeStruct((seqs, 2, RIM, features), bf16),
        ],
        scratch_shapes=[
            pltpu.VMEM((seqs, marks, features), bf16), pltpu.VMEM((seqs, 2, RIM, features), bf16),
            dma((seqs, ranks)), dma((seqs, ranks)), dma((seqs,)), dma((seqs, 2)), dma((seqs, 2)), dma((seqs,)),
        ],
        compiler_params=params(62 * MB, collective_id=0, has_side_effects=True),
        name="project",
    )(tokens, w_qkv)


def fill_taps(taps, f_ref):
    taps[0:KW, :] = f_ref[...].astype(f32)


def fill_pad(pad, x_ref, rim_ref):
    rows = x_ref.shape[1]
    me, count = seq_place()
    pad[0:RIM, :] = jnp.where(me > 0, rim_ref[0, 0].astype(f32), 0.0)
    pad[RIM : RIM + rows, :] = x_ref[0].astype(f32)
    pad[RIM + rows : RIM + rows + RIM, :] = jnp.where(me < count - 1, rim_ref[0, 1].astype(f32), 0.0)


def conv_tile(v_ref, rim_ref, taps_ref, o_ref, pad, f_ref):
    rows = v_ref.shape[1]
    fill_pad(pad, v_ref, rim_ref)
    fill_taps(f_ref, taps_ref)
    for c in range(0, rows, 64):
        acc = jnp.zeros((64, 128), f32)
        for j in range(KW):
            acc = acc + f_ref[j : j + 1, :] * pad[c + j : c + j + 64, :]
        o_ref[0, c : c + 64, :] = acc.astype(bf16)


def conv_specs(rows, first_step, first_group, groups):
    at = lambda i: jnp.maximum(i - first_step, 0)
    seq = lambda i: at(i) // groups
    group = lambda i: at(i) % groups
    return (
        pl.BlockSpec((1, rows, 128), lambda i: (seq(i), 0, first_group + group(i))),
        pl.BlockSpec((1, 2, RIM, 128), lambda i: (seq(i), 0, 0, first_group + group(i))),
        pl.BlockSpec((KW, 128), lambda i: (0, first_group + group(i))),
        pl.BlockSpec((1, rows, 128), lambda i: (seq(i), 0, group(i))),
    )


def conv_back_tile(seq, seqs, g_ref, rim_ref, v_ref, taps_ref, o_ref, gf_ref, pad, facc, f_ref):
    rows = v_ref.shape[1]
    fill_pad(pad, g_ref, rim_ref)
    fill_taps(f_ref, taps_ref)

    @pl.when(seq == 0)
    def _():
        facc[...] = jnp.zeros_like(facc)

    for c in range(0, rows, 64):
        acc = jnp.zeros((64, 128), f32)
        vals = v_ref[0, c : c + 64, :].astype(f32)
        for j in range(KW):
            moved = pad[c + 2 * RIM - j : c + 2 * RIM - j + 64, :]
            acc = acc + f_ref[j : j + 1, :] * moved
            facc[8 * j : 8 * j + 8, :] += (vals * moved).reshape(8, 8, 128).sum(0)
        o_ref[0, c : c + 64, :] = acc.astype(bf16)

    @pl.when(seq == seqs - 1)
    def _():
        gf_ref[...] = facc[...].reshape(KW, 8, 128).sum(1)


def conv_back_kernel(g_ref, rim_ref, v_ref, f_ref, o_ref, gf_ref, pad, facc, taps):
    conv_back_tile(
        pl.program_id(1), pl.num_programs(1), g_ref, rim_ref, v_ref, f_ref, o_ref, gf_ref, pad, facc, taps
    )


def conv_back_specs(rows, seqs, first_step, first_group):
    at = lambda i: jnp.maximum(i - first_step, 0)
    seq = lambda i: at(i) % seqs
    group = lambda i: at(i) // seqs
    return (
        pl.BlockSpec((1, rows, 128), lambda i: (seq(i), 0, first_group + group(i))),
        pl.BlockSpec((1, 2, RIM, 128), lambda i: (seq(i), 0, 0, first_group + group(i))),
        pl.BlockSpec((KW, 128), lambda i: (0, first_group + group(i))),
        pl.BlockSpec((1, rows, 128), lambda i: (seq(i), 0, group(i))),
        pl.BlockSpec((KW, 128), lambda i: (0, group(i))),
    )


def conv_back(g, rim, v, taps):
    seqs, rows, features = v.shape
    sp = lambda n: pl.BlockSpec((1, n, 128), lambda g, s: (s, 0, g))
    fs = pl.BlockSpec((KW, 128), lambda g, s: (0, g))
    return pl.pallas_call(
        conv_back_kernel,
        grid=(features // 128, seqs),
        in_specs=[sp(rows), pl.BlockSpec((1, 2, RIM, 128), lambda g, s: (s, 0, 0, g)), sp(rows), fs],
        out_specs=[sp(rows), fs],
        out_shape=[jax.ShapeDtypeStruct(v.shape, bf16), jax.ShapeDtypeStruct((KW, features), f32)],
        scratch_shapes=[pltpu.VMEM((rows + 2 * RIM, 128), f32), pltpu.VMEM((KW * 8, 128), f32), pltpu.VMEM((40, 128), f32)],
        name="conv_back",
    )(g, rim, v, taps)


def third_score_step(step, k_ref, v_ref, ql_ref, w_ref, num_ref, stat_ref, own):
    features = k_ref.shape[2]
    pairs = features // 128
    masks = group_masks((M, 4 * E), 4, bf16)
    masks_wide = group_masks((M, 4 * E), 4, f32)
    for g in range(features // 256):
        sl = slice(256 * g, 256 * g + 256)
        s3 = dot_nt(k_ref[0, :, sl], block_diag(ql_ref[0, :, sl], masks))
        peak = jnp.max(s3, axis=0, keepdims=True)
        e3 = jnp.exp(s3 - peak)
        total = jnp.sum(e3, axis=0, keepdims=True)
        low = e3.astype(bf16)
        w_ref[0, :, sl] = low
        num = diag_blocks(dot_tn(low, v_ref[0, :, sl]), masks_wide).astype(bf16)
        for i in range(2):
            lanes = slice(128 * i, 128 * i + 128)
            p = step * pairs + 2 * g + i
            num_ref[p] = num[:, lanes]
            stat_ref[p // own, pl.ds(p % own, 1), :] = peak[:, lanes]
            stat_ref[p // own, pl.ds(8 + p % own, 1), :] = total[:, lanes]


def first_score_step(q_ref, kl, p_ref):
    features = q_ref.shape[2]
    masks = group_masks((M, 4 * E), 4, bf16)
    for g in range(features // 256):
        sl = slice(256 * g, 256 * g + 256)
        s1 = dot_nt(block_diag(kl[:, sl], masks), q_ref[0, :, sl])
        for h in range(4):
            x = s1[E * h : E * h + E]
            e1 = jnp.exp(x - jnp.max(x, axis=0, keepdims=True))
            at = 256 * g + E * h
            p_ref[0, at : at + E, :] = (e1 * (1.0 / jnp.sum(e1, axis=0, keepdims=True))).astype(bf16)


def scores_kernel(
    seqs, own, q_ref, k_ref, v_ref, ql_ref, kp_ref, cv_ref, rim_ref, f_ref, w_ref, p_ref, kl_ref, co_ref, num_out,
    stat_out, num, stat, kl, pad, taps, num_sems, stat_sems, kl_sems,
):
    step = pl.program_id(0)
    steps = pl.num_programs(0)
    pairs = q_ref.shape[2] // 128
    marks = kp_ref.shape[1]
    me, _ = seq_place()

    def mark_copies():
        spot = kl.at[:, pl.ds(me * marks, marks)]
        sends = [
            remote(kp_ref, spot, kl_sems.at[0, o], kl_sems.at[1, o], {"seq": peer}) for o, peer in seq_peers()
        ]
        return sends, pltpu.make_async_copy(kp_ref, spot, kl_sems.at[0, 0])

    @pl.when(step == 0)
    def _():
        greet()
        begin(mark_copies())
        stat[...] = jnp.zeros_like(stat)
        if num.shape[0] > seqs * pairs:
            num[seqs * pairs :] = jnp.zeros_like(num[seqs * pairs :])

    @pl.when(step < seqs)
    def _():
        third_score_step(step, k_ref, v_ref, ql_ref, w_ref, num, stat, own)

    @pl.when(step == seqs - 1)
    def _():
        begin(swap_copies(num, num_out, own, num_sems))
        begin(swap_rows(stat, stat_out, stat_sems))

    @pl.when(step == seqs)
    def _():
        finish(mark_copies())
        kl_ref[...] = kl[...]

    @pl.when((step >= seqs) & (step < 2 * seqs))
    def _():
        first_score_step(q_ref, kl[step - seqs], p_ref)

    @pl.when(step >= 2 * seqs)
    def _():
        conv_tile(cv_ref, rim_ref, f_ref, co_ref, pad, taps)

    @pl.when(step == steps - 1)
    def _():
        finish(swap_copies(num, num_out, own, num_sems))
        finish(swap_rows(stat, stat_out, stat_sems))


def scores(q, k, v, q_land, k_part, rim, taps, own, groups):
    seqs, rows, features = q.shape
    marks = k_part.shape[1]
    ranks = lax.axis_size("seq")
    here = lambda i: jnp.minimum(i, seqs - 1)
    then = lambda i: jnp.clip(i - seqs, 0, seqs - 1)
    full = pl.BlockSpec((1, rows, features), lambda i: (here(i), 0, 0))
    next_full = pl.BlockSpec((1, rows, features), lambda i: (then(i), 0, 0))
    whole = lambda a: pl.BlockSpec(a.shape, lambda i: (0,) * len(a.shape), pipeline_mode=pl.Buffered(1))
    k_land = jax.ShapeDtypeStruct((seqs, M, features), bf16)
    cv, rims, ft, co = conv_specs(rows, 2 * seqs, 0, groups)
    return pl.pallas_call(
        functools.partial(scores_kernel, seqs, own),
        grid=(2 * seqs + seqs * groups,),
        in_specs=[
            next_full, full, full, pl.BlockSpec((1, M, features), lambda i: (here(i), 0, 0)), whole(k_part), cv,
            rims, ft,
        ],
        out_specs=[full, pl.BlockSpec((1, features, rows), lambda i: (then(i), 0, 0)), whole(k_land), co, ANY, ANY],
        out_shape=[
            jax.ShapeDtypeStruct(q.shape, bf16),
            jax.ShapeDtypeStruct((seqs, features, rows), bf16),
            k_land,
            jax.ShapeDtypeStruct((seqs, rows, 128 * groups), bf16),
            jax.ShapeDtypeStruct((ranks, own, M, 128), bf16),
            jax.ShapeDtypeStruct((ranks, 16, 128), f32),
        ],
        scratch_shapes=[
            pltpu.VMEM((ranks * own, M, 128), bf16), pltpu.VMEM((ranks, 16, 128), f32),
            pltpu.VMEM((seqs, M, features), bf16), pltpu.VMEM((rows + 2 * RIM, 128), f32),
            pltpu.VMEM((40, 128), f32), rank_sems(), rank_sems(), rank_sems(),
        ],
        compiler_params=params(62 * MB, collective_id=1, has_side_effects=True),
        name="scores",
    )(q, k, v, q_land, k_part, v, rim, taps)


def split(x):
    hi = x.astype(bf16)
    return hi, (x - hi.astype(f32)).astype(bf16)


def stack_parts(xs, axis):
    return jnp.concatenate([part for x in xs for part in split(x)], axis=axis)


def pair_sums(out, count):
    top = lambda i, j: out[128 * i + 64 * j : 128 * i + 64 * j + 64]
    return [
        top(i, 0)[:, :128] + (top(i, 0)[:, 128:] + top(i, 1)[:, :128]) for i in range(count)
    ]


def pair_nn(lefts, right, masks):
    hi, lo = split(right)
    packed = jnp.concatenate([block_diag(hi, masks), block_diag(lo, masks)], axis=1)
    return pair_sums(dot(stack_parts(lefts, 0), packed), len(lefts))


def pair_nt(lefts, right, masks):
    hi, lo = split(right)
    packed = jnp.concatenate([block_diag(hi, masks), block_diag(lo, masks)], axis=0)
    return pair_sums(dot_nt(stack_parts(lefts, 0), packed), len(lefts))


def pair_tn(left, rights, masks_wide):
    out = dot_tn(stack_parts([left], 1), stack_parts(rights, 1))
    results = []
    for i in range(len(rights)):
        full = out[:128, 256 * i : 256 * i + 128] + (
            out[:128, 256 * i + 128 : 256 * i + 256] + out[128:, 256 * i : 256 * i + 128]
        )
        results.append(diag_blocks(full, masks_wide))
    return results


def half_reduce(x, upper, op, fill):
    a = op(jnp.where(upper, fill, x), axis=1, keepdims=True)
    b = op(jnp.where(upper, x, fill), axis=1, keepdims=True)
    return jnp.where(upper, b, a)


def to_column(row, same, upper):
    return half_reduce(jnp.where(same, row, 0.0), upper, jnp.sum, 0.0)


def to_row(col, same):
    return jnp.sum(jnp.where(same, col, 0.0), axis=0, keepdims=True)


def pair_consts():
    lane = lax.broadcasted_iota(jnp.int32, (M, 128), 1)
    row = lax.broadcasted_iota(jnp.int32, (M, 128), 0)
    return lane >= E, row == lane % E, group_masks((M, 128), 2, bf16), group_masks((M, 128), 2, f32)


def own_pair(land_ref, i, own):
    me, _ = seq_place()
    per = land_ref.shape[2] // 128
    p = jnp.minimum(me * own + i, land_ref.shape[0] * per - 1)
    return land_ref[p // per, :, pl.ds(pl.multiple_of((p % per) * 128, 128), 128)]


def inverse_step(
    num_ref, stat_ref, ql_ref, kl_ref, mixed_ref, sum_ref, mid_ref, z_ref, p_ref, a_ref, w_ref,
    scale_ref, tot_ref, alpha_ref,
):
    ranks, own = num_ref.shape[:2]
    upper, same, masks, masks_wide = pair_consts()
    for i in range(own):
        peak = stat_ref[0, i : i + 1, :]
        for r in range(1, ranks):
            peak = jnp.maximum(peak, stat_ref[r, i : i + 1, :])
        total = jnp.zeros((1, 128), f32)
        numer = jnp.zeros((M, 128), f32)
        for r in range(ranks):
            alpha = jnp.exp(stat_ref[r, i : i + 1, :] - peak)
            total = total + alpha * stat_ref[r, 8 + i : 9 + i, :]
            column = to_column(alpha, same, upper)
            alpha_ref[r, i] = column
            numer = numer + column * num_ref[r, i].astype(f32)
        total = to_column(total, same, upper)
        tot_ref[i] = total
        sum_ref[i] = numer / total
        ql, kl = own_pair(ql_ref, i, own), own_pair(kl_ref, i, own)
        s2 = dot_nt(ql, block_diag(kl, masks))
        e2 = jnp.exp(s2 - half_reduce(s2, upper, jnp.max, -jnp.inf))
        middle = e2 / half_reduce(e2, upper, jnp.sum, 0.0)
        mid_ref[i] = middle
        st = dot_nt(kl, block_diag(ql, masks))
        et = jnp.exp(st - jnp.max(st, axis=0, keepdims=True))
        flipped = et / jnp.sum(et, axis=0, keepdims=True)
        column = jnp.sum(middle, axis=0, keepdims=True)
        scale = 1.0 / half_reduce(column, upper[0:1], jnp.max, -jnp.inf)
        scale_ref[i] = jnp.broadcast_to(scale, (8, 128))
        z_ref[0, i] = flipped * scale

    def step(it, carry):
        zs = [z_ref[it, i] for i in range(own)]
        ps = [pair_nn([mid_ref[i]], zs[i], masks)[0] for i in range(own)]
        second = [pair_nn([ps[i], zs[i]], ps[i], masks) for i in range(own)]
        for i in range(own):
            p2, a = second[i]
            w = 7.0 * ps[i] - p2
            p_ref[it, i] = ps[i]
            a_ref[it, i] = a
            w_ref[it, i] = w
            z_ref[it + 1, i] = 0.25 * (13.0 * zs[i] - 15.0 * a + pair_nn([a], w, masks)[0])
        return carry

    lax.fori_loop(0, NEWTON, step, 0)
    for i in range(own):
        mixed_ref[i] = pair_nn([z_ref[NEWTON, i]], sum_ref[i], masks)[0].astype(bf16)


def inverse_kernel(
    num_ref, stat_ref, ql_ref, kl_ref, cv_ref, rim_ref, f_ref, mixed_out, co_ref, sum_ref, mid_ref, z_ref, p_ref,
    a_ref, w_ref, scale_ref, tot_ref, alpha_ref, mixed, pad, taps, sems,
):
    step = pl.program_id(0)
    own = num_ref.shape[1]

    @pl.when(step == 0)
    def _():
        greet()
        inverse_step(
            num_ref, stat_ref, ql_ref, kl_ref, mixed, sum_ref, mid_ref, z_ref, p_ref, a_ref, w_ref, scale_ref,
            tot_ref, alpha_ref,
        )
        begin(spread_copies(mixed, mixed_out, own, sems))

    @pl.when(step > 0)
    def _():
        conv_tile(cv_ref, rim_ref, f_ref, co_ref, pad, taps)

    @pl.when(step == pl.num_programs(0) - 1)
    def _():
        finish(spread_copies(mixed, mixed_out, own, sems))


def inverse(num, stat, q_land, k_land, v, rim, taps, first_group):
    ranks, own = num.shape[:2]
    seqs, rows, features = v.shape
    groups = features // 128 - first_group
    mat = jax.ShapeDtypeStruct((own, M, 128), f32)
    steps = lambda n: jax.ShapeDtypeStruct((n, own, M, 128), f32)
    whole = lambda a: pl.BlockSpec(a.shape, lambda i: (0,) * len(a.shape), pipeline_mode=pl.Buffered(1))
    saved = [
        mat, mat, steps(NEWTON + 1), steps(NEWTON), steps(NEWTON), steps(NEWTON),
        jax.ShapeDtypeStruct((own, 8, 128), f32), mat, steps(ranks),
    ]
    cv, rims, ft, co = conv_specs(rows, 1, first_group, groups)
    return pl.pallas_call(
        inverse_kernel,
        grid=(1 + seqs * groups,),
        in_specs=[whole(num), whole(stat), whole(q_land), whole(k_land), cv, rims, ft],
        out_specs=[ANY, co] + [whole(a) for a in saved],
        out_shape=[
            jax.ShapeDtypeStruct((ranks * own, M, 128), bf16),
            jax.ShapeDtypeStruct((seqs, rows, 128 * groups), bf16),
        ]
        + saved,
        scratch_shapes=[
            pltpu.VMEM((own, M, 128), bf16), pltpu.VMEM((rows + 2 * RIM, 128), f32), pltpu.VMEM((40, 128), f32),
            rank_sems(),
        ],
        compiler_params=params(62 * MB, collective_id=2, has_side_effects=True),
        name="inverse",
    )(num, stat, q_land, k_land, v, rim, taps)


def inverse_back_step(
    land_ref, ql_ref, kl_ref, sum_ref, mid_ref, z_ref, p_ref, a_ref, w_ref, scale_ref, tot_ref,
    alpha_ref, gn_ref, gt_ref, mq_ref, mk_ref, g_ref, dk_ref,
):
    ranks, own = land_ref.shape[:2]
    upper, same, masks, masks_wide = pair_consts()
    for i in range(own):
        land = land_ref[0, i].astype(f32)
        for r in range(1, ranks):
            land = land + land_ref[r, i].astype(f32)
        summary, total = sum_ref[i], tot_ref[i]
        gs = pair_tn(z_ref[NEWTON, i], [land], masks_wide)[0].astype(bf16).astype(f32)
        gn = (gs / total).astype(bf16).astype(f32)
        gt = -half_reduce(gs * summary, upper, jnp.sum, 0.0) / total
        for r in range(ranks):
            gn_ref[r, i] = (alpha_ref[r, i] * gn).astype(bf16)
            gt_ref[r, i] = jnp.broadcast_to(to_row(alpha_ref[r, i] * gt, same), (8, 128))
        g_ref[i] = pair_nt([land], summary, masks)[0]
        dk_ref[i] = jnp.zeros((M, 128), f32)

    def step(back, carry):
        it = NEWTON - 1 - back
        gs = [g_ref[i] for i in range(own)]
        das, dws = [], []
        for i in range(own):
            das.append(0.25 * (pair_nt([gs[i]], w_ref[it, i], masks)[0] - 15.0 * gs[i]))
            dws.append(0.25 * pair_tn(a_ref[it, i], [gs[i]], masks_wide)[0])
        dps, parts = [], []
        for i in range(own):
            right = pair_nt([dws[i], das[i]], p_ref[it, i], masks)
            left = pair_tn(p_ref[it, i], [dws[i]], masks_wide)[0]
            dps.append(7.0 * dws[i] - right[0] - left + pair_tn(z_ref[it, i], [das[i]], masks_wide)[0])
            parts.append(3.25 * gs[i] + right[1])
        for i in range(own):
            g_ref[i] = parts[i] + pair_tn(mid_ref[i], [dps[i]], masks_wide)[0]
            dk_ref[i] += pair_nt([dps[i]], z_ref[it, i], masks)[0]
        return carry

    lax.fori_loop(0, NEWTON, step, 0)
    eye = jnp.where(same, 1.0, 0.0).astype(bf16)
    for i in range(own):
        g, middle, scale = g_ref[i], mid_ref[i], scale_ref[i, 0:1, :]
        turned = dot_tn(stack_parts([g], 1), eye)
        turned = diag_blocks(turned[:128] + turned[128:], masks_wide)
        column = jnp.sum(middle, axis=0, keepdims=True)
        top = half_reduce(column, upper[0:1], jnp.max, -jnp.inf)
        hit = jnp.where(column == top, 1.0, 0.0)
        share = hit / half_reduce(hit, upper[0:1], jnp.sum, 0.0)
        d_scale = half_reduce(jnp.sum(turned * middle, axis=0, keepdims=True), upper[0:1], jnp.sum, 0.0)
        dk = dk_ref[i] + turned * scale - share * (d_scale * scale * scale)
        ds = middle * (dk - half_reduce(middle * dk, upper, jnp.sum, 0.0))
        hi, lo = split(ds)
        both = dot(jnp.concatenate([hi, lo], axis=0), block_diag(own_pair(kl_ref, i, own), masks))
        mq_ref[i] = both[:M] + both[M:]
        turned = dot_tn(jnp.concatenate([hi, lo], axis=1), own_pair(ql_ref, i, own))
        mk_ref[i] = diag_blocks(turned[:128] + turned[128:], masks_wide)


def inverse_back(land, q_land, k_land, saved):
    ranks, own = land.shape[:2]
    mat = jax.ShapeDtypeStruct((own, M, 128), f32)
    return pl.pallas_call(
        inverse_back_step,
        out_shape=[
            jax.ShapeDtypeStruct((ranks, own, M, 128), bf16),
            jax.ShapeDtypeStruct((ranks, own, 8, 128), f32), mat, mat,
        ],
        scratch_shapes=[pltpu.VMEM((own, M, 128), f32)] * 2,
        compiler_params=params(62 * MB),
        name="inverse_back",
    )(land, q_land, k_land, *saved)


def mean_of(x):
    return jnp.mean(x, axis=-1, keepdims=True)


def gelu_and_slope(u):
    u = u.astype(bf16)
    low = lambda c: jnp.asarray(c, bf16)
    t = low(1.0) / (low(1.0) + low(ERFC_P * root_half) * jnp.abs(u))
    bell = jnp.exp2((u * u) * low(-0.5 * log2_e))
    poly = jnp.full_like(t, 0.5 * ERFC_C[-1])
    for c in ERFC_C[-2::-1]:
        poly = poly * t + low(0.5 * c)
    half = (poly * t) * bell
    cdf = jnp.where(u < 0, half, low(1.0) - half)
    return u * cdf, cdf + u * (bell * low(inv_root_two_pi))


def row_block(
    step, tok_ref, p_ref, conv_a_ref, conv_b_ref, mix_ref, top_ref, w_out_ref, w_up_ref, w_down_ref, ga_ref,
    gf_ref, out_ref, proj_ref, gm_ref, gains_ref, act, gul, slope, hid_t, gdl_t, mix_t, gpr, resid, whole,
):
    size, features = tok_ref.shape
    ff = act.shape[1]
    wide = features
    start = pl.multiple_of(step * size, size)
    rows = pl.ds(start, size)
    near = rows if whole else pl.ds(0, size)
    masks = group_masks((M, 4 * E), 4, bf16)
    for g in range(features // 256):
        sl = slice(256 * g, 256 * g + 256)
        att = dot_tn(p_ref[0, sl, :], block_diag(quad(mix_ref, g), masks))
        split_at = conv_a_ref.shape[1]
        ref, lane = (conv_a_ref, 256 * g) if 256 * g < split_at else (conv_b_ref, 256 * g - split_at)
        resid[:, sl] = (att + ref[:, lane : lane + 256].astype(f32)).astype(bf16)
    mixed = resid[...]
    mix_t[:, near] = mixed.T
    residual = tok_ref[...].astype(f32) + dot(mixed, w_out_ref[...])
    centre = residual - mean_of(residual)
    s_att = lax.rsqrt(mean_of(centre * centre) + epsilon)
    normed = centre * s_att
    gain_att = ga_ref[...].reshape(1, features)
    hidden = normed * gain_att
    hid_low = hidden.astype(bf16)
    hid_t[:, rows] = hid_low.T
    down = jnp.zeros((size, features), f32)
    for j in range(0, ff, wide):
        up = dot(hid_low, w_up_ref[:, j : j + wide])
        low, sl = gelu_and_slope(up)
        act[near, j : j + wide] = low
        slope[:, j : j + wide] = sl
        down = down + dot(low, w_down_ref[j : j + wide, :])
    residual_two = hidden + down
    centre_two = residual_two - mean_of(residual_two)
    s_ffn = lax.rsqrt(mean_of(centre_two * centre_two) + epsilon)
    normed_two = centre_two * s_ffn
    gain_ffn = gf_ref[...].reshape(1, features)
    out_ref[...] = (normed_two * gain_ffn).astype(bf16)
    top = top_ref[...].astype(f32)
    gains_ref[8:16, :] += (top * normed_two).reshape(size // 8, 8, features).sum(0)
    g = top * gain_ffn
    grad_two = s_ffn * (g - mean_of(g) - normed_two * mean_of(g * normed_two))
    gdl = grad_two.astype(bf16)
    gdl_t[:, near] = gdl.T
    back = jnp.zeros((size, features), f32)
    for j in range(0, ff, wide):
        gu = dot_nt(gdl, w_down_ref[j : j + wide, :]) * slope[:, j : j + wide].astype(f32)
        low = gu.astype(bf16)
        gul[rows, j : j + wide] = low
        back = back + dot_nt(low, w_up_ref[:, j : j + wide])
    grad_hidden = grad_two + back
    gains_ref[0:8, :] += (grad_hidden * normed).reshape(size // 8, 8, features).sum(0)
    g = grad_hidden * gain_att
    proj = (s_att * (g - mean_of(g) - normed * mean_of(g * normed))).astype(bf16)
    proj_ref[...] = proj
    if whole:
        gpr[rows, :] = proj
    gm_ref[...] = dot_nt(proj, w_out_ref[...]).astype(bf16)


def row_kernel(
    tok_ref, p_ref, conv_a_ref, conv_b_ref, mix_ref, top_ref, w_out_ref, w_up_ref, w_down_ref, ga_ref, gf_ref,
    out_ref, proj_ref, gm_ref, wg_ref, gains_ref,
    act, gul, slope, hid_t, gdl_t, mix_t, gpr, resid,
):
    step = pl.program_id(0)
    size, features = tok_ref.shape
    blocks = act.shape[0] // size
    ff = act.shape[1]
    wide = features

    @pl.when(step == 0)
    def _():
        gains_ref[...] = jnp.zeros_like(gains_ref)

    @pl.when(step < blocks)
    def _():
        row_block(
            step, tok_ref, p_ref, conv_a_ref, conv_b_ref, mix_ref, top_ref, w_out_ref, w_up_ref, w_down_ref,
            ga_ref, gf_ref, out_ref, proj_ref, gm_ref, gains_ref, act, gul, slope, hid_t, gdl_t, mix_t, gpr,
            resid, True,
        )

    chunks = ff // wide
    for first, left, right in ((0, hid_t, gul), (chunks, gdl_t, act), (2 * chunks, mix_t, gpr)):
        count = chunks if first < 2 * chunks else 1

        @pl.when((step >= blocks + first) & (step < blocks + first + count))
        def _(first=first, left=left, right=right):
            base = (step - blocks - first) * wide
            for c in range(0, wide, 256):
                cols = pl.ds(pl.multiple_of(base + c, 256), 256)
                wg_ref[0, :, c : c + 256] = dot(left[...], right[:, cols]).astype(bf16)


def row_pass(tokens, probs, conv_a, conv_b, mixed, grad_out, w_out, w_up, w_down, gain_att, gain_ffn):
    seqs, rows, features = tokens.shape
    ff = w_up.shape[1]
    size = min(256, rows)
    total = seqs * rows
    blocks = total // size
    grads = 2 * (ff // features) + 1
    here = lambda i: jnp.minimum(i, blocks - 1)
    block = pl.BlockSpec((size, features), lambda i: (here(i), 0))
    whole = lambda a: pl.BlockSpec(a.shape, lambda i: (0,) * a.ndim, pipeline_mode=pl.Buffered(1))
    flat = lambda a: a.reshape(total, a.shape[2])
    part = lambda a: pl.BlockSpec((size, a.shape[2]), lambda i: (here(i), 0))
    gains = [gain_att, gain_ffn]
    row_out = jax.ShapeDtypeStruct((total, features), bf16)
    tall = pltpu.VMEM((features, total), bf16)
    return pl.pallas_call(
        row_kernel,
        grid=(blocks + grads,),
        in_specs=[
            block, pl.BlockSpec((1, features, size), lambda i: (here(i) * size // rows, 0, here(i) % (rows // size))),
            part(conv_a), part(conv_b),
            pl.BlockSpec((features // 128, M, 128), lambda i: (here(i) * size // rows, 0, 0)),
            block, whole(w_out), whole(w_up), whole(w_down), whole(gains[0]), whole(gains[1]),
        ],
        out_specs=[block] * 3
        + [
            pl.BlockSpec((1, features, features), lambda i: (jnp.maximum(i - blocks, 0), 0, 0)),
            pl.BlockSpec((16, features), lambda i: (0, 0)),
        ],
        out_shape=[row_out] * 3
        + [
            jax.ShapeDtypeStruct((grads, features, features), bf16),
            jax.ShapeDtypeStruct((16, features), f32),
        ],
        scratch_shapes=[
            pltpu.VMEM((total, ff), bf16), pltpu.VMEM((total, ff), bf16), pltpu.VMEM((size, ff), bf16),
            tall, tall, tall, pltpu.VMEM((total, features), bf16), pltpu.VMEM((size, features), bf16),
        ],
        compiler_params=params(62 * MB),
        name="row_pass",
    )(flat(tokens), probs, flat(conv_a), flat(conv_b), mixed, flat(grad_out), w_out, w_up, w_down, *gains)


def row_share_kernel(
    tok_ref, p_ref, conv_a_ref, conv_b_ref, mix_ref, top_ref, w_out_ref, w_up_ref, w_down_ref, ga_ref, gf_ref,
    out_ref, proj_ref, gm_ref, gains_ref, act_ref, gdl_t_ref, mix_t_ref, g_out, rim_out,
    gul, slope, hid_t, resid, rim, parts, got, sums, send, recv, out_sem, rim_send, rim_recv,
):
    step = pl.program_id(0)
    size, features = tok_ref.shape
    blocks = gul.shape[0] // size
    seqs = rim.shape[0]
    per = blocks // seqs
    chunks = gul.shape[1] // features
    me, count = seq_place()
    core, _, _, sibling, _, _ = cube()
    half = features // 2

    @pl.when(step == 0)
    def _():
        gains_ref[...] = jnp.zeros_like(gains_ref)
        greet([sibling])

    def rim_copy(s, side):
        there = lax.rem(me + (1 if side == 0 else count - 1), count)
        return remote(
            rim.at[s, side], rim_out.at[s, side], rim_send.at[s, side], rim_recv.at[s, side], {"seq": there}
        )

    @pl.when(step < blocks)
    def _():
        row_block(
            step, tok_ref, p_ref, conv_a_ref, conv_b_ref, mix_ref, top_ref, w_out_ref, w_up_ref, w_down_ref,
            ga_ref, gf_ref, out_ref, proj_ref, gm_ref, gains_ref, act_ref, gul, slope, hid_t, gdl_t_ref,
            mix_t_ref, None, resid, False,
        )
        s = step // per

        @pl.when(step % per == 0)
        def _():
            rim[s, 1] = gm_ref[:RIM, :]
            rim_copy(s, 1).start()

        @pl.when(step % per == per - 1)
        def _():
            rim[s, 0] = gm_ref[size - RIM :, :]
            rim_copy(s, 0).start()

    j = step - blocks
    slot = lax.rem(jnp.maximum(j, 0), 2)

    def share(at):
        return remote(parts.at[at % 2, 1 - core], got.at[at], send.at[at], recv.at[at], sibling)

    def out_copy(at):
        return pltpu.make_async_copy(sums.at[at % 2], g_out.at[at], out_sem.at[at % 2])

    @pl.when((j >= 2) & (j < chunks))
    def _():
        share(j - 2).wait_send()

    @pl.when((j >= 0) & (j < chunks))
    def _():
        for c in range(0, features, 256):
            cols = pl.ds(pl.multiple_of(j * features + c, 256), 256)
            low = dot(hid_t[...], gul[:, cols]).astype(bf16)
            for l in range(0, 256, 128):
                side, lane = (c + l) // half, (c + l) % half
                for d in range(8):
                    parts[slot, d % 2, d // 2, 96 * side : 96 * side + 96, lane : lane + 128] = low[
                        96 * d : 96 * d + 96, l : l + 128
                    ]
        share(j).start()

    done = j - 1

    @pl.when(done >= 2)
    def _():
        out_copy(done - 2).wait()

    @pl.when(done >= 0)
    def _():
        share(done).wait_recv()
        sums[done % 2] = add_low(parts[done % 2, core], got[done])
        out_copy(done).start()

    @pl.when(done == chunks - 1)
    def _():
        share(done - 1).wait_send()
        share(done).wait_send()
        out_copy(done - 1).wait()
        out_copy(done).wait()

        def rims(s, carry):
            for side in range(2):
                rim_copy(s, side).wait()
            return carry

        lax.fori_loop(0, seqs, rims, 0)


def row_share(tokens, probs, conv_a, conv_b, mixed, grad_out, w_out, w_up, w_down, gain_att, gain_ffn):
    seqs, rows, features = tokens.shape
    ff = w_up.shape[1]
    size = min(256, rows)
    total = seqs * rows
    blocks = total // size
    chunks = ff // features
    here = lambda i: jnp.minimum(i, blocks - 1)
    block = pl.BlockSpec((size, features), lambda i: (here(i), 0))
    turned = pl.BlockSpec((features, size), lambda i: (0, here(i)))
    whole = lambda a: pl.BlockSpec(a.shape, lambda i: (0,) * a.ndim, pipeline_mode=pl.Buffered(1))
    flat = lambda a: a.reshape(total, a.shape[2])
    part = lambda a: pl.BlockSpec((size, a.shape[2]), lambda i: (here(i), 0))
    gains = [gain_att, gain_ffn]
    row_out = jax.ShapeDtypeStruct((total, features), bf16)
    turned_out = jax.ShapeDtypeStruct((features, total), bf16)
    dma = pltpu.SemaphoreType.DMA
    return pl.pallas_call(
        row_share_kernel,
        grid=(blocks + chunks + 1,),
        in_specs=[
            block, pl.BlockSpec((1, features, size), lambda i: (here(i) * size // rows, 0, here(i) % (rows // size))),
            part(conv_a), part(conv_b),
            pl.BlockSpec((features // 128, M, 128), lambda i: (here(i) * size // rows, 0, 0)),
            block, whole(w_out), whole(w_up), whole(w_down), whole(gains[0]), whole(gains[1]),
        ],
        out_specs=[block] * 3
        + [
            pl.BlockSpec((16, features), lambda i: (0, 0)), pl.BlockSpec((size, ff), lambda i: (here(i), 0)),
            turned, turned, ANY, ANY,
        ],
        out_shape=[row_out] * 3
        + [
            jax.ShapeDtypeStruct((16, features), f32), jax.ShapeDtypeStruct((total, ff), bf16),
            turned_out, turned_out, jax.ShapeDtypeStruct((chunks, 4, 192, 384), bf16),
            jax.ShapeDtypeStruct((seqs, 2, RIM, features), bf16),
        ],
        scratch_shapes=[
            pltpu.VMEM((total, ff), bf16), pltpu.VMEM((size, ff), bf16), pltpu.VMEM((features, total), bf16),
            pltpu.VMEM((size, features), bf16), pltpu.VMEM((seqs, 2, RIM, features), bf16),
            pltpu.VMEM((2, 2, 4, 192, 384), bf16), pltpu.VMEM((chunks, 4, 192, 384), bf16),
            pltpu.VMEM((2, 4, 192, 384), bf16),
            dma((chunks,)), dma((chunks,)), dma((2,)), dma((seqs, 2)), dma((seqs, 2)),
        ],
        compiler_params=params(62 * MB, collective_id=3, has_side_effects=True),
        name="row_share",
    )(flat(tokens), probs, flat(conv_a), flat(conv_b), mixed, flat(grad_out), w_out, w_up, w_down, *gains)


def first_back_step(gm_ref, p_ref, q_ref, mix_ref, kl_of, put_land, gq_ref, put_klp):
    features = gm_ref.shape[2]
    masks = group_masks((M, 4 * E), 4, bf16)
    masks_wide = group_masks((M, 4 * E), 4, f32)
    for g in range(features // 256):
        sl = slice(256 * g, 256 * g + 256)
        gm, p = gm_ref[0, :, sl], p_ref[0, sl, :]
        put_land(g, diag_blocks(dot(p, gm), masks_wide).astype(bf16))
        d = dot_nt(block_diag(quad(mix_ref, g), masks), gm)
        parts = []
        for h in range(4):
            pw = p[E * h : E * h + E].astype(f32)
            dh = d[E * h : E * h + E]
            parts.append((pw * (dh - jnp.sum(pw * dh, axis=0, keepdims=True))).astype(bf16))
        gs = jnp.concatenate(parts, axis=0)
        gq_ref[0, :, sl] = dot_tn(gs, block_diag(kl_of(sl), masks)).astype(bf16)
        put_klp(g, diag_blocks(dot(gs, q_ref[0, :, sl]), masks_wide))


def first_back_kernel(gm_ref, p_ref, q_ref, mix_ref, kl_ref, land_ref, gq_ref, klp_ref):
    def put_land(g, x):
        for i in range(2):
            land_ref[2 * g + i] = x[:, 128 * i : 128 * i + 128]

    def put_klp(g, x):
        klp_ref[0, :, 256 * g : 256 * g + 256] = x

    first_back_step(gm_ref, p_ref, q_ref, mix_ref, lambda sl: kl_ref[0, :, sl], put_land, gq_ref, put_klp)


def first_back(gm, probs, q, mixed, k_land):
    seqs, rows, features = q.shape
    pairs = features // 128
    full = pl.BlockSpec((1, rows, features), lambda s: (s, 0, 0))
    land = pl.BlockSpec((1, M, features), lambda s: (s, 0, 0))
    return pl.pallas_call(
        first_back_kernel,
        grid=(seqs,),
        in_specs=[full, pl.BlockSpec((1, features, rows), lambda s: (s, 0, 0)), full, pl.BlockSpec((pairs, M, 128), lambda s: (s, 0, 0)), land],
        out_specs=[pl.BlockSpec((pairs, M, 128), lambda s: (s, 0, 0)), full, land],
        out_shape=[
            jax.ShapeDtypeStruct((seqs * pairs, M, 128), bf16),
            jax.ShapeDtypeStruct(q.shape, bf16),
            jax.ShapeDtypeStruct((seqs, M, features), f32),
        ],
        compiler_params=params(62 * MB),
        name="first_back",
    )(gm, probs, q, mixed, k_land)


def third_back_kernel(w_ref, v_ref, k_ref, gc_ref, gn_ref, gt_ref, ql_ref, gv_ref, gk_ref, qlp_ref):
    features = w_ref.shape[2]
    masks = group_masks((M, 4 * E), 4, bf16)
    masks_wide = group_masks((M, 4 * E), 4, f32)
    for g in range(features // 256):
        sl = slice(256 * g, 256 * g + 256)
        w = w_ref[0, :, sl]
        gn = jnp.concatenate([gn_ref[2 * g], gn_ref[2 * g + 1]], axis=1)
        gt = jnp.concatenate([gt_ref[2 * g, 0:1, :], gt_ref[2 * g + 1, 0:1, :]], axis=1)
        gd = block_diag(gn, masks)
        gs = (w.astype(f32) * (dot_nt(v_ref[0, :, sl], gd) + gt)).astype(bf16)
        gv_ref[0, :, sl] = (dot(w, gd) + gc_ref[0, :, sl].astype(f32)).astype(bf16)
        gk_ref[0, :, sl] = dot(gs, block_diag(ql_ref[0, :, sl], masks)).astype(bf16)
        qlp_ref[0, :, sl] = diag_blocks(dot_tn(gs, k_ref[0, :, sl]), masks_wide)


def third_back(w, v, k, grad_conv, gn, gt, q_land):
    seqs, rows, features = v.shape
    pairs = features // 128
    full = pl.BlockSpec((1, rows, features), lambda s: (s, 0, 0))
    land = pl.BlockSpec((1, M, features), lambda s: (s, 0, 0))
    return pl.pallas_call(
        third_back_kernel,
        grid=(seqs,),
        in_specs=[full] * 4
        + [
            pl.BlockSpec((pairs, M, 128), lambda s: (s, 0, 0)),
            pl.BlockSpec((pairs, 8, 128), lambda s: (s, 0, 0)),
            land,
        ],
        out_specs=[full, full, land],
        out_shape=[jax.ShapeDtypeStruct(v.shape, bf16)] * 2
        + [jax.ShapeDtypeStruct((seqs, M, features), f32)],
        compiler_params=params(62 * MB),
        name="third_back",
    )(w, v, k, grad_conv, gn, gt, q_land)


def last_kernel(tok_ref, gq_ref, gk_ref, gv_ref, qo_ref, ko_ref, proj_ref, w_ref, gt_ref, wg_ref, d, tok_t):
    step = pl.program_id(0)
    seqs = tok_t.shape[1] // tok_ref.shape[1]
    rows, features = tok_ref.shape[1:]
    marks = qo_ref.shape[1]
    seg = rows // marks

    @pl.when(step < seqs)
    def _():
        here = pl.ds(pl.multiple_of(step * rows, rows), rows)
        for part, (core, own) in enumerate(((gq_ref, qo_ref), (gk_ref, ko_ref))):
            for m in range(marks):
                at = pl.ds(pl.multiple_of(step * rows + m * seg, seg), seg)
                x = core[0, m * seg : m * seg + seg, :].astype(f32) + own[0, m : m + 1, :] * (1.0 / seg)
                x = x.astype(bf16)
                if part == 0:
                    x = x * jnp.asarray(0.125, bf16)
                d[at, part * features : part * features + features] = x
        d[here, 2 * features :] = gv_ref[0]
        tok_t[:, here] = tok_ref[0].T
        for c in range(0, rows, 128):
            at = pl.ds(pl.multiple_of(step * rows + c, 128), 128)
            gt_ref[0, c : c + 128, :] = (
                proj_ref[0, c : c + 128, :].astype(f32) + dot_nt(d[at, :], w_ref[...])
            ).astype(bf16)

    @pl.when(step >= seqs)
    def _():
        base = (step - seqs) * features
        for c in range(0, features, 256):
            cols = pl.ds(pl.multiple_of(base + c, 256), 256)
            wg_ref[0, :, c : c + 256] = dot(tok_t[...], d[:, cols]).astype(bf16)


def last_pass(tokens, gq, gk, gv, q_own, k_own, proj, w_qkv):
    seqs, rows, features = tokens.shape
    marks = q_own.shape[1]
    here = lambda i: jnp.minimum(i, seqs - 1)
    full = pl.BlockSpec((1, rows, features), lambda i: (here(i), 0, 0))
    land = pl.BlockSpec((1, marks, features), lambda i: (here(i), 0, 0))
    return pl.pallas_call(
        last_kernel,
        grid=(seqs + 3,),
        in_specs=[full] * 4 + [land] * 2
        + [full, pl.BlockSpec(w_qkv.shape, lambda i: (0, 0), pipeline_mode=pl.Buffered(1))],
        out_specs=[full, pl.BlockSpec((1, features, features), lambda i: (jnp.maximum(i - seqs, 0), 0, 0))],
        out_shape=[
            jax.ShapeDtypeStruct(tokens.shape, bf16),
            jax.ShapeDtypeStruct((3, features, features), bf16),
        ],
        scratch_shapes=[
            pltpu.VMEM((seqs * rows, 3 * features), bf16), pltpu.VMEM((features, seqs * rows), bf16),
        ],
        compiler_params=params(62 * MB),
        name="last_pass",
    )(tokens, gq, gk, gv, q_own, k_own, proj, w_qkv)


def add_pairs(dst, own, start, pairs):
    for i in range(own.shape[0]):
        @pl.when(start + i < pairs)
        def _(i=i):
            dst[start + i] += own[i]


def cross_copies(src, got, sems):
    _, x, y, _, along_x, along_y = cube()
    return [
        remote(src.at[0:2, :, 1 - x], got.at[0], sems.at[0, 0], sems.at[1, 0], along_x),
        remote(src.at[2:4, 1 - y], got.at[1], sems.at[0, 1], sems.at[1, 1], along_y),
    ]


def kept_copies(src, kept, sems):
    _, x, y, _, _, _ = cube()
    return [
        pltpu.make_async_copy(src.at[0:2, :, x], kept.at[0], sems.at[0]),
        pltpu.make_async_copy(src.at[2:4, y], kept.at[1], sems.at[1]),
    ]


def turn_copies(kept, got, sems):
    _, x, y, _, along_x, along_y = cube()
    return [
        remote(kept.at[0, :, 1 - y], got.at[0], sems.at[0, 0], sems.at[1, 0], along_y),
        remote(kept.at[1, :, 1 - x], got.at[1], sems.at[0, 1], sems.at[1, 1], along_x),
    ]


def cross_add(kept, got):
    for half in range(2):
        for rank in range(2):
            kept[half, rank] = add_low(kept[half, rank], got[half, rank])


def turn_add(out, kept, got):
    _, x, y, _, _, _ = cube()
    for half, place in ((0, y), (1, x)):
        for rank in range(2):
            out[2 * half + rank] = add_low(kept[half, rank, place], got[half, rank])


def stage_scratch(rows):
    dma = pltpu.SemaphoreType.DMA
    return [
        pltpu.VMEM((2, 2, 2, rows, 384), bf16), pltpu.VMEM((2, 2, 2, rows, 384), bf16),
        pltpu.VMEM((2, 2, rows, 384), bf16), dma((2,)), dma((2, 2)), dma((2, 2)),
    ]


def down_first_kernel(
    act_ref, gdl_t_ref, mix_t_ref, proj_ref, gm_ref, p_ref, q_ref, mix_ref, marks_ref, cg_ref, rim_ref, cv_ref,
    f_ref, up_in,
    gq_ref, klp_ref, co_ref, gf_ref, up_ref, g_out, land_out,
    parts, got, sums, land, pad, facc, taps, kept, crossed, turned, kept_sems, cross_sems, turn_sems,
    send, recv, out_sem, last_sem, land_sems,
):
    step = pl.program_id(0)
    steps = pl.num_programs(0)
    features = q_ref.shape[2]
    pairs = features // 128
    seqs = klp_ref.shape[0] // pairs
    own = land_out.shape[1]
    core, _, _, sibling, along_x, along_y = cube()
    half = features // 2
    chunks = 4
    first = chunks + 1
    conv = first + seqs
    cross = cross_copies(up_in, crossed, cross_sems)
    keep = kept_copies(up_in, kept, kept_sems)
    turn = turn_copies(kept, turned, turn_sems)

    @pl.when(step == 0)
    def _():
        greet([sibling, along_x, along_y])
        for copy in cross + keep:
            copy.start()
        if land.shape[0] > seqs * pairs:
            land[seqs * pairs :] = jnp.zeros_like(land[seqs * pairs :])

    slot = lax.rem(step, 2)

    def share(at):
        return remote(parts.at[at % 2, 1 - core], got.at[at], send.at[at], recv.at[at], sibling)

    def down_copy(at):
        return pltpu.make_async_copy(sums.at[at % 2], g_out.at[:, at, 0:192, :], out_sem.at[at % 2])

    def out_copy(z):
        return pltpu.make_async_copy(
            sums.at[0, :, 48 * z : 48 * z + 48, :], g_out.at[z, :, 192:240, :], last_sem.at[z]
        )

    @pl.when((step >= 2) & (step <= chunks))
    def _():
        share(step - 2).wait_send()

    @pl.when(step < chunks)
    def _():
        for c in range(0, features, 256):
            low = dot(gdl_t_ref[...], act_ref[:, c : c + 256]).astype(bf16)
            for l in range(0, 256, 128):
                side, lane = (c + l) // half, (c + l) % half
                for z in range(4):
                    parts[slot, side, z, :, lane : lane + 128] = low[192 * z : 192 * z + 192, l : l + 128]
        share(step).start()

    @pl.when(step == chunks)
    def _():
        for c in range(2):
            low = dot(mix_t_ref[...], proj_ref[:, half * c : half * c + half]).astype(bf16)
            for zz in range(2):
                z = 2 * c + zz
                for d in range(8):
                    block = low[96 * d : 96 * d + 96, 192 * zz : 192 * zz + 192]
                    parts[slot, d % 2, d // 2, 48 * z : 48 * z + 48, :] = jnp.concatenate(
                        [block[:48], block[48:]], axis=1
                    )
        share(step).start()

    done = step - 1

    @pl.when((done >= 2) & (done <= chunks))
    def _():
        down_copy(done - 2).wait()

    @pl.when((done >= 0) & (done <= chunks))
    def _():
        share(done).wait_recv()
        sums[done % 2] = add_low(parts[done % 2, core], got[done])

    @pl.when((done >= 0) & (done < chunks))
    def _():
        down_copy(done).start()

    @pl.when(done == chunks)
    def _():
        for z in range(4):
            out_copy(z).start()

    @pl.when((step >= first) & (step < conv))
    def _():
        seq = step - first

        def put_land(g, v):
            for i in range(2):
                land[seq * pairs + 2 * g + i] = v[:, 128 * i : 128 * i + 128]

        def put_klp(g, v):
            for i in range(2):
                klp_ref[seq * pairs + 2 * g + i] = v[:, 128 * i : 128 * i + 128]

        first_back_step(
            gm_ref, p_ref, q_ref, mix_ref, lambda sl: marks_ref[0, :, sl], put_land, gq_ref, put_klp
        )

    @pl.when(step == conv - 1)
    def _():
        begin(swap_copies(land, land_out, own, land_sems))

    @pl.when(step == conv)
    def _():
        for copy in cross + keep:
            copy.wait()
        cross_add(kept, crossed)
        for copy in turn:
            copy.start()

    @pl.when(step >= conv)
    def _():
        seq = (step - conv) % seqs
        conv_back_tile(seq, seqs, cg_ref, rim_ref, cv_ref, f_ref, co_ref, gf_ref, pad, facc, taps)

    @pl.when(step == steps - 1)
    def _():
        for copy in turn:
            copy.wait()
        turn_add(up_ref, kept, turned)
        share(chunks - 1).wait_send()
        share(chunks).wait_send()
        down_copy(chunks - 1).wait()
        for z in range(4):
            out_copy(z).wait()
        finish(swap_copies(land, land_out, own, land_sems))


def down_first(act, gdl_t, mix_t, proj, gm, probs, q, mixed, k_land, rim, v, taps, ups, own, groups):
    seqs, rows, features = q.shape
    total, ff = act.shape
    ranks = lax.axis_size("seq")
    pairs = features // 128
    chunks = ff // features
    first = chunks + 1
    here = lambda i: jnp.clip(i - first, 0, seqs - 1)
    full = pl.BlockSpec((1, rows, features), lambda i: (here(i), 0, 0))
    whole = lambda a: pl.BlockSpec(a.shape, lambda i: (0,) * len(a.shape), pipeline_mode=pl.Buffered(1))
    cv, rims, ft, co, go = conv_back_specs(rows, seqs, first + seqs, 0)
    up_sum = jax.ShapeDtypeStruct((4, 192, 384), bf16)
    dma = pltpu.SemaphoreType.DMA
    return pl.pallas_call(
        down_first_kernel,
        grid=(first + seqs + seqs * groups,),
        in_specs=[
            pl.BlockSpec((total, features), lambda i: (0, jnp.minimum(i, chunks - 1))),
            whole(gdl_t), whole(mix_t), whole(proj), full,
            pl.BlockSpec((1, features, rows), lambda i: (here(i), 0, 0)), full,
            pl.BlockSpec((pairs, M, 128), lambda i: (here(i), 0, 0)),
            pl.BlockSpec((1, M, features), lambda i: (here(i), 0, 0)),
            cv, rims, cv, ft, ANY,
        ],
        out_specs=[full, pl.BlockSpec((seqs * pairs, M, 128), lambda i: (0, 0, 0)), co, go, whole(up_sum), ANY, ANY],
        out_shape=[
            jax.ShapeDtypeStruct(q.shape, bf16),
            jax.ShapeDtypeStruct((seqs * pairs, M, 128), f32),
            jax.ShapeDtypeStruct((seqs, rows, 128 * groups), bf16),
            jax.ShapeDtypeStruct((KW, 128 * groups), f32),
            up_sum,
            jax.ShapeDtypeStruct((4, 4, 240, 384), bf16),
            jax.ShapeDtypeStruct((ranks, own, M, 128), bf16),
        ],
        scratch_shapes=[
            pltpu.VMEM((2, 2, 4, 192, 384), bf16), pltpu.VMEM((chunks + 1, 4, 192, 384), bf16),
            pltpu.VMEM((2, 4, 192, 384), bf16), pltpu.VMEM((ranks * own, M, 128), bf16),
            pltpu.VMEM((rows + 2 * RIM, 128), f32), pltpu.VMEM((KW * 8, 128), f32), pltpu.VMEM((40, 128), f32),
        ]
        + stage_scratch(192)
        + [dma((chunks + 1,)), dma((chunks + 1,)), dma((2,)), dma((4,)), rank_sems()],
        compiler_params=params(62 * MB, collective_id=4, has_side_effects=True),
        name="down_first",
    )(act, gdl_t, mix_t, proj, gm, probs, q, mixed, k_land, gm, rim, v, taps, ups)


def inverse_conv_kernel(
    late, land_ref, ql_ref, kl_ref, sum_ref, mid_ref, z_ref, p_ref, a_ref, w_ref, scale_ref, tot_ref, alpha_ref, klp_ref,
    cg_ref, rim_ref, cv_ref, f_ref, down_in, up_in,
    mq_ref, co_ref, gf_ref, down_ref, gn_out, gt_out, kl_out, up_out,
    gn, gt, gt_low, mk, g_acc, dk_acc, kl, pad, facc, taps, kept, crossed, turned, kept_sems, cross_sems, turn_sems,
    gn_sems, gt_sems, kl_sems, up_sems,
):
    step = pl.program_id(0)
    ranks, own = land_ref.shape[:2]
    me, _ = seq_place()
    marks = kl_out.shape[2]
    seqs = ql_ref.shape[0]
    _, _, _, _, along_x, along_y = cube()
    cross = cross_copies(down_in, crossed, cross_sems)
    keep = kept_copies(down_in, kept, kept_sems)
    turn = turn_copies(kept, turned, turn_sems)

    def mark_copies():
        sends = [
            remote(
                kl.at[:, pl.ds(peer * marks, marks)], kl_out.at[me], kl_sems.at[0, o], kl_sems.at[1, o],
                {"seq": peer},
            )
            for o, peer in seq_peers()
        ]
        return sends, pltpu.make_async_copy(
            kl.at[:, pl.ds(me * marks, marks)], kl_out.at[me], kl_sems.at[0, 0]
        )

    exchanges = [swap_rows(gn, gn_out, gn_sems), swap_rows(gt_low, gt_out, gt_sems), mark_copies()]
    ups = swap_rows(up_in, up_out, up_sems)

    @pl.when(step == 0)
    def _():
        greet([along_x, along_y])
        for copy in cross + keep:
            copy.start()
        begin(ups)
        inverse_back_step(
            land_ref, ql_ref, kl_ref, sum_ref, mid_ref, z_ref, p_ref, a_ref, w_ref, scale_ref, tot_ref, alpha_ref,
            gn, gt, mq_ref, mk, g_acc, dk_acc,
        )
        for r in range(ranks):
            gt_low[r] = jnp.concatenate(
                [gt[r, i, 0:1, :] for i in range(own)] + [jnp.zeros((8 - own, 128), f32)], axis=0
            )
        add_pairs(klp_ref, mk, me * own, klp_ref.shape[0])
        kl[...] = klp_ref[...].astype(bf16)
        for pair in exchanges:
            begin(pair)

    @pl.when(step == late)
    def _():
        for copy in cross + keep:
            copy.wait()
        cross_add(kept, crossed)
        for copy in turn:
            copy.start()

    @pl.when(step > 0)
    def _():
        conv_back_tile((step - 1) % seqs, seqs, cg_ref, rim_ref, cv_ref, f_ref, co_ref, gf_ref, pad, facc, taps)

    @pl.when(step == pl.num_programs(0) - 1)
    def _():
        for copy in turn:
            copy.wait()
        turn_add(down_ref, kept, turned)
        for pair in exchanges:
            finish(pair)
        finish(ups)


def inverse_conv(land_parts, q_land, k_land, saved, klp, gm, rim, v, taps, downs, ups, first_group):
    ranks, own = land_parts.shape[:2]
    seqs, rows, features = v.shape
    pairs = features // 128 * seqs
    groups = features // 128 - first_group
    marks = M // ranks
    mat = jax.ShapeDtypeStruct((own, M, 128), f32)
    down_sum = jax.ShapeDtypeStruct((4, 240, 384), bf16)
    whole = lambda a: pl.BlockSpec(a.shape, lambda i: (0,) * len(a.shape), pipeline_mode=pl.Buffered(1))
    cv, rims, ft, co, go = conv_back_specs(rows, seqs, 1, first_group)
    return pl.pallas_call(
        functools.partial(inverse_conv_kernel, 7),
        grid=(1 + seqs * groups,),
        in_specs=[whole(land_parts), whole(q_land), whole(k_land)]
        + [whole(a) for a in saved]
        + [whole(klp), cv, rims, cv, ft, ANY, ANY],
        out_specs=[whole(mat), co, go, whole(down_sum)] + [ANY] * 4,
        out_shape=[
            mat,
            jax.ShapeDtypeStruct((seqs, rows, 128 * groups), bf16),
            jax.ShapeDtypeStruct((KW, 128 * groups), f32),
            down_sum,
            jax.ShapeDtypeStruct((ranks, own, M, 128), bf16),
            jax.ShapeDtypeStruct((ranks, 8, 128), f32),
            jax.ShapeDtypeStruct((ranks, pairs, marks, 128), bf16),
            jax.ShapeDtypeStruct(ups.shape, bf16),
        ],
        scratch_shapes=[
            pltpu.VMEM((ranks, own, M, 128), bf16), pltpu.VMEM((ranks, own, 8, 128), f32),
            pltpu.VMEM((ranks, 8, 128), f32),
            pltpu.VMEM((own, M, 128), f32), pltpu.VMEM((own, M, 128), f32), pltpu.VMEM((own, M, 128), f32),
            pltpu.VMEM((pairs, M, 128), bf16), pltpu.VMEM((rows + 2 * RIM, 128), f32),
            pltpu.VMEM((KW * 8, 128), f32), pltpu.VMEM((40, 128), f32),
        ]
        + stage_scratch(240)
        + [rank_sems(), rank_sems(), rank_sems(), rank_sems()],
        compiler_params=params(62 * MB, collective_id=5, has_side_effects=True),
        name="inverse_conv",
    )(land_parts, q_land, k_land, *saved, klp, gm, rim, v, taps, downs, ups)


def third_step(w_ref, v_ref, k_ref, conv_of, gn_of, gt_of, ql_of, put_v, put_k, put_qlp):
    features = w_ref.shape[2]
    masks = group_masks((M, 4 * E), 4, bf16)
    masks_wide = group_masks((M, 4 * E), 4, f32)
    for g in range(features // 256):
        sl = slice(256 * g, 256 * g + 256)
        w = w_ref[0, :, sl]
        gd = block_diag(jnp.concatenate([gn_of(2 * g), gn_of(2 * g + 1)], axis=1), masks)
        gt = jnp.concatenate([gt_of(2 * g), gt_of(2 * g + 1)], axis=1)
        gs = (w.astype(f32) * (dot_nt(v_ref[0, :, sl], gd) + gt)).astype(bf16)
        put_v(g, (dot(w, gd) + conv_of(g)).astype(bf16))
        put_k(g, dot(gs, block_diag(ql_of(sl), masks)))
        put_qlp(g, diag_blocks(dot_tn(gs, k_ref[0, :, sl]), masks_wide))


def final_kernel(
    w_ref, v_ref, k_ref, tok_ref, ca_ref, cb_ref, gn_ref, gt_ref, marks_ref, gq_ref, kl_ref, mq_ref, proj_ref,
    wq_ref, ta_ref, tb_ref, gains_ref, up_ref, down_in,
    gtok_ref, up_out, down_out, out_out, qkv_out, taps_out, ga_out, gf_out,
    d, tok_t, qlp, qlow, qgot, part, got_a, sum_a, got_b, sum_b, got_c, sum_c, got_z, down,
    sm_got, sm_sum, q_sems, z_sems, late_sems, a_send, a_recv, b_sems, c_sems, zq_send, zq_recv, s_send, s_recv,
    s_sems,
):
    step = pl.program_id(0)
    rows, features = tok_ref.shape[1:]
    seqs = gq_ref.shape[0]
    pairs = features // 128
    ranks, marks = kl_ref.shape[0], kl_ref.shape[2]
    own = mq_ref.shape[0]
    seg = rows // marks
    last = pl.num_programs(0) - 1
    me, _ = seq_place()
    core, x, y, sibling, along_x, along_y = cube()

    def z_copies(rows_of, sems):
        sends = [
            remote(down_in.at[peer, rows_of], down.at[me, rows_of], sems.at[0, o], sems.at[1, o], {"seq": peer})
            for o, peer in seq_peers()
        ]
        return sends, pltpu.make_async_copy(down_in.at[me, rows_of], down.at[me, rows_of], sems.at[0, 0])

    early = z_copies(pl.ds(0, 96), z_sems)
    late = z_copies(pl.ds(96, 144), late_sems)

    def q_copies():
        sends = [
            remote(
                qlow.at[:, pl.ds(peer * marks, marks)], qgot.at[me], q_sems.at[0, o], q_sems.at[1, o],
                {"seq": peer},
            )
            for o, peer in seq_peers()
        ]
        return sends, pltpu.make_async_copy(
            qlow.at[:, pl.ds(me * marks, marks)], qgot.at[me], q_sems.at[0, 0]
        )

    def a_copy(p):
        return remote(
            part.at[1 - core, pl.ds(4 * p, 4)], got_a.at[pl.ds(4 * p, 4)], a_send.at[p], a_recv.at[p], sibling
        )

    def b_copies(p):
        return [
            remote(
                sum_a.at[4 * p : 4 * p + 2, :, 1 - x], got_b.at[p, 0], b_sems.at[0, p, 0], b_sems.at[1, p, 0],
                along_x,
            ),
            remote(
                sum_a.at[4 * p + 2 : 4 * p + 4, 1 - y], got_b.at[p, 1], b_sems.at[0, p, 1], b_sems.at[1, p, 1],
                along_y,
            ),
        ]

    def c_copies(p):
        return [
            remote(
                sum_b.at[p, 0, :, 1 - y], got_c.at[p, 0], c_sems.at[0, p, 0], c_sems.at[1, p, 0], along_y
            ),
            remote(
                sum_b.at[p, 1, :, 1 - x], got_c.at[p, 1], c_sems.at[0, p, 1], c_sems.at[1, p, 1], along_x
            ),
        ]

    def zq_copy(group):
        rank, place = group // 3, group % 3
        offset = lax.rem(rank - me + ranks, ranks)
        return rank, remote(
            sum_c.at[group], got_z.at[me, place], zq_send.at[group], zq_recv.at[place, offset], {"seq": rank}
        )

    def stage_b(p):
        a_copy(p).wait()
        for yx in range(4):
            sum_a[4 * p : 4 * p + 4, yx // 2, yx % 2] = add_low(
                part[core, 4 * p : 4 * p + 4, yx], got_a[4 * p : 4 * p + 4, yx]
            )
        for copy in b_copies(p):
            copy.start()

    def stage_c(p):
        for copy in b_copies(p):
            copy.wait()
        sum_b[p, 0] = add_low(sum_a[4 * p : 4 * p + 2, :, x], got_b[p, 0])
        sum_b[p, 1] = add_low(sum_a[4 * p + 2 : 4 * p + 4, y], got_b[p, 1])
        for copy in c_copies(p):
            copy.start()

    def stage_z(p):
        for copy in c_copies(p):
            copy.wait()
        sum_c[4 * p : 4 * p + 2] = add_low(sum_b[p, 0, :, y], got_c[p, 0])
        sum_c[4 * p + 2 : 4 * p + 4] = add_low(sum_b[p, 1, :, x], got_c[p, 1])
        for group in range(4 * p, 4 * p + 4):
            rank, copy = zq_copy(group)

            @pl.when(rank != me)
            def _(copy=copy):
                copy.start()

    small_copies = [
        remote(sm_sum.at[i], sm_got.at[i], s_send.at[i], s_recv.at[i], target)
        for i, target in enumerate((sibling, along_x, along_y))
    ]

    def small_spread():
        return [
            remote(sm_sum.at[3], sm_got.at[3 + me], s_sems.at[0, o], s_sems.at[1, o], {"seq": peer})
            for o, peer in seq_peers()
        ]

    @pl.when(step == 0)
    def _():
        greet([sibling, along_x, along_y])
        begin(early)
        sm_sum[0, KW:, :] = jnp.zeros_like(sm_sum[0, KW:, :])
        split_at = ta_ref.shape[1]
        sm_sum[0, :KW, :split_at] = ta_ref[...]
        sm_sum[0, :KW, split_at:] = tb_ref[...]
        for i in range(2):
            sm_sum[0, KW + i : KW + i + 1, :] = jnp.sum(gains_ref[8 * i : 8 * i + 8, :], axis=0, keepdims=True)
        small_copies[0].start()
        up = up_ref[0].astype(f32)
        for r in range(1, ranks):
            up = up + up_ref[r].astype(f32)
        up_out[:, :384] = up[:96]
        up_out[:, 384:] = up[96:]

    for i in range(1, 4):
        @pl.when(step == i)
        def _(i=i):
            small_copies[i - 1].wait()
            sm_sum[i] = sm_sum[i - 1] + sm_got[i - 1]
            if i < 3:
                small_copies[i].start()
            else:
                for copy in small_spread():
                    copy.start()

    def land_rows(of):
        total = of(0).astype(f32)
        for r in range(1, ranks):
            total = total + of(r).astype(f32)
        return total * (1.0 / seg)

    @pl.when(step < seqs)
    def _():
        start = step * rows

        def conv_of(g):
            half = ca_ref.shape[2]
            at = 256 * g
            pieces = []
            for l in (at, at + 128):
                ref, lane = (ca_ref, l) if l < half else (cb_ref, l - half)
                pieces.append(ref[0, :, lane : lane + 128].astype(f32))
            return jnp.concatenate(pieces, axis=1)

        def gt_of(i):
            p = step * pairs + i
            return gt_ref[p // own, pl.ds(p % own, 1), :]

        def gn_of(i):
            p = step * pairs + i
            return gn_ref[p // own, p % own]

        def put_v(g, val):
            d[pl.ds(pl.multiple_of(start, rows), rows), 2 * features + 256 * g : 2 * features + 256 * g + 256] = val

        def put_k(g, val):
            for i in range(2):
                p = step * pairs + 2 * g + i
                spread = land_rows(lambda r: kl_ref[r, p])
                lane = features + 256 * g + 128 * i
                for m in range(marks):
                    at = pl.ds(pl.multiple_of(start + m * seg, seg), seg)
                    d[at, lane : lane + 128] = (
                        val[m * seg : m * seg + seg, 128 * i : 128 * i + 128] + spread[m : m + 1]
                    ).astype(bf16)

        def put_qlp(g, val):
            for i in range(2):
                qlp[step * pairs + 2 * g + i] = val[:, 128 * i : 128 * i + 128]

        third_step(
            w_ref, v_ref, k_ref, conv_of, gn_of, gt_of, lambda sl: marks_ref[0, :, sl], put_v, put_k, put_qlp
        )
        tok_t[:, pl.ds(pl.multiple_of(start, rows), rows)] = tok_ref[0].T

    @pl.when(step == seqs - 1)
    def _():
        add_pairs(qlp, mq_ref, me * own, seqs * pairs)
        qlow[...] = qlp[...].astype(bf16)
        begin(q_copies())

    @pl.when(step == seqs + 2)
    def _():
        stage_b(2)
        finish(q_copies())
        begin(late)

        def fill(s, carry):
            for g in range(pairs):
                spread = land_rows(lambda r: qgot[r, s * pairs + g])
                for m in range(marks):
                    at = pl.ds(pl.multiple_of(s * rows + m * seg, seg), seg)
                    val = gq_ref[s, m * seg : m * seg + seg, 128 * g : 128 * g + 128].astype(f32)
                    low = (val + spread[m : m + 1]).astype(bf16) * jnp.asarray(0.125, bf16)
                    d[at, 128 * g : 128 * g + 128] = low
            return carry

        lax.fori_loop(0, seqs, fill, 0)

    for at, stages in (
        (seqs + 3, [(stage_b, 1)]),
        (seqs + 4, [(stage_b, 0)]),
        (seqs + 5, [(stage_c, 2)]),
        (seqs + 7, [(stage_z, 2)]),
        (seqs + 8, [(stage_c, 1)]),
    ):
        @pl.when(step == at)
        def _(stages=stages):
            for stage, p in stages:
                stage(p)

    @pl.when((step >= seqs) & (step < seqs + 3))
    def _():
        p = seqs + 2 - step
        for c in range(2):
            cols = pl.ds(pl.multiple_of(p * features + 384 * c, 128), 384)
            low = dot(tok_t[...], d[:, cols]).astype(bf16)
            for i in range(2):
                for dd in range(8):
                    block = low[96 * dd : 96 * dd + 96, 192 * i : 192 * i + 192]
                    part[dd % 2, 4 * p + 2 * c + i, dd // 2] = jnp.concatenate([block[:48], block[48:]], axis=1)
        a_copy(p).start()

    @pl.when((step >= seqs + 3) & (step < last))
    def _():
        size = gtok_ref.shape[0]
        start = (step - seqs - 3) * size
        for c in range(0, size, 128):
            at = pl.ds(pl.multiple_of(start + c, 128), 128)
            gtok_ref[c : c + 128, :] = (
                proj_ref[c : c + 128, :].astype(f32) + dot_nt(d[at, :], wq_ref[...])
            ).astype(bf16)

    def unfold(block):
        return jnp.concatenate([block[:, :192], block[:, 192:]], axis=0)

    @pl.when(step == last)
    def _():
        stage_z(1)
        stage_c(0)
        for copy in small_spread():
            copy.wait()
        sm_got[3 + me] = sm_sum[3]
        small = (sm_got[3] + sm_got[4]) + (sm_got[5] + sm_got[6])
        taps_out[...] = small[:KW]
        ga_out[...] = small[KW : KW + 1].reshape(features)
        gf_out[...] = small[KW + 1 : KW + 2].reshape(features)
        finish(early)
        finish(late)
        total = down[0].astype(f32)
        for r in range(1, ranks):
            total = total + down[r].astype(f32)
        down_out[...] = total[:192].T
        out_out[...] = unfold(total[192:240])
        stage_z(0)
        for group in range(12):
            rank, copy = zq_copy(group)

            @pl.when(rank != me)
            def _(copy=copy):
                copy.wait_send()

        for o in range(1, ranks):
            source = lax.rem(me - o + ranks, ranks)
            for place in range(3):
                remote(
                    sum_c.at[0], got_z.at[source, place], zq_send.at[0], zq_recv.at[place, o], {"seq": source}
                ).wait_recv()
        for place in range(3):
            got_z[me, place] = sum_c[3 * me + place]
        shares = []
        for place in range(3):
            total = got_z[0, place].astype(f32)
            for r in range(1, ranks):
                total = total + got_z[r, place].astype(f32)
            shares.append(unfold(total))
        qkv_out[...] = jnp.concatenate(shares, axis=1)


def final_pass(
    weights, v, k, tokens, conv_a, conv_b, gn, gt, q_land, gq, kl_parts, mid_q, proj, w_qkv, taps_a, taps_b, gains, ups,
    downs,
):
    seqs, rows, features = tokens.shape
    ranks = lax.axis_size("seq")
    pairs = features // 128 * seqs
    marks = M // ranks
    total = seqs * rows
    size = 256
    blocks = total // size
    here = lambda i: jnp.minimum(i, seqs - 1)
    late = lambda i: jnp.clip(i - seqs - 3, 0, blocks - 1)
    full = lambda a: pl.BlockSpec((1, rows, a.shape[2]), lambda i: (here(i), 0, 0))
    later = pl.BlockSpec((size, features), lambda i: (late(i), 0))
    whole = lambda a: pl.BlockSpec(a.shape, lambda i: (0,) * len(a.shape), pipeline_mode=pl.Buffered(1))
    vm = lambda *shape: pltpu.VMEM(shape, bf16)
    dma = pltpu.SemaphoreType.DMA
    shares = [jax.ShapeDtypeStruct(s, f32) for s in ((96, 768), (384, 192), (96, 192), (96, 576), (KW, 768), (768,), (768,))]
    return pl.pallas_call(
        final_kernel,
        grid=(seqs + 3 + blocks + 1,),
        in_specs=[full(weights), full(v), full(k), full(tokens), full(conv_a), full(conv_b), whole(gn), whole(gt)]
        + [pl.BlockSpec((1, M, features), lambda i: (here(i), 0, 0)), whole(gq), whole(kl_parts), whole(mid_q)]
        + [later, whole(w_qkv), whole(taps_a), whole(taps_b), whole(gains), whole(ups), ANY],
        out_specs=[later] + [whole(a) for a in shares],
        out_shape=[jax.ShapeDtypeStruct((total, features), bf16)]
        + shares,
        scratch_shapes=[
            vm(total, 3 * features), vm(features, total), pltpu.VMEM((pairs, M, 128), f32),
            vm(pairs, M, 128), vm(ranks, pairs, marks, 128), vm(2, 12, 4, 48, 384), vm(12, 4, 48, 384),
            vm(12, 2, 2, 48, 384), vm(3, 2, 2, 2, 48, 384), vm(3, 2, 2, 2, 48, 384), vm(3, 2, 2, 48, 384),
            vm(12, 48, 384), vm(ranks, 3, 48, 384), vm(ranks, 240, 384),
            pltpu.VMEM((3 + ranks, 40, features), f32), pltpu.VMEM((4, 40, features), f32),
            rank_sems(), rank_sems(), rank_sems(), dma((3,)), dma((3,)), dma((2, 3, 2)), dma((2, 3, 2)),
            dma((12,)), dma((3, ranks)), dma((3,)), dma((3,)), rank_sems(),
        ],
        compiler_params=params(62 * MB, collective_id=6, has_side_effects=True),
        name="final_pass",
    )(
        weights, v, k, tokens, conv_a, conv_b, gn, gt, q_land, gq, kl_parts, mid_q, proj, w_qkv, taps_a, taps_b,
        gains, ups, downs,
    )


def halo(cells, width):
    count = lax.axis_size("seq")
    head, tail = cells[:, :width], cells[:, cells.shape[1] - width :]
    left = lax.ppermute(tail, "seq", [(i, i + 1) for i in range(count - 1)])
    right = lax.ppermute(head, "seq", [(i + 1, i) for i in range(count - 1)])
    return jnp.stack([left, right], axis=1)


def scatter_sum(grad):
    share = lax.psum_scatter(grad, "dp", scatter_dimension=0, tiled=True)
    return lax.psum_scatter(share, "seq", scatter_dimension=1, tiled=True).astype(f32)


def per_device_general(tokens, w_qkv, w_out, w_up, w_down, conv_filter, gain_att, gain_ffn, grad_out):
    seqs, rows, features = tokens.shape
    ranks = lax.axis_size("seq")
    rank = lax.axis_index("seq")
    marks = M // ranks
    ff = w_up.shape[1]
    pairs = seqs * (features // 128)
    own = -(-pairs // ranks)

    def from_pairs(x):
        x = x[:pairs].reshape(seqs, features // 128, M, 128).transpose(0, 2, 1, 3)
        return x.reshape(seqs, M, features)

    def pad_pairs(x):
        return jnp.pad(x, ((0, ranks * own - pairs),) + ((0, 0),) * (x.ndim - 1))

    def exchange(x):
        out = lax.all_to_all(pad_pairs(x), "seq", 0, 0, tiled=True)
        return out.reshape((ranks, own) + x.shape[1:])

    taps = conv_filter
    q, k, v, k_part, q_land, v_rim = project(tokens, w_qkv, marks)
    first_group = 4
    weights, probs, k_land, conv_a, num_parts, stat_parts = scores(
        q, k, v, q_land, k_part, v_rim, taps, own, first_group
    )
    mixed_pairs, conv_b, *saved = inverse(num_parts, stat_parts, q_land, k_land, v, v_rim, taps, first_group)
    mixed = mixed_pairs
    layer_out, proj, gm, wg, gains = row_pass(
        tokens, probs, conv_a, conv_b, mixed, grad_out, w_out, w_up, w_down, gain_att, gain_ffn
    )
    shape3 = (seqs, rows, features)
    gm = gm.reshape(shape3)
    chunks = ff // features
    up_share = scatter_sum(wg[:chunks].transpose(1, 0, 2).reshape(features, ff))
    down_share = scatter_sum(wg[chunks : 2 * chunks].transpose(0, 2, 1).reshape(ff, features))
    out_share = scatter_sum(wg[2 * chunks])
    land_part, gq, k_land_part = first_back(gm, probs, q, mixed, k_land)
    g_rim = halo(gm, RIM)
    land_parts = exchange(land_part)
    grad_conv, taps_grad = conv_back(gm, g_rim, v, taps)
    gn_own, gt_own, mid_q, mid_k = inverse_back(land_parts, q_land, k_land, saved)

    def give_back(x):
        x = x.reshape((ranks * own,) + x.shape[2:])
        return lax.all_to_all(x, "seq", 0, 0, tiled=True)[:pairs]

    grad_values, gk, q_land_part = third_back(
        weights, v, k, grad_conv, give_back(gn_own), give_back(gt_own), q_land
    )

    def place(x):
        full = jnp.zeros((ranks * own, M, 128), f32)
        return from_pairs(lax.dynamic_update_slice_in_dim(full, x, rank * own, 0))

    both = jnp.stack([q_land_part + place(mid_q), k_land_part + place(mid_k)]).astype(bf16)
    both = both.reshape(2, seqs, ranks, marks, features).transpose(2, 0, 1, 3, 4)
    both = lax.all_to_all(both, "seq", 0, 0, tiled=True).astype(f32).sum(0)
    grad_tokens, qkv_grad = last_pass(tokens, gq, gk, grad_values, both[0], both[1], proj.reshape(shape3), w_qkv)
    qkv_share = scatter_sum(qkv_grad.transpose(1, 0, 2).reshape(features, 3 * features))
    gains = gains.reshape(2, 8, features).sum(1)
    small = lax.psum(jnp.concatenate([taps_grad, gains]), ("dp", "seq"))
    return (
        layer_out.reshape(shape3),
        grad_tokens,
        qkv_share,
        out_share,
        up_share,
        down_share,
        small[:KW],
        small[KW],
        small[KW + 1],
    )


def per_device(tokens, w_qkv, w_out, w_up, w_down, conv_filter, gain_att, gain_ffn, grad_out):
    seqs, rows, features = tokens.shape
    ranks = lax.axis_size("seq")
    marks = M // ranks
    pairs = seqs * (features // 128)
    own = -(-pairs // ranks)
    taps = conv_filter
    half = 4
    shape3 = (seqs, rows, features)

    q, k, v, k_part, q_land, v_rim = project(tokens, w_qkv, marks)
    weights, probs, k_land, conv_a, num_parts, stat_parts = scores(q, k, v, q_land, k_part, v_rim, taps, own, half)
    mixed, conv_b, *saved = inverse(num_parts, stat_parts, q_land, k_land, v, v_rim, taps, half)
    layer_out, proj, gm, gains, act, gdl_t, mix_t, ups, g_rim = row_share(
        tokens, probs, conv_a, conv_b, mixed, grad_out, w_out, w_up, w_down, gain_att, gain_ffn
    )
    gm = gm.reshape(shape3)
    early = 2
    gq, klp, gconv_a, taps_a, ups, downs, land_parts = down_first(
        act, gdl_t, mix_t, proj, gm, probs, q, mixed, k_land, g_rim, v, taps, ups.reshape(4, 2, 2, 192, 384), own,
        early,
    )
    mid_q, gconv_b, taps_b, downs, gn, gt, kl_parts, ups = inverse_conv(
        land_parts, q_land, k_land, saved, klp, gm, g_rim, v, taps, downs.reshape(4, 2, 2, 240, 384), ups, early
    )
    grad_tokens, up, down, out, qkv, taps_all, gain_att_all, gain_ffn_all = final_pass(
        weights, v, k, tokens, gconv_a, gconv_b, gn, gt, q_land, gq, kl_parts, mid_q, proj, w_qkv, taps_a, taps_b,
        gains, ups, downs,
    )
    return (
        layer_out.reshape(shape3),
        grad_tokens.reshape(shape3),
        qkv,
        out,
        up,
        down,
        taps_all,
        gain_att_all,
        gain_ffn_all,
    )


def solution(mesh):
    placed = (P("dp", "seq", None), P(), P(), P(), P(), P(), P(), P(), P("dp", "seq", None))
    eight_by_four = mesh.shape["dp"] == 8 and mesh.shape["seq"] == 4
    return jax.shard_map(
        per_device if eight_by_four else per_device_general,
        mesh=mesh,
        in_specs=placed,
        out_specs=(
            P("dp", "seq", None),
            P("dp", "seq", None),
            P("dp", "seq"),
            P("dp", "seq"),
            P("dp", "seq"),
            P("dp", "seq"),
            P(),
            P(),
            P(),
        ),
        check_vma=False,
    )
```

```python
import functools

import jax
import jax.numpy as jnp
from jax import lax
from jax.experimental import pallas as pl
from jax.experimental.pallas import tpu as pltpu
from jax.sharding import PartitionSpec as P

H = 12
E = 64
M = 64
KW = 33
RIM = KW // 2
NEWTON = 6

f32 = jnp.float32
bf16 = jnp.bfloat16
epsilon = 1e-05
root_half = 0.7071067811865476
inv_root_two_pi = 0.3989422804014327
MB = 1 << 20

ERFC_P = 0.6
ERFC_C = (0.37028039425845705, 0.14043533559747823, 0.7278464793107866, -0.23856251479455173)
log2_e = 1.4426950408889634


def dot(a, b):
    return lax.dot_general(a, b, (((1,), (0,)), ((), ())), preferred_element_type=f32)


def dot_nt(a, b):
    return lax.dot_general(a, b, (((1,), (1,)), ((), ())), preferred_element_type=f32)


def dot_tn(a, b):
    return lax.dot_general(a, b, (((0,), (0,)), ((), ())), preferred_element_type=f32)


def lane_group(shape):
    return lax.broadcasted_iota(jnp.int32, shape, len(shape) - 1) // E


def group_masks(shape, count, dtype):
    groups = lane_group(shape)
    return [(groups == h).astype(f32).astype(dtype) for h in range(count)]


def block_diag(x, masks):
    return jnp.concatenate([x * m for m in masks], axis=0)


def diag_blocks(n, masks):
    return sum(n[E * h : E * h + E] * m for h, m in enumerate(masks))


def quad(ref, g):
    return jnp.concatenate([ref[2 * g], ref[2 * g + 1]], axis=1)


def params(limit=None, **kw):
    return pltpu.CompilerParams(vmem_limit_bytes=limit, **kw)


MESH = pl.DeviceIdType.MESH
ANY = pl.BlockSpec(memory_space=pl.ANY)


def seq_place():
    return lax.axis_index("seq"), lax.axis_size("seq")


def seq_peers():
    me, count = seq_place()
    return [(o, lax.rem(me + o, count)) for o in range(1, count)]


def greet(extra=()):
    barrier = pltpu.get_barrier_semaphore()
    targets = [{"seq": peer} for _, peer in seq_peers()] + list(extra)
    for target in targets:
        pl.semaphore_signal(barrier, inc=1, device_id=target, device_id_type=MESH)
    pl.semaphore_wait(barrier, len(targets))


def remote(src, dst, send, recv, target):
    return pltpu.make_async_remote_copy(
        src_ref=src, dst_ref=dst, send_sem=send, recv_sem=recv, device_id=target, device_id_type=MESH
    )


def swap_copies(src, dst, own, sems):
    me, count = seq_place()
    copies = [
        remote(src.at[pl.ds(peer * own, own)], dst.at[me], sems.at[0, o], sems.at[1, o], {"seq": peer})
        for o, peer in seq_peers()
    ]
    return copies, pltpu.make_async_copy(src.at[pl.ds(me * own, own)], dst.at[me], sems.at[0, 0])


def spread_copies(src, dst, own, sems):
    me, count = seq_place()
    at = dst.at[pl.ds(me * own, own)]
    copies = [
        remote(src, at, sems.at[0, o], sems.at[1, o], {"seq": peer}) for o, peer in seq_peers()
    ]
    return copies, pltpu.make_async_copy(src, at, sems.at[0, 0])


def begin(pair):
    for copy in pair[0]:
        copy.start()
    pair[1].start()


def finish(pair):
    for copy in pair[0]:
        copy.wait()
    pair[1].wait()


def swap_rows(src, dst, sems):
    me, _ = seq_place()
    copies = [
        remote(src.at[peer], dst.at[me], sems.at[0, o], sems.at[1, o], {"seq": peer}) for o, peer in seq_peers()
    ]
    return copies, pltpu.make_async_copy(src.at[me], dst.at[me], sems.at[0, 0])


def cube():
    d = lax.axis_index("dp")
    core, x, y = d % 2, (d // 2) % 2, d // 4
    return core, x, y, {"dp": d + 1 - 2 * core}, {"dp": d + 2 - 4 * x}, {"dp": d + 4 - 8 * y}


def add_low(a, b):
    return (a.astype(f32) + b.astype(f32)).astype(bf16)


def rank_sems():
    return pltpu.SemaphoreType.DMA((2, lax.axis_size("seq")))


def project_kernel(
    tok_ref, w_ref, q_ref, k_ref, v_ref, kl_ref, land_out, rim_out, land, rim, send, recv, local, rim_send, rim_recv,
    rim_local,
):
    step = pl.program_id(0)
    seqs = pl.num_programs(0)
    me, count = seq_place()
    rows, features = tok_ref.shape[1:]
    marks = land.shape[1]
    seg = rows // marks

    @pl.when(step == 0)
    def _():
        greet()

    x = tok_ref[0]
    for part, out in enumerate((q_ref, k_ref, v_ref)):
        for c in range(0, features, 256):
            p = dot(x, w_ref[:, part * features + c : part * features + c + 256])
            if part == 0:
                p = 0.125 * p
            low = p.astype(bf16)
            out[0, :, c : c + 256] = low
            if part < 2:
                total = low.astype(f32).reshape(marks, seg, 256).sum(1)
                mean = (total * (1.0 / seg)).astype(bf16)
                if part == 0:
                    land[step, :, c : c + 256] = mean
                else:
                    kl_ref[0, :, c : c + 256] = mean
            else:
                rim[step, 0, :, c : c + 256] = low[rows - RIM :]
                rim[step, 1, :, c : c + 256] = low[:RIM]

    def copies(s):
        spot = land_out.at[s, pl.ds(me * marks, marks)]
        sends = [
            remote(land.at[s], spot, send.at[s, o], recv.at[s, o], {"seq": peer}) for o, peer in seq_peers()
        ]
        return sends, pltpu.make_async_copy(land.at[s], spot, local.at[s])

    def rim_copy(s, side):
        there = lax.rem(me + (1 if side == 0 else count - 1), count)
        return remote(
            rim.at[s, side], rim_out.at[s, side], rim_send.at[s, side], rim_recv.at[s, side], {"seq": there}
        )

    begin(copies(step))
    for side in range(2):
        rim_copy(step, side).start()

    @pl.when(step == seqs - 1)
    def _():
        def drain(s, carry):
            finish(copies(s))
            for side in range(2):
                rim_copy(s, side).wait()
            return carry

        lax.fori_loop(0, seqs, drain, 0)


def project(tokens, w_qkv, marks):
    seqs, rows, features = tokens.shape
    ranks = lax.axis_size("seq")
    full = pl.BlockSpec((1, rows, features), lambda s: (s, 0, 0))
    dma = pltpu.SemaphoreType.DMA
    return pl.pallas_call(
        project_kernel,
        grid=(seqs,),
        in_specs=[full, pl.BlockSpec(w_qkv.shape, lambda s: (0, 0), pipeline_mode=pl.Buffered(1))],
        out_specs=[full] * 3 + [pl.BlockSpec((1, marks, features), lambda s: (s, 0, 0))] + [ANY] * 2,
        out_shape=[jax.ShapeDtypeStruct(tokens.shape, bf16)] * 3
        + [
            jax.ShapeDtypeStruct((seqs, marks, features), bf16),
            jax.ShapeDtypeStruct((seqs, M, features), bf16),
            jax.ShapeDtypeStruct((seqs, 2, RIM, features), bf16),
        ],
        scratch_shapes=[
            pltpu.VMEM((seqs, marks, features), bf16), pltpu.VMEM((seqs, 2, RIM, features), bf16),
            dma((seqs, ranks)), dma((seqs, ranks)), dma((seqs,)), dma((seqs, 2)), dma((seqs, 2)), dma((seqs,)),
        ],
        compiler_params=params(62 * MB, collective_id=0, has_side_effects=True),
        name="project",
    )(tokens, w_qkv)


def fill_taps(taps, f_ref):
    taps[0:KW, :] = f_ref[...].astype(f32)


def fill_pad(pad, x_ref, rim_ref):
    rows = x_ref.shape[1]
    me, count = seq_place()
    pad[0:RIM, :] = jnp.where(me > 0, rim_ref[0, 0].astype(f32), 0.0)
    pad[RIM : RIM + rows, :] = x_ref[0].astype(f32)
    pad[RIM + rows : RIM + rows + RIM, :] = jnp.where(me < count - 1, rim_ref[0, 1].astype(f32), 0.0)


def conv_tile(v_ref, rim_ref, taps_ref, o_ref, pad, f_ref):
    rows = v_ref.shape[1]
    fill_pad(pad, v_ref, rim_ref)
    fill_taps(f_ref, taps_ref)
    conv_rows(o_ref, pad, f_ref, rows)


def conv_rows(o_ref, pad, f_ref, rows):
    for c in range(0, rows, 64):
        acc = jnp.zeros((64, 128), f32)
        for j in range(KW):
            acc = acc + f_ref[j : j + 1, :] * pad[c + j : c + j + 64, :]
        o_ref[0, c : c + 64, :] = acc.astype(bf16)


def conv_specs(rows, first_step, first_group, groups):
    at = lambda i: jnp.maximum(i - first_step, 0)
    seq = lambda i: at(i) // groups
    group = lambda i: at(i) % groups
    return (
        pl.BlockSpec((1, rows, 128), lambda i: (seq(i), 0, first_group + group(i))),
        pl.BlockSpec((1, 2, RIM, 128), lambda i: (seq(i), 0, 0, first_group + group(i))),
        pl.BlockSpec((KW, 128), lambda i: (0, first_group + group(i))),
        pl.BlockSpec((1, rows, 128), lambda i: (seq(i), 0, group(i))),
    )


def conv_back_rows(seq, seqs, g_ref, rim_ref, v_ref, taps_ref, put, put_taps, pad, facc, f_ref):
    rows = v_ref.shape[1]
    fill_pad(pad, g_ref, rim_ref)
    fill_taps(f_ref, taps_ref)

    @pl.when(seq == 0)
    def _():
        facc[...] = jnp.zeros_like(facc)

    for c in range(0, rows, 64):
        acc = jnp.zeros((64, 128), f32)
        vals = v_ref[0, c : c + 64, :].astype(f32)
        for j in range(KW):
            moved = pad[c + 2 * RIM - j : c + 2 * RIM - j + 64, :]
            acc = acc + f_ref[j : j + 1, :] * moved
            facc[8 * j : 8 * j + 8, :] += (vals * moved).reshape(8, 8, 128).sum(0)
        put(c, acc.astype(bf16))

    @pl.when(seq == seqs - 1)
    def _():
        put_taps(facc[...].reshape(KW, 8, 128).sum(1))


def conv_back_tile(seq, seqs, g_ref, rim_ref, v_ref, taps_ref, o_ref, gf_ref, pad, facc, f_ref):
    def put(c, v):
        o_ref[0, c : c + 64, :] = v

    def put_taps(v):
        gf_ref[...] = v

    conv_back_rows(seq, seqs, g_ref, rim_ref, v_ref, taps_ref, put, put_taps, pad, facc, f_ref)


def conv_back_kernel(g_ref, rim_ref, v_ref, f_ref, o_ref, gf_ref, pad, facc, taps):
    conv_back_tile(
        pl.program_id(1), pl.num_programs(1), g_ref, rim_ref, v_ref, f_ref, o_ref, gf_ref, pad, facc, taps
    )


def conv_back_specs(rows, seqs, first_step, first_group):
    at = lambda i: jnp.maximum(i - first_step, 0)
    seq = lambda i: at(i) % seqs
    group = lambda i: at(i) // seqs
    return (
        pl.BlockSpec((1, rows, 128), lambda i: (seq(i), 0, first_group + group(i))),
        pl.BlockSpec((1, 2, RIM, 128), lambda i: (seq(i), 0, 0, first_group + group(i))),
        pl.BlockSpec((KW, 128), lambda i: (0, first_group + group(i))),
        pl.BlockSpec((1, rows, 128), lambda i: (seq(i), 0, group(i))),
        pl.BlockSpec((KW, 128), lambda i: (0, group(i))),
    )


def conv_back(g, rim, v, taps):
    seqs, rows, features = v.shape
    sp = lambda n: pl.BlockSpec((1, n, 128), lambda g, s: (s, 0, g))
    fs = pl.BlockSpec((KW, 128), lambda g, s: (0, g))
    return pl.pallas_call(
        conv_back_kernel,
        grid=(features // 128, seqs),
        in_specs=[sp(rows), pl.BlockSpec((1, 2, RIM, 128), lambda g, s: (s, 0, 0, g)), sp(rows), fs],
        out_specs=[sp(rows), fs],
        out_shape=[jax.ShapeDtypeStruct(v.shape, bf16), jax.ShapeDtypeStruct((KW, features), f32)],
        scratch_shapes=[pltpu.VMEM((rows + 2 * RIM, 128), f32), pltpu.VMEM((KW * 8, 128), f32), pltpu.VMEM((40, 128), f32)],
        name="conv_back",
    )(g, rim, v, taps)


def third_score_step(step, k_ref, v_ref, ql_ref, w_ref, num_ref, stat_ref, own):
    features = k_ref.shape[2]
    pairs = features // 128
    masks = group_masks((M, 4 * E), 4, bf16)
    masks_wide = group_masks((M, 4 * E), 4, f32)
    for g in range(features // 256):
        sl = slice(256 * g, 256 * g + 256)
        s3 = dot_nt(k_ref[0, :, sl], block_diag(ql_ref[0, :, sl], masks))
        peak = jnp.max(s3, axis=0, keepdims=True)
        e3 = jnp.exp(s3 - peak)
        total = jnp.sum(e3, axis=0, keepdims=True)
        low = e3.astype(bf16)
        w_ref[0, :, sl] = low
        num = diag_blocks(dot_tn(low, v_ref[0, :, sl]), masks_wide).astype(bf16)
        for i in range(2):
            lanes = slice(128 * i, 128 * i + 128)
            p = step * pairs + 2 * g + i
            num_ref[p] = num[:, lanes]
            stat_ref[p // own, pl.ds(p % own, 1), :] = peak[:, lanes]
            stat_ref[p // own, pl.ds(8 + p % own, 1), :] = total[:, lanes]


def first_score_step(q_ref, kl, p_ref):
    features = q_ref.shape[2]
    masks = group_masks((M, 4 * E), 4, bf16)
    for g in range(features // 256):
        sl = slice(256 * g, 256 * g + 256)
        s1 = dot_nt(block_diag(kl[:, sl], masks), q_ref[0, :, sl])
        for h in range(4):
            x = s1[E * h : E * h + E]
            e1 = jnp.exp(x - jnp.max(x, axis=0, keepdims=True))
            at = 256 * g + E * h
            p_ref[0, at : at + E, :] = (e1 * (1.0 / jnp.sum(e1, axis=0, keepdims=True))).astype(bf16)


def scores_kernel(
    seqs, own, q_ref, k_ref, v_ref, ql_ref, kp_ref, cv_ref, rim_ref, f_ref, w_ref, p_ref, kl_ref, co_ref, num_out,
    stat_out, num, stat, kl, pad, taps, num_sems, stat_sems, kl_sems,
):
    step = pl.program_id(0)
    steps = pl.num_programs(0)
    pairs = q_ref.shape[2] // 128
    marks = kp_ref.shape[1]
    me, _ = seq_place()

    def mark_copies():
        spot = kl.at[:, pl.ds(me * marks, marks)]
        sends = [
            remote(kp_ref, spot, kl_sems.at[0, o], kl_sems.at[1, o], {"seq": peer}) for o, peer in seq_peers()
        ]
        return sends, pltpu.make_async_copy(kp_ref, spot, kl_sems.at[0, 0])

    @pl.when(step == 0)
    def _():
        greet()
        begin(mark_copies())
        stat[...] = jnp.zeros_like(stat)
        if num.shape[0] > seqs * pairs:
            num[seqs * pairs :] = jnp.zeros_like(num[seqs * pairs :])

    @pl.when(step < seqs)
    def _():
        third_score_step(step, k_ref, v_ref, ql_ref, w_ref, num, stat, own)

    @pl.when(step == seqs - 1)
    def _():
        begin(swap_copies(num, num_out, own, num_sems))
        begin(swap_rows(stat, stat_out, stat_sems))

    @pl.when(step == seqs)
    def _():
        finish(mark_copies())
        kl_ref[...] = kl[...]

    @pl.when((step >= seqs) & (step < 2 * seqs))
    def _():
        first_score_step(q_ref, kl[step - seqs], p_ref)

    @pl.when(step >= 2 * seqs)
    def _():
        conv_tile(cv_ref, rim_ref, f_ref, co_ref, pad, taps)

    @pl.when(step == steps - 1)
    def _():
        finish(swap_copies(num, num_out, own, num_sems))
        finish(swap_rows(stat, stat_out, stat_sems))


def scores(q, k, v, q_land, k_part, rim, taps, own, groups):
    seqs, rows, features = q.shape
    marks = k_part.shape[1]
    ranks = lax.axis_size("seq")
    here = lambda i: jnp.minimum(i, seqs - 1)
    then = lambda i: jnp.clip(i - seqs, 0, seqs - 1)
    full = pl.BlockSpec((1, rows, features), lambda i: (here(i), 0, 0))
    next_full = pl.BlockSpec((1, rows, features), lambda i: (then(i), 0, 0))
    whole = lambda a: pl.BlockSpec(a.shape, lambda i: (0,) * len(a.shape), pipeline_mode=pl.Buffered(1))
    k_land = jax.ShapeDtypeStruct((seqs, M, features), bf16)
    cv, rims, ft, co = conv_specs(rows, 2 * seqs, 0, groups)
    return pl.pallas_call(
        functools.partial(scores_kernel, seqs, own),
        grid=(2 * seqs + seqs * groups,),
        in_specs=[
            next_full, full, full, pl.BlockSpec((1, M, features), lambda i: (here(i), 0, 0)), whole(k_part), cv,
            rims, ft,
        ],
        out_specs=[full, pl.BlockSpec((1, features, rows), lambda i: (then(i), 0, 0)), whole(k_land), co, ANY, ANY],
        out_shape=[
            jax.ShapeDtypeStruct(q.shape, bf16),
            jax.ShapeDtypeStruct((seqs, features, rows), bf16),
            k_land,
            jax.ShapeDtypeStruct((seqs, rows, 128 * groups), bf16),
            jax.ShapeDtypeStruct((ranks, own, M, 128), bf16),
            jax.ShapeDtypeStruct((ranks, 16, 128), f32),
        ],
        scratch_shapes=[
            pltpu.VMEM((ranks * own, M, 128), bf16), pltpu.VMEM((ranks, 16, 128), f32),
            pltpu.VMEM((seqs, M, features), bf16), pltpu.VMEM((rows + 2 * RIM, 128), f32),
            pltpu.VMEM((40, 128), f32), rank_sems(), rank_sems(), rank_sems(),
        ],
        compiler_params=params(62 * MB, collective_id=1, has_side_effects=True),
        name="scores",
    )(q, k, v, q_land, k_part, v, rim, taps)


def split(x):
    hi = x.astype(bf16)
    return hi, (x - hi.astype(f32)).astype(bf16)


def stack_parts(xs, axis):
    return jnp.concatenate([part for x in xs for part in split(x)], axis=axis)


def pair_sums(out, count):
    top = lambda i, j: out[128 * i + 64 * j : 128 * i + 64 * j + 64]
    return [
        top(i, 0)[:, :128] + (top(i, 0)[:, 128:] + top(i, 1)[:, :128]) for i in range(count)
    ]


def pair_nn(lefts, right, masks):
    hi, lo = split(right)
    packed = jnp.concatenate([block_diag(hi, masks), block_diag(lo, masks)], axis=1)
    return pair_sums(dot(stack_parts(lefts, 0), packed), len(lefts))


def pair_nt(lefts, right, masks):
    hi, lo = split(right)
    packed = jnp.concatenate([block_diag(hi, masks), block_diag(lo, masks)], axis=0)
    return pair_sums(dot_nt(stack_parts(lefts, 0), packed), len(lefts))


def pair_tn(left, rights, masks_wide):
    out = dot_tn(stack_parts([left], 1), stack_parts(rights, 1))
    results = []
    for i in range(len(rights)):
        full = out[:128, 256 * i : 256 * i + 128] + (
            out[:128, 256 * i + 128 : 256 * i + 256] + out[128:, 256 * i : 256 * i + 128]
        )
        results.append(diag_blocks(full, masks_wide))
    return results


def half_reduce(x, upper, op, fill):
    a = op(jnp.where(upper, fill, x), axis=1, keepdims=True)
    b = op(jnp.where(upper, x, fill), axis=1, keepdims=True)
    return jnp.where(upper, b, a)


def to_column(row, same, upper):
    return half_reduce(jnp.where(same, row, 0.0), upper, jnp.sum, 0.0)


def to_row(col, same):
    return jnp.sum(jnp.where(same, col, 0.0), axis=0, keepdims=True)


def pair_consts():
    lane = lax.broadcasted_iota(jnp.int32, (M, 128), 1)
    row = lax.broadcasted_iota(jnp.int32, (M, 128), 0)
    return lane >= E, row == lane % E, group_masks((M, 128), 2, bf16), group_masks((M, 128), 2, f32)


def own_pair(land_ref, i, own):
    me, _ = seq_place()
    per = land_ref.shape[2] // 128
    p = jnp.minimum(me * own + i, land_ref.shape[0] * per - 1)
    return land_ref[p // per, :, pl.ds(pl.multiple_of((p % per) * 128, 128), 128)]


def inverse_step(
    num_ref, stat_ref, ql_ref, kl_ref, mixed_ref, sum_ref, mid_ref, z_ref, p_ref, a_ref, w_ref,
    scale_ref, tot_ref, alpha_ref,
):
    ranks, own = num_ref.shape[:2]
    upper, same, masks, masks_wide = pair_consts()
    for i in range(own):
        peak = stat_ref[0, i : i + 1, :]
        for r in range(1, ranks):
            peak = jnp.maximum(peak, stat_ref[r, i : i + 1, :])
        total = jnp.zeros((1, 128), f32)
        numer = jnp.zeros((M, 128), f32)
        for r in range(ranks):
            alpha = jnp.exp(stat_ref[r, i : i + 1, :] - peak)
            total = total + alpha * stat_ref[r, 8 + i : 9 + i, :]
            column = to_column(alpha, same, upper)
            alpha_ref[r, i] = column
            numer = numer + column * num_ref[r, i].astype(f32)
        total = to_column(total, same, upper)
        tot_ref[i] = total
        sum_ref[i] = numer / total
        ql, kl = own_pair(ql_ref, i, own), own_pair(kl_ref, i, own)
        s2 = dot_nt(ql, block_diag(kl, masks))
        e2 = jnp.exp(s2 - half_reduce(s2, upper, jnp.max, -jnp.inf))
        middle = e2 / half_reduce(e2, upper, jnp.sum, 0.0)
        mid_ref[i] = middle
        st = dot_nt(kl, block_diag(ql, masks))
        et = jnp.exp(st - jnp.max(st, axis=0, keepdims=True))
        flipped = et / jnp.sum(et, axis=0, keepdims=True)
        column = jnp.sum(middle, axis=0, keepdims=True)
        scale = 1.0 / half_reduce(column, upper[0:1], jnp.max, -jnp.inf)
        scale_ref[i] = jnp.broadcast_to(scale, (8, 128))
        z_ref[0, i] = flipped * scale

    def step(it, carry):
        zs = [z_ref[it, i] for i in range(own)]
        ps = [pair_nn([mid_ref[i]], zs[i], masks)[0] for i in range(own)]
        second = [pair_nn([ps[i], zs[i]], ps[i], masks) for i in range(own)]
        for i in range(own):
            p2, a = second[i]
            w = 7.0 * ps[i] - p2
            p_ref[it, i] = ps[i]
            a_ref[it, i] = a
            w_ref[it, i] = w
            z_ref[it + 1, i] = 0.25 * (13.0 * zs[i] - 15.0 * a + pair_nn([a], w, masks)[0])
        return carry

    lax.fori_loop(0, NEWTON, step, 0)
    for i in range(own):
        mixed_ref[i] = pair_nn([z_ref[NEWTON, i]], sum_ref[i], masks)[0].astype(bf16)


def inverse_kernel(
    num_ref, stat_ref, ql_ref, kl_ref, cv_ref, rim_ref, f_ref, mixed_out, co_ref, sum_ref, mid_ref, z_ref, p_ref,
    a_ref, w_ref, scale_ref, tot_ref, alpha_ref, mixed, pad, taps, sems,
):
    step = pl.program_id(0)
    own = num_ref.shape[1]

    @pl.when(step == 0)
    def _():
        greet()
        inverse_step(
            num_ref, stat_ref, ql_ref, kl_ref, mixed, sum_ref, mid_ref, z_ref, p_ref, a_ref, w_ref, scale_ref,
            tot_ref, alpha_ref,
        )
        begin(spread_copies(mixed, mixed_out, own, sems))

    @pl.when(step > 0)
    def _():
        conv_tile(cv_ref, rim_ref, f_ref, co_ref, pad, taps)

    @pl.when(step == pl.num_programs(0) - 1)
    def _():
        finish(spread_copies(mixed, mixed_out, own, sems))


def inverse(num, stat, q_land, k_land, v, rim, taps, first_group):
    ranks, own = num.shape[:2]
    seqs, rows, features = v.shape
    groups = features // 128 - first_group
    mat = jax.ShapeDtypeStruct((own, M, 128), f32)
    steps = lambda n: jax.ShapeDtypeStruct((n, own, M, 128), f32)
    whole = lambda a: pl.BlockSpec(a.shape, lambda i: (0,) * len(a.shape), pipeline_mode=pl.Buffered(1))
    saved = [
        mat, mat, steps(NEWTON + 1), steps(NEWTON), steps(NEWTON), steps(NEWTON),
        jax.ShapeDtypeStruct((own, 8, 128), f32), mat, steps(ranks),
    ]
    cv, rims, ft, co = conv_specs(rows, 1, first_group, groups)
    return pl.pallas_call(
        inverse_kernel,
        grid=(1 + seqs * groups,),
        in_specs=[whole(num), whole(stat), whole(q_land), whole(k_land), cv, rims, ft],
        out_specs=[ANY, co] + [whole(a) for a in saved],
        out_shape=[
            jax.ShapeDtypeStruct((ranks * own, M, 128), bf16),
            jax.ShapeDtypeStruct((seqs, rows, 128 * groups), bf16),
        ]
        + saved,
        scratch_shapes=[
            pltpu.VMEM((own, M, 128), bf16), pltpu.VMEM((rows + 2 * RIM, 128), f32), pltpu.VMEM((40, 128), f32),
            rank_sems(),
        ],
        compiler_params=params(62 * MB, collective_id=2, has_side_effects=True),
        name="inverse",
    )(num, stat, q_land, k_land, v, rim, taps)


def inverse_back_step(
    land_ref, ql_ref, kl_ref, sum_ref, mid_ref, z_ref, p_ref, a_ref, w_ref, scale_ref, tot_ref,
    alpha_ref, gn_ref, gt_ref, mq_ref, mk_ref, g_ref, dk_ref, shared=lambda: None,
):
    ranks, own = land_ref.shape[:2]
    upper, same, masks, masks_wide = pair_consts()
    for i in range(own):
        land = land_ref[0, i].astype(f32)
        for r in range(1, ranks):
            land = land + land_ref[r, i].astype(f32)
        summary, total = sum_ref[i], tot_ref[i]
        gs = pair_tn(z_ref[NEWTON, i], [land], masks_wide)[0].astype(bf16).astype(f32)
        gn = (gs / total).astype(bf16).astype(f32)
        gt = -half_reduce(gs * summary, upper, jnp.sum, 0.0) / total
        for r in range(ranks):
            gn_ref[r, i] = (alpha_ref[r, i] * gn).astype(bf16)
            gt_ref[r, i] = jnp.broadcast_to(to_row(alpha_ref[r, i] * gt, same), (8, 128))
        g_ref[i] = pair_nt([land], summary, masks)[0]
        dk_ref[i] = jnp.zeros((M, 128), f32)
    shared()

    def step(back, carry):
        it = NEWTON - 1 - back
        gs = [g_ref[i] for i in range(own)]
        das, dws = [], []
        for i in range(own):
            das.append(0.25 * (pair_nt([gs[i]], w_ref[it, i], masks)[0] - 15.0 * gs[i]))
            dws.append(0.25 * pair_tn(a_ref[it, i], [gs[i]], masks_wide)[0])
        dps, parts = [], []
        for i in range(own):
            right = pair_nt([dws[i], das[i]], p_ref[it, i], masks)
            left = pair_tn(p_ref[it, i], [dws[i]], masks_wide)[0]
            dps.append(7.0 * dws[i] - right[0] - left + pair_tn(z_ref[it, i], [das[i]], masks_wide)[0])
            parts.append(3.25 * gs[i] + right[1])
        for i in range(own):
            g_ref[i] = parts[i] + pair_tn(mid_ref[i], [dps[i]], masks_wide)[0]
            dk_ref[i] += pair_nt([dps[i]], z_ref[it, i], masks)[0]
        return carry

    lax.fori_loop(0, NEWTON, step, 0)
    eye = jnp.where(same, 1.0, 0.0).astype(bf16)
    for i in range(own):
        g, middle, scale = g_ref[i], mid_ref[i], scale_ref[i, 0:1, :]
        turned = dot_tn(stack_parts([g], 1), eye)
        turned = diag_blocks(turned[:128] + turned[128:], masks_wide)
        column = jnp.sum(middle, axis=0, keepdims=True)
        top = half_reduce(column, upper[0:1], jnp.max, -jnp.inf)
        hit = jnp.where(column == top, 1.0, 0.0)
        share = hit / half_reduce(hit, upper[0:1], jnp.sum, 0.0)
        d_scale = half_reduce(jnp.sum(turned * middle, axis=0, keepdims=True), upper[0:1], jnp.sum, 0.0)
        dk = dk_ref[i] + turned * scale - share * (d_scale * scale * scale)
        ds = middle * (dk - half_reduce(middle * dk, upper, jnp.sum, 0.0))
        hi, lo = split(ds)
        both = dot(jnp.concatenate([hi, lo], axis=0), block_diag(own_pair(kl_ref, i, own), masks))
        mq_ref[i] = both[:M] + both[M:]
        turned = dot_tn(jnp.concatenate([hi, lo], axis=1), own_pair(ql_ref, i, own))
        mk_ref[i] = diag_blocks(turned[:128] + turned[128:], masks_wide)


def inverse_back(land, q_land, k_land, saved):
    ranks, own = land.shape[:2]
    mat = jax.ShapeDtypeStruct((own, M, 128), f32)
    return pl.pallas_call(
        inverse_back_step,
        out_shape=[
            jax.ShapeDtypeStruct((ranks, own, M, 128), bf16),
            jax.ShapeDtypeStruct((ranks, own, 8, 128), f32), mat, mat,
        ],
        scratch_shapes=[pltpu.VMEM((own, M, 128), f32)] * 2,
        compiler_params=params(62 * MB),
        name="inverse_back",
    )(land, q_land, k_land, *saved)


def pick_tile(step, plan):
    tile = 0
    done = 0
    for first, count in plan:
        tile = tile + jnp.clip(step - first, -1 if done else 0, count - 1) + (1 if done else 0)
        done += count
    return tile


def front_kernel(
    tok_ref, wq_ref, f_ref,
    q_ref, k_ref, v_ref, w_ref, p_ref, ql_out, kl_out, rim_out, conv_ref, mixed_out, sum_ref, mid_ref, z_ref, zp_ref,
    za_ref, zw_ref, scale_ref, tot_ref, alpha_ref,
    land_q, land_k, ql, kl, rim, rims, num, stat, num_got, stat_got, mixed, pad, taps,
    q_sems, k_sems, rim_send, rim_recv, num_sems, stat_sems, mixed_sems, *, plan, at_third, at_first, at_inverse,
):
    step = pl.program_id(0)
    seqs, rows, features = q_ref.shape
    marks = land_q.shape[1]
    seg = rows // marks
    pairs = features // 128
    own = num_got.shape[1]
    me, count = seq_place()

    def mark_copies(src, dst, sems, s):
        spot = dst.at[s, pl.ds(me * marks, marks)]
        sends = [
            remote(src.at[s], spot, sems.at[0, s, o], sems.at[1, s, o], {"seq": peer}) for o, peer in seq_peers()
        ]
        return sends, pltpu.make_async_copy(src.at[s], spot, sems.at[0, s, 0])

    def rim_copy(s, side):
        there = lax.rem(me + (1 if side == 0 else count - 1), count)
        return remote(
            rim.at[s, side], rims.at[s, side], rim_send.at[s, side], rim_recv.at[s, side], {"seq": there}
        )

    def has_next(side):
        return me < count - 1 if side == 0 else me > 0

    @pl.when(step == 0)
    def _():
        rims[...] = jnp.zeros_like(rims)
        greet()
        stat[...] = jnp.zeros_like(stat)
        num[seqs * pairs :] = jnp.zeros_like(num[seqs * pairs :])

    @pl.when(step < seqs)
    def _():
        x = tok_ref[0]
        for part, out in enumerate((q_ref, k_ref, v_ref)):
            for c in range(0, features, 256):
                p = dot(x, wq_ref[:, part * features + c : part * features + c + 256])
                if part == 0:
                    p = 0.125 * p
                low = p.astype(bf16)
                out[step, :, c : c + 256] = low
                if part < 2:
                    total = low.astype(f32).reshape(marks, seg, 256).sum(1)
                    (land_q, land_k)[part][step, :, c : c + 256] = (total * (1.0 / seg)).astype(bf16)
                else:
                    rim[step, 0, :, c : c + 256] = low[rows - RIM :]
                    rim[step, 1, :, c : c + 256] = low[:RIM]
        begin(mark_copies(land_q, ql, q_sems, step))

        @pl.when(step > 0)
        def _():
            for side in range(2):
                @pl.when(has_next(side))
                def _(side=side):
                    rim_copy(step, side).start()

    @pl.when(step == 1)
    def _():
        for side in range(2):
            @pl.when(has_next(side))
            def _(side=side):
                rim_copy(0, side).start()

    @pl.when(step == seqs)
    def _():
        for s in range(seqs):
            begin(mark_copies(land_k, kl, k_sems, s))

    tile = pick_tile(step, plan)
    seq, group = tile // pairs, tile % pairs
    for first, tiles in plan:
        @pl.when((step >= first) & (step < first + tiles))
        def _():
            @pl.when(group == 0)
            def _():
                for side in range(2):
                    @pl.when(has_next(side))
                    def _(side=side):
                        rim_copy(seq, side).wait_send()

                    @pl.when(has_next(1 - side))
                    def _(side=side):
                        rim_copy(seq, side).wait_recv()

            lanes = pl.ds(pl.multiple_of(group * 128, 128), 128)
            taps[0:KW, :] = f_ref[:, lanes].astype(f32)
            pad[0:RIM, :] = rims[seq, 0, :, lanes].astype(f32)
            pad[RIM : RIM + rows, :] = v_ref[seq, :, lanes].astype(f32)
            pad[RIM + rows : RIM + rows + RIM, :] = rims[seq, 1, :, lanes].astype(f32)
            conv_rows(conv_ref, pad, taps, rows)

    @pl.when(step == at_third)
    def _():
        for s in range(seqs):
            finish(mark_copies(land_q, ql, q_sems, s))
        ql_out[...] = ql[...]

    @pl.when((step >= at_third) & (step < at_third + seqs))
    def _():
        s = step - at_third
        third_score_step(s, k_ref.at[pl.ds(s, 1)], v_ref.at[pl.ds(s, 1)], ql.at[pl.ds(s, 1)], w_ref, num, stat, own)

    @pl.when(step == at_third + seqs - 1)
    def _():
        begin(swap_copies(num, num_got, own, num_sems))
        begin(swap_rows(stat, stat_got, stat_sems))

    @pl.when(step == at_first)
    def _():
        for s in range(seqs):
            finish(mark_copies(land_k, kl, k_sems, s))
        kl_out[...] = kl[...]

    @pl.when((step >= at_first) & (step < at_first + seqs))
    def _():
        s = step - at_first
        first_score_step(q_ref.at[pl.ds(s, 1)], kl[s], p_ref)

    @pl.when(step == at_inverse)
    def _():
        finish(swap_copies(num, num_got, own, num_sems))
        finish(swap_rows(stat, stat_got, stat_sems))
        inverse_step(
            num_got, stat_got, ql, kl, mixed, sum_ref, mid_ref, z_ref, zp_ref, za_ref, zw_ref, scale_ref, tot_ref,
            alpha_ref,
        )
        begin(spread_copies(mixed, mixed_out, own, mixed_sems))

    @pl.when(step == pl.num_programs(0) - 1)
    def _():
        finish(spread_copies(mixed, mixed_out, own, mixed_sems))
        rim_out[...] = rims[...]


def front(tokens, w_qkv, taps, own):
    seqs, rows, features = tokens.shape
    ranks = lax.axis_size("seq")
    marks = M // ranks
    pairs = features // 128
    tiles = (4, 5, seqs * pairs - 9)
    third = seqs + tiles[0]
    first = third + seqs + tiles[1]
    at = dict(at_third=third, at_first=first, at_inverse=first + seqs)
    plan = ((seqs, tiles[0]), (third + seqs, tiles[1]), (first + seqs + 1, tiles[2]))
    here = lambda first: (lambda i: jnp.clip(i - first, 0, seqs - 1))
    score, prob = here(at["at_third"]), here(at["at_first"])
    whole = lambda a: pl.BlockSpec(a.shape, lambda i: (0,) * len(a.shape), pipeline_mode=pl.Buffered(1))
    tile = lambda i: pick_tile(i, plan)
    rows_out = jax.ShapeDtypeStruct(tokens.shape, bf16)
    land = jax.ShapeDtypeStruct((seqs, M, features), bf16)
    rim_out = jax.ShapeDtypeStruct((seqs, 2, RIM, features), bf16)
    mat = jax.ShapeDtypeStruct((own, M, 128), f32)
    steps = lambda n: jax.ShapeDtypeStruct((n, own, M, 128), f32)
    saved = [
        mat, mat, steps(NEWTON + 1), steps(NEWTON), steps(NEWTON), steps(NEWTON),
        jax.ShapeDtypeStruct((own, 8, 128), f32), mat, steps(ranks),
    ]
    vm = lambda *shape: pltpu.VMEM(shape, bf16)
    dma = pltpu.SemaphoreType.DMA
    return pl.pallas_call(
        functools.partial(front_kernel, plan=plan, **at),
        grid=(plan[-1][0] + tiles[2],),
        in_specs=[
            pl.BlockSpec((1, rows, features), lambda i: (jnp.minimum(i, seqs - 1), 0, 0)), whole(w_qkv), whole(taps),
        ],
        out_specs=[whole(rows_out)] * 3
        + [
            pl.BlockSpec((1, rows, features), lambda i: (score(i), 0, 0)),
            pl.BlockSpec((1, features, rows), lambda i: (prob(i), 0, 0)),
            whole(land), whole(land), whole(rim_out),
            pl.BlockSpec((1, rows, 128), lambda i: (tile(i) // pairs, 0, tile(i) % pairs)), ANY,
        ]
        + [whole(a) for a in saved],
        out_shape=[rows_out] * 4
        + [
            jax.ShapeDtypeStruct((seqs, features, rows), bf16), land, land, rim_out, rows_out,
            jax.ShapeDtypeStruct((ranks * own, M, 128), bf16),
        ]
        + saved,
        scratch_shapes=[
            vm(seqs, marks, features), vm(seqs, marks, features), vm(seqs, M, features), vm(seqs, M, features),
            vm(seqs, 2, RIM, features), vm(seqs, 2, RIM, features), vm(ranks * own, M, 128),
            pltpu.VMEM((ranks, 16, 128), f32), vm(ranks, own, M, 128), pltpu.VMEM((ranks, 16, 128), f32),
            vm(own, M, 128), pltpu.VMEM((rows + 2 * RIM, 128), f32), pltpu.VMEM((40, 128), f32),
            dma((2, seqs, ranks)), dma((2, seqs, ranks)), dma((seqs, 2)), dma((seqs, 2)), rank_sems(), rank_sems(),
            rank_sems(),
        ],
        compiler_params=params(62 * MB, collective_id=0, has_side_effects=True),
        name="front",
    )(tokens, w_qkv, taps)


def mean_of(x):
    return jnp.mean(x, axis=-1, keepdims=True)


def gelu_and_slope(u):
    u = u.astype(bf16)
    low = lambda c: jnp.asarray(c, bf16)
    t = low(1.0) / (low(1.0) + low(ERFC_P * root_half) * jnp.abs(u))
    bell = jnp.exp2((u * u) * low(-0.5 * log2_e))
    poly = jnp.full_like(t, 0.5 * ERFC_C[-1])
    for c in ERFC_C[-2::-1]:
        poly = poly * t + low(0.5 * c)
    half = (poly * t) * bell
    cdf = jnp.where(u < 0, half, low(1.0) - half)
    return u * cdf, cdf + u * (bell * low(inv_root_two_pi))


def row_block(
    step, tok_ref, p_ref, conv_refs, mix_ref, top_ref, w_out_ref, w_up_ref, w_down_ref, ga_ref,
    gf_ref, out_ref, proj_ref, gm_ref, gains_ref, act, gul, slope, hid_t, gdl_t, mix_t, gpr, resid, whole, ready=lambda i: None,
):
    size, features = tok_ref.shape
    ff = act.shape[1]
    wide = features
    start = pl.multiple_of(step * size, size)
    rows = pl.ds(start, size)
    near = rows if whole else pl.ds(0, size)
    masks = group_masks((M, 4 * E), 4, bf16)
    for g in range(features // 256):
        sl = slice(256 * g, 256 * g + 256)
        att = dot_tn(p_ref[0, sl, :], block_diag(quad(mix_ref, g), masks))
        split_at = conv_refs[0].shape[1]
        ref, lane = (conv_refs[0], 256 * g) if 256 * g < split_at else (conv_refs[1], 256 * g - split_at)
        resid[:, sl] = (att + ref[:, lane : lane + 256].astype(f32)).astype(bf16)
    mixed = resid[...]
    mix_t[:, near] = mixed.T
    residual = tok_ref[...].astype(f32) + dot(mixed, w_out_ref[...])
    centre = residual - mean_of(residual)
    s_att = lax.rsqrt(mean_of(centre * centre) + epsilon)
    normed = centre * s_att
    gain_att = ga_ref[...].reshape(1, features)
    hidden = normed * gain_att
    hid_low = hidden.astype(bf16)
    hid_t[:, rows] = hid_low.T
    down = jnp.zeros((size, features), f32)
    for j in range(0, ff, wide):
        if j == 0:
            ready(0)
        up = dot(hid_low, w_up_ref[:, j : j + wide])
        low, sl = gelu_and_slope(up)
        act[near, j : j + wide] = low
        slope[:, j : j + wide] = sl
        if j == 0:
            ready(1)
        down = down + dot(low, w_down_ref[j : j + wide, :])
    residual_two = hidden + down
    centre_two = residual_two - mean_of(residual_two)
    s_ffn = lax.rsqrt(mean_of(centre_two * centre_two) + epsilon)
    normed_two = centre_two * s_ffn
    gain_ffn = gf_ref[...].reshape(1, features)
    out_ref[...] = (normed_two * gain_ffn).astype(bf16)
    top = top_ref[...].astype(f32)
    gains_ref[8:16, :] += (top * normed_two).reshape(size // 8, 8, features).sum(0)
    g = top * gain_ffn
    grad_two = s_ffn * (g - mean_of(g) - normed_two * mean_of(g * normed_two))
    gdl = grad_two.astype(bf16)
    gdl_t[:, near] = gdl.T
    back = jnp.zeros((size, features), f32)
    for j in range(0, ff, wide):
        gu = dot_nt(gdl, w_down_ref[j : j + wide, :]) * slope[:, j : j + wide].astype(f32)
        low = gu.astype(bf16)
        gul[rows, j : j + wide] = low
        back = back + dot_nt(low, w_up_ref[:, j : j + wide])
    grad_hidden = grad_two + back
    gains_ref[0:8, :] += (grad_hidden * normed).reshape(size // 8, 8, features).sum(0)
    g = grad_hidden * gain_att
    proj = (s_att * (g - mean_of(g) - normed * mean_of(g * normed))).astype(bf16)
    proj_ref[...] = proj
    if whole:
        gpr[rows, :] = proj
    gm_ref[...] = dot_nt(proj, w_out_ref[...]).astype(bf16)


def row_kernel(
    tok_ref, p_ref, conv_a_ref, conv_b_ref, mix_ref, top_ref, w_out_ref, w_up_ref, w_down_ref, ga_ref, gf_ref,
    out_ref, proj_ref, gm_ref, wg_ref, gains_ref,
    act, gul, slope, hid_t, gdl_t, mix_t, gpr, resid,
):
    step = pl.program_id(0)
    size, features = tok_ref.shape
    blocks = act.shape[0] // size
    ff = act.shape[1]
    wide = features

    @pl.when(step == 0)
    def _():
        gains_ref[...] = jnp.zeros_like(gains_ref)

    @pl.when(step < blocks)
    def _():
        row_block(
            step, tok_ref, p_ref, (conv_a_ref, conv_b_ref), mix_ref, top_ref, w_out_ref, w_up_ref, w_down_ref,
            ga_ref, gf_ref, out_ref, proj_ref, gm_ref, gains_ref, act, gul, slope, hid_t, gdl_t, mix_t, gpr,
            resid, True,
        )

    chunks = ff // wide
    for first, left, right in ((0, hid_t, gul), (chunks, gdl_t, act), (2 * chunks, mix_t, gpr)):
        count = chunks if first < 2 * chunks else 1

        @pl.when((step >= blocks + first) & (step < blocks + first + count))
        def _(first=first, left=left, right=right):
            base = (step - blocks - first) * wide
            for c in range(0, wide, 256):
                cols = pl.ds(pl.multiple_of(base + c, 256), 256)
                wg_ref[0, :, c : c + 256] = dot(left[...], right[:, cols]).astype(bf16)


def row_pass(tokens, probs, conv_a, conv_b, mixed, grad_out, w_out, w_up, w_down, gain_att, gain_ffn):
    seqs, rows, features = tokens.shape
    ff = w_up.shape[1]
    size = min(256, rows)
    total = seqs * rows
    blocks = total // size
    grads = 2 * (ff // features) + 1
    here = lambda i: jnp.minimum(i, blocks - 1)
    block = pl.BlockSpec((size, features), lambda i: (here(i), 0))
    whole = lambda a: pl.BlockSpec(a.shape, lambda i: (0,) * a.ndim, pipeline_mode=pl.Buffered(1))
    flat = lambda a: a.reshape(total, a.shape[2])
    part = lambda a: pl.BlockSpec((size, a.shape[2]), lambda i: (here(i), 0))
    gains = [gain_att, gain_ffn]
    row_out = jax.ShapeDtypeStruct((total, features), bf16)
    tall = pltpu.VMEM((features, total), bf16)
    return pl.pallas_call(
        row_kernel,
        grid=(blocks + grads,),
        in_specs=[
            block, pl.BlockSpec((1, features, size), lambda i: (here(i) * size // rows, 0, here(i) % (rows // size))),
            part(conv_a), part(conv_b),
            pl.BlockSpec((features // 128, M, 128), lambda i: (here(i) * size // rows, 0, 0)),
            block, whole(w_out), whole(w_up), whole(w_down), whole(gains[0]), whole(gains[1]),
        ],
        out_specs=[block] * 3
        + [
            pl.BlockSpec((1, features, features), lambda i: (jnp.maximum(i - blocks, 0), 0, 0)),
            pl.BlockSpec((16, features), lambda i: (0, 0)),
        ],
        out_shape=[row_out] * 3
        + [
            jax.ShapeDtypeStruct((grads, features, features), bf16),
            jax.ShapeDtypeStruct((16, features), f32),
        ],
        scratch_shapes=[
            pltpu.VMEM((total, ff), bf16), pltpu.VMEM((total, ff), bf16), pltpu.VMEM((size, ff), bf16),
            tall, tall, tall, pltpu.VMEM((total, features), bf16), pltpu.VMEM((size, features), bf16),
        ],
        compiler_params=params(62 * MB),
        name="row_pass",
    )(flat(tokens), probs, flat(conv_a), flat(conv_b), mixed, flat(grad_out), w_out, w_up, w_down, *gains)


def put_parts(parts, slot, low, c, by_rows):
    for l in range(0, low.shape[1], 128):
        side, lane = (c + l) // 384, (c + l) % 384
        if by_rows:
            for d in range(8):
                parts[slot, d % 2, d // 2, 96 * side : 96 * side + 96, lane : lane + 128] = low[
                    96 * d : 96 * d + 96, l : l + 128
                ]
        else:
            for z in range(4):
                parts[slot, side, z, :, lane : lane + 128] = low[192 * z : 192 * z + 192, l : l + 128]


def fold(block):
    return jnp.concatenate([block[:48], block[48:]], axis=1)


def rows_forward_kernel(
    tok_ref, p_ref, conv_ref, mix_ref, top_ref, w_out_ref, w_up_in, w_down_in, ga_ref, gf_ref,
    out_ref, normed_ref, s_ref, gdl_ref, slope_ref, hid_t_ref, mix_t_ref, gains_ref, g_out,
    w_up_ref, w_down_ref, load_sems, act, gdl_t, mixed_ref, parts, got, sums, send, recv, out_sem,
):
    step = pl.program_id(0)
    size, features = tok_ref.shape
    blocks = act.shape[0] // size
    ff = act.shape[1]
    chunks = ff // features
    core, _, _, sibling, _, _ = cube()
    loads = [
        pltpu.make_async_copy(w_up_in, w_up_ref, load_sems.at[0]),
        pltpu.make_async_copy(w_down_in, w_down_ref, load_sems.at[1]),
    ]

    @pl.when(step == 0)
    def _():
        for load in loads:
            load.start()
        gains_ref[...] = jnp.zeros_like(gains_ref)
        greet([sibling])

    @pl.when(step < blocks)
    def _():
        rows = pl.ds(pl.multiple_of(step * size, size), size)
        masks = group_masks((M, 4 * E), 4, bf16)
        for g in range(features // 256):
            sl = slice(256 * g, 256 * g + 256)
            att = dot_tn(p_ref[0, sl, :], block_diag(quad(mix_ref, g), masks))
            mixed_ref[:, sl] = (att + conv_ref[:, sl].astype(f32)).astype(bf16)
        mixed = mixed_ref[...]
        mix_t_ref[...] = mixed.T
        residual = tok_ref[...].astype(f32) + dot(mixed, w_out_ref[...])
        centre = residual - mean_of(residual)
        s_att = lax.rsqrt(mean_of(centre * centre) + epsilon)
        normed = centre * s_att
        s_ref[...] = jnp.broadcast_to(s_att, s_ref.shape)
        normed_ref[...] = normed.astype(bf16)
        hidden = normed * ga_ref[...].reshape(1, features)
        hid_low = hidden.astype(bf16)
        hid_t_ref[...] = hid_low.T

        @pl.when(step == 0)
        def _():
            for load in loads:
                load.wait()

        down = jnp.zeros((size, features), f32)
        for j in range(0, ff, features):
            low, sl = gelu_and_slope(dot(hid_low, w_up_ref[:, j : j + features]))
            act[rows, j : j + features] = low
            slope_ref[:, j : j + features] = sl
            down = down + dot(low, w_down_ref[j : j + features, :])
        residual_two = hidden + down
        centre_two = residual_two - mean_of(residual_two)
        s_ffn = lax.rsqrt(mean_of(centre_two * centre_two) + epsilon)
        normed_two = centre_two * s_ffn
        gain_ffn = gf_ref[...].reshape(1, features)
        out_ref[...] = (normed_two * gain_ffn).astype(bf16)
        top = top_ref[...].astype(f32)
        gains_ref[...] += (top * normed_two).reshape(size // 8, 8, features).sum(0)
        g = top * gain_ffn
        gdl = (s_ffn * (g - mean_of(g) - normed_two * mean_of(g * normed_two))).astype(bf16)
        gdl_ref[...] = gdl
        gdl_t[:, rows] = gdl.T

    j = step - blocks
    slot = lax.rem(jnp.maximum(j, 0), 2)

    def share(at):
        return remote(parts.at[at % 2, 1 - core], got.at[at], send.at[at], recv.at[at], sibling)

    def out_copy(at):
        return pltpu.make_async_copy(sums.at[at % 2], g_out.at[:, at], out_sem.at[at % 2])

    @pl.when((j >= 2) & (j < chunks))
    def _():
        share(j - 2).wait_send()

    @pl.when((j >= 0) & (j < chunks))
    def _():
        for c in range(0, features, 256):
            cols = pl.ds(pl.multiple_of(j * features + c, 256), 256)
            put_parts(parts, slot, dot(gdl_t[...], act[:, cols]).astype(bf16), c, False)
        share(j).start()

    done = j - 1

    @pl.when(done >= 2)
    def _():
        out_copy(done - 2).wait()

    @pl.when(done >= 0)
    def _():
        share(done).wait_recv()
        sums[done % 2] = add_low(parts[done % 2, core], got[done])
        out_copy(done).start()

    @pl.when(done == chunks - 1)
    def _():
        for at in (done - 1, done):
            share(at).wait_send()
            out_copy(at).wait()


def rows_forward(tokens, probs, conv_out, mixed, grad_out, w_out, w_up, w_down, gain_att, gain_ffn):
    seqs, rows, features = tokens.shape
    ff = w_up.shape[1]
    size = rows
    total = seqs * rows
    blocks = total // size
    chunks = ff // features
    here = lambda i: jnp.minimum(i, blocks - 1)
    block = lambda n: pl.BlockSpec((size, n), lambda i: (here(i), 0))
    turned = pl.BlockSpec((features, size), lambda i: (0, here(i)))
    whole = lambda a: pl.BlockSpec(a.shape, lambda i: (0,) * a.ndim, pipeline_mode=pl.Buffered(1))
    flat = lambda a: a.reshape(total, a.shape[2])
    shape = jax.ShapeDtypeStruct
    dma = pltpu.SemaphoreType.DMA
    return pl.pallas_call(
        rows_forward_kernel,
        grid=(blocks + chunks + 1,),
        in_specs=[
            block(features),
            pl.BlockSpec((1, features, size), lambda i: (here(i) * size // rows, 0, here(i) % (rows // size))),
            block(features), pl.BlockSpec((features // 128, M, 128), lambda i: (here(i) * size // rows, 0, 0)),
            block(features), whole(w_out), ANY, ANY, whole(gain_att), whole(gain_ffn),
        ],
        out_specs=[block(features), block(features), block(128), block(features), block(ff), turned, turned]
        + [pl.BlockSpec((8, features), lambda i: (0, 0)), ANY],
        out_shape=[
            shape((total, features), bf16), shape((total, features), bf16), shape((total, 128), f32),
            shape((total, features), bf16), shape((total, ff), bf16), shape((features, total), bf16),
            shape((features, total), bf16), shape((8, features), f32), shape((4, chunks, 192, 384), bf16),
        ],
        scratch_shapes=[
            pltpu.VMEM(w_up.shape, bf16), pltpu.VMEM(w_down.shape, bf16), dma((2,)), pltpu.VMEM((total, ff), bf16),
            pltpu.VMEM((features, total), bf16), pltpu.VMEM((size, features), bf16),
            pltpu.VMEM((2, 2, 4, 192, 384), bf16), pltpu.VMEM((chunks, 4, 192, 384), bf16),
            pltpu.VMEM((2, 4, 192, 384), bf16), dma((chunks,)), dma((chunks,)), dma((2,)),
        ],
        compiler_params=params(62 * MB, collective_id=3, has_side_effects=True),
        name="rows_forward",
    )(
        flat(tokens), probs, flat(conv_out), mixed, flat(grad_out), w_out, w_up, w_down, gain_att, gain_ffn
    )


def rows_backward_kernel(
    turn_at, gdl_ref, slope_ref, normed_ref, s_ref, w_out_ref, ga_ref, w_down_in, w_up_in, hid_t_in, mix_t_in, down_in,
    proj_ref, gm_ref, gains_ref, down_ref, g_out, rim_out,
    w_down_ref, w_up_ref, hid_t, mix_t, load_sems, gul, gpr, rim, parts, got, sums,
    kept, crossed, turned, kept_sems, cross_sems, turn_sems,
    send, recv, out_sem, last_sem, rim_send, rim_recv,
):
    step = pl.program_id(0)
    size, features = gdl_ref.shape
    ff = gul.shape[1]
    blocks = gul.shape[0] // size
    chunks = ff // features
    seqs = rim.shape[0]
    per = blocks // seqs
    me, count = seq_place()
    core, _, _, sibling, along_x, along_y = cube()
    loads = [
        pltpu.make_async_copy(a, b, load_sems.at[i])
        for i, (a, b) in enumerate(
            ((w_down_in, w_down_ref), (w_up_in, w_up_ref), (hid_t_in, hid_t), (mix_t_in, mix_t))
        )
    ]
    cross = cross_copies(down_in, crossed, cross_sems)
    keep = kept_copies(down_in, kept, kept_sems)
    turn = turn_copies(kept, turned, turn_sems)

    @pl.when(step == 0)
    def _():
        for load in loads:
            load.start()
        gains_ref[...] = jnp.zeros_like(gains_ref)
        greet([sibling, along_x, along_y])
        for copy in cross + keep:
            copy.start()

    @pl.when(step == turn_at)
    def _():
        for copy in cross + keep:
            copy.wait()
        cross_add(kept, crossed)
        for copy in turn:
            copy.start()

    def rim_copy(s, side):
        there = lax.rem(me + (1 if side == 0 else count - 1), count)
        return remote(
            rim.at[s, side], rim_out.at[s, side], rim_send.at[s, side], rim_recv.at[s, side], {"seq": there}
        )

    @pl.when(step < blocks)
    def _():
        rows = pl.ds(pl.multiple_of(step * size, size), size)

        @pl.when(step == 0)
        def _():
            loads[0].wait()

        gdl = gdl_ref[...]
        back = gdl.astype(f32)
        for j in range(0, ff, features):
            gu = dot_nt(gdl, w_down_ref[j : j + features, :]) * slope_ref[:, j : j + features].astype(f32)
            low = gu.astype(bf16)
            gul[rows, j : j + features] = low
            if j == 0:
                @pl.when(step == 0)
                def _():
                    loads[1].wait()
            back = back + dot_nt(low, w_up_ref[:, j : j + features])
        normed = normed_ref[...].astype(f32)
        gains_ref[...] += (back * normed).reshape(size // 8, 8, features).sum(0)
        g = back * ga_ref[...].reshape(1, features)
        proj = (s_ref[:, 0:1] * (g - mean_of(g) - normed * mean_of(g * normed))).astype(bf16)
        proj_ref[...] = proj
        gpr[rows, :] = proj
        gm_ref[...] = dot_nt(proj, w_out_ref[...]).astype(bf16)
        s = step // per

        @pl.when(step % per == 0)
        def _():
            rim[s, 1] = gm_ref[:RIM, :]
            rim_copy(s, 1).start()

        @pl.when(step % per == per - 1)
        def _():
            rim[s, 0] = gm_ref[size - RIM :, :]
            rim_copy(s, 0).start()

    j = step - blocks
    slot = lax.rem(jnp.maximum(j, 0), 2)

    def share(at):
        return remote(parts.at[at % 2, 1 - core], got.at[at], send.at[at], recv.at[at], sibling)

    def up_copy(at):
        return pltpu.make_async_copy(sums.at[at % 2], g_out.at[at, :, 0:192, :], out_sem.at[at % 2])

    def out_copy(z):
        return pltpu.make_async_copy(
            sums.at[0, :, 48 * z : 48 * z + 48, :], g_out.at[z, :, 192:240, :], last_sem.at[z]
        )

    @pl.when((j >= 2) & (j <= chunks))
    def _():
        share(j - 2).wait_send()

    @pl.when(j == 0)
    def _():
        loads[2].wait()
        loads[3].wait()

    @pl.when((j >= 0) & (j < chunks))
    def _():
        for c in range(0, features, 256):
            cols = pl.ds(pl.multiple_of(j * features + c, 256), 256)
            put_parts(parts, slot, dot(hid_t[...], gul[:, cols]).astype(bf16), c, True)
        share(j).start()

    @pl.when(j == chunks)
    def _():
        for c in range(2):
            low = dot(mix_t[...], gpr[:, 384 * c : 384 * c + 384]).astype(bf16)
            for zz in range(2):
                z = 2 * c + zz
                for d in range(8):
                    parts[slot, d % 2, d // 2, 48 * z : 48 * z + 48, :] = fold(
                        low[96 * d : 96 * d + 96, 192 * zz : 192 * zz + 192]
                    )
        share(j).start()

    done = j - 1

    @pl.when(done >= 2)
    def _():
        up_copy(done - 2).wait()

    @pl.when(done >= 0)
    def _():
        share(done).wait_recv()
        sums[done % 2] = add_low(parts[done % 2, core], got[done])

    @pl.when((done >= 0) & (done < chunks))
    def _():
        up_copy(done).start()

    @pl.when(done == chunks)
    def _():
        for z in range(4):
            out_copy(z).start()
        for copy in turn:
            copy.wait()
        turn_add(down_ref, kept, turned)
        share(done - 1).wait_send()
        share(done).wait_send()
        up_copy(done - 1).wait()
        for z in range(4):
            out_copy(z).wait()

        def rims(s, carry):
            for side in range(2):
                rim_copy(s, side).wait()
            return carry

        lax.fori_loop(0, seqs, rims, 0)


def rows_backward(gdl, slope, normed, s_att, w_out, gain_att, w_down, w_up, hid_t, mix_t, downs, seqs):
    total, features = gdl.shape
    ff = w_up.shape[1]
    size = total // seqs
    blocks = total // size
    chunks = ff // features
    here = lambda i: jnp.minimum(i, blocks - 1)
    block = lambda n: pl.BlockSpec((size, n), lambda i: (here(i), 0))
    whole = lambda a: pl.BlockSpec(a.shape, lambda i: (0,) * len(a.shape), pipeline_mode=pl.Buffered(1))
    shape = jax.ShapeDtypeStruct
    down_sum = shape((4, 192, 384), bf16)
    dma = pltpu.SemaphoreType.DMA
    return pl.pallas_call(
        functools.partial(rows_backward_kernel, 2),
        grid=(blocks + chunks + 2,),
        in_specs=[block(features), block(ff), block(features), block(128), whole(w_out), whole(gain_att)] + [ANY] * 5,
        out_specs=[block(features), block(features), pl.BlockSpec((8, features), lambda i: (0, 0)), whole(down_sum)]
        + [ANY] * 2,
        out_shape=[
            shape((total, features), bf16), shape((total, features), bf16), shape((8, features), f32), down_sum,
            shape((4, chunks, 240, 384), bf16), shape((seqs, 2, RIM, features), bf16),
        ],
        scratch_shapes=[
            pltpu.VMEM(w_down.shape, bf16), pltpu.VMEM(w_up.shape, bf16), pltpu.VMEM(hid_t.shape, bf16),
            pltpu.VMEM(mix_t.shape, bf16), dma((4,)), pltpu.VMEM((total, ff), bf16),
            pltpu.VMEM((total, features), bf16), pltpu.VMEM((seqs, 2, RIM, features), bf16),
            pltpu.VMEM((2, 2, 4, 192, 384), bf16), pltpu.VMEM((chunks + 1, 4, 192, 384), bf16),
            pltpu.VMEM((2, 4, 192, 384), bf16),
        ]
        + stage_scratch(192)
        + [dma((chunks + 1,)), dma((chunks + 1,)), dma((2,)), dma((4,)), dma((seqs, 2)), dma((seqs, 2))],
        compiler_params=params(62 * MB, collective_id=4, has_side_effects=True),
        name="rows_backward",
    )(gdl, slope, normed, s_att, w_out, gain_att, w_down, w_up, hid_t, mix_t, downs)


def first_back_step(gm_ref, p_ref, q_ref, mix_ref, kl_of, put_land, put_gq, put_klp):
    features = gm_ref.shape[2]
    masks = group_masks((M, 4 * E), 4, bf16)
    masks_wide = group_masks((M, 4 * E), 4, f32)
    for g in range(features // 256):
        sl = slice(256 * g, 256 * g + 256)
        gm, p = gm_ref[0, :, sl], p_ref[0, sl, :]
        put_land(g, diag_blocks(dot(p, gm), masks_wide).astype(bf16))
        d = dot_nt(block_diag(quad(mix_ref, g), masks), gm)
        parts = []
        for h in range(4):
            pw = p[E * h : E * h + E].astype(f32)
            dh = d[E * h : E * h + E]
            parts.append((pw * (dh - jnp.sum(pw * dh, axis=0, keepdims=True))).astype(bf16))
        gs = jnp.concatenate(parts, axis=0)
        put_gq(g, dot_tn(gs, block_diag(kl_of(sl), masks)).astype(bf16))
        put_klp(g, diag_blocks(dot(gs, q_ref[0, :, sl]), masks_wide))


def first_back_kernel(gm_ref, p_ref, q_ref, mix_ref, kl_ref, land_ref, gq_ref, klp_ref):
    def put_land(g, x):
        for i in range(2):
            land_ref[2 * g + i] = x[:, 128 * i : 128 * i + 128]

    def put_klp(g, x):
        klp_ref[0, :, 256 * g : 256 * g + 256] = x

    def put_gq(g, x):
        gq_ref[0, :, 256 * g : 256 * g + 256] = x

    first_back_step(gm_ref, p_ref, q_ref, mix_ref, lambda sl: kl_ref[0, :, sl], put_land, put_gq, put_klp)


def first_back(gm, probs, q, mixed, k_land):
    seqs, rows, features = q.shape
    pairs = features // 128
    full = pl.BlockSpec((1, rows, features), lambda s: (s, 0, 0))
    land = pl.BlockSpec((1, M, features), lambda s: (s, 0, 0))
    return pl.pallas_call(
        first_back_kernel,
        grid=(seqs,),
        in_specs=[full, pl.BlockSpec((1, features, rows), lambda s: (s, 0, 0)), full, pl.BlockSpec((pairs, M, 128), lambda s: (s, 0, 0)), land],
        out_specs=[pl.BlockSpec((pairs, M, 128), lambda s: (s, 0, 0)), full, land],
        out_shape=[
            jax.ShapeDtypeStruct((seqs * pairs, M, 128), bf16),
            jax.ShapeDtypeStruct(q.shape, bf16),
            jax.ShapeDtypeStruct((seqs, M, features), f32),
        ],
        compiler_params=params(62 * MB),
        name="first_back",
    )(gm, probs, q, mixed, k_land)


def third_back_kernel(w_ref, v_ref, k_ref, gc_ref, gn_ref, gt_ref, ql_ref, gv_ref, gk_ref, qlp_ref):
    features = w_ref.shape[2]
    masks = group_masks((M, 4 * E), 4, bf16)
    masks_wide = group_masks((M, 4 * E), 4, f32)
    for g in range(features // 256):
        sl = slice(256 * g, 256 * g + 256)
        w = w_ref[0, :, sl]
        gn = jnp.concatenate([gn_ref[2 * g], gn_ref[2 * g + 1]], axis=1)
        gt = jnp.concatenate([gt_ref[2 * g, 0:1, :], gt_ref[2 * g + 1, 0:1, :]], axis=1)
        gd = block_diag(gn, masks)
        gs = (w.astype(f32) * (dot_nt(v_ref[0, :, sl], gd) + gt)).astype(bf16)
        gv_ref[0, :, sl] = (dot(w, gd) + gc_ref[0, :, sl].astype(f32)).astype(bf16)
        gk_ref[0, :, sl] = dot(gs, block_diag(ql_ref[0, :, sl], masks)).astype(bf16)
        qlp_ref[0, :, sl] = diag_blocks(dot_tn(gs, k_ref[0, :, sl]), masks_wide)


def third_back(w, v, k, grad_conv, gn, gt, q_land):
    seqs, rows, features = v.shape
    pairs = features // 128
    full = pl.BlockSpec((1, rows, features), lambda s: (s, 0, 0))
    land = pl.BlockSpec((1, M, features), lambda s: (s, 0, 0))
    return pl.pallas_call(
        third_back_kernel,
        grid=(seqs,),
        in_specs=[full] * 4
        + [
            pl.BlockSpec((pairs, M, 128), lambda s: (s, 0, 0)),
            pl.BlockSpec((pairs, 8, 128), lambda s: (s, 0, 0)),
            land,
        ],
        out_specs=[full, full, land],
        out_shape=[jax.ShapeDtypeStruct(v.shape, bf16)] * 2
        + [jax.ShapeDtypeStruct((seqs, M, features), f32)],
        compiler_params=params(62 * MB),
        name="third_back",
    )(w, v, k, grad_conv, gn, gt, q_land)


def last_kernel(tok_ref, gq_ref, gk_ref, gv_ref, qo_ref, ko_ref, proj_ref, w_ref, gt_ref, wg_ref, d, tok_t):
    step = pl.program_id(0)
    seqs = tok_t.shape[1] // tok_ref.shape[1]
    rows, features = tok_ref.shape[1:]
    marks = qo_ref.shape[1]
    seg = rows // marks

    @pl.when(step < seqs)
    def _():
        here = pl.ds(pl.multiple_of(step * rows, rows), rows)
        for part, (core, own) in enumerate(((gq_ref, qo_ref), (gk_ref, ko_ref))):
            for m in range(marks):
                at = pl.ds(pl.multiple_of(step * rows + m * seg, seg), seg)
                x = core[0, m * seg : m * seg + seg, :].astype(f32) + own[0, m : m + 1, :] * (1.0 / seg)
                x = x.astype(bf16)
                if part == 0:
                    x = x * jnp.asarray(0.125, bf16)
                d[at, part * features : part * features + features] = x
        d[here, 2 * features :] = gv_ref[0]
        tok_t[:, here] = tok_ref[0].T
        for c in range(0, rows, 128):
            at = pl.ds(pl.multiple_of(step * rows + c, 128), 128)
            gt_ref[0, c : c + 128, :] = (
                proj_ref[0, c : c + 128, :].astype(f32) + dot_nt(d[at, :], w_ref[...])
            ).astype(bf16)

    @pl.when(step >= seqs)
    def _():
        base = (step - seqs) * features
        for c in range(0, features, 256):
            cols = pl.ds(pl.multiple_of(base + c, 256), 256)
            wg_ref[0, :, c : c + 256] = dot(tok_t[...], d[:, cols]).astype(bf16)


def last_pass(tokens, gq, gk, gv, q_own, k_own, proj, w_qkv):
    seqs, rows, features = tokens.shape
    marks = q_own.shape[1]
    here = lambda i: jnp.minimum(i, seqs - 1)
    full = pl.BlockSpec((1, rows, features), lambda i: (here(i), 0, 0))
    land = pl.BlockSpec((1, marks, features), lambda i: (here(i), 0, 0))
    return pl.pallas_call(
        last_kernel,
        grid=(seqs + 3,),
        in_specs=[full] * 4 + [land] * 2
        + [full, pl.BlockSpec(w_qkv.shape, lambda i: (0, 0), pipeline_mode=pl.Buffered(1))],
        out_specs=[full, pl.BlockSpec((1, features, features), lambda i: (jnp.maximum(i - seqs, 0), 0, 0))],
        out_shape=[
            jax.ShapeDtypeStruct(tokens.shape, bf16),
            jax.ShapeDtypeStruct((3, features, features), bf16),
        ],
        scratch_shapes=[
            pltpu.VMEM((seqs * rows, 3 * features), bf16), pltpu.VMEM((features, seqs * rows), bf16),
        ],
        compiler_params=params(62 * MB),
        name="last_pass",
    )(tokens, gq, gk, gv, q_own, k_own, proj, w_qkv)


def add_pairs(dst, own, start, pairs):
    for i in range(own.shape[0]):
        @pl.when(start + i < pairs)
        def _(i=i):
            dst[start + i] += own[i]


def cross_copies(src, got, sems):
    _, x, y, _, along_x, along_y = cube()
    return [
        remote(src.at[0:2, :, 1 - x], got.at[0], sems.at[0, 0], sems.at[1, 0], along_x),
        remote(src.at[2:4, 1 - y], got.at[1], sems.at[0, 1], sems.at[1, 1], along_y),
    ]


def kept_copies(src, kept, sems):
    _, x, y, _, _, _ = cube()
    return [
        pltpu.make_async_copy(src.at[0:2, :, x], kept.at[0], sems.at[0]),
        pltpu.make_async_copy(src.at[2:4, y], kept.at[1], sems.at[1]),
    ]


def turn_copies(kept, got, sems):
    _, x, y, _, along_x, along_y = cube()
    return [
        remote(kept.at[0, :, 1 - y], got.at[0], sems.at[0, 0], sems.at[1, 0], along_y),
        remote(kept.at[1, :, 1 - x], got.at[1], sems.at[0, 1], sems.at[1, 1], along_x),
    ]


def cross_add(kept, got):
    for half in range(2):
        for rank in range(2):
            kept[half, rank] = add_low(kept[half, rank], got[half, rank])


def turn_add(out, kept, got):
    _, x, y, _, _, _ = cube()
    for half, place in ((0, y), (1, x)):
        for rank in range(2):
            out[2 * half + rank] = add_low(kept[half, rank, place], got[half, rank])


def stage_scratch(rows):
    dma = pltpu.SemaphoreType.DMA
    return [
        pltpu.VMEM((2, 2, 2, rows, 384), bf16), pltpu.VMEM((2, 2, 2, rows, 384), bf16),
        pltpu.VMEM((2, 2, rows, 384), bf16), dma((2,)), dma((2, 2)), dma((2, 2)),
    ]


def first_third(w_ref, v_ref, k_ref, gn_of, gt_of, put_gs, put_qlp):
    features = w_ref.shape[2]
    masks = group_masks((M, 4 * E), 4, bf16)
    masks_wide = group_masks((M, 4 * E), 4, f32)
    for g in range(features // 256):
        sl = slice(256 * g, 256 * g + 256)
        gd = block_diag(jnp.concatenate([gn_of(2 * g), gn_of(2 * g + 1)], axis=1), masks)
        gt = jnp.concatenate([gt_of(2 * g), gt_of(2 * g + 1)], axis=1)
        gs = (w_ref[0, :, sl].astype(f32) * (dot_nt(v_ref[0, :, sl], gd) + gt)).astype(bf16)
        put_gs(g, gs)
        put_qlp(g, diag_blocks(dot_tn(gs, k_ref[0, :, sl]), masks_wide))


def tail_plan(seqs, pairs, blocks):
    tiles = (6, 7, seqs * pairs - 13)
    at, step = {}, 0
    for name, count in (
        ("first", seqs), ("conv_a", tiles[0]), ("inverse", 1), ("one", seqs), ("conv_b", tiles[1]), ("q", 1),
        ("keys", seqs), ("k", 1), ("conv_c", tiles[2]), ("values", seqs), ("v", 1), ("tok", blocks), ("last", 1),
    ):
        at[name] = step
        step += count
    return at, tuple((at[n], c) for n, c in zip(("conv_a", "conv_b", "conv_c"), tiles)), step


def tail_kernel(
    seqs, gm_ref, p_ref, q_ref, mix_ref, ql_ref, kl_ref, cg_ref, rim_ref, cv_ref, f_ref,
    sum_ref, mid_ref, z_ref, zp_ref, za_ref, zw_ref, scale_ref, tot_ref, alpha_ref,
    w_ref, v_ref, k_ref, tok_ref, proj_ref, gain_a_ref, gain_f_ref, wq_in, down_in, up_in,
    gtok_ref, up_out, down_out, out_out, qkv_out, taps_out, ga_out, gf_out,
    d, tok_t, wq_ref, klp, land, land_got, gn, gn_got, gt, gt_low, gt_got, mq, mk, g_acc, dk_acc, kl_low, kl_got,
    qlp, qlow, qgot, pad, facc, taps, tapsg, up_sum, up_got, down_got,
    part, got_a, sum_a, got_b, sum_b, got_c, sum_c, got_z, sm_got, sm_sum,
    kept, crossed, turned, kept_sems, cross_sems, turn_sems,
    load_sem, land_sems, gn_sems, gt_sems, kl_sems, q_sems, zd_sems, ze_sems, zu_sems, zv_sems,
    a_send, a_recv, b_sems, c_sems, zq_send, zq_recv, s_send, s_recv, s_sems,
):
    step = pl.program_id(0)
    last = pl.num_programs(0) - 1
    rows, features = tok_ref.shape[1:]
    pairs = features // 128
    ranks, own = land_got.shape[:2]
    marks = kl_got.shape[2]
    seg = rows // marks
    at, plan, _ = tail_plan(seqs, pairs, d.shape[0] // gtok_ref.shape[0])
    me, _ = seq_place()
    core, x, y, sibling, along_x, along_y = cube()
    cross = cross_copies(up_in, crossed, cross_sems)
    keep = kept_copies(up_in, kept, kept_sems)
    turn = turn_copies(kept, turned, turn_sems)
    load = pltpu.make_async_copy(wq_in, wq_ref, load_sem.at[0])

    def z_copies(src, dst, first, count, sems):
        span = pl.ds(first, count)
        sends = [
            remote(src.at[peer, span], dst.at[me, span], sems.at[0, o], sems.at[1, o], {"seq": peer})
            for o, peer in seq_peers()
        ]
        return sends, pltpu.make_async_copy(src.at[me, span], dst.at[me, span], sems.at[0, 0])

    downs = [z_copies(down_in, down_got, 0, 96, zd_sems), z_copies(down_in, down_got, 96, 96, ze_sems)]
    ups = [z_copies(up_sum, up_got, 0, 80, zu_sems), z_copies(up_sum, up_got, 80, 160, zv_sems)]

    def mark_copies(src, dst, sems):
        sends = [
            remote(
                src.at[:, pl.ds(peer * marks, marks)], dst.at[me], sems.at[0, o], sems.at[1, o], {"seq": peer}
            )
            for o, peer in seq_peers()
        ]
        return sends, pltpu.make_async_copy(src.at[:, pl.ds(me * marks, marks)], dst.at[me], sems.at[0, 0])

    gn_exchange = [swap_rows(gn, gn_got, gn_sems), swap_rows(gt_low, gt_got, gt_sems)]
    kl_exchange = mark_copies(kl_low, kl_got, kl_sems)
    q_exchange = mark_copies(qlow, qgot, q_sems)

    def a_copy(p):
        return remote(
            part.at[1 - core, pl.ds(4 * p, 4)], got_a.at[pl.ds(4 * p, 4)], a_send.at[p], a_recv.at[p], sibling
        )

    def b_copies(p):
        return [
            remote(
                sum_a.at[4 * p : 4 * p + 2, :, 1 - x], got_b.at[p, 0], b_sems.at[0, p, 0], b_sems.at[1, p, 0],
                along_x,
            ),
            remote(
                sum_a.at[4 * p + 2 : 4 * p + 4, 1 - y], got_b.at[p, 1], b_sems.at[0, p, 1], b_sems.at[1, p, 1],
                along_y,
            ),
        ]

    def c_copies(p):
        return [
            remote(
                sum_b.at[p, 0, :, 1 - y], got_c.at[p, 0], c_sems.at[0, p, 0], c_sems.at[1, p, 0], along_y
            ),
            remote(
                sum_b.at[p, 1, :, 1 - x], got_c.at[p, 1], c_sems.at[0, p, 1], c_sems.at[1, p, 1], along_x
            ),
        ]

    def zq_copy(group):
        rank, place = group // 3, group % 3
        offset = lax.rem(rank - me + ranks, ranks)
        return rank, remote(
            sum_c.at[group], got_z.at[me, place], zq_send.at[group], zq_recv.at[place, offset], {"seq": rank}
        )

    def stage_b(p):
        a_copy(p).wait()
        for yx in range(4):
            sum_a[4 * p : 4 * p + 4, yx // 2, yx % 2] = add_low(
                part[core, 4 * p : 4 * p + 4, yx], got_a[4 * p : 4 * p + 4, yx]
            )
        for copy in b_copies(p):
            copy.start()

    def stage_c(p):
        for copy in b_copies(p):
            copy.wait()
        sum_b[p, 0] = add_low(sum_a[4 * p : 4 * p + 2, :, x], got_b[p, 0])
        sum_b[p, 1] = add_low(sum_a[4 * p + 2 : 4 * p + 4, y], got_b[p, 1])
        for copy in c_copies(p):
            copy.start()

    def stage_z(p):
        for copy in c_copies(p):
            copy.wait()
        sum_c[4 * p : 4 * p + 2] = add_low(sum_b[p, 0, :, y], got_c[p, 0])
        sum_c[4 * p + 2 : 4 * p + 4] = add_low(sum_b[p, 1, :, x], got_c[p, 1])
        for group in range(4 * p, 4 * p + 4):
            rank, copy = zq_copy(group)

            @pl.when(rank != me)
            def _(copy=copy):
                copy.start()

    small_copies = [
        remote(sm_sum.at[i], sm_got.at[i], s_send.at[i], s_recv.at[i], target)
        for i, target in enumerate((sibling, along_x, along_y))
    ]

    def small_spread():
        return [
            remote(sm_sum.at[3], sm_got.at[3 + me], s_sems.at[0, o], s_sems.at[1, o], {"seq": peer})
            for o, peer in seq_peers()
        ]

    def seq_rows(s):
        return pl.ds(pl.multiple_of(s * rows, rows), rows)

    @pl.when(step == 0)
    def _():
        load.start()
        greet([sibling, along_x, along_y])
        for copy in cross + keep:
            copy.start()
        begin(downs[0])
        land[seqs * pairs :] = jnp.zeros_like(land[seqs * pairs :])

    @pl.when(step < seqs)
    def _():
        def put_land(g, v):
            for i in range(2):
                land[step * pairs + 2 * g + i] = v[:, 128 * i : 128 * i + 128]

        def put_klp(g, v):
            for i in range(2):
                klp[step * pairs + 2 * g + i] = v[:, 128 * i : 128 * i + 128]

        def put_gq(g, v):
            d[seq_rows(step), 256 * g : 256 * g + 256] = v

        first_back_step(gm_ref, p_ref, q_ref, mix_ref, lambda sl: kl_ref[step, :, sl], put_land, put_gq, put_klp)

    @pl.when(step == seqs - 1)
    def _():
        begin(swap_copies(land, land_got, own, land_sems))

    tile = pick_tile(step, plan)
    for first, tiles in plan:
        @pl.when((step >= first) & (step < first + tiles))
        def _():
            seq, group = tile % seqs, tile // seqs
            lanes = pl.ds(pl.multiple_of(group * 128, 128), 128)

            def put(c, v):
                spot = pl.ds(pl.multiple_of(seq * rows + c, 64), 64)
                d[spot, pl.ds(pl.multiple_of(2 * features + group * 128, 128), 128)] = v

            def put_taps(v):
                tapsg[0:KW, lanes] = v

            conv_back_rows(seq, seqs, cg_ref, rim_ref, cv_ref, f_ref, put, put_taps, pad, facc, taps)

    @pl.when(step == at["inverse"])
    def _():
        finish(swap_copies(land, land_got, own, land_sems))

        def shared():
            for r in range(ranks):
                gt_low[r] = jnp.concatenate(
                    [gt[r, i, 0:1, :] for i in range(own)] + [jnp.zeros((8 - own, 128), f32)], axis=0
                )
            for pair in gn_exchange:
                begin(pair)

        inverse_back_step(
            land_got, ql_ref, kl_ref, sum_ref, mid_ref, z_ref, zp_ref, za_ref, zw_ref, scale_ref, tot_ref, alpha_ref,
            gn, gt, mq, mk, g_acc, dk_acc, shared,
        )
        add_pairs(klp, mk, me * own, seqs * pairs)
        kl_low[...] = klp[...].astype(bf16)
        begin(kl_exchange)

    @pl.when(step == at["one"])
    def _():
        for copy in cross + keep:
            copy.wait()
        cross_add(kept, crossed)
        for copy in turn:
            copy.start()
        for pair in gn_exchange:
            finish(pair)

    def gn_of(s):
        def of(i):
            p = s * pairs + i
            return gn_got[p // own, p % own]

        return of

    def land_rows(of):
        total = of(0).astype(f32)
        for r in range(1, ranks):
            total = total + of(r).astype(f32)
        return total * (1.0 / seg)

    @pl.when(step == at["values"])
    def _():
        sm_sum[0, KW:, :] = jnp.zeros_like(sm_sum[0, KW:, :])
        sm_sum[0, :KW, :] = tapsg[:KW]
        sm_sum[0, KW : KW + 1, :] = jnp.sum(gain_a_ref[...], axis=0, keepdims=True)
        sm_sum[0, KW + 1 : KW + 2, :] = jnp.sum(gain_f_ref[...], axis=0, keepdims=True)
        small_copies[0].start()

    for i in range(1, 4):
        @pl.when(step == at["values"] + i)
        def _(i=i):
            small_copies[i - 1].wait()
            sm_sum[i] = sm_sum[i - 1] + sm_got[i - 1]
            if i < 3:
                small_copies[i].start()
            else:
                for copy in small_spread():
                    copy.start()

    @pl.when((step >= at["one"]) & (step < at["one"] + seqs))
    def _():
        s = step - at["one"]

        def gt_of(i):
            p = s * pairs + i
            return gt_got[p // own, pl.ds(p % own, 1), :]

        def put_gs(g, val):
            d[seq_rows(s), features + 256 * g : features + 256 * g + 256] = val

        def put_qlp(g, val):
            for i in range(2):
                qlp[s * pairs + 2 * g + i] = val[:, 128 * i : 128 * i + 128]

        first_third(w_ref, v_ref, k_ref, gn_of(s), gt_of, put_gs, put_qlp)
        tok_t[:, seq_rows(s)] = tok_ref[0].T

    @pl.when(step == at["one"] + seqs - 1)
    def _():
        add_pairs(qlp, mq, me * own, seqs * pairs)
        qlow[...] = qlp[...].astype(bf16)
        begin(q_exchange)

    @pl.when(step == at["q"])
    def _():
        finish(q_exchange)
        for copy in turn:
            copy.wait()
        turn_add(up_sum, kept, turned)
        begin(downs[1])
        begin(ups[0])

        def fill(s, carry):
            for g in range(pairs):
                spread = land_rows(lambda r: qgot[r, s * pairs + g])
                for m in range(marks):
                    spot = pl.ds(pl.multiple_of(s * rows + m * seg, seg), seg)
                    val = d[spot, 128 * g : 128 * g + 128].astype(f32)
                    low = (val + spread[m : m + 1]).astype(bf16) * jnp.asarray(0.125, bf16)
                    d[spot, 128 * g : 128 * g + 128] = low
            return carry

        lax.fori_loop(0, seqs, fill, 0)

    @pl.when(step == at["keys"])
    def _():
        finish(kl_exchange)

    @pl.when((step >= at["keys"]) & (step < at["keys"] + seqs))
    def _():
        s = step - at["keys"]
        masks = group_masks((M, 4 * E), 4, bf16)
        for g in range(features // 256):
            ks = slice(features + 256 * g, features + 256 * g + 256)
            val = dot(d[seq_rows(s), ks], block_diag(ql_ref[s, :, 256 * g : 256 * g + 256], masks))
            for i in range(2):
                p = s * pairs + 2 * g + i
                spread = land_rows(lambda r: kl_got[r, p])
                lane = features + 256 * g + 128 * i
                for m in range(marks):
                    spot = pl.ds(pl.multiple_of(s * rows + m * seg, seg), seg)
                    d[spot, lane : lane + 128] = (
                        val[m * seg : m * seg + seg, 128 * i : 128 * i + 128] + spread[m : m + 1]
                    ).astype(bf16)

    @pl.when((step >= at["values"]) & (step < at["values"] + seqs))
    def _():
        s = step - at["values"]
        masks = group_masks((M, 4 * E), 4, bf16)
        of = gn_of(s)
        for g in range(features // 256):
            gd = block_diag(jnp.concatenate([of(2 * g), of(2 * g + 1)], axis=1), masks)
            vs = slice(2 * features + 256 * g, 2 * features + 256 * g + 256)
            here = seq_rows(s)
            d[here, vs] = (
                dot(w_ref[0, :, 256 * g : 256 * g + 256], gd) + d[here, vs].astype(f32)
            ).astype(bf16)

    @pl.when(step == at["tok"])
    def _():
        load.wait()

    for when, stages in (
        (at["keys"] + 1, [(stage_b, 0)]),
        (at["conv_c"] + 1, [(stage_c, 0), (stage_b, 1)]),
        (at["conv_c"] + 4, [(stage_z, 0)]),
        (at["values"], [(stage_c, 1)]),
        (at["tok"], [(stage_z, 1)]),
        (at["tok"] + 1, [(stage_b, 2)]),
        (at["tok"] + 5, [(stage_c, 2)]),
    ):
        @pl.when(step == when)
        def _(stages=stages):
            for stage, p in stages:
                stage(p)

    @pl.when(step == at["conv_c"])
    def _():
        begin(ups[1])

    @pl.when((step == at["q"]) | (step == at["k"]) | (step == at["v"]))
    def _():
        p = jnp.where(step == at["q"], 0, jnp.where(step == at["k"], 1, 2))
        for c in range(2):
            cols = pl.ds(pl.multiple_of(p * features + 384 * c, 128), 384)
            low = dot(tok_t[...], d[:, cols]).astype(bf16)
            for i in range(2):
                for dd in range(8):
                    part[dd % 2, 4 * p + 2 * c + i, dd // 2] = fold(
                        low[96 * dd : 96 * dd + 96, 192 * i : 192 * i + 192]
                    )
        a_copy(p).start()

    @pl.when((step >= at["tok"]) & (step < last))
    def _():
        size = gtok_ref.shape[0]
        spot = pl.ds(pl.multiple_of((step - at["tok"]) * size, size), size)
        gtok_ref[...] = (proj_ref[...].astype(f32) + dot_nt(d[spot, :], wq_ref[...])).astype(bf16)

    def unfold(block):
        return jnp.concatenate([block[:, :192], block[:, 192:]], axis=0)

    def rank_sum(got):
        total = got[0].astype(f32)
        for r in range(1, ranks):
            total = total + got[r].astype(f32)
        return total

    @pl.when(step == last)
    def _():
        stage_z(2)
        for copy in small_spread():
            copy.wait()
        sm_got[3 + me] = sm_sum[3]
        small = (sm_got[3] + sm_got[4]) + (sm_got[5] + sm_got[6])
        taps_out[...] = small[:KW]
        ga_out[...] = small[KW : KW + 1].reshape(features)
        gf_out[...] = small[KW + 1 : KW + 2].reshape(features)
        for pair in downs + ups:
            finish(pair)
        down_out[...] = rank_sum(down_got)
        total = rank_sum(up_got)
        up_out[:, :384] = total[:96]
        up_out[:, 384:] = total[96:192]
        out_out[...] = unfold(total[192:240])
        for group in range(12):
            rank, copy = zq_copy(group)

            @pl.when(rank != me)
            def _(copy=copy):
                copy.wait_send()

        for o in range(1, ranks):
            source = lax.rem(me - o + ranks, ranks)
            for place in range(3):
                remote(
                    sum_c.at[0], got_z.at[source, place], zq_send.at[0], zq_recv.at[place, o], {"seq": source}
                ).wait_recv()
        for place in range(3):
            got_z[me, place] = sum_c[3 * me + place]
        qkv_out[...] = jnp.concatenate(
            [unfold(sum(got_z[r, place].astype(f32) for r in range(ranks))) for place in range(3)], axis=1
        )


def tail(
    gm, probs, q, mixed, q_land, k_land, rim, v, taps, saved, weights, k, tokens, proj, gain_a, gain_f, w_qkv, downs, ups
):
    seqs, rows, features = tokens.shape
    ranks = lax.axis_size("seq")
    pairs = features // 128
    count = seqs * pairs
    own = saved[0].shape[0]
    marks = M // ranks
    total = seqs * rows
    size = 256
    blocks = total // size
    at, plan, steps = tail_plan(seqs, pairs, blocks)
    clip = lambda i, name: jnp.clip(i - at[name], 0, seqs - 1)
    tile = lambda i: pick_tile(i, plan)
    by_seq = lambda shape, of: pl.BlockSpec((1,) + shape, lambda i: (of(i), 0, 0))
    head = lambda i: clip(i, "first")
    one = lambda i: clip(i, "one")
    both = lambda i: jnp.where(i < at["conv_c"], one(i), clip(i, "values"))
    conv_spec = pl.BlockSpec((1, rows, 128), lambda i: (tile(i) % seqs, 0, tile(i) // seqs))
    rim_spec = pl.BlockSpec((1, 2, RIM, 128), lambda i: (tile(i) % seqs, 0, 0, tile(i) // seqs))
    tap_spec = pl.BlockSpec((KW, 128), lambda i: (0, tile(i) // seqs))
    later = pl.BlockSpec((size, features), lambda i: (jnp.clip(i - at["tok"], 0, blocks - 1), 0))
    whole = lambda a: pl.BlockSpec(a.shape, lambda i: (0,) * len(a.shape), pipeline_mode=pl.Buffered(1))
    flat = (rows, features)
    vm = lambda *shape: pltpu.VMEM(shape, bf16)
    wide = lambda *shape: pltpu.VMEM(shape, f32)
    dma = pltpu.SemaphoreType.DMA
    shares = [
        jax.ShapeDtypeStruct(s, f32)
        for s in ((96, 768), (192, 384), (96, 192), (96, 576), (KW, 768), (768,), (768,))
    ]
    return pl.pallas_call(
        functools.partial(tail_kernel, seqs),
        grid=(steps,),
        in_specs=[
            by_seq(flat, head), by_seq((features, rows), head), by_seq(flat, head),
            pl.BlockSpec((pairs, M, 128), lambda i: (head(i), 0, 0)), whole(q_land), whole(k_land),
            conv_spec, rim_spec, conv_spec, tap_spec,
        ]
        + [whole(a) for a in saved]
        + [by_seq(flat, both), by_seq(flat, one), by_seq(flat, one), by_seq(flat, one), later]
        + [whole(gain_a), whole(gain_f), ANY, ANY, ANY],
        out_specs=[later] + [whole(a) for a in shares],
        out_shape=[jax.ShapeDtypeStruct((total, features), bf16)] + shares,
        scratch_shapes=[
            vm(total, 3 * features), vm(features, total), vm(*w_qkv.shape), wide(count, M, 128),
            vm(ranks * own, M, 128), vm(ranks, own, M, 128), vm(ranks, own, M, 128), vm(ranks, own, M, 128),
            wide(ranks, own, 8, 128), wide(ranks, 8, 128), wide(ranks, 8, 128), wide(own, M, 128), wide(own, M, 128),
            wide(own, M, 128), wide(own, M, 128), vm(count, M, 128), vm(ranks, count, marks, 128),
            wide(count, M, 128), vm(count, M, 128), vm(ranks, count, marks, 128), wide(rows + 2 * RIM, 128),
            wide(KW * 8, 128), wide(40, 128), wide(40, features), vm(4, 240, 384), vm(ranks, 240, 384),
            vm(ranks, 192, 384),
            vm(2, 12, 4, 48, 384), vm(12, 4, 48, 384), vm(12, 2, 2, 48, 384), vm(3, 2, 2, 2, 48, 384),
            vm(3, 2, 2, 2, 48, 384), vm(3, 2, 2, 48, 384), vm(12, 48, 384), vm(ranks, 3, 48, 384),
            wide(3 + ranks, 40, features), wide(4, 40, features),
        ]
        + stage_scratch(240)
        + [dma((1,))]
        + [rank_sems() for _ in range(9)]
        + [
            dma((3,)), dma((3,)), dma((2, 3, 2)), dma((2, 3, 2)), dma((12,)), dma((3, ranks)), dma((3,)), dma((3,)),
            rank_sems(),
        ],
        compiler_params=params(63 * MB, collective_id=5, has_side_effects=True),
        name="tail",
    )(
        gm, probs, q, mixed, q_land, k_land, gm, rim, v, taps, *saved, weights, v, k, tokens, proj, gain_a, gain_f,
        w_qkv, downs, ups,
    )


def halo(cells, width):
    count = lax.axis_size("seq")
    head, tail = cells[:, :width], cells[:, cells.shape[1] - width :]
    left = lax.ppermute(tail, "seq", [(i, i + 1) for i in range(count - 1)])
    right = lax.ppermute(head, "seq", [(i + 1, i) for i in range(count - 1)])
    return jnp.stack([left, right], axis=1)


def scatter_sum(grad):
    share = lax.psum_scatter(grad, "dp", scatter_dimension=0, tiled=True)
    return lax.psum_scatter(share, "seq", scatter_dimension=1, tiled=True).astype(f32)


def per_device_general(tokens, w_qkv, w_out, w_up, w_down, conv_filter, gain_att, gain_ffn, grad_out):
    seqs, rows, features = tokens.shape
    ranks = lax.axis_size("seq")
    rank = lax.axis_index("seq")
    marks = M // ranks
    ff = w_up.shape[1]
    pairs = seqs * (features // 128)
    own = -(-pairs // ranks)

    def from_pairs(x):
        x = x[:pairs].reshape(seqs, features // 128, M, 128).transpose(0, 2, 1, 3)
        return x.reshape(seqs, M, features)

    def pad_pairs(x):
        return jnp.pad(x, ((0, ranks * own - pairs),) + ((0, 0),) * (x.ndim - 1))

    def exchange(x):
        out = lax.all_to_all(pad_pairs(x), "seq", 0, 0, tiled=True)
        return out.reshape((ranks, own) + x.shape[1:])

    taps = conv_filter
    q, k, v, k_part, q_land, v_rim = project(tokens, w_qkv, marks)
    first_group = 4
    weights, probs, k_land, conv_a, num_parts, stat_parts = scores(
        q, k, v, q_land, k_part, v_rim, taps, own, first_group
    )
    mixed_pairs, conv_b, *saved = inverse(num_parts, stat_parts, q_land, k_land, v, v_rim, taps, first_group)
    mixed = mixed_pairs
    layer_out, proj, gm, wg, gains = row_pass(
        tokens, probs, conv_a, conv_b, mixed, grad_out, w_out, w_up, w_down, gain_att, gain_ffn
    )
    shape3 = (seqs, rows, features)
    gm = gm.reshape(shape3)
    chunks = ff // features
    up_share = scatter_sum(wg[:chunks].transpose(1, 0, 2).reshape(features, ff))
    down_share = scatter_sum(wg[chunks : 2 * chunks].transpose(0, 2, 1).reshape(ff, features))
    out_share = scatter_sum(wg[2 * chunks])
    land_part, gq, k_land_part = first_back(gm, probs, q, mixed, k_land)
    g_rim = halo(gm, RIM)
    land_parts = exchange(land_part)
    grad_conv, taps_grad = conv_back(gm, g_rim, v, taps)
    gn_own, gt_own, mid_q, mid_k = inverse_back(land_parts, q_land, k_land, saved)

    def give_back(x):
        x = x.reshape((ranks * own,) + x.shape[2:])
        return lax.all_to_all(x, "seq", 0, 0, tiled=True)[:pairs]

    grad_values, gk, q_land_part = third_back(
        weights, v, k, grad_conv, give_back(gn_own), give_back(gt_own), q_land
    )

    def place(x):
        full = jnp.zeros((ranks * own, M, 128), f32)
        return from_pairs(lax.dynamic_update_slice_in_dim(full, x, rank * own, 0))

    both = jnp.stack([q_land_part + place(mid_q), k_land_part + place(mid_k)]).astype(bf16)
    both = both.reshape(2, seqs, ranks, marks, features).transpose(2, 0, 1, 3, 4)
    both = lax.all_to_all(both, "seq", 0, 0, tiled=True).astype(f32).sum(0)
    grad_tokens, qkv_grad = last_pass(tokens, gq, gk, grad_values, both[0], both[1], proj.reshape(shape3), w_qkv)
    qkv_share = scatter_sum(qkv_grad.transpose(1, 0, 2).reshape(features, 3 * features))
    gains = gains.reshape(2, 8, features).sum(1)
    small = lax.psum(jnp.concatenate([taps_grad, gains]), ("dp", "seq"))
    return (
        layer_out.reshape(shape3),
        grad_tokens,
        qkv_share,
        out_share,
        up_share,
        down_share,
        small[:KW],
        small[KW],
        small[KW + 1],
    )


def deliver_kernel(*refs):
    count = len(refs) // 2
    for i in range(count):
        if i < 2:
            refs[count + i][...] = refs[i][...]
        else:
            @pl.when(pl.program_id(0) == 0)
            def _(i=i):
                refs[count + i][...] = refs[i][...]


def deliver(*arrays):
    steps = 4
    split = lambda a: pl.BlockSpec((a.shape[0] // steps, a.shape[1]), lambda i: (i, 0))
    whole = lambda a: pl.BlockSpec(a.shape, lambda i: (0,) * len(a.shape))
    specs = [split(a) for a in arrays[:2]] + [whole(a) for a in arrays[2:]]
    return pl.pallas_call(
        deliver_kernel,
        grid=(steps,),
        in_specs=specs,
        out_specs=specs,
        out_shape=[jax.ShapeDtypeStruct(a.shape, a.dtype) for a in arrays],
        compiler_params=params(62 * MB),
        name="deliver",
    )(*arrays)


def per_device(tokens, w_qkv, w_out, w_up, w_down, conv_filter, gain_att, gain_ffn, grad_out):
    seqs, rows, features = tokens.shape
    ranks = lax.axis_size("seq")
    marks = M // ranks
    pairs = seqs * (features // 128)
    own = -(-pairs // ranks)
    taps = conv_filter
    shape3 = (seqs, rows, features)

    q, k, v, weights, probs, q_land, k_land, v_rim, conv_out, mixed, *saved = front(tokens, w_qkv, taps, own)
    layer_out, normed, s_att, gdl, slope, hid_t, mix_t, gain_f, downs = rows_forward(
        tokens, probs, conv_out, mixed, grad_out, w_out, w_up, w_down, gain_att, gain_ffn
    )
    proj, gm, gain_a, downs, ups, g_rim = rows_backward(
        gdl, slope, normed, s_att, w_out, gain_att, w_down, w_up, hid_t, mix_t, downs.reshape(4, 2, 2, 192, 384), seqs
    )
    grad_tokens, up, down, out, qkv, taps_all, gain_att_all, gain_ffn_all = tail(
        gm.reshape(shape3), probs, q, mixed, q_land, k_land, g_rim, v, taps, saved, weights, k, tokens, proj, gain_a,
        gain_f, w_qkv, downs, ups.reshape(4, 2, 2, 240, 384),
    )
    layer_out, grad_tokens, qkv, out, up, down, taps_all, gain_att_all, gain_ffn_all = deliver(
        layer_out, grad_tokens, qkv, out, up, down, taps_all, gain_att_all, gain_ffn_all
    )
    return (
        layer_out.reshape(shape3),
        grad_tokens.reshape(shape3),
        qkv,
        out,
        up,
        down.T,
        taps_all,
        gain_att_all,
        gain_ffn_all,
    )


def solution(mesh):
    placed = (P("dp", "seq", None), P(), P(), P(), P(), P(), P(), P(), P("dp", "seq", None))
    eight_by_four = mesh.shape["dp"] == 8 and mesh.shape["seq"] == 4
    return jax.shard_map(
        per_device if eight_by_four else per_device_general,
        mesh=mesh,
        in_specs=placed,
        out_specs=(
            P("dp", "seq", None),
            P("dp", "seq", None),
            P("dp", "seq"),
            P("dp", "seq"),
            P("dp", "seq"),
            P("dp", "seq"),
            P(),
            P(),
            P(),
        ),
        check_vma=False,
    )
```

```python
import functools

import jax
import jax.numpy as jnp
from jax import lax
from jax.experimental import pallas as pl
from jax.experimental.pallas import tpu as pltpu
from jax.sharding import PartitionSpec as P

H = 12
E = 64
M = 64
KW = 33
RIM = KW // 2
NEWTON = 6

f32 = jnp.float32
bf16 = jnp.bfloat16
epsilon = 1e-05
root_half = 0.7071067811865476
inv_root_two_pi = 0.3989422804014327
MB = 1 << 20

ERFC_P = 0.6
ERFC_C = (0.37028039425845705, 0.14043533559747823, 0.7278464793107866, -0.23856251479455173)
log2_e = 1.4426950408889634


def dot(a, b):
    return lax.dot_general(a, b, (((1,), (0,)), ((), ())), preferred_element_type=f32)


def dot_nt(a, b):
    return lax.dot_general(a, b, (((1,), (1,)), ((), ())), preferred_element_type=f32)


def dot_tn(a, b):
    return lax.dot_general(a, b, (((0,), (0,)), ((), ())), preferred_element_type=f32)


def lane_group(shape):
    return lax.broadcasted_iota(jnp.int32, shape, len(shape) - 1) // E


def group_masks(shape, count, dtype):
    groups = lane_group(shape)
    return [(groups == h).astype(f32).astype(dtype) for h in range(count)]


def block_diag(x, masks):
    return jnp.concatenate([x * m for m in masks], axis=0)


def diag_blocks(n, masks):
    return sum(n[E * h : E * h + E] * m for h, m in enumerate(masks))


def quad(ref, g):
    return jnp.concatenate([ref[2 * g], ref[2 * g + 1]], axis=1)


def params(limit=None, **kw):
    return pltpu.CompilerParams(vmem_limit_bytes=limit, **kw)


MESH = pl.DeviceIdType.MESH
ANY = pl.BlockSpec(memory_space=pl.ANY)


def seq_place():
    return lax.axis_index("seq"), lax.axis_size("seq")


def seq_peers():
    me, count = seq_place()
    return [(o, lax.rem(me + o, count)) for o in range(1, count)]


def greet(extra=()):
    barrier = pltpu.get_barrier_semaphore()
    targets = [{"seq": peer} for _, peer in seq_peers()] + list(extra)
    for target in targets:
        pl.semaphore_signal(barrier, inc=1, device_id=target, device_id_type=MESH)
    pl.semaphore_wait(barrier, len(targets))


def remote(src, dst, send, recv, target):
    return pltpu.make_async_remote_copy(
        src_ref=src, dst_ref=dst, send_sem=send, recv_sem=recv, device_id=target, device_id_type=MESH
    )


def swap_copies(src, dst, own, sems):
    me, count = seq_place()
    copies = [
        remote(src.at[pl.ds(peer * own, own)], dst.at[me], sems.at[0, o], sems.at[1, o], {"seq": peer})
        for o, peer in seq_peers()
    ]
    return copies, pltpu.make_async_copy(src.at[pl.ds(me * own, own)], dst.at[me], sems.at[0, 0])


def spread_copies(src, dst, own, sems):
    me, count = seq_place()
    at = dst.at[pl.ds(me * own, own)]
    copies = [
        remote(src, at, sems.at[0, o], sems.at[1, o], {"seq": peer}) for o, peer in seq_peers()
    ]
    return copies, pltpu.make_async_copy(src, at, sems.at[0, 0])


def begin(pair):
    for copy in pair[0]:
        copy.start()
    pair[1].start()


def finish(pair):
    for copy in pair[0]:
        copy.wait()
    pair[1].wait()


def swap_rows(src, dst, sems):
    me, _ = seq_place()
    copies = [
        remote(src.at[peer], dst.at[me], sems.at[0, o], sems.at[1, o], {"seq": peer}) for o, peer in seq_peers()
    ]
    return copies, pltpu.make_async_copy(src.at[me], dst.at[me], sems.at[0, 0])


def cube():
    d = lax.axis_index("dp")
    core, x, y = d % 2, (d // 2) % 2, d // 4
    return core, x, y, {"dp": d + 1 - 2 * core}, {"dp": d + 2 - 4 * x}, {"dp": d + 4 - 8 * y}


def add_low(a, b):
    return (a.astype(f32) + b.astype(f32)).astype(bf16)


def rank_sems():
    return pltpu.SemaphoreType.DMA((2, lax.axis_size("seq")))


def project_kernel(
    tok_ref, w_ref, q_ref, k_ref, v_ref, kl_ref, land_out, rim_out, land, rim, send, recv, local, rim_send, rim_recv,
    rim_local,
):
    step = pl.program_id(0)
    seqs = pl.num_programs(0)
    me, count = seq_place()
    rows, features = tok_ref.shape[1:]
    marks = land.shape[1]
    seg = rows // marks

    @pl.when(step == 0)
    def _():
        greet()

    x = tok_ref[0]
    for part, out in enumerate((q_ref, k_ref, v_ref)):
        for c in range(0, features, 256):
            p = dot(x, w_ref[:, part * features + c : part * features + c + 256])
            if part == 0:
                p = 0.125 * p
            low = p.astype(bf16)
            out[0, :, c : c + 256] = low
            if part < 2:
                total = low.astype(f32).reshape(marks, seg, 256).sum(1)
                mean = (total * (1.0 / seg)).astype(bf16)
                if part == 0:
                    land[step, :, c : c + 256] = mean
                else:
                    kl_ref[0, :, c : c + 256] = mean
            else:
                rim[step, 0, :, c : c + 256] = low[rows - RIM :]
                rim[step, 1, :, c : c + 256] = low[:RIM]

    def copies(s):
        spot = land_out.at[s, pl.ds(me * marks, marks)]
        sends = [
            remote(land.at[s], spot, send.at[s, o], recv.at[s, o], {"seq": peer}) for o, peer in seq_peers()
        ]
        return sends, pltpu.make_async_copy(land.at[s], spot, local.at[s])

    def rim_copy(s, side):
        there = lax.rem(me + (1 if side == 0 else count - 1), count)
        return remote(
            rim.at[s, side], rim_out.at[s, side], rim_send.at[s, side], rim_recv.at[s, side], {"seq": there}
        )

    begin(copies(step))
    for side in range(2):
        rim_copy(step, side).start()

    @pl.when(step == seqs - 1)
    def _():
        def drain(s, carry):
            finish(copies(s))
            for side in range(2):
                rim_copy(s, side).wait()
            return carry

        lax.fori_loop(0, seqs, drain, 0)


def project(tokens, w_qkv, marks):
    seqs, rows, features = tokens.shape
    ranks = lax.axis_size("seq")
    full = pl.BlockSpec((1, rows, features), lambda s: (s, 0, 0))
    dma = pltpu.SemaphoreType.DMA
    return pl.pallas_call(
        project_kernel,
        grid=(seqs,),
        in_specs=[full, pl.BlockSpec(w_qkv.shape, lambda s: (0, 0), pipeline_mode=pl.Buffered(1))],
        out_specs=[full] * 3 + [pl.BlockSpec((1, marks, features), lambda s: (s, 0, 0))] + [ANY] * 2,
        out_shape=[jax.ShapeDtypeStruct(tokens.shape, bf16)] * 3
        + [
            jax.ShapeDtypeStruct((seqs, marks, features), bf16),
            jax.ShapeDtypeStruct((seqs, M, features), bf16),
            jax.ShapeDtypeStruct((seqs, 2, RIM, features), bf16),
        ],
        scratch_shapes=[
            pltpu.VMEM((seqs, marks, features), bf16), pltpu.VMEM((seqs, 2, RIM, features), bf16),
            dma((seqs, ranks)), dma((seqs, ranks)), dma((seqs,)), dma((seqs, 2)), dma((seqs, 2)), dma((seqs,)),
        ],
        compiler_params=params(62 * MB, collective_id=0, has_side_effects=True),
        name="project",
    )(tokens, w_qkv)


def fill_taps(taps, f_ref):
    taps[0:KW, :] = f_ref[...].astype(f32)


def fill_pad(pad, x_ref, rim_ref):
    rows = x_ref.shape[1]
    me, count = seq_place()
    pad[0:RIM, :] = jnp.where(me > 0, rim_ref[0, 0].astype(f32), 0.0)
    pad[RIM : RIM + rows, :] = x_ref[0].astype(f32)
    pad[RIM + rows : RIM + rows + RIM, :] = jnp.where(me < count - 1, rim_ref[0, 1].astype(f32), 0.0)


def conv_tile(v_ref, rim_ref, taps_ref, o_ref, pad, f_ref):
    rows = v_ref.shape[1]
    fill_pad(pad, v_ref, rim_ref)
    fill_taps(f_ref, taps_ref)
    conv_rows(o_ref, pad, f_ref, rows)


def conv_rows(o_ref, pad, f_ref, rows):
    for c in range(0, rows, 64):
        acc = jnp.zeros((64, 128), f32)
        for j in range(KW):
            acc = acc + f_ref[j : j + 1, :] * pad[c + j : c + j + 64, :]
        o_ref[0, c : c + 64, :] = acc.astype(bf16)


def conv_specs(rows, first_step, first_group, groups):
    at = lambda i: jnp.maximum(i - first_step, 0)
    seq = lambda i: at(i) // groups
    group = lambda i: at(i) % groups
    return (
        pl.BlockSpec((1, rows, 128), lambda i: (seq(i), 0, first_group + group(i))),
        pl.BlockSpec((1, 2, RIM, 128), lambda i: (seq(i), 0, 0, first_group + group(i))),
        pl.BlockSpec((KW, 128), lambda i: (0, first_group + group(i))),
        pl.BlockSpec((1, rows, 128), lambda i: (seq(i), 0, group(i))),
    )


def conv_back_rows(seq, seqs, g_ref, rim_ref, v_ref, taps_ref, put, put_taps, pad, facc, f_ref):
    rows = v_ref.shape[1]
    fill_pad(pad, g_ref, rim_ref)
    fill_taps(f_ref, taps_ref)

    @pl.when(seq == 0)
    def _():
        facc[...] = jnp.zeros_like(facc)

    for c in range(0, rows, 64):
        acc = jnp.zeros((64, 128), f32)
        vals = v_ref[0, c : c + 64, :].astype(f32)
        for j in range(KW):
            moved = pad[c + 2 * RIM - j : c + 2 * RIM - j + 64, :]
            acc = acc + f_ref[j : j + 1, :] * moved
            facc[8 * j : 8 * j + 8, :] += (vals * moved).reshape(8, 8, 128).sum(0)
        put(c, acc.astype(bf16))

    @pl.when(seq == seqs - 1)
    def _():
        put_taps(facc[...].reshape(KW, 8, 128).sum(1))


def conv_back_tile(seq, seqs, g_ref, rim_ref, v_ref, taps_ref, o_ref, gf_ref, pad, facc, f_ref):
    def put(c, v):
        o_ref[0, c : c + 64, :] = v

    def put_taps(v):
        gf_ref[...] = v

    conv_back_rows(seq, seqs, g_ref, rim_ref, v_ref, taps_ref, put, put_taps, pad, facc, f_ref)


def conv_back_kernel(g_ref, rim_ref, v_ref, f_ref, o_ref, gf_ref, pad, facc, taps):
    conv_back_tile(
        pl.program_id(1), pl.num_programs(1), g_ref, rim_ref, v_ref, f_ref, o_ref, gf_ref, pad, facc, taps
    )


def conv_back_specs(rows, seqs, first_step, first_group):
    at = lambda i: jnp.maximum(i - first_step, 0)
    seq = lambda i: at(i) % seqs
    group = lambda i: at(i) // seqs
    return (
        pl.BlockSpec((1, rows, 128), lambda i: (seq(i), 0, first_group + group(i))),
        pl.BlockSpec((1, 2, RIM, 128), lambda i: (seq(i), 0, 0, first_group + group(i))),
        pl.BlockSpec((KW, 128), lambda i: (0, first_group + group(i))),
        pl.BlockSpec((1, rows, 128), lambda i: (seq(i), 0, group(i))),
        pl.BlockSpec((KW, 128), lambda i: (0, group(i))),
    )


def conv_back(g, rim, v, taps):
    seqs, rows, features = v.shape
    sp = lambda n: pl.BlockSpec((1, n, 128), lambda g, s: (s, 0, g))
    fs = pl.BlockSpec((KW, 128), lambda g, s: (0, g))
    return pl.pallas_call(
        conv_back_kernel,
        grid=(features // 128, seqs),
        in_specs=[sp(rows), pl.BlockSpec((1, 2, RIM, 128), lambda g, s: (s, 0, 0, g)), sp(rows), fs],
        out_specs=[sp(rows), fs],
        out_shape=[jax.ShapeDtypeStruct(v.shape, bf16), jax.ShapeDtypeStruct((KW, features), f32)],
        scratch_shapes=[pltpu.VMEM((rows + 2 * RIM, 128), f32), pltpu.VMEM((KW * 8, 128), f32), pltpu.VMEM((40, 128), f32)],
        name="conv_back",
    )(g, rim, v, taps)


def third_score_step(step, k_ref, v_ref, ql_ref, w_ref, num_ref, stat_ref, own):
    features = k_ref.shape[2]
    pairs = features // 128
    masks = group_masks((M, 4 * E), 4, bf16)
    masks_wide = group_masks((M, 4 * E), 4, f32)
    for g in range(features // 256):
        sl = slice(256 * g, 256 * g + 256)
        s3 = dot_nt(k_ref[0, :, sl], block_diag(ql_ref[0, :, sl], masks))
        peak = jnp.max(s3, axis=0, keepdims=True)
        e3 = jnp.exp(s3 - peak)
        total = jnp.sum(e3, axis=0, keepdims=True)
        low = e3.astype(bf16)
        w_ref[0, :, sl] = low
        num = diag_blocks(dot_tn(low, v_ref[0, :, sl]), masks_wide).astype(bf16)
        for i in range(2):
            lanes = slice(128 * i, 128 * i + 128)
            p = step * pairs + 2 * g + i
            num_ref[p] = num[:, lanes]
            stat_ref[p // own, pl.ds(p % own, 1), :] = peak[:, lanes]
            stat_ref[p // own, pl.ds(8 + p % own, 1), :] = total[:, lanes]


def first_score_step(q_ref, kl, p_ref):
    features = q_ref.shape[2]
    masks = group_masks((M, 4 * E), 4, bf16)
    for g in range(features // 256):
        sl = slice(256 * g, 256 * g + 256)
        s1 = dot_nt(block_diag(kl[:, sl], masks), q_ref[0, :, sl])
        for h in range(4):
            x = s1[E * h : E * h + E]
            e1 = jnp.exp(x - jnp.max(x, axis=0, keepdims=True))
            at = 256 * g + E * h
            p_ref[0, at : at + E, :] = (e1 * (1.0 / jnp.sum(e1, axis=0, keepdims=True))).astype(bf16)


def scores_kernel(
    seqs, own, q_ref, k_ref, v_ref, ql_ref, kp_ref, cv_ref, rim_ref, f_ref, w_ref, p_ref, kl_ref, co_ref, num_out,
    stat_out, num, stat, kl, pad, taps, num_sems, stat_sems, kl_sems,
):
    step = pl.program_id(0)
    steps = pl.num_programs(0)
    pairs = q_ref.shape[2] // 128
    marks = kp_ref.shape[1]
    me, _ = seq_place()

    def mark_copies():
        spot = kl.at[:, pl.ds(me * marks, marks)]
        sends = [
            remote(kp_ref, spot, kl_sems.at[0, o], kl_sems.at[1, o], {"seq": peer}) for o, peer in seq_peers()
        ]
        return sends, pltpu.make_async_copy(kp_ref, spot, kl_sems.at[0, 0])

    @pl.when(step == 0)
    def _():
        greet()
        begin(mark_copies())
        stat[...] = jnp.zeros_like(stat)
        if num.shape[0] > seqs * pairs:
            num[seqs * pairs :] = jnp.zeros_like(num[seqs * pairs :])

    @pl.when(step < seqs)
    def _():
        third_score_step(step, k_ref, v_ref, ql_ref, w_ref, num, stat, own)

    @pl.when(step == seqs - 1)
    def _():
        begin(swap_copies(num, num_out, own, num_sems))
        begin(swap_rows(stat, stat_out, stat_sems))

    @pl.when(step == seqs)
    def _():
        finish(mark_copies())
        kl_ref[...] = kl[...]

    @pl.when((step >= seqs) & (step < 2 * seqs))
    def _():
        first_score_step(q_ref, kl[step - seqs], p_ref)

    @pl.when(step >= 2 * seqs)
    def _():
        conv_tile(cv_ref, rim_ref, f_ref, co_ref, pad, taps)

    @pl.when(step == steps - 1)
    def _():
        finish(swap_copies(num, num_out, own, num_sems))
        finish(swap_rows(stat, stat_out, stat_sems))


def scores(q, k, v, q_land, k_part, rim, taps, own, groups):
    seqs, rows, features = q.shape
    marks = k_part.shape[1]
    ranks = lax.axis_size("seq")
    here = lambda i: jnp.minimum(i, seqs - 1)
    then = lambda i: jnp.clip(i - seqs, 0, seqs - 1)
    full = pl.BlockSpec((1, rows, features), lambda i: (here(i), 0, 0))
    next_full = pl.BlockSpec((1, rows, features), lambda i: (then(i), 0, 0))
    whole = lambda a: pl.BlockSpec(a.shape, lambda i: (0,) * len(a.shape), pipeline_mode=pl.Buffered(1))
    k_land = jax.ShapeDtypeStruct((seqs, M, features), bf16)
    cv, rims, ft, co = conv_specs(rows, 2 * seqs, 0, groups)
    return pl.pallas_call(
        functools.partial(scores_kernel, seqs, own),
        grid=(2 * seqs + seqs * groups,),
        in_specs=[
            next_full, full, full, pl.BlockSpec((1, M, features), lambda i: (here(i), 0, 0)), whole(k_part), cv,
            rims, ft,
        ],
        out_specs=[full, pl.BlockSpec((1, features, rows), lambda i: (then(i), 0, 0)), whole(k_land), co, ANY, ANY],
        out_shape=[
            jax.ShapeDtypeStruct(q.shape, bf16),
            jax.ShapeDtypeStruct((seqs, features, rows), bf16),
            k_land,
            jax.ShapeDtypeStruct((seqs, rows, 128 * groups), bf16),
            jax.ShapeDtypeStruct((ranks, own, M, 128), bf16),
            jax.ShapeDtypeStruct((ranks, 16, 128), f32),
        ],
        scratch_shapes=[
            pltpu.VMEM((ranks * own, M, 128), bf16), pltpu.VMEM((ranks, 16, 128), f32),
            pltpu.VMEM((seqs, M, features), bf16), pltpu.VMEM((rows + 2 * RIM, 128), f32),
            pltpu.VMEM((40, 128), f32), rank_sems(), rank_sems(), rank_sems(),
        ],
        compiler_params=params(62 * MB, collective_id=1, has_side_effects=True),
        name="scores",
    )(q, k, v, q_land, k_part, v, rim, taps)


def split(x):
    hi = x.astype(bf16)
    return hi, (x - hi.astype(f32)).astype(bf16)


def stack_parts(xs, axis):
    return jnp.concatenate([part for x in xs for part in split(x)], axis=axis)


def pair_sums(out, count):
    top = lambda i, j: out[128 * i + 64 * j : 128 * i + 64 * j + 64]
    return [
        top(i, 0)[:, :128] + (top(i, 0)[:, 128:] + top(i, 1)[:, :128]) for i in range(count)
    ]


def pair_nn(lefts, right, masks):
    hi, lo = split(right)
    packed = jnp.concatenate([block_diag(hi, masks), block_diag(lo, masks)], axis=1)
    return pair_sums(dot(stack_parts(lefts, 0), packed), len(lefts))


def pair_nt(lefts, right, masks):
    hi, lo = split(right)
    packed = jnp.concatenate([block_diag(hi, masks), block_diag(lo, masks)], axis=0)
    return pair_sums(dot_nt(stack_parts(lefts, 0), packed), len(lefts))


def pair_tn(left, rights, masks_wide):
    out = dot_tn(stack_parts([left], 1), stack_parts(rights, 1))
    results = []
    for i in range(len(rights)):
        full = out[:128, 256 * i : 256 * i + 128] + (
            out[:128, 256 * i + 128 : 256 * i + 256] + out[128:, 256 * i : 256 * i + 128]
        )
        results.append(diag_blocks(full, masks_wide))
    return results


def half_reduce(x, upper, op, fill):
    a = op(jnp.where(upper, fill, x), axis=1, keepdims=True)
    b = op(jnp.where(upper, x, fill), axis=1, keepdims=True)
    return jnp.where(upper, b, a)


def to_column(row, same, upper):
    return half_reduce(jnp.where(same, row, 0.0), upper, jnp.sum, 0.0)


def to_row(col, same):
    return jnp.sum(jnp.where(same, col, 0.0), axis=0, keepdims=True)


def pair_consts():
    lane = lax.broadcasted_iota(jnp.int32, (M, 128), 1)
    row = lax.broadcasted_iota(jnp.int32, (M, 128), 0)
    return lane >= E, row == lane % E, group_masks((M, 128), 2, bf16), group_masks((M, 128), 2, f32)


def own_pair(land_ref, i, own):
    me, _ = seq_place()
    per = land_ref.shape[2] // 128
    p = jnp.minimum(me * own + i, land_ref.shape[0] * per - 1)
    return land_ref[p // per, :, pl.ds(pl.multiple_of((p % per) * 128, 128), 128)]


def inverse_step(
    num_ref, stat_ref, ql_ref, kl_ref, mixed_ref, sum_ref, mid_ref, z_ref, p_ref, a_ref, w_ref,
    scale_ref, tot_ref, alpha_ref,
):
    ranks, own = num_ref.shape[:2]
    upper, same, masks, masks_wide = pair_consts()
    for i in range(own):
        peak = stat_ref[0, i : i + 1, :]
        for r in range(1, ranks):
            peak = jnp.maximum(peak, stat_ref[r, i : i + 1, :])
        total = jnp.zeros((1, 128), f32)
        numer = jnp.zeros((M, 128), f32)
        for r in range(ranks):
            alpha = jnp.exp(stat_ref[r, i : i + 1, :] - peak)
            total = total + alpha * stat_ref[r, 8 + i : 9 + i, :]
            column = to_column(alpha, same, upper)
            alpha_ref[r, i] = column
            numer = numer + column * num_ref[r, i].astype(f32)
        total = to_column(total, same, upper)
        tot_ref[i] = total
        sum_ref[i] = numer / total
        ql, kl = own_pair(ql_ref, i, own), own_pair(kl_ref, i, own)
        s2 = dot_nt(ql, block_diag(kl, masks))
        e2 = jnp.exp(s2 - half_reduce(s2, upper, jnp.max, -jnp.inf))
        middle = e2 / half_reduce(e2, upper, jnp.sum, 0.0)
        mid_ref[i] = middle
        st = dot_nt(kl, block_diag(ql, masks))
        et = jnp.exp(st - jnp.max(st, axis=0, keepdims=True))
        flipped = et / jnp.sum(et, axis=0, keepdims=True)
        column = jnp.sum(middle, axis=0, keepdims=True)
        scale = 1.0 / half_reduce(column, upper[0:1], jnp.max, -jnp.inf)
        scale_ref[i] = jnp.broadcast_to(scale, (8, 128))
        z_ref[0, i] = flipped * scale

    def step(it, carry):
        zs = [z_ref[it, i] for i in range(own)]
        ps = [pair_nn([mid_ref[i]], zs[i], masks)[0] for i in range(own)]
        second = [pair_nn([ps[i], zs[i]], ps[i], masks) for i in range(own)]
        for i in range(own):
            p2, a = second[i]
            w = 7.0 * ps[i] - p2
            p_ref[it, i] = ps[i]
            a_ref[it, i] = a
            w_ref[it, i] = w
            z_ref[it + 1, i] = 0.25 * (13.0 * zs[i] - 15.0 * a + pair_nn([a], w, masks)[0])
        return carry

    lax.fori_loop(0, NEWTON, step, 0)
    for i in range(own):
        mixed_ref[i] = pair_nn([z_ref[NEWTON, i]], sum_ref[i], masks)[0].astype(bf16)


def inverse_kernel(
    num_ref, stat_ref, ql_ref, kl_ref, cv_ref, rim_ref, f_ref, mixed_out, co_ref, sum_ref, mid_ref, z_ref, p_ref,
    a_ref, w_ref, scale_ref, tot_ref, alpha_ref, mixed, pad, taps, sems,
):
    step = pl.program_id(0)
    own = num_ref.shape[1]

    @pl.when(step == 0)
    def _():
        greet()
        inverse_step(
            num_ref, stat_ref, ql_ref, kl_ref, mixed, sum_ref, mid_ref, z_ref, p_ref, a_ref, w_ref, scale_ref,
            tot_ref, alpha_ref,
        )
        begin(spread_copies(mixed, mixed_out, own, sems))

    @pl.when(step > 0)
    def _():
        conv_tile(cv_ref, rim_ref, f_ref, co_ref, pad, taps)

    @pl.when(step == pl.num_programs(0) - 1)
    def _():
        finish(spread_copies(mixed, mixed_out, own, sems))


def inverse(num, stat, q_land, k_land, v, rim, taps, first_group):
    ranks, own = num.shape[:2]
    seqs, rows, features = v.shape
    groups = features // 128 - first_group
    mat = jax.ShapeDtypeStruct((own, M, 128), f32)
    steps = lambda n: jax.ShapeDtypeStruct((n, own, M, 128), f32)
    whole = lambda a: pl.BlockSpec(a.shape, lambda i: (0,) * len(a.shape), pipeline_mode=pl.Buffered(1))
    saved = [
        mat, mat, steps(NEWTON + 1), steps(NEWTON), steps(NEWTON), steps(NEWTON),
        jax.ShapeDtypeStruct((own, 8, 128), f32), mat, steps(ranks),
    ]
    cv, rims, ft, co = conv_specs(rows, 1, first_group, groups)
    return pl.pallas_call(
        inverse_kernel,
        grid=(1 + seqs * groups,),
        in_specs=[whole(num), whole(stat), whole(q_land), whole(k_land), cv, rims, ft],
        out_specs=[ANY, co] + [whole(a) for a in saved],
        out_shape=[
            jax.ShapeDtypeStruct((ranks * own, M, 128), bf16),
            jax.ShapeDtypeStruct((seqs, rows, 128 * groups), bf16),
        ]
        + saved,
        scratch_shapes=[
            pltpu.VMEM((own, M, 128), bf16), pltpu.VMEM((rows + 2 * RIM, 128), f32), pltpu.VMEM((40, 128), f32),
            rank_sems(),
        ],
        compiler_params=params(62 * MB, collective_id=2, has_side_effects=True),
        name="inverse",
    )(num, stat, q_land, k_land, v, rim, taps)


def inverse_back_step(
    land_ref, ql_ref, kl_ref, sum_ref, mid_ref, z_ref, p_ref, a_ref, w_ref, scale_ref, tot_ref,
    alpha_ref, gn_ref, gt_ref, mq_ref, mk_ref, g_ref, dk_ref, shared=lambda: None,
):
    ranks, own = land_ref.shape[:2]
    upper, same, masks, masks_wide = pair_consts()
    for i in range(own):
        land = land_ref[0, i].astype(f32)
        for r in range(1, ranks):
            land = land + land_ref[r, i].astype(f32)
        summary, total = sum_ref[i], tot_ref[i]
        gs = pair_tn(z_ref[NEWTON, i], [land], masks_wide)[0].astype(bf16).astype(f32)
        gn = (gs / total).astype(bf16).astype(f32)
        gt = -half_reduce(gs * summary, upper, jnp.sum, 0.0) / total
        for r in range(ranks):
            gn_ref[r, i] = (alpha_ref[r, i] * gn).astype(bf16)
            gt_ref[r, i] = jnp.broadcast_to(to_row(alpha_ref[r, i] * gt, same), (8, 128))
        g_ref[i] = pair_nt([land], summary, masks)[0]
        dk_ref[i] = jnp.zeros((M, 128), f32)
    shared()

    def step(back, carry):
        it = NEWTON - 1 - back
        gs = [g_ref[i] for i in range(own)]
        das, dws = [], []
        for i in range(own):
            das.append(0.25 * (pair_nt([gs[i]], w_ref[it, i], masks)[0] - 15.0 * gs[i]))
            dws.append(0.25 * pair_tn(a_ref[it, i], [gs[i]], masks_wide)[0])
        dps, parts = [], []
        for i in range(own):
            right = pair_nt([dws[i], das[i]], p_ref[it, i], masks)
            left = pair_tn(p_ref[it, i], [dws[i]], masks_wide)[0]
            dps.append(7.0 * dws[i] - right[0] - left + pair_tn(z_ref[it, i], [das[i]], masks_wide)[0])
            parts.append(3.25 * gs[i] + right[1])
        for i in range(own):
            g_ref[i] = parts[i] + pair_tn(mid_ref[i], [dps[i]], masks_wide)[0]
            dk_ref[i] += pair_nt([dps[i]], z_ref[it, i], masks)[0]
        return carry

    lax.fori_loop(0, NEWTON, step, 0)
    eye = jnp.where(same, 1.0, 0.0).astype(bf16)
    for i in range(own):
        g, middle, scale = g_ref[i], mid_ref[i], scale_ref[i, 0:1, :]
        turned = dot_tn(stack_parts([g], 1), eye)
        turned = diag_blocks(turned[:128] + turned[128:], masks_wide)
        column = jnp.sum(middle, axis=0, keepdims=True)
        top = half_reduce(column, upper[0:1], jnp.max, -jnp.inf)
        hit = jnp.where(column == top, 1.0, 0.0)
        share = hit / half_reduce(hit, upper[0:1], jnp.sum, 0.0)
        d_scale = half_reduce(jnp.sum(turned * middle, axis=0, keepdims=True), upper[0:1], jnp.sum, 0.0)
        dk = dk_ref[i] + turned * scale - share * (d_scale * scale * scale)
        ds = middle * (dk - half_reduce(middle * dk, upper, jnp.sum, 0.0))
        hi, lo = split(ds)
        both = dot(jnp.concatenate([hi, lo], axis=0), block_diag(own_pair(kl_ref, i, own), masks))
        mq_ref[i] = both[:M] + both[M:]
        turned = dot_tn(jnp.concatenate([hi, lo], axis=1), own_pair(ql_ref, i, own))
        mk_ref[i] = diag_blocks(turned[:128] + turned[128:], masks_wide)


def inverse_back(land, q_land, k_land, saved):
    ranks, own = land.shape[:2]
    mat = jax.ShapeDtypeStruct((own, M, 128), f32)
    return pl.pallas_call(
        inverse_back_step,
        out_shape=[
            jax.ShapeDtypeStruct((ranks, own, M, 128), bf16),
            jax.ShapeDtypeStruct((ranks, own, 8, 128), f32), mat, mat,
        ],
        scratch_shapes=[pltpu.VMEM((own, M, 128), f32)] * 2,
        compiler_params=params(62 * MB),
        name="inverse_back",
    )(land, q_land, k_land, *saved)


def pick_tile(step, plan):
    tile = 0
    done = 0
    for first, count in plan:
        tile = tile + jnp.clip(step - first, -1 if done else 0, count - 1) + (1 if done else 0)
        done += count
    return tile


def front_kernel(
    tok_ref, wq_ref, f_ref,
    q_ref, k_ref, v_ref, w_ref, p_ref, ql_out, kl_out, rim_out, conv_ref, mixed_out, sum_ref, mid_ref, z_ref, zp_ref,
    za_ref, zw_ref, scale_ref, tot_ref, alpha_ref,
    land_q, land_k, ql, kl, rim, rims, num, stat, num_got, stat_got, mixed, pad, taps,
    q_sems, k_sems, rim_send, rim_recv, num_sems, stat_sems, mixed_sems, *, plan, at_third, at_first, at_inverse,
):
    step = pl.program_id(0)
    seqs, rows, features = q_ref.shape
    marks = land_q.shape[1]
    seg = rows // marks
    pairs = features // 128
    own = num_got.shape[1]
    me, count = seq_place()

    def mark_copies(src, dst, sems, s):
        spot = dst.at[s, pl.ds(me * marks, marks)]
        sends = [
            remote(src.at[s], spot, sems.at[0, s, o], sems.at[1, s, o], {"seq": peer}) for o, peer in seq_peers()
        ]
        return sends, pltpu.make_async_copy(src.at[s], spot, sems.at[0, s, 0])

    def rim_copy(s, side):
        there = lax.rem(me + (1 if side == 0 else count - 1), count)
        return remote(
            rim.at[s, side], rims.at[s, side], rim_send.at[s, side], rim_recv.at[s, side], {"seq": there}
        )

    def has_next(side):
        return me < count - 1 if side == 0 else me > 0

    @pl.when(step == 0)
    def _():
        rims[...] = jnp.zeros_like(rims)
        greet()
        stat[...] = jnp.zeros_like(stat)
        num[seqs * pairs :] = jnp.zeros_like(num[seqs * pairs :])

    @pl.when(step < seqs)
    def _():
        x = tok_ref[0]
        for part, out in enumerate((q_ref, k_ref, v_ref)):
            for c in range(0, features, 256):
                p = dot(x, wq_ref[:, part * features + c : part * features + c + 256])
                if part == 0:
                    p = 0.125 * p
                low = p.astype(bf16)
                out[step, :, c : c + 256] = low
                if part < 2:
                    total = low.astype(f32).reshape(marks, seg, 256).sum(1)
                    (land_q, land_k)[part][step, :, c : c + 256] = (total * (1.0 / seg)).astype(bf16)
                else:
                    rim[step, 0, :, c : c + 256] = low[rows - RIM :]
                    rim[step, 1, :, c : c + 256] = low[:RIM]
        begin(mark_copies(land_q, ql, q_sems, step))

        @pl.when(step > 0)
        def _():
            for side in range(2):
                @pl.when(has_next(side))
                def _(side=side):
                    rim_copy(step, side).start()

    @pl.when(step == 1)
    def _():
        for side in range(2):
            @pl.when(has_next(side))
            def _(side=side):
                rim_copy(0, side).start()

    @pl.when(step == seqs)
    def _():
        for s in range(seqs):
            begin(mark_copies(land_k, kl, k_sems, s))

    tile = pick_tile(step, plan)
    seq, group = tile // pairs, tile % pairs
    for first, tiles in plan:
        @pl.when((step >= first) & (step < first + tiles))
        def _():
            @pl.when(group == 0)
            def _():
                for side in range(2):
                    @pl.when(has_next(side))
                    def _(side=side):
                        rim_copy(seq, side).wait_send()

                    @pl.when(has_next(1 - side))
                    def _(side=side):
                        rim_copy(seq, side).wait_recv()

            lanes = pl.ds(pl.multiple_of(group * 128, 128), 128)
            taps[0:KW, :] = f_ref[:, lanes].astype(f32)
            pad[0:RIM, :] = rims[seq, 0, :, lanes].astype(f32)
            pad[RIM : RIM + rows, :] = v_ref[seq, :, lanes].astype(f32)
            pad[RIM + rows : RIM + rows + RIM, :] = rims[seq, 1, :, lanes].astype(f32)
            conv_rows(conv_ref, pad, taps, rows)

    @pl.when(step == at_third)
    def _():
        for s in range(seqs):
            finish(mark_copies(land_q, ql, q_sems, s))
        ql_out[...] = ql[...]

    @pl.when((step >= at_third) & (step < at_third + seqs))
    def _():
        s = step - at_third
        third_score_step(s, k_ref.at[pl.ds(s, 1)], v_ref.at[pl.ds(s, 1)], ql.at[pl.ds(s, 1)], w_ref, num, stat, own)

    @pl.when(step == at_third + seqs - 1)
    def _():
        begin(swap_copies(num, num_got, own, num_sems))
        begin(swap_rows(stat, stat_got, stat_sems))

    @pl.when(step == at_first)
    def _():
        for s in range(seqs):
            finish(mark_copies(land_k, kl, k_sems, s))
        kl_out[...] = kl[...]

    @pl.when((step >= at_first) & (step < at_first + seqs))
    def _():
        s = step - at_first
        first_score_step(q_ref.at[pl.ds(s, 1)], kl[s], p_ref)

    @pl.when(step == at_inverse)
    def _():
        finish(swap_copies(num, num_got, own, num_sems))
        finish(swap_rows(stat, stat_got, stat_sems))
        inverse_step(
            num_got, stat_got, ql, kl, mixed, sum_ref, mid_ref, z_ref, zp_ref, za_ref, zw_ref, scale_ref, tot_ref,
            alpha_ref,
        )
        begin(spread_copies(mixed, mixed_out, own, mixed_sems))

    @pl.when(step == pl.num_programs(0) - 1)
    def _():
        finish(spread_copies(mixed, mixed_out, own, mixed_sems))
        rim_out[...] = rims[...]


def front(tokens, w_qkv, taps, own):
    seqs, rows, features = tokens.shape
    ranks = lax.axis_size("seq")
    marks = M // ranks
    pairs = features // 128
    tiles = (4, 5, seqs * pairs - 9)
    third = seqs + tiles[0]
    first = third + seqs + tiles[1]
    at = dict(at_third=third, at_first=first, at_inverse=first + seqs)
    plan = ((seqs, tiles[0]), (third + seqs, tiles[1]), (first + seqs + 1, tiles[2]))
    here = lambda first: (lambda i: jnp.clip(i - first, 0, seqs - 1))
    score, prob = here(at["at_third"]), here(at["at_first"])
    whole = lambda a: pl.BlockSpec(a.shape, lambda i: (0,) * len(a.shape), pipeline_mode=pl.Buffered(1))
    tile = lambda i: pick_tile(i, plan)
    rows_out = jax.ShapeDtypeStruct(tokens.shape, bf16)
    land = jax.ShapeDtypeStruct((seqs, M, features), bf16)
    rim_out = jax.ShapeDtypeStruct((seqs, 2, RIM, features), bf16)
    mat = jax.ShapeDtypeStruct((own, M, 128), f32)
    steps = lambda n: jax.ShapeDtypeStruct((n, own, M, 128), f32)
    saved = [
        mat, mat, steps(NEWTON + 1), steps(NEWTON), steps(NEWTON), steps(NEWTON),
        jax.ShapeDtypeStruct((own, 8, 128), f32), mat, steps(ranks),
    ]
    vm = lambda *shape: pltpu.VMEM(shape, bf16)
    dma = pltpu.SemaphoreType.DMA
    return pl.pallas_call(
        functools.partial(front_kernel, plan=plan, **at),
        grid=(plan[-1][0] + tiles[2],),
        in_specs=[
            pl.BlockSpec((1, rows, features), lambda i: (jnp.minimum(i, seqs - 1), 0, 0)), whole(w_qkv), whole(taps),
        ],
        out_specs=[whole(rows_out)] * 3
        + [
            pl.BlockSpec((1, rows, features), lambda i: (score(i), 0, 0)),
            pl.BlockSpec((1, features, rows), lambda i: (prob(i), 0, 0)),
            whole(land), whole(land), whole(rim_out),
            pl.BlockSpec((1, rows, 128), lambda i: (tile(i) // pairs, 0, tile(i) % pairs)), ANY,
        ]
        + [whole(a) for a in saved],
        out_shape=[rows_out] * 4
        + [
            jax.ShapeDtypeStruct((seqs, features, rows), bf16), land, land, rim_out, rows_out,
            jax.ShapeDtypeStruct((ranks * own, M, 128), bf16),
        ]
        + saved,
        scratch_shapes=[
            vm(seqs, marks, features), vm(seqs, marks, features), vm(seqs, M, features), vm(seqs, M, features),
            vm(seqs, 2, RIM, features), vm(seqs, 2, RIM, features), vm(ranks * own, M, 128),
            pltpu.VMEM((ranks, 16, 128), f32), vm(ranks, own, M, 128), pltpu.VMEM((ranks, 16, 128), f32),
            vm(own, M, 128), pltpu.VMEM((rows + 2 * RIM, 128), f32), pltpu.VMEM((40, 128), f32),
            dma((2, seqs, ranks)), dma((2, seqs, ranks)), dma((seqs, 2)), dma((seqs, 2)), rank_sems(), rank_sems(),
            rank_sems(),
        ],
        compiler_params=params(62 * MB, collective_id=0, has_side_effects=True),
        name="front",
    )(tokens, w_qkv, taps)


def mean_of(x):
    return jnp.mean(x, axis=-1, keepdims=True)


def gelu_and_slope(u):
    u = u.astype(bf16)
    low = lambda c: jnp.asarray(c, bf16)
    t = low(1.0) / (low(1.0) + low(ERFC_P * root_half) * jnp.abs(u))
    bell = jnp.exp2((u * u) * low(-0.5 * log2_e))
    poly = jnp.full_like(t, 0.5 * ERFC_C[-1])
    for c in ERFC_C[-2::-1]:
        poly = poly * t + low(0.5 * c)
    half = (poly * t) * bell
    cdf = jnp.where(u < 0, half, low(1.0) - half)
    return u * cdf, cdf + u * (bell * low(inv_root_two_pi))


def row_block(
    step, tok_ref, p_ref, conv_refs, mix_ref, top_ref, w_out_ref, w_up_ref, w_down_ref, ga_ref,
    gf_ref, out_ref, proj_ref, gm_ref, gains_ref, act, gul, slope, hid_t, gdl_t, mix_t, gpr, resid, whole, ready=lambda i: None,
):
    size, features = tok_ref.shape
    ff = act.shape[1]
    wide = features
    start = pl.multiple_of(step * size, size)
    rows = pl.ds(start, size)
    near = rows if whole else pl.ds(0, size)
    masks = group_masks((M, 4 * E), 4, bf16)
    for g in range(features // 256):
        sl = slice(256 * g, 256 * g + 256)
        att = dot_tn(p_ref[0, sl, :], block_diag(quad(mix_ref, g), masks))
        split_at = conv_refs[0].shape[1]
        ref, lane = (conv_refs[0], 256 * g) if 256 * g < split_at else (conv_refs[1], 256 * g - split_at)
        resid[:, sl] = (att + ref[:, lane : lane + 256].astype(f32)).astype(bf16)
    mixed = resid[...]
    mix_t[:, near] = mixed.T
    residual = tok_ref[...].astype(f32) + dot(mixed, w_out_ref[...])
    centre = residual - mean_of(residual)
    s_att = lax.rsqrt(mean_of(centre * centre) + epsilon)
    normed = centre * s_att
    gain_att = ga_ref[...].reshape(1, features)
    hidden = normed * gain_att
    hid_low = hidden.astype(bf16)
    hid_t[:, rows] = hid_low.T
    down = jnp.zeros((size, features), f32)
    for j in range(0, ff, wide):
        if j == 0:
            ready(0)
        up = dot(hid_low, w_up_ref[:, j : j + wide])
        low, sl = gelu_and_slope(up)
        act[near, j : j + wide] = low
        slope[:, j : j + wide] = sl
        if j == 0:
            ready(1)
        down = down + dot(low, w_down_ref[j : j + wide, :])
    residual_two = hidden + down
    centre_two = residual_two - mean_of(residual_two)
    s_ffn = lax.rsqrt(mean_of(centre_two * centre_two) + epsilon)
    normed_two = centre_two * s_ffn
    gain_ffn = gf_ref[...].reshape(1, features)
    out_ref[...] = (normed_two * gain_ffn).astype(bf16)
    top = top_ref[...].astype(f32)
    gains_ref[8:16, :] += (top * normed_two).reshape(size // 8, 8, features).sum(0)
    g = top * gain_ffn
    grad_two = s_ffn * (g - mean_of(g) - normed_two * mean_of(g * normed_two))
    gdl = grad_two.astype(bf16)
    gdl_t[:, near] = gdl.T
    back = jnp.zeros((size, features), f32)
    for j in range(0, ff, wide):
        gu = dot_nt(gdl, w_down_ref[j : j + wide, :]) * slope[:, j : j + wide].astype(f32)
        low = gu.astype(bf16)
        gul[rows, j : j + wide] = low
        back = back + dot_nt(low, w_up_ref[:, j : j + wide])
    grad_hidden = grad_two + back
    gains_ref[0:8, :] += (grad_hidden * normed).reshape(size // 8, 8, features).sum(0)
    g = grad_hidden * gain_att
    proj = (s_att * (g - mean_of(g) - normed * mean_of(g * normed))).astype(bf16)
    proj_ref[...] = proj
    if whole:
        gpr[rows, :] = proj
    gm_ref[...] = dot_nt(proj, w_out_ref[...]).astype(bf16)


def row_kernel(
    tok_ref, p_ref, conv_a_ref, conv_b_ref, mix_ref, top_ref, w_out_ref, w_up_ref, w_down_ref, ga_ref, gf_ref,
    out_ref, proj_ref, gm_ref, wg_ref, gains_ref,
    act, gul, slope, hid_t, gdl_t, mix_t, gpr, resid,
):
    step = pl.program_id(0)
    size, features = tok_ref.shape
    blocks = act.shape[0] // size
    ff = act.shape[1]
    wide = features

    @pl.when(step == 0)
    def _():
        gains_ref[...] = jnp.zeros_like(gains_ref)

    @pl.when(step < blocks)
    def _():
        row_block(
            step, tok_ref, p_ref, (conv_a_ref, conv_b_ref), mix_ref, top_ref, w_out_ref, w_up_ref, w_down_ref,
            ga_ref, gf_ref, out_ref, proj_ref, gm_ref, gains_ref, act, gul, slope, hid_t, gdl_t, mix_t, gpr,
            resid, True,
        )

    chunks = ff // wide
    for first, left, right in ((0, hid_t, gul), (chunks, gdl_t, act), (2 * chunks, mix_t, gpr)):
        count = chunks if first < 2 * chunks else 1

        @pl.when((step >= blocks + first) & (step < blocks + first + count))
        def _(first=first, left=left, right=right):
            base = (step - blocks - first) * wide
            for c in range(0, wide, 256):
                cols = pl.ds(pl.multiple_of(base + c, 256), 256)
                wg_ref[0, :, c : c + 256] = dot(left[...], right[:, cols]).astype(bf16)


def row_pass(tokens, probs, conv_a, conv_b, mixed, grad_out, w_out, w_up, w_down, gain_att, gain_ffn):
    seqs, rows, features = tokens.shape
    ff = w_up.shape[1]
    size = min(256, rows)
    total = seqs * rows
    blocks = total // size
    grads = 2 * (ff // features) + 1
    here = lambda i: jnp.minimum(i, blocks - 1)
    block = pl.BlockSpec((size, features), lambda i: (here(i), 0))
    whole = lambda a: pl.BlockSpec(a.shape, lambda i: (0,) * a.ndim, pipeline_mode=pl.Buffered(1))
    flat = lambda a: a.reshape(total, a.shape[2])
    part = lambda a: pl.BlockSpec((size, a.shape[2]), lambda i: (here(i), 0))
    gains = [gain_att, gain_ffn]
    row_out = jax.ShapeDtypeStruct((total, features), bf16)
    tall = pltpu.VMEM((features, total), bf16)
    return pl.pallas_call(
        row_kernel,
        grid=(blocks + grads,),
        in_specs=[
            block, pl.BlockSpec((1, features, size), lambda i: (here(i) * size // rows, 0, here(i) % (rows // size))),
            part(conv_a), part(conv_b),
            pl.BlockSpec((features // 128, M, 128), lambda i: (here(i) * size // rows, 0, 0)),
            block, whole(w_out), whole(w_up), whole(w_down), whole(gains[0]), whole(gains[1]),
        ],
        out_specs=[block] * 3
        + [
            pl.BlockSpec((1, features, features), lambda i: (jnp.maximum(i - blocks, 0), 0, 0)),
            pl.BlockSpec((16, features), lambda i: (0, 0)),
        ],
        out_shape=[row_out] * 3
        + [
            jax.ShapeDtypeStruct((grads, features, features), bf16),
            jax.ShapeDtypeStruct((16, features), f32),
        ],
        scratch_shapes=[
            pltpu.VMEM((total, ff), bf16), pltpu.VMEM((total, ff), bf16), pltpu.VMEM((size, ff), bf16),
            tall, tall, tall, pltpu.VMEM((total, features), bf16), pltpu.VMEM((size, features), bf16),
        ],
        compiler_params=params(62 * MB),
        name="row_pass",
    )(flat(tokens), probs, flat(conv_a), flat(conv_b), mixed, flat(grad_out), w_out, w_up, w_down, *gains)


def put_parts(parts, slot, low, c, by_rows):
    for l in range(0, low.shape[1], 128):
        side, lane = (c + l) // 384, (c + l) % 384
        if by_rows:
            for d in range(8):
                parts[slot, d % 2, d // 2, 96 * side : 96 * side + 96, lane : lane + 128] = low[
                    96 * d : 96 * d + 96, l : l + 128
                ]
        else:
            for z in range(4):
                parts[slot, side, z, :, lane : lane + 128] = low[192 * z : 192 * z + 192, l : l + 128]


def fold(block):
    return jnp.concatenate([block[:48], block[48:]], axis=1)


def rows_forward_kernel(
    tok_ref, p_ref, conv_ref, mix_ref, top_ref, w_out_ref, w_up_in, w_down_in, ga_ref, gf_ref,
    out_ref, normed_ref, s_ref, gdl_ref, slope_ref, hid_t_ref, mix_t_ref, gains_ref, g_out,
    w_up_ref, w_down_ref, load_sems, act, gdl_t, mixed_ref, parts, got, sums, send, recv, out_sem,
):
    step = pl.program_id(0)
    size, features = tok_ref.shape
    blocks = act.shape[0] // size
    ff = act.shape[1]
    chunks = ff // features
    core, _, _, sibling, _, _ = cube()
    loads = [
        pltpu.make_async_copy(w_up_in, w_up_ref, load_sems.at[0]),
        pltpu.make_async_copy(w_down_in, w_down_ref, load_sems.at[1]),
    ]

    @pl.when(step == 0)
    def _():
        for load in loads:
            load.start()
        gains_ref[...] = jnp.zeros_like(gains_ref)
        greet([sibling])

    @pl.when(step < blocks)
    def _():
        rows = pl.ds(pl.multiple_of(step * size, size), size)
        masks = group_masks((M, 4 * E), 4, bf16)
        for g in range(features // 256):
            sl = slice(256 * g, 256 * g + 256)
            att = dot_tn(p_ref[0, sl, :], block_diag(quad(mix_ref, g), masks))
            mixed_ref[:, sl] = (att + conv_ref[:, sl].astype(f32)).astype(bf16)
        mixed = mixed_ref[...]
        mix_t_ref[...] = mixed.T
        residual = tok_ref[...].astype(f32) + dot(mixed, w_out_ref[...])
        centre = residual - mean_of(residual)
        s_att = lax.rsqrt(mean_of(centre * centre) + epsilon)
        normed = centre * s_att
        s_ref[...] = jnp.broadcast_to(s_att, s_ref.shape)
        normed_ref[...] = normed.astype(bf16)
        hidden = normed * ga_ref[...].reshape(1, features)
        hid_low = hidden.astype(bf16)
        hid_t_ref[...] = hid_low.T

        @pl.when(step == 0)
        def _():
            for load in loads:
                load.wait()

        down = jnp.zeros((size, features), f32)
        for j in range(0, ff, features):
            low, sl = gelu_and_slope(dot(hid_low, w_up_ref[:, j : j + features]))
            act[rows, j : j + features] = low
            slope_ref[:, j : j + features] = sl
            down = down + dot(low, w_down_ref[j : j + features, :])
        residual_two = hidden + down
        centre_two = residual_two - mean_of(residual_two)
        s_ffn = lax.rsqrt(mean_of(centre_two * centre_two) + epsilon)
        normed_two = centre_two * s_ffn
        gain_ffn = gf_ref[...].reshape(1, features)
        out_ref[...] = (normed_two * gain_ffn).astype(bf16)
        top = top_ref[...].astype(f32)
        gains_ref[...] += (top * normed_two).reshape(size // 8, 8, features).sum(0)
        g = top * gain_ffn
        gdl = (s_ffn * (g - mean_of(g) - normed_two * mean_of(g * normed_two))).astype(bf16)
        gdl_ref[...] = gdl
        gdl_t[:, rows] = gdl.T

    j = step - blocks
    slot = lax.rem(jnp.maximum(j, 0), 2)

    def share(at):
        return remote(parts.at[at % 2, 1 - core], got.at[at], send.at[at], recv.at[at], sibling)

    def out_copy(at):
        return pltpu.make_async_copy(sums.at[at % 2], g_out.at[:, at], out_sem.at[at % 2])

    @pl.when((j >= 2) & (j < chunks))
    def _():
        share(j - 2).wait_send()

    @pl.when((j >= 0) & (j < chunks))
    def _():
        for c in range(0, features, 256):
            cols = pl.ds(pl.multiple_of(j * features + c, 256), 256)
            put_parts(parts, slot, dot(gdl_t[...], act[:, cols]).astype(bf16), c, False)
        share(j).start()

    done = j - 1

    @pl.when(done >= 2)
    def _():
        out_copy(done - 2).wait()

    @pl.when(done >= 0)
    def _():
        share(done).wait_recv()
        sums[done % 2] = add_low(parts[done % 2, core], got[done])
        out_copy(done).start()

    @pl.when(done == chunks - 1)
    def _():
        for at in (done - 1, done):
            share(at).wait_send()
            out_copy(at).wait()


def rows_forward(tokens, probs, conv_out, mixed, grad_out, w_out, w_up, w_down, gain_att, gain_ffn):
    seqs, rows, features = tokens.shape
    ff = w_up.shape[1]
    size = rows
    total = seqs * rows
    blocks = total // size
    chunks = ff // features
    here = lambda i: jnp.minimum(i, blocks - 1)
    block = lambda n: pl.BlockSpec((size, n), lambda i: (here(i), 0))
    turned = pl.BlockSpec((features, size), lambda i: (0, here(i)))
    whole = lambda a: pl.BlockSpec(a.shape, lambda i: (0,) * a.ndim, pipeline_mode=pl.Buffered(1))
    flat = lambda a: a.reshape(total, a.shape[2])
    shape = jax.ShapeDtypeStruct
    dma = pltpu.SemaphoreType.DMA
    return pl.pallas_call(
        rows_forward_kernel,
        grid=(blocks + chunks + 1,),
        in_specs=[
            block(features),
            pl.BlockSpec((1, features, size), lambda i: (here(i) * size // rows, 0, here(i) % (rows // size))),
            block(features), pl.BlockSpec((features // 128, M, 128), lambda i: (here(i) * size // rows, 0, 0)),
            block(features), whole(w_out), ANY, ANY, whole(gain_att), whole(gain_ffn),
        ],
        out_specs=[block(features), block(features), block(128), block(features), block(ff), turned, turned]
        + [pl.BlockSpec((8, features), lambda i: (0, 0)), ANY],
        out_shape=[
            shape((total, features), bf16), shape((total, features), bf16), shape((total, 128), f32),
            shape((total, features), bf16), shape((total, ff), bf16), shape((features, total), bf16),
            shape((features, total), bf16), shape((8, features), f32), shape((4, chunks, 192, 384), bf16),
        ],
        scratch_shapes=[
            pltpu.VMEM(w_up.shape, bf16), pltpu.VMEM(w_down.shape, bf16), dma((2,)), pltpu.VMEM((total, ff), bf16),
            pltpu.VMEM((features, total), bf16), pltpu.VMEM((size, features), bf16),
            pltpu.VMEM((2, 2, 4, 192, 384), bf16), pltpu.VMEM((chunks, 4, 192, 384), bf16),
            pltpu.VMEM((2, 4, 192, 384), bf16), dma((chunks,)), dma((chunks,)), dma((2,)),
        ],
        compiler_params=params(62 * MB, collective_id=3, has_side_effects=True),
        name="rows_forward",
    )(
        flat(tokens), probs, flat(conv_out), mixed, flat(grad_out), w_out, w_up, w_down, gain_att, gain_ffn
    )


def rows_backward_kernel(
    turn_at, gdl_ref, slope_ref, normed_ref, s_ref, w_out_ref, ga_ref, w_down_in, w_up_in, hid_t_in, mix_t_in, down_in,
    proj_ref, gm_ref, gains_ref, down_ref, g_out, rim_out,
    w_down_ref, w_up_ref, hid_t, mix_t, load_sems, gul, gpr, rim, parts, got, sums,
    kept, crossed, turned, kept_sems, cross_sems, turn_sems,
    send, recv, out_sem, last_sem, rim_send, rim_recv,
):
    step = pl.program_id(0)
    size, features = gdl_ref.shape
    ff = gul.shape[1]
    blocks = gul.shape[0] // size
    chunks = ff // features
    seqs = rim.shape[0]
    per = blocks // seqs
    me, count = seq_place()
    core, _, _, sibling, along_x, along_y = cube()
    loads = [
        pltpu.make_async_copy(a, b, load_sems.at[i])
        for i, (a, b) in enumerate(
            ((w_down_in, w_down_ref), (w_up_in, w_up_ref), (hid_t_in, hid_t), (mix_t_in, mix_t))
        )
    ]
    cross = cross_copies(down_in, crossed, cross_sems)
    keep = kept_copies(down_in, kept, kept_sems)
    turn = turn_copies(kept, turned, turn_sems)

    @pl.when(step == 0)
    def _():
        for load in loads:
            load.start()
        gains_ref[...] = jnp.zeros_like(gains_ref)
        greet([sibling, along_x, along_y])
        for copy in cross + keep:
            copy.start()

    @pl.when(step == turn_at)
    def _():
        for copy in cross + keep:
            copy.wait()
        cross_add(kept, crossed)
        for copy in turn:
            copy.start()

    def rim_copy(s, side):
        there = lax.rem(me + (1 if side == 0 else count - 1), count)
        return remote(
            rim.at[s, side], rim_out.at[s, side], rim_send.at[s, side], rim_recv.at[s, side], {"seq": there}
        )

    @pl.when(step < blocks)
    def _():
        rows = pl.ds(pl.multiple_of(step * size, size), size)

        @pl.when(step == 0)
        def _():
            loads[0].wait()

        gdl = gdl_ref[...]
        back = gdl.astype(f32)
        for j in range(0, ff, features):
            gu = dot_nt(gdl, w_down_ref[j : j + features, :]) * slope_ref[:, j : j + features].astype(f32)
            low = gu.astype(bf16)
            gul[rows, j : j + features] = low
            if j == 0:
                @pl.when(step == 0)
                def _():
                    loads[1].wait()
            back = back + dot_nt(low, w_up_ref[:, j : j + features])
        normed = normed_ref[...].astype(f32)
        gains_ref[...] += (back * normed).reshape(size // 8, 8, features).sum(0)
        g = back * ga_ref[...].reshape(1, features)
        proj = (s_ref[:, 0:1] * (g - mean_of(g) - normed * mean_of(g * normed))).astype(bf16)
        proj_ref[...] = proj
        gpr[rows, :] = proj
        gm_ref[...] = dot_nt(proj, w_out_ref[...]).astype(bf16)
        s = step // per

        @pl.when(step % per == 0)
        def _():
            rim[s, 1] = gm_ref[:RIM, :]
            rim_copy(s, 1).start()

        @pl.when(step % per == per - 1)
        def _():
            rim[s, 0] = gm_ref[size - RIM :, :]
            rim_copy(s, 0).start()

    j = step - blocks
    slot = lax.rem(jnp.maximum(j, 0), 2)

    def share(at):
        return remote(parts.at[at % 2, 1 - core], got.at[at], send.at[at], recv.at[at], sibling)

    def up_copy(at):
        return pltpu.make_async_copy(sums.at[at % 2], g_out.at[at, :, 0:192, :], out_sem.at[at % 2])

    def out_copy(z):
        return pltpu.make_async_copy(
            sums.at[0, :, 48 * z : 48 * z + 48, :], g_out.at[z, :, 192:240, :], last_sem.at[z]
        )

    @pl.when((j >= 2) & (j <= chunks))
    def _():
        share(j - 2).wait_send()

    @pl.when(j == 0)
    def _():
        loads[2].wait()
        loads[3].wait()

    @pl.when((j >= 0) & (j < chunks))
    def _():
        for c in range(0, features, 256):
            cols = pl.ds(pl.multiple_of(j * features + c, 256), 256)
            put_parts(parts, slot, dot(hid_t[...], gul[:, cols]).astype(bf16), c, True)
        share(j).start()

    @pl.when(j == chunks)
    def _():
        for c in range(2):
            low = dot(mix_t[...], gpr[:, 384 * c : 384 * c + 384]).astype(bf16)
            for zz in range(2):
                z = 2 * c + zz
                for d in range(8):
                    parts[slot, d % 2, d // 2, 48 * z : 48 * z + 48, :] = fold(
                        low[96 * d : 96 * d + 96, 192 * zz : 192 * zz + 192]
                    )
        share(j).start()

    done = j - 1

    @pl.when(done >= 2)
    def _():
        up_copy(done - 2).wait()

    @pl.when(done >= 0)
    def _():
        share(done).wait_recv()
        sums[done % 2] = add_low(parts[done % 2, core], got[done])

    @pl.when((done >= 0) & (done < chunks))
    def _():
        up_copy(done).start()

    @pl.when(done == chunks)
    def _():
        for z in range(4):
            out_copy(z).start()
        for copy in turn:
            copy.wait()
        turn_add(down_ref, kept, turned)
        share(done - 1).wait_send()
        share(done).wait_send()
        up_copy(done - 1).wait()
        for z in range(4):
            out_copy(z).wait()

        def rims(s, carry):
            for side in range(2):
                rim_copy(s, side).wait()
            return carry

        lax.fori_loop(0, seqs, rims, 0)


def rows_backward(gdl, slope, normed, s_att, w_out, gain_att, w_down, w_up, hid_t, mix_t, downs, seqs):
    total, features = gdl.shape
    ff = w_up.shape[1]
    size = total // seqs
    blocks = total // size
    chunks = ff // features
    here = lambda i: jnp.minimum(i, blocks - 1)
    block = lambda n: pl.BlockSpec((size, n), lambda i: (here(i), 0))
    whole = lambda a: pl.BlockSpec(a.shape, lambda i: (0,) * len(a.shape), pipeline_mode=pl.Buffered(1))
    shape = jax.ShapeDtypeStruct
    down_sum = shape((4, 192, 384), bf16)
    dma = pltpu.SemaphoreType.DMA
    return pl.pallas_call(
        functools.partial(rows_backward_kernel, 2),
        grid=(blocks + chunks + 2,),
        in_specs=[block(features), block(ff), block(features), block(128), whole(w_out), whole(gain_att)] + [ANY] * 5,
        out_specs=[block(features), block(features), pl.BlockSpec((8, features), lambda i: (0, 0)), whole(down_sum)]
        + [ANY] * 2,
        out_shape=[
            shape((total, features), bf16), shape((total, features), bf16), shape((8, features), f32), down_sum,
            shape((4, chunks, 240, 384), bf16), shape((seqs, 2, RIM, features), bf16),
        ],
        scratch_shapes=[
            pltpu.VMEM(w_down.shape, bf16), pltpu.VMEM(w_up.shape, bf16), pltpu.VMEM(hid_t.shape, bf16),
            pltpu.VMEM(mix_t.shape, bf16), dma((4,)), pltpu.VMEM((total, ff), bf16),
            pltpu.VMEM((total, features), bf16), pltpu.VMEM((seqs, 2, RIM, features), bf16),
            pltpu.VMEM((2, 2, 4, 192, 384), bf16), pltpu.VMEM((chunks + 1, 4, 192, 384), bf16),
            pltpu.VMEM((2, 4, 192, 384), bf16),
        ]
        + stage_scratch(192)
        + [dma((chunks + 1,)), dma((chunks + 1,)), dma((2,)), dma((4,)), dma((seqs, 2)), dma((seqs, 2))],
        compiler_params=params(62 * MB, collective_id=4, has_side_effects=True),
        name="rows_backward",
    )(gdl, slope, normed, s_att, w_out, gain_att, w_down, w_up, hid_t, mix_t, downs)


def first_back_step(gm_ref, p_ref, q_ref, mix_ref, kl_of, put_land, put_gq, put_klp):
    features = gm_ref.shape[2]
    masks = group_masks((M, 4 * E), 4, bf16)
    masks_wide = group_masks((M, 4 * E), 4, f32)
    for g in range(features // 256):
        sl = slice(256 * g, 256 * g + 256)
        gm, p = gm_ref[0, :, sl], p_ref[0, sl, :]
        put_land(g, diag_blocks(dot(p, gm), masks_wide).astype(bf16))
        d = dot_nt(block_diag(quad(mix_ref, g), masks), gm)
        parts = []
        for h in range(4):
            pw = p[E * h : E * h + E].astype(f32)
            dh = d[E * h : E * h + E]
            parts.append((pw * (dh - jnp.sum(pw * dh, axis=0, keepdims=True))).astype(bf16))
        gs = jnp.concatenate(parts, axis=0)
        put_gq(g, dot_tn(gs, block_diag(kl_of(sl), masks)).astype(bf16))
        put_klp(g, diag_blocks(dot(gs, q_ref[0, :, sl]), masks_wide))


def first_back_kernel(gm_ref, p_ref, q_ref, mix_ref, kl_ref, land_ref, gq_ref, klp_ref):
    def put_land(g, x):
        for i in range(2):
            land_ref[2 * g + i] = x[:, 128 * i : 128 * i + 128]

    def put_klp(g, x):
        klp_ref[0, :, 256 * g : 256 * g + 256] = x

    def put_gq(g, x):
        gq_ref[0, :, 256 * g : 256 * g + 256] = x

    first_back_step(gm_ref, p_ref, q_ref, mix_ref, lambda sl: kl_ref[0, :, sl], put_land, put_gq, put_klp)


def first_back(gm, probs, q, mixed, k_land):
    seqs, rows, features = q.shape
    pairs = features // 128
    full = pl.BlockSpec((1, rows, features), lambda s: (s, 0, 0))
    land = pl.BlockSpec((1, M, features), lambda s: (s, 0, 0))
    return pl.pallas_call(
        first_back_kernel,
        grid=(seqs,),
        in_specs=[full, pl.BlockSpec((1, features, rows), lambda s: (s, 0, 0)), full, pl.BlockSpec((pairs, M, 128), lambda s: (s, 0, 0)), land],
        out_specs=[pl.BlockSpec((pairs, M, 128), lambda s: (s, 0, 0)), full, land],
        out_shape=[
            jax.ShapeDtypeStruct((seqs * pairs, M, 128), bf16),
            jax.ShapeDtypeStruct(q.shape, bf16),
            jax.ShapeDtypeStruct((seqs, M, features), f32),
        ],
        compiler_params=params(62 * MB),
        name="first_back",
    )(gm, probs, q, mixed, k_land)


def third_back_kernel(w_ref, v_ref, k_ref, gc_ref, gn_ref, gt_ref, ql_ref, gv_ref, gk_ref, qlp_ref):
    features = w_ref.shape[2]
    masks = group_masks((M, 4 * E), 4, bf16)
    masks_wide = group_masks((M, 4 * E), 4, f32)
    for g in range(features // 256):
        sl = slice(256 * g, 256 * g + 256)
        w = w_ref[0, :, sl]
        gn = jnp.concatenate([gn_ref[2 * g], gn_ref[2 * g + 1]], axis=1)
        gt = jnp.concatenate([gt_ref[2 * g, 0:1, :], gt_ref[2 * g + 1, 0:1, :]], axis=1)
        gd = block_diag(gn, masks)
        gs = (w.astype(f32) * (dot_nt(v_ref[0, :, sl], gd) + gt)).astype(bf16)
        gv_ref[0, :, sl] = (dot(w, gd) + gc_ref[0, :, sl].astype(f32)).astype(bf16)
        gk_ref[0, :, sl] = dot(gs, block_diag(ql_ref[0, :, sl], masks)).astype(bf16)
        qlp_ref[0, :, sl] = diag_blocks(dot_tn(gs, k_ref[0, :, sl]), masks_wide)


def third_back(w, v, k, grad_conv, gn, gt, q_land):
    seqs, rows, features = v.shape
    pairs = features // 128
    full = pl.BlockSpec((1, rows, features), lambda s: (s, 0, 0))
    land = pl.BlockSpec((1, M, features), lambda s: (s, 0, 0))
    return pl.pallas_call(
        third_back_kernel,
        grid=(seqs,),
        in_specs=[full] * 4
        + [
            pl.BlockSpec((pairs, M, 128), lambda s: (s, 0, 0)),
            pl.BlockSpec((pairs, 8, 128), lambda s: (s, 0, 0)),
            land,
        ],
        out_specs=[full, full, land],
        out_shape=[jax.ShapeDtypeStruct(v.shape, bf16)] * 2
        + [jax.ShapeDtypeStruct((seqs, M, features), f32)],
        compiler_params=params(62 * MB),
        name="third_back",
    )(w, v, k, grad_conv, gn, gt, q_land)


def last_kernel(tok_ref, gq_ref, gk_ref, gv_ref, qo_ref, ko_ref, proj_ref, w_ref, gt_ref, wg_ref, d, tok_t):
    step = pl.program_id(0)
    seqs = tok_t.shape[1] // tok_ref.shape[1]
    rows, features = tok_ref.shape[1:]
    marks = qo_ref.shape[1]
    seg = rows // marks

    @pl.when(step < seqs)
    def _():
        here = pl.ds(pl.multiple_of(step * rows, rows), rows)
        for part, (core, own) in enumerate(((gq_ref, qo_ref), (gk_ref, ko_ref))):
            for m in range(marks):
                at = pl.ds(pl.multiple_of(step * rows + m * seg, seg), seg)
                x = core[0, m * seg : m * seg + seg, :].astype(f32) + own[0, m : m + 1, :] * (1.0 / seg)
                x = x.astype(bf16)
                if part == 0:
                    x = x * jnp.asarray(0.125, bf16)
                d[at, part * features : part * features + features] = x
        d[here, 2 * features :] = gv_ref[0]
        tok_t[:, here] = tok_ref[0].T
        for c in range(0, rows, 128):
            at = pl.ds(pl.multiple_of(step * rows + c, 128), 128)
            gt_ref[0, c : c + 128, :] = (
                proj_ref[0, c : c + 128, :].astype(f32) + dot_nt(d[at, :], w_ref[...])
            ).astype(bf16)

    @pl.when(step >= seqs)
    def _():
        base = (step - seqs) * features
        for c in range(0, features, 256):
            cols = pl.ds(pl.multiple_of(base + c, 256), 256)
            wg_ref[0, :, c : c + 256] = dot(tok_t[...], d[:, cols]).astype(bf16)


def last_pass(tokens, gq, gk, gv, q_own, k_own, proj, w_qkv):
    seqs, rows, features = tokens.shape
    marks = q_own.shape[1]
    here = lambda i: jnp.minimum(i, seqs - 1)
    full = pl.BlockSpec((1, rows, features), lambda i: (here(i), 0, 0))
    land = pl.BlockSpec((1, marks, features), lambda i: (here(i), 0, 0))
    return pl.pallas_call(
        last_kernel,
        grid=(seqs + 3,),
        in_specs=[full] * 4 + [land] * 2
        + [full, pl.BlockSpec(w_qkv.shape, lambda i: (0, 0), pipeline_mode=pl.Buffered(1))],
        out_specs=[full, pl.BlockSpec((1, features, features), lambda i: (jnp.maximum(i - seqs, 0), 0, 0))],
        out_shape=[
            jax.ShapeDtypeStruct(tokens.shape, bf16),
            jax.ShapeDtypeStruct((3, features, features), bf16),
        ],
        scratch_shapes=[
            pltpu.VMEM((seqs * rows, 3 * features), bf16), pltpu.VMEM((features, seqs * rows), bf16),
        ],
        compiler_params=params(62 * MB),
        name="last_pass",
    )(tokens, gq, gk, gv, q_own, k_own, proj, w_qkv)


def add_pairs(dst, own, start, pairs):
    for i in range(own.shape[0]):
        @pl.when(start + i < pairs)
        def _(i=i):
            dst[start + i] += own[i]


def cross_copies(src, got, sems):
    _, x, y, _, along_x, along_y = cube()
    return [
        remote(src.at[0:2, :, 1 - x], got.at[0], sems.at[0, 0], sems.at[1, 0], along_x),
        remote(src.at[2:4, 1 - y], got.at[1], sems.at[0, 1], sems.at[1, 1], along_y),
    ]


def kept_copies(src, kept, sems):
    _, x, y, _, _, _ = cube()
    return [
        pltpu.make_async_copy(src.at[0:2, :, x], kept.at[0], sems.at[0]),
        pltpu.make_async_copy(src.at[2:4, y], kept.at[1], sems.at[1]),
    ]


def turn_copies(kept, got, sems):
    _, x, y, _, along_x, along_y = cube()
    return [
        remote(kept.at[0, :, 1 - y], got.at[0], sems.at[0, 0], sems.at[1, 0], along_y),
        remote(kept.at[1, :, 1 - x], got.at[1], sems.at[0, 1], sems.at[1, 1], along_x),
    ]


def cross_add(kept, got):
    for half in range(2):
        for rank in range(2):
            kept[half, rank] = add_low(kept[half, rank], got[half, rank])


def turn_add(out, kept, got):
    _, x, y, _, _, _ = cube()
    for half, place in ((0, y), (1, x)):
        for rank in range(2):
            out[2 * half + rank] = add_low(kept[half, rank, place], got[half, rank])


def stage_scratch(rows):
    dma = pltpu.SemaphoreType.DMA
    return [
        pltpu.VMEM((2, 2, 2, rows, 384), bf16), pltpu.VMEM((2, 2, 2, rows, 384), bf16),
        pltpu.VMEM((2, 2, rows, 384), bf16), dma((2,)), dma((2, 2)), dma((2, 2)),
    ]


def first_third(w_ref, v_ref, k_ref, gn_of, gt_of, put_gs, put_qlp):
    features = w_ref.shape[2]
    masks = group_masks((M, 4 * E), 4, bf16)
    masks_wide = group_masks((M, 4 * E), 4, f32)
    for g in range(features // 256):
        sl = slice(256 * g, 256 * g + 256)
        gd = block_diag(jnp.concatenate([gn_of(2 * g), gn_of(2 * g + 1)], axis=1), masks)
        gt = jnp.concatenate([gt_of(2 * g), gt_of(2 * g + 1)], axis=1)
        gs = (w_ref[0, :, sl].astype(f32) * (dot_nt(v_ref[0, :, sl], gd) + gt)).astype(bf16)
        put_gs(g, gs)
        put_qlp(g, diag_blocks(dot_tn(gs, k_ref[0, :, sl]), masks_wide))


def tail_plan(seqs, pairs, blocks):
    tiles = (2, 2, pairs - 4)
    at, step = {}, 0
    for name, count in (
        ("first", seqs), ("conv_a", tiles[0]), ("inverse", 1), ("one", seqs), ("conv_b", tiles[1]), ("q", 1),
        ("conv_c", tiles[2]), ("values", 1), ("v", 1), ("keys", 1), ("k", 1), ("tok", blocks), ("last", 1),
    ):
        at[name] = step
        step += count
    return at, tuple((at[n], c) for n, c in zip(("conv_a", "conv_b", "conv_c"), tiles)), step


def tail_kernel(
    seqs, gm_ref, p_ref, q_ref, mix_ref, ql_ref, kl_ref, cg_ref, rim_ref, cv_ref, f_ref,
    sum_ref, mid_ref, z_ref, zp_ref, za_ref, zw_ref, scale_ref, tot_ref, alpha_ref,
    wts_in, v_ref, k_ref, tok_ref, proj_ref, gain_a_ref, gain_f_ref, wq_in, down_in, up_in,
    gtok_ref, up_out, down_out, out_out, qkv_out, taps_out, ga_out, gf_out,
    d, tok_t, wq_ref, wts_ref, klp, land, land_got, gn, gn_got, gt, gt_low, gt_got, mq, mk, g_acc, dk_acc, kl_low, kl_got,
    qlp, qlow, qgot, pad, facc, taps, tapsg, up_sum, up_got, down_got,
    part, got_a, sum_a, got_b, sum_b, got_c, sum_c, got_z, sm_got, sm_sum,
    kept, crossed, turned, kept_sems, cross_sems, turn_sems,
    load_sem, land_sems, gn_sems, gt_sems, kl_sems, q_sems, zd_sems, ze_sems, zu_sems, zv_sems,
    a_send, a_recv, b_sems, c_sems, zq_send, zq_recv, s_send, s_recv, s_sems,
):
    step = pl.program_id(0)
    last = pl.num_programs(0) - 1
    rows, features = tok_ref.shape[1:]
    pairs = features // 128
    ranks, own = land_got.shape[:2]
    marks = kl_got.shape[2]
    seg = rows // marks
    at, plan, _ = tail_plan(seqs, pairs, d.shape[0] // gtok_ref.shape[0])
    me, _ = seq_place()
    core, x, y, sibling, along_x, along_y = cube()
    cross = cross_copies(up_in, crossed, cross_sems)
    keep = kept_copies(up_in, kept, kept_sems)
    turn = turn_copies(kept, turned, turn_sems)
    load = pltpu.make_async_copy(wq_in, wq_ref, load_sem.at[0])
    load_wts = pltpu.make_async_copy(wts_in, wts_ref, load_sem.at[1])

    def z_copies(src, dst, first, count, sems):
        span = pl.ds(first, count)
        sends = [
            remote(src.at[peer, span], dst.at[me, span], sems.at[0, o], sems.at[1, o], {"seq": peer})
            for o, peer in seq_peers()
        ]
        return sends, pltpu.make_async_copy(src.at[me, span], dst.at[me, span], sems.at[0, 0])

    downs = [z_copies(down_in, down_got, 0, 96, zd_sems), z_copies(down_in, down_got, 96, 96, ze_sems)]
    ups = [z_copies(up_sum, up_got, 0, 80, zu_sems), z_copies(up_sum, up_got, 80, 160, zv_sems)]

    def mark_copies(src, dst, sems):
        sends = [
            remote(
                src.at[:, pl.ds(peer * marks, marks)], dst.at[me], sems.at[0, o], sems.at[1, o], {"seq": peer}
            )
            for o, peer in seq_peers()
        ]
        return sends, pltpu.make_async_copy(src.at[:, pl.ds(me * marks, marks)], dst.at[me], sems.at[0, 0])

    gn_exchange = [swap_rows(gn, gn_got, gn_sems), swap_rows(gt_low, gt_got, gt_sems)]
    kl_exchange = mark_copies(kl_low, kl_got, kl_sems)
    q_exchange = mark_copies(qlow, qgot, q_sems)

    def a_copy(p):
        return remote(
            part.at[1 - core, pl.ds(4 * p, 4)], got_a.at[pl.ds(4 * p, 4)], a_send.at[p], a_recv.at[p], sibling
        )

    def b_copies(p):
        return [
            remote(
                sum_a.at[4 * p : 4 * p + 2, :, 1 - x], got_b.at[p, 0], b_sems.at[0, p, 0], b_sems.at[1, p, 0],
                along_x,
            ),
            remote(
                sum_a.at[4 * p + 2 : 4 * p + 4, 1 - y], got_b.at[p, 1], b_sems.at[0, p, 1], b_sems.at[1, p, 1],
                along_y,
            ),
        ]

    def c_copies(p):
        return [
            remote(
                sum_b.at[p, 0, :, 1 - y], got_c.at[p, 0], c_sems.at[0, p, 0], c_sems.at[1, p, 0], along_y
            ),
            remote(
                sum_b.at[p, 1, :, 1 - x], got_c.at[p, 1], c_sems.at[0, p, 1], c_sems.at[1, p, 1], along_x
            ),
        ]

    def zq_copy(group):
        rank, place = group // 3, group % 3
        offset = lax.rem(rank - me + ranks, ranks)
        return rank, remote(
            sum_c.at[group], got_z.at[me, place], zq_send.at[group], zq_recv.at[place, offset], {"seq": rank}
        )

    def stage_b(p):
        a_copy(p).wait()
        for yx in range(4):
            sum_a[4 * p : 4 * p + 4, yx // 2, yx % 2] = add_low(
                part[core, 4 * p : 4 * p + 4, yx], got_a[4 * p : 4 * p + 4, yx]
            )
        for copy in b_copies(p):
            copy.start()

    def stage_c(p):
        for copy in b_copies(p):
            copy.wait()
        sum_b[p, 0] = add_low(sum_a[4 * p : 4 * p + 2, :, x], got_b[p, 0])
        sum_b[p, 1] = add_low(sum_a[4 * p + 2 : 4 * p + 4, y], got_b[p, 1])
        for copy in c_copies(p):
            copy.start()

    def stage_z(p):
        for copy in c_copies(p):
            copy.wait()
        sum_c[4 * p : 4 * p + 2] = add_low(sum_b[p, 0, :, y], got_c[p, 0])
        sum_c[4 * p + 2 : 4 * p + 4] = add_low(sum_b[p, 1, :, x], got_c[p, 1])
        for group in range(4 * p, 4 * p + 4):
            rank, copy = zq_copy(group)

            @pl.when(rank != me)
            def _(copy=copy):
                copy.start()

    small_copies = [
        remote(sm_sum.at[i], sm_got.at[i], s_send.at[i], s_recv.at[i], target)
        for i, target in enumerate((sibling, along_x, along_y))
    ]

    def small_spread():
        return [
            remote(sm_sum.at[3], sm_got.at[3 + me], s_sems.at[0, o], s_sems.at[1, o], {"seq": peer})
            for o, peer in seq_peers()
        ]

    def seq_rows(s):
        return pl.ds(pl.multiple_of(s * rows, rows), rows)

    @pl.when(step == 0)
    def _():
        load_wts.start()
        load.start()
        greet([sibling, along_x, along_y])
        for copy in cross + keep:
            copy.start()
        begin(downs[0])
        land[seqs * pairs :] = jnp.zeros_like(land[seqs * pairs :])

    @pl.when(step < seqs)
    def _():
        def put_land(g, v):
            for i in range(2):
                land[step * pairs + 2 * g + i] = v[:, 128 * i : 128 * i + 128]

        def put_klp(g, v):
            for i in range(2):
                klp[step * pairs + 2 * g + i] = v[:, 128 * i : 128 * i + 128]

        def put_gq(g, v):
            d[seq_rows(step), 256 * g : 256 * g + 256] = v

        first_back_step(gm_ref, p_ref, q_ref, mix_ref, lambda sl: kl_ref[step, :, sl], put_land, put_gq, put_klp)

    @pl.when(step == seqs - 1)
    def _():
        begin(swap_copies(land, land_got, own, land_sems))

    group = pick_tile(step, plan)
    moving = functools.reduce(
        jnp.logical_or, [(step >= first) & (step < first + tiles) for first, tiles in plan]
    )

    @pl.when(moving)
    def _():
        lanes = pl.ds(pl.multiple_of(group * 128, 128), 128)

        def put_taps(v):
            tapsg[0:KW, lanes] = v

        def one_sequence(seq, carry):
            def put(c, v):
                spot = pl.ds(pl.multiple_of(seq * rows + c, 64), 64)
                d[spot, pl.ds(pl.multiple_of(2 * features + group * 128, 128), 128)] = v

            one = pl.ds(seq, 1)
            conv_back_rows(
                seq, seqs, cg_ref.at[one], rim_ref.at[one], cv_ref.at[one], f_ref, put, put_taps, pad, facc, taps
            )
            return carry

        lax.fori_loop(0, seqs, one_sequence, 0)

    @pl.when(step == at["inverse"])
    def _():
        finish(swap_copies(land, land_got, own, land_sems))

        def shared():
            for r in range(ranks):
                gt_low[r] = jnp.concatenate(
                    [gt[r, i, 0:1, :] for i in range(own)] + [jnp.zeros((8 - own, 128), f32)], axis=0
                )
            for pair in gn_exchange:
                begin(pair)

        inverse_back_step(
            land_got, ql_ref, kl_ref, sum_ref, mid_ref, z_ref, zp_ref, za_ref, zw_ref, scale_ref, tot_ref, alpha_ref,
            gn, gt, mq, mk, g_acc, dk_acc, shared,
        )
        add_pairs(klp, mk, me * own, seqs * pairs)
        kl_low[...] = klp[...].astype(bf16)
        begin(kl_exchange)

    @pl.when(step == at["one"])
    def _():
        for copy in cross + keep:
            copy.wait()
        cross_add(kept, crossed)
        for copy in turn:
            copy.start()
        for pair in gn_exchange:
            finish(pair)
        load_wts.wait()

    def gn_of(s):
        def of(i):
            p = s * pairs + i
            return gn_got[p // own, p % own]

        return of

    def land_rows(of):
        total = of(0).astype(f32)
        for r in range(1, ranks):
            total = total + of(r).astype(f32)
        return total * (1.0 / seg)

    @pl.when(step == at["values"])
    def _():
        sm_sum[0, KW:, :] = jnp.zeros_like(sm_sum[0, KW:, :])
        sm_sum[0, :KW, :] = tapsg[:KW]
        sm_sum[0, KW : KW + 1, :] = jnp.sum(gain_a_ref[...], axis=0, keepdims=True)
        sm_sum[0, KW + 1 : KW + 2, :] = jnp.sum(gain_f_ref[...], axis=0, keepdims=True)
        small_copies[0].start()

    for i in range(1, 4):
        @pl.when(step == at["values"] + i)
        def _(i=i):
            small_copies[i - 1].wait()
            sm_sum[i] = sm_sum[i - 1] + sm_got[i - 1]
            if i < 3:
                small_copies[i].start()
            else:
                for copy in small_spread():
                    copy.start()

    @pl.when((step >= at["one"]) & (step < at["one"] + seqs))
    def _():
        s = step - at["one"]

        def gt_of(i):
            p = s * pairs + i
            return gt_got[p // own, pl.ds(p % own, 1), :]

        def put_gs(g, val):
            d[seq_rows(s), features + 256 * g : features + 256 * g + 256] = val

        def put_qlp(g, val):
            for i in range(2):
                qlp[s * pairs + 2 * g + i] = val[:, 128 * i : 128 * i + 128]

        first_third(wts_ref.at[pl.ds(s, 1)], v_ref, k_ref, gn_of(s), gt_of, put_gs, put_qlp)
        tok_t[:, seq_rows(s)] = tok_ref[0].T

    @pl.when(step == at["one"] + seqs - 1)
    def _():
        add_pairs(qlp, mq, me * own, seqs * pairs)
        qlow[...] = qlp[...].astype(bf16)
        begin(q_exchange)

    @pl.when(step == at["q"])
    def _():
        finish(q_exchange)
        for copy in turn:
            copy.wait()
        turn_add(up_sum, kept, turned)
        begin(downs[1])
        begin(ups[0])

        def fill(s, carry):
            for g in range(pairs):
                spread = land_rows(lambda r: qgot[r, s * pairs + g])
                for m in range(marks):
                    spot = pl.ds(pl.multiple_of(s * rows + m * seg, seg), seg)
                    val = d[spot, 128 * g : 128 * g + 128].astype(f32)
                    low = (val + spread[m : m + 1]).astype(bf16) * jnp.asarray(0.125, bf16)
                    d[spot, 128 * g : 128 * g + 128] = low
            return carry

        lax.fori_loop(0, seqs, fill, 0)

    @pl.when(step == at["keys"])
    def _():
        finish(kl_exchange)

    @pl.when(step == at["keys"])
    def _():
        masks = group_masks((M, 4 * E), 4, bf16)

        def keys(s, carry):
            for g in range(features // 256):
                ks = slice(features + 256 * g, features + 256 * g + 256)
                val = dot(d[seq_rows(s), ks], block_diag(ql_ref[s, :, 256 * g : 256 * g + 256], masks))
                for i in range(2):
                    p = s * pairs + 2 * g + i
                    spread = land_rows(lambda r: kl_got[r, p])
                    lane = features + 256 * g + 128 * i
                    for m in range(marks):
                        spot = pl.ds(pl.multiple_of(s * rows + m * seg, seg), seg)
                        d[spot, lane : lane + 128] = (
                            val[m * seg : m * seg + seg, 128 * i : 128 * i + 128] + spread[m : m + 1]
                        ).astype(bf16)
            return carry

        lax.fori_loop(0, seqs, keys, 0)

    @pl.when(step == at["values"])
    def _():
        masks = group_masks((M, 4 * E), 4, bf16)

        def values(s, carry):
            of = gn_of(s)
            for g in range(features // 256):
                gd = block_diag(jnp.concatenate([of(2 * g), of(2 * g + 1)], axis=1), masks)
                vs = slice(2 * features + 256 * g, 2 * features + 256 * g + 256)
                here = seq_rows(s)
                d[here, vs] = (
                    dot(wts_ref[s, :, 256 * g : 256 * g + 256], gd) + d[here, vs].astype(f32)
                ).astype(bf16)
            return carry

        lax.fori_loop(0, seqs, values, 0)

    @pl.when(step == at["tok"])
    def _():
        load.wait()

    for when, stages in (
        (at["conv_c"] + 1, [(stage_b, 0)]),
        (at["values"], [(stage_c, 0)]),
        (at["keys"], [(stage_z, 0)]),
        (at["k"], [(stage_b, 2)]),
    ):
        @pl.when(step == when)
        def _(stages=stages):
            for stage, p in stages:
                stage(p)

    @pl.when(step == at["conv_c"])
    def _():
        begin(ups[1])

    @pl.when((step == at["q"]) | (step == at["k"]) | (step == at["v"]))
    def _():
        p = jnp.where(step == at["q"], 0, jnp.where(step == at["k"], 1, 2))
        for c in range(2):
            cols = pl.ds(pl.multiple_of(p * features + 384 * c, 128), 384)
            low = dot(tok_t[...], d[:, cols]).astype(bf16)
            for i in range(2):
                for dd in range(8):
                    part[dd % 2, 4 * p + 2 * c + i, dd // 2] = fold(
                        low[96 * dd : 96 * dd + 96, 192 * i : 192 * i + 192]
                    )
        a_copy(p).start()

    late_stages = {1: [(stage_b, 1)], 2: [(stage_c, 2)], 5: [(stage_c, 1), (stage_z, 2)]}

    @pl.when((step >= at["tok"]) & (step < last))
    def _():
        size = gtok_ref.shape[0] // 2
        for h in range(2):
            for slot, stages in late_stages.items():
                if slot % 2 == h:
                    @pl.when(step == at["tok"] + slot // 2)
                    def _(stages=stages):
                        for stage, p in stages:
                            stage(p)

            spot = pl.ds(pl.multiple_of((step - at["tok"]) * 2 * size + h * size, size), size)
            near = slice(h * size, h * size + size)
            gtok_ref[near, :] = (proj_ref[near, :].astype(f32) + dot_nt(d[spot, :], wq_ref[...])).astype(bf16)

    def unfold(block):
        return jnp.concatenate([block[:, :192], block[:, 192:]], axis=0)

    def rank_sum(got):
        total = got[0].astype(f32)
        for r in range(1, ranks):
            total = total + got[r].astype(f32)
        return total

    @pl.when(step == last)
    def _():
        stage_z(1)
        for copy in small_spread():
            copy.wait()
        sm_got[3 + me] = sm_sum[3]
        small = (sm_got[3] + sm_got[4]) + (sm_got[5] + sm_got[6])
        taps_out[...] = small[:KW]
        ga_out[...] = small[KW : KW + 1].reshape(features)
        gf_out[...] = small[KW + 1 : KW + 2].reshape(features)
        for pair in downs + ups:
            finish(pair)
        down_out[...] = rank_sum(down_got)
        total = rank_sum(up_got)
        up_out[:, :384] = total[:96]
        up_out[:, 384:] = total[96:192]
        out_out[...] = unfold(total[192:240])
        for group in range(12):
            rank, copy = zq_copy(group)

            @pl.when(rank != me)
            def _(copy=copy):
                copy.wait_send()

        for o in range(1, ranks):
            source = lax.rem(me - o + ranks, ranks)
            for place in range(3):
                remote(
                    sum_c.at[0], got_z.at[source, place], zq_send.at[0], zq_recv.at[place, o], {"seq": source}
                ).wait_recv()
        for place in range(3):
            got_z[me, place] = sum_c[3 * me + place]
        qkv_out[...] = jnp.concatenate(
            [unfold(sum(got_z[r, place].astype(f32) for r in range(ranks))) for place in range(3)], axis=1
        )


def tail(
    gm, probs, q, mixed, q_land, k_land, rim, v, taps, saved, weights, k, tokens, proj, gain_a, gain_f, w_qkv, downs, ups
):
    seqs, rows, features = tokens.shape
    ranks = lax.axis_size("seq")
    pairs = features // 128
    count = seqs * pairs
    own = saved[0].shape[0]
    marks = M // ranks
    total = seqs * rows
    size = 512
    blocks = total // size
    at, plan, steps = tail_plan(seqs, pairs, blocks)
    clip = lambda i, name: jnp.clip(i - at[name], 0, seqs - 1)
    tile = lambda i: pick_tile(i, plan)
    by_seq = lambda shape, of: pl.BlockSpec((1,) + shape, lambda i: (of(i), 0, 0))
    head = lambda i: clip(i, "first")
    one = lambda i: clip(i, "one")
    conv_spec = pl.BlockSpec((seqs, rows, 128), lambda i: (0, 0, tile(i)))
    rim_spec = pl.BlockSpec((seqs, 2, RIM, 128), lambda i: (0, 0, 0, tile(i)))
    tap_spec = pl.BlockSpec((KW, 128), lambda i: (0, tile(i)))
    later = pl.BlockSpec((size, features), lambda i: (jnp.clip(i - at["tok"], 0, blocks - 1), 0))
    whole = lambda a: pl.BlockSpec(a.shape, lambda i: (0,) * len(a.shape), pipeline_mode=pl.Buffered(1))
    flat = (rows, features)
    vm = lambda *shape: pltpu.VMEM(shape, bf16)
    wide = lambda *shape: pltpu.VMEM(shape, f32)
    dma = pltpu.SemaphoreType.DMA
    shares = [
        jax.ShapeDtypeStruct(s, f32)
        for s in ((96, 768), (192, 384), (96, 192), (96, 576), (KW, 768), (768,), (768,))
    ]
    return pl.pallas_call(
        functools.partial(tail_kernel, seqs),
        grid=(steps,),
        in_specs=[
            by_seq(flat, head), by_seq((features, rows), head), by_seq(flat, head),
            pl.BlockSpec((pairs, M, 128), lambda i: (head(i), 0, 0)), whole(q_land), whole(k_land),
            conv_spec, rim_spec, conv_spec, tap_spec,
        ]
        + [whole(a) for a in saved]
        + [ANY, by_seq(flat, one), by_seq(flat, one), by_seq(flat, one), later]
        + [whole(gain_a), whole(gain_f), ANY, ANY, ANY],
        out_specs=[later] + [whole(a) for a in shares],
        out_shape=[jax.ShapeDtypeStruct((total, features), bf16)] + shares,
        scratch_shapes=[
            vm(total, 3 * features), vm(features, total), vm(*w_qkv.shape), vm(*weights.shape), wide(count, M, 128),
            vm(ranks * own, M, 128), vm(ranks, own, M, 128), vm(ranks, own, M, 128), vm(ranks, own, M, 128),
            wide(ranks, own, 8, 128), wide(ranks, 8, 128), wide(ranks, 8, 128), wide(own, M, 128), wide(own, M, 128),
            wide(own, M, 128), wide(own, M, 128), vm(count, M, 128), vm(ranks, count, marks, 128),
            wide(count, M, 128), vm(count, M, 128), vm(ranks, count, marks, 128), wide(rows + 2 * RIM, 128),
            wide(KW * 8, 128), wide(40, 128), wide(40, features), vm(4, 240, 384), vm(ranks, 240, 384),
            vm(ranks, 192, 384),
            vm(2, 12, 4, 48, 384), vm(12, 4, 48, 384), vm(12, 2, 2, 48, 384), vm(3, 2, 2, 2, 48, 384),
            vm(3, 2, 2, 2, 48, 384), vm(3, 2, 2, 48, 384), vm(12, 48, 384), vm(ranks, 3, 48, 384),
            wide(3 + ranks, 40, features), wide(4, 40, features),
        ]
        + stage_scratch(240)
        + [dma((2,))]
        + [rank_sems() for _ in range(9)]
        + [
            dma((3,)), dma((3,)), dma((2, 3, 2)), dma((2, 3, 2)), dma((12,)), dma((3, ranks)), dma((3,)), dma((3,)),
            rank_sems(),
        ],
        compiler_params=params(63 * MB, collective_id=5, has_side_effects=True),
        name="tail",
    )(
        gm, probs, q, mixed, q_land, k_land, gm, rim, v, taps, *saved, weights, v, k, tokens, proj, gain_a, gain_f,
        w_qkv, downs, ups,
    )


def halo(cells, width):
    count = lax.axis_size("seq")
    head, tail = cells[:, :width], cells[:, cells.shape[1] - width :]
    left = lax.ppermute(tail, "seq", [(i, i + 1) for i in range(count - 1)])
    right = lax.ppermute(head, "seq", [(i + 1, i) for i in range(count - 1)])
    return jnp.stack([left, right], axis=1)


def scatter_sum(grad):
    share = lax.psum_scatter(grad, "dp", scatter_dimension=0, tiled=True)
    return lax.psum_scatter(share, "seq", scatter_dimension=1, tiled=True).astype(f32)


def per_device_general(tokens, w_qkv, w_out, w_up, w_down, conv_filter, gain_att, gain_ffn, grad_out):
    seqs, rows, features = tokens.shape
    ranks = lax.axis_size("seq")
    rank = lax.axis_index("seq")
    marks = M // ranks
    ff = w_up.shape[1]
    pairs = seqs * (features // 128)
    own = -(-pairs // ranks)

    def from_pairs(x):
        x = x[:pairs].reshape(seqs, features // 128, M, 128).transpose(0, 2, 1, 3)
        return x.reshape(seqs, M, features)

    def pad_pairs(x):
        return jnp.pad(x, ((0, ranks * own - pairs),) + ((0, 0),) * (x.ndim - 1))

    def exchange(x):
        out = lax.all_to_all(pad_pairs(x), "seq", 0, 0, tiled=True)
        return out.reshape((ranks, own) + x.shape[1:])

    taps = conv_filter
    q, k, v, k_part, q_land, v_rim = project(tokens, w_qkv, marks)
    first_group = 4
    weights, probs, k_land, conv_a, num_parts, stat_parts = scores(
        q, k, v, q_land, k_part, v_rim, taps, own, first_group
    )
    mixed_pairs, conv_b, *saved = inverse(num_parts, stat_parts, q_land, k_land, v, v_rim, taps, first_group)
    mixed = mixed_pairs
    layer_out, proj, gm, wg, gains = row_pass(
        tokens, probs, conv_a, conv_b, mixed, grad_out, w_out, w_up, w_down, gain_att, gain_ffn
    )
    shape3 = (seqs, rows, features)
    gm = gm.reshape(shape3)
    chunks = ff // features
    up_share = scatter_sum(wg[:chunks].transpose(1, 0, 2).reshape(features, ff))
    down_share = scatter_sum(wg[chunks : 2 * chunks].transpose(0, 2, 1).reshape(ff, features))
    out_share = scatter_sum(wg[2 * chunks])
    land_part, gq, k_land_part = first_back(gm, probs, q, mixed, k_land)
    g_rim = halo(gm, RIM)
    land_parts = exchange(land_part)
    grad_conv, taps_grad = conv_back(gm, g_rim, v, taps)
    gn_own, gt_own, mid_q, mid_k = inverse_back(land_parts, q_land, k_land, saved)

    def give_back(x):
        x = x.reshape((ranks * own,) + x.shape[2:])
        return lax.all_to_all(x, "seq", 0, 0, tiled=True)[:pairs]

    grad_values, gk, q_land_part = third_back(
        weights, v, k, grad_conv, give_back(gn_own), give_back(gt_own), q_land
    )

    def place(x):
        full = jnp.zeros((ranks * own, M, 128), f32)
        return from_pairs(lax.dynamic_update_slice_in_dim(full, x, rank * own, 0))

    both = jnp.stack([q_land_part + place(mid_q), k_land_part + place(mid_k)]).astype(bf16)
    both = both.reshape(2, seqs, ranks, marks, features).transpose(2, 0, 1, 3, 4)
    both = lax.all_to_all(both, "seq", 0, 0, tiled=True).astype(f32).sum(0)
    grad_tokens, qkv_grad = last_pass(tokens, gq, gk, grad_values, both[0], both[1], proj.reshape(shape3), w_qkv)
    qkv_share = scatter_sum(qkv_grad.transpose(1, 0, 2).reshape(features, 3 * features))
    gains = gains.reshape(2, 8, features).sum(1)
    small = lax.psum(jnp.concatenate([taps_grad, gains]), ("dp", "seq"))
    return (
        layer_out.reshape(shape3),
        grad_tokens,
        qkv_share,
        out_share,
        up_share,
        down_share,
        small[:KW],
        small[KW],
        small[KW + 1],
    )


def deliver_kernel(*refs):
    count = len(refs) // 2
    for i in range(count):
        if i < 2:
            refs[count + i][...] = refs[i][...]
        else:
            @pl.when(pl.program_id(0) == 0)
            def _(i=i):
                refs[count + i][...] = refs[i][...]


def deliver(*arrays):
    steps = 4
    split = lambda a: pl.BlockSpec((a.shape[0] // steps, a.shape[1]), lambda i: (i, 0))
    whole = lambda a: pl.BlockSpec(a.shape, lambda i: (0,) * len(a.shape))
    specs = [split(a) for a in arrays[:2]] + [whole(a) for a in arrays[2:]]
    return pl.pallas_call(
        deliver_kernel,
        grid=(steps,),
        in_specs=specs,
        out_specs=specs,
        out_shape=[jax.ShapeDtypeStruct(a.shape, a.dtype) for a in arrays],
        compiler_params=params(62 * MB),
        name="deliver",
    )(*arrays)


def per_device(tokens, w_qkv, w_out, w_up, w_down, conv_filter, gain_att, gain_ffn, grad_out):
    seqs, rows, features = tokens.shape
    ranks = lax.axis_size("seq")
    marks = M // ranks
    pairs = seqs * (features // 128)
    own = -(-pairs // ranks)
    taps = conv_filter
    shape3 = (seqs, rows, features)

    q, k, v, weights, probs, q_land, k_land, v_rim, conv_out, mixed, *saved = front(tokens, w_qkv, taps, own)
    layer_out, normed, s_att, gdl, slope, hid_t, mix_t, gain_f, downs = rows_forward(
        tokens, probs, conv_out, mixed, grad_out, w_out, w_up, w_down, gain_att, gain_ffn
    )
    proj, gm, gain_a, downs, ups, g_rim = rows_backward(
        gdl, slope, normed, s_att, w_out, gain_att, w_down, w_up, hid_t, mix_t, downs.reshape(4, 2, 2, 192, 384), seqs
    )
    grad_tokens, up, down, out, qkv, taps_all, gain_att_all, gain_ffn_all = tail(
        gm.reshape(shape3), probs, q, mixed, q_land, k_land, g_rim, v, taps, saved, weights, k, tokens, proj, gain_a,
        gain_f, w_qkv, downs, ups.reshape(4, 2, 2, 240, 384),
    )
    layer_out, grad_tokens, qkv, out, up, down, taps_all, gain_att_all, gain_ffn_all = deliver(
        layer_out, grad_tokens, qkv, out, up, down, taps_all, gain_att_all, gain_ffn_all
    )
    return (
        layer_out.reshape(shape3),
        grad_tokens.reshape(shape3),
        qkv,
        out,
        up,
        down.T,
        taps_all,
        gain_att_all,
        gain_ffn_all,
    )


def solution(mesh):
    placed = (P("dp", "seq", None), P(), P(), P(), P(), P(), P(), P(), P("dp", "seq", None))
    eight_by_four = mesh.shape["dp"] == 8 and mesh.shape["seq"] == 4
    return jax.shard_map(
        per_device if eight_by_four else per_device_general,
        mesh=mesh,
        in_specs=placed,
        out_specs=(
            P("dp", "seq", None),
            P("dp", "seq", None),
            P("dp", "seq"),
            P("dp", "seq"),
            P("dp", "seq"),
            P("dp", "seq"),
            P(),
            P(),
            P(),
        ),
        check_vma=False,
    )
```

```python
import functools

import jax
import jax.numpy as jnp
from jax import lax
from jax.experimental import pallas as pl
from jax.experimental.pallas import tpu as pltpu
from jax.sharding import PartitionSpec as P

H = 12
E = 64
M = 64
KW = 33
RIM = KW // 2
NEWTON = 6

f32 = jnp.float32
bf16 = jnp.bfloat16
epsilon = 1e-05
root_half = 0.7071067811865476
inv_root_two_pi = 0.3989422804014327
MB = 1 << 20

ERFC_P = 0.6
ERFC_C = (0.37028039425845705, 0.14043533559747823, 0.7278464793107866, -0.23856251479455173)
log2_e = 1.4426950408889634


def dot(a, b):
    return lax.dot_general(a, b, (((1,), (0,)), ((), ())), preferred_element_type=f32)


def dot_nt(a, b):
    return lax.dot_general(a, b, (((1,), (1,)), ((), ())), preferred_element_type=f32)


def dot_tn(a, b):
    return lax.dot_general(a, b, (((0,), (0,)), ((), ())), preferred_element_type=f32)


def lane_group(shape):
    return lax.broadcasted_iota(jnp.int32, shape, len(shape) - 1) // E


def group_masks(shape, count, dtype):
    groups = lane_group(shape)
    return [(groups == h).astype(f32).astype(dtype) for h in range(count)]


def block_diag(x, masks):
    return jnp.concatenate([x * m for m in masks], axis=0)


def diag_blocks(n, masks):
    return sum(n[E * h : E * h + E] * m for h, m in enumerate(masks))


def quad(ref, g):
    return jnp.concatenate([ref[2 * g], ref[2 * g + 1]], axis=1)


def params(limit=None, **kw):
    return pltpu.CompilerParams(vmem_limit_bytes=limit, **kw)


MESH = pl.DeviceIdType.MESH
ANY = pl.BlockSpec(memory_space=pl.ANY)


def seq_place():
    return lax.axis_index("seq"), lax.axis_size("seq")


def seq_peers():
    me, count = seq_place()
    return [(o, lax.rem(me + o, count)) for o in range(1, count)]


def greet(extra=()):
    barrier = pltpu.get_barrier_semaphore()
    targets = [{"seq": peer} for _, peer in seq_peers()] + list(extra)
    for target in targets:
        pl.semaphore_signal(barrier, inc=1, device_id=target, device_id_type=MESH)
    pl.semaphore_wait(barrier, len(targets))


def remote(src, dst, send, recv, target):
    return pltpu.make_async_remote_copy(
        src_ref=src, dst_ref=dst, send_sem=send, recv_sem=recv, device_id=target, device_id_type=MESH
    )


def swap_copies(src, dst, own, sems):
    me, count = seq_place()
    copies = [
        remote(src.at[pl.ds(peer * own, own)], dst.at[me], sems.at[0, o], sems.at[1, o], {"seq": peer})
        for o, peer in seq_peers()
    ]
    return copies, pltpu.make_async_copy(src.at[pl.ds(me * own, own)], dst.at[me], sems.at[0, 0])


def spread_copies(src, dst, own, sems):
    me, count = seq_place()
    at = dst.at[pl.ds(me * own, own)]
    copies = [
        remote(src, at, sems.at[0, o], sems.at[1, o], {"seq": peer}) for o, peer in seq_peers()
    ]
    return copies, pltpu.make_async_copy(src, at, sems.at[0, 0])


def begin(pair):
    for copy in pair[0]:
        copy.start()
    pair[1].start()


def finish(pair):
    for copy in pair[0]:
        copy.wait()
    pair[1].wait()


def swap_rows(src, dst, sems):
    me, _ = seq_place()
    copies = [
        remote(src.at[peer], dst.at[me], sems.at[0, o], sems.at[1, o], {"seq": peer}) for o, peer in seq_peers()
    ]
    return copies, pltpu.make_async_copy(src.at[me], dst.at[me], sems.at[0, 0])


def cube():
    d = lax.axis_index("dp")
    core, x, y = d % 2, (d // 2) % 2, d // 4
    return core, x, y, {"dp": d + 1 - 2 * core}, {"dp": d + 2 - 4 * x}, {"dp": d + 4 - 8 * y}


def add_low(a, b):
    return (a.astype(f32) + b.astype(f32)).astype(bf16)


def rank_sems():
    return pltpu.SemaphoreType.DMA((2, lax.axis_size("seq")))


def project_kernel(
    tok_ref, w_ref, q_ref, k_ref, v_ref, kl_ref, land_out, rim_out, land, rim, send, recv, local, rim_send, rim_recv,
    rim_local,
):
    step = pl.program_id(0)
    seqs = pl.num_programs(0)
    me, count = seq_place()
    rows, features = tok_ref.shape[1:]
    marks = land.shape[1]
    seg = rows // marks

    @pl.when(step == 0)
    def _():
        greet()

    x = tok_ref[0]
    for part, out in enumerate((q_ref, k_ref, v_ref)):
        for c in range(0, features, 256):
            p = dot(x, w_ref[:, part * features + c : part * features + c + 256])
            if part == 0:
                p = 0.125 * p
            low = p.astype(bf16)
            out[0, :, c : c + 256] = low
            if part < 2:
                total = low.astype(f32).reshape(marks, seg, 256).sum(1)
                mean = (total * (1.0 / seg)).astype(bf16)
                if part == 0:
                    land[step, :, c : c + 256] = mean
                else:
                    kl_ref[0, :, c : c + 256] = mean
            else:
                rim[step, 0, :, c : c + 256] = low[rows - RIM :]
                rim[step, 1, :, c : c + 256] = low[:RIM]

    def copies(s):
        spot = land_out.at[s, pl.ds(me * marks, marks)]
        sends = [
            remote(land.at[s], spot, send.at[s, o], recv.at[s, o], {"seq": peer}) for o, peer in seq_peers()
        ]
        return sends, pltpu.make_async_copy(land.at[s], spot, local.at[s])

    def rim_copy(s, side):
        there = lax.rem(me + (1 if side == 0 else count - 1), count)
        return remote(
            rim.at[s, side], rim_out.at[s, side], rim_send.at[s, side], rim_recv.at[s, side], {"seq": there}
        )

    begin(copies(step))
    for side in range(2):
        rim_copy(step, side).start()

    @pl.when(step == seqs - 1)
    def _():
        def drain(s, carry):
            finish(copies(s))
            for side in range(2):
                rim_copy(s, side).wait()
            return carry

        lax.fori_loop(0, seqs, drain, 0)


def project(tokens, w_qkv, marks):
    seqs, rows, features = tokens.shape
    ranks = lax.axis_size("seq")
    full = pl.BlockSpec((1, rows, features), lambda s: (s, 0, 0))
    dma = pltpu.SemaphoreType.DMA
    return pl.pallas_call(
        project_kernel,
        grid=(seqs,),
        in_specs=[full, pl.BlockSpec(w_qkv.shape, lambda s: (0, 0), pipeline_mode=pl.Buffered(1))],
        out_specs=[full] * 3 + [pl.BlockSpec((1, marks, features), lambda s: (s, 0, 0))] + [ANY] * 2,
        out_shape=[jax.ShapeDtypeStruct(tokens.shape, bf16)] * 3
        + [
            jax.ShapeDtypeStruct((seqs, marks, features), bf16),
            jax.ShapeDtypeStruct((seqs, M, features), bf16),
            jax.ShapeDtypeStruct((seqs, 2, RIM, features), bf16),
        ],
        scratch_shapes=[
            pltpu.VMEM((seqs, marks, features), bf16), pltpu.VMEM((seqs, 2, RIM, features), bf16),
            dma((seqs, ranks)), dma((seqs, ranks)), dma((seqs,)), dma((seqs, 2)), dma((seqs, 2)), dma((seqs,)),
        ],
        compiler_params=params(62 * MB, collective_id=0, has_side_effects=True),
        name="project",
    )(tokens, w_qkv)


def fill_taps(taps, f_ref):
    taps[0:KW, :] = f_ref[...].astype(f32)


def fill_pad(pad, x_ref, rim_ref):
    rows = x_ref.shape[1]
    me, count = seq_place()
    pad[0:RIM, :] = jnp.where(me > 0, rim_ref[0, 0].astype(f32), 0.0)
    pad[RIM : RIM + rows, :] = x_ref[0].astype(f32)
    pad[RIM + rows : RIM + rows + RIM, :] = jnp.where(me < count - 1, rim_ref[0, 1].astype(f32), 0.0)


def conv_tile(v_ref, rim_ref, taps_ref, o_ref, pad, f_ref):
    rows = v_ref.shape[1]
    fill_pad(pad, v_ref, rim_ref)
    fill_taps(f_ref, taps_ref)
    conv_rows(o_ref, pad, f_ref, rows)


def conv_rows(o_ref, pad, f_ref, rows):
    for c in range(0, rows, 64):
        acc = jnp.zeros((64, 128), f32)
        for j in range(KW):
            acc = acc + f_ref[j : j + 1, :] * pad[c + j : c + j + 64, :]
        o_ref[0, c : c + 64, :] = acc.astype(bf16)


def conv_specs(rows, first_step, first_group, groups):
    at = lambda i: jnp.maximum(i - first_step, 0)
    seq = lambda i: at(i) // groups
    group = lambda i: at(i) % groups
    return (
        pl.BlockSpec((1, rows, 128), lambda i: (seq(i), 0, first_group + group(i))),
        pl.BlockSpec((1, 2, RIM, 128), lambda i: (seq(i), 0, 0, first_group + group(i))),
        pl.BlockSpec((KW, 128), lambda i: (0, first_group + group(i))),
        pl.BlockSpec((1, rows, 128), lambda i: (seq(i), 0, group(i))),
    )


def conv_back_rows(seq, seqs, g_ref, rim_ref, v_ref, taps_ref, put, put_taps, pad, facc, f_ref):
    rows = v_ref.shape[1]
    fill_pad(pad, g_ref, rim_ref)
    fill_taps(f_ref, taps_ref)

    @pl.when(seq == 0)
    def _():
        facc[...] = jnp.zeros_like(facc)

    for c in range(0, rows, 64):
        acc = jnp.zeros((64, 128), f32)
        vals = v_ref[0, c : c + 64, :].astype(f32)
        for j in range(KW):
            moved = pad[c + 2 * RIM - j : c + 2 * RIM - j + 64, :]
            acc = acc + f_ref[j : j + 1, :] * moved
            facc[8 * j : 8 * j + 8, :] += (vals * moved).reshape(8, 8, 128).sum(0)
        put(c, acc.astype(bf16))

    @pl.when(seq == seqs - 1)
    def _():
        put_taps(facc[...].reshape(KW, 8, 128).sum(1))


def conv_back_tile(seq, seqs, g_ref, rim_ref, v_ref, taps_ref, o_ref, gf_ref, pad, facc, f_ref):
    def put(c, v):
        o_ref[0, c : c + 64, :] = v

    def put_taps(v):
        gf_ref[...] = v

    conv_back_rows(seq, seqs, g_ref, rim_ref, v_ref, taps_ref, put, put_taps, pad, facc, f_ref)


def conv_back_kernel(g_ref, rim_ref, v_ref, f_ref, o_ref, gf_ref, pad, facc, taps):
    conv_back_tile(
        pl.program_id(1), pl.num_programs(1), g_ref, rim_ref, v_ref, f_ref, o_ref, gf_ref, pad, facc, taps
    )


def conv_back_specs(rows, seqs, first_step, first_group):
    at = lambda i: jnp.maximum(i - first_step, 0)
    seq = lambda i: at(i) % seqs
    group = lambda i: at(i) // seqs
    return (
        pl.BlockSpec((1, rows, 128), lambda i: (seq(i), 0, first_group + group(i))),
        pl.BlockSpec((1, 2, RIM, 128), lambda i: (seq(i), 0, 0, first_group + group(i))),
        pl.BlockSpec((KW, 128), lambda i: (0, first_group + group(i))),
        pl.BlockSpec((1, rows, 128), lambda i: (seq(i), 0, group(i))),
        pl.BlockSpec((KW, 128), lambda i: (0, group(i))),
    )


def conv_back(g, rim, v, taps):
    seqs, rows, features = v.shape
    sp = lambda n: pl.BlockSpec((1, n, 128), lambda g, s: (s, 0, g))
    fs = pl.BlockSpec((KW, 128), lambda g, s: (0, g))
    return pl.pallas_call(
        conv_back_kernel,
        grid=(features // 128, seqs),
        in_specs=[sp(rows), pl.BlockSpec((1, 2, RIM, 128), lambda g, s: (s, 0, 0, g)), sp(rows), fs],
        out_specs=[sp(rows), fs],
        out_shape=[jax.ShapeDtypeStruct(v.shape, bf16), jax.ShapeDtypeStruct((KW, features), f32)],
        scratch_shapes=[pltpu.VMEM((rows + 2 * RIM, 128), f32), pltpu.VMEM((KW * 8, 128), f32), pltpu.VMEM((40, 128), f32)],
        name="conv_back",
    )(g, rim, v, taps)


def third_score_step(step, k_ref, v_ref, ql_ref, w_ref, num_ref, stat_ref, own):
    features = k_ref.shape[2]
    pairs = features // 128
    masks = group_masks((M, 4 * E), 4, bf16)
    masks_wide = group_masks((M, 4 * E), 4, f32)
    for g in range(features // 256):
        sl = slice(256 * g, 256 * g + 256)
        s3 = dot_nt(k_ref[0, :, sl], block_diag(ql_ref[0, :, sl], masks))
        peak = jnp.max(s3, axis=0, keepdims=True)
        e3 = jnp.exp(s3 - peak)
        total = jnp.sum(e3, axis=0, keepdims=True)
        low = e3.astype(bf16)
        w_ref[0, :, sl] = low
        num = diag_blocks(dot_tn(low, v_ref[0, :, sl]), masks_wide).astype(bf16)
        for i in range(2):
            lanes = slice(128 * i, 128 * i + 128)
            p = step * pairs + 2 * g + i
            num_ref[p] = num[:, lanes]
            stat_ref[p // own, pl.ds(p % own, 1), :] = peak[:, lanes]
            stat_ref[p // own, pl.ds(8 + p % own, 1), :] = total[:, lanes]


def first_score_step(q_ref, kl, p_ref):
    features = q_ref.shape[2]
    masks = group_masks((M, 4 * E), 4, bf16)
    for g in range(features // 256):
        sl = slice(256 * g, 256 * g + 256)
        s1 = dot_nt(block_diag(kl[:, sl], masks), q_ref[0, :, sl])
        for h in range(4):
            x = s1[E * h : E * h + E]
            e1 = jnp.exp(x - jnp.max(x, axis=0, keepdims=True))
            at = 256 * g + E * h
            p_ref[0, at : at + E, :] = (e1 * (1.0 / jnp.sum(e1, axis=0, keepdims=True))).astype(bf16)


def scores_kernel(
    seqs, own, q_ref, k_ref, v_ref, ql_ref, kp_ref, cv_ref, rim_ref, f_ref, w_ref, p_ref, kl_ref, co_ref, num_out,
    stat_out, num, stat, kl, pad, taps, num_sems, stat_sems, kl_sems,
):
    step = pl.program_id(0)
    steps = pl.num_programs(0)
    pairs = q_ref.shape[2] // 128
    marks = kp_ref.shape[1]
    me, _ = seq_place()

    def mark_copies():
        spot = kl.at[:, pl.ds(me * marks, marks)]
        sends = [
            remote(kp_ref, spot, kl_sems.at[0, o], kl_sems.at[1, o], {"seq": peer}) for o, peer in seq_peers()
        ]
        return sends, pltpu.make_async_copy(kp_ref, spot, kl_sems.at[0, 0])

    @pl.when(step == 0)
    def _():
        greet()
        begin(mark_copies())
        stat[...] = jnp.zeros_like(stat)
        if num.shape[0] > seqs * pairs:
            num[seqs * pairs :] = jnp.zeros_like(num[seqs * pairs :])

    @pl.when(step < seqs)
    def _():
        third_score_step(step, k_ref, v_ref, ql_ref, w_ref, num, stat, own)

    @pl.when(step == seqs - 1)
    def _():
        begin(swap_copies(num, num_out, own, num_sems))
        begin(swap_rows(stat, stat_out, stat_sems))

    @pl.when(step == seqs)
    def _():
        finish(mark_copies())
        kl_ref[...] = kl[...]

    @pl.when((step >= seqs) & (step < 2 * seqs))
    def _():
        first_score_step(q_ref, kl[step - seqs], p_ref)

    @pl.when(step >= 2 * seqs)
    def _():
        conv_tile(cv_ref, rim_ref, f_ref, co_ref, pad, taps)

    @pl.when(step == steps - 1)
    def _():
        finish(swap_copies(num, num_out, own, num_sems))
        finish(swap_rows(stat, stat_out, stat_sems))


def scores(q, k, v, q_land, k_part, rim, taps, own, groups):
    seqs, rows, features = q.shape
    marks = k_part.shape[1]
    ranks = lax.axis_size("seq")
    here = lambda i: jnp.minimum(i, seqs - 1)
    then = lambda i: jnp.clip(i - seqs, 0, seqs - 1)
    full = pl.BlockSpec((1, rows, features), lambda i: (here(i), 0, 0))
    next_full = pl.BlockSpec((1, rows, features), lambda i: (then(i), 0, 0))
    whole = lambda a: pl.BlockSpec(a.shape, lambda i: (0,) * len(a.shape), pipeline_mode=pl.Buffered(1))
    k_land = jax.ShapeDtypeStruct((seqs, M, features), bf16)
    cv, rims, ft, co = conv_specs(rows, 2 * seqs, 0, groups)
    return pl.pallas_call(
        functools.partial(scores_kernel, seqs, own),
        grid=(2 * seqs + seqs * groups,),
        in_specs=[
            next_full, full, full, pl.BlockSpec((1, M, features), lambda i: (here(i), 0, 0)), whole(k_part), cv,
            rims, ft,
        ],
        out_specs=[full, pl.BlockSpec((1, features, rows), lambda i: (then(i), 0, 0)), whole(k_land), co, ANY, ANY],
        out_shape=[
            jax.ShapeDtypeStruct(q.shape, bf16),
            jax.ShapeDtypeStruct((seqs, features, rows), bf16),
            k_land,
            jax.ShapeDtypeStruct((seqs, rows, 128 * groups), bf16),
            jax.ShapeDtypeStruct((ranks, own, M, 128), bf16),
            jax.ShapeDtypeStruct((ranks, 16, 128), f32),
        ],
        scratch_shapes=[
            pltpu.VMEM((ranks * own, M, 128), bf16), pltpu.VMEM((ranks, 16, 128), f32),
            pltpu.VMEM((seqs, M, features), bf16), pltpu.VMEM((rows + 2 * RIM, 128), f32),
            pltpu.VMEM((40, 128), f32), rank_sems(), rank_sems(), rank_sems(),
        ],
        compiler_params=params(62 * MB, collective_id=1, has_side_effects=True),
        name="scores",
    )(q, k, v, q_land, k_part, v, rim, taps)


def split(x):
    hi = x.astype(bf16)
    return hi, (x - hi.astype(f32)).astype(bf16)


def stack_parts(xs, axis):
    return jnp.concatenate([part for x in xs for part in split(x)], axis=axis)


def pair_sums(out, count):
    top = lambda i, j: out[128 * i + 64 * j : 128 * i + 64 * j + 64]
    return [
        top(i, 0)[:, :128] + (top(i, 0)[:, 128:] + top(i, 1)[:, :128]) for i in range(count)
    ]


def pair_nn(lefts, right, masks):
    hi, lo = split(right)
    packed = jnp.concatenate([block_diag(hi, masks), block_diag(lo, masks)], axis=1)
    return pair_sums(dot(stack_parts(lefts, 0), packed), len(lefts))


def pair_nt(lefts, right, masks):
    hi, lo = split(right)
    packed = jnp.concatenate([block_diag(hi, masks), block_diag(lo, masks)], axis=0)
    return pair_sums(dot_nt(stack_parts(lefts, 0), packed), len(lefts))


def pair_tn(left, rights, masks_wide):
    out = dot_tn(stack_parts([left], 1), stack_parts(rights, 1))
    results = []
    for i in range(len(rights)):
        full = out[:128, 256 * i : 256 * i + 128] + (
            out[:128, 256 * i + 128 : 256 * i + 256] + out[128:, 256 * i : 256 * i + 128]
        )
        results.append(diag_blocks(full, masks_wide))
    return results


def half_reduce(x, upper, op, fill):
    a = op(jnp.where(upper, fill, x), axis=1, keepdims=True)
    b = op(jnp.where(upper, x, fill), axis=1, keepdims=True)
    return jnp.where(upper, b, a)


def to_column(row, same, upper):
    return half_reduce(jnp.where(same, row, 0.0), upper, jnp.sum, 0.0)


def to_row(col, same):
    return jnp.sum(jnp.where(same, col, 0.0), axis=0, keepdims=True)


def pair_consts():
    lane = lax.broadcasted_iota(jnp.int32, (M, 128), 1)
    row = lax.broadcasted_iota(jnp.int32, (M, 128), 0)
    return lane >= E, row == lane % E, group_masks((M, 128), 2, bf16), group_masks((M, 128), 2, f32)


def own_pair(land_ref, i, own):
    me, _ = seq_place()
    per = land_ref.shape[2] // 128
    p = jnp.minimum(me * own + i, land_ref.shape[0] * per - 1)
    return land_ref[p // per, :, pl.ds(pl.multiple_of((p % per) * 128, 128), 128)]


def inverse_step(
    num_ref, stat_ref, ql_ref, kl_ref, mixed_ref, sum_ref, mid_ref, z_ref, p_ref, a_ref, w_ref,
    scale_ref, tot_ref, alpha_ref,
):
    ranks, own = num_ref.shape[:2]
    upper, same, masks, masks_wide = pair_consts()
    for i in range(own):
        peak = stat_ref[0, i : i + 1, :]
        for r in range(1, ranks):
            peak = jnp.maximum(peak, stat_ref[r, i : i + 1, :])
        total = jnp.zeros((1, 128), f32)
        numer = jnp.zeros((M, 128), f32)
        for r in range(ranks):
            alpha = jnp.exp(stat_ref[r, i : i + 1, :] - peak)
            total = total + alpha * stat_ref[r, 8 + i : 9 + i, :]
            column = to_column(alpha, same, upper)
            alpha_ref[r, i] = column
            numer = numer + column * num_ref[r, i].astype(f32)
        total = to_column(total, same, upper)
        tot_ref[i] = total
        sum_ref[i] = numer / total
        ql, kl = own_pair(ql_ref, i, own), own_pair(kl_ref, i, own)
        s2 = dot_nt(ql, block_diag(kl, masks))
        e2 = jnp.exp(s2 - half_reduce(s2, upper, jnp.max, -jnp.inf))
        middle = e2 / half_reduce(e2, upper, jnp.sum, 0.0)
        mid_ref[i] = middle
        st = dot_nt(kl, block_diag(ql, masks))
        et = jnp.exp(st - jnp.max(st, axis=0, keepdims=True))
        flipped = et / jnp.sum(et, axis=0, keepdims=True)
        column = jnp.sum(middle, axis=0, keepdims=True)
        scale = 1.0 / half_reduce(column, upper[0:1], jnp.max, -jnp.inf)
        scale_ref[i] = jnp.broadcast_to(scale, (8, 128))
        z_ref[0, i] = flipped * scale

    def step(it, carry):
        zs = [z_ref[it, i] for i in range(own)]
        ps = [pair_nn([mid_ref[i]], zs[i], masks)[0] for i in range(own)]
        second = [pair_nn([ps[i], zs[i]], ps[i], masks) for i in range(own)]
        for i in range(own):
            p2, a = second[i]
            w = 7.0 * ps[i] - p2
            p_ref[it, i] = ps[i]
            a_ref[it, i] = a
            w_ref[it, i] = w
            z_ref[it + 1, i] = 0.25 * (13.0 * zs[i] - 15.0 * a + pair_nn([a], w, masks)[0])
        return carry

    lax.fori_loop(0, NEWTON, step, 0)
    for i in range(own):
        mixed_ref[i] = pair_nn([z_ref[NEWTON, i]], sum_ref[i], masks)[0].astype(bf16)


def inverse_kernel(
    num_ref, stat_ref, ql_ref, kl_ref, cv_ref, rim_ref, f_ref, mixed_out, co_ref, sum_ref, mid_ref, z_ref, p_ref,
    a_ref, w_ref, scale_ref, tot_ref, alpha_ref, mixed, pad, taps, sems,
):
    step = pl.program_id(0)
    own = num_ref.shape[1]

    @pl.when(step == 0)
    def _():
        greet()
        inverse_step(
            num_ref, stat_ref, ql_ref, kl_ref, mixed, sum_ref, mid_ref, z_ref, p_ref, a_ref, w_ref, scale_ref,
            tot_ref, alpha_ref,
        )
        begin(spread_copies(mixed, mixed_out, own, sems))

    @pl.when(step > 0)
    def _():
        conv_tile(cv_ref, rim_ref, f_ref, co_ref, pad, taps)

    @pl.when(step == pl.num_programs(0) - 1)
    def _():
        finish(spread_copies(mixed, mixed_out, own, sems))


def inverse(num, stat, q_land, k_land, v, rim, taps, first_group):
    ranks, own = num.shape[:2]
    seqs, rows, features = v.shape
    groups = features // 128 - first_group
    mat = jax.ShapeDtypeStruct((own, M, 128), f32)
    steps = lambda n: jax.ShapeDtypeStruct((n, own, M, 128), f32)
    whole = lambda a: pl.BlockSpec(a.shape, lambda i: (0,) * len(a.shape), pipeline_mode=pl.Buffered(1))
    saved = [
        mat, mat, steps(NEWTON + 1), steps(NEWTON), steps(NEWTON), steps(NEWTON),
        jax.ShapeDtypeStruct((own, 8, 128), f32), mat, steps(ranks),
    ]
    cv, rims, ft, co = conv_specs(rows, 1, first_group, groups)
    return pl.pallas_call(
        inverse_kernel,
        grid=(1 + seqs * groups,),
        in_specs=[whole(num), whole(stat), whole(q_land), whole(k_land), cv, rims, ft],
        out_specs=[ANY, co] + [whole(a) for a in saved],
        out_shape=[
            jax.ShapeDtypeStruct((ranks * own, M, 128), bf16),
            jax.ShapeDtypeStruct((seqs, rows, 128 * groups), bf16),
        ]
        + saved,
        scratch_shapes=[
            pltpu.VMEM((own, M, 128), bf16), pltpu.VMEM((rows + 2 * RIM, 128), f32), pltpu.VMEM((40, 128), f32),
            rank_sems(),
        ],
        compiler_params=params(62 * MB, collective_id=2, has_side_effects=True),
        name="inverse",
    )(num, stat, q_land, k_land, v, rim, taps)


def inverse_back_step(
    land_ref, ql_ref, kl_ref, sum_ref, mid_ref, z_ref, p_ref, a_ref, w_ref, scale_ref, tot_ref,
    alpha_ref, gn_ref, gt_ref, mq_ref, mk_ref, g_ref, dk_ref, shared=lambda: None,
):
    ranks, own = land_ref.shape[:2]
    upper, same, masks, masks_wide = pair_consts()
    for i in range(own):
        land = land_ref[0, i].astype(f32)
        for r in range(1, ranks):
            land = land + land_ref[r, i].astype(f32)
        summary, total = sum_ref[i], tot_ref[i]
        gs = pair_tn(z_ref[NEWTON, i], [land], masks_wide)[0].astype(bf16).astype(f32)
        gn = (gs / total).astype(bf16).astype(f32)
        gt = -half_reduce(gs * summary, upper, jnp.sum, 0.0) / total
        for r in range(ranks):
            gn_ref[r, i] = (alpha_ref[r, i] * gn).astype(bf16)
            gt_ref[r, i] = jnp.broadcast_to(to_row(alpha_ref[r, i] * gt, same), (8, 128))
        g_ref[i] = pair_nt([land], summary, masks)[0]
        dk_ref[i] = jnp.zeros((M, 128), f32)
    shared()

    def step(back, carry):
        it = NEWTON - 1 - back
        gs = [g_ref[i] for i in range(own)]
        das, dws = [], []
        for i in range(own):
            das.append(0.25 * (pair_nt([gs[i]], w_ref[it, i], masks)[0] - 15.0 * gs[i]))
            dws.append(0.25 * pair_tn(a_ref[it, i], [gs[i]], masks_wide)[0])
        dps, parts = [], []
        for i in range(own):
            right = pair_nt([dws[i], das[i]], p_ref[it, i], masks)
            left = pair_tn(p_ref[it, i], [dws[i]], masks_wide)[0]
            dps.append(7.0 * dws[i] - right[0] - left + pair_tn(z_ref[it, i], [das[i]], masks_wide)[0])
            parts.append(3.25 * gs[i] + right[1])
        for i in range(own):
            g_ref[i] = parts[i] + pair_tn(mid_ref[i], [dps[i]], masks_wide)[0]
            dk_ref[i] += pair_nt([dps[i]], z_ref[it, i], masks)[0]
        return carry

    lax.fori_loop(0, NEWTON, step, 0)
    eye = jnp.where(same, 1.0, 0.0).astype(bf16)
    for i in range(own):
        g, middle, scale = g_ref[i], mid_ref[i], scale_ref[i, 0:1, :]
        turned = dot_tn(stack_parts([g], 1), eye)
        turned = diag_blocks(turned[:128] + turned[128:], masks_wide)
        column = jnp.sum(middle, axis=0, keepdims=True)
        top = half_reduce(column, upper[0:1], jnp.max, -jnp.inf)
        hit = jnp.where(column == top, 1.0, 0.0)
        share = hit / half_reduce(hit, upper[0:1], jnp.sum, 0.0)
        d_scale = half_reduce(jnp.sum(turned * middle, axis=0, keepdims=True), upper[0:1], jnp.sum, 0.0)
        dk = dk_ref[i] + turned * scale - share * (d_scale * scale * scale)
        ds = middle * (dk - half_reduce(middle * dk, upper, jnp.sum, 0.0))
        hi, lo = split(ds)
        both = dot(jnp.concatenate([hi, lo], axis=0), block_diag(own_pair(kl_ref, i, own), masks))
        mq_ref[i] = both[:M] + both[M:]
        turned = dot_tn(jnp.concatenate([hi, lo], axis=1), own_pair(ql_ref, i, own))
        mk_ref[i] = diag_blocks(turned[:128] + turned[128:], masks_wide)


def inverse_back(land, q_land, k_land, saved):
    ranks, own = land.shape[:2]
    mat = jax.ShapeDtypeStruct((own, M, 128), f32)
    return pl.pallas_call(
        inverse_back_step,
        out_shape=[
            jax.ShapeDtypeStruct((ranks, own, M, 128), bf16),
            jax.ShapeDtypeStruct((ranks, own, 8, 128), f32), mat, mat,
        ],
        scratch_shapes=[pltpu.VMEM((own, M, 128), f32)] * 2,
        compiler_params=params(62 * MB),
        name="inverse_back",
    )(land, q_land, k_land, *saved)


def pick_tile(step, plan):
    tile = 0
    done = 0
    for first, count in plan:
        tile = tile + jnp.clip(step - first, -1 if done else 0, count - 1) + (1 if done else 0)
        done += count
    return tile


def front_kernel(
    tok_ref, wq_ref, f_ref,
    q_ref, k_ref, v_ref, w_ref, p_ref, ql_out, kl_out, rim_out, conv_ref, mixed_out, sum_ref, mid_ref, z_ref, zp_ref,
    za_ref, zw_ref, scale_ref, tot_ref, alpha_ref,
    land_q, land_k, ql, kl, rim, rims, num, stat, num_got, stat_got, mixed, pad, taps,
    q_sems, k_sems, rim_send, rim_recv, num_sems, stat_sems, mixed_sems, *, plan, at_third, at_first, at_inverse,
):
    step = pl.program_id(0)
    seqs, rows, features = q_ref.shape
    marks = land_q.shape[1]
    seg = rows // marks
    pairs = features // 128
    own = num_got.shape[1]
    me, count = seq_place()

    def mark_copies(src, dst, sems, s):
        spot = dst.at[s, pl.ds(me * marks, marks)]
        sends = [
            remote(src.at[s], spot, sems.at[0, s, o], sems.at[1, s, o], {"seq": peer}) for o, peer in seq_peers()
        ]
        return sends, pltpu.make_async_copy(src.at[s], spot, sems.at[0, s, 0])

    def rim_copy(s, side):
        there = lax.rem(me + (1 if side == 0 else count - 1), count)
        return remote(
            rim.at[s, side], rims.at[s, side], rim_send.at[s, side], rim_recv.at[s, side], {"seq": there}
        )

    def has_next(side):
        return me < count - 1 if side == 0 else me > 0

    @pl.when(step == 0)
    def _():
        rims[...] = jnp.zeros_like(rims)
        greet()
        stat[...] = jnp.zeros_like(stat)
        num[seqs * pairs :] = jnp.zeros_like(num[seqs * pairs :])

    @pl.when(step < seqs)
    def _():
        x = tok_ref[0]
        for part, out in enumerate((q_ref, k_ref, v_ref)):
            for c in range(0, features, 256):
                p = dot(x, wq_ref[:, part * features + c : part * features + c + 256])
                if part == 0:
                    p = 0.125 * p
                low = p.astype(bf16)
                out[step, :, c : c + 256] = low
                if part < 2:
                    total = low.astype(f32).reshape(marks, seg, 256).sum(1)
                    (land_q, land_k)[part][step, :, c : c + 256] = (total * (1.0 / seg)).astype(bf16)
                else:
                    rim[step, 0, :, c : c + 256] = low[rows - RIM :]
                    rim[step, 1, :, c : c + 256] = low[:RIM]
        begin(mark_copies(land_q, ql, q_sems, step))

        @pl.when(step > 0)
        def _():
            for side in range(2):
                @pl.when(has_next(side))
                def _(side=side):
                    rim_copy(step, side).start()

    @pl.when(step == 1)
    def _():
        for side in range(2):
            @pl.when(has_next(side))
            def _(side=side):
                rim_copy(0, side).start()

    @pl.when(step == seqs)
    def _():
        for s in range(seqs):
            begin(mark_copies(land_k, kl, k_sems, s))

    tile = pick_tile(step, plan)
    seq, group = tile // pairs, tile % pairs
    for first, tiles in plan:
        @pl.when((step >= first) & (step < first + tiles))
        def _():
            @pl.when(group == 0)
            def _():
                for side in range(2):
                    @pl.when(has_next(side))
                    def _(side=side):
                        rim_copy(seq, side).wait_send()

                    @pl.when(has_next(1 - side))
                    def _(side=side):
                        rim_copy(seq, side).wait_recv()

            lanes = pl.ds(pl.multiple_of(group * 128, 128), 128)
            taps[0:KW, :] = f_ref[:, lanes].astype(f32)
            pad[0:RIM, :] = rims[seq, 0, :, lanes].astype(f32)
            pad[RIM : RIM + rows, :] = v_ref[seq, :, lanes].astype(f32)
            pad[RIM + rows : RIM + rows + RIM, :] = rims[seq, 1, :, lanes].astype(f32)
            conv_rows(conv_ref, pad, taps, rows)

    @pl.when(step == at_third)
    def _():
        for s in range(seqs):
            finish(mark_copies(land_q, ql, q_sems, s))
        ql_out[...] = ql[...]

    @pl.when((step >= at_third) & (step < at_third + seqs))
    def _():
        s = step - at_third
        third_score_step(s, k_ref.at[pl.ds(s, 1)], v_ref.at[pl.ds(s, 1)], ql.at[pl.ds(s, 1)], w_ref, num, stat, own)

    @pl.when(step == at_third + seqs - 1)
    def _():
        begin(swap_copies(num, num_got, own, num_sems))
        begin(swap_rows(stat, stat_got, stat_sems))

    @pl.when(step == at_first)
    def _():
        for s in range(seqs):
            finish(mark_copies(land_k, kl, k_sems, s))
        kl_out[...] = kl[...]

    @pl.when((step >= at_first) & (step < at_first + seqs))
    def _():
        s = step - at_first
        first_score_step(q_ref.at[pl.ds(s, 1)], kl[s], p_ref)

    @pl.when(step == at_inverse)
    def _():
        finish(swap_copies(num, num_got, own, num_sems))
        finish(swap_rows(stat, stat_got, stat_sems))
        inverse_step(
            num_got, stat_got, ql, kl, mixed, sum_ref, mid_ref, z_ref, zp_ref, za_ref, zw_ref, scale_ref, tot_ref,
            alpha_ref,
        )
        begin(spread_copies(mixed, mixed_out, own, mixed_sems))

    @pl.when(step == pl.num_programs(0) - 1)
    def _():
        finish(spread_copies(mixed, mixed_out, own, mixed_sems))
        rim_out[...] = rims[...]


def front(tokens, w_qkv, taps, own):
    seqs, rows, features = tokens.shape
    ranks = lax.axis_size("seq")
    marks = M // ranks
    pairs = features // 128
    tiles = (4, 5, seqs * pairs - 9)
    third = seqs + tiles[0]
    first = third + seqs + tiles[1]
    at = dict(at_third=third, at_first=first, at_inverse=first + seqs)
    plan = ((seqs, tiles[0]), (third + seqs, tiles[1]), (first + seqs + 1, tiles[2]))
    here = lambda first: (lambda i: jnp.clip(i - first, 0, seqs - 1))
    score, prob = here(at["at_third"]), here(at["at_first"])
    whole = lambda a: pl.BlockSpec(a.shape, lambda i: (0,) * len(a.shape), pipeline_mode=pl.Buffered(1))
    tile = lambda i: pick_tile(i, plan)
    rows_out = jax.ShapeDtypeStruct(tokens.shape, bf16)
    land = jax.ShapeDtypeStruct((seqs, M, features), bf16)
    rim_out = jax.ShapeDtypeStruct((seqs, 2, RIM, features), bf16)
    mat = jax.ShapeDtypeStruct((own, M, 128), f32)
    steps = lambda n: jax.ShapeDtypeStruct((n, own, M, 128), f32)
    saved = [
        mat, mat, steps(NEWTON + 1), steps(NEWTON), steps(NEWTON), steps(NEWTON),
        jax.ShapeDtypeStruct((own, 8, 128), f32), mat, steps(ranks),
    ]
    vm = lambda *shape: pltpu.VMEM(shape, bf16)
    dma = pltpu.SemaphoreType.DMA
    return pl.pallas_call(
        functools.partial(front_kernel, plan=plan, **at),
        grid=(plan[-1][0] + tiles[2],),
        in_specs=[
            pl.BlockSpec((1, rows, features), lambda i: (jnp.minimum(i, seqs - 1), 0, 0)), whole(w_qkv), whole(taps),
        ],
        out_specs=[whole(rows_out)] * 3
        + [
            pl.BlockSpec((1, rows, features), lambda i: (score(i), 0, 0)),
            pl.BlockSpec((1, features, rows), lambda i: (prob(i), 0, 0)),
            whole(land), whole(land), whole(rim_out),
            pl.BlockSpec((1, rows, 128), lambda i: (tile(i) // pairs, 0, tile(i) % pairs)), ANY,
        ]
        + [whole(a) for a in saved],
        out_shape=[rows_out] * 4
        + [
            jax.ShapeDtypeStruct((seqs, features, rows), bf16), land, land, rim_out, rows_out,
            jax.ShapeDtypeStruct((ranks * own, M, 128), bf16),
        ]
        + saved,
        scratch_shapes=[
            vm(seqs, marks, features), vm(seqs, marks, features), vm(seqs, M, features), vm(seqs, M, features),
            vm(seqs, 2, RIM, features), vm(seqs, 2, RIM, features), vm(ranks * own, M, 128),
            pltpu.VMEM((ranks, 16, 128), f32), vm(ranks, own, M, 128), pltpu.VMEM((ranks, 16, 128), f32),
            vm(own, M, 128), pltpu.VMEM((rows + 2 * RIM, 128), f32), pltpu.VMEM((40, 128), f32),
            dma((2, seqs, ranks)), dma((2, seqs, ranks)), dma((seqs, 2)), dma((seqs, 2)), rank_sems(), rank_sems(),
            rank_sems(),
        ],
        compiler_params=params(62 * MB, collective_id=0, has_side_effects=True),
        name="front",
    )(tokens, w_qkv, taps)


def mean_of(x):
    return jnp.mean(x, axis=-1, keepdims=True)


def gelu_and_slope(u):
    u = u.astype(bf16)
    low = lambda c: jnp.asarray(c, bf16)
    t = low(1.0) / (low(1.0) + low(ERFC_P * root_half) * jnp.abs(u))
    bell = jnp.exp2((u * u) * low(-0.5 * log2_e))
    poly = jnp.full_like(t, 0.5 * ERFC_C[-1])
    for c in ERFC_C[-2::-1]:
        poly = poly * t + low(0.5 * c)
    half = (poly * t) * bell
    cdf = jnp.where(u < 0, half, low(1.0) - half)
    return u * cdf, cdf + u * (bell * low(inv_root_two_pi))


def row_block(
    step, tok_ref, p_ref, conv_refs, mix_ref, top_ref, w_out_ref, w_up_ref, w_down_ref, ga_ref,
    gf_ref, out_ref, proj_ref, gm_ref, gains_ref, act, gul, slope, hid_t, gdl_t, mix_t, gpr, resid, whole, ready=lambda i: None,
):
    size, features = tok_ref.shape
    ff = act.shape[1]
    wide = features
    start = pl.multiple_of(step * size, size)
    rows = pl.ds(start, size)
    near = rows if whole else pl.ds(0, size)
    masks = group_masks((M, 4 * E), 4, bf16)
    for g in range(features // 256):
        sl = slice(256 * g, 256 * g + 256)
        att = dot_tn(p_ref[0, sl, :], block_diag(quad(mix_ref, g), masks))
        split_at = conv_refs[0].shape[1]
        ref, lane = (conv_refs[0], 256 * g) if 256 * g < split_at else (conv_refs[1], 256 * g - split_at)
        resid[:, sl] = (att + ref[:, lane : lane + 256].astype(f32)).astype(bf16)
    mixed = resid[...]
    mix_t[:, near] = mixed.T
    residual = tok_ref[...].astype(f32) + dot(mixed, w_out_ref[...])
    centre = residual - mean_of(residual)
    s_att = lax.rsqrt(mean_of(centre * centre) + epsilon)
    normed = centre * s_att
    gain_att = ga_ref[...].reshape(1, features)
    hidden = normed * gain_att
    hid_low = hidden.astype(bf16)
    hid_t[:, rows] = hid_low.T
    down = jnp.zeros((size, features), f32)
    for j in range(0, ff, wide):
        if j == 0:
            ready(0)
        up = dot(hid_low, w_up_ref[:, j : j + wide])
        low, sl = gelu_and_slope(up)
        act[near, j : j + wide] = low
        slope[:, j : j + wide] = sl
        if j == 0:
            ready(1)
        down = down + dot(low, w_down_ref[j : j + wide, :])
    residual_two = hidden + down
    centre_two = residual_two - mean_of(residual_two)
    s_ffn = lax.rsqrt(mean_of(centre_two * centre_two) + epsilon)
    normed_two = centre_two * s_ffn
    gain_ffn = gf_ref[...].reshape(1, features)
    out_ref[...] = (normed_two * gain_ffn).astype(bf16)
    top = top_ref[...].astype(f32)
    gains_ref[8:16, :] += (top * normed_two).reshape(size // 8, 8, features).sum(0)
    g = top * gain_ffn
    grad_two = s_ffn * (g - mean_of(g) - normed_two * mean_of(g * normed_two))
    gdl = grad_two.astype(bf16)
    gdl_t[:, near] = gdl.T
    back = jnp.zeros((size, features), f32)
    for j in range(0, ff, wide):
        gu = dot_nt(gdl, w_down_ref[j : j + wide, :]) * slope[:, j : j + wide].astype(f32)
        low = gu.astype(bf16)
        gul[rows, j : j + wide] = low
        back = back + dot_nt(low, w_up_ref[:, j : j + wide])
    grad_hidden = grad_two + back
    gains_ref[0:8, :] += (grad_hidden * normed).reshape(size // 8, 8, features).sum(0)
    g = grad_hidden * gain_att
    proj = (s_att * (g - mean_of(g) - normed * mean_of(g * normed))).astype(bf16)
    proj_ref[...] = proj
    if whole:
        gpr[rows, :] = proj
    gm_ref[...] = dot_nt(proj, w_out_ref[...]).astype(bf16)


def row_kernel(
    tok_ref, p_ref, conv_a_ref, conv_b_ref, mix_ref, top_ref, w_out_ref, w_up_ref, w_down_ref, ga_ref, gf_ref,
    out_ref, proj_ref, gm_ref, wg_ref, gains_ref,
    act, gul, slope, hid_t, gdl_t, mix_t, gpr, resid,
):
    step = pl.program_id(0)
    size, features = tok_ref.shape
    blocks = act.shape[0] // size
    ff = act.shape[1]
    wide = features

    @pl.when(step == 0)
    def _():
        gains_ref[...] = jnp.zeros_like(gains_ref)

    @pl.when(step < blocks)
    def _():
        row_block(
            step, tok_ref, p_ref, (conv_a_ref, conv_b_ref), mix_ref, top_ref, w_out_ref, w_up_ref, w_down_ref,
            ga_ref, gf_ref, out_ref, proj_ref, gm_ref, gains_ref, act, gul, slope, hid_t, gdl_t, mix_t, gpr,
            resid, True,
        )

    chunks = ff // wide
    for first, left, right in ((0, hid_t, gul), (chunks, gdl_t, act), (2 * chunks, mix_t, gpr)):
        count = chunks if first < 2 * chunks else 1

        @pl.when((step >= blocks + first) & (step < blocks + first + count))
        def _(first=first, left=left, right=right):
            base = (step - blocks - first) * wide
            for c in range(0, wide, 256):
                cols = pl.ds(pl.multiple_of(base + c, 256), 256)
                wg_ref[0, :, c : c + 256] = dot(left[...], right[:, cols]).astype(bf16)


def row_pass(tokens, probs, conv_a, conv_b, mixed, grad_out, w_out, w_up, w_down, gain_att, gain_ffn):
    seqs, rows, features = tokens.shape
    ff = w_up.shape[1]
    size = min(256, rows)
    total = seqs * rows
    blocks = total // size
    grads = 2 * (ff // features) + 1
    here = lambda i: jnp.minimum(i, blocks - 1)
    block = pl.BlockSpec((size, features), lambda i: (here(i), 0))
    whole = lambda a: pl.BlockSpec(a.shape, lambda i: (0,) * a.ndim, pipeline_mode=pl.Buffered(1))
    flat = lambda a: a.reshape(total, a.shape[2])
    part = lambda a: pl.BlockSpec((size, a.shape[2]), lambda i: (here(i), 0))
    gains = [gain_att, gain_ffn]
    row_out = jax.ShapeDtypeStruct((total, features), bf16)
    tall = pltpu.VMEM((features, total), bf16)
    return pl.pallas_call(
        row_kernel,
        grid=(blocks + grads,),
        in_specs=[
            block, pl.BlockSpec((1, features, size), lambda i: (here(i) * size // rows, 0, here(i) % (rows // size))),
            part(conv_a), part(conv_b),
            pl.BlockSpec((features // 128, M, 128), lambda i: (here(i) * size // rows, 0, 0)),
            block, whole(w_out), whole(w_up), whole(w_down), whole(gains[0]), whole(gains[1]),
        ],
        out_specs=[block] * 3
        + [
            pl.BlockSpec((1, features, features), lambda i: (jnp.maximum(i - blocks, 0), 0, 0)),
            pl.BlockSpec((16, features), lambda i: (0, 0)),
        ],
        out_shape=[row_out] * 3
        + [
            jax.ShapeDtypeStruct((grads, features, features), bf16),
            jax.ShapeDtypeStruct((16, features), f32),
        ],
        scratch_shapes=[
            pltpu.VMEM((total, ff), bf16), pltpu.VMEM((total, ff), bf16), pltpu.VMEM((size, ff), bf16),
            tall, tall, tall, pltpu.VMEM((total, features), bf16), pltpu.VMEM((size, features), bf16),
        ],
        compiler_params=params(62 * MB),
        name="row_pass",
    )(flat(tokens), probs, flat(conv_a), flat(conv_b), mixed, flat(grad_out), w_out, w_up, w_down, *gains)


def put_parts(parts, slot, low, c, by_rows):
    for l in range(0, low.shape[1], 128):
        side, lane = (c + l) // 384, (c + l) % 384
        if by_rows:
            for d in range(8):
                parts[slot, d % 2, d // 2, 96 * side : 96 * side + 96, lane : lane + 128] = low[
                    96 * d : 96 * d + 96, l : l + 128
                ]
        else:
            for z in range(4):
                parts[slot, side, z, :, lane : lane + 128] = low[192 * z : 192 * z + 192, l : l + 128]


def fold(block):
    return jnp.concatenate([block[:48], block[48:]], axis=1)


def rows_forward_kernel(
    tok_ref, p_ref, conv_ref, mix_ref, top_ref, w_out_ref, w_up_in, w_down_in, ga_ref, gf_ref,
    out_ref, normed_ref, s_ref, gdl_ref, slope_ref, hid_t_ref, mix_t_ref, gains_ref, g_out,
    w_up_ref, w_down_ref, load_sems, act, gdl_t, mixed_ref, parts, got, sums, send, recv, out_sem,
):
    step = pl.program_id(0)
    size, features = tok_ref.shape
    blocks = act.shape[0] // size
    ff = act.shape[1]
    chunks = ff // features
    core, _, _, sibling, _, _ = cube()
    loads = [
        pltpu.make_async_copy(w_up_in, w_up_ref, load_sems.at[0]),
        pltpu.make_async_copy(w_down_in, w_down_ref, load_sems.at[1]),
    ]

    @pl.when(step == 0)
    def _():
        for load in loads:
            load.start()
        gains_ref[...] = jnp.zeros_like(gains_ref)
        greet([sibling])

    @pl.when(step < blocks)
    def _():
        rows = pl.ds(pl.multiple_of(step * size, size), size)
        masks = group_masks((M, 4 * E), 4, bf16)
        for g in range(features // 256):
            sl = slice(256 * g, 256 * g + 256)
            att = dot_tn(p_ref[0, sl, :], block_diag(quad(mix_ref, g), masks))
            mixed_ref[:, sl] = (att + conv_ref[:, sl].astype(f32)).astype(bf16)
        mixed = mixed_ref[...]
        mix_t_ref[...] = mixed.T
        residual = tok_ref[...].astype(f32) + dot(mixed, w_out_ref[...])
        centre = residual - mean_of(residual)
        s_att = lax.rsqrt(mean_of(centre * centre) + epsilon)
        normed = centre * s_att
        s_ref[...] = jnp.broadcast_to(s_att, s_ref.shape)
        normed_ref[...] = normed.astype(bf16)
        hidden = normed * ga_ref[...].reshape(1, features)
        hid_low = hidden.astype(bf16)
        hid_t_ref[...] = hid_low.T

        @pl.when(step == 0)
        def _():
            for load in loads:
                load.wait()

        down = jnp.zeros((size, features), f32)
        for j in range(0, ff, features):
            low, sl = gelu_and_slope(dot(hid_low, w_up_ref[:, j : j + features]))
            act[rows, j : j + features] = low
            slope_ref[:, j : j + features] = sl
            down = down + dot(low, w_down_ref[j : j + features, :])
        residual_two = hidden + down
        centre_two = residual_two - mean_of(residual_two)
        s_ffn = lax.rsqrt(mean_of(centre_two * centre_two) + epsilon)
        normed_two = centre_two * s_ffn
        gain_ffn = gf_ref[...].reshape(1, features)
        out_ref[...] = (normed_two * gain_ffn).astype(bf16)
        top = top_ref[...].astype(f32)
        gains_ref[...] += (top * normed_two).reshape(size // 8, 8, features).sum(0)
        g = top * gain_ffn
        gdl = (s_ffn * (g - mean_of(g) - normed_two * mean_of(g * normed_two))).astype(bf16)
        gdl_ref[...] = gdl
        gdl_t[:, rows] = gdl.T

    j = step - blocks
    slot = lax.rem(jnp.maximum(j, 0), 2)

    def share(at):
        return remote(parts.at[at % 2, 1 - core], got.at[at], send.at[at], recv.at[at], sibling)

    def out_copy(at):
        return pltpu.make_async_copy(sums.at[at % 2], g_out.at[:, at], out_sem.at[at % 2])

    @pl.when((j >= 2) & (j < chunks))
    def _():
        share(j - 2).wait_send()

    @pl.when((j >= 0) & (j < chunks))
    def _():
        for c in range(0, features, 256):
            cols = pl.ds(pl.multiple_of(j * features + c, 256), 256)
            put_parts(parts, slot, dot(gdl_t[...], act[:, cols]).astype(bf16), c, False)
        share(j).start()

    done = j - 1

    @pl.when(done >= 2)
    def _():
        out_copy(done - 2).wait()

    @pl.when(done >= 0)
    def _():
        share(done).wait_recv()
        sums[done % 2] = add_low(parts[done % 2, core], got[done])
        out_copy(done).start()

    @pl.when(done == chunks - 1)
    def _():
        for at in (done - 1, done):
            share(at).wait_send()
            out_copy(at).wait()


def rows_forward(tokens, probs, conv_out, mixed, grad_out, w_out, w_up, w_down, gain_att, gain_ffn):
    seqs, rows, features = tokens.shape
    ff = w_up.shape[1]
    size = rows
    total = seqs * rows
    blocks = total // size
    chunks = ff // features
    here = lambda i: jnp.minimum(i, blocks - 1)
    block = lambda n: pl.BlockSpec((size, n), lambda i: (here(i), 0))
    turned = pl.BlockSpec((features, size), lambda i: (0, here(i)))
    whole = lambda a: pl.BlockSpec(a.shape, lambda i: (0,) * a.ndim, pipeline_mode=pl.Buffered(1))
    flat = lambda a: a.reshape(total, a.shape[2])
    shape = jax.ShapeDtypeStruct
    dma = pltpu.SemaphoreType.DMA
    return pl.pallas_call(
        rows_forward_kernel,
        grid=(blocks + chunks + 1,),
        in_specs=[
            block(features),
            pl.BlockSpec((1, features, size), lambda i: (here(i) * size // rows, 0, here(i) % (rows // size))),
            block(features), pl.BlockSpec((features // 128, M, 128), lambda i: (here(i) * size // rows, 0, 0)),
            block(features), whole(w_out), ANY, ANY, whole(gain_att), whole(gain_ffn),
        ],
        out_specs=[block(features), block(features), block(128), block(features), block(ff), turned, turned]
        + [pl.BlockSpec((8, features), lambda i: (0, 0)), ANY],
        out_shape=[
            shape((total, features), bf16), shape((total, features), bf16), shape((total, 128), f32),
            shape((total, features), bf16), shape((total, ff), bf16), shape((features, total), bf16),
            shape((features, total), bf16), shape((8, features), f32), shape((4, chunks, 192, 384), bf16),
        ],
        scratch_shapes=[
            pltpu.VMEM(w_up.shape, bf16), pltpu.VMEM(w_down.shape, bf16), dma((2,)), pltpu.VMEM((total, ff), bf16),
            pltpu.VMEM((features, total), bf16), pltpu.VMEM((size, features), bf16),
            pltpu.VMEM((2, 2, 4, 192, 384), bf16), pltpu.VMEM((chunks, 4, 192, 384), bf16),
            pltpu.VMEM((2, 4, 192, 384), bf16), dma((chunks,)), dma((chunks,)), dma((2,)),
        ],
        compiler_params=params(62 * MB, collective_id=3, has_side_effects=True),
        name="rows_forward",
    )(
        flat(tokens), probs, flat(conv_out), mixed, flat(grad_out), w_out, w_up, w_down, gain_att, gain_ffn
    )


def rows_backward_kernel(
    turn_at, gdl_ref, slope_ref, normed_ref, s_ref, w_out_ref, ga_ref, w_down_in, w_up_in, hid_t_in, mix_t_in, down_in,
    proj_ref, gm_ref, gains_ref, down_ref, g_out, rim_out,
    w_down_ref, w_up_ref, hid_t, mix_t, load_sems, gul, gpr, rim, parts, got, sums,
    kept, crossed, turned, kept_sems, cross_sems, turn_sems,
    send, recv, out_sem, last_sem, rim_send, rim_recv,
):
    step = pl.program_id(0)
    size, features = gdl_ref.shape
    ff = gul.shape[1]
    blocks = gul.shape[0] // size
    chunks = ff // features
    seqs = rim.shape[0]
    per = blocks // seqs
    me, count = seq_place()
    core, _, _, sibling, along_x, along_y = cube()
    loads = [
        pltpu.make_async_copy(a, b, load_sems.at[i])
        for i, (a, b) in enumerate(
            ((w_down_in, w_down_ref), (w_up_in, w_up_ref), (hid_t_in, hid_t), (mix_t_in, mix_t))
        )
    ]
    cross = cross_copies(down_in, crossed, cross_sems)
    keep = kept_copies(down_in, kept, kept_sems)
    turn = turn_copies(kept, turned, turn_sems)

    @pl.when(step == 0)
    def _():
        for load in loads[:2]:
            load.start()
        gains_ref[...] = jnp.zeros_like(gains_ref)
        greet([sibling, along_x, along_y])
        for copy in cross + keep:
            copy.start()

    @pl.when(step == 1)
    def _():
        for load in loads[2:]:
            load.start()

    @pl.when(step == turn_at)
    def _():
        for copy in cross + keep:
            copy.wait()
        cross_add(kept, crossed)
        for copy in turn:
            copy.start()

    def rim_copy(s, side):
        there = lax.rem(me + (1 if side == 0 else count - 1), count)
        return remote(
            rim.at[s, side], rim_out.at[s, side], rim_send.at[s, side], rim_recv.at[s, side], {"seq": there}
        )

    @pl.when(step < blocks)
    def _():
        rows = pl.ds(pl.multiple_of(step * size, size), size)

        @pl.when(step == 0)
        def _():
            loads[0].wait()

        gdl = gdl_ref[...]
        back = gdl.astype(f32)
        for j in range(0, ff, features):
            gu = dot_nt(gdl, w_down_ref[j : j + features, :]) * slope_ref[:, j : j + features].astype(f32)
            low = gu.astype(bf16)
            gul[rows, j : j + features] = low
            if j == 0:
                @pl.when(step == 0)
                def _():
                    loads[1].wait()
            back = back + dot_nt(low, w_up_ref[:, j : j + features])
        normed = normed_ref[...].astype(f32)
        gains_ref[...] += (back * normed).reshape(size // 8, 8, features).sum(0)
        g = back * ga_ref[...].reshape(1, features)
        proj = (s_ref[:, 0:1] * (g - mean_of(g) - normed * mean_of(g * normed))).astype(bf16)
        proj_ref[...] = proj
        gpr[rows, :] = proj
        gm_ref[...] = dot_nt(proj, w_out_ref[...]).astype(bf16)
        s = step // per

        @pl.when(step % per == 0)
        def _():
            rim[s, 1] = gm_ref[:RIM, :]
            rim_copy(s, 1).start()

        @pl.when(step % per == per - 1)
        def _():
            rim[s, 0] = gm_ref[size - RIM :, :]
            rim_copy(s, 0).start()

    j = step - blocks
    slot = lax.rem(jnp.maximum(j, 0), 2)

    def share(at):
        return remote(parts.at[at % 2, 1 - core], got.at[at], send.at[at], recv.at[at], sibling)

    def up_copy(at):
        return pltpu.make_async_copy(sums.at[at % 2], g_out.at[at, :, 0:192, :], out_sem.at[at % 2])

    def out_copy(z):
        return pltpu.make_async_copy(
            sums.at[0, :, 48 * z : 48 * z + 48, :], g_out.at[z, :, 192:240, :], last_sem.at[z]
        )

    @pl.when((j >= 2) & (j <= chunks))
    def _():
        share(j - 2).wait_send()

    @pl.when(j == 0)
    def _():
        loads[2].wait()
        loads[3].wait()

    @pl.when((j >= 0) & (j < chunks))
    def _():
        for c in range(0, features, 256):
            cols = pl.ds(pl.multiple_of(j * features + c, 256), 256)
            put_parts(parts, slot, dot(hid_t[...], gul[:, cols]).astype(bf16), c, True)
        share(j).start()

    @pl.when(j == chunks)
    def _():
        for c in range(2):
            low = dot(mix_t[...], gpr[:, 384 * c : 384 * c + 384]).astype(bf16)
            for zz in range(2):
                z = 2 * c + zz
                for d in range(8):
                    parts[slot, d % 2, d // 2, 48 * z : 48 * z + 48, :] = fold(
                        low[96 * d : 96 * d + 96, 192 * zz : 192 * zz + 192]
                    )
        share(j).start()

    done = j - 1

    @pl.when(done >= 2)
    def _():
        up_copy(done - 2).wait()

    @pl.when(done >= 0)
    def _():
        share(done).wait_recv()
        sums[done % 2] = add_low(parts[done % 2, core], got[done])

    @pl.when((done >= 0) & (done < chunks))
    def _():
        up_copy(done).start()

    @pl.when(done == chunks)
    def _():
        for z in range(4):
            out_copy(z).start()
        for copy in turn:
            copy.wait()
        turn_add(down_ref, kept, turned)
        share(done - 1).wait_send()
        share(done).wait_send()
        up_copy(done - 1).wait()
        for z in range(4):
            out_copy(z).wait()

        def rims(s, carry):
            for side in range(2):
                rim_copy(s, side).wait()
            return carry

        lax.fori_loop(0, seqs, rims, 0)


def rows_backward(gdl, slope, normed, s_att, w_out, gain_att, w_down, w_up, hid_t, mix_t, downs, seqs):
    total, features = gdl.shape
    ff = w_up.shape[1]
    size = total // seqs
    blocks = total // size
    chunks = ff // features
    here = lambda i: jnp.minimum(i, blocks - 1)
    block = lambda n: pl.BlockSpec((size, n), lambda i: (here(i), 0))
    whole = lambda a: pl.BlockSpec(a.shape, lambda i: (0,) * len(a.shape), pipeline_mode=pl.Buffered(1))
    shape = jax.ShapeDtypeStruct
    down_sum = shape((4, 192, 384), bf16)
    dma = pltpu.SemaphoreType.DMA
    return pl.pallas_call(
        functools.partial(rows_backward_kernel, 2),
        grid=(blocks + chunks + 2,),
        in_specs=[block(features), block(ff), block(features), block(128), whole(w_out), whole(gain_att)] + [ANY] * 5,
        out_specs=[block(features), block(features), pl.BlockSpec((8, features), lambda i: (0, 0)), whole(down_sum)]
        + [ANY] * 2,
        out_shape=[
            shape((total, features), bf16), shape((total, features), bf16), shape((8, features), f32), down_sum,
            shape((4, chunks, 240, 384), bf16), shape((seqs, 2, RIM, features), bf16),
        ],
        scratch_shapes=[
            pltpu.VMEM(w_down.shape, bf16), pltpu.VMEM(w_up.shape, bf16), pltpu.VMEM(hid_t.shape, bf16),
            pltpu.VMEM(mix_t.shape, bf16), dma((4,)), pltpu.VMEM((total, ff), bf16),
            pltpu.VMEM((total, features), bf16), pltpu.VMEM((seqs, 2, RIM, features), bf16),
            pltpu.VMEM((2, 2, 4, 192, 384), bf16), pltpu.VMEM((chunks + 1, 4, 192, 384), bf16),
            pltpu.VMEM((2, 4, 192, 384), bf16),
        ]
        + stage_scratch(192)
        + [dma((chunks + 1,)), dma((chunks + 1,)), dma((2,)), dma((4,)), dma((seqs, 2)), dma((seqs, 2))],
        compiler_params=params(62 * MB, collective_id=4, has_side_effects=True),
        name="rows_backward",
    )(gdl, slope, normed, s_att, w_out, gain_att, w_down, w_up, hid_t, mix_t, downs)


def first_back_step(gm_ref, p_ref, q_ref, mix_ref, kl_of, put_land, put_gq, put_klp):
    features = gm_ref.shape[2]
    masks = group_masks((M, 4 * E), 4, bf16)
    masks_wide = group_masks((M, 4 * E), 4, f32)
    for g in range(features // 256):
        sl = slice(256 * g, 256 * g + 256)
        gm, p = gm_ref[0, :, sl], p_ref[0, sl, :]
        put_land(g, diag_blocks(dot(p, gm), masks_wide).astype(bf16))
        d = dot_nt(block_diag(quad(mix_ref, g), masks), gm)
        parts = []
        for h in range(4):
            pw = p[E * h : E * h + E].astype(f32)
            dh = d[E * h : E * h + E]
            parts.append((pw * (dh - jnp.sum(pw * dh, axis=0, keepdims=True))).astype(bf16))
        gs = jnp.concatenate(parts, axis=0)
        put_gq(g, dot_tn(gs, block_diag(kl_of(sl), masks)).astype(bf16))
        put_klp(g, diag_blocks(dot(gs, q_ref[0, :, sl]), masks_wide))


def first_back_kernel(gm_ref, p_ref, q_ref, mix_ref, kl_ref, land_ref, gq_ref, klp_ref):
    def put_land(g, x):
        for i in range(2):
            land_ref[2 * g + i] = x[:, 128 * i : 128 * i + 128]

    def put_klp(g, x):
        klp_ref[0, :, 256 * g : 256 * g + 256] = x

    def put_gq(g, x):
        gq_ref[0, :, 256 * g : 256 * g + 256] = x

    first_back_step(gm_ref, p_ref, q_ref, mix_ref, lambda sl: kl_ref[0, :, sl], put_land, put_gq, put_klp)


def first_back(gm, probs, q, mixed, k_land):
    seqs, rows, features = q.shape
    pairs = features // 128
    full = pl.BlockSpec((1, rows, features), lambda s: (s, 0, 0))
    land = pl.BlockSpec((1, M, features), lambda s: (s, 0, 0))
    return pl.pallas_call(
        first_back_kernel,
        grid=(seqs,),
        in_specs=[full, pl.BlockSpec((1, features, rows), lambda s: (s, 0, 0)), full, pl.BlockSpec((pairs, M, 128), lambda s: (s, 0, 0)), land],
        out_specs=[pl.BlockSpec((pairs, M, 128), lambda s: (s, 0, 0)), full, land],
        out_shape=[
            jax.ShapeDtypeStruct((seqs * pairs, M, 128), bf16),
            jax.ShapeDtypeStruct(q.shape, bf16),
            jax.ShapeDtypeStruct((seqs, M, features), f32),
        ],
        compiler_params=params(62 * MB),
        name="first_back",
    )(gm, probs, q, mixed, k_land)


def third_back_kernel(w_ref, v_ref, k_ref, gc_ref, gn_ref, gt_ref, ql_ref, gv_ref, gk_ref, qlp_ref):
    features = w_ref.shape[2]
    masks = group_masks((M, 4 * E), 4, bf16)
    masks_wide = group_masks((M, 4 * E), 4, f32)
    for g in range(features // 256):
        sl = slice(256 * g, 256 * g + 256)
        w = w_ref[0, :, sl]
        gn = jnp.concatenate([gn_ref[2 * g], gn_ref[2 * g + 1]], axis=1)
        gt = jnp.concatenate([gt_ref[2 * g, 0:1, :], gt_ref[2 * g + 1, 0:1, :]], axis=1)
        gd = block_diag(gn, masks)
        gs = (w.astype(f32) * (dot_nt(v_ref[0, :, sl], gd) + gt)).astype(bf16)
        gv_ref[0, :, sl] = (dot(w, gd) + gc_ref[0, :, sl].astype(f32)).astype(bf16)
        gk_ref[0, :, sl] = dot(gs, block_diag(ql_ref[0, :, sl], masks)).astype(bf16)
        qlp_ref[0, :, sl] = diag_blocks(dot_tn(gs, k_ref[0, :, sl]), masks_wide)


def third_back(w, v, k, grad_conv, gn, gt, q_land):
    seqs, rows, features = v.shape
    pairs = features // 128
    full = pl.BlockSpec((1, rows, features), lambda s: (s, 0, 0))
    land = pl.BlockSpec((1, M, features), lambda s: (s, 0, 0))
    return pl.pallas_call(
        third_back_kernel,
        grid=(seqs,),
        in_specs=[full] * 4
        + [
            pl.BlockSpec((pairs, M, 128), lambda s: (s, 0, 0)),
            pl.BlockSpec((pairs, 8, 128), lambda s: (s, 0, 0)),
            land,
        ],
        out_specs=[full, full, land],
        out_shape=[jax.ShapeDtypeStruct(v.shape, bf16)] * 2
        + [jax.ShapeDtypeStruct((seqs, M, features), f32)],
        compiler_params=params(62 * MB),
        name="third_back",
    )(w, v, k, grad_conv, gn, gt, q_land)


def last_kernel(tok_ref, gq_ref, gk_ref, gv_ref, qo_ref, ko_ref, proj_ref, w_ref, gt_ref, wg_ref, d, tok_t):
    step = pl.program_id(0)
    seqs = tok_t.shape[1] // tok_ref.shape[1]
    rows, features = tok_ref.shape[1:]
    marks = qo_ref.shape[1]
    seg = rows // marks

    @pl.when(step < seqs)
    def _():
        here = pl.ds(pl.multiple_of(step * rows, rows), rows)
        for part, (core, own) in enumerate(((gq_ref, qo_ref), (gk_ref, ko_ref))):
            for m in range(marks):
                at = pl.ds(pl.multiple_of(step * rows + m * seg, seg), seg)
                x = core[0, m * seg : m * seg + seg, :].astype(f32) + own[0, m : m + 1, :] * (1.0 / seg)
                x = x.astype(bf16)
                if part == 0:
                    x = x * jnp.asarray(0.125, bf16)
                d[at, part * features : part * features + features] = x
        d[here, 2 * features :] = gv_ref[0]
        tok_t[:, here] = tok_ref[0].T
        for c in range(0, rows, 128):
            at = pl.ds(pl.multiple_of(step * rows + c, 128), 128)
            gt_ref[0, c : c + 128, :] = (
                proj_ref[0, c : c + 128, :].astype(f32) + dot_nt(d[at, :], w_ref[...])
            ).astype(bf16)

    @pl.when(step >= seqs)
    def _():
        base = (step - seqs) * features
        for c in range(0, features, 256):
            cols = pl.ds(pl.multiple_of(base + c, 256), 256)
            wg_ref[0, :, c : c + 256] = dot(tok_t[...], d[:, cols]).astype(bf16)


def last_pass(tokens, gq, gk, gv, q_own, k_own, proj, w_qkv):
    seqs, rows, features = tokens.shape
    marks = q_own.shape[1]
    here = lambda i: jnp.minimum(i, seqs - 1)
    full = pl.BlockSpec((1, rows, features), lambda i: (here(i), 0, 0))
    land = pl.BlockSpec((1, marks, features), lambda i: (here(i), 0, 0))
    return pl.pallas_call(
        last_kernel,
        grid=(seqs + 3,),
        in_specs=[full] * 4 + [land] * 2
        + [full, pl.BlockSpec(w_qkv.shape, lambda i: (0, 0), pipeline_mode=pl.Buffered(1))],
        out_specs=[full, pl.BlockSpec((1, features, features), lambda i: (jnp.maximum(i - seqs, 0), 0, 0))],
        out_shape=[
            jax.ShapeDtypeStruct(tokens.shape, bf16),
            jax.ShapeDtypeStruct((3, features, features), bf16),
        ],
        scratch_shapes=[
            pltpu.VMEM((seqs * rows, 3 * features), bf16), pltpu.VMEM((features, seqs * rows), bf16),
        ],
        compiler_params=params(62 * MB),
        name="last_pass",
    )(tokens, gq, gk, gv, q_own, k_own, proj, w_qkv)


def add_pairs(dst, own, start, pairs):
    for i in range(own.shape[0]):
        @pl.when(start + i < pairs)
        def _(i=i):
            dst[start + i] += own[i]


def cross_copies(src, got, sems):
    _, x, y, _, along_x, along_y = cube()
    return [
        remote(src.at[0:2, :, 1 - x], got.at[0], sems.at[0, 0], sems.at[1, 0], along_x),
        remote(src.at[2:4, 1 - y], got.at[1], sems.at[0, 1], sems.at[1, 1], along_y),
    ]


def kept_copies(src, kept, sems):
    _, x, y, _, _, _ = cube()
    return [
        pltpu.make_async_copy(src.at[0:2, :, x], kept.at[0], sems.at[0]),
        pltpu.make_async_copy(src.at[2:4, y], kept.at[1], sems.at[1]),
    ]


def turn_copies(kept, got, sems):
    _, x, y, _, along_x, along_y = cube()
    return [
        remote(kept.at[0, :, 1 - y], got.at[0], sems.at[0, 0], sems.at[1, 0], along_y),
        remote(kept.at[1, :, 1 - x], got.at[1], sems.at[0, 1], sems.at[1, 1], along_x),
    ]


def cross_add(kept, got):
    for half in range(2):
        for rank in range(2):
            kept[half, rank] = add_low(kept[half, rank], got[half, rank])


def turn_add(out, kept, got):
    _, x, y, _, _, _ = cube()
    for half, place in ((0, y), (1, x)):
        for rank in range(2):
            out[2 * half + rank] = add_low(kept[half, rank, place], got[half, rank])


def stage_scratch(rows):
    dma = pltpu.SemaphoreType.DMA
    return [
        pltpu.VMEM((2, 2, 2, rows, 384), bf16), pltpu.VMEM((2, 2, 2, rows, 384), bf16),
        pltpu.VMEM((2, 2, rows, 384), bf16), dma((2,)), dma((2, 2)), dma((2, 2)),
    ]


def first_third(w_ref, v_ref, k_ref, gn_of, gt_of, put_gs, put_qlp):
    features = w_ref.shape[2]
    masks = group_masks((M, 4 * E), 4, bf16)
    masks_wide = group_masks((M, 4 * E), 4, f32)
    for g in range(features // 256):
        sl = slice(256 * g, 256 * g + 256)
        gd = block_diag(jnp.concatenate([gn_of(2 * g), gn_of(2 * g + 1)], axis=1), masks)
        gt = jnp.concatenate([gt_of(2 * g), gt_of(2 * g + 1)], axis=1)
        gs = (w_ref[0, :, sl].astype(f32) * (dot_nt(v_ref[0, :, sl], gd) + gt)).astype(bf16)
        put_gs(g, gs)
        put_qlp(g, diag_blocks(dot_tn(gs, k_ref[0, :, sl]), masks_wide))


def tail_plan(seqs, pairs, blocks):
    tiles = (2, 2, pairs - 4)
    at, step = {}, 0
    for name, count in (
        ("first", seqs), ("conv_a", tiles[0]), ("inverse", 1), ("one", seqs), ("conv_b", tiles[1]), ("q", 1),
        ("conv_c", tiles[2]), ("values", 1), ("v", 1), ("keys", 1), ("k", 1), ("tok", blocks), ("last", 1),
    ):
        at[name] = step
        step += count
    return at, tuple((at[n], c) for n, c in zip(("conv_a", "conv_b", "conv_c"), tiles)), step


def tail_kernel(
    seqs, gm_ref, p_ref, q_ref, mix_ref, ql_ref, kl_ref, cg_ref, rim_ref, cv_ref, f_ref,
    sum_in, mid_in, z_in, zp_in, za_in, zw_in, scale_in, tot_in, alpha_in,
    wts_in, v_ref, k_ref, tok_ref, proj_ref, gain_a_ref, gain_f_ref, wq_in, down_in, up_in,
    gtok_ref, up_out, down_out, out_out, qkv_out, taps_out, ga_out, gf_out,
    sum_ref, mid_ref, z_ref, zp_ref, za_ref, zw_ref, scale_ref, tot_ref, alpha_ref, save_sems,
    d, tok_t, wq_ref, wts_ref, klp, land, land_got, gn, gn_got, gt, gt_low, gt_got, mq, mk, g_acc, dk_acc, kl_low, kl_got,
    qlp, qlow, qgot, pad, facc, taps, tapsg, up_sum, up_got, down_got,
    part, got_a, sum_a, got_b, sum_b, got_c, sum_c, got_z, sm_got, sm_sum,
    kept, crossed, turned, kept_sems, cross_sems, turn_sems,
    load_sem, land_sems, gn_sems, gt_sems, kl_sems, q_sems, zd_sems, ze_sems, zu_sems, zv_sems,
    a_send, a_recv, b_sems, c_sems, zq_send, zq_recv, s_send, s_recv, s_sems,
):
    step = pl.program_id(0)
    last = pl.num_programs(0) - 1
    rows, features = tok_ref.shape[1:]
    pairs = features // 128
    ranks, own = land_got.shape[:2]
    marks = kl_got.shape[2]
    seg = rows // marks
    at, plan, _ = tail_plan(seqs, pairs, d.shape[0] // gtok_ref.shape[0])
    me, _ = seq_place()
    core, x, y, sibling, along_x, along_y = cube()
    cross = cross_copies(up_in, crossed, cross_sems)
    keep = kept_copies(up_in, kept, kept_sems)
    turn = turn_copies(kept, turned, turn_sems)
    load = pltpu.make_async_copy(wq_in, wq_ref, load_sem.at[0])
    saves = [
        pltpu.make_async_copy(a, b, save_sems.at[i])
        for i, (a, b) in enumerate(
            (
                (sum_in, sum_ref), (mid_in, mid_ref), (z_in, z_ref), (zp_in, zp_ref), (za_in, za_ref),
                (zw_in, zw_ref), (scale_in, scale_ref), (tot_in, tot_ref), (alpha_in, alpha_ref),
            )
        )
    ]
    load_wts = pltpu.make_async_copy(wts_in, wts_ref, load_sem.at[1])

    def z_copies(src, dst, first, count, sems):
        span = pl.ds(first, count)
        sends = [
            remote(src.at[peer, span], dst.at[me, span], sems.at[0, o], sems.at[1, o], {"seq": peer})
            for o, peer in seq_peers()
        ]
        return sends, pltpu.make_async_copy(src.at[me, span], dst.at[me, span], sems.at[0, 0])

    downs = [z_copies(down_in, down_got, 0, 96, zd_sems), z_copies(down_in, down_got, 96, 96, ze_sems)]
    ups = [z_copies(up_sum, up_got, 0, 80, zu_sems), z_copies(up_sum, up_got, 80, 160, zv_sems)]

    def mark_copies(src, dst, sems):
        sends = [
            remote(
                src.at[:, pl.ds(peer * marks, marks)], dst.at[me], sems.at[0, o], sems.at[1, o], {"seq": peer}
            )
            for o, peer in seq_peers()
        ]
        return sends, pltpu.make_async_copy(src.at[:, pl.ds(me * marks, marks)], dst.at[me], sems.at[0, 0])

    gn_exchange = [swap_rows(gn, gn_got, gn_sems), swap_rows(gt_low, gt_got, gt_sems)]
    kl_exchange = mark_copies(kl_low, kl_got, kl_sems)
    q_exchange = mark_copies(qlow, qgot, q_sems)

    def a_copy(p):
        return remote(
            part.at[1 - core, pl.ds(4 * p, 4)], got_a.at[pl.ds(4 * p, 4)], a_send.at[p], a_recv.at[p], sibling
        )

    def b_copies(p):
        return [
            remote(
                sum_a.at[4 * p : 4 * p + 2, :, 1 - x], got_b.at[p, 0], b_sems.at[0, p, 0], b_sems.at[1, p, 0],
                along_x,
            ),
            remote(
                sum_a.at[4 * p + 2 : 4 * p + 4, 1 - y], got_b.at[p, 1], b_sems.at[0, p, 1], b_sems.at[1, p, 1],
                along_y,
            ),
        ]

    def c_copies(p):
        return [
            remote(
                sum_b.at[p, 0, :, 1 - y], got_c.at[p, 0], c_sems.at[0, p, 0], c_sems.at[1, p, 0], along_y
            ),
            remote(
                sum_b.at[p, 1, :, 1 - x], got_c.at[p, 1], c_sems.at[0, p, 1], c_sems.at[1, p, 1], along_x
            ),
        ]

    def zq_copy(group):
        rank, place = group // 3, group % 3
        offset = lax.rem(rank - me + ranks, ranks)
        return rank, remote(
            sum_c.at[group], got_z.at[me, place], zq_send.at[group], zq_recv.at[place, offset], {"seq": rank}
        )

    def stage_b(p):
        a_copy(p).wait()
        for yx in range(4):
            sum_a[4 * p : 4 * p + 4, yx // 2, yx % 2] = add_low(
                part[core, 4 * p : 4 * p + 4, yx], got_a[4 * p : 4 * p + 4, yx]
            )
        for copy in b_copies(p):
            copy.start()

    def stage_c(p):
        for copy in b_copies(p):
            copy.wait()
        sum_b[p, 0] = add_low(sum_a[4 * p : 4 * p + 2, :, x], got_b[p, 0])
        sum_b[p, 1] = add_low(sum_a[4 * p + 2 : 4 * p + 4, y], got_b[p, 1])
        for copy in c_copies(p):
            copy.start()

    def stage_z(p):
        for copy in c_copies(p):
            copy.wait()
        sum_c[4 * p : 4 * p + 2] = add_low(sum_b[p, 0, :, y], got_c[p, 0])
        sum_c[4 * p + 2 : 4 * p + 4] = add_low(sum_b[p, 1, :, x], got_c[p, 1])
        for group in range(4 * p, 4 * p + 4):
            rank, copy = zq_copy(group)

            @pl.when(rank != me)
            def _(copy=copy):
                copy.start()

    small_copies = [
        remote(sm_sum.at[i], sm_got.at[i], s_send.at[i], s_recv.at[i], target)
        for i, target in enumerate((sibling, along_x, along_y))
    ]

    def small_spread():
        return [
            remote(sm_sum.at[3], sm_got.at[3 + me], s_sems.at[0, o], s_sems.at[1, o], {"seq": peer})
            for o, peer in seq_peers()
        ]

    def seq_rows(s):
        return pl.ds(pl.multiple_of(s * rows, rows), rows)

    @pl.when(step == 0)
    def _():
        greet([sibling, along_x, along_y])
        for copy in cross + keep:
            copy.start()
        begin(downs[0])
        land[seqs * pairs :] = jnp.zeros_like(land[seqs * pairs :])

    @pl.when(step == 1)
    def _():
        for save in saves:
            save.start()

    @pl.when(step == at["conv_a"])
    def _():
        load_wts.start()
        load.start()

    @pl.when(step < seqs)
    def _():
        def put_land(g, v):
            for i in range(2):
                land[step * pairs + 2 * g + i] = v[:, 128 * i : 128 * i + 128]

        def put_klp(g, v):
            for i in range(2):
                klp[step * pairs + 2 * g + i] = v[:, 128 * i : 128 * i + 128]

        def put_gq(g, v):
            d[seq_rows(step), 256 * g : 256 * g + 256] = v

        first_back_step(gm_ref, p_ref, q_ref, mix_ref, lambda sl: kl_ref[step, :, sl], put_land, put_gq, put_klp)

    @pl.when(step == seqs - 1)
    def _():
        begin(swap_copies(land, land_got, own, land_sems))

    group = pick_tile(step, plan)
    moving = functools.reduce(
        jnp.logical_or, [(step >= first) & (step < first + tiles) for first, tiles in plan]
    )

    @pl.when(moving)
    def _():
        lanes = pl.ds(pl.multiple_of(group * 128, 128), 128)

        def put_taps(v):
            tapsg[0:KW, lanes] = v

        def one_sequence(seq, carry):
            def put(c, v):
                spot = pl.ds(pl.multiple_of(seq * rows + c, 64), 64)
                d[spot, pl.ds(pl.multiple_of(2 * features + group * 128, 128), 128)] = v

            one = pl.ds(seq, 1)
            conv_back_rows(
                seq, seqs, cg_ref.at[one], rim_ref.at[one], cv_ref.at[one], f_ref, put, put_taps, pad, facc, taps
            )
            return carry

        lax.fori_loop(0, seqs, one_sequence, 0)

    @pl.when(step == at["inverse"])
    def _():
        finish(swap_copies(land, land_got, own, land_sems))
        for save in saves:
            save.wait()

        def shared():
            for r in range(ranks):
                gt_low[r] = jnp.concatenate(
                    [gt[r, i, 0:1, :] for i in range(own)] + [jnp.zeros((8 - own, 128), f32)], axis=0
                )
            for pair in gn_exchange:
                begin(pair)

        inverse_back_step(
            land_got, ql_ref, kl_ref, sum_ref, mid_ref, z_ref, zp_ref, za_ref, zw_ref, scale_ref, tot_ref, alpha_ref,
            gn, gt, mq, mk, g_acc, dk_acc, shared,
        )
        add_pairs(klp, mk, me * own, seqs * pairs)
        kl_low[...] = klp[...].astype(bf16)
        begin(kl_exchange)

    @pl.when(step == at["one"])
    def _():
        for copy in cross + keep:
            copy.wait()
        cross_add(kept, crossed)
        for copy in turn:
            copy.start()
        for pair in gn_exchange:
            finish(pair)
        load_wts.wait()

    def gn_of(s):
        def of(i):
            p = s * pairs + i
            return gn_got[p // own, p % own]

        return of

    def land_rows(of):
        total = of(0).astype(f32)
        for r in range(1, ranks):
            total = total + of(r).astype(f32)
        return total * (1.0 / seg)

    @pl.when(step == at["values"])
    def _():
        sm_sum[0, KW:, :] = jnp.zeros_like(sm_sum[0, KW:, :])
        sm_sum[0, :KW, :] = tapsg[:KW]
        sm_sum[0, KW : KW + 1, :] = jnp.sum(gain_a_ref[...], axis=0, keepdims=True)
        sm_sum[0, KW + 1 : KW + 2, :] = jnp.sum(gain_f_ref[...], axis=0, keepdims=True)
        small_copies[0].start()

    for i in range(1, 4):
        @pl.when(step == at["values"] + i)
        def _(i=i):
            small_copies[i - 1].wait()
            sm_sum[i] = sm_sum[i - 1] + sm_got[i - 1]
            if i < 3:
                small_copies[i].start()
            else:
                for copy in small_spread():
                    copy.start()

    @pl.when((step >= at["one"]) & (step < at["one"] + seqs))
    def _():
        s = step - at["one"]

        def gt_of(i):
            p = s * pairs + i
            return gt_got[p // own, pl.ds(p % own, 1), :]

        def put_gs(g, val):
            d[seq_rows(s), features + 256 * g : features + 256 * g + 256] = val

        def put_qlp(g, val):
            for i in range(2):
                qlp[s * pairs + 2 * g + i] = val[:, 128 * i : 128 * i + 128]

        first_third(wts_ref.at[pl.ds(s, 1)], v_ref, k_ref, gn_of(s), gt_of, put_gs, put_qlp)
        tok_t[:, seq_rows(s)] = tok_ref[0].T

    @pl.when(step == at["one"] + seqs - 1)
    def _():
        add_pairs(qlp, mq, me * own, seqs * pairs)
        qlow[...] = qlp[...].astype(bf16)
        begin(q_exchange)

    @pl.when(step == at["q"])
    def _():
        finish(q_exchange)
        for copy in turn:
            copy.wait()
        turn_add(up_sum, kept, turned)
        begin(downs[1])
        begin(ups[0])

        def fill(s, carry):
            for g in range(pairs):
                spread = land_rows(lambda r: qgot[r, s * pairs + g])
                for m in range(marks):
                    spot = pl.ds(pl.multiple_of(s * rows + m * seg, seg), seg)
                    val = d[spot, 128 * g : 128 * g + 128].astype(f32)
                    low = (val + spread[m : m + 1]).astype(bf16) * jnp.asarray(0.125, bf16)
                    d[spot, 128 * g : 128 * g + 128] = low
            return carry

        lax.fori_loop(0, seqs, fill, 0)

    @pl.when(step == at["keys"])
    def _():
        finish(kl_exchange)

    @pl.when(step == at["keys"])
    def _():
        masks = group_masks((M, 4 * E), 4, bf16)

        def keys(s, carry):
            for g in range(features // 256):
                ks = slice(features + 256 * g, features + 256 * g + 256)
                val = dot(d[seq_rows(s), ks], block_diag(ql_ref[s, :, 256 * g : 256 * g + 256], masks))
                for i in range(2):
                    p = s * pairs + 2 * g + i
                    spread = land_rows(lambda r: kl_got[r, p])
                    lane = features + 256 * g + 128 * i
                    for m in range(marks):
                        spot = pl.ds(pl.multiple_of(s * rows + m * seg, seg), seg)
                        d[spot, lane : lane + 128] = (
                            val[m * seg : m * seg + seg, 128 * i : 128 * i + 128] + spread[m : m + 1]
                        ).astype(bf16)
            return carry

        lax.fori_loop(0, seqs, keys, 0)

    @pl.when(step == at["values"])
    def _():
        masks = group_masks((M, 4 * E), 4, bf16)

        def values(s, carry):
            of = gn_of(s)
            for g in range(features // 256):
                gd = block_diag(jnp.concatenate([of(2 * g), of(2 * g + 1)], axis=1), masks)
                vs = slice(2 * features + 256 * g, 2 * features + 256 * g + 256)
                here = seq_rows(s)
                d[here, vs] = (
                    dot(wts_ref[s, :, 256 * g : 256 * g + 256], gd) + d[here, vs].astype(f32)
                ).astype(bf16)
            return carry

        lax.fori_loop(0, seqs, values, 0)

    @pl.when(step == at["tok"])
    def _():
        load.wait()

    for when, stages in (
        (at["conv_c"] + 1, [(stage_b, 0)]),
        (at["values"], [(stage_c, 0)]),
        (at["keys"], [(stage_z, 0)]),
        (at["k"], [(stage_b, 2)]),
    ):
        @pl.when(step == when)
        def _(stages=stages):
            for stage, p in stages:
                stage(p)

    @pl.when(step == at["conv_c"])
    def _():
        begin(ups[1])

    @pl.when((step == at["q"]) | (step == at["k"]) | (step == at["v"]))
    def _():
        p = jnp.where(step == at["q"], 0, jnp.where(step == at["k"], 1, 2))
        for c in range(2):
            cols = pl.ds(pl.multiple_of(p * features + 384 * c, 128), 384)
            low = dot(tok_t[...], d[:, cols]).astype(bf16)
            for i in range(2):
                for dd in range(8):
                    part[dd % 2, 4 * p + 2 * c + i, dd // 2] = fold(
                        low[96 * dd : 96 * dd + 96, 192 * i : 192 * i + 192]
                    )
        a_copy(p).start()

    late_stages = {1: [(stage_b, 1)], 2: [(stage_c, 2)], 5: [(stage_c, 1), (stage_z, 2)]}

    @pl.when((step >= at["tok"]) & (step < last))
    def _():
        size = gtok_ref.shape[0] // 2
        for h in range(2):
            for slot, stages in late_stages.items():
                if slot % 2 == h:
                    @pl.when(step == at["tok"] + slot // 2)
                    def _(stages=stages):
                        for stage, p in stages:
                            stage(p)

            spot = pl.ds(pl.multiple_of((step - at["tok"]) * 2 * size + h * size, size), size)
            near = slice(h * size, h * size + size)
            gtok_ref[near, :] = (proj_ref[near, :].astype(f32) + dot_nt(d[spot, :], wq_ref[...])).astype(bf16)

    def unfold(block):
        return jnp.concatenate([block[:, :192], block[:, 192:]], axis=0)

    def rank_sum(got):
        total = got[0].astype(f32)
        for r in range(1, ranks):
            total = total + got[r].astype(f32)
        return total

    @pl.when(step == last)
    def _():
        stage_z(1)
        for copy in small_spread():
            copy.wait()
        sm_got[3 + me] = sm_sum[3]
        small = (sm_got[3] + sm_got[4]) + (sm_got[5] + sm_got[6])
        taps_out[...] = small[:KW]
        ga_out[...] = small[KW : KW + 1].reshape(features)
        gf_out[...] = small[KW + 1 : KW + 2].reshape(features)
        for pair in downs + ups:
            finish(pair)
        down_out[...] = rank_sum(down_got)
        total = rank_sum(up_got)
        up_out[:, :384] = total[:96]
        up_out[:, 384:] = total[96:192]
        out_out[...] = unfold(total[192:240])
        for group in range(12):
            rank, copy = zq_copy(group)

            @pl.when(rank != me)
            def _(copy=copy):
                copy.wait_send()

        for o in range(1, ranks):
            source = lax.rem(me - o + ranks, ranks)
            for place in range(3):
                remote(
                    sum_c.at[0], got_z.at[source, place], zq_send.at[0], zq_recv.at[place, o], {"seq": source}
                ).wait_recv()
        for place in range(3):
            got_z[me, place] = sum_c[3 * me + place]
        qkv_out[...] = jnp.concatenate(
            [unfold(sum(got_z[r, place].astype(f32) for r in range(ranks))) for place in range(3)], axis=1
        )


def tail(
    gm, probs, q, mixed, q_land, k_land, rim, v, taps, saved, weights, k, tokens, proj, gain_a, gain_f, w_qkv, downs, ups
):
    seqs, rows, features = tokens.shape
    ranks = lax.axis_size("seq")
    pairs = features // 128
    count = seqs * pairs
    own = saved[0].shape[0]
    marks = M // ranks
    total = seqs * rows
    size = 512
    blocks = total // size
    at, plan, steps = tail_plan(seqs, pairs, blocks)
    clip = lambda i, name: jnp.clip(i - at[name], 0, seqs - 1)
    tile = lambda i: pick_tile(i, plan)
    by_seq = lambda shape, of: pl.BlockSpec((1,) + shape, lambda i: (of(i), 0, 0))
    head = lambda i: clip(i, "first")
    one = lambda i: clip(i, "one")
    conv_spec = pl.BlockSpec((seqs, rows, 128), lambda i: (0, 0, tile(i)))
    rim_spec = pl.BlockSpec((seqs, 2, RIM, 128), lambda i: (0, 0, 0, tile(i)))
    tap_spec = pl.BlockSpec((KW, 128), lambda i: (0, tile(i)))
    later = pl.BlockSpec((size, features), lambda i: (jnp.clip(i - at["tok"], 0, blocks - 1), 0))
    whole = lambda a: pl.BlockSpec(a.shape, lambda i: (0,) * len(a.shape), pipeline_mode=pl.Buffered(1))
    flat = (rows, features)
    vm = lambda *shape: pltpu.VMEM(shape, bf16)
    wide = lambda *shape: pltpu.VMEM(shape, f32)
    dma = pltpu.SemaphoreType.DMA
    shares = [
        jax.ShapeDtypeStruct(s, f32)
        for s in ((96, 768), (192, 384), (96, 192), (96, 576), (KW, 768), (768,), (768,))
    ]
    return pl.pallas_call(
        functools.partial(tail_kernel, seqs),
        grid=(steps,),
        in_specs=[
            by_seq(flat, head), by_seq((features, rows), head), by_seq(flat, head),
            pl.BlockSpec((pairs, M, 128), lambda i: (head(i), 0, 0)), whole(q_land), whole(k_land),
            conv_spec, rim_spec, conv_spec, tap_spec,
        ]
        + [ANY] * len(saved)
        + [ANY, by_seq(flat, one), by_seq(flat, one), by_seq(flat, one), later]
        + [whole(gain_a), whole(gain_f), ANY, ANY, ANY],
        out_specs=[later] + [whole(a) for a in shares],
        out_shape=[jax.ShapeDtypeStruct((total, features), bf16)] + shares,
        scratch_shapes=[pltpu.VMEM(a.shape, a.dtype) for a in saved]
        + [
            dma((len(saved),)), vm(total, 3 * features), vm(features, total), vm(*w_qkv.shape), vm(*weights.shape), wide(count, M, 128),
            vm(ranks * own, M, 128), vm(ranks, own, M, 128), vm(ranks, own, M, 128), vm(ranks, own, M, 128),
            wide(ranks, own, 8, 128), wide(ranks, 8, 128), wide(ranks, 8, 128), wide(own, M, 128), wide(own, M, 128),
            wide(own, M, 128), wide(own, M, 128), vm(count, M, 128), vm(ranks, count, marks, 128),
            wide(count, M, 128), vm(count, M, 128), vm(ranks, count, marks, 128), wide(rows + 2 * RIM, 128),
            wide(KW * 8, 128), wide(40, 128), wide(40, features), vm(4, 240, 384), vm(ranks, 240, 384),
            vm(ranks, 192, 384),
            vm(2, 12, 4, 48, 384), vm(12, 4, 48, 384), vm(12, 2, 2, 48, 384), vm(3, 2, 2, 2, 48, 384),
            vm(3, 2, 2, 2, 48, 384), vm(3, 2, 2, 48, 384), vm(12, 48, 384), vm(ranks, 3, 48, 384),
            wide(3 + ranks, 40, features), wide(4, 40, features),
        ]
        + stage_scratch(240)
        + [dma((2,))]
        + [rank_sems() for _ in range(9)]
        + [
            dma((3,)), dma((3,)), dma((2, 3, 2)), dma((2, 3, 2)), dma((12,)), dma((3, ranks)), dma((3,)), dma((3,)),
            rank_sems(),
        ],
        compiler_params=params(63 * MB, collective_id=5, has_side_effects=True),
        name="tail",
    )(
        gm, probs, q, mixed, q_land, k_land, gm, rim, v, taps, *saved, weights, v, k, tokens, proj, gain_a, gain_f,
        w_qkv, downs, ups,
    )


def halo(cells, width):
    count = lax.axis_size("seq")
    head, tail = cells[:, :width], cells[:, cells.shape[1] - width :]
    left = lax.ppermute(tail, "seq", [(i, i + 1) for i in range(count - 1)])
    right = lax.ppermute(head, "seq", [(i + 1, i) for i in range(count - 1)])
    return jnp.stack([left, right], axis=1)


def scatter_sum(grad):
    share = lax.psum_scatter(grad, "dp", scatter_dimension=0, tiled=True)
    return lax.psum_scatter(share, "seq", scatter_dimension=1, tiled=True).astype(f32)


def per_device_general(tokens, w_qkv, w_out, w_up, w_down, conv_filter, gain_att, gain_ffn, grad_out):
    seqs, rows, features = tokens.shape
    ranks = lax.axis_size("seq")
    rank = lax.axis_index("seq")
    marks = M // ranks
    ff = w_up.shape[1]
    pairs = seqs * (features // 128)
    own = -(-pairs // ranks)

    def from_pairs(x):
        x = x[:pairs].reshape(seqs, features // 128, M, 128).transpose(0, 2, 1, 3)
        return x.reshape(seqs, M, features)

    def pad_pairs(x):
        return jnp.pad(x, ((0, ranks * own - pairs),) + ((0, 0),) * (x.ndim - 1))

    def exchange(x):
        out = lax.all_to_all(pad_pairs(x), "seq", 0, 0, tiled=True)
        return out.reshape((ranks, own) + x.shape[1:])

    taps = conv_filter
    q, k, v, k_part, q_land, v_rim = project(tokens, w_qkv, marks)
    first_group = 4
    weights, probs, k_land, conv_a, num_parts, stat_parts = scores(
        q, k, v, q_land, k_part, v_rim, taps, own, first_group
    )
    mixed_pairs, conv_b, *saved = inverse(num_parts, stat_parts, q_land, k_land, v, v_rim, taps, first_group)
    mixed = mixed_pairs
    layer_out, proj, gm, wg, gains = row_pass(
        tokens, probs, conv_a, conv_b, mixed, grad_out, w_out, w_up, w_down, gain_att, gain_ffn
    )
    shape3 = (seqs, rows, features)
    gm = gm.reshape(shape3)
    chunks = ff // features
    up_share = scatter_sum(wg[:chunks].transpose(1, 0, 2).reshape(features, ff))
    down_share = scatter_sum(wg[chunks : 2 * chunks].transpose(0, 2, 1).reshape(ff, features))
    out_share = scatter_sum(wg[2 * chunks])
    land_part, gq, k_land_part = first_back(gm, probs, q, mixed, k_land)
    g_rim = halo(gm, RIM)
    land_parts = exchange(land_part)
    grad_conv, taps_grad = conv_back(gm, g_rim, v, taps)
    gn_own, gt_own, mid_q, mid_k = inverse_back(land_parts, q_land, k_land, saved)

    def give_back(x):
        x = x.reshape((ranks * own,) + x.shape[2:])
        return lax.all_to_all(x, "seq", 0, 0, tiled=True)[:pairs]

    grad_values, gk, q_land_part = third_back(
        weights, v, k, grad_conv, give_back(gn_own), give_back(gt_own), q_land
    )

    def place(x):
        full = jnp.zeros((ranks * own, M, 128), f32)
        return from_pairs(lax.dynamic_update_slice_in_dim(full, x, rank * own, 0))

    both = jnp.stack([q_land_part + place(mid_q), k_land_part + place(mid_k)]).astype(bf16)
    both = both.reshape(2, seqs, ranks, marks, features).transpose(2, 0, 1, 3, 4)
    both = lax.all_to_all(both, "seq", 0, 0, tiled=True).astype(f32).sum(0)
    grad_tokens, qkv_grad = last_pass(tokens, gq, gk, grad_values, both[0], both[1], proj.reshape(shape3), w_qkv)
    qkv_share = scatter_sum(qkv_grad.transpose(1, 0, 2).reshape(features, 3 * features))
    gains = gains.reshape(2, 8, features).sum(1)
    small = lax.psum(jnp.concatenate([taps_grad, gains]), ("dp", "seq"))
    return (
        layer_out.reshape(shape3),
        grad_tokens,
        qkv_share,
        out_share,
        up_share,
        down_share,
        small[:KW],
        small[KW],
        small[KW + 1],
    )


def deliver_kernel(*refs):
    count = len(refs) // 2
    for i in range(count):
        if i < 2:
            refs[count + i][...] = refs[i][...]
        else:
            @pl.when(pl.program_id(0) == 0)
            def _(i=i):
                refs[count + i][...] = refs[i][...]


def deliver(*arrays):
    steps = 4
    split = lambda a: pl.BlockSpec((a.shape[0] // steps, a.shape[1]), lambda i: (i, 0))
    whole = lambda a: pl.BlockSpec(a.shape, lambda i: (0,) * len(a.shape))
    specs = [split(a) for a in arrays[:2]] + [whole(a) for a in arrays[2:]]
    return pl.pallas_call(
        deliver_kernel,
        grid=(steps,),
        in_specs=specs,
        out_specs=specs,
        out_shape=[jax.ShapeDtypeStruct(a.shape, a.dtype) for a in arrays],
        compiler_params=params(62 * MB),
        name="deliver",
    )(*arrays)


def per_device(tokens, w_qkv, w_out, w_up, w_down, conv_filter, gain_att, gain_ffn, grad_out):
    seqs, rows, features = tokens.shape
    ranks = lax.axis_size("seq")
    marks = M // ranks
    pairs = seqs * (features // 128)
    own = -(-pairs // ranks)
    taps = conv_filter
    shape3 = (seqs, rows, features)

    q, k, v, weights, probs, q_land, k_land, v_rim, conv_out, mixed, *saved = front(tokens, w_qkv, taps, own)
    layer_out, normed, s_att, gdl, slope, hid_t, mix_t, gain_f, downs = rows_forward(
        tokens, probs, conv_out, mixed, grad_out, w_out, w_up, w_down, gain_att, gain_ffn
    )
    proj, gm, gain_a, downs, ups, g_rim = rows_backward(
        gdl, slope, normed, s_att, w_out, gain_att, w_down, w_up, hid_t, mix_t, downs.reshape(4, 2, 2, 192, 384), seqs
    )
    grad_tokens, up, down, out, qkv, taps_all, gain_att_all, gain_ffn_all = tail(
        gm.reshape(shape3), probs, q, mixed, q_land, k_land, g_rim, v, taps, saved, weights, k, tokens, proj, gain_a,
        gain_f, w_qkv, downs, ups.reshape(4, 2, 2, 240, 384),
    )
    layer_out, grad_tokens, qkv, out, up, down, taps_all, gain_att_all, gain_ffn_all = deliver(
        layer_out, grad_tokens, qkv, out, up, down, taps_all, gain_att_all, gain_ffn_all
    )
    return (
        layer_out.reshape(shape3),
        grad_tokens.reshape(shape3),
        qkv,
        out,
        up,
        down.T,
        taps_all,
        gain_att_all,
        gain_ffn_all,
    )


def solution(mesh):
    placed = (P("dp", "seq", None), P(), P(), P(), P(), P(), P(), P(), P("dp", "seq", None))
    eight_by_four = mesh.shape["dp"] == 8 and mesh.shape["seq"] == 4
    return jax.shard_map(
        per_device if eight_by_four else per_device_general,
        mesh=mesh,
        in_specs=placed,
        out_specs=(
            P("dp", "seq", None),
            P("dp", "seq", None),
            P("dp", "seq"),
            P("dp", "seq"),
            P("dp", "seq"),
            P("dp", "seq"),
            P(),
            P(),
            P(),
        ),
        check_vma=False,
    )
```

```python
import functools

import jax
import jax.numpy as jnp
from jax import lax
from jax.experimental import pallas as pl
from jax.experimental.pallas import tpu as pltpu
from jax.sharding import PartitionSpec as P

H = 12
E = 64
M = 64
KW = 33
RIM = KW // 2
NEWTON = 6

f32 = jnp.float32
bf16 = jnp.bfloat16
epsilon = 1e-05
root_half = 0.7071067811865476
inv_root_two_pi = 0.3989422804014327
MB = 1 << 20

ERFC_P = 0.6
ERFC_C = (0.37028039425845705, 0.14043533559747823, 0.7278464793107866, -0.23856251479455173)
log2_e = 1.4426950408889634


def dot(a, b):
    return lax.dot_general(a, b, (((1,), (0,)), ((), ())), preferred_element_type=f32)


def dot_nt(a, b):
    return lax.dot_general(a, b, (((1,), (1,)), ((), ())), preferred_element_type=f32)


def dot_tn(a, b):
    return lax.dot_general(a, b, (((0,), (0,)), ((), ())), preferred_element_type=f32)


def lane_group(shape):
    return lax.broadcasted_iota(jnp.int32, shape, len(shape) - 1) // E


def group_masks(shape, count, dtype):
    groups = lane_group(shape)
    return [(groups == h).astype(f32).astype(dtype) for h in range(count)]


def block_diag(x, masks):
    return jnp.concatenate([x * m for m in masks], axis=0)


def diag_blocks(n, masks):
    return sum(n[E * h : E * h + E] * m for h, m in enumerate(masks))


def quad(ref, g):
    return jnp.concatenate([ref[2 * g], ref[2 * g + 1]], axis=1)


def params(limit=None, **kw):
    return pltpu.CompilerParams(vmem_limit_bytes=limit, **kw)


MESH = pl.DeviceIdType.MESH
ANY = pl.BlockSpec(memory_space=pl.ANY)


def seq_place():
    return lax.axis_index("seq"), lax.axis_size("seq")


def seq_peers():
    me, count = seq_place()
    return [(o, lax.rem(me + o, count)) for o in range(1, count)]


def greet(extra=()):
    barrier = pltpu.get_barrier_semaphore()
    targets = [{"seq": peer} for _, peer in seq_peers()] + list(extra)
    for target in targets:
        pl.semaphore_signal(barrier, inc=1, device_id=target, device_id_type=MESH)
    pl.semaphore_wait(barrier, len(targets))


def remote(src, dst, send, recv, target):
    return pltpu.make_async_remote_copy(
        src_ref=src, dst_ref=dst, send_sem=send, recv_sem=recv, device_id=target, device_id_type=MESH
    )


def swap_copies(src, dst, own, sems):
    me, count = seq_place()
    copies = [
        remote(src.at[pl.ds(peer * own, own)], dst.at[me], sems.at[0, o], sems.at[1, o], {"seq": peer})
        for o, peer in seq_peers()
    ]
    return copies, pltpu.make_async_copy(src.at[pl.ds(me * own, own)], dst.at[me], sems.at[0, 0])


def spread_copies(src, dst, own, sems):
    me, count = seq_place()
    at = dst.at[pl.ds(me * own, own)]
    copies = [
        remote(src, at, sems.at[0, o], sems.at[1, o], {"seq": peer}) for o, peer in seq_peers()
    ]
    return copies, pltpu.make_async_copy(src, at, sems.at[0, 0])


def begin(pair):
    for copy in pair[0]:
        copy.start()
    pair[1].start()


def finish(pair):
    for copy in pair[0]:
        copy.wait()
    pair[1].wait()


def swap_rows(src, dst, sems):
    me, _ = seq_place()
    copies = [
        remote(src.at[peer], dst.at[me], sems.at[0, o], sems.at[1, o], {"seq": peer}) for o, peer in seq_peers()
    ]
    return copies, pltpu.make_async_copy(src.at[me], dst.at[me], sems.at[0, 0])


def cube():
    d = lax.axis_index("dp")
    core, x, y = d % 2, (d // 2) % 2, d // 4
    return core, x, y, {"dp": d + 1 - 2 * core}, {"dp": d + 2 - 4 * x}, {"dp": d + 4 - 8 * y}


def add_low(a, b):
    return (a.astype(f32) + b.astype(f32)).astype(bf16)


def rank_sems():
    return pltpu.SemaphoreType.DMA((2, lax.axis_size("seq")))


def project_kernel(
    tok_ref, w_ref, q_ref, k_ref, v_ref, kl_ref, land_out, rim_out, land, rim, send, recv, local, rim_send, rim_recv,
    rim_local,
):
    step = pl.program_id(0)
    seqs = pl.num_programs(0)
    me, count = seq_place()
    rows, features = tok_ref.shape[1:]
    marks = land.shape[1]
    seg = rows // marks

    @pl.when(step == 0)
    def _():
        greet()

    x = tok_ref[0]
    for part, out in enumerate((q_ref, k_ref, v_ref)):
        for c in range(0, features, 256):
            p = dot(x, w_ref[:, part * features + c : part * features + c + 256])
            if part == 0:
                p = 0.125 * p
            low = p.astype(bf16)
            out[0, :, c : c + 256] = low
            if part < 2:
                total = low.astype(f32).reshape(marks, seg, 256).sum(1)
                mean = (total * (1.0 / seg)).astype(bf16)
                if part == 0:
                    land[step, :, c : c + 256] = mean
                else:
                    kl_ref[0, :, c : c + 256] = mean
            else:
                rim[step, 0, :, c : c + 256] = low[rows - RIM :]
                rim[step, 1, :, c : c + 256] = low[:RIM]

    def copies(s):
        spot = land_out.at[s, pl.ds(me * marks, marks)]
        sends = [
            remote(land.at[s], spot, send.at[s, o], recv.at[s, o], {"seq": peer}) for o, peer in seq_peers()
        ]
        return sends, pltpu.make_async_copy(land.at[s], spot, local.at[s])

    def rim_copy(s, side):
        there = lax.rem(me + (1 if side == 0 else count - 1), count)
        return remote(
            rim.at[s, side], rim_out.at[s, side], rim_send.at[s, side], rim_recv.at[s, side], {"seq": there}
        )

    begin(copies(step))
    for side in range(2):
        rim_copy(step, side).start()

    @pl.when(step == seqs - 1)
    def _():
        def drain(s, carry):
            finish(copies(s))
            for side in range(2):
                rim_copy(s, side).wait()
            return carry

        lax.fori_loop(0, seqs, drain, 0)


def project(tokens, w_qkv, marks):
    seqs, rows, features = tokens.shape
    ranks = lax.axis_size("seq")
    full = pl.BlockSpec((1, rows, features), lambda s: (s, 0, 0))
    dma = pltpu.SemaphoreType.DMA
    return pl.pallas_call(
        project_kernel,
        grid=(seqs,),
        in_specs=[full, pl.BlockSpec(w_qkv.shape, lambda s: (0, 0), pipeline_mode=pl.Buffered(1))],
        out_specs=[full] * 3 + [pl.BlockSpec((1, marks, features), lambda s: (s, 0, 0))] + [ANY] * 2,
        out_shape=[jax.ShapeDtypeStruct(tokens.shape, bf16)] * 3
        + [
            jax.ShapeDtypeStruct((seqs, marks, features), bf16),
            jax.ShapeDtypeStruct((seqs, M, features), bf16),
            jax.ShapeDtypeStruct((seqs, 2, RIM, features), bf16),
        ],
        scratch_shapes=[
            pltpu.VMEM((seqs, marks, features), bf16), pltpu.VMEM((seqs, 2, RIM, features), bf16),
            dma((seqs, ranks)), dma((seqs, ranks)), dma((seqs,)), dma((seqs, 2)), dma((seqs, 2)), dma((seqs,)),
        ],
        compiler_params=params(62 * MB, collective_id=0, has_side_effects=True),
        name="project",
    )(tokens, w_qkv)


def fill_taps(taps, f_ref):
    taps[0:KW, :] = f_ref[...].astype(f32)


def fill_pad(pad, x_ref, rim_ref):
    rows = x_ref.shape[1]
    me, count = seq_place()
    pad[0:RIM, :] = jnp.where(me > 0, rim_ref[0, 0].astype(f32), 0.0)
    pad[RIM : RIM + rows, :] = x_ref[0].astype(f32)
    pad[RIM + rows : RIM + rows + RIM, :] = jnp.where(me < count - 1, rim_ref[0, 1].astype(f32), 0.0)


def conv_tile(v_ref, rim_ref, taps_ref, o_ref, pad, f_ref):
    rows = v_ref.shape[1]
    fill_pad(pad, v_ref, rim_ref)
    fill_taps(f_ref, taps_ref)
    conv_rows(o_ref, pad, f_ref, rows)


def conv_rows(o_ref, pad, f_ref, rows):
    for c in range(0, rows, 64):
        acc = jnp.zeros((64, 128), f32)
        for j in range(KW):
            acc = acc + f_ref[j : j + 1, :] * pad[c + j : c + j + 64, :]
        o_ref[0, c : c + 64, :] = acc.astype(bf16)


def conv_specs(rows, first_step, first_group, groups):
    at = lambda i: jnp.maximum(i - first_step, 0)
    seq = lambda i: at(i) // groups
    group = lambda i: at(i) % groups
    return (
        pl.BlockSpec((1, rows, 128), lambda i: (seq(i), 0, first_group + group(i))),
        pl.BlockSpec((1, 2, RIM, 128), lambda i: (seq(i), 0, 0, first_group + group(i))),
        pl.BlockSpec((KW, 128), lambda i: (0, first_group + group(i))),
        pl.BlockSpec((1, rows, 128), lambda i: (seq(i), 0, group(i))),
    )


def conv_back_rows(seq, seqs, g_ref, rim_ref, v_ref, taps_ref, put, put_taps, pad, facc, f_ref):
    rows = v_ref.shape[1]
    fill_pad(pad, g_ref, rim_ref)
    fill_taps(f_ref, taps_ref)

    @pl.when(seq == 0)
    def _():
        facc[...] = jnp.zeros_like(facc)

    for c in range(0, rows, 64):
        acc = jnp.zeros((64, 128), f32)
        vals = v_ref[0, c : c + 64, :].astype(f32)
        for j in range(KW):
            moved = pad[c + 2 * RIM - j : c + 2 * RIM - j + 64, :]
            acc = acc + f_ref[j : j + 1, :] * moved
            facc[8 * j : 8 * j + 8, :] += (vals * moved).reshape(8, 8, 128).sum(0)
        put(c, acc.astype(bf16))

    @pl.when(seq == seqs - 1)
    def _():
        put_taps(facc[...].reshape(KW, 8, 128).sum(1))


def conv_back_tile(seq, seqs, g_ref, rim_ref, v_ref, taps_ref, o_ref, gf_ref, pad, facc, f_ref):
    def put(c, v):
        o_ref[0, c : c + 64, :] = v

    def put_taps(v):
        gf_ref[...] = v

    conv_back_rows(seq, seqs, g_ref, rim_ref, v_ref, taps_ref, put, put_taps, pad, facc, f_ref)


def conv_back_kernel(g_ref, rim_ref, v_ref, f_ref, o_ref, gf_ref, pad, facc, taps):
    conv_back_tile(
        pl.program_id(1), pl.num_programs(1), g_ref, rim_ref, v_ref, f_ref, o_ref, gf_ref, pad, facc, taps
    )


def conv_back_specs(rows, seqs, first_step, first_group):
    at = lambda i: jnp.maximum(i - first_step, 0)
    seq = lambda i: at(i) % seqs
    group = lambda i: at(i) // seqs
    return (
        pl.BlockSpec((1, rows, 128), lambda i: (seq(i), 0, first_group + group(i))),
        pl.BlockSpec((1, 2, RIM, 128), lambda i: (seq(i), 0, 0, first_group + group(i))),
        pl.BlockSpec((KW, 128), lambda i: (0, first_group + group(i))),
        pl.BlockSpec((1, rows, 128), lambda i: (seq(i), 0, group(i))),
        pl.BlockSpec((KW, 128), lambda i: (0, group(i))),
    )


def conv_back(g, rim, v, taps):
    seqs, rows, features = v.shape
    sp = lambda n: pl.BlockSpec((1, n, 128), lambda g, s: (s, 0, g))
    fs = pl.BlockSpec((KW, 128), lambda g, s: (0, g))
    return pl.pallas_call(
        conv_back_kernel,
        grid=(features // 128, seqs),
        in_specs=[sp(rows), pl.BlockSpec((1, 2, RIM, 128), lambda g, s: (s, 0, 0, g)), sp(rows), fs],
        out_specs=[sp(rows), fs],
        out_shape=[jax.ShapeDtypeStruct(v.shape, bf16), jax.ShapeDtypeStruct((KW, features), f32)],
        scratch_shapes=[pltpu.VMEM((rows + 2 * RIM, 128), f32), pltpu.VMEM((KW * 8, 128), f32), pltpu.VMEM((40, 128), f32)],
        name="conv_back",
    )(g, rim, v, taps)


def third_score_step(step, k_ref, v_ref, ql_ref, w_ref, num_ref, stat_ref, own):
    features = k_ref.shape[2]
    pairs = features // 128
    masks = group_masks((M, 4 * E), 4, bf16)
    masks_wide = group_masks((M, 4 * E), 4, f32)
    for g in range(features // 256):
        sl = slice(256 * g, 256 * g + 256)
        s3 = dot_nt(k_ref[0, :, sl], block_diag(ql_ref[0, :, sl], masks))
        peak = jnp.max(s3, axis=0, keepdims=True)
        e3 = jnp.exp(s3 - peak)
        total = jnp.sum(e3, axis=0, keepdims=True)
        low = e3.astype(bf16)
        w_ref[0, :, sl] = low
        num = diag_blocks(dot_tn(low, v_ref[0, :, sl]), masks_wide).astype(bf16)
        for i in range(2):
            lanes = slice(128 * i, 128 * i + 128)
            p = step * pairs + 2 * g + i
            num_ref[p] = num[:, lanes]
            stat_ref[p // own, pl.ds(p % own, 1), :] = peak[:, lanes]
            stat_ref[p // own, pl.ds(8 + p % own, 1), :] = total[:, lanes]


def first_score_step(q_ref, kl, p_ref):
    features = q_ref.shape[2]
    masks = group_masks((M, 4 * E), 4, bf16)
    for g in range(features // 256):
        sl = slice(256 * g, 256 * g + 256)
        s1 = dot_nt(block_diag(kl[:, sl], masks), q_ref[0, :, sl])
        for h in range(4):
            x = s1[E * h : E * h + E]
            e1 = jnp.exp(x - jnp.max(x, axis=0, keepdims=True))
            at = 256 * g + E * h
            p_ref[0, at : at + E, :] = (e1 * (1.0 / jnp.sum(e1, axis=0, keepdims=True))).astype(bf16)


def scores_kernel(
    seqs, own, q_ref, k_ref, v_ref, ql_ref, kp_ref, cv_ref, rim_ref, f_ref, w_ref, p_ref, kl_ref, co_ref, num_out,
    stat_out, num, stat, kl, pad, taps, num_sems, stat_sems, kl_sems,
):
    step = pl.program_id(0)
    steps = pl.num_programs(0)
    pairs = q_ref.shape[2] // 128
    marks = kp_ref.shape[1]
    me, _ = seq_place()

    def mark_copies():
        spot = kl.at[:, pl.ds(me * marks, marks)]
        sends = [
            remote(kp_ref, spot, kl_sems.at[0, o], kl_sems.at[1, o], {"seq": peer}) for o, peer in seq_peers()
        ]
        return sends, pltpu.make_async_copy(kp_ref, spot, kl_sems.at[0, 0])

    @pl.when(step == 0)
    def _():
        greet()
        begin(mark_copies())
        stat[...] = jnp.zeros_like(stat)
        if num.shape[0] > seqs * pairs:
            num[seqs * pairs :] = jnp.zeros_like(num[seqs * pairs :])

    @pl.when(step < seqs)
    def _():
        third_score_step(step, k_ref, v_ref, ql_ref, w_ref, num, stat, own)

    @pl.when(step == seqs - 1)
    def _():
        begin(swap_copies(num, num_out, own, num_sems))
        begin(swap_rows(stat, stat_out, stat_sems))

    @pl.when(step == seqs)
    def _():
        finish(mark_copies())
        kl_ref[...] = kl[...]

    @pl.when((step >= seqs) & (step < 2 * seqs))
    def _():
        first_score_step(q_ref, kl[step - seqs], p_ref)

    @pl.when(step >= 2 * seqs)
    def _():
        conv_tile(cv_ref, rim_ref, f_ref, co_ref, pad, taps)

    @pl.when(step == steps - 1)
    def _():
        finish(swap_copies(num, num_out, own, num_sems))
        finish(swap_rows(stat, stat_out, stat_sems))


def scores(q, k, v, q_land, k_part, rim, taps, own, groups):
    seqs, rows, features = q.shape
    marks = k_part.shape[1]
    ranks = lax.axis_size("seq")
    here = lambda i: jnp.minimum(i, seqs - 1)
    then = lambda i: jnp.clip(i - seqs, 0, seqs - 1)
    full = pl.BlockSpec((1, rows, features), lambda i: (here(i), 0, 0))
    next_full = pl.BlockSpec((1, rows, features), lambda i: (then(i), 0, 0))
    whole = lambda a: pl.BlockSpec(a.shape, lambda i: (0,) * len(a.shape), pipeline_mode=pl.Buffered(1))
    k_land = jax.ShapeDtypeStruct((seqs, M, features), bf16)
    cv, rims, ft, co = conv_specs(rows, 2 * seqs, 0, groups)
    return pl.pallas_call(
        functools.partial(scores_kernel, seqs, own),
        grid=(2 * seqs + seqs * groups,),
        in_specs=[
            next_full, full, full, pl.BlockSpec((1, M, features), lambda i: (here(i), 0, 0)), whole(k_part), cv,
            rims, ft,
        ],
        out_specs=[full, pl.BlockSpec((1, features, rows), lambda i: (then(i), 0, 0)), whole(k_land), co, ANY, ANY],
        out_shape=[
            jax.ShapeDtypeStruct(q.shape, bf16),
            jax.ShapeDtypeStruct((seqs, features, rows), bf16),
            k_land,
            jax.ShapeDtypeStruct((seqs, rows, 128 * groups), bf16),
            jax.ShapeDtypeStruct((ranks, own, M, 128), bf16),
            jax.ShapeDtypeStruct((ranks, 16, 128), f32),
        ],
        scratch_shapes=[
            pltpu.VMEM((ranks * own, M, 128), bf16), pltpu.VMEM((ranks, 16, 128), f32),
            pltpu.VMEM((seqs, M, features), bf16), pltpu.VMEM((rows + 2 * RIM, 128), f32),
            pltpu.VMEM((40, 128), f32), rank_sems(), rank_sems(), rank_sems(),
        ],
        compiler_params=params(62 * MB, collective_id=1, has_side_effects=True),
        name="scores",
    )(q, k, v, q_land, k_part, v, rim, taps)


def split(x):
    hi = x.astype(bf16)
    return hi, (x - hi.astype(f32)).astype(bf16)


def stack_parts(xs, axis):
    return jnp.concatenate([part for x in xs for part in split(x)], axis=axis)


def pair_sums(out, count):
    top = lambda i, j: out[128 * i + 64 * j : 128 * i + 64 * j + 64]
    return [
        top(i, 0)[:, :128] + (top(i, 0)[:, 128:] + top(i, 1)[:, :128]) for i in range(count)
    ]


def pair_nn(lefts, right, masks):
    hi, lo = split(right)
    packed = jnp.concatenate([block_diag(hi, masks), block_diag(lo, masks)], axis=1)
    return pair_sums(dot(stack_parts(lefts, 0), packed), len(lefts))


def pair_nt(lefts, right, masks):
    hi, lo = split(right)
    packed = jnp.concatenate([block_diag(hi, masks), block_diag(lo, masks)], axis=0)
    return pair_sums(dot_nt(stack_parts(lefts, 0), packed), len(lefts))


def pair_tn(left, rights, masks_wide):
    out = dot_tn(stack_parts([left], 1), stack_parts(rights, 1))
    results = []
    for i in range(len(rights)):
        full = out[:128, 256 * i : 256 * i + 128] + (
            out[:128, 256 * i + 128 : 256 * i + 256] + out[128:, 256 * i : 256 * i + 128]
        )
        results.append(diag_blocks(full, masks_wide))
    return results


def half_reduce(x, upper, op, fill):
    a = op(jnp.where(upper, fill, x), axis=1, keepdims=True)
    b = op(jnp.where(upper, x, fill), axis=1, keepdims=True)
    return jnp.where(upper, b, a)


def to_column(row, same, upper):
    return half_reduce(jnp.where(same, row, 0.0), upper, jnp.sum, 0.0)


def to_row(col, same):
    return jnp.sum(jnp.where(same, col, 0.0), axis=0, keepdims=True)


def pair_consts():
    lane = lax.broadcasted_iota(jnp.int32, (M, 128), 1)
    row = lax.broadcasted_iota(jnp.int32, (M, 128), 0)
    return lane >= E, row == lane % E, group_masks((M, 128), 2, bf16), group_masks((M, 128), 2, f32)


def own_pair(land_ref, i, own):
    me, _ = seq_place()
    per = land_ref.shape[2] // 128
    p = jnp.minimum(me * own + i, land_ref.shape[0] * per - 1)
    return land_ref[p // per, :, pl.ds(pl.multiple_of((p % per) * 128, 128), 128)]


def inverse_step(
    num_ref, stat_ref, ql_ref, kl_ref, mixed_ref, sum_ref, mid_ref, z_ref, p_ref, a_ref, w_ref,
    scale_ref, tot_ref, alpha_ref,
):
    ranks, own = num_ref.shape[:2]
    upper, same, masks, masks_wide = pair_consts()
    for i in range(own):
        peak = stat_ref[0, i : i + 1, :]
        for r in range(1, ranks):
            peak = jnp.maximum(peak, stat_ref[r, i : i + 1, :])
        total = jnp.zeros((1, 128), f32)
        numer = jnp.zeros((M, 128), f32)
        for r in range(ranks):
            alpha = jnp.exp(stat_ref[r, i : i + 1, :] - peak)
            total = total + alpha * stat_ref[r, 8 + i : 9 + i, :]
            column = to_column(alpha, same, upper)
            alpha_ref[r, i] = column
            numer = numer + column * num_ref[r, i].astype(f32)
        total = to_column(total, same, upper)
        tot_ref[i] = total
        sum_ref[i] = numer / total
        ql, kl = own_pair(ql_ref, i, own), own_pair(kl_ref, i, own)
        s2 = dot_nt(ql, block_diag(kl, masks))
        e2 = jnp.exp(s2 - half_reduce(s2, upper, jnp.max, -jnp.inf))
        middle = e2 / half_reduce(e2, upper, jnp.sum, 0.0)
        mid_ref[i] = middle
        st = dot_nt(kl, block_diag(ql, masks))
        et = jnp.exp(st - jnp.max(st, axis=0, keepdims=True))
        flipped = et / jnp.sum(et, axis=0, keepdims=True)
        column = jnp.sum(middle, axis=0, keepdims=True)
        scale = 1.0 / half_reduce(column, upper[0:1], jnp.max, -jnp.inf)
        scale_ref[i] = jnp.broadcast_to(scale, (8, 128))
        z_ref[0, i] = flipped * scale

    def step(it, carry):
        zs = [z_ref[it, i] for i in range(own)]
        ps = [pair_nn([mid_ref[i]], zs[i], masks)[0] for i in range(own)]
        second = [pair_nn([ps[i], zs[i]], ps[i], masks) for i in range(own)]
        for i in range(own):
            p2, a = second[i]
            w = 7.0 * ps[i] - p2
            p_ref[it, i] = ps[i]
            a_ref[it, i] = a
            w_ref[it, i] = w
            z_ref[it + 1, i] = 0.25 * (13.0 * zs[i] - 15.0 * a + pair_nn([a], w, masks)[0])
        return carry

    lax.fori_loop(0, NEWTON, step, 0)
    for i in range(own):
        mixed_ref[i] = pair_nn([z_ref[NEWTON, i]], sum_ref[i], masks)[0].astype(bf16)


def inverse_kernel(
    num_ref, stat_ref, ql_ref, kl_ref, cv_ref, rim_ref, f_ref, mixed_out, co_ref, sum_ref, mid_ref, z_ref, p_ref,
    a_ref, w_ref, scale_ref, tot_ref, alpha_ref, mixed, pad, taps, sems,
):
    step = pl.program_id(0)
    own = num_ref.shape[1]

    @pl.when(step == 0)
    def _():
        greet()
        inverse_step(
            num_ref, stat_ref, ql_ref, kl_ref, mixed, sum_ref, mid_ref, z_ref, p_ref, a_ref, w_ref, scale_ref,
            tot_ref, alpha_ref,
        )
        begin(spread_copies(mixed, mixed_out, own, sems))

    @pl.when(step > 0)
    def _():
        conv_tile(cv_ref, rim_ref, f_ref, co_ref, pad, taps)

    @pl.when(step == pl.num_programs(0) - 1)
    def _():
        finish(spread_copies(mixed, mixed_out, own, sems))


def inverse(num, stat, q_land, k_land, v, rim, taps, first_group):
    ranks, own = num.shape[:2]
    seqs, rows, features = v.shape
    groups = features // 128 - first_group
    mat = jax.ShapeDtypeStruct((own, M, 128), f32)
    steps = lambda n: jax.ShapeDtypeStruct((n, own, M, 128), f32)
    whole = lambda a: pl.BlockSpec(a.shape, lambda i: (0,) * len(a.shape), pipeline_mode=pl.Buffered(1))
    saved = [
        mat, mat, steps(NEWTON + 1), steps(NEWTON), steps(NEWTON), steps(NEWTON),
        jax.ShapeDtypeStruct((own, 8, 128), f32), mat, steps(ranks),
    ]
    cv, rims, ft, co = conv_specs(rows, 1, first_group, groups)
    return pl.pallas_call(
        inverse_kernel,
        grid=(1 + seqs * groups,),
        in_specs=[whole(num), whole(stat), whole(q_land), whole(k_land), cv, rims, ft],
        out_specs=[ANY, co] + [whole(a) for a in saved],
        out_shape=[
            jax.ShapeDtypeStruct((ranks * own, M, 128), bf16),
            jax.ShapeDtypeStruct((seqs, rows, 128 * groups), bf16),
        ]
        + saved,
        scratch_shapes=[
            pltpu.VMEM((own, M, 128), bf16), pltpu.VMEM((rows + 2 * RIM, 128), f32), pltpu.VMEM((40, 128), f32),
            rank_sems(),
        ],
        compiler_params=params(62 * MB, collective_id=2, has_side_effects=True),
        name="inverse",
    )(num, stat, q_land, k_land, v, rim, taps)


def inverse_back_step(
    land_ref, ql_ref, kl_ref, sum_ref, mid_ref, z_ref, p_ref, a_ref, w_ref, scale_ref, tot_ref,
    alpha_ref, gn_ref, gt_ref, mq_ref, mk_ref, g_ref, dk_ref, shared=lambda: None,
):
    ranks, own = land_ref.shape[:2]
    upper, same, masks, masks_wide = pair_consts()
    for i in range(own):
        land = land_ref[0, i].astype(f32)
        for r in range(1, ranks):
            land = land + land_ref[r, i].astype(f32)
        summary, total = sum_ref[i], tot_ref[i]
        gs = pair_tn(z_ref[NEWTON, i], [land], masks_wide)[0].astype(bf16).astype(f32)
        gn = (gs / total).astype(bf16).astype(f32)
        gt = -half_reduce(gs * summary, upper, jnp.sum, 0.0) / total
        for r in range(ranks):
            gn_ref[r, i] = (alpha_ref[r, i] * gn).astype(bf16)
            gt_ref[r, i] = jnp.broadcast_to(to_row(alpha_ref[r, i] * gt, same), (8, 128))
        g_ref[i] = pair_nt([land], summary, masks)[0]
        dk_ref[i] = jnp.zeros((M, 128), f32)
    shared()

    def step(back, carry):
        it = NEWTON - 1 - back
        gs = [g_ref[i] for i in range(own)]
        das, dws = [], []
        for i in range(own):
            das.append(0.25 * (pair_nt([gs[i]], w_ref[it, i], masks)[0] - 15.0 * gs[i]))
            dws.append(0.25 * pair_tn(a_ref[it, i], [gs[i]], masks_wide)[0])
        dps, parts = [], []
        for i in range(own):
            right = pair_nt([dws[i], das[i]], p_ref[it, i], masks)
            left = pair_tn(p_ref[it, i], [dws[i]], masks_wide)[0]
            dps.append(7.0 * dws[i] - right[0] - left + pair_tn(z_ref[it, i], [das[i]], masks_wide)[0])
            parts.append(3.25 * gs[i] + right[1])
        for i in range(own):
            g_ref[i] = parts[i] + pair_tn(mid_ref[i], [dps[i]], masks_wide)[0]
            dk_ref[i] += pair_nt([dps[i]], z_ref[it, i], masks)[0]
        return carry

    lax.fori_loop(0, NEWTON, step, 0)
    eye = jnp.where(same, 1.0, 0.0).astype(bf16)
    for i in range(own):
        g, middle, scale = g_ref[i], mid_ref[i], scale_ref[i, 0:1, :]
        turned = dot_tn(stack_parts([g], 1), eye)
        turned = diag_blocks(turned[:128] + turned[128:], masks_wide)
        column = jnp.sum(middle, axis=0, keepdims=True)
        top = half_reduce(column, upper[0:1], jnp.max, -jnp.inf)
        hit = jnp.where(column == top, 1.0, 0.0)
        share = hit / half_reduce(hit, upper[0:1], jnp.sum, 0.0)
        d_scale = half_reduce(jnp.sum(turned * middle, axis=0, keepdims=True), upper[0:1], jnp.sum, 0.0)
        dk = dk_ref[i] + turned * scale - share * (d_scale * scale * scale)
        ds = middle * (dk - half_reduce(middle * dk, upper, jnp.sum, 0.0))
        hi, lo = split(ds)
        both = dot(jnp.concatenate([hi, lo], axis=0), block_diag(own_pair(kl_ref, i, own), masks))
        mq_ref[i] = both[:M] + both[M:]
        turned = dot_tn(jnp.concatenate([hi, lo], axis=1), own_pair(ql_ref, i, own))
        mk_ref[i] = diag_blocks(turned[:128] + turned[128:], masks_wide)


def inverse_back(land, q_land, k_land, saved):
    ranks, own = land.shape[:2]
    mat = jax.ShapeDtypeStruct((own, M, 128), f32)
    return pl.pallas_call(
        inverse_back_step,
        out_shape=[
            jax.ShapeDtypeStruct((ranks, own, M, 128), bf16),
            jax.ShapeDtypeStruct((ranks, own, 8, 128), f32), mat, mat,
        ],
        scratch_shapes=[pltpu.VMEM((own, M, 128), f32)] * 2,
        compiler_params=params(62 * MB),
        name="inverse_back",
    )(land, q_land, k_land, *saved)


def pick_tile(step, plan):
    tile = 0
    done = 0
    for first, count in plan:
        tile = tile + jnp.clip(step - first, -1 if done else 0, count - 1) + (1 if done else 0)
        done += count
    return tile


def front_kernel(
    tok_ref, wq_ref, f_ref,
    q_ref, k_ref, v_ref, w_ref, p_ref, ql_out, kl_out, rim_out, conv_ref, mixed_out, sum_ref, mid_ref, z_ref, zp_ref,
    za_ref, zw_ref, scale_ref, tot_ref, alpha_ref,
    land_q, land_k, ql, kl, rim, rims, num, stat, num_got, stat_got, mixed, pad, taps,
    q_sems, k_sems, rim_send, rim_recv, num_sems, stat_sems, mixed_sems, *, plan, at_third, at_first, at_inverse,
):
    step = pl.program_id(0)
    seqs, rows, features = q_ref.shape
    marks = land_q.shape[1]
    seg = rows // marks
    pairs = features // 128
    own = num_got.shape[1]
    me, count = seq_place()

    def mark_copies(src, dst, sems, s):
        spot = dst.at[s, pl.ds(me * marks, marks)]
        sends = [
            remote(src.at[s], spot, sems.at[0, s, o], sems.at[1, s, o], {"seq": peer}) for o, peer in seq_peers()
        ]
        return sends, pltpu.make_async_copy(src.at[s], spot, sems.at[0, s, 0])

    def rim_copy(s, side):
        there = lax.rem(me + (1 if side == 0 else count - 1), count)
        return remote(
            rim.at[s, side], rims.at[s, side], rim_send.at[s, side], rim_recv.at[s, side], {"seq": there}
        )

    def has_next(side):
        return me < count - 1 if side == 0 else me > 0

    @pl.when(step == 0)
    def _():
        rims[...] = jnp.zeros_like(rims)
        greet()
        stat[...] = jnp.zeros_like(stat)
        num[seqs * pairs :] = jnp.zeros_like(num[seqs * pairs :])

    @pl.when(step < seqs)
    def _():
        x = tok_ref[0]
        for part, out in enumerate((q_ref, k_ref, v_ref)):
            for c in range(0, features, 256):
                p = dot(x, wq_ref[:, part * features + c : part * features + c + 256])
                if part == 0:
                    p = 0.125 * p
                low = p.astype(bf16)
                out[step, :, c : c + 256] = low
                if part < 2:
                    total = low.astype(f32).reshape(marks, seg, 256).sum(1)
                    (land_q, land_k)[part][step, :, c : c + 256] = (total * (1.0 / seg)).astype(bf16)
                else:
                    rim[step, 0, :, c : c + 256] = low[rows - RIM :]
                    rim[step, 1, :, c : c + 256] = low[:RIM]
        begin(mark_copies(land_q, ql, q_sems, step))

        @pl.when(step > 0)
        def _():
            for side in range(2):
                @pl.when(has_next(side))
                def _(side=side):
                    rim_copy(step, side).start()

    @pl.when(step == 1)
    def _():
        for side in range(2):
            @pl.when(has_next(side))
            def _(side=side):
                rim_copy(0, side).start()

    @pl.when(step == seqs)
    def _():
        for s in range(seqs):
            begin(mark_copies(land_k, kl, k_sems, s))

    tile = pick_tile(step, plan)
    seq, group = tile // pairs, tile % pairs
    for first, tiles in plan:
        @pl.when((step >= first) & (step < first + tiles))
        def _():
            @pl.when(group == 0)
            def _():
                for side in range(2):
                    @pl.when(has_next(side))
                    def _(side=side):
                        rim_copy(seq, side).wait_send()

                    @pl.when(has_next(1 - side))
                    def _(side=side):
                        rim_copy(seq, side).wait_recv()

            lanes = pl.ds(pl.multiple_of(group * 128, 128), 128)
            taps[0:KW, :] = f_ref[:, lanes].astype(f32)
            pad[0:RIM, :] = rims[seq, 0, :, lanes].astype(f32)
            pad[RIM : RIM + rows, :] = v_ref[seq, :, lanes].astype(f32)
            pad[RIM + rows : RIM + rows + RIM, :] = rims[seq, 1, :, lanes].astype(f32)
            conv_rows(conv_ref, pad, taps, rows)

    @pl.when(step == at_third)
    def _():
        for s in range(seqs):
            finish(mark_copies(land_q, ql, q_sems, s))
        ql_out[...] = ql[...]

    @pl.when((step >= at_third) & (step < at_third + seqs))
    def _():
        s = step - at_third
        third_score_step(s, k_ref.at[pl.ds(s, 1)], v_ref.at[pl.ds(s, 1)], ql.at[pl.ds(s, 1)], w_ref, num, stat, own)

    @pl.when(step == at_third + seqs - 1)
    def _():
        begin(swap_copies(num, num_got, own, num_sems))
        begin(swap_rows(stat, stat_got, stat_sems))

    @pl.when(step == at_first)
    def _():
        for s in range(seqs):
            finish(mark_copies(land_k, kl, k_sems, s))
        kl_out[...] = kl[...]

    @pl.when((step >= at_first) & (step < at_first + seqs))
    def _():
        s = step - at_first
        first_score_step(q_ref.at[pl.ds(s, 1)], kl[s], p_ref)

    @pl.when(step == at_inverse)
    def _():
        finish(swap_copies(num, num_got, own, num_sems))
        finish(swap_rows(stat, stat_got, stat_sems))
        inverse_step(
            num_got, stat_got, ql, kl, mixed, sum_ref, mid_ref, z_ref, zp_ref, za_ref, zw_ref, scale_ref, tot_ref,
            alpha_ref,
        )
        begin(spread_copies(mixed, mixed_out, own, mixed_sems))

    @pl.when(step == pl.num_programs(0) - 1)
    def _():
        finish(spread_copies(mixed, mixed_out, own, mixed_sems))
        rim_out[...] = rims[...]


def front(tokens, w_qkv, taps, own):
    seqs, rows, features = tokens.shape
    ranks = lax.axis_size("seq")
    marks = M // ranks
    pairs = features // 128
    tiles = (4, 5, seqs * pairs - 9)
    third = seqs + tiles[0]
    first = third + seqs + tiles[1]
    at = dict(at_third=third, at_first=first, at_inverse=first + seqs)
    plan = ((seqs, tiles[0]), (third + seqs, tiles[1]), (first + seqs + 1, tiles[2]))
    here = lambda first: (lambda i: jnp.clip(i - first, 0, seqs - 1))
    score, prob = here(at["at_third"]), here(at["at_first"])
    whole = lambda a: pl.BlockSpec(a.shape, lambda i: (0,) * len(a.shape), pipeline_mode=pl.Buffered(1))
    tile = lambda i: pick_tile(i, plan)
    rows_out = jax.ShapeDtypeStruct(tokens.shape, bf16)
    land = jax.ShapeDtypeStruct((seqs, M, features), bf16)
    rim_out = jax.ShapeDtypeStruct((seqs, 2, RIM, features), bf16)
    mat = jax.ShapeDtypeStruct((own, M, 128), f32)
    steps = lambda n: jax.ShapeDtypeStruct((n, own, M, 128), f32)
    saved = [
        mat, mat, steps(NEWTON + 1), steps(NEWTON), steps(NEWTON), steps(NEWTON),
        jax.ShapeDtypeStruct((own, 8, 128), f32), mat, steps(ranks),
    ]
    vm = lambda *shape: pltpu.VMEM(shape, bf16)
    dma = pltpu.SemaphoreType.DMA
    return pl.pallas_call(
        functools.partial(front_kernel, plan=plan, **at),
        grid=(plan[-1][0] + tiles[2],),
        in_specs=[
            pl.BlockSpec((1, rows, features), lambda i: (jnp.minimum(i, seqs - 1), 0, 0)), whole(w_qkv), whole(taps),
        ],
        out_specs=[whole(rows_out)] * 3
        + [
            pl.BlockSpec((1, rows, features), lambda i: (score(i), 0, 0)),
            pl.BlockSpec((1, features, rows), lambda i: (prob(i), 0, 0)),
            whole(land), whole(land), whole(rim_out),
            pl.BlockSpec((1, rows, 128), lambda i: (tile(i) // pairs, 0, tile(i) % pairs)), ANY,
        ]
        + [whole(a) for a in saved],
        out_shape=[rows_out] * 4
        + [
            jax.ShapeDtypeStruct((seqs, features, rows), bf16), land, land, rim_out, rows_out,
            jax.ShapeDtypeStruct((ranks * own, M, 128), bf16),
        ]
        + saved,
        scratch_shapes=[
            vm(seqs, marks, features), vm(seqs, marks, features), vm(seqs, M, features), vm(seqs, M, features),
            vm(seqs, 2, RIM, features), vm(seqs, 2, RIM, features), vm(ranks * own, M, 128),
            pltpu.VMEM((ranks, 16, 128), f32), vm(ranks, own, M, 128), pltpu.VMEM((ranks, 16, 128), f32),
            vm(own, M, 128), pltpu.VMEM((rows + 2 * RIM, 128), f32), pltpu.VMEM((40, 128), f32),
            dma((2, seqs, ranks)), dma((2, seqs, ranks)), dma((seqs, 2)), dma((seqs, 2)), rank_sems(), rank_sems(),
            rank_sems(),
        ],
        compiler_params=params(62 * MB, collective_id=0, has_side_effects=True),
        name="front",
    )(tokens, w_qkv, taps)


def mean_of(x):
    return jnp.mean(x, axis=-1, keepdims=True)


def gelu_and_slope(u):
    u = u.astype(bf16)
    low = lambda c: jnp.asarray(c, bf16)
    t = low(1.0) / (low(1.0) + low(ERFC_P * root_half) * jnp.abs(u))
    bell = jnp.exp2((u * u) * low(-0.5 * log2_e))
    poly = jnp.full_like(t, 0.5 * ERFC_C[-1])
    for c in ERFC_C[-2::-1]:
        poly = poly * t + low(0.5 * c)
    half = (poly * t) * bell
    cdf = jnp.where(u < 0, half, low(1.0) - half)
    return u * cdf, cdf + u * (bell * low(inv_root_two_pi))


def row_block(
    step, tok_ref, p_ref, conv_refs, mix_ref, top_ref, w_out_ref, w_up_ref, w_down_ref, ga_ref,
    gf_ref, out_ref, proj_ref, gm_ref, gains_ref, act, gul, slope, hid_t, gdl_t, mix_t, gpr, resid, whole, ready=lambda i: None,
):
    size, features = tok_ref.shape
    ff = act.shape[1]
    wide = features
    start = pl.multiple_of(step * size, size)
    rows = pl.ds(start, size)
    near = rows if whole else pl.ds(0, size)
    masks = group_masks((M, 4 * E), 4, bf16)
    for g in range(features // 256):
        sl = slice(256 * g, 256 * g + 256)
        att = dot_tn(p_ref[0, sl, :], block_diag(quad(mix_ref, g), masks))
        split_at = conv_refs[0].shape[1]
        ref, lane = (conv_refs[0], 256 * g) if 256 * g < split_at else (conv_refs[1], 256 * g - split_at)
        resid[:, sl] = (att + ref[:, lane : lane + 256].astype(f32)).astype(bf16)
    mixed = resid[...]
    mix_t[:, near] = mixed.T
    residual = tok_ref[...].astype(f32) + dot(mixed, w_out_ref[...])
    centre = residual - mean_of(residual)
    s_att = lax.rsqrt(mean_of(centre * centre) + epsilon)
    normed = centre * s_att
    gain_att = ga_ref[...].reshape(1, features)
    hidden = normed * gain_att
    hid_low = hidden.astype(bf16)
    hid_t[:, rows] = hid_low.T
    down = jnp.zeros((size, features), f32)
    for j in range(0, ff, wide):
        if j == 0:
            ready(0)
        up = dot(hid_low, w_up_ref[:, j : j + wide])
        low, sl = gelu_and_slope(up)
        act[near, j : j + wide] = low
        slope[:, j : j + wide] = sl
        if j == 0:
            ready(1)
        down = down + dot(low, w_down_ref[j : j + wide, :])
    residual_two = hidden + down
    centre_two = residual_two - mean_of(residual_two)
    s_ffn = lax.rsqrt(mean_of(centre_two * centre_two) + epsilon)
    normed_two = centre_two * s_ffn
    gain_ffn = gf_ref[...].reshape(1, features)
    out_ref[...] = (normed_two * gain_ffn).astype(bf16)
    top = top_ref[...].astype(f32)
    gains_ref[8:16, :] += (top * normed_two).reshape(size // 8, 8, features).sum(0)
    g = top * gain_ffn
    grad_two = s_ffn * (g - mean_of(g) - normed_two * mean_of(g * normed_two))
    gdl = grad_two.astype(bf16)
    gdl_t[:, near] = gdl.T
    back = jnp.zeros((size, features), f32)
    for j in range(0, ff, wide):
        gu = dot_nt(gdl, w_down_ref[j : j + wide, :]) * slope[:, j : j + wide].astype(f32)
        low = gu.astype(bf16)
        gul[rows, j : j + wide] = low
        back = back + dot_nt(low, w_up_ref[:, j : j + wide])
    grad_hidden = grad_two + back
    gains_ref[0:8, :] += (grad_hidden * normed).reshape(size // 8, 8, features).sum(0)
    g = grad_hidden * gain_att
    proj = (s_att * (g - mean_of(g) - normed * mean_of(g * normed))).astype(bf16)
    proj_ref[...] = proj
    if whole:
        gpr[rows, :] = proj
    gm_ref[...] = dot_nt(proj, w_out_ref[...]).astype(bf16)


def row_kernel(
    tok_ref, p_ref, conv_a_ref, conv_b_ref, mix_ref, top_ref, w_out_ref, w_up_ref, w_down_ref, ga_ref, gf_ref,
    out_ref, proj_ref, gm_ref, wg_ref, gains_ref,
    act, gul, slope, hid_t, gdl_t, mix_t, gpr, resid,
):
    step = pl.program_id(0)
    size, features = tok_ref.shape
    blocks = act.shape[0] // size
    ff = act.shape[1]
    wide = features

    @pl.when(step == 0)
    def _():
        gains_ref[...] = jnp.zeros_like(gains_ref)

    @pl.when(step < blocks)
    def _():
        row_block(
            step, tok_ref, p_ref, (conv_a_ref, conv_b_ref), mix_ref, top_ref, w_out_ref, w_up_ref, w_down_ref,
            ga_ref, gf_ref, out_ref, proj_ref, gm_ref, gains_ref, act, gul, slope, hid_t, gdl_t, mix_t, gpr,
            resid, True,
        )

    chunks = ff // wide
    for first, left, right in ((0, hid_t, gul), (chunks, gdl_t, act), (2 * chunks, mix_t, gpr)):
        count = chunks if first < 2 * chunks else 1

        @pl.when((step >= blocks + first) & (step < blocks + first + count))
        def _(first=first, left=left, right=right):
            base = (step - blocks - first) * wide
            for c in range(0, wide, 256):
                cols = pl.ds(pl.multiple_of(base + c, 256), 256)
                wg_ref[0, :, c : c + 256] = dot(left[...], right[:, cols]).astype(bf16)


def row_pass(tokens, probs, conv_a, conv_b, mixed, grad_out, w_out, w_up, w_down, gain_att, gain_ffn):
    seqs, rows, features = tokens.shape
    ff = w_up.shape[1]
    size = min(256, rows)
    total = seqs * rows
    blocks = total // size
    grads = 2 * (ff // features) + 1
    here = lambda i: jnp.minimum(i, blocks - 1)
    block = pl.BlockSpec((size, features), lambda i: (here(i), 0))
    whole = lambda a: pl.BlockSpec(a.shape, lambda i: (0,) * a.ndim, pipeline_mode=pl.Buffered(1))
    flat = lambda a: a.reshape(total, a.shape[2])
    part = lambda a: pl.BlockSpec((size, a.shape[2]), lambda i: (here(i), 0))
    gains = [gain_att, gain_ffn]
    row_out = jax.ShapeDtypeStruct((total, features), bf16)
    tall = pltpu.VMEM((features, total), bf16)
    return pl.pallas_call(
        row_kernel,
        grid=(blocks + grads,),
        in_specs=[
            block, pl.BlockSpec((1, features, size), lambda i: (here(i) * size // rows, 0, here(i) % (rows // size))),
            part(conv_a), part(conv_b),
            pl.BlockSpec((features // 128, M, 128), lambda i: (here(i) * size // rows, 0, 0)),
            block, whole(w_out), whole(w_up), whole(w_down), whole(gains[0]), whole(gains[1]),
        ],
        out_specs=[block] * 3
        + [
            pl.BlockSpec((1, features, features), lambda i: (jnp.maximum(i - blocks, 0), 0, 0)),
            pl.BlockSpec((16, features), lambda i: (0, 0)),
        ],
        out_shape=[row_out] * 3
        + [
            jax.ShapeDtypeStruct((grads, features, features), bf16),
            jax.ShapeDtypeStruct((16, features), f32),
        ],
        scratch_shapes=[
            pltpu.VMEM((total, ff), bf16), pltpu.VMEM((total, ff), bf16), pltpu.VMEM((size, ff), bf16),
            tall, tall, tall, pltpu.VMEM((total, features), bf16), pltpu.VMEM((size, features), bf16),
        ],
        compiler_params=params(62 * MB),
        name="row_pass",
    )(flat(tokens), probs, flat(conv_a), flat(conv_b), mixed, flat(grad_out), w_out, w_up, w_down, *gains)


def put_parts(parts, slot, low, c, by_rows):
    for l in range(0, low.shape[1], 128):
        side, lane = (c + l) // 384, (c + l) % 384
        if by_rows:
            for d in range(8):
                parts[slot, d % 2, d // 2, 96 * side : 96 * side + 96, lane : lane + 128] = low[
                    96 * d : 96 * d + 96, l : l + 128
                ]
        else:
            for z in range(4):
                parts[slot, side, z, :, lane : lane + 128] = low[192 * z : 192 * z + 192, l : l + 128]


def fold(block):
    return jnp.concatenate([block[:48], block[48:]], axis=1)


def rows_forward_kernel(
    tok_ref, p_ref, conv_ref, mix_ref, top_ref, w_out_ref, w_up_in, w_down_in, ga_ref, gf_ref,
    out_ref, normed_ref, s_ref, gdl_ref, slope_ref, hid_t_ref, mix_t_ref, gains_ref, g_out,
    w_up_ref, w_down_ref, load_sems, act, gdl_t, mixed_ref, parts, got, sums, send, recv, out_sem,
):
    step = pl.program_id(0)
    size, features = tok_ref.shape
    blocks = act.shape[0] // size
    ff = act.shape[1]
    chunks = ff // features
    core, _, _, sibling, _, _ = cube()
    loads = [
        pltpu.make_async_copy(w_up_in, w_up_ref, load_sems.at[0]),
        pltpu.make_async_copy(w_down_in, w_down_ref, load_sems.at[1]),
    ]

    @pl.when(step == 0)
    def _():
        for load in loads:
            load.start()
        gains_ref[...] = jnp.zeros_like(gains_ref)
        greet([sibling])

    @pl.when(step < blocks)
    def _():
        rows = pl.ds(pl.multiple_of(step * size, size), size)
        masks = group_masks((M, 4 * E), 4, bf16)
        for g in range(features // 256):
            sl = slice(256 * g, 256 * g + 256)
            att = dot_tn(p_ref[0, sl, :], block_diag(quad(mix_ref, g), masks))
            mixed_ref[:, sl] = (att + conv_ref[:, sl].astype(f32)).astype(bf16)
        mixed = mixed_ref[...]
        mix_t_ref[...] = mixed.T
        residual = tok_ref[...].astype(f32) + dot(mixed, w_out_ref[...])
        centre = residual - mean_of(residual)
        s_att = lax.rsqrt(mean_of(centre * centre) + epsilon)
        normed = centre * s_att
        s_ref[...] = jnp.broadcast_to(s_att, s_ref.shape)
        normed_ref[...] = normed.astype(bf16)
        hidden = normed * ga_ref[...].reshape(1, features)
        hid_low = hidden.astype(bf16)
        hid_t_ref[...] = hid_low.T

        @pl.when(step == 0)
        def _():
            for load in loads:
                load.wait()

        down = jnp.zeros((size, features), f32)
        for j in range(0, ff, features):
            low, sl = gelu_and_slope(dot(hid_low, w_up_ref[:, j : j + features]))
            act[rows, j : j + features] = low
            slope_ref[:, j : j + features] = sl
            down = down + dot(low, w_down_ref[j : j + features, :])
        residual_two = hidden + down
        centre_two = residual_two - mean_of(residual_two)
        s_ffn = lax.rsqrt(mean_of(centre_two * centre_two) + epsilon)
        normed_two = centre_two * s_ffn
        gain_ffn = gf_ref[...].reshape(1, features)
        out_ref[...] = (normed_two * gain_ffn).astype(bf16)
        top = top_ref[...].astype(f32)
        gains_ref[...] += (top * normed_two).reshape(size // 8, 8, features).sum(0)
        g = top * gain_ffn
        gdl = (s_ffn * (g - mean_of(g) - normed_two * mean_of(g * normed_two))).astype(bf16)
        gdl_ref[...] = gdl
        gdl_t[:, rows] = gdl.T

    j = step - blocks
    slot = lax.rem(jnp.maximum(j, 0), 2)

    def share(at):
        return remote(parts.at[at % 2, 1 - core], got.at[at], send.at[at], recv.at[at], sibling)

    def out_copy(at):
        return pltpu.make_async_copy(sums.at[at % 2], g_out.at[:, at], out_sem.at[at % 2])

    @pl.when((j >= 2) & (j < chunks))
    def _():
        share(j - 2).wait_send()

    @pl.when((j >= 0) & (j < chunks))
    def _():
        for c in range(0, features, 256):
            cols = pl.ds(pl.multiple_of(j * features + c, 256), 256)
            put_parts(parts, slot, dot(gdl_t[...], act[:, cols]).astype(bf16), c, False)
        share(j).start()

    done = j - 1

    @pl.when(done >= 2)
    def _():
        out_copy(done - 2).wait()

    @pl.when(done >= 0)
    def _():
        share(done).wait_recv()
        sums[done % 2] = add_low(parts[done % 2, core], got[done])
        out_copy(done).start()

    @pl.when(done == chunks - 1)
    def _():
        for at in (done - 1, done):
            share(at).wait_send()
            out_copy(at).wait()


def rows_forward(tokens, probs, conv_out, mixed, grad_out, w_out, w_up, w_down, gain_att, gain_ffn):
    seqs, rows, features = tokens.shape
    ff = w_up.shape[1]
    size = rows
    total = seqs * rows
    blocks = total // size
    chunks = ff // features
    here = lambda i: jnp.minimum(i, blocks - 1)
    block = lambda n: pl.BlockSpec((size, n), lambda i: (here(i), 0))
    turned = pl.BlockSpec((features, size), lambda i: (0, here(i)))
    whole = lambda a: pl.BlockSpec(a.shape, lambda i: (0,) * a.ndim, pipeline_mode=pl.Buffered(1))
    flat = lambda a: a.reshape(total, a.shape[2])
    shape = jax.ShapeDtypeStruct
    dma = pltpu.SemaphoreType.DMA
    return pl.pallas_call(
        rows_forward_kernel,
        grid=(blocks + chunks + 1,),
        in_specs=[
            block(features),
            pl.BlockSpec((1, features, size), lambda i: (here(i) * size // rows, 0, here(i) % (rows // size))),
            block(features), pl.BlockSpec((features // 128, M, 128), lambda i: (here(i) * size // rows, 0, 0)),
            block(features), whole(w_out), ANY, ANY, whole(gain_att), whole(gain_ffn),
        ],
        out_specs=[block(features), block(features), block(128), block(features), block(ff), turned, turned]
        + [pl.BlockSpec((8, features), lambda i: (0, 0)), ANY],
        out_shape=[
            shape((total, features), bf16), shape((total, features), bf16), shape((total, 128), f32),
            shape((total, features), bf16), shape((total, ff), bf16), shape((features, total), bf16),
            shape((features, total), bf16), shape((8, features), f32), shape((4, chunks, 192, 384), bf16),
        ],
        scratch_shapes=[
            pltpu.VMEM(w_up.shape, bf16), pltpu.VMEM(w_down.shape, bf16), dma((2,)), pltpu.VMEM((total, ff), bf16),
            pltpu.VMEM((features, total), bf16), pltpu.VMEM((size, features), bf16),
            pltpu.VMEM((2, 2, 4, 192, 384), bf16), pltpu.VMEM((chunks, 4, 192, 384), bf16),
            pltpu.VMEM((2, 4, 192, 384), bf16), dma((chunks,)), dma((chunks,)), dma((2,)),
        ],
        compiler_params=params(62 * MB, collective_id=3, has_side_effects=True),
        name="rows_forward",
    )(
        flat(tokens), probs, flat(conv_out), mixed, flat(grad_out), w_out, w_up, w_down, gain_att, gain_ffn
    )


def rows_backward_kernel(
    turn_at, gdl_ref, slope_ref, normed_ref, s_ref, w_out_ref, ga_ref, w_down_in, w_up_in, hid_t_in, mix_t_in, down_in,
    proj_ref, gm_ref, gains_ref, down_ref, g_out, rim_out,
    w_down_ref, w_up_ref, hid_t, mix_t, load_sems, gul, gpr, rim, parts, got, sums,
    kept, crossed, turned, kept_sems, cross_sems, turn_sems,
    send, recv, out_sem, last_sem, rim_send, rim_recv,
):
    step = pl.program_id(0)
    size, features = gdl_ref.shape
    ff = gul.shape[1]
    blocks = gul.shape[0] // size
    chunks = ff // features
    seqs = rim.shape[0]
    per = blocks // seqs
    me, count = seq_place()
    core, _, _, sibling, along_x, along_y = cube()
    loads = [
        pltpu.make_async_copy(a, b, load_sems.at[i])
        for i, (a, b) in enumerate(
            ((w_down_in, w_down_ref), (w_up_in, w_up_ref), (hid_t_in, hid_t), (mix_t_in, mix_t))
        )
    ]
    cross = cross_copies(down_in, crossed, cross_sems)
    keep = kept_copies(down_in, kept, kept_sems)
    turn = turn_copies(kept, turned, turn_sems)

    @pl.when(step == 0)
    def _():
        for load in loads[:2]:
            load.start()
        gains_ref[...] = jnp.zeros_like(gains_ref)
        greet([sibling, along_x, along_y])
        for copy in cross + keep:
            copy.start()

    @pl.when(step == 1)
    def _():
        for load in loads[2:]:
            load.start()

    @pl.when(step == turn_at)
    def _():
        for copy in cross + keep:
            copy.wait()
        cross_add(kept, crossed)
        for copy in turn:
            copy.start()

    def rim_copy(s, side):
        there = lax.rem(me + (1 if side == 0 else count - 1), count)
        return remote(
            rim.at[s, side], rim_out.at[s, side], rim_send.at[s, side], rim_recv.at[s, side], {"seq": there}
        )

    @pl.when(step < blocks)
    def _():
        rows = pl.ds(pl.multiple_of(step * size, size), size)

        @pl.when(step == 0)
        def _():
            loads[0].wait()

        gdl = gdl_ref[...]
        back = gdl.astype(f32)
        for j in range(0, ff, features):
            gu = dot_nt(gdl, w_down_ref[j : j + features, :]) * slope_ref[:, j : j + features].astype(f32)
            low = gu.astype(bf16)
            gul[rows, j : j + features] = low
            if j == 0:
                @pl.when(step == 0)
                def _():
                    loads[1].wait()
            back = back + dot_nt(low, w_up_ref[:, j : j + features])
        normed = normed_ref[...].astype(f32)
        gains_ref[...] += (back * normed).reshape(size // 8, 8, features).sum(0)
        g = back * ga_ref[...].reshape(1, features)
        proj = (s_ref[:, 0:1] * (g - mean_of(g) - normed * mean_of(g * normed))).astype(bf16)
        proj_ref[...] = proj
        gpr[rows, :] = proj
        gm_ref[...] = dot_nt(proj, w_out_ref[...]).astype(bf16)
        s = step // per

        @pl.when(step % per == 0)
        def _():
            rim[s, 1] = gm_ref[:RIM, :]
            rim_copy(s, 1).start()

        @pl.when(step % per == per - 1)
        def _():
            rim[s, 0] = gm_ref[size - RIM :, :]
            rim_copy(s, 0).start()

    j = step - blocks
    slot = lax.rem(jnp.maximum(j, 0), 2)

    def share(at):
        return remote(parts.at[at % 2, 1 - core], got.at[at], send.at[at], recv.at[at], sibling)

    def up_copy(at):
        return pltpu.make_async_copy(sums.at[at % 2], g_out.at[at, :, 0:192, :], out_sem.at[at % 2])

    def out_copy(z):
        return pltpu.make_async_copy(
            sums.at[0, :, 48 * z : 48 * z + 48, :], g_out.at[z, :, 192:240, :], last_sem.at[z]
        )

    @pl.when((j >= 2) & (j <= chunks))
    def _():
        share(j - 2).wait_send()

    @pl.when(j == 0)
    def _():
        loads[2].wait()
        loads[3].wait()

    @pl.when((j >= 0) & (j < chunks))
    def _():
        for c in range(0, features, 256):
            cols = pl.ds(pl.multiple_of(j * features + c, 256), 256)
            put_parts(parts, slot, dot(hid_t[...], gul[:, cols]).astype(bf16), c, True)
        share(j).start()

    @pl.when(j == chunks)
    def _():
        for c in range(2):
            low = dot(mix_t[...], gpr[:, 384 * c : 384 * c + 384]).astype(bf16)
            for zz in range(2):
                z = 2 * c + zz
                for d in range(8):
                    parts[slot, d % 2, d // 2, 48 * z : 48 * z + 48, :] = fold(
                        low[96 * d : 96 * d + 96, 192 * zz : 192 * zz + 192]
                    )
        share(j).start()

    done = j - 1

    @pl.when(done >= 2)
    def _():
        up_copy(done - 2).wait()

    @pl.when(done >= 0)
    def _():
        share(done).wait_recv()
        sums[done % 2] = add_low(parts[done % 2, core], got[done])

    @pl.when((done >= 0) & (done < chunks))
    def _():
        up_copy(done).start()

    @pl.when(done == chunks)
    def _():
        for z in range(4):
            out_copy(z).start()
        for copy in turn:
            copy.wait()
        turn_add(down_ref, kept, turned)
        share(done - 1).wait_send()
        share(done).wait_send()
        up_copy(done - 1).wait()
        for z in range(4):
            out_copy(z).wait()

        def rims(s, carry):
            for side in range(2):
                rim_copy(s, side).wait()
            return carry

        lax.fori_loop(0, seqs, rims, 0)


def rows_backward(gdl, slope, normed, s_att, w_out, gain_att, w_down, w_up, hid_t, mix_t, downs, seqs):
    total, features = gdl.shape
    ff = w_up.shape[1]
    size = total // seqs
    blocks = total // size
    chunks = ff // features
    here = lambda i: jnp.minimum(i, blocks - 1)
    block = lambda n: pl.BlockSpec((size, n), lambda i: (here(i), 0))
    whole = lambda a: pl.BlockSpec(a.shape, lambda i: (0,) * len(a.shape), pipeline_mode=pl.Buffered(1))
    shape = jax.ShapeDtypeStruct
    down_sum = shape((4, 192, 384), bf16)
    dma = pltpu.SemaphoreType.DMA
    return pl.pallas_call(
        functools.partial(rows_backward_kernel, 2),
        grid=(blocks + chunks + 2,),
        in_specs=[block(features), block(ff), block(features), block(128), whole(w_out), whole(gain_att)] + [ANY] * 5,
        out_specs=[block(features), block(features), pl.BlockSpec((8, features), lambda i: (0, 0)), whole(down_sum)]
        + [ANY] * 2,
        out_shape=[
            shape((total, features), bf16), shape((total, features), bf16), shape((8, features), f32), down_sum,
            shape((4, chunks, 240, 384), bf16), shape((seqs, 2, RIM, features), bf16),
        ],
        scratch_shapes=[
            pltpu.VMEM(w_down.shape, bf16), pltpu.VMEM(w_up.shape, bf16), pltpu.VMEM(hid_t.shape, bf16),
            pltpu.VMEM(mix_t.shape, bf16), dma((4,)), pltpu.VMEM((total, ff), bf16),
            pltpu.VMEM((total, features), bf16), pltpu.VMEM((seqs, 2, RIM, features), bf16),
            pltpu.VMEM((2, 2, 4, 192, 384), bf16), pltpu.VMEM((chunks + 1, 4, 192, 384), bf16),
            pltpu.VMEM((2, 4, 192, 384), bf16),
        ]
        + stage_scratch(192)
        + [dma((chunks + 1,)), dma((chunks + 1,)), dma((2,)), dma((4,)), dma((seqs, 2)), dma((seqs, 2))],
        compiler_params=params(62 * MB, collective_id=4, has_side_effects=True),
        name="rows_backward",
    )(gdl, slope, normed, s_att, w_out, gain_att, w_down, w_up, hid_t, mix_t, downs)


def first_back_step(gm_ref, p_ref, q_ref, mix_ref, kl_of, put_land, put_gq, put_klp):
    features = gm_ref.shape[2]
    masks = group_masks((M, 4 * E), 4, bf16)
    masks_wide = group_masks((M, 4 * E), 4, f32)
    for g in range(features // 256):
        sl = slice(256 * g, 256 * g + 256)
        gm, p = gm_ref[0, :, sl], p_ref[0, sl, :]
        put_land(g, diag_blocks(dot(p, gm), masks_wide).astype(bf16))
        d = dot_nt(block_diag(quad(mix_ref, g), masks), gm)
        parts = []
        for h in range(4):
            pw = p[E * h : E * h + E].astype(f32)
            dh = d[E * h : E * h + E]
            parts.append((pw * (dh - jnp.sum(pw * dh, axis=0, keepdims=True))).astype(bf16))
        gs = jnp.concatenate(parts, axis=0)
        put_gq(g, dot_tn(gs, block_diag(kl_of(sl), masks)).astype(bf16))
        put_klp(g, diag_blocks(dot(gs, q_ref[0, :, sl]), masks_wide))


def first_back_kernel(gm_ref, p_ref, q_ref, mix_ref, kl_ref, land_ref, gq_ref, klp_ref):
    def put_land(g, x):
        for i in range(2):
            land_ref[2 * g + i] = x[:, 128 * i : 128 * i + 128]

    def put_klp(g, x):
        klp_ref[0, :, 256 * g : 256 * g + 256] = x

    def put_gq(g, x):
        gq_ref[0, :, 256 * g : 256 * g + 256] = x

    first_back_step(gm_ref, p_ref, q_ref, mix_ref, lambda sl: kl_ref[0, :, sl], put_land, put_gq, put_klp)


def first_back(gm, probs, q, mixed, k_land):
    seqs, rows, features = q.shape
    pairs = features // 128
    full = pl.BlockSpec((1, rows, features), lambda s: (s, 0, 0))
    land = pl.BlockSpec((1, M, features), lambda s: (s, 0, 0))
    return pl.pallas_call(
        first_back_kernel,
        grid=(seqs,),
        in_specs=[full, pl.BlockSpec((1, features, rows), lambda s: (s, 0, 0)), full, pl.BlockSpec((pairs, M, 128), lambda s: (s, 0, 0)), land],
        out_specs=[pl.BlockSpec((pairs, M, 128), lambda s: (s, 0, 0)), full, land],
        out_shape=[
            jax.ShapeDtypeStruct((seqs * pairs, M, 128), bf16),
            jax.ShapeDtypeStruct(q.shape, bf16),
            jax.ShapeDtypeStruct((seqs, M, features), f32),
        ],
        compiler_params=params(62 * MB),
        name="first_back",
    )(gm, probs, q, mixed, k_land)


def third_back_kernel(w_ref, v_ref, k_ref, gc_ref, gn_ref, gt_ref, ql_ref, gv_ref, gk_ref, qlp_ref):
    features = w_ref.shape[2]
    masks = group_masks((M, 4 * E), 4, bf16)
    masks_wide = group_masks((M, 4 * E), 4, f32)
    for g in range(features // 256):
        sl = slice(256 * g, 256 * g + 256)
        w = w_ref[0, :, sl]
        gn = jnp.concatenate([gn_ref[2 * g], gn_ref[2 * g + 1]], axis=1)
        gt = jnp.concatenate([gt_ref[2 * g, 0:1, :], gt_ref[2 * g + 1, 0:1, :]], axis=1)
        gd = block_diag(gn, masks)
        gs = (w.astype(f32) * (dot_nt(v_ref[0, :, sl], gd) + gt)).astype(bf16)
        gv_ref[0, :, sl] = (dot(w, gd) + gc_ref[0, :, sl].astype(f32)).astype(bf16)
        gk_ref[0, :, sl] = dot(gs, block_diag(ql_ref[0, :, sl], masks)).astype(bf16)
        qlp_ref[0, :, sl] = diag_blocks(dot_tn(gs, k_ref[0, :, sl]), masks_wide)


def third_back(w, v, k, grad_conv, gn, gt, q_land):
    seqs, rows, features = v.shape
    pairs = features // 128
    full = pl.BlockSpec((1, rows, features), lambda s: (s, 0, 0))
    land = pl.BlockSpec((1, M, features), lambda s: (s, 0, 0))
    return pl.pallas_call(
        third_back_kernel,
        grid=(seqs,),
        in_specs=[full] * 4
        + [
            pl.BlockSpec((pairs, M, 128), lambda s: (s, 0, 0)),
            pl.BlockSpec((pairs, 8, 128), lambda s: (s, 0, 0)),
            land,
        ],
        out_specs=[full, full, land],
        out_shape=[jax.ShapeDtypeStruct(v.shape, bf16)] * 2
        + [jax.ShapeDtypeStruct((seqs, M, features), f32)],
        compiler_params=params(62 * MB),
        name="third_back",
    )(w, v, k, grad_conv, gn, gt, q_land)


def last_kernel(tok_ref, gq_ref, gk_ref, gv_ref, qo_ref, ko_ref, proj_ref, w_ref, gt_ref, wg_ref, d, tok_t):
    step = pl.program_id(0)
    seqs = tok_t.shape[1] // tok_ref.shape[1]
    rows, features = tok_ref.shape[1:]
    marks = qo_ref.shape[1]
    seg = rows // marks

    @pl.when(step < seqs)
    def _():
        here = pl.ds(pl.multiple_of(step * rows, rows), rows)
        for part, (core, own) in enumerate(((gq_ref, qo_ref), (gk_ref, ko_ref))):
            for m in range(marks):
                at = pl.ds(pl.multiple_of(step * rows + m * seg, seg), seg)
                x = core[0, m * seg : m * seg + seg, :].astype(f32) + own[0, m : m + 1, :] * (1.0 / seg)
                x = x.astype(bf16)
                if part == 0:
                    x = x * jnp.asarray(0.125, bf16)
                d[at, part * features : part * features + features] = x
        d[here, 2 * features :] = gv_ref[0]
        tok_t[:, here] = tok_ref[0].T
        for c in range(0, rows, 128):
            at = pl.ds(pl.multiple_of(step * rows + c, 128), 128)
            gt_ref[0, c : c + 128, :] = (
                proj_ref[0, c : c + 128, :].astype(f32) + dot_nt(d[at, :], w_ref[...])
            ).astype(bf16)

    @pl.when(step >= seqs)
    def _():
        base = (step - seqs) * features
        for c in range(0, features, 256):
            cols = pl.ds(pl.multiple_of(base + c, 256), 256)
            wg_ref[0, :, c : c + 256] = dot(tok_t[...], d[:, cols]).astype(bf16)


def last_pass(tokens, gq, gk, gv, q_own, k_own, proj, w_qkv):
    seqs, rows, features = tokens.shape
    marks = q_own.shape[1]
    here = lambda i: jnp.minimum(i, seqs - 1)
    full = pl.BlockSpec((1, rows, features), lambda i: (here(i), 0, 0))
    land = pl.BlockSpec((1, marks, features), lambda i: (here(i), 0, 0))
    return pl.pallas_call(
        last_kernel,
        grid=(seqs + 3,),
        in_specs=[full] * 4 + [land] * 2
        + [full, pl.BlockSpec(w_qkv.shape, lambda i: (0, 0), pipeline_mode=pl.Buffered(1))],
        out_specs=[full, pl.BlockSpec((1, features, features), lambda i: (jnp.maximum(i - seqs, 0), 0, 0))],
        out_shape=[
            jax.ShapeDtypeStruct(tokens.shape, bf16),
            jax.ShapeDtypeStruct((3, features, features), bf16),
        ],
        scratch_shapes=[
            pltpu.VMEM((seqs * rows, 3 * features), bf16), pltpu.VMEM((features, seqs * rows), bf16),
        ],
        compiler_params=params(62 * MB),
        name="last_pass",
    )(tokens, gq, gk, gv, q_own, k_own, proj, w_qkv)


def add_pairs(dst, own, start, pairs):
    for i in range(own.shape[0]):
        @pl.when(start + i < pairs)
        def _(i=i):
            dst[start + i] += own[i]


def cross_copies(src, got, sems):
    _, x, y, _, along_x, along_y = cube()
    return [
        remote(src.at[0:2, :, 1 - x], got.at[0], sems.at[0, 0], sems.at[1, 0], along_x),
        remote(src.at[2:4, 1 - y], got.at[1], sems.at[0, 1], sems.at[1, 1], along_y),
    ]


def kept_copies(src, kept, sems):
    _, x, y, _, _, _ = cube()
    return [
        pltpu.make_async_copy(src.at[0:2, :, x], kept.at[0], sems.at[0]),
        pltpu.make_async_copy(src.at[2:4, y], kept.at[1], sems.at[1]),
    ]


def turn_copies(kept, got, sems):
    _, x, y, _, along_x, along_y = cube()
    return [
        remote(kept.at[0, :, 1 - y], got.at[0], sems.at[0, 0], sems.at[1, 0], along_y),
        remote(kept.at[1, :, 1 - x], got.at[1], sems.at[0, 1], sems.at[1, 1], along_x),
    ]


def cross_add(kept, got):
    for half in range(2):
        for rank in range(2):
            kept[half, rank] = add_low(kept[half, rank], got[half, rank])


def turn_add(out, kept, got):
    _, x, y, _, _, _ = cube()
    for half, place in ((0, y), (1, x)):
        for rank in range(2):
            out[2 * half + rank] = add_low(kept[half, rank, place], got[half, rank])


def stage_scratch(rows):
    dma = pltpu.SemaphoreType.DMA
    return [
        pltpu.VMEM((2, 2, 2, rows, 384), bf16), pltpu.VMEM((2, 2, 2, rows, 384), bf16),
        pltpu.VMEM((2, 2, rows, 384), bf16), dma((2,)), dma((2, 2)), dma((2, 2)),
    ]


def first_third(w_ref, v_ref, k_ref, gn_of, gt_of, put_gs, put_qlp):
    features = w_ref.shape[2]
    masks = group_masks((M, 4 * E), 4, bf16)
    masks_wide = group_masks((M, 4 * E), 4, f32)
    for g in range(features // 256):
        sl = slice(256 * g, 256 * g + 256)
        gd = block_diag(jnp.concatenate([gn_of(2 * g), gn_of(2 * g + 1)], axis=1), masks)
        gt = jnp.concatenate([gt_of(2 * g), gt_of(2 * g + 1)], axis=1)
        gs = (w_ref[0, :, sl].astype(f32) * (dot_nt(v_ref[0, :, sl], gd) + gt)).astype(bf16)
        put_gs(g, gs)
        put_qlp(g, diag_blocks(dot_tn(gs, k_ref[0, :, sl]), masks_wide))


def tail_plan(seqs, pairs, blocks):
    tiles = (2, 2, pairs - 4)
    at, step = {}, 0
    for name, count in (
        ("first", seqs), ("conv_a", tiles[0]), ("inverse", 1), ("one", seqs), ("conv_b", tiles[1]), ("q", 1),
        ("conv_c", tiles[2]), ("values", 1), ("v", 1), ("keys", 1), ("k", 1), ("tok", blocks), ("last", 1),
    ):
        at[name] = step
        step += count
    return at, tuple((at[n], c) for n, c in zip(("conv_a", "conv_b", "conv_c"), tiles)), step


def tail_kernel(
    seqs, gm_ref, p_ref, q_ref, mix_ref, ql_ref, kl_ref, cg_ref, rim_ref, cv_ref, f_ref,
    sum_in, mid_in, z_in, zp_in, za_in, zw_in, scale_in, tot_in, alpha_in,
    wts_in, v_ref, k_ref, tok_ref, proj_ref, gain_a_ref, gain_f_ref, wq_in, down_in, up_in,
    gtok_ref, up_out, down_out, out_out, qkv_out, taps_out, ga_out, gf_out,
    sum_ref, mid_ref, z_ref, zp_ref, za_ref, zw_ref, scale_ref, tot_ref, alpha_ref, save_sems,
    d, tok_t, wq_ref, wts_ref, klp, land, land_got, gn, gn_got, gt, gt_low, gt_got, mq, mk, g_acc, dk_acc, kl_low, kl_got,
    qlp, qlow, qgot, pad, facc, taps, tapsg, up_sum, up_got, down_got,
    part, got_a, sum_a, got_b, sum_b, got_c, sum_c, got_z, sm_got, sm_sum,
    kept, crossed, turned, kept_sems, cross_sems, turn_sems,
    load_sem, land_sems, gn_sems, gt_sems, kl_sems, q_sems, zd_sems, ze_sems, zu_sems, zv_sems,
    a_send, a_recv, b_sems, c_sems, zq_send, zq_recv, s_send, s_recv, s_sems,
):
    step = pl.program_id(0)
    last = pl.num_programs(0) - 1
    rows, features = tok_ref.shape[1:]
    pairs = features // 128
    ranks, own = land_got.shape[:2]
    marks = kl_got.shape[2]
    seg = rows // marks
    at, plan, _ = tail_plan(seqs, pairs, d.shape[0] // gtok_ref.shape[0])
    me, _ = seq_place()
    core, x, y, sibling, along_x, along_y = cube()
    cross = cross_copies(up_in, crossed, cross_sems)
    keep = kept_copies(up_in, kept, kept_sems)
    turn = turn_copies(kept, turned, turn_sems)
    load = pltpu.make_async_copy(wq_in, wq_ref, load_sem.at[0])
    saves = [
        pltpu.make_async_copy(a, b, save_sems.at[i])
        for i, (a, b) in enumerate(
            (
                (sum_in, sum_ref), (mid_in, mid_ref), (z_in, z_ref), (zp_in, zp_ref), (za_in, za_ref),
                (zw_in, zw_ref), (scale_in, scale_ref), (tot_in, tot_ref), (alpha_in, alpha_ref),
            )
        )
    ]
    load_wts = pltpu.make_async_copy(wts_in, wts_ref, load_sem.at[1])

    def z_copies(src, dst, first, count, sems):
        span = pl.ds(first, count)
        sends = [
            remote(src.at[peer, span], dst.at[me, span], sems.at[0, o], sems.at[1, o], {"seq": peer})
            for o, peer in seq_peers()
        ]
        return sends, pltpu.make_async_copy(src.at[me, span], dst.at[me, span], sems.at[0, 0])

    downs = [z_copies(down_in, down_got, 0, 96, zd_sems), z_copies(down_in, down_got, 96, 96, ze_sems)]
    ups = [z_copies(up_sum, up_got, 0, 80, zu_sems), z_copies(up_sum, up_got, 80, 160, zv_sems)]

    def mark_copies(src, dst, sems):
        sends = [
            remote(
                src.at[:, pl.ds(peer * marks, marks)], dst.at[me], sems.at[0, o], sems.at[1, o], {"seq": peer}
            )
            for o, peer in seq_peers()
        ]
        return sends, pltpu.make_async_copy(src.at[:, pl.ds(me * marks, marks)], dst.at[me], sems.at[0, 0])

    gn_exchange = [swap_rows(gn, gn_got, gn_sems), swap_rows(gt_low, gt_got, gt_sems)]
    kl_exchange = mark_copies(kl_low, kl_got, kl_sems)
    q_exchange = mark_copies(qlow, qgot, q_sems)

    def a_copy(p, c):
        spot = pl.ds(4 * p + 2 * c, 2)
        return remote(
            part.at[1 - core, spot], got_a.at[spot], a_send.at[2 * p + c], a_recv.at[2 * p + c], sibling
        )

    def b_copies(p):
        return [
            remote(
                sum_a.at[4 * p : 4 * p + 2, :, 1 - x], got_b.at[p, 0], b_sems.at[0, p, 0], b_sems.at[1, p, 0],
                along_x,
            ),
            remote(
                sum_a.at[4 * p + 2 : 4 * p + 4, 1 - y], got_b.at[p, 1], b_sems.at[0, p, 1], b_sems.at[1, p, 1],
                along_y,
            ),
        ]

    def c_copies(p):
        return [
            remote(
                sum_b.at[p, 0, :, 1 - y], got_c.at[p, 0], c_sems.at[0, p, 0], c_sems.at[1, p, 0], along_y
            ),
            remote(
                sum_b.at[p, 1, :, 1 - x], got_c.at[p, 1], c_sems.at[0, p, 1], c_sems.at[1, p, 1], along_x
            ),
        ]

    def zq_copy(group):
        rank, place = group // 3, group % 3
        offset = lax.rem(rank - me + ranks, ranks)
        return rank, remote(
            sum_c.at[group], got_z.at[me, place], zq_send.at[group], zq_recv.at[place, offset], {"seq": rank}
        )

    def stage_b(p):
        for c in range(2):
            a_copy(p, c).wait()
        for yx in range(4):
            sum_a[4 * p : 4 * p + 4, yx // 2, yx % 2] = add_low(
                part[core, 4 * p : 4 * p + 4, yx], got_a[4 * p : 4 * p + 4, yx]
            )
        for copy in b_copies(p):
            copy.start()

    def stage_c(p):
        for copy in b_copies(p):
            copy.wait()
        sum_b[p, 0] = add_low(sum_a[4 * p : 4 * p + 2, :, x], got_b[p, 0])
        sum_b[p, 1] = add_low(sum_a[4 * p + 2 : 4 * p + 4, y], got_b[p, 1])
        for copy in c_copies(p):
            copy.start()

    def stage_z(p):
        for copy in c_copies(p):
            copy.wait()
        sum_c[4 * p : 4 * p + 2] = add_low(sum_b[p, 0, :, y], got_c[p, 0])
        sum_c[4 * p + 2 : 4 * p + 4] = add_low(sum_b[p, 1, :, x], got_c[p, 1])
        for group in range(4 * p, 4 * p + 4):
            rank, copy = zq_copy(group)

            @pl.when(rank != me)
            def _(copy=copy):
                copy.start()

    small_copies = [
        remote(sm_sum.at[i], sm_got.at[i], s_send.at[i], s_recv.at[i], target)
        for i, target in enumerate((sibling, along_x, along_y))
    ]

    def small_spread():
        return [
            remote(sm_sum.at[3], sm_got.at[3 + me], s_sems.at[0, o], s_sems.at[1, o], {"seq": peer})
            for o, peer in seq_peers()
        ]

    def seq_rows(s):
        return pl.ds(pl.multiple_of(s * rows, rows), rows)

    @pl.when(step == 0)
    def _():
        greet([sibling, along_x, along_y])
        for copy in cross + keep:
            copy.start()
        begin(downs[0])
        land[seqs * pairs :] = jnp.zeros_like(land[seqs * pairs :])

    @pl.when(step == 1)
    def _():
        for save in saves:
            save.start()

    @pl.when(step == at["conv_a"])
    def _():
        load_wts.start()
        load.start()

    @pl.when(step < seqs)
    def _():
        def put_land(g, v):
            for i in range(2):
                land[step * pairs + 2 * g + i] = v[:, 128 * i : 128 * i + 128]

        def put_klp(g, v):
            for i in range(2):
                klp[step * pairs + 2 * g + i] = v[:, 128 * i : 128 * i + 128]

        def put_gq(g, v):
            d[seq_rows(step), 256 * g : 256 * g + 256] = v

        first_back_step(gm_ref, p_ref, q_ref, mix_ref, lambda sl: kl_ref[step, :, sl], put_land, put_gq, put_klp)

    @pl.when(step == seqs - 1)
    def _():
        begin(swap_copies(land, land_got, own, land_sems))

    group = pick_tile(step, plan)
    moving = functools.reduce(
        jnp.logical_or, [(step >= first) & (step < first + tiles) for first, tiles in plan]
    )

    @pl.when(moving)
    def _():
        lanes = pl.ds(pl.multiple_of(group * 128, 128), 128)

        def put_taps(v):
            tapsg[0:KW, lanes] = v

        def one_sequence(seq, carry):
            def put(c, v):
                spot = pl.ds(pl.multiple_of(seq * rows + c, 64), 64)
                d[spot, pl.ds(pl.multiple_of(2 * features + group * 128, 128), 128)] = v

            one = pl.ds(seq, 1)
            conv_back_rows(
                seq, seqs, cg_ref.at[one], rim_ref.at[one], cv_ref.at[one], f_ref, put, put_taps, pad, facc, taps
            )
            return carry

        lax.fori_loop(0, seqs, one_sequence, 0)

    @pl.when(step == at["inverse"])
    def _():
        finish(swap_copies(land, land_got, own, land_sems))
        for save in saves:
            save.wait()

        def shared():
            for r in range(ranks):
                gt_low[r] = jnp.concatenate(
                    [gt[r, i, 0:1, :] for i in range(own)] + [jnp.zeros((8 - own, 128), f32)], axis=0
                )
            for pair in gn_exchange:
                begin(pair)

        inverse_back_step(
            land_got, ql_ref, kl_ref, sum_ref, mid_ref, z_ref, zp_ref, za_ref, zw_ref, scale_ref, tot_ref, alpha_ref,
            gn, gt, mq, mk, g_acc, dk_acc, shared,
        )
        add_pairs(klp, mk, me * own, seqs * pairs)
        kl_low[...] = klp[...].astype(bf16)
        begin(kl_exchange)

    @pl.when(step == at["one"])
    def _():
        for copy in cross + keep:
            copy.wait()
        cross_add(kept, crossed)
        for copy in turn:
            copy.start()
        for pair in gn_exchange:
            finish(pair)
        load_wts.wait()

    def gn_of(s):
        def of(i):
            p = s * pairs + i
            return gn_got[p // own, p % own]

        return of

    def land_rows(of):
        total = of(0).astype(f32)
        for r in range(1, ranks):
            total = total + of(r).astype(f32)
        return total * (1.0 / seg)

    @pl.when(step == at["values"])
    def _():
        sm_sum[0, KW:, :] = jnp.zeros_like(sm_sum[0, KW:, :])
        sm_sum[0, :KW, :] = tapsg[:KW]
        sm_sum[0, KW : KW + 1, :] = jnp.sum(gain_a_ref[...], axis=0, keepdims=True)
        sm_sum[0, KW + 1 : KW + 2, :] = jnp.sum(gain_f_ref[...], axis=0, keepdims=True)
        small_copies[0].start()

    for i in range(1, 4):
        @pl.when(step == at["values"] + i)
        def _(i=i):
            small_copies[i - 1].wait()
            sm_sum[i] = sm_sum[i - 1] + sm_got[i - 1]
            if i < 3:
                small_copies[i].start()
            else:
                for copy in small_spread():
                    copy.start()

    @pl.when((step >= at["one"]) & (step < at["one"] + seqs))
    def _():
        s = step - at["one"]

        def gt_of(i):
            p = s * pairs + i
            return gt_got[p // own, pl.ds(p % own, 1), :]

        def put_gs(g, val):
            d[seq_rows(s), features + 256 * g : features + 256 * g + 256] = val

        def put_qlp(g, val):
            for i in range(2):
                qlp[s * pairs + 2 * g + i] = val[:, 128 * i : 128 * i + 128]

        first_third(wts_ref.at[pl.ds(s, 1)], v_ref, k_ref, gn_of(s), gt_of, put_gs, put_qlp)
        tok_t[:, seq_rows(s)] = tok_ref[0].T

    @pl.when(step == at["one"] + seqs - 1)
    def _():
        add_pairs(qlp, mq, me * own, seqs * pairs)
        qlow[...] = qlp[...].astype(bf16)
        begin(q_exchange)

    @pl.when(step == at["q"])
    def _():
        finish(q_exchange)
        for copy in turn:
            copy.wait()
        turn_add(up_sum, kept, turned)
        begin(downs[1])
        begin(ups[0])

        def fill(s, carry):
            for g in range(pairs):
                spread = land_rows(lambda r: qgot[r, s * pairs + g])
                for m in range(marks):
                    spot = pl.ds(pl.multiple_of(s * rows + m * seg, seg), seg)
                    val = d[spot, 128 * g : 128 * g + 128].astype(f32)
                    low = (val + spread[m : m + 1]).astype(bf16) * jnp.asarray(0.125, bf16)
                    d[spot, 128 * g : 128 * g + 128] = low
            return carry

        lax.fori_loop(0, seqs, fill, 0)

    @pl.when(step == at["keys"])
    def _():
        finish(kl_exchange)

    @pl.when(step == at["keys"])
    def _():
        masks = group_masks((M, 4 * E), 4, bf16)

        def keys(s, carry):
            for g in range(features // 256):
                ks = slice(features + 256 * g, features + 256 * g + 256)
                val = dot(d[seq_rows(s), ks], block_diag(ql_ref[s, :, 256 * g : 256 * g + 256], masks))
                for i in range(2):
                    p = s * pairs + 2 * g + i
                    spread = land_rows(lambda r: kl_got[r, p])
                    lane = features + 256 * g + 128 * i
                    for m in range(marks):
                        spot = pl.ds(pl.multiple_of(s * rows + m * seg, seg), seg)
                        d[spot, lane : lane + 128] = (
                            val[m * seg : m * seg + seg, 128 * i : 128 * i + 128] + spread[m : m + 1]
                        ).astype(bf16)
            return carry

        lax.fori_loop(0, seqs, keys, 0)

    @pl.when(step == at["values"])
    def _():
        masks = group_masks((M, 4 * E), 4, bf16)

        def values(s, carry):
            of = gn_of(s)
            for g in range(features // 256):
                gd = block_diag(jnp.concatenate([of(2 * g), of(2 * g + 1)], axis=1), masks)
                vs = slice(2 * features + 256 * g, 2 * features + 256 * g + 256)
                here = seq_rows(s)
                d[here, vs] = (
                    dot(wts_ref[s, :, 256 * g : 256 * g + 256], gd) + d[here, vs].astype(f32)
                ).astype(bf16)
            return carry

        lax.fori_loop(0, seqs, values, 0)

    @pl.when(step == at["tok"])
    def _():
        load.wait()

    for when, stages in (
        (at["conv_c"] + 1, [(stage_b, 0)]),
        (at["values"], [(stage_c, 0)]),
        (at["keys"], [(stage_z, 0)]),
        (at["k"], [(stage_b, 2)]),
    ):
        @pl.when(step == when)
        def _(stages=stages):
            for stage, p in stages:
                stage(p)

    @pl.when(step == at["conv_c"])
    def _():
        begin(ups[1])

    @pl.when((step == at["q"]) | (step == at["k"]) | (step == at["v"]))
    def _():
        p = jnp.where(step == at["q"], 0, jnp.where(step == at["k"], 1, 2))
        for c in range(2):
            cols = pl.ds(pl.multiple_of(p * features + 384 * c, 128), 384)
            low = dot(tok_t[...], d[:, cols]).astype(bf16)
            for i in range(2):
                for dd in range(8):
                    part[dd % 2, 4 * p + 2 * c + i, dd // 2] = fold(
                        low[96 * dd : 96 * dd + 96, 192 * i : 192 * i + 192]
                    )
            a_copy(p, c).start()

    late_stages = {1: [(stage_b, 1)], 2: [(stage_c, 2)], 5: [(stage_c, 1), (stage_z, 2)]}

    @pl.when((step >= at["tok"]) & (step < last))
    def _():
        size = gtok_ref.shape[0] // 2
        for h in range(2):
            for slot, stages in late_stages.items():
                if slot % 2 == h:
                    @pl.when(step == at["tok"] + slot // 2)
                    def _(stages=stages):
                        for stage, p in stages:
                            stage(p)

            spot = pl.ds(pl.multiple_of((step - at["tok"]) * 2 * size + h * size, size), size)
            near = slice(h * size, h * size + size)
            gtok_ref[near, :] = (proj_ref[near, :].astype(f32) + dot_nt(d[spot, :], wq_ref[...])).astype(bf16)

    def unfold(block):
        return jnp.concatenate([block[:, :192], block[:, 192:]], axis=0)

    def rank_sum(got):
        total = got[0].astype(f32)
        for r in range(1, ranks):
            total = total + got[r].astype(f32)
        return total

    @pl.when(step == last)
    def _():
        stage_z(1)
        for copy in small_spread():
            copy.wait()
        sm_got[3 + me] = sm_sum[3]
        small = (sm_got[3] + sm_got[4]) + (sm_got[5] + sm_got[6])
        taps_out[...] = small[:KW]
        ga_out[...] = small[KW : KW + 1].reshape(features)
        gf_out[...] = small[KW + 1 : KW + 2].reshape(features)
        for pair in downs + ups:
            finish(pair)
        down_out[...] = rank_sum(down_got)
        total = rank_sum(up_got)
        up_out[:, :384] = total[:96]
        up_out[:, 384:] = total[96:192]
        out_out[...] = unfold(total[192:240])
        for group in range(12):
            rank, copy = zq_copy(group)

            @pl.when(rank != me)
            def _(copy=copy):
                copy.wait_send()

        for o in range(1, ranks):
            source = lax.rem(me - o + ranks, ranks)
            for place in range(3):
                remote(
                    sum_c.at[0], got_z.at[source, place], zq_send.at[0], zq_recv.at[place, o], {"seq": source}
                ).wait_recv()
        for place in range(3):
            got_z[me, place] = sum_c[3 * me + place]
        qkv_out[...] = jnp.concatenate(
            [unfold(sum(got_z[r, place].astype(f32) for r in range(ranks))) for place in range(3)], axis=1
        )


def tail(
    gm, probs, q, mixed, q_land, k_land, rim, v, taps, saved, weights, k, tokens, proj, gain_a, gain_f, w_qkv, downs, ups
):
    seqs, rows, features = tokens.shape
    ranks = lax.axis_size("seq")
    pairs = features // 128
    count = seqs * pairs
    own = saved[0].shape[0]
    marks = M // ranks
    total = seqs * rows
    size = 512
    blocks = total // size
    at, plan, steps = tail_plan(seqs, pairs, blocks)
    clip = lambda i, name: jnp.clip(i - at[name], 0, seqs - 1)
    tile = lambda i: pick_tile(i, plan)
    by_seq = lambda shape, of: pl.BlockSpec((1,) + shape, lambda i: (of(i), 0, 0))
    head = lambda i: clip(i, "first")
    one = lambda i: clip(i, "one")
    conv_spec = pl.BlockSpec((seqs, rows, 128), lambda i: (0, 0, tile(i)))
    rim_spec = pl.BlockSpec((seqs, 2, RIM, 128), lambda i: (0, 0, 0, tile(i)))
    tap_spec = pl.BlockSpec((KW, 128), lambda i: (0, tile(i)))
    later = pl.BlockSpec((size, features), lambda i: (jnp.clip(i - at["tok"], 0, blocks - 1), 0))
    whole = lambda a: pl.BlockSpec(a.shape, lambda i: (0,) * len(a.shape), pipeline_mode=pl.Buffered(1))
    flat = (rows, features)
    vm = lambda *shape: pltpu.VMEM(shape, bf16)
    wide = lambda *shape: pltpu.VMEM(shape, f32)
    dma = pltpu.SemaphoreType.DMA
    shares = [
        jax.ShapeDtypeStruct(s, f32)
        for s in ((96, 768), (192, 384), (96, 192), (96, 576), (KW, 768), (768,), (768,))
    ]
    return pl.pallas_call(
        functools.partial(tail_kernel, seqs),
        grid=(steps,),
        in_specs=[
            by_seq(flat, head), by_seq((features, rows), head), by_seq(flat, head),
            pl.BlockSpec((pairs, M, 128), lambda i: (head(i), 0, 0)), whole(q_land), whole(k_land),
            conv_spec, rim_spec, conv_spec, tap_spec,
        ]
        + [ANY] * len(saved)
        + [ANY, by_seq(flat, one), by_seq(flat, one), by_seq(flat, one), later]
        + [whole(gain_a), whole(gain_f), ANY, ANY, ANY],
        out_specs=[later] + [whole(a) for a in shares],
        out_shape=[jax.ShapeDtypeStruct((total, features), bf16)] + shares,
        scratch_shapes=[pltpu.VMEM(a.shape, a.dtype) for a in saved]
        + [
            dma((len(saved),)), vm(total, 3 * features), vm(features, total), vm(*w_qkv.shape), vm(*weights.shape), wide(count, M, 128),
            vm(ranks * own, M, 128), vm(ranks, own, M, 128), vm(ranks, own, M, 128), vm(ranks, own, M, 128),
            wide(ranks, own, 8, 128), wide(ranks, 8, 128), wide(ranks, 8, 128), wide(own, M, 128), wide(own, M, 128),
            wide(own, M, 128), wide(own, M, 128), vm(count, M, 128), vm(ranks, count, marks, 128),
            wide(count, M, 128), vm(count, M, 128), vm(ranks, count, marks, 128), wide(rows + 2 * RIM, 128),
            wide(KW * 8, 128), wide(40, 128), wide(40, features), vm(4, 240, 384), vm(ranks, 240, 384),
            vm(ranks, 192, 384),
            vm(2, 12, 4, 48, 384), vm(12, 4, 48, 384), vm(12, 2, 2, 48, 384), vm(3, 2, 2, 2, 48, 384),
            vm(3, 2, 2, 2, 48, 384), vm(3, 2, 2, 48, 384), vm(12, 48, 384), vm(ranks, 3, 48, 384),
            wide(3 + ranks, 40, features), wide(4, 40, features),
        ]
        + stage_scratch(240)
        + [dma((2,))]
        + [rank_sems() for _ in range(9)]
        + [
            dma((6,)), dma((6,)), dma((2, 3, 2)), dma((2, 3, 2)), dma((12,)), dma((3, ranks)), dma((3,)), dma((3,)),
            rank_sems(),
        ],
        compiler_params=params(63 * MB, collective_id=5, has_side_effects=True),
        name="tail",
    )(
        gm, probs, q, mixed, q_land, k_land, gm, rim, v, taps, *saved, weights, v, k, tokens, proj, gain_a, gain_f,
        w_qkv, downs, ups,
    )


def halo(cells, width):
    count = lax.axis_size("seq")
    head, tail = cells[:, :width], cells[:, cells.shape[1] - width :]
    left = lax.ppermute(tail, "seq", [(i, i + 1) for i in range(count - 1)])
    right = lax.ppermute(head, "seq", [(i + 1, i) for i in range(count - 1)])
    return jnp.stack([left, right], axis=1)


def scatter_sum(grad):
    share = lax.psum_scatter(grad, "dp", scatter_dimension=0, tiled=True)
    return lax.psum_scatter(share, "seq", scatter_dimension=1, tiled=True).astype(f32)


def per_device_general(tokens, w_qkv, w_out, w_up, w_down, conv_filter, gain_att, gain_ffn, grad_out):
    seqs, rows, features = tokens.shape
    ranks = lax.axis_size("seq")
    rank = lax.axis_index("seq")
    marks = M // ranks
    ff = w_up.shape[1]
    pairs = seqs * (features // 128)
    own = -(-pairs // ranks)

    def from_pairs(x):
        x = x[:pairs].reshape(seqs, features // 128, M, 128).transpose(0, 2, 1, 3)
        return x.reshape(seqs, M, features)

    def pad_pairs(x):
        return jnp.pad(x, ((0, ranks * own - pairs),) + ((0, 0),) * (x.ndim - 1))

    def exchange(x):
        out = lax.all_to_all(pad_pairs(x), "seq", 0, 0, tiled=True)
        return out.reshape((ranks, own) + x.shape[1:])

    taps = conv_filter
    q, k, v, k_part, q_land, v_rim = project(tokens, w_qkv, marks)
    first_group = 4
    weights, probs, k_land, conv_a, num_parts, stat_parts = scores(
        q, k, v, q_land, k_part, v_rim, taps, own, first_group
    )
    mixed_pairs, conv_b, *saved = inverse(num_parts, stat_parts, q_land, k_land, v, v_rim, taps, first_group)
    mixed = mixed_pairs
    layer_out, proj, gm, wg, gains = row_pass(
        tokens, probs, conv_a, conv_b, mixed, grad_out, w_out, w_up, w_down, gain_att, gain_ffn
    )
    shape3 = (seqs, rows, features)
    gm = gm.reshape(shape3)
    chunks = ff // features
    up_share = scatter_sum(wg[:chunks].transpose(1, 0, 2).reshape(features, ff))
    down_share = scatter_sum(wg[chunks : 2 * chunks].transpose(0, 2, 1).reshape(ff, features))
    out_share = scatter_sum(wg[2 * chunks])
    land_part, gq, k_land_part = first_back(gm, probs, q, mixed, k_land)
    g_rim = halo(gm, RIM)
    land_parts = exchange(land_part)
    grad_conv, taps_grad = conv_back(gm, g_rim, v, taps)
    gn_own, gt_own, mid_q, mid_k = inverse_back(land_parts, q_land, k_land, saved)

    def give_back(x):
        x = x.reshape((ranks * own,) + x.shape[2:])
        return lax.all_to_all(x, "seq", 0, 0, tiled=True)[:pairs]

    grad_values, gk, q_land_part = third_back(
        weights, v, k, grad_conv, give_back(gn_own), give_back(gt_own), q_land
    )

    def place(x):
        full = jnp.zeros((ranks * own, M, 128), f32)
        return from_pairs(lax.dynamic_update_slice_in_dim(full, x, rank * own, 0))

    both = jnp.stack([q_land_part + place(mid_q), k_land_part + place(mid_k)]).astype(bf16)
    both = both.reshape(2, seqs, ranks, marks, features).transpose(2, 0, 1, 3, 4)
    both = lax.all_to_all(both, "seq", 0, 0, tiled=True).astype(f32).sum(0)
    grad_tokens, qkv_grad = last_pass(tokens, gq, gk, grad_values, both[0], both[1], proj.reshape(shape3), w_qkv)
    qkv_share = scatter_sum(qkv_grad.transpose(1, 0, 2).reshape(features, 3 * features))
    gains = gains.reshape(2, 8, features).sum(1)
    small = lax.psum(jnp.concatenate([taps_grad, gains]), ("dp", "seq"))
    return (
        layer_out.reshape(shape3),
        grad_tokens,
        qkv_share,
        out_share,
        up_share,
        down_share,
        small[:KW],
        small[KW],
        small[KW + 1],
    )


def deliver_kernel(*refs):
    count = len(refs) // 2
    for i in range(count):
        if i < 2:
            refs[count + i][...] = refs[i][...]
        else:
            @pl.when(pl.program_id(0) == 0)
            def _(i=i):
                refs[count + i][...] = refs[i][...]


def deliver(*arrays):
    steps = 4
    split = lambda a: pl.BlockSpec((a.shape[0] // steps, a.shape[1]), lambda i: (i, 0))
    whole = lambda a: pl.BlockSpec(a.shape, lambda i: (0,) * len(a.shape))
    specs = [split(a) for a in arrays[:2]] + [whole(a) for a in arrays[2:]]
    return pl.pallas_call(
        deliver_kernel,
        grid=(steps,),
        in_specs=specs,
        out_specs=specs,
        out_shape=[jax.ShapeDtypeStruct(a.shape, a.dtype) for a in arrays],
        compiler_params=params(62 * MB),
        name="deliver",
    )(*arrays)


def per_device(tokens, w_qkv, w_out, w_up, w_down, conv_filter, gain_att, gain_ffn, grad_out):
    seqs, rows, features = tokens.shape
    ranks = lax.axis_size("seq")
    marks = M // ranks
    pairs = seqs * (features // 128)
    own = -(-pairs // ranks)
    taps = conv_filter
    shape3 = (seqs, rows, features)

    q, k, v, weights, probs, q_land, k_land, v_rim, conv_out, mixed, *saved = front(tokens, w_qkv, taps, own)
    layer_out, normed, s_att, gdl, slope, hid_t, mix_t, gain_f, downs = rows_forward(
        tokens, probs, conv_out, mixed, grad_out, w_out, w_up, w_down, gain_att, gain_ffn
    )
    proj, gm, gain_a, downs, ups, g_rim = rows_backward(
        gdl, slope, normed, s_att, w_out, gain_att, w_down, w_up, hid_t, mix_t, downs.reshape(4, 2, 2, 192, 384), seqs
    )
    grad_tokens, up, down, out, qkv, taps_all, gain_att_all, gain_ffn_all = tail(
        gm.reshape(shape3), probs, q, mixed, q_land, k_land, g_rim, v, taps, saved, weights, k, tokens, proj, gain_a,
        gain_f, w_qkv, downs, ups.reshape(4, 2, 2, 240, 384),
    )
    layer_out, grad_tokens, qkv, out, up, down, taps_all, gain_att_all, gain_ffn_all = deliver(
        layer_out, grad_tokens, qkv, out, up, down, taps_all, gain_att_all, gain_ffn_all
    )
    return (
        layer_out.reshape(shape3),
        grad_tokens.reshape(shape3),
        qkv,
        out,
        up,
        down.T,
        taps_all,
        gain_att_all,
        gain_ffn_all,
    )


def solution(mesh):
    placed = (P("dp", "seq", None), P(), P(), P(), P(), P(), P(), P(), P("dp", "seq", None))
    eight_by_four = mesh.shape["dp"] == 8 and mesh.shape["seq"] == 4
    return jax.shard_map(
        per_device if eight_by_four else per_device_general,
        mesh=mesh,
        in_specs=placed,
        out_specs=(
            P("dp", "seq", None),
            P("dp", "seq", None),
            P("dp", "seq"),
            P("dp", "seq"),
            P("dp", "seq"),
            P("dp", "seq"),
            P(),
            P(),
            P(),
        ),
        check_vma=False,
    )
```

```python
import functools

import jax
import jax.numpy as jnp
from jax import lax
from jax.experimental import pallas as pl
from jax.experimental.pallas import tpu as pltpu
from jax.sharding import PartitionSpec as P

H = 12
E = 64
M = 64
KW = 33
RIM = KW // 2
NEWTON = 6

f32 = jnp.float32
bf16 = jnp.bfloat16
epsilon = 1e-05
root_half = 0.7071067811865476
inv_root_two_pi = 0.3989422804014327
MB = 1 << 20

ERFC_P = 0.6
ERFC_C = (0.37028039425845705, 0.14043533559747823, 0.7278464793107866, -0.23856251479455173)
log2_e = 1.4426950408889634


def dot(a, b):
    return lax.dot_general(a, b, (((1,), (0,)), ((), ())), preferred_element_type=f32)


def dot_nt(a, b):
    return lax.dot_general(a, b, (((1,), (1,)), ((), ())), preferred_element_type=f32)


def dot_tn(a, b):
    return lax.dot_general(a, b, (((0,), (0,)), ((), ())), preferred_element_type=f32)


def lane_group(shape):
    return lax.broadcasted_iota(jnp.int32, shape, len(shape) - 1) // E


def group_masks(shape, count, dtype):
    groups = lane_group(shape)
    return [(groups == h).astype(f32).astype(dtype) for h in range(count)]


def block_diag(x, masks):
    return jnp.concatenate([x * m for m in masks], axis=0)


def diag_blocks(n, masks):
    return sum(n[E * h : E * h + E] * m for h, m in enumerate(masks))


def quad(ref, g):
    return jnp.concatenate([ref[2 * g], ref[2 * g + 1]], axis=1)


def params(limit=None, **kw):
    return pltpu.CompilerParams(vmem_limit_bytes=limit, **kw)


MESH = pl.DeviceIdType.MESH
ANY = pl.BlockSpec(memory_space=pl.ANY)


def seq_place():
    return lax.axis_index("seq"), lax.axis_size("seq")


def seq_peers():
    me, count = seq_place()
    return [(o, lax.rem(me + o, count)) for o in range(1, count)]


def greet(extra=()):
    barrier = pltpu.get_barrier_semaphore()
    targets = [{"seq": peer} for _, peer in seq_peers()] + list(extra)
    for target in targets:
        pl.semaphore_signal(barrier, inc=1, device_id=target, device_id_type=MESH)
    pl.semaphore_wait(barrier, len(targets))


def remote(src, dst, send, recv, target):
    return pltpu.make_async_remote_copy(
        src_ref=src, dst_ref=dst, send_sem=send, recv_sem=recv, device_id=target, device_id_type=MESH
    )


def swap_copies(src, dst, own, sems):
    me, count = seq_place()
    copies = [
        remote(src.at[pl.ds(peer * own, own)], dst.at[me], sems.at[0, o], sems.at[1, o], {"seq": peer})
        for o, peer in seq_peers()
    ]
    return copies, pltpu.make_async_copy(src.at[pl.ds(me * own, own)], dst.at[me], sems.at[0, 0])


def spread_copies(src, dst, own, sems):
    me, count = seq_place()
    at = dst.at[pl.ds(me * own, own)]
    copies = [
        remote(src, at, sems.at[0, o], sems.at[1, o], {"seq": peer}) for o, peer in seq_peers()
    ]
    return copies, pltpu.make_async_copy(src, at, sems.at[0, 0])


def begin(pair):
    for copy in pair[0]:
        copy.start()
    pair[1].start()


def finish(pair):
    for copy in pair[0]:
        copy.wait()
    pair[1].wait()


def swap_rows(src, dst, sems):
    me, _ = seq_place()
    copies = [
        remote(src.at[peer], dst.at[me], sems.at[0, o], sems.at[1, o], {"seq": peer}) for o, peer in seq_peers()
    ]
    return copies, pltpu.make_async_copy(src.at[me], dst.at[me], sems.at[0, 0])


def cube():
    d = lax.axis_index("dp")
    core, x, y = d % 2, (d // 2) % 2, d // 4
    return core, x, y, {"dp": d + 1 - 2 * core}, {"dp": d + 2 - 4 * x}, {"dp": d + 4 - 8 * y}


def add_low(a, b):
    return (a.astype(f32) + b.astype(f32)).astype(bf16)


def rank_sems():
    return pltpu.SemaphoreType.DMA((2, lax.axis_size("seq")))


def project_kernel(
    tok_ref, w_ref, q_ref, k_ref, v_ref, kl_ref, land_out, rim_out, land, rim, send, recv, local, rim_send, rim_recv,
    rim_local,
):
    step = pl.program_id(0)
    seqs = pl.num_programs(0)
    me, count = seq_place()
    rows, features = tok_ref.shape[1:]
    marks = land.shape[1]
    seg = rows // marks

    @pl.when(step == 0)
    def _():
        greet()

    x = tok_ref[0]
    for part, out in enumerate((q_ref, k_ref, v_ref)):
        for c in range(0, features, 256):
            p = dot(x, w_ref[:, part * features + c : part * features + c + 256])
            if part == 0:
                p = 0.125 * p
            low = p.astype(bf16)
            out[0, :, c : c + 256] = low
            if part < 2:
                total = low.astype(f32).reshape(marks, seg, 256).sum(1)
                mean = (total * (1.0 / seg)).astype(bf16)
                if part == 0:
                    land[step, :, c : c + 256] = mean
                else:
                    kl_ref[0, :, c : c + 256] = mean
            else:
                rim[step, 0, :, c : c + 256] = low[rows - RIM :]
                rim[step, 1, :, c : c + 256] = low[:RIM]

    def copies(s):
        spot = land_out.at[s, pl.ds(me * marks, marks)]
        sends = [
            remote(land.at[s], spot, send.at[s, o], recv.at[s, o], {"seq": peer}) for o, peer in seq_peers()
        ]
        return sends, pltpu.make_async_copy(land.at[s], spot, local.at[s])

    def rim_copy(s, side):
        there = lax.rem(me + (1 if side == 0 else count - 1), count)
        return remote(
            rim.at[s, side], rim_out.at[s, side], rim_send.at[s, side], rim_recv.at[s, side], {"seq": there}
        )

    begin(copies(step))
    for side in range(2):
        rim_copy(step, side).start()

    @pl.when(step == seqs - 1)
    def _():
        def drain(s, carry):
            finish(copies(s))
            for side in range(2):
                rim_copy(s, side).wait()
            return carry

        lax.fori_loop(0, seqs, drain, 0)


def project(tokens, w_qkv, marks):
    seqs, rows, features = tokens.shape
    ranks = lax.axis_size("seq")
    full = pl.BlockSpec((1, rows, features), lambda s: (s, 0, 0))
    dma = pltpu.SemaphoreType.DMA
    return pl.pallas_call(
        project_kernel,
        grid=(seqs,),
        in_specs=[full, pl.BlockSpec(w_qkv.shape, lambda s: (0, 0), pipeline_mode=pl.Buffered(1))],
        out_specs=[full] * 3 + [pl.BlockSpec((1, marks, features), lambda s: (s, 0, 0))] + [ANY] * 2,
        out_shape=[jax.ShapeDtypeStruct(tokens.shape, bf16)] * 3
        + [
            jax.ShapeDtypeStruct((seqs, marks, features), bf16),
            jax.ShapeDtypeStruct((seqs, M, features), bf16),
            jax.ShapeDtypeStruct((seqs, 2, RIM, features), bf16),
        ],
        scratch_shapes=[
            pltpu.VMEM((seqs, marks, features), bf16), pltpu.VMEM((seqs, 2, RIM, features), bf16),
            dma((seqs, ranks)), dma((seqs, ranks)), dma((seqs,)), dma((seqs, 2)), dma((seqs, 2)), dma((seqs,)),
        ],
        compiler_params=params(62 * MB, collective_id=0, has_side_effects=True),
        name="project",
    )(tokens, w_qkv)


def fill_taps(taps, f_ref):
    taps[0:KW, :] = f_ref[...].astype(f32)


def fill_pad(pad, x_ref, rim_ref):
    rows = x_ref.shape[1]
    me, count = seq_place()
    pad[0:RIM, :] = jnp.where(me > 0, rim_ref[0, 0].astype(f32), 0.0)
    pad[RIM : RIM + rows, :] = x_ref[0].astype(f32)
    pad[RIM + rows : RIM + rows + RIM, :] = jnp.where(me < count - 1, rim_ref[0, 1].astype(f32), 0.0)


def conv_tile(v_ref, rim_ref, taps_ref, o_ref, pad, f_ref):
    rows = v_ref.shape[1]
    fill_pad(pad, v_ref, rim_ref)
    fill_taps(f_ref, taps_ref)
    conv_rows(o_ref, pad, f_ref, rows)


def conv_rows(o_ref, pad, f_ref, rows):
    for c in range(0, rows, 64):
        acc = jnp.zeros((64, 128), f32)
        for j in range(KW):
            acc = acc + f_ref[j : j + 1, :] * pad[c + j : c + j + 64, :]
        o_ref[0, c : c + 64, :] = acc.astype(bf16)


def conv_specs(rows, first_step, first_group, groups):
    at = lambda i: jnp.maximum(i - first_step, 0)
    seq = lambda i: at(i) // groups
    group = lambda i: at(i) % groups
    return (
        pl.BlockSpec((1, rows, 128), lambda i: (seq(i), 0, first_group + group(i))),
        pl.BlockSpec((1, 2, RIM, 128), lambda i: (seq(i), 0, 0, first_group + group(i))),
        pl.BlockSpec((KW, 128), lambda i: (0, first_group + group(i))),
        pl.BlockSpec((1, rows, 128), lambda i: (seq(i), 0, group(i))),
    )


def conv_back_rows(seq, seqs, g_ref, rim_ref, v_ref, taps_ref, put, put_taps, pad, facc, f_ref):
    rows = v_ref.shape[1]
    fill_pad(pad, g_ref, rim_ref)
    fill_taps(f_ref, taps_ref)

    @pl.when(seq == 0)
    def _():
        facc[...] = jnp.zeros_like(facc)

    for c in range(0, rows, 64):
        acc = jnp.zeros((64, 128), f32)
        vals = v_ref[0, c : c + 64, :].astype(f32)
        for j in range(KW):
            moved = pad[c + 2 * RIM - j : c + 2 * RIM - j + 64, :]
            acc = acc + f_ref[j : j + 1, :] * moved
            facc[8 * j : 8 * j + 8, :] += (vals * moved).reshape(8, 8, 128).sum(0)
        put(c, acc.astype(bf16))

    @pl.when(seq == seqs - 1)
    def _():
        put_taps(facc[...].reshape(KW, 8, 128).sum(1))


def conv_back_tile(seq, seqs, g_ref, rim_ref, v_ref, taps_ref, o_ref, gf_ref, pad, facc, f_ref):
    def put(c, v):
        o_ref[0, c : c + 64, :] = v

    def put_taps(v):
        gf_ref[...] = v

    conv_back_rows(seq, seqs, g_ref, rim_ref, v_ref, taps_ref, put, put_taps, pad, facc, f_ref)


def conv_back_kernel(g_ref, rim_ref, v_ref, f_ref, o_ref, gf_ref, pad, facc, taps):
    conv_back_tile(
        pl.program_id(1), pl.num_programs(1), g_ref, rim_ref, v_ref, f_ref, o_ref, gf_ref, pad, facc, taps
    )


def conv_back_specs(rows, seqs, first_step, first_group):
    at = lambda i: jnp.maximum(i - first_step, 0)
    seq = lambda i: at(i) % seqs
    group = lambda i: at(i) // seqs
    return (
        pl.BlockSpec((1, rows, 128), lambda i: (seq(i), 0, first_group + group(i))),
        pl.BlockSpec((1, 2, RIM, 128), lambda i: (seq(i), 0, 0, first_group + group(i))),
        pl.BlockSpec((KW, 128), lambda i: (0, first_group + group(i))),
        pl.BlockSpec((1, rows, 128), lambda i: (seq(i), 0, group(i))),
        pl.BlockSpec((KW, 128), lambda i: (0, group(i))),
    )


def conv_back(g, rim, v, taps):
    seqs, rows, features = v.shape
    sp = lambda n: pl.BlockSpec((1, n, 128), lambda g, s: (s, 0, g))
    fs = pl.BlockSpec((KW, 128), lambda g, s: (0, g))
    return pl.pallas_call(
        conv_back_kernel,
        grid=(features // 128, seqs),
        in_specs=[sp(rows), pl.BlockSpec((1, 2, RIM, 128), lambda g, s: (s, 0, 0, g)), sp(rows), fs],
        out_specs=[sp(rows), fs],
        out_shape=[jax.ShapeDtypeStruct(v.shape, bf16), jax.ShapeDtypeStruct((KW, features), f32)],
        scratch_shapes=[pltpu.VMEM((rows + 2 * RIM, 128), f32), pltpu.VMEM((KW * 8, 128), f32), pltpu.VMEM((40, 128), f32)],
        name="conv_back",
    )(g, rim, v, taps)


def third_score_step(step, k_ref, v_ref, ql_ref, w_ref, num_ref, stat_ref, own):
    features = k_ref.shape[2]
    pairs = features // 128
    masks = group_masks((M, 4 * E), 4, bf16)
    masks_wide = group_masks((M, 4 * E), 4, f32)
    for g in range(features // 256):
        sl = slice(256 * g, 256 * g + 256)
        s3 = dot_nt(k_ref[0, :, sl], block_diag(ql_ref[0, :, sl], masks))
        peak = jnp.max(s3, axis=0, keepdims=True)
        e3 = jnp.exp(s3 - peak)
        total = jnp.sum(e3, axis=0, keepdims=True)
        low = e3.astype(bf16)
        w_ref[0, :, sl] = low
        num = diag_blocks(dot_tn(low, v_ref[0, :, sl]), masks_wide).astype(bf16)
        for i in range(2):
            lanes = slice(128 * i, 128 * i + 128)
            p = step * pairs + 2 * g + i
            num_ref[p] = num[:, lanes]
            stat_ref[p // own, pl.ds(p % own, 1), :] = peak[:, lanes]
            stat_ref[p // own, pl.ds(8 + p % own, 1), :] = total[:, lanes]


def first_score_step(q_ref, kl, p_ref):
    features = q_ref.shape[2]
    masks = group_masks((M, 4 * E), 4, bf16)
    for g in range(features // 256):
        sl = slice(256 * g, 256 * g + 256)
        s1 = dot_nt(block_diag(kl[:, sl], masks), q_ref[0, :, sl])
        for h in range(4):
            x = s1[E * h : E * h + E]
            e1 = jnp.exp(x - jnp.max(x, axis=0, keepdims=True))
            at = 256 * g + E * h
            p_ref[0, at : at + E, :] = (e1 * (1.0 / jnp.sum(e1, axis=0, keepdims=True))).astype(bf16)


def scores_kernel(
    seqs, own, q_ref, k_ref, v_ref, ql_ref, kp_ref, cv_ref, rim_ref, f_ref, w_ref, p_ref, kl_ref, co_ref, num_out,
    stat_out, num, stat, kl, pad, taps, num_sems, stat_sems, kl_sems,
):
    step = pl.program_id(0)
    steps = pl.num_programs(0)
    pairs = q_ref.shape[2] // 128
    marks = kp_ref.shape[1]
    me, _ = seq_place()

    def mark_copies():
        spot = kl.at[:, pl.ds(me * marks, marks)]
        sends = [
            remote(kp_ref, spot, kl_sems.at[0, o], kl_sems.at[1, o], {"seq": peer}) for o, peer in seq_peers()
        ]
        return sends, pltpu.make_async_copy(kp_ref, spot, kl_sems.at[0, 0])

    @pl.when(step == 0)
    def _():
        greet()
        begin(mark_copies())
        stat[...] = jnp.zeros_like(stat)
        if num.shape[0] > seqs * pairs:
            num[seqs * pairs :] = jnp.zeros_like(num[seqs * pairs :])

    @pl.when(step < seqs)
    def _():
        third_score_step(step, k_ref, v_ref, ql_ref, w_ref, num, stat, own)

    @pl.when(step == seqs - 1)
    def _():
        begin(swap_copies(num, num_out, own, num_sems))
        begin(swap_rows(stat, stat_out, stat_sems))

    @pl.when(step == seqs)
    def _():
        finish(mark_copies())
        kl_ref[...] = kl[...]

    @pl.when((step >= seqs) & (step < 2 * seqs))
    def _():
        first_score_step(q_ref, kl[step - seqs], p_ref)

    @pl.when(step >= 2 * seqs)
    def _():
        conv_tile(cv_ref, rim_ref, f_ref, co_ref, pad, taps)

    @pl.when(step == steps - 1)
    def _():
        finish(swap_copies(num, num_out, own, num_sems))
        finish(swap_rows(stat, stat_out, stat_sems))


def scores(q, k, v, q_land, k_part, rim, taps, own, groups):
    seqs, rows, features = q.shape
    marks = k_part.shape[1]
    ranks = lax.axis_size("seq")
    here = lambda i: jnp.minimum(i, seqs - 1)
    then = lambda i: jnp.clip(i - seqs, 0, seqs - 1)
    full = pl.BlockSpec((1, rows, features), lambda i: (here(i), 0, 0))
    next_full = pl.BlockSpec((1, rows, features), lambda i: (then(i), 0, 0))
    whole = lambda a: pl.BlockSpec(a.shape, lambda i: (0,) * len(a.shape), pipeline_mode=pl.Buffered(1))
    k_land = jax.ShapeDtypeStruct((seqs, M, features), bf16)
    cv, rims, ft, co = conv_specs(rows, 2 * seqs, 0, groups)
    return pl.pallas_call(
        functools.partial(scores_kernel, seqs, own),
        grid=(2 * seqs + seqs * groups,),
        in_specs=[
            next_full, full, full, pl.BlockSpec((1, M, features), lambda i: (here(i), 0, 0)), whole(k_part), cv,
            rims, ft,
        ],
        out_specs=[full, pl.BlockSpec((1, features, rows), lambda i: (then(i), 0, 0)), whole(k_land), co, ANY, ANY],
        out_shape=[
            jax.ShapeDtypeStruct(q.shape, bf16),
            jax.ShapeDtypeStruct((seqs, features, rows), bf16),
            k_land,
            jax.ShapeDtypeStruct((seqs, rows, 128 * groups), bf16),
            jax.ShapeDtypeStruct((ranks, own, M, 128), bf16),
            jax.ShapeDtypeStruct((ranks, 16, 128), f32),
        ],
        scratch_shapes=[
            pltpu.VMEM((ranks * own, M, 128), bf16), pltpu.VMEM((ranks, 16, 128), f32),
            pltpu.VMEM((seqs, M, features), bf16), pltpu.VMEM((rows + 2 * RIM, 128), f32),
            pltpu.VMEM((40, 128), f32), rank_sems(), rank_sems(), rank_sems(),
        ],
        compiler_params=params(62 * MB, collective_id=1, has_side_effects=True),
        name="scores",
    )(q, k, v, q_land, k_part, v, rim, taps)


def split(x):
    hi = x.astype(bf16)
    return hi, (x - hi.astype(f32)).astype(bf16)


def stack_parts(xs, axis):
    return jnp.concatenate([part for x in xs for part in split(x)], axis=axis)


def pair_sums(out, count):
    top = lambda i, j: out[128 * i + 64 * j : 128 * i + 64 * j + 64]
    return [
        top(i, 0)[:, :128] + (top(i, 0)[:, 128:] + top(i, 1)[:, :128]) for i in range(count)
    ]


def pair_nn(lefts, right, masks):
    hi, lo = split(right)
    packed = jnp.concatenate([block_diag(hi, masks), block_diag(lo, masks)], axis=1)
    return pair_sums(dot(stack_parts(lefts, 0), packed), len(lefts))


def pair_nt(lefts, right, masks):
    hi, lo = split(right)
    packed = jnp.concatenate([block_diag(hi, masks), block_diag(lo, masks)], axis=0)
    return pair_sums(dot_nt(stack_parts(lefts, 0), packed), len(lefts))


def pair_tn(left, rights, masks_wide):
    out = dot_tn(stack_parts([left], 1), stack_parts(rights, 1))
    results = []
    for i in range(len(rights)):
        full = out[:128, 256 * i : 256 * i + 128] + (
            out[:128, 256 * i + 128 : 256 * i + 256] + out[128:, 256 * i : 256 * i + 128]
        )
        results.append(diag_blocks(full, masks_wide))
    return results


def half_reduce(x, upper, op, fill):
    a = op(jnp.where(upper, fill, x), axis=1, keepdims=True)
    b = op(jnp.where(upper, x, fill), axis=1, keepdims=True)
    return jnp.where(upper, b, a)


def to_column(row, same, upper):
    return half_reduce(jnp.where(same, row, 0.0), upper, jnp.sum, 0.0)


def to_row(col, same):
    return jnp.sum(jnp.where(same, col, 0.0), axis=0, keepdims=True)


def pair_consts():
    lane = lax.broadcasted_iota(jnp.int32, (M, 128), 1)
    row = lax.broadcasted_iota(jnp.int32, (M, 128), 0)
    return lane >= E, row == lane % E, group_masks((M, 128), 2, bf16), group_masks((M, 128), 2, f32)


def own_pair(land_ref, i, own):
    me, _ = seq_place()
    per = land_ref.shape[2] // 128
    p = jnp.minimum(me * own + i, land_ref.shape[0] * per - 1)
    return land_ref[p // per, :, pl.ds(pl.multiple_of((p % per) * 128, 128), 128)]


def inverse_step(
    num_ref, stat_ref, ql_ref, kl_ref, mixed_ref, sum_ref, mid_ref, z_ref, p_ref, a_ref, w_ref,
    scale_ref, tot_ref, alpha_ref,
):
    ranks, own = num_ref.shape[:2]
    upper, same, masks, masks_wide = pair_consts()
    for i in range(own):
        peak = stat_ref[0, i : i + 1, :]
        for r in range(1, ranks):
            peak = jnp.maximum(peak, stat_ref[r, i : i + 1, :])
        total = jnp.zeros((1, 128), f32)
        numer = jnp.zeros((M, 128), f32)
        for r in range(ranks):
            alpha = jnp.exp(stat_ref[r, i : i + 1, :] - peak)
            total = total + alpha * stat_ref[r, 8 + i : 9 + i, :]
            column = to_column(alpha, same, upper)
            alpha_ref[r, i] = column
            numer = numer + column * num_ref[r, i].astype(f32)
        total = to_column(total, same, upper)
        tot_ref[i] = total
        sum_ref[i] = numer / total
        ql, kl = own_pair(ql_ref, i, own), own_pair(kl_ref, i, own)
        s2 = dot_nt(ql, block_diag(kl, masks))
        e2 = jnp.exp(s2 - half_reduce(s2, upper, jnp.max, -jnp.inf))
        middle = e2 / half_reduce(e2, upper, jnp.sum, 0.0)
        mid_ref[i] = middle
        st = dot_nt(kl, block_diag(ql, masks))
        et = jnp.exp(st - jnp.max(st, axis=0, keepdims=True))
        flipped = et / jnp.sum(et, axis=0, keepdims=True)
        column = jnp.sum(middle, axis=0, keepdims=True)
        scale = 1.0 / half_reduce(column, upper[0:1], jnp.max, -jnp.inf)
        scale_ref[i] = jnp.broadcast_to(scale, (8, 128))
        z_ref[0, i] = flipped * scale

    def step(it, carry):
        zs = [z_ref[it, i] for i in range(own)]
        ps = [pair_nn([mid_ref[i]], zs[i], masks)[0] for i in range(own)]
        second = [pair_nn([ps[i], zs[i]], ps[i], masks) for i in range(own)]
        for i in range(own):
            p2, a = second[i]
            w = 7.0 * ps[i] - p2
            p_ref[it, i] = ps[i]
            a_ref[it, i] = a
            w_ref[it, i] = w
            z_ref[it + 1, i] = 0.25 * (13.0 * zs[i] - 15.0 * a + pair_nn([a], w, masks)[0])
        return carry

    lax.fori_loop(0, NEWTON, step, 0)
    for i in range(own):
        mixed_ref[i] = pair_nn([z_ref[NEWTON, i]], sum_ref[i], masks)[0].astype(bf16)


def inverse_kernel(
    num_ref, stat_ref, ql_ref, kl_ref, cv_ref, rim_ref, f_ref, mixed_out, co_ref, sum_ref, mid_ref, z_ref, p_ref,
    a_ref, w_ref, scale_ref, tot_ref, alpha_ref, mixed, pad, taps, sems,
):
    step = pl.program_id(0)
    own = num_ref.shape[1]

    @pl.when(step == 0)
    def _():
        greet()
        inverse_step(
            num_ref, stat_ref, ql_ref, kl_ref, mixed, sum_ref, mid_ref, z_ref, p_ref, a_ref, w_ref, scale_ref,
            tot_ref, alpha_ref,
        )
        begin(spread_copies(mixed, mixed_out, own, sems))

    @pl.when(step > 0)
    def _():
        conv_tile(cv_ref, rim_ref, f_ref, co_ref, pad, taps)

    @pl.when(step == pl.num_programs(0) - 1)
    def _():
        finish(spread_copies(mixed, mixed_out, own, sems))


def inverse(num, stat, q_land, k_land, v, rim, taps, first_group):
    ranks, own = num.shape[:2]
    seqs, rows, features = v.shape
    groups = features // 128 - first_group
    mat = jax.ShapeDtypeStruct((own, M, 128), f32)
    steps = lambda n: jax.ShapeDtypeStruct((n, own, M, 128), f32)
    whole = lambda a: pl.BlockSpec(a.shape, lambda i: (0,) * len(a.shape), pipeline_mode=pl.Buffered(1))
    saved = [
        mat, mat, steps(NEWTON + 1), steps(NEWTON), steps(NEWTON), steps(NEWTON),
        jax.ShapeDtypeStruct((own, 8, 128), f32), mat, steps(ranks),
    ]
    cv, rims, ft, co = conv_specs(rows, 1, first_group, groups)
    return pl.pallas_call(
        inverse_kernel,
        grid=(1 + seqs * groups,),
        in_specs=[whole(num), whole(stat), whole(q_land), whole(k_land), cv, rims, ft],
        out_specs=[ANY, co] + [whole(a) for a in saved],
        out_shape=[
            jax.ShapeDtypeStruct((ranks * own, M, 128), bf16),
            jax.ShapeDtypeStruct((seqs, rows, 128 * groups), bf16),
        ]
        + saved,
        scratch_shapes=[
            pltpu.VMEM((own, M, 128), bf16), pltpu.VMEM((rows + 2 * RIM, 128), f32), pltpu.VMEM((40, 128), f32),
            rank_sems(),
        ],
        compiler_params=params(62 * MB, collective_id=2, has_side_effects=True),
        name="inverse",
    )(num, stat, q_land, k_land, v, rim, taps)


def inverse_back_step(
    land_ref, ql_ref, kl_ref, sum_ref, mid_ref, z_ref, p_ref, a_ref, w_ref, scale_ref, tot_ref,
    alpha_ref, gn_ref, gt_ref, mq_ref, mk_ref, g_ref, dk_ref, shared=lambda: None,
):
    ranks, own = land_ref.shape[:2]
    upper, same, masks, masks_wide = pair_consts()
    for i in range(own):
        land = land_ref[0, i].astype(f32)
        for r in range(1, ranks):
            land = land + land_ref[r, i].astype(f32)
        summary, total = sum_ref[i], tot_ref[i]
        gs = pair_tn(z_ref[NEWTON, i], [land], masks_wide)[0].astype(bf16).astype(f32)
        gn = (gs / total).astype(bf16).astype(f32)
        gt = -half_reduce(gs * summary, upper, jnp.sum, 0.0) / total
        for r in range(ranks):
            gn_ref[r, i] = (alpha_ref[r, i] * gn).astype(bf16)
            gt_ref[r, i] = jnp.broadcast_to(to_row(alpha_ref[r, i] * gt, same), (8, 128))
        g_ref[i] = pair_nt([land], summary, masks)[0]
        dk_ref[i] = jnp.zeros((M, 128), f32)
    shared()

    def step(back, carry):
        it = NEWTON - 1 - back
        gs = [g_ref[i] for i in range(own)]
        das, dws = [], []
        for i in range(own):
            das.append(0.25 * (pair_nt([gs[i]], w_ref[it, i], masks)[0] - 15.0 * gs[i]))
            dws.append(0.25 * pair_tn(a_ref[it, i], [gs[i]], masks_wide)[0])
        dps, parts = [], []
        for i in range(own):
            right = pair_nt([dws[i], das[i]], p_ref[it, i], masks)
            left = pair_tn(p_ref[it, i], [dws[i]], masks_wide)[0]
            dps.append(7.0 * dws[i] - right[0] - left + pair_tn(z_ref[it, i], [das[i]], masks_wide)[0])
            parts.append(3.25 * gs[i] + right[1])
        for i in range(own):
            g_ref[i] = parts[i] + pair_tn(mid_ref[i], [dps[i]], masks_wide)[0]
            dk_ref[i] += pair_nt([dps[i]], z_ref[it, i], masks)[0]
        return carry

    lax.fori_loop(0, NEWTON, step, 0)
    eye = jnp.where(same, 1.0, 0.0).astype(bf16)
    for i in range(own):
        g, middle, scale = g_ref[i], mid_ref[i], scale_ref[i, 0:1, :]
        turned = dot_tn(stack_parts([g], 1), eye)
        turned = diag_blocks(turned[:128] + turned[128:], masks_wide)
        column = jnp.sum(middle, axis=0, keepdims=True)
        top = half_reduce(column, upper[0:1], jnp.max, -jnp.inf)
        hit = jnp.where(column == top, 1.0, 0.0)
        share = hit / half_reduce(hit, upper[0:1], jnp.sum, 0.0)
        d_scale = half_reduce(jnp.sum(turned * middle, axis=0, keepdims=True), upper[0:1], jnp.sum, 0.0)
        dk = dk_ref[i] + turned * scale - share * (d_scale * scale * scale)
        ds = middle * (dk - half_reduce(middle * dk, upper, jnp.sum, 0.0))
        hi, lo = split(ds)
        both = dot(jnp.concatenate([hi, lo], axis=0), block_diag(own_pair(kl_ref, i, own), masks))
        mq_ref[i] = both[:M] + both[M:]
        turned = dot_tn(jnp.concatenate([hi, lo], axis=1), own_pair(ql_ref, i, own))
        mk_ref[i] = diag_blocks(turned[:128] + turned[128:], masks_wide)


def inverse_back(land, q_land, k_land, saved):
    ranks, own = land.shape[:2]
    mat = jax.ShapeDtypeStruct((own, M, 128), f32)
    return pl.pallas_call(
        inverse_back_step,
        out_shape=[
            jax.ShapeDtypeStruct((ranks, own, M, 128), bf16),
            jax.ShapeDtypeStruct((ranks, own, 8, 128), f32), mat, mat,
        ],
        scratch_shapes=[pltpu.VMEM((own, M, 128), f32)] * 2,
        compiler_params=params(62 * MB),
        name="inverse_back",
    )(land, q_land, k_land, *saved)


def pick_tile(step, plan):
    tile = 0
    done = 0
    for first, count in plan:
        tile = tile + jnp.clip(step - first, -1 if done else 0, count - 1) + (1 if done else 0)
        done += count
    return tile


def front_kernel(
    tok_ref, wq_ref, f_ref,
    q_ref, k_ref, v_ref, w_ref, p_ref, ql_out, kl_out, rim_out, conv_ref, mixed_out, sum_ref, mid_ref, z_ref, zp_ref,
    za_ref, zw_ref, scale_ref, tot_ref, alpha_ref,
    land_q, land_k, ql, kl, rim, rims, num, stat, num_got, stat_got, mixed, pad, taps,
    q_sems, k_sems, rim_send, rim_recv, num_sems, stat_sems, mixed_sems, *, plan, at_third, at_first, at_inverse,
):
    step = pl.program_id(0)
    seqs, rows, features = q_ref.shape
    marks = land_q.shape[1]
    seg = rows // marks
    pairs = features // 128
    own = num_got.shape[1]
    me, count = seq_place()

    def mark_copies(src, dst, sems, s):
        spot = dst.at[s, pl.ds(me * marks, marks)]
        sends = [
            remote(src.at[s], spot, sems.at[0, s, o], sems.at[1, s, o], {"seq": peer}) for o, peer in seq_peers()
        ]
        return sends, pltpu.make_async_copy(src.at[s], spot, sems.at[0, s, 0])

    def rim_copy(s, side):
        there = lax.rem(me + (1 if side == 0 else count - 1), count)
        return remote(
            rim.at[s, side], rims.at[s, side], rim_send.at[s, side], rim_recv.at[s, side], {"seq": there}
        )

    def has_next(side):
        return me < count - 1 if side == 0 else me > 0

    @pl.when(step == 0)
    def _():
        rims[...] = jnp.zeros_like(rims)
        greet()
        stat[...] = jnp.zeros_like(stat)
        num[seqs * pairs :] = jnp.zeros_like(num[seqs * pairs :])

    @pl.when(step < seqs)
    def _():
        x = tok_ref[0]
        for part, out in enumerate((q_ref, k_ref, v_ref)):
            for c in range(0, features, 256):
                p = dot(x, wq_ref[:, part * features + c : part * features + c + 256])
                if part == 0:
                    p = 0.125 * p
                low = p.astype(bf16)
                out[step, :, c : c + 256] = low
                if part < 2:
                    total = low.astype(f32).reshape(marks, seg, 256).sum(1)
                    (land_q, land_k)[part][step, :, c : c + 256] = (total * (1.0 / seg)).astype(bf16)
                else:
                    rim[step, 0, :, c : c + 256] = low[rows - RIM :]
                    rim[step, 1, :, c : c + 256] = low[:RIM]
        begin(mark_copies(land_q, ql, q_sems, step))

        @pl.when(step > 0)
        def _():
            for side in range(2):
                @pl.when(has_next(side))
                def _(side=side):
                    rim_copy(step, side).start()

    @pl.when(step == 1)
    def _():
        for side in range(2):
            @pl.when(has_next(side))
            def _(side=side):
                rim_copy(0, side).start()

    @pl.when(step == seqs)
    def _():
        for s in range(seqs):
            begin(mark_copies(land_k, kl, k_sems, s))

    tile = pick_tile(step, plan)
    seq, group = tile // pairs, tile % pairs
    for first, tiles in plan:
        @pl.when((step >= first) & (step < first + tiles))
        def _():
            @pl.when(group == 0)
            def _():
                for side in range(2):
                    @pl.when(has_next(side))
                    def _(side=side):
                        rim_copy(seq, side).wait_send()

                    @pl.when(has_next(1 - side))
                    def _(side=side):
                        rim_copy(seq, side).wait_recv()

            lanes = pl.ds(pl.multiple_of(group * 128, 128), 128)
            taps[0:KW, :] = f_ref[:, lanes].astype(f32)
            pad[0:RIM, :] = rims[seq, 0, :, lanes].astype(f32)
            pad[RIM : RIM + rows, :] = v_ref[seq, :, lanes].astype(f32)
            pad[RIM + rows : RIM + rows + RIM, :] = rims[seq, 1, :, lanes].astype(f32)
            conv_rows(conv_ref, pad, taps, rows)

    @pl.when(step == at_third)
    def _():
        for s in range(seqs):
            finish(mark_copies(land_q, ql, q_sems, s))
        ql_out[...] = ql[...]

    @pl.when((step >= at_third) & (step < at_third + seqs))
    def _():
        s = step - at_third
        third_score_step(s, k_ref.at[pl.ds(s, 1)], v_ref.at[pl.ds(s, 1)], ql.at[pl.ds(s, 1)], w_ref, num, stat, own)

    @pl.when(step == at_third + seqs - 1)
    def _():
        begin(swap_copies(num, num_got, own, num_sems))
        begin(swap_rows(stat, stat_got, stat_sems))

    @pl.when(step == at_first)
    def _():
        for s in range(seqs):
            finish(mark_copies(land_k, kl, k_sems, s))
        kl_out[...] = kl[...]

    @pl.when((step >= at_first) & (step < at_first + seqs))
    def _():
        s = step - at_first
        first_score_step(q_ref.at[pl.ds(s, 1)], kl[s], p_ref)

    @pl.when(step == at_inverse)
    def _():
        finish(swap_copies(num, num_got, own, num_sems))
        finish(swap_rows(stat, stat_got, stat_sems))
        inverse_step(
            num_got, stat_got, ql, kl, mixed, sum_ref, mid_ref, z_ref, zp_ref, za_ref, zw_ref, scale_ref, tot_ref,
            alpha_ref,
        )
        begin(spread_copies(mixed, mixed_out, own, mixed_sems))

    @pl.when(step == pl.num_programs(0) - 1)
    def _():
        finish(spread_copies(mixed, mixed_out, own, mixed_sems))
        rim_out[...] = rims[...]


def front(tokens, w_qkv, taps, own):
    seqs, rows, features = tokens.shape
    ranks = lax.axis_size("seq")
    marks = M // ranks
    pairs = features // 128
    tiles = (4, 5, seqs * pairs - 9)
    third = seqs + tiles[0]
    first = third + seqs + tiles[1]
    at = dict(at_third=third, at_first=first, at_inverse=first + seqs)
    plan = ((seqs, tiles[0]), (third + seqs, tiles[1]), (first + seqs + 1, tiles[2]))
    here = lambda first: (lambda i: jnp.clip(i - first, 0, seqs - 1))
    score, prob = here(at["at_third"]), here(at["at_first"])
    whole = lambda a: pl.BlockSpec(a.shape, lambda i: (0,) * len(a.shape), pipeline_mode=pl.Buffered(1))
    tile = lambda i: pick_tile(i, plan)
    rows_out = jax.ShapeDtypeStruct(tokens.shape, bf16)
    land = jax.ShapeDtypeStruct((seqs, M, features), bf16)
    rim_out = jax.ShapeDtypeStruct((seqs, 2, RIM, features), bf16)
    mat = jax.ShapeDtypeStruct((own, M, 128), f32)
    steps = lambda n: jax.ShapeDtypeStruct((n, own, M, 128), f32)
    saved = [
        mat, mat, steps(NEWTON + 1), steps(NEWTON), steps(NEWTON), steps(NEWTON),
        jax.ShapeDtypeStruct((own, 8, 128), f32), mat, steps(ranks),
    ]
    vm = lambda *shape: pltpu.VMEM(shape, bf16)
    dma = pltpu.SemaphoreType.DMA
    return pl.pallas_call(
        functools.partial(front_kernel, plan=plan, **at),
        grid=(plan[-1][0] + tiles[2],),
        in_specs=[
            pl.BlockSpec((1, rows, features), lambda i: (jnp.minimum(i, seqs - 1), 0, 0)), whole(w_qkv), whole(taps),
        ],
        out_specs=[whole(rows_out)] * 3
        + [
            pl.BlockSpec((1, rows, features), lambda i: (score(i), 0, 0)),
            pl.BlockSpec((1, features, rows), lambda i: (prob(i), 0, 0)),
            whole(land), whole(land), whole(rim_out),
            pl.BlockSpec((1, rows, 128), lambda i: (tile(i) // pairs, 0, tile(i) % pairs)), ANY,
        ]
        + [whole(a) for a in saved],
        out_shape=[rows_out] * 4
        + [
            jax.ShapeDtypeStruct((seqs, features, rows), bf16), land, land, rim_out, rows_out,
            jax.ShapeDtypeStruct((ranks * own, M, 128), bf16),
        ]
        + saved,
        scratch_shapes=[
            vm(seqs, marks, features), vm(seqs, marks, features), vm(seqs, M, features), vm(seqs, M, features),
            vm(seqs, 2, RIM, features), vm(seqs, 2, RIM, features), vm(ranks * own, M, 128),
            pltpu.VMEM((ranks, 16, 128), f32), vm(ranks, own, M, 128), pltpu.VMEM((ranks, 16, 128), f32),
            vm(own, M, 128), pltpu.VMEM((rows + 2 * RIM, 128), f32), pltpu.VMEM((40, 128), f32),
            dma((2, seqs, ranks)), dma((2, seqs, ranks)), dma((seqs, 2)), dma((seqs, 2)), rank_sems(), rank_sems(),
            rank_sems(),
        ],
        compiler_params=params(62 * MB, collective_id=0, has_side_effects=True),
        name="front",
    )(tokens, w_qkv, taps)


def mean_of(x):
    return jnp.mean(x, axis=-1, keepdims=True)


def gelu_and_slope(u):
    u = u.astype(bf16)
    low = lambda c: jnp.asarray(c, bf16)
    t = low(1.0) / (low(1.0) + low(ERFC_P * root_half) * jnp.abs(u))
    bell = jnp.exp2((u * u) * low(-0.5 * log2_e))
    poly = jnp.full_like(t, 0.5 * ERFC_C[-1])
    for c in ERFC_C[-2::-1]:
        poly = poly * t + low(0.5 * c)
    half = (poly * t) * bell
    cdf = jnp.where(u < 0, half, low(1.0) - half)
    return u * cdf, cdf + u * (bell * low(inv_root_two_pi))


def row_block(
    step, tok_ref, p_ref, conv_refs, mix_ref, top_ref, w_out_ref, w_up_ref, w_down_ref, ga_ref,
    gf_ref, out_ref, proj_ref, gm_ref, gains_ref, act, gul, slope, hid_t, gdl_t, mix_t, gpr, resid, whole, ready=lambda i: None,
):
    size, features = tok_ref.shape
    ff = act.shape[1]
    wide = features
    start = pl.multiple_of(step * size, size)
    rows = pl.ds(start, size)
    near = rows if whole else pl.ds(0, size)
    masks = group_masks((M, 4 * E), 4, bf16)
    for g in range(features // 256):
        sl = slice(256 * g, 256 * g + 256)
        att = dot_tn(p_ref[0, sl, :], block_diag(quad(mix_ref, g), masks))
        split_at = conv_refs[0].shape[1]
        ref, lane = (conv_refs[0], 256 * g) if 256 * g < split_at else (conv_refs[1], 256 * g - split_at)
        resid[:, sl] = (att + ref[:, lane : lane + 256].astype(f32)).astype(bf16)
    mixed = resid[...]
    mix_t[:, near] = mixed.T
    residual = tok_ref[...].astype(f32) + dot(mixed, w_out_ref[...])
    centre = residual - mean_of(residual)
    s_att = lax.rsqrt(mean_of(centre * centre) + epsilon)
    normed = centre * s_att
    gain_att = ga_ref[...].reshape(1, features)
    hidden = normed * gain_att
    hid_low = hidden.astype(bf16)
    hid_t[:, rows] = hid_low.T
    down = jnp.zeros((size, features), f32)
    for j in range(0, ff, wide):
        if j == 0:
            ready(0)
        up = dot(hid_low, w_up_ref[:, j : j + wide])
        low, sl = gelu_and_slope(up)
        act[near, j : j + wide] = low
        slope[:, j : j + wide] = sl
        if j == 0:
            ready(1)
        down = down + dot(low, w_down_ref[j : j + wide, :])
    residual_two = hidden + down
    centre_two = residual_two - mean_of(residual_two)
    s_ffn = lax.rsqrt(mean_of(centre_two * centre_two) + epsilon)
    normed_two = centre_two * s_ffn
    gain_ffn = gf_ref[...].reshape(1, features)
    out_ref[...] = (normed_two * gain_ffn).astype(bf16)
    top = top_ref[...].astype(f32)
    gains_ref[8:16, :] += (top * normed_two).reshape(size // 8, 8, features).sum(0)
    g = top * gain_ffn
    grad_two = s_ffn * (g - mean_of(g) - normed_two * mean_of(g * normed_two))
    gdl = grad_two.astype(bf16)
    gdl_t[:, near] = gdl.T
    back = jnp.zeros((size, features), f32)
    for j in range(0, ff, wide):
        gu = dot_nt(gdl, w_down_ref[j : j + wide, :]) * slope[:, j : j + wide].astype(f32)
        low = gu.astype(bf16)
        gul[rows, j : j + wide] = low
        back = back + dot_nt(low, w_up_ref[:, j : j + wide])
    grad_hidden = grad_two + back
    gains_ref[0:8, :] += (grad_hidden * normed).reshape(size // 8, 8, features).sum(0)
    g = grad_hidden * gain_att
    proj = (s_att * (g - mean_of(g) - normed * mean_of(g * normed))).astype(bf16)
    proj_ref[...] = proj
    if whole:
        gpr[rows, :] = proj
    gm_ref[...] = dot_nt(proj, w_out_ref[...]).astype(bf16)


def row_kernel(
    tok_ref, p_ref, conv_a_ref, conv_b_ref, mix_ref, top_ref, w_out_ref, w_up_ref, w_down_ref, ga_ref, gf_ref,
    out_ref, proj_ref, gm_ref, wg_ref, gains_ref,
    act, gul, slope, hid_t, gdl_t, mix_t, gpr, resid,
):
    step = pl.program_id(0)
    size, features = tok_ref.shape
    blocks = act.shape[0] // size
    ff = act.shape[1]
    wide = features

    @pl.when(step == 0)
    def _():
        gains_ref[...] = jnp.zeros_like(gains_ref)

    @pl.when(step < blocks)
    def _():
        row_block(
            step, tok_ref, p_ref, (conv_a_ref, conv_b_ref), mix_ref, top_ref, w_out_ref, w_up_ref, w_down_ref,
            ga_ref, gf_ref, out_ref, proj_ref, gm_ref, gains_ref, act, gul, slope, hid_t, gdl_t, mix_t, gpr,
            resid, True,
        )

    chunks = ff // wide
    for first, left, right in ((0, hid_t, gul), (chunks, gdl_t, act), (2 * chunks, mix_t, gpr)):
        count = chunks if first < 2 * chunks else 1

        @pl.when((step >= blocks + first) & (step < blocks + first + count))
        def _(first=first, left=left, right=right):
            base = (step - blocks - first) * wide
            for c in range(0, wide, 256):
                cols = pl.ds(pl.multiple_of(base + c, 256), 256)
                wg_ref[0, :, c : c + 256] = dot(left[...], right[:, cols]).astype(bf16)


def row_pass(tokens, probs, conv_a, conv_b, mixed, grad_out, w_out, w_up, w_down, gain_att, gain_ffn):
    seqs, rows, features = tokens.shape
    ff = w_up.shape[1]
    size = min(256, rows)
    total = seqs * rows
    blocks = total // size
    grads = 2 * (ff // features) + 1
    here = lambda i: jnp.minimum(i, blocks - 1)
    block = pl.BlockSpec((size, features), lambda i: (here(i), 0))
    whole = lambda a: pl.BlockSpec(a.shape, lambda i: (0,) * a.ndim, pipeline_mode=pl.Buffered(1))
    flat = lambda a: a.reshape(total, a.shape[2])
    part = lambda a: pl.BlockSpec((size, a.shape[2]), lambda i: (here(i), 0))
    gains = [gain_att, gain_ffn]
    row_out = jax.ShapeDtypeStruct((total, features), bf16)
    tall = pltpu.VMEM((features, total), bf16)
    return pl.pallas_call(
        row_kernel,
        grid=(blocks + grads,),
        in_specs=[
            block, pl.BlockSpec((1, features, size), lambda i: (here(i) * size // rows, 0, here(i) % (rows // size))),
            part(conv_a), part(conv_b),
            pl.BlockSpec((features // 128, M, 128), lambda i: (here(i) * size // rows, 0, 0)),
            block, whole(w_out), whole(w_up), whole(w_down), whole(gains[0]), whole(gains[1]),
        ],
        out_specs=[block] * 3
        + [
            pl.BlockSpec((1, features, features), lambda i: (jnp.maximum(i - blocks, 0), 0, 0)),
            pl.BlockSpec((16, features), lambda i: (0, 0)),
        ],
        out_shape=[row_out] * 3
        + [
            jax.ShapeDtypeStruct((grads, features, features), bf16),
            jax.ShapeDtypeStruct((16, features), f32),
        ],
        scratch_shapes=[
            pltpu.VMEM((total, ff), bf16), pltpu.VMEM((total, ff), bf16), pltpu.VMEM((size, ff), bf16),
            tall, tall, tall, pltpu.VMEM((total, features), bf16), pltpu.VMEM((size, features), bf16),
        ],
        compiler_params=params(62 * MB),
        name="row_pass",
    )(flat(tokens), probs, flat(conv_a), flat(conv_b), mixed, flat(grad_out), w_out, w_up, w_down, *gains)


def put_parts(parts, slot, low, c, by_rows):
    for l in range(0, low.shape[1], 128):
        side, lane = (c + l) // 384, (c + l) % 384
        if by_rows:
            for d in range(8):
                parts[slot, d % 2, d // 2, 96 * side : 96 * side + 96, lane : lane + 128] = low[
                    96 * d : 96 * d + 96, l : l + 128
                ]
        else:
            for z in range(4):
                parts[slot, side, z, :, lane : lane + 128] = low[192 * z : 192 * z + 192, l : l + 128]


def fold(block):
    return jnp.concatenate([block[:48], block[48:]], axis=1)


def rows_forward_kernel(
    tok_ref, p_ref, conv_ref, mix_ref, top_ref, w_out_ref, w_up_in, w_down_in, ga_ref, gf_ref,
    out_ref, normed_ref, s_ref, gdl_ref, slope_ref, hid_t_ref, mix_t_ref, gains_ref, g_out,
    w_up_ref, w_down_ref, load_sems, act, gdl_t, mixed_ref, parts, got, sums, send, recv, out_sem,
):
    step = pl.program_id(0)
    size, features = tok_ref.shape
    blocks = act.shape[0] // size
    ff = act.shape[1]
    chunks = ff // features
    core, _, _, sibling, _, _ = cube()
    loads = [
        pltpu.make_async_copy(w_up_in, w_up_ref, load_sems.at[0]),
        pltpu.make_async_copy(w_down_in, w_down_ref, load_sems.at[1]),
    ]

    @pl.when(step == 0)
    def _():
        for load in loads:
            load.start()
        gains_ref[...] = jnp.zeros_like(gains_ref)
        greet([sibling])

    @pl.when(step < blocks)
    def _():
        rows = pl.ds(pl.multiple_of(step * size, size), size)
        masks = group_masks((M, 4 * E), 4, bf16)
        for g in range(features // 256):
            sl = slice(256 * g, 256 * g + 256)
            att = dot_tn(p_ref[0, sl, :], block_diag(quad(mix_ref, g), masks))
            mixed_ref[:, sl] = (att + conv_ref[:, sl].astype(f32)).astype(bf16)
        mixed = mixed_ref[...]
        mix_t_ref[...] = mixed.T
        residual = tok_ref[...].astype(f32) + dot(mixed, w_out_ref[...])
        centre = residual - mean_of(residual)
        s_att = lax.rsqrt(mean_of(centre * centre) + epsilon)
        normed = centre * s_att
        s_ref[...] = jnp.broadcast_to(s_att, s_ref.shape)
        normed_ref[...] = normed.astype(bf16)
        hidden = normed * ga_ref[...].reshape(1, features)
        hid_low = hidden.astype(bf16)
        hid_t_ref[...] = hid_low.T

        @pl.when(step == 0)
        def _():
            for load in loads:
                load.wait()

        down = jnp.zeros((size, features), f32)
        for j in range(0, ff, features):
            low, sl = gelu_and_slope(dot(hid_low, w_up_ref[:, j : j + features]))
            act[rows, j : j + features] = low
            slope_ref[:, j : j + features] = sl
            down = down + dot(low, w_down_ref[j : j + features, :])
        residual_two = hidden + down
        centre_two = residual_two - mean_of(residual_two)
        s_ffn = lax.rsqrt(mean_of(centre_two * centre_two) + epsilon)
        normed_two = centre_two * s_ffn
        gain_ffn = gf_ref[...].reshape(1, features)
        out_ref[...] = (normed_two * gain_ffn).astype(bf16)
        top = top_ref[...].astype(f32)
        gains_ref[...] += (top * normed_two).reshape(size // 8, 8, features).sum(0)
        g = top * gain_ffn
        gdl = (s_ffn * (g - mean_of(g) - normed_two * mean_of(g * normed_two))).astype(bf16)
        gdl_ref[...] = gdl
        gdl_t[:, rows] = gdl.T

    j = step - blocks
    slot = lax.rem(jnp.maximum(j, 0), 2)

    def share(at):
        return remote(parts.at[at % 2, 1 - core], got.at[at], send.at[at], recv.at[at], sibling)

    def out_copy(at):
        return pltpu.make_async_copy(sums.at[at % 2], g_out.at[:, at], out_sem.at[at % 2])

    @pl.when((j >= 2) & (j < chunks))
    def _():
        share(j - 2).wait_send()

    @pl.when((j >= 0) & (j < chunks))
    def _():
        for c in range(0, features, 256):
            cols = pl.ds(pl.multiple_of(j * features + c, 256), 256)
            put_parts(parts, slot, dot(gdl_t[...], act[:, cols]).astype(bf16), c, False)
        share(j).start()

    done = j - 1

    @pl.when(done >= 2)
    def _():
        out_copy(done - 2).wait()

    @pl.when(done >= 0)
    def _():
        share(done).wait_recv()
        sums[done % 2] = add_low(parts[done % 2, core], got[done])
        out_copy(done).start()

    @pl.when(done == chunks - 1)
    def _():
        for at in (done - 1, done):
            share(at).wait_send()
            out_copy(at).wait()


def rows_forward(tokens, probs, conv_out, mixed, grad_out, w_out, w_up, w_down, gain_att, gain_ffn):
    seqs, rows, features = tokens.shape
    ff = w_up.shape[1]
    size = rows
    total = seqs * rows
    blocks = total // size
    chunks = ff // features
    here = lambda i: jnp.minimum(i, blocks - 1)
    block = lambda n: pl.BlockSpec((size, n), lambda i: (here(i), 0))
    turned = pl.BlockSpec((features, size), lambda i: (0, here(i)))
    whole = lambda a: pl.BlockSpec(a.shape, lambda i: (0,) * a.ndim, pipeline_mode=pl.Buffered(1))
    flat = lambda a: a.reshape(total, a.shape[2])
    shape = jax.ShapeDtypeStruct
    dma = pltpu.SemaphoreType.DMA
    return pl.pallas_call(
        rows_forward_kernel,
        grid=(blocks + chunks + 1,),
        in_specs=[
            block(features),
            pl.BlockSpec((1, features, size), lambda i: (here(i) * size // rows, 0, here(i) % (rows // size))),
            block(features), pl.BlockSpec((features // 128, M, 128), lambda i: (here(i) * size // rows, 0, 0)),
            block(features), whole(w_out), ANY, ANY, whole(gain_att), whole(gain_ffn),
        ],
        out_specs=[block(features), block(features), block(128), block(features), block(ff), turned, turned]
        + [pl.BlockSpec((8, features), lambda i: (0, 0)), ANY],
        out_shape=[
            shape((total, features), bf16), shape((total, features), bf16), shape((total, 128), f32),
            shape((total, features), bf16), shape((total, ff), bf16), shape((features, total), bf16),
            shape((features, total), bf16), shape((8, features), f32), shape((4, chunks, 192, 384), bf16),
        ],
        scratch_shapes=[
            pltpu.VMEM(w_up.shape, bf16), pltpu.VMEM(w_down.shape, bf16), dma((2,)), pltpu.VMEM((total, ff), bf16),
            pltpu.VMEM((features, total), bf16), pltpu.VMEM((size, features), bf16),
            pltpu.VMEM((2, 2, 4, 192, 384), bf16), pltpu.VMEM((chunks, 4, 192, 384), bf16),
            pltpu.VMEM((2, 4, 192, 384), bf16), dma((chunks,)), dma((chunks,)), dma((2,)),
        ],
        compiler_params=params(62 * MB, collective_id=3, has_side_effects=True),
        name="rows_forward",
    )(
        flat(tokens), probs, flat(conv_out), mixed, flat(grad_out), w_out, w_up, w_down, gain_att, gain_ffn
    )


def rows_backward_kernel(
    turn_at, gdl_ref, slope_ref, normed_ref, s_ref, w_out_ref, ga_ref, w_down_in, w_up_in, hid_t_in, mix_t_in, down_in,
    proj_ref, gm_ref, gains_ref, down_ref, g_out, rim_out,
    w_down_ref, w_up_ref, hid_t, mix_t, load_sems, gul, gpr, rim, parts, got, sums,
    kept, crossed, turned, kept_sems, cross_sems, turn_sems,
    send, recv, out_sem, last_sem, rim_send, rim_recv,
):
    step = pl.program_id(0)
    size, features = gdl_ref.shape
    ff = gul.shape[1]
    blocks = gul.shape[0] // size
    chunks = ff // features
    seqs = rim.shape[0]
    per = blocks // seqs
    me, count = seq_place()
    core, _, _, sibling, along_x, along_y = cube()
    loads = [
        pltpu.make_async_copy(a, b, load_sems.at[i])
        for i, (a, b) in enumerate(
            ((w_down_in, w_down_ref), (w_up_in, w_up_ref), (hid_t_in, hid_t), (mix_t_in, mix_t))
        )
    ]
    cross = cross_copies(down_in, crossed, cross_sems)
    keep = kept_copies(down_in, kept, kept_sems)
    turn = turn_copies(kept, turned, turn_sems)

    @pl.when(step == 0)
    def _():
        for load in loads[:2]:
            load.start()
        gains_ref[...] = jnp.zeros_like(gains_ref)
        greet([sibling, along_x, along_y])
        for copy in cross + keep:
            copy.start()

    @pl.when(step == 1)
    def _():
        for load in loads[2:]:
            load.start()

    @pl.when(step == turn_at)
    def _():
        for copy in cross + keep:
            copy.wait()
        cross_add(kept, crossed)
        for copy in turn:
            copy.start()

    def rim_copy(s, side):
        there = lax.rem(me + (1 if side == 0 else count - 1), count)
        return remote(
            rim.at[s, side], rim_out.at[s, side], rim_send.at[s, side], rim_recv.at[s, side], {"seq": there}
        )

    @pl.when(step < blocks)
    def _():
        rows = pl.ds(pl.multiple_of(step * size, size), size)

        @pl.when(step == 0)
        def _():
            loads[0].wait()

        gdl = gdl_ref[...]
        back = gdl.astype(f32)
        for j in range(0, ff, features):
            gu = dot_nt(gdl, w_down_ref[j : j + features, :]) * slope_ref[:, j : j + features].astype(f32)
            low = gu.astype(bf16)
            gul[rows, j : j + features] = low
            if j == 0:
                @pl.when(step == 0)
                def _():
                    loads[1].wait()
            back = back + dot_nt(low, w_up_ref[:, j : j + features])
        normed = normed_ref[...].astype(f32)
        gains_ref[...] += (back * normed).reshape(size // 8, 8, features).sum(0)
        g = back * ga_ref[...].reshape(1, features)
        proj = (s_ref[:, 0:1] * (g - mean_of(g) - normed * mean_of(g * normed))).astype(bf16)
        proj_ref[...] = proj
        gpr[rows, :] = proj
        gm_ref[...] = dot_nt(proj, w_out_ref[...]).astype(bf16)
        s = step // per

        @pl.when(step % per == 0)
        def _():
            rim[s, 1] = gm_ref[:RIM, :]
            rim_copy(s, 1).start()

        @pl.when(step % per == per - 1)
        def _():
            rim[s, 0] = gm_ref[size - RIM :, :]
            rim_copy(s, 0).start()

    j = step - blocks
    slot = lax.rem(jnp.maximum(j, 0), 2)

    def share(at):
        return remote(parts.at[at % 2, 1 - core], got.at[at], send.at[at], recv.at[at], sibling)

    def up_copy(at):
        return pltpu.make_async_copy(sums.at[at % 2], g_out.at[at, :, 0:192, :], out_sem.at[at % 2])

    def out_copy(z):
        return pltpu.make_async_copy(
            sums.at[0, :, 48 * z : 48 * z + 48, :], g_out.at[z, :, 192:240, :], last_sem.at[z]
        )

    @pl.when((j >= 2) & (j <= chunks))
    def _():
        share(j - 2).wait_send()

    @pl.when(j == 0)
    def _():
        loads[2].wait()
        loads[3].wait()

    @pl.when((j >= 0) & (j < chunks))
    def _():
        for c in range(0, features, 256):
            cols = pl.ds(pl.multiple_of(j * features + c, 256), 256)
            put_parts(parts, slot, dot(hid_t[...], gul[:, cols]).astype(bf16), c, True)
        share(j).start()

    @pl.when(j == chunks)
    def _():
        for c in range(2):
            low = dot(mix_t[...], gpr[:, 384 * c : 384 * c + 384]).astype(bf16)
            for zz in range(2):
                z = 2 * c + zz
                for d in range(8):
                    parts[slot, d % 2, d // 2, 48 * z : 48 * z + 48, :] = fold(
                        low[96 * d : 96 * d + 96, 192 * zz : 192 * zz + 192]
                    )
        share(j).start()

    done = j - 1

    @pl.when(done >= 2)
    def _():
        up_copy(done - 2).wait()

    @pl.when(done >= 0)
    def _():
        share(done).wait_recv()
        sums[done % 2] = add_low(parts[done % 2, core], got[done])

    @pl.when((done >= 0) & (done < chunks))
    def _():
        up_copy(done).start()

    @pl.when(done == chunks)
    def _():
        for z in range(4):
            out_copy(z).start()
        for copy in turn:
            copy.wait()
        turn_add(down_ref, kept, turned)
        share(done - 1).wait_send()
        share(done).wait_send()
        up_copy(done - 1).wait()
        for z in range(4):
            out_copy(z).wait()

        def rims(s, carry):
            for side in range(2):
                rim_copy(s, side).wait()
            return carry

        lax.fori_loop(0, seqs, rims, 0)


def rows_backward(gdl, slope, normed, s_att, w_out, gain_att, w_down, w_up, hid_t, mix_t, downs, seqs):
    total, features = gdl.shape
    ff = w_up.shape[1]
    size = total // seqs
    blocks = total // size
    chunks = ff // features
    here = lambda i: jnp.minimum(i, blocks - 1)
    block = lambda n: pl.BlockSpec((size, n), lambda i: (here(i), 0))
    whole = lambda a: pl.BlockSpec(a.shape, lambda i: (0,) * len(a.shape), pipeline_mode=pl.Buffered(1))
    shape = jax.ShapeDtypeStruct
    down_sum = shape((4, 192, 384), bf16)
    dma = pltpu.SemaphoreType.DMA
    return pl.pallas_call(
        functools.partial(rows_backward_kernel, 2),
        grid=(blocks + chunks + 2,),
        in_specs=[block(features), block(ff), block(features), block(128), whole(w_out), whole(gain_att)] + [ANY] * 5,
        out_specs=[block(features), block(features), pl.BlockSpec((8, features), lambda i: (0, 0)), whole(down_sum)]
        + [ANY] * 2,
        out_shape=[
            shape((total, features), bf16), shape((total, features), bf16), shape((8, features), f32), down_sum,
            shape((4, chunks, 240, 384), bf16), shape((seqs, 2, RIM, features), bf16),
        ],
        scratch_shapes=[
            pltpu.VMEM(w_down.shape, bf16), pltpu.VMEM(w_up.shape, bf16), pltpu.VMEM(hid_t.shape, bf16),
            pltpu.VMEM(mix_t.shape, bf16), dma((4,)), pltpu.VMEM((total, ff), bf16),
            pltpu.VMEM((total, features), bf16), pltpu.VMEM((seqs, 2, RIM, features), bf16),
            pltpu.VMEM((2, 2, 4, 192, 384), bf16), pltpu.VMEM((chunks + 1, 4, 192, 384), bf16),
            pltpu.VMEM((2, 4, 192, 384), bf16),
        ]
        + stage_scratch(192)
        + [dma((chunks + 1,)), dma((chunks + 1,)), dma((2,)), dma((4,)), dma((seqs, 2)), dma((seqs, 2))],
        compiler_params=params(62 * MB, collective_id=4, has_side_effects=True),
        name="rows_backward",
    )(gdl, slope, normed, s_att, w_out, gain_att, w_down, w_up, hid_t, mix_t, downs)


def first_back_step(gm_ref, p_ref, q_ref, mix_ref, kl_of, put_land, put_gq, put_klp):
    features = gm_ref.shape[2]
    masks = group_masks((M, 4 * E), 4, bf16)
    masks_wide = group_masks((M, 4 * E), 4, f32)
    for g in range(features // 256):
        sl = slice(256 * g, 256 * g + 256)
        gm, p = gm_ref[0, :, sl], p_ref[0, sl, :]
        put_land(g, diag_blocks(dot(p, gm), masks_wide).astype(bf16))
        d = dot_nt(block_diag(quad(mix_ref, g), masks), gm)
        parts = []
        for h in range(4):
            pw = p[E * h : E * h + E].astype(f32)
            dh = d[E * h : E * h + E]
            parts.append((pw * (dh - jnp.sum(pw * dh, axis=0, keepdims=True))).astype(bf16))
        gs = jnp.concatenate(parts, axis=0)
        put_gq(g, dot_tn(gs, block_diag(kl_of(sl), masks)).astype(bf16))
        put_klp(g, diag_blocks(dot(gs, q_ref[0, :, sl]), masks_wide))


def first_back_kernel(gm_ref, p_ref, q_ref, mix_ref, kl_ref, land_ref, gq_ref, klp_ref):
    def put_land(g, x):
        for i in range(2):
            land_ref[2 * g + i] = x[:, 128 * i : 128 * i + 128]

    def put_klp(g, x):
        klp_ref[0, :, 256 * g : 256 * g + 256] = x

    def put_gq(g, x):
        gq_ref[0, :, 256 * g : 256 * g + 256] = x

    first_back_step(gm_ref, p_ref, q_ref, mix_ref, lambda sl: kl_ref[0, :, sl], put_land, put_gq, put_klp)


def first_back(gm, probs, q, mixed, k_land):
    seqs, rows, features = q.shape
    pairs = features // 128
    full = pl.BlockSpec((1, rows, features), lambda s: (s, 0, 0))
    land = pl.BlockSpec((1, M, features), lambda s: (s, 0, 0))
    return pl.pallas_call(
        first_back_kernel,
        grid=(seqs,),
        in_specs=[full, pl.BlockSpec((1, features, rows), lambda s: (s, 0, 0)), full, pl.BlockSpec((pairs, M, 128), lambda s: (s, 0, 0)), land],
        out_specs=[pl.BlockSpec((pairs, M, 128), lambda s: (s, 0, 0)), full, land],
        out_shape=[
            jax.ShapeDtypeStruct((seqs * pairs, M, 128), bf16),
            jax.ShapeDtypeStruct(q.shape, bf16),
            jax.ShapeDtypeStruct((seqs, M, features), f32),
        ],
        compiler_params=params(62 * MB),
        name="first_back",
    )(gm, probs, q, mixed, k_land)


def third_back_kernel(w_ref, v_ref, k_ref, gc_ref, gn_ref, gt_ref, ql_ref, gv_ref, gk_ref, qlp_ref):
    features = w_ref.shape[2]
    masks = group_masks((M, 4 * E), 4, bf16)
    masks_wide = group_masks((M, 4 * E), 4, f32)
    for g in range(features // 256):
        sl = slice(256 * g, 256 * g + 256)
        w = w_ref[0, :, sl]
        gn = jnp.concatenate([gn_ref[2 * g], gn_ref[2 * g + 1]], axis=1)
        gt = jnp.concatenate([gt_ref[2 * g, 0:1, :], gt_ref[2 * g + 1, 0:1, :]], axis=1)
        gd = block_diag(gn, masks)
        gs = (w.astype(f32) * (dot_nt(v_ref[0, :, sl], gd) + gt)).astype(bf16)
        gv_ref[0, :, sl] = (dot(w, gd) + gc_ref[0, :, sl].astype(f32)).astype(bf16)
        gk_ref[0, :, sl] = dot(gs, block_diag(ql_ref[0, :, sl], masks)).astype(bf16)
        qlp_ref[0, :, sl] = diag_blocks(dot_tn(gs, k_ref[0, :, sl]), masks_wide)


def third_back(w, v, k, grad_conv, gn, gt, q_land):
    seqs, rows, features = v.shape
    pairs = features // 128
    full = pl.BlockSpec((1, rows, features), lambda s: (s, 0, 0))
    land = pl.BlockSpec((1, M, features), lambda s: (s, 0, 0))
    return pl.pallas_call(
        third_back_kernel,
        grid=(seqs,),
        in_specs=[full] * 4
        + [
            pl.BlockSpec((pairs, M, 128), lambda s: (s, 0, 0)),
            pl.BlockSpec((pairs, 8, 128), lambda s: (s, 0, 0)),
            land,
        ],
        out_specs=[full, full, land],
        out_shape=[jax.ShapeDtypeStruct(v.shape, bf16)] * 2
        + [jax.ShapeDtypeStruct((seqs, M, features), f32)],
        compiler_params=params(62 * MB),
        name="third_back",
    )(w, v, k, grad_conv, gn, gt, q_land)


def last_kernel(tok_ref, gq_ref, gk_ref, gv_ref, qo_ref, ko_ref, proj_ref, w_ref, gt_ref, wg_ref, d, tok_t):
    step = pl.program_id(0)
    seqs = tok_t.shape[1] // tok_ref.shape[1]
    rows, features = tok_ref.shape[1:]
    marks = qo_ref.shape[1]
    seg = rows // marks

    @pl.when(step < seqs)
    def _():
        here = pl.ds(pl.multiple_of(step * rows, rows), rows)
        for part, (core, own) in enumerate(((gq_ref, qo_ref), (gk_ref, ko_ref))):
            for m in range(marks):
                at = pl.ds(pl.multiple_of(step * rows + m * seg, seg), seg)
                x = core[0, m * seg : m * seg + seg, :].astype(f32) + own[0, m : m + 1, :] * (1.0 / seg)
                x = x.astype(bf16)
                if part == 0:
                    x = x * jnp.asarray(0.125, bf16)
                d[at, part * features : part * features + features] = x
        d[here, 2 * features :] = gv_ref[0]
        tok_t[:, here] = tok_ref[0].T
        for c in range(0, rows, 128):
            at = pl.ds(pl.multiple_of(step * rows + c, 128), 128)
            gt_ref[0, c : c + 128, :] = (
                proj_ref[0, c : c + 128, :].astype(f32) + dot_nt(d[at, :], w_ref[...])
            ).astype(bf16)

    @pl.when(step >= seqs)
    def _():
        base = (step - seqs) * features
        for c in range(0, features, 256):
            cols = pl.ds(pl.multiple_of(base + c, 256), 256)
            wg_ref[0, :, c : c + 256] = dot(tok_t[...], d[:, cols]).astype(bf16)


def last_pass(tokens, gq, gk, gv, q_own, k_own, proj, w_qkv):
    seqs, rows, features = tokens.shape
    marks = q_own.shape[1]
    here = lambda i: jnp.minimum(i, seqs - 1)
    full = pl.BlockSpec((1, rows, features), lambda i: (here(i), 0, 0))
    land = pl.BlockSpec((1, marks, features), lambda i: (here(i), 0, 0))
    return pl.pallas_call(
        last_kernel,
        grid=(seqs + 3,),
        in_specs=[full] * 4 + [land] * 2
        + [full, pl.BlockSpec(w_qkv.shape, lambda i: (0, 0), pipeline_mode=pl.Buffered(1))],
        out_specs=[full, pl.BlockSpec((1, features, features), lambda i: (jnp.maximum(i - seqs, 0), 0, 0))],
        out_shape=[
            jax.ShapeDtypeStruct(tokens.shape, bf16),
            jax.ShapeDtypeStruct((3, features, features), bf16),
        ],
        scratch_shapes=[
            pltpu.VMEM((seqs * rows, 3 * features), bf16), pltpu.VMEM((features, seqs * rows), bf16),
        ],
        compiler_params=params(62 * MB),
        name="last_pass",
    )(tokens, gq, gk, gv, q_own, k_own, proj, w_qkv)


def add_pairs(dst, own, start, pairs):
    for i in range(own.shape[0]):
        @pl.when(start + i < pairs)
        def _(i=i):
            dst[start + i] += own[i]


def cross_copies(src, got, sems):
    _, x, y, _, along_x, along_y = cube()
    return [
        remote(src.at[0:2, :, 1 - x], got.at[0], sems.at[0, 0], sems.at[1, 0], along_x),
        remote(src.at[2:4, 1 - y], got.at[1], sems.at[0, 1], sems.at[1, 1], along_y),
    ]


def kept_copies(src, kept, sems):
    _, x, y, _, _, _ = cube()
    return [
        pltpu.make_async_copy(src.at[0:2, :, x], kept.at[0], sems.at[0]),
        pltpu.make_async_copy(src.at[2:4, y], kept.at[1], sems.at[1]),
    ]


def turn_copies(kept, got, sems):
    _, x, y, _, along_x, along_y = cube()
    return [
        remote(kept.at[0, :, 1 - y], got.at[0], sems.at[0, 0], sems.at[1, 0], along_y),
        remote(kept.at[1, :, 1 - x], got.at[1], sems.at[0, 1], sems.at[1, 1], along_x),
    ]


def cross_add(kept, got):
    for half in range(2):
        for rank in range(2):
            kept[half, rank] = add_low(kept[half, rank], got[half, rank])


def turn_add(out, kept, got):
    _, x, y, _, _, _ = cube()
    for half, place in ((0, y), (1, x)):
        for rank in range(2):
            out[2 * half + rank] = add_low(kept[half, rank, place], got[half, rank])


def stage_scratch(rows):
    dma = pltpu.SemaphoreType.DMA
    return [
        pltpu.VMEM((2, 2, 2, rows, 384), bf16), pltpu.VMEM((2, 2, 2, rows, 384), bf16),
        pltpu.VMEM((2, 2, rows, 384), bf16), dma((2,)), dma((2, 2)), dma((2, 2)),
    ]


def first_third(w_ref, v_ref, k_ref, gn_of, gt_of, put_gs, put_qlp):
    features = w_ref.shape[2]
    masks = group_masks((M, 4 * E), 4, bf16)
    masks_wide = group_masks((M, 4 * E), 4, f32)
    for g in range(features // 256):
        sl = slice(256 * g, 256 * g + 256)
        gd = block_diag(jnp.concatenate([gn_of(2 * g), gn_of(2 * g + 1)], axis=1), masks)
        gt = jnp.concatenate([gt_of(2 * g), gt_of(2 * g + 1)], axis=1)
        gs = (w_ref[0, :, sl].astype(f32) * (dot_nt(v_ref[0, :, sl], gd) + gt)).astype(bf16)
        put_gs(g, gs)
        put_qlp(g, diag_blocks(dot_tn(gs, k_ref[0, :, sl]), masks_wide))


def tail_plan(seqs, pairs, blocks):
    tiles = (2, 2, pairs - 4)
    at, step = {}, 0
    for name, count in (
        ("first", seqs), ("conv_a", tiles[0]), ("inverse", 1), ("one", seqs), ("conv_b", tiles[1]), ("q", 1),
        ("conv_c", tiles[2]), ("values", 1), ("v", 1), ("keys", 1), ("k", 1), ("tok", blocks), ("last", 1),
    ):
        at[name] = step
        step += count
    return at, tuple((at[n], c) for n, c in zip(("conv_a", "conv_b", "conv_c"), tiles)), step


def tail_kernel(
    seqs, gm_ref, p_ref, q_ref, mix_ref, ql_ref, kl_ref, cg_ref, rim_ref, cv_ref, f_ref,
    sum_in, mid_in, z_in, zp_in, za_in, zw_in, scale_in, tot_in, alpha_in,
    wts_in, v_ref, k_ref, tok_ref, proj_ref, gain_a_ref, gain_f_ref, wq_in, down_in, up_in,
    gtok_ref, up_out, down_out, out_out, qkv_out, taps_out, ga_out, gf_out,
    sum_ref, mid_ref, z_ref, zp_ref, za_ref, zw_ref, scale_ref, tot_ref, alpha_ref, save_sems,
    d, tok_t, wq_ref, wts_ref, klp, land, land_got, gn, gn_got, gt, gt_low, gt_got, mq, mk, g_acc, dk_acc, kl_low, kl_got,
    qlp, qlow, qgot, pad, facc, taps, tapsg, up_sum, up_got, down_got,
    part, got_a, sum_a, got_b, sum_b, got_c, sum_c, got_z, sm_got, sm_sum,
    kept, crossed, turned, kept_sems, cross_sems, turn_sems,
    load_sem, land_sems, gn_sems, gt_sems, kl_sems, q_sems, zd_sems, ze_sems, zu_sems, zv_sems,
    a_send, a_recv, b_sems, c_sems, zq_send, zq_recv, s_send, s_recv, s_sems,
):
    step = pl.program_id(0)
    last = pl.num_programs(0) - 1
    rows, features = tok_ref.shape[1:]
    pairs = features // 128
    ranks, own = land_got.shape[:2]
    marks = kl_got.shape[2]
    seg = rows // marks
    at, plan, _ = tail_plan(seqs, pairs, d.shape[0] // gtok_ref.shape[0])
    me, _ = seq_place()
    core, x, y, sibling, along_x, along_y = cube()
    cross = cross_copies(up_in, crossed, cross_sems)
    keep = kept_copies(up_in, kept, kept_sems)
    turn = turn_copies(kept, turned, turn_sems)
    load = pltpu.make_async_copy(wq_in, wq_ref, load_sem.at[0])
    saves = [
        pltpu.make_async_copy(a, b, save_sems.at[i])
        for i, (a, b) in enumerate(
            (
                (sum_in, sum_ref), (mid_in, mid_ref), (z_in, z_ref), (zp_in, zp_ref), (za_in, za_ref),
                (zw_in, zw_ref), (scale_in, scale_ref), (tot_in, tot_ref), (alpha_in, alpha_ref),
            )
        )
    ]
    load_wts = pltpu.make_async_copy(wts_in, wts_ref, load_sem.at[1])

    def z_copies(src, dst, first, count, sems):
        span = pl.ds(first, count)
        sends = [
            remote(src.at[peer, span], dst.at[me, span], sems.at[0, o], sems.at[1, o], {"seq": peer})
            for o, peer in seq_peers()
        ]
        return sends, pltpu.make_async_copy(src.at[me, span], dst.at[me, span], sems.at[0, 0])

    downs = [z_copies(down_in, down_got, 0, 96, zd_sems), z_copies(down_in, down_got, 96, 96, ze_sems)]
    ups = [z_copies(up_sum, up_got, 0, 80, zu_sems), z_copies(up_sum, up_got, 80, 160, zv_sems)]

    def mark_copies(src, dst, sems):
        sends = [
            remote(
                src.at[:, pl.ds(peer * marks, marks)], dst.at[me], sems.at[0, o], sems.at[1, o], {"seq": peer}
            )
            for o, peer in seq_peers()
        ]
        return sends, pltpu.make_async_copy(src.at[:, pl.ds(me * marks, marks)], dst.at[me], sems.at[0, 0])

    gn_exchange = [swap_rows(gn, gn_got, gn_sems), swap_rows(gt_low, gt_got, gt_sems)]
    kl_exchange = mark_copies(kl_low, kl_got, kl_sems)
    q_exchange = mark_copies(qlow, qgot, q_sems)

    def a_copy(p, c):
        spot = pl.ds(4 * p + 2 * c, 2)
        return remote(
            part.at[1 - core, spot], got_a.at[spot], a_send.at[2 * p + c], a_recv.at[2 * p + c], sibling
        )

    def b_copies(p):
        return [
            remote(
                sum_a.at[4 * p : 4 * p + 2, :, 1 - x], got_b.at[p, 0], b_sems.at[0, p, 0], b_sems.at[1, p, 0],
                along_x,
            ),
            remote(
                sum_a.at[4 * p + 2 : 4 * p + 4, 1 - y], got_b.at[p, 1], b_sems.at[0, p, 1], b_sems.at[1, p, 1],
                along_y,
            ),
        ]

    def c_copies(p):
        return [
            remote(
                sum_b.at[p, 0, :, 1 - y], got_c.at[p, 0], c_sems.at[0, p, 0], c_sems.at[1, p, 0], along_y
            ),
            remote(
                sum_b.at[p, 1, :, 1 - x], got_c.at[p, 1], c_sems.at[0, p, 1], c_sems.at[1, p, 1], along_x
            ),
        ]

    def zq_copy(group):
        rank, place = group // 3, group % 3
        offset = lax.rem(rank - me + ranks, ranks)
        return rank, remote(
            sum_c.at[group], got_z.at[me, place], zq_send.at[group], zq_recv.at[place, offset], {"seq": rank}
        )

    def stage_b(p):
        for c in range(2):
            a_copy(p, c).wait()
        for yx in range(4):
            sum_a[4 * p : 4 * p + 4, yx // 2, yx % 2] = add_low(
                part[core, 4 * p : 4 * p + 4, yx], got_a[4 * p : 4 * p + 4, yx]
            )
        for copy in b_copies(p):
            copy.start()

    def stage_c(p):
        for copy in b_copies(p):
            copy.wait()
        sum_b[p, 0] = add_low(sum_a[4 * p : 4 * p + 2, :, x], got_b[p, 0])
        sum_b[p, 1] = add_low(sum_a[4 * p + 2 : 4 * p + 4, y], got_b[p, 1])
        for copy in c_copies(p):
            copy.start()

    def stage_z(p):
        for copy in c_copies(p):
            copy.wait()
        sum_c[4 * p : 4 * p + 2] = add_low(sum_b[p, 0, :, y], got_c[p, 0])
        sum_c[4 * p + 2 : 4 * p + 4] = add_low(sum_b[p, 1, :, x], got_c[p, 1])
        for group in range(4 * p, 4 * p + 4):
            rank, copy = zq_copy(group)

            @pl.when(rank != me)
            def _(copy=copy):
                copy.start()

    small_copies = [
        remote(sm_sum.at[i], sm_got.at[i], s_send.at[i], s_recv.at[i], target)
        for i, target in enumerate((sibling, along_x, along_y))
    ]

    def small_spread():
        return [
            remote(sm_sum.at[3], sm_got.at[3 + me], s_sems.at[0, o], s_sems.at[1, o], {"seq": peer})
            for o, peer in seq_peers()
        ]

    def seq_rows(s):
        return pl.ds(pl.multiple_of(s * rows, rows), rows)

    @pl.when(step == 0)
    def _():
        greet([sibling, along_x, along_y])
        for copy in cross + keep:
            copy.start()
        begin(downs[0])
        land[seqs * pairs :] = jnp.zeros_like(land[seqs * pairs :])

    @pl.when(step == 1)
    def _():
        for save in saves:
            save.start()

    @pl.when(step == at["conv_a"])
    def _():
        load_wts.start()
        load.start()

    @pl.when(step < seqs)
    def _():
        def put_land(g, v):
            for i in range(2):
                land[step * pairs + 2 * g + i] = v[:, 128 * i : 128 * i + 128]

        def put_klp(g, v):
            for i in range(2):
                klp[step * pairs + 2 * g + i] = v[:, 128 * i : 128 * i + 128]

        def put_gq(g, v):
            d[seq_rows(step), 256 * g : 256 * g + 256] = v

        first_back_step(gm_ref, p_ref, q_ref, mix_ref, lambda sl: kl_ref[step, :, sl], put_land, put_gq, put_klp)

    @pl.when(step == seqs - 1)
    def _():
        begin(swap_copies(land, land_got, own, land_sems))

    group = pick_tile(step, plan)
    moving = functools.reduce(
        jnp.logical_or, [(step >= first) & (step < first + tiles) for first, tiles in plan]
    )

    @pl.when(moving)
    def _():
        lanes = pl.ds(pl.multiple_of(group * 128, 128), 128)

        def put_taps(v):
            tapsg[0:KW, lanes] = v

        def one_sequence(seq, carry):
            def put(c, v):
                spot = pl.ds(pl.multiple_of(seq * rows + c, 64), 64)
                d[spot, pl.ds(pl.multiple_of(2 * features + group * 128, 128), 128)] = v

            one = pl.ds(seq, 1)
            conv_back_rows(
                seq, seqs, cg_ref.at[one], rim_ref.at[one], cv_ref.at[one], f_ref, put, put_taps, pad, facc, taps
            )
            return carry

        lax.fori_loop(0, seqs, one_sequence, 0)

    @pl.when(step == at["inverse"])
    def _():
        finish(swap_copies(land, land_got, own, land_sems))
        for save in saves:
            save.wait()

        def shared():
            for r in range(ranks):
                gt_low[r] = jnp.concatenate(
                    [gt[r, i, 0:1, :] for i in range(own)] + [jnp.zeros((8 - own, 128), f32)], axis=0
                )
            for pair in gn_exchange:
                begin(pair)

        inverse_back_step(
            land_got, ql_ref, kl_ref, sum_ref, mid_ref, z_ref, zp_ref, za_ref, zw_ref, scale_ref, tot_ref, alpha_ref,
            gn, gt, mq, mk, g_acc, dk_acc, shared,
        )
        add_pairs(klp, mk, me * own, seqs * pairs)
        kl_low[...] = klp[...].astype(bf16)
        begin(kl_exchange)

    @pl.when(step == at["one"])
    def _():
        for copy in cross + keep:
            copy.wait()
        cross_add(kept, crossed)
        for copy in turn:
            copy.start()
        for pair in gn_exchange:
            finish(pair)
        load_wts.wait()

    def gn_of(s):
        def of(i):
            p = s * pairs + i
            return gn_got[p // own, p % own]

        return of

    def land_rows(of):
        total = of(0).astype(f32)
        for r in range(1, ranks):
            total = total + of(r).astype(f32)
        return total * (1.0 / seg)

    @pl.when(step == at["values"])
    def _():
        sm_sum[0, KW:, :] = jnp.zeros_like(sm_sum[0, KW:, :])
        sm_sum[0, :KW, :] = tapsg[:KW]
        sm_sum[0, KW : KW + 1, :] = jnp.sum(gain_a_ref[...], axis=0, keepdims=True)
        sm_sum[0, KW + 1 : KW + 2, :] = jnp.sum(gain_f_ref[...], axis=0, keepdims=True)
        small_copies[0].start()

    for i in range(1, 4):
        @pl.when(step == at["values"] + i)
        def _(i=i):
            small_copies[i - 1].wait()
            sm_sum[i] = sm_sum[i - 1] + sm_got[i - 1]
            if i < 3:
                small_copies[i].start()
            else:
                for copy in small_spread():
                    copy.start()

    @pl.when((step >= at["one"]) & (step < at["one"] + seqs))
    def _():
        s = step - at["one"]

        def gt_of(i):
            p = s * pairs + i
            return gt_got[p // own, pl.ds(p % own, 1), :]

        def put_gs(g, val):
            d[seq_rows(s), features + 256 * g : features + 256 * g + 256] = val

        def put_qlp(g, val):
            for i in range(2):
                qlp[s * pairs + 2 * g + i] = val[:, 128 * i : 128 * i + 128]

        first_third(wts_ref.at[pl.ds(s, 1)], v_ref, k_ref, gn_of(s), gt_of, put_gs, put_qlp)
        tok_t[:, seq_rows(s)] = tok_ref[0].T

    @pl.when(step == at["one"] + seqs - 1)
    def _():
        add_pairs(qlp, mq, me * own, seqs * pairs)
        qlow[...] = qlp[...].astype(bf16)
        begin(q_exchange)

    @pl.when(step == at["q"])
    def _():
        finish(q_exchange)
        for copy in turn:
            copy.wait()
        turn_add(up_sum, kept, turned)
        begin(downs[1])
        begin(ups[0])

        def fill(s, carry):
            for g in range(pairs):
                spread = land_rows(lambda r: qgot[r, s * pairs + g])
                for m in range(marks):
                    spot = pl.ds(pl.multiple_of(s * rows + m * seg, seg), seg)
                    val = d[spot, 128 * g : 128 * g + 128].astype(f32)
                    low = (val + spread[m : m + 1]).astype(bf16) * jnp.asarray(0.125, bf16)
                    d[spot, 128 * g : 128 * g + 128] = low
            return carry

        lax.fori_loop(0, seqs, fill, 0)

    @pl.when(step == at["keys"])
    def _():
        finish(kl_exchange)

    @pl.when(step == at["keys"])
    def _():
        masks = group_masks((M, 4 * E), 4, bf16)

        def keys(s, carry):
            for g in range(features // 256):
                ks = slice(features + 256 * g, features + 256 * g + 256)
                val = dot(d[seq_rows(s), ks], block_diag(ql_ref[s, :, 256 * g : 256 * g + 256], masks))
                for i in range(2):
                    p = s * pairs + 2 * g + i
                    spread = land_rows(lambda r: kl_got[r, p])
                    lane = features + 256 * g + 128 * i
                    for m in range(marks):
                        spot = pl.ds(pl.multiple_of(s * rows + m * seg, seg), seg)
                        d[spot, lane : lane + 128] = (
                            val[m * seg : m * seg + seg, 128 * i : 128 * i + 128] + spread[m : m + 1]
                        ).astype(bf16)
            return carry

        lax.fori_loop(0, seqs, keys, 0)

    @pl.when(step == at["values"])
    def _():
        masks = group_masks((M, 4 * E), 4, bf16)

        def values(s, carry):
            of = gn_of(s)
            for g in range(features // 256):
                gd = block_diag(jnp.concatenate([of(2 * g), of(2 * g + 1)], axis=1), masks)
                vs = slice(2 * features + 256 * g, 2 * features + 256 * g + 256)
                here = seq_rows(s)
                d[here, vs] = (
                    dot(wts_ref[s, :, 256 * g : 256 * g + 256], gd) + d[here, vs].astype(f32)
                ).astype(bf16)
            return carry

        lax.fori_loop(0, seqs, values, 0)

    @pl.when(step == at["tok"])
    def _():
        load.wait()

    for when, stages in (
        (at["conv_c"] + 1, [(stage_b, 0)]),
        (at["values"], [(stage_c, 0)]),
        (at["keys"], [(stage_z, 0)]),
        (at["k"], [(stage_b, 2)]),
    ):
        @pl.when(step == when)
        def _(stages=stages):
            for stage, p in stages:
                stage(p)

    @pl.when(step == at["conv_c"])
    def _():
        begin(ups[1])

    @pl.when((step == at["q"]) | (step == at["k"]) | (step == at["v"]))
    def _():
        p = jnp.where(step == at["q"], 0, jnp.where(step == at["k"], 1, 2))
        for c in range(2):
            cols = pl.ds(pl.multiple_of(p * features + 384 * c, 128), 384)
            low = dot(tok_t[...], d[:, cols]).astype(bf16)
            for i in range(2):
                for dd in range(8):
                    part[dd % 2, 4 * p + 2 * c + i, dd // 2] = fold(
                        low[96 * dd : 96 * dd + 96, 192 * i : 192 * i + 192]
                    )
            a_copy(p, c).start()

    late_stages = {1: [(stage_b, 1)], 2: [(stage_c, 2)], 5: [(stage_c, 1), (stage_z, 2)]}

    @pl.when((step >= at["tok"]) & (step < last))
    def _():
        size = gtok_ref.shape[0] // 2
        for h in range(2):
            for slot, stages in late_stages.items():
                if slot % 2 == h:
                    @pl.when(step == at["tok"] + slot // 2)
                    def _(stages=stages):
                        for stage, p in stages:
                            stage(p)

            spot = pl.ds(pl.multiple_of((step - at["tok"]) * 2 * size + h * size, size), size)
            near = slice(h * size, h * size + size)
            gtok_ref[near, :] = (proj_ref[near, :].astype(f32) + dot_nt(d[spot, :], wq_ref[...])).astype(bf16)

    def unfold(block):
        return jnp.concatenate([block[:, :192], block[:, 192:]], axis=0)

    def rank_sum(got):
        total = got[0].astype(f32)
        for r in range(1, ranks):
            total = total + got[r].astype(f32)
        return total

    @pl.when(step == last)
    def _():
        stage_z(1)
        for copy in small_spread():
            copy.wait()
        sm_got[3 + me] = sm_sum[3]
        small = (sm_got[3] + sm_got[4]) + (sm_got[5] + sm_got[6])
        taps_out[...] = small[:KW]
        ga_out[...] = small[KW : KW + 1].reshape(features)
        gf_out[...] = small[KW + 1 : KW + 2].reshape(features)
        for pair in downs + ups:
            finish(pair)
        down_out[...] = rank_sum(down_got)
        total = rank_sum(up_got)
        up_out[:, :384] = total[:96]
        up_out[:, 384:] = total[96:192]
        out_out[...] = unfold(total[192:240])
        for group in range(12):
            rank, copy = zq_copy(group)

            @pl.when(rank != me)
            def _(copy=copy):
                copy.wait_send()

        for o in range(1, ranks):
            source = lax.rem(me - o + ranks, ranks)
            for place in range(3):
                remote(
                    sum_c.at[0], got_z.at[source, place], zq_send.at[0], zq_recv.at[place, o], {"seq": source}
                ).wait_recv()
        for place in range(3):
            got_z[me, place] = sum_c[3 * me + place]
        qkv_out[...] = jnp.concatenate(
            [unfold(sum(got_z[r, place].astype(f32) for r in range(ranks))) for place in range(3)], axis=1
        )


def tail(
    gm, probs, q, mixed, q_land, k_land, rim, v, taps, saved, weights, k, tokens, proj, gain_a, gain_f, w_qkv, downs, ups
):
    seqs, rows, features = tokens.shape
    ranks = lax.axis_size("seq")
    pairs = features // 128
    count = seqs * pairs
    own = saved[0].shape[0]
    marks = M // ranks
    total = seqs * rows
    size = 512
    blocks = total // size
    at, plan, steps = tail_plan(seqs, pairs, blocks)
    clip = lambda i, name: jnp.clip(i - at[name], 0, seqs - 1)
    tile = lambda i: pick_tile(i, plan)
    by_seq = lambda shape, of: pl.BlockSpec((1,) + shape, lambda i: (of(i), 0, 0))
    head = lambda i: clip(i, "first")
    one = lambda i: clip(i, "one")
    conv_spec = pl.BlockSpec((seqs, rows, 128), lambda i: (0, 0, tile(i)))
    rim_spec = pl.BlockSpec((seqs, 2, RIM, 128), lambda i: (0, 0, 0, tile(i)))
    tap_spec = pl.BlockSpec((KW, 128), lambda i: (0, tile(i)))
    later = pl.BlockSpec((size, features), lambda i: (jnp.clip(i - at["tok"], 0, blocks - 1), 0))
    whole = lambda a: pl.BlockSpec(a.shape, lambda i: (0,) * len(a.shape), pipeline_mode=pl.Buffered(1))
    flat = (rows, features)
    vm = lambda *shape: pltpu.VMEM(shape, bf16)
    wide = lambda *shape: pltpu.VMEM(shape, f32)
    dma = pltpu.SemaphoreType.DMA
    shares = [
        jax.ShapeDtypeStruct(s, f32)
        for s in ((96, 768), (192, 384), (96, 192), (96, 576), (KW, 768), (768,), (768,))
    ]
    return pl.pallas_call(
        functools.partial(tail_kernel, seqs),
        grid=(steps,),
        in_specs=[
            by_seq(flat, head), by_seq((features, rows), head), by_seq(flat, head),
            pl.BlockSpec((pairs, M, 128), lambda i: (head(i), 0, 0)), whole(q_land), whole(k_land),
            conv_spec, rim_spec, conv_spec, tap_spec,
        ]
        + [ANY] * len(saved)
        + [ANY, by_seq(flat, one), by_seq(flat, one), by_seq(flat, one), later]
        + [whole(gain_a), whole(gain_f), ANY, ANY, ANY],
        out_specs=[later] + [whole(a) for a in shares],
        out_shape=[jax.ShapeDtypeStruct((total, features), bf16)] + shares,
        scratch_shapes=[pltpu.VMEM(a.shape, a.dtype) for a in saved]
        + [
            dma((len(saved),)), vm(total, 3 * features), vm(features, total), vm(*w_qkv.shape), vm(*weights.shape), wide(count, M, 128),
            vm(ranks * own, M, 128), vm(ranks, own, M, 128), vm(ranks, own, M, 128), vm(ranks, own, M, 128),
            wide(ranks, own, 8, 128), wide(ranks, 8, 128), wide(ranks, 8, 128), wide(own, M, 128), wide(own, M, 128),
            wide(own, M, 128), wide(own, M, 128), vm(count, M, 128), vm(ranks, count, marks, 128),
            wide(count, M, 128), vm(count, M, 128), vm(ranks, count, marks, 128), wide(rows + 2 * RIM, 128),
            wide(KW * 8, 128), wide(40, 128), wide(40, features), vm(4, 240, 384), vm(ranks, 240, 384),
            vm(ranks, 192, 384),
            vm(2, 12, 4, 48, 384), vm(12, 4, 48, 384), vm(12, 2, 2, 48, 384), vm(3, 2, 2, 2, 48, 384),
            vm(3, 2, 2, 2, 48, 384), vm(3, 2, 2, 48, 384), vm(12, 48, 384), vm(ranks, 3, 48, 384),
            wide(3 + ranks, 40, features), wide(4, 40, features),
        ]
        + stage_scratch(240)
        + [dma((2,))]
        + [rank_sems() for _ in range(9)]
        + [
            dma((6,)), dma((6,)), dma((2, 3, 2)), dma((2, 3, 2)), dma((12,)), dma((3, ranks)), dma((3,)), dma((3,)),
            rank_sems(),
        ],
        compiler_params=params(63 * MB, collective_id=5, has_side_effects=True),
        name="tail",
    )(
        gm, probs, q, mixed, q_land, k_land, gm, rim, v, taps, *saved, weights, v, k, tokens, proj, gain_a, gain_f,
        w_qkv, downs, ups,
    )


def halo(cells, width):
    count = lax.axis_size("seq")
    head, tail = cells[:, :width], cells[:, cells.shape[1] - width :]
    left = lax.ppermute(tail, "seq", [(i, i + 1) for i in range(count - 1)])
    right = lax.ppermute(head, "seq", [(i + 1, i) for i in range(count - 1)])
    return jnp.stack([left, right], axis=1)


def scatter_sum(grad):
    share = lax.psum_scatter(grad, "dp", scatter_dimension=0, tiled=True)
    return lax.psum_scatter(share, "seq", scatter_dimension=1, tiled=True).astype(f32)


def per_device_general(tokens, w_qkv, w_out, w_up, w_down, conv_filter, gain_att, gain_ffn, grad_out):
    seqs, rows, features = tokens.shape
    ranks = lax.axis_size("seq")
    rank = lax.axis_index("seq")
    marks = M // ranks
    ff = w_up.shape[1]
    pairs = seqs * (features // 128)
    own = -(-pairs // ranks)

    def from_pairs(x):
        x = x[:pairs].reshape(seqs, features // 128, M, 128).transpose(0, 2, 1, 3)
        return x.reshape(seqs, M, features)

    def pad_pairs(x):
        return jnp.pad(x, ((0, ranks * own - pairs),) + ((0, 0),) * (x.ndim - 1))

    def exchange(x):
        out = lax.all_to_all(pad_pairs(x), "seq", 0, 0, tiled=True)
        return out.reshape((ranks, own) + x.shape[1:])

    taps = conv_filter
    q, k, v, k_part, q_land, v_rim = project(tokens, w_qkv, marks)
    first_group = 4
    weights, probs, k_land, conv_a, num_parts, stat_parts = scores(
        q, k, v, q_land, k_part, v_rim, taps, own, first_group
    )
    mixed_pairs, conv_b, *saved = inverse(num_parts, stat_parts, q_land, k_land, v, v_rim, taps, first_group)
    mixed = mixed_pairs
    layer_out, proj, gm, wg, gains = row_pass(
        tokens, probs, conv_a, conv_b, mixed, grad_out, w_out, w_up, w_down, gain_att, gain_ffn
    )
    shape3 = (seqs, rows, features)
    gm = gm.reshape(shape3)
    chunks = ff // features
    up_share = scatter_sum(wg[:chunks].transpose(1, 0, 2).reshape(features, ff))
    down_share = scatter_sum(wg[chunks : 2 * chunks].transpose(0, 2, 1).reshape(ff, features))
    out_share = scatter_sum(wg[2 * chunks])
    land_part, gq, k_land_part = first_back(gm, probs, q, mixed, k_land)
    g_rim = halo(gm, RIM)
    land_parts = exchange(land_part)
    grad_conv, taps_grad = conv_back(gm, g_rim, v, taps)
    gn_own, gt_own, mid_q, mid_k = inverse_back(land_parts, q_land, k_land, saved)

    def give_back(x):
        x = x.reshape((ranks * own,) + x.shape[2:])
        return lax.all_to_all(x, "seq", 0, 0, tiled=True)[:pairs]

    grad_values, gk, q_land_part = third_back(
        weights, v, k, grad_conv, give_back(gn_own), give_back(gt_own), q_land
    )

    def place(x):
        full = jnp.zeros((ranks * own, M, 128), f32)
        return from_pairs(lax.dynamic_update_slice_in_dim(full, x, rank * own, 0))

    both = jnp.stack([q_land_part + place(mid_q), k_land_part + place(mid_k)]).astype(bf16)
    both = both.reshape(2, seqs, ranks, marks, features).transpose(2, 0, 1, 3, 4)
    both = lax.all_to_all(both, "seq", 0, 0, tiled=True).astype(f32).sum(0)
    grad_tokens, qkv_grad = last_pass(tokens, gq, gk, grad_values, both[0], both[1], proj.reshape(shape3), w_qkv)
    qkv_share = scatter_sum(qkv_grad.transpose(1, 0, 2).reshape(features, 3 * features))
    gains = gains.reshape(2, 8, features).sum(1)
    small = lax.psum(jnp.concatenate([taps_grad, gains]), ("dp", "seq"))
    return (
        layer_out.reshape(shape3),
        grad_tokens,
        qkv_share,
        out_share,
        up_share,
        down_share,
        small[:KW],
        small[KW],
        small[KW + 1],
    )


def deliver_kernel(*refs):
    count = len(refs) // 2
    for i in range(count):
        if i < 2:
            refs[count + i][...] = refs[i][...]
        else:
            @pl.when(pl.program_id(0) == 0)
            def _(i=i):
                refs[count + i][...] = refs[i][...]


def deliver(*arrays):
    steps = 2
    split = lambda a: pl.BlockSpec((a.shape[0] // steps, a.shape[1]), lambda i: (i, 0))
    whole = lambda a: pl.BlockSpec(a.shape, lambda i: (0,) * len(a.shape))
    specs = [split(a) for a in arrays[:2]] + [whole(a) for a in arrays[2:]]
    return pl.pallas_call(
        deliver_kernel,
        grid=(steps,),
        in_specs=specs,
        out_specs=specs,
        out_shape=[jax.ShapeDtypeStruct(a.shape, a.dtype) for a in arrays],
        compiler_params=params(62 * MB),
        name="deliver",
    )(*arrays)


def per_device(tokens, w_qkv, w_out, w_up, w_down, conv_filter, gain_att, gain_ffn, grad_out):
    seqs, rows, features = tokens.shape
    ranks = lax.axis_size("seq")
    marks = M // ranks
    pairs = seqs * (features // 128)
    own = -(-pairs // ranks)
    taps = conv_filter
    shape3 = (seqs, rows, features)

    q, k, v, weights, probs, q_land, k_land, v_rim, conv_out, mixed, *saved = front(tokens, w_qkv, taps, own)
    layer_out, normed, s_att, gdl, slope, hid_t, mix_t, gain_f, downs = rows_forward(
        tokens, probs, conv_out, mixed, grad_out, w_out, w_up, w_down, gain_att, gain_ffn
    )
    proj, gm, gain_a, downs, ups, g_rim = rows_backward(
        gdl, slope, normed, s_att, w_out, gain_att, w_down, w_up, hid_t, mix_t, downs.reshape(4, 2, 2, 192, 384), seqs
    )
    grad_tokens, up, down, out, qkv, taps_all, gain_att_all, gain_ffn_all = tail(
        gm.reshape(shape3), probs, q, mixed, q_land, k_land, g_rim, v, taps, saved, weights, k, tokens, proj, gain_a,
        gain_f, w_qkv, downs, ups.reshape(4, 2, 2, 240, 384),
    )
    layer_out, grad_tokens, qkv, out, up, down, taps_all, gain_att_all, gain_ffn_all = deliver(
        layer_out, grad_tokens, qkv, out, up, down, taps_all, gain_att_all, gain_ffn_all
    )
    return (
        layer_out.reshape(shape3),
        grad_tokens.reshape(shape3),
        qkv,
        out,
        up,
        down.T,
        taps_all,
        gain_att_all,
        gain_ffn_all,
    )


def solution(mesh):
    placed = (P("dp", "seq", None), P(), P(), P(), P(), P(), P(), P(), P("dp", "seq", None))
    eight_by_four = mesh.shape["dp"] == 8 and mesh.shape["seq"] == 4
    return jax.shard_map(
        per_device if eight_by_four else per_device_general,
        mesh=mesh,
        in_specs=placed,
        out_specs=(
            P("dp", "seq", None),
            P("dp", "seq", None),
            P("dp", "seq"),
            P("dp", "seq"),
            P("dp", "seq"),
            P("dp", "seq"),
            P(),
            P(),
            P(),
        ),
        check_vma=False,
    )
```
